32 devices in a mesh: ep: 8 (over z, y), tp: 4 (over x, core).
Axes of the slice: x: 2, y: 2, z: 4, core: 2. Of those that a mesh axis runs over, the one named last changes fastest.
Arguments:
- hidden_in: bfloat16 [4096, 1536], P(('ep', 'tp')), may hold values from -6 to 6
- gain_attn: bfloat16 [1536], replicated, may hold values from 0.5 to 1.5
- w_query: bfloat16 [1536, 1536], P('tp'), may hold values from -0.15625 to 0.15625
- key_projection_weight: bfloat16 [512, 1536], P('tp'), may hold values from -0.15625 to 0.15625
- value_projection_weight: bfloat16 [512, 1536], P('tp'), may hold values from -0.15625 to 0.15625
- w_out: bfloat16 [1536, 1536], P('tp'), may hold values from -0.625 to 0.625
- gain_ffn: bfloat16 [1536], replicated, may hold values from 0.5 to 1.5
- w_router: bfloat16 [16, 1536], replicated, may hold values from -0.078125 to 0.078125
- w_gate: bfloat16 [16, 1536, 512], P('ep', None, 'tp'), may hold values from -0.15625 to 0.15625
- w_up: bfloat16 [16, 1536, 512], P('ep', None, 'tp'), may hold values from -0.15625 to 0.15625
- w_down: bfloat16 [16, 512, 1536], P('ep', 'tp'), may hold values from -0.75 to 0.75
- expert_ids: int32 [4096, 8], P('ep'), may hold values from 0 to 15, all different within a row; in each aligned block of 512 rows (0 to 511, 512 to 1023, ...) at most 512 rows name the same one
- slot_order: int32 [4096, 8], P('ep'), may hold values from 0 to 4095, as said below
- segment: int32 [4096], P('ep'), may hold values from 0 to 12, as said below
- position: int32 [4096], P('ep'), may hold values from 0 to 303, as said below
- cotangent: bfloat16 [4096, 1536], P(('ep', 'tp')), may hold values from -6 to 6
Outputs:
- output: bfloat16 [4096, 1536], P(('ep', 'tp'))
- grad_input: float32 [4096, 1536], P(('ep', 'tp'))
- grad_gain_attn: float32 [1536], replicated
- grad_query: float32 [1536, 1536], P('tp')
- grad_key: float32 [512, 1536], P('tp')
- grad_value: float32 [512, 1536], P('tp')
- grad_out: float32 [1536, 1536], P('tp')
- grad_gain_ffn: float32 [1536], replicated
- grad_router: float32 [16, 1536], replicated
- grad_gate: float32 [16, 1536, 512], P('ep', None, 'tp')
- grad_up: float32 [16, 1536, 512], P('ep', None, 'tp')
- grad_down: float32 [16, 512, 1536], P('ep', 'tp')
The draws below stay inside these ranges and needn't reach their ends.
Inputs may be any that keep to these rules, and one draw needn't show every extreme that they name: `expert_ids`: in the 512 rows of one index of ep no expert is named by more than 512 rows, a bound that some block reaches of them. `slot_order`: within the 512 rows of one index of ep every number from 0 to 4095 appears once. Each tree is 512 consecutive tokens: its first 256 tokens are segment 0; segments 1 to 4 (branches, parent 0) hold 32 tokens each and segments 5 to 12 (leaves, parent 1 + (s - 5) // 2) hold 16 tokens each, each segment contiguous, in an order drawn for every tree. A token's position is its depth on its path: trunk 0 to 255, a branch from 256, a leaf from 288, rising by one along its segment.
All inputs are finite; a program needn't handle non-finite values.
Results may differ from the reference program's by a relative error of at most 0.02.
Values may be sent and summed in bfloat16 or wider, within the bound.
A program may use at most 320 MiB of HBM per device.

```python
import math
import jax
import jax.numpy as jnp
import numpy as np
from jax import lax

MODEL_DIMENSION = 1536
QUERY_HEADS = 24
KEY_VALUE_HEADS = 8
HEAD_DIMENSION = 64
FE = 512
TOP = 8
TRUNK = 256
BR = 32
LF = 16
TREE_TOKENS = 512
TOK_DEV = 512
TOTAL_TOKENS = 4096
EXPERTS = 16
C_SRC = 512
CAP = 2304
N_TP = 4


def tree_layout(key):
    base_key = jax.random.fold_in(key, 11)
    number_of_trees = TOTAL_TOKENS // TREE_TOKENS

    def one_tree(index):
        tree_key = jax.random.fold_in(base_key, index)
        kinds = (jax.random.permutation(tree_key, 12) + 1).astype(jnp.int32)
        lengths = jnp.where(kinds <= 4, BR, LF).astype(jnp.int32)
        starts = TRUNK + jnp.cumsum(lengths) - lengths
        cells = jnp.arange(TREE_TOKENS, dtype=jnp.int32)
        which = jnp.sum((cells[:, None] >= starts[None, :]).astype(jnp.int32), axis=1) - 1
        which = jnp.maximum(which, 0)
        chosen = which[:, None] == jnp.arange(12, dtype=jnp.int32)[None, :]
        kind = jnp.sum(jnp.where(chosen, kinds[None, :], 0), axis=1)
        begin = jnp.sum(jnp.where(chosen, starts[None, :], 0), axis=1)
        depth = jnp.where(kind <= 4, TRUNK, TRUNK + BR)
        in_trunk = cells < TRUNK
        seg_ids = jnp.where(in_trunk, 0, kind)
        depths = jnp.where(in_trunk, cells, depth + cells - begin)
        return (seg_ids.astype(jnp.int32), depths.astype(jnp.int32))
    seg_all, pos_all = jax.vmap(one_tree)(jnp.arange(number_of_trees, dtype=jnp.int32))
    return (seg_all.reshape(-1), pos_all.reshape(-1))


def draw_segment(key, part):
    seg_all, pos_all = tree_layout(key)
    return seg_all


def draw_position(key, part):
    seg_all, pos_all = tree_layout(key)
    return pos_all


def draw_slot_order(key, part):
    block_count = TOTAL_TOKENS // TOK_DEV
    order_key = jax.random.fold_in(key, 23)
    block_keys = jax.random.split(order_key, block_count)
    perms = jax.vmap(lambda one_key: jax.random.permutation(one_key, TOK_DEV * TOP))(block_keys)
    return perms.reshape(TOTAL_TOKENS, TOP).astype(jnp.int32)


def block_scale(key, dims, cuts, smallest, largest):
    level = 1.0
    for axis_at, blocks in cuts:
        steps = jax.random.uniform(jax.random.fold_in(jax.random.fold_in(key, 6), axis_at), (blocks,), jnp.float32, smallest / len(cuts), largest / len(cuts))
        level = level * jnp.repeat(jnp.exp(steps), dims[axis_at] // blocks).reshape((-1,) + (1,) * (len(dims) - 1 - axis_at))
    return level


def assign_block(key, own, number, rows, count, top, most, skew):
    sequence = jax.random.permutation(key, count)
    heavy_load, common = portions_of(count, rows * top, most, skew, True), portions_of(count, rows * top, most, skew, False)
    places = jnp.arange(count)

    def named(tallies, offset_by):
        used = int((tallies > 0).sum())
        fixed = max(1, used // 4)
        moved = fixed + (places - fixed + offset_by * (used - fixed)) % max(1, count - fixed)
        return jnp.zeros((count,), jnp.int32).at[sequence[jnp.where(places < fixed, places, moved)]].set(jnp.asarray(tallies, jnp.int32))

    tallies = jnp.where(number % 4 == 0, named(heavy_load, number // 4), named(common, number - number // 4 - 1))
    mixed = jax.random.permutation(jax.random.fold_in(own, 3), count)
    giver, sink = mixed[0:count // 2 * 2:2], mixed[1:count // 2 * 2:2]
    slack = jnp.minimum(tallies[giver] - 1, most - tallies[sink]) // 2
    slack = jnp.where((giver == sequence[0]) | (sink == sequence[0]) | (tallies[sink] == 0), 0, jnp.maximum(slack, 0))
    moved = jax.random.randint(jax.random.fold_in(own, 4), (count // 2,), 0, 1 << 20) % (slack + 1)
    tallies = tallies.at[giver].add(-moved).at[sink].add(moved)
    members = jnp.searchsorted(jnp.cumsum(tallies), jnp.arange(rows * top), side="right").astype(jnp.int32)
    grid = members.reshape(top, rows).T
    grid = grid[jax.random.permutation(jax.random.fold_in(own, 1), rows)]
    offset_by = jax.random.randint(jax.random.fold_in(own, 2), (rows, 1), 0, top)
    return jnp.take_along_axis(grid, (jnp.arange(top)[None, :] + offset_by) % top, axis=1)


def portions_of(number_of, total, limit, skew, full):
    weights = [(1 << 20) // math.isqrt(standing ** skew) + 1 for standing in range(1, number_of + 1)]
    largest = limit if full else min(limit, max(-(-total // number_of), total * weights[0] // sum(weights)))
    least = 1 if total - largest >= number_of - 1 else 0
    given, spare = [largest] + [least] * (number_of - 1), total - largest - least * (number_of - 1)
    while spare > 0:
        movable = [i for i in range(1, number_of) if given[i] < largest] or [i for i in range(1, number_of) if given[i] < limit]
        mass, budget = sum([weights[i] for i in movable]), spare
        for i in movable:
            addition = min(limit - given[i], max(1, budget * weights[i] // mass), spare)
            given[i] = given[i] + addition
            spare = spare - addition
    return np.array(given)


def normal_values(stream_key, extent, deviation, reach, shards=(), kind=jnp.bfloat16):
    drawn = deviation * jax.random.normal(stream_key, extent, jnp.float32)
    if shards:
        drawn = drawn * block_scale(stream_key, extent, shards, -0.22, 0.18)
    return jnp.clip(drawn, -reach, reach).astype(kind)


def setup_inputs(seed: int = 0) -> dict:
    arg_keys = jax.random.split(jax.random.key(seed), 17)
    hidden_in = normal_values(arg_keys[0], (TOTAL_TOKENS, MODEL_DIMENSION), 1.0, 6.0, ((0, 32),))
    gain_attn = jnp.clip(1.0 + 0.1 * jax.random.normal(arg_keys[1], (MODEL_DIMENSION,), jnp.float32), 0.5, 1.5).astype(jnp.bfloat16)
    w_query = normal_values(arg_keys[2], (QUERY_HEADS * HEAD_DIMENSION, MODEL_DIMENSION), MODEL_DIMENSION ** -0.5, 0.15625, ((0, 4),))
    key_projection_weight = normal_values(arg_keys[3], (KEY_VALUE_HEADS * HEAD_DIMENSION, MODEL_DIMENSION), MODEL_DIMENSION ** -0.5, 0.15625, ((0, 4),))
    value_projection_weight = normal_values(arg_keys[4], (KEY_VALUE_HEADS * HEAD_DIMENSION, MODEL_DIMENSION), MODEL_DIMENSION ** -0.5, 0.15625, ((0, 4),))
    w_out = normal_values(arg_keys[5], (QUERY_HEADS * HEAD_DIMENSION, MODEL_DIMENSION), (QUERY_HEADS * HEAD_DIMENSION // 16) ** -0.5, 0.625, ((0, 4),))
    gain_ffn = jnp.clip(1.0 + 0.1 * jax.random.normal(arg_keys[6], (MODEL_DIMENSION,), jnp.float32), 0.5, 1.5).astype(jnp.bfloat16)
    w_router = normal_values(arg_keys[7], (EXPERTS, MODEL_DIMENSION), (4 * MODEL_DIMENSION) ** -0.5, 0.078125)
    w_gate = normal_values(arg_keys[8], (EXPERTS, MODEL_DIMENSION, FE), MODEL_DIMENSION ** -0.5, 0.15625, ((0, 8), (2, 4)))
    w_up = normal_values(arg_keys[9], (EXPERTS, MODEL_DIMENSION, FE), MODEL_DIMENSION ** -0.5, 0.15625, ((0, 8), (2, 4)))
    w_down = normal_values(arg_keys[10], (EXPERTS, FE, MODEL_DIMENSION), (FE // 8) ** -0.5, 0.75, ((0, 8), (1, 4)))
    expert_ids_keys = jax.random.split(jax.random.fold_in(arg_keys[11], 1), TOTAL_TOKENS // TOK_DEV)
    expert_ids_turns = jax.random.permutation(jax.random.fold_in(arg_keys[11], 3), TOTAL_TOKENS // TOK_DEV)
    expert_ids = jax.vmap(lambda own, number: assign_block(jax.random.fold_in(arg_keys[11], 2), own, number, TOK_DEV, EXPERTS, TOP, C_SRC, 1))(expert_ids_keys, expert_ids_turns).reshape((TOTAL_TOKENS, TOP))
    slot_order = draw_slot_order(jax.random.fold_in(arg_keys[16], 71), 0)
    segment = draw_segment(jax.random.fold_in(arg_keys[16], 71), 0)
    position = draw_position(jax.random.fold_in(arg_keys[16], 71), 0)
    cotangent = normal_values(arg_keys[15], (TOTAL_TOKENS, MODEL_DIMENSION), 1.0, 6.0, ((0, 32),))
    return dict(hidden_in=hidden_in, gain_attn=gain_attn, w_query=w_query, key_projection_weight=key_projection_weight, value_projection_weight=value_projection_weight, w_out=w_out, gain_ffn=gain_ffn, w_router=w_router, w_gate=w_gate, w_up=w_up, w_down=w_down, expert_ids=expert_ids, slot_order=slot_order, segment=segment, position=position, cotangent=cotangent)


EPSILON = 1e-06
ROPE_BASE = 10000.0
EXACT_PRECISION = lax.Precision.HIGHEST

@jax.custom_vjp
def lower_precision(v):
    return lax.optimization_barrier(v.astype(jnp.bfloat16)).astype(jnp.float32)

@jax.custom_vjp
def lower_precision_backward(v):
    return v

def low_keep(v):
    return (lower_precision(v), None)

def low_pass(kept, grad):
    return (grad,)

def back_keep(v):
    return (v, None)

def back_low(kept, grad):
    return (lower_precision(grad),)
lower_precision.defvjp(low_keep, low_pass)
lower_precision_backward.defvjp(back_keep, back_low)

def rms_norm(value_rows, gain):
    return value_rows * lax.rsqrt(lax.optimization_barrier(jnp.mean(value_rows * value_rows, axis=-1, keepdims=True)) + EPSILON) * gain

def rope_tables(position):
    half_width = HEAD_DIMENSION // 2
    freqs = ROPE_BASE ** (-(jnp.arange(half_width, dtype=jnp.float32) * 2.0 / HEAD_DIMENSION))
    angle = position.astype(jnp.float32)[:, None] * freqs[None, :]
    return (jnp.cos(angle)[:, None, :], jnp.sin(angle)[:, None, :])

def apply_rotation(value_rows, cosine_lookup, sine_lookup):
    half_width = value_rows.shape[-1] // 2
    first = value_rows[..., :half_width]
    second = value_rows[..., half_width:]
    return jnp.concatenate([first * cosine_lookup - second * sine_lookup, first * sine_lookup + second * cosine_lookup], axis=-1)

def visible(query_seg, query_pos, key_seg, key_pos):
    seg_q = query_seg[:, None]
    seg_k = key_seg[None, :]
    above = (seg_k == seg_q) | (seg_k == 0) | (seg_k >= 1) & (seg_k <= 4) & (seg_q >= 5) & ((seg_q - 5) // 2 + 1 == seg_k)
    return above & (key_pos[None, :] <= query_pos[:, None])

def attention_over_trees(packed):
    query_tree_ids, key_tree, value_tree, seg_tree, pos_tree = packed
    group_factor = QUERY_HEADS // KEY_VALUE_HEADS
    grouped_heads = query_tree_ids.reshape(TREE_TOKENS, KEY_VALUE_HEADS, group_factor, HEAD_DIMENSION)
    raw_scores = jnp.einsum('qkgd,pkd->kgqp', grouped_heads, key_tree, precision=EXACT_PRECISION)
    scores = lower_precision_backward(raw_scores * HEAD_DIMENSION ** (-0.5))
    allowed = visible(seg_tree, pos_tree, seg_tree, pos_tree)
    scores = jnp.where(allowed[None, None], scores, -1e+30)
    probs = lower_precision(jax.nn.softmax(scores, axis=-1))
    mixed = jnp.einsum('kgqp,pkd->qkgd', probs, value_tree, precision=EXACT_PRECISION)
    return mixed.reshape(TREE_TOKENS, QUERY_HEADS * HEAD_DIMENSION)

def expert_rows(packed):
    slot_rows, gate_weight, up_weight, down_weight = packed
    group_width = FE // N_TP
    spread = lower_precision_backward(jnp.broadcast_to(slot_rows[None], (N_TP, CAP, MODEL_DIMENSION)))
    gate_act = lower_precision_backward(jnp.einsum('tcd,dtf->tcf', spread, gate_weight.reshape(MODEL_DIMENSION, N_TP, group_width), precision=EXACT_PRECISION))
    up_act = lower_precision_backward(jnp.einsum('tcd,dtf->tcf', spread, up_weight.reshape(MODEL_DIMENSION, N_TP, group_width), precision=EXACT_PRECISION))
    hidden = lower_precision(jax.nn.silu(gate_act) * up_act)
    partial_value = lower_precision(jnp.einsum('tcf,tfd->tcd', hidden, down_weight.reshape(N_TP, group_width, MODEL_DIMENSION), precision=EXACT_PRECISION))
    return lower_precision_backward(lax.optimization_barrier(jnp.sum(partial_value, axis=0)))

def slot_tables(expert_ids, slot_order):
    block_count = TOTAL_TOKENS // TOK_DEV
    pair_count = TOK_DEV * TOP
    ids_block = expert_ids.reshape(block_count, pair_count)
    order_block = slot_order.reshape(block_count, pair_count)

    def local_rank(ids_row, order_row):
        sorted_ids = jnp.zeros((pair_count,), jnp.int32).at[order_row].set(ids_row)
        hits = (sorted_ids[:, None] == jnp.arange(EXPERTS, dtype=jnp.int32)[None, :]).astype(jnp.int32)
        running = jnp.cumsum(hits, axis=0)
        rank_sorted = lax.optimization_barrier(jnp.sum(running * hits, axis=1)) - 1
        return (rank_sorted[order_row], lax.optimization_barrier(jnp.sum(hits, axis=0)))
    ranks, counts = jax.vmap(local_rank)(ids_block, order_block)
    offsets = jnp.cumsum(counts, axis=0) - counts
    global_rank = ranks + jnp.take_along_axis(offsets, ids_block, axis=1)
    kept = global_rank < CAP
    return jnp.where(kept, ids_block * CAP + global_rank, EXPERTS * CAP).reshape(-1).astype(jnp.int32)

def reference(hidden_in, gain_attn, w_query, key_projection_weight, value_projection_weight, w_out, gain_ffn, w_router, w_gate, w_up, w_down, expert_ids, slot_order, segment, position, cotangent):
    slot_index = slot_tables(expert_ids, slot_order)
    pair_token = (jnp.arange(TOTAL_TOKENS * TOP, dtype=jnp.int32) // TOP).astype(jnp.int32)
    token_of_slot = jnp.full((EXPERTS * CAP + 1,), TOTAL_TOKENS, jnp.int32).at[slot_index].set(pair_token)[:EXPERTS * CAP]
    cosine_lookup, sine_lookup = rope_tables(position)
    number_of_trees = TOTAL_TOKENS // TREE_TOKENS

    def forward(inputs_f, gain_one, query_w, key_matrix, value_matrix, out_w, gain_two, router_w, gate_w, up_w, down_w):
        first_normalized = lower_precision(rms_norm(inputs_f, gain_one))
        query_rows = lower_precision(apply_rotation(lower_precision_backward(jnp.dot(first_normalized, query_w.T, precision=EXACT_PRECISION)).reshape(TOTAL_TOKENS, QUERY_HEADS, HEAD_DIMENSION), cosine_lookup, sine_lookup))
        key_rows = lower_precision(apply_rotation(lower_precision_backward(jnp.dot(first_normalized, key_matrix.T, precision=EXACT_PRECISION)).reshape(TOTAL_TOKENS, KEY_VALUE_HEADS, HEAD_DIMENSION), cosine_lookup, sine_lookup))
        value_rows = lower_precision(lower_precision_backward(jnp.dot(first_normalized, value_matrix.T, precision=EXACT_PRECISION))).reshape(TOTAL_TOKENS, KEY_VALUE_HEADS, HEAD_DIMENSION)
        head_outputs = lax.map(jax.checkpoint(attention_over_trees), (query_rows.reshape(number_of_trees, TREE_TOKENS, QUERY_HEADS, HEAD_DIMENSION), key_rows.reshape(number_of_trees, TREE_TOKENS, KEY_VALUE_HEADS, HEAD_DIMENSION), value_rows.reshape(number_of_trees, TREE_TOKENS, KEY_VALUE_HEADS, HEAD_DIMENSION), segment.reshape(number_of_trees, TREE_TOKENS), position.reshape(number_of_trees, TREE_TOKENS)))
        head_outputs = lower_precision(lower_precision_backward(head_outputs.reshape(TOTAL_TOKENS, QUERY_HEADS * HEAD_DIMENSION)))
        middle = inputs_f + lower_precision_backward(jnp.dot(head_outputs, out_w, precision=EXACT_PRECISION))
        normed_two = lower_precision(rms_norm(middle, gain_two))
        logits = jnp.dot(normed_two, router_w.T, precision=EXACT_PRECISION)
        gates = jax.nn.softmax(jnp.take_along_axis(logits, expert_ids, axis=1), axis=-1)
        slot_rows = jnp.take(normed_two, token_of_slot, axis=0, mode='fill', fill_value=0.0).reshape(EXPERTS, CAP, MODEL_DIMENSION)
        results = lax.map(jax.checkpoint(expert_rows), (slot_rows, gate_w, up_w, down_w))
        picked = jnp.take(results.reshape(EXPERTS * CAP, MODEL_DIMENSION), slot_index, axis=0, mode='fill', fill_value=0.0).reshape(TOTAL_TOKENS, TOP, MODEL_DIMENSION)
        return middle + jnp.einsum('tk,tkd->td', gates, picked, precision=EXACT_PRECISION)
    primal, pullback = jax.vjp(forward, hidden_in.astype(jnp.float32), gain_attn.astype(jnp.float32), w_query.astype(jnp.float32), key_projection_weight.astype(jnp.float32), value_projection_weight.astype(jnp.float32), w_out.astype(jnp.float32), gain_ffn.astype(jnp.float32), w_router.astype(jnp.float32), w_gate.astype(jnp.float32), w_up.astype(jnp.float32), w_down.astype(jnp.float32))
    grads = pullback(cotangent.astype(jnp.float32))
    return (primal.astype(jnp.bfloat16), grads[0], grads[1], grads[2], grads[3], grads[4], grads[5], grads[6], grads[7], grads[8], grads[9], grads[10])
```

```python
import jax
import jax.numpy as jnp
from jax import lax
from jax.sharding import PartitionSpec as P

HEAD_DIMENSION = 64
TREE_TOKENS = 512
CAP = 2304


EPSILON = 1e-06
ROPE_BASE = 10000.0
EXACT_PRECISION = lax.Precision.HIGHEST


def rope_tables(position, head_width):
    half_width = head_width // 2
    freqs = ROPE_BASE ** (-(jnp.arange(half_width, dtype=jnp.float32) * 2.0 / head_width))
    angle = position.astype(jnp.float32)[:, None] * freqs[None, :]
    return (jnp.cos(angle)[:, None, :], jnp.sin(angle)[:, None, :])


def apply_rotation(value_rows, cosine_lookup, sine_lookup):
    half_width = value_rows.shape[-1] // 2
    first = value_rows[..., :half_width]
    second = value_rows[..., half_width:]
    return jnp.concatenate(
        [
            first * cosine_lookup - second * sine_lookup,
            first * sine_lookup + second * cosine_lookup,
        ],
        axis=-1,
    )


def rotate_back(grads, cosine_lookup, sine_lookup):
    half_width = grads.shape[-1] // 2
    first = grads[..., :half_width]
    second = grads[..., half_width:]
    return jnp.concatenate(
        [
            first * cosine_lookup + second * sine_lookup,
            second * cosine_lookup - first * sine_lookup,
        ],
        axis=-1,
    )


def norm_scale(value_rows):
    return lax.rsqrt(jnp.mean(value_rows * value_rows, axis=-1, keepdims=True) + EPSILON)


def norm_back(value_rows, scale, gain, grad_normed):
    weighted = grad_normed * gain
    inner = jnp.mean(value_rows * weighted, axis=-1, keepdims=True)
    grad_values = scale * weighted - value_rows * (scale * scale * scale) * inner
    return (grad_values, jnp.sum(grad_normed * value_rows * scale, axis=0))


def group_rows(value_rows):
    return lax.all_gather(value_rows, "tp", axis=0, tiled=True)


def group_totals(value_rows):
    return lax.psum_scatter(value_rows, "tp", scatter_dimension=0, tiled=True)


def gather_all(value_rows):
    return lax.all_gather(value_rows, ("ep", "tp"), axis=0, tiled=True)


def total_all(value_rows):
    return lax.psum_scatter(value_rows, ("ep", "tp"), scatter_dimension=0, tiled=True)


def kept_pairs(expert_ids, slot_order, expert_count, row_start, share):
    experts = jnp.arange(expert_count, dtype=jnp.int32)
    chosen = expert_ids[:, :, None] == experts[None, None, :]
    last = jnp.int32(1 << 30)
    order = jnp.min(jnp.where(chosen, slot_order[:, :, None], last), axis=1)
    counts = jnp.sum((order < last).astype(jnp.int32), axis=0)
    every = lax.all_gather(counts, "ep")
    earlier = jnp.arange(every.shape[0], dtype=jnp.int32) < lax.axis_index("ep")
    offsets = jnp.sum(jnp.where(earlier[:, None], every, 0), axis=0)
    own = lax.dynamic_slice_in_dim(order, row_start, share, 0)
    rank = jnp.sum((order[:, None, :] < own[None, :, :]).astype(jnp.int32), axis=0)
    used = own < last
    return used, used & (rank + offsets[None, :] < CAP)


def visible_block(query_seg, query_pos, query_row, key_seg, key_pos, key_row):
    seg_q = query_seg[:, None]
    seg_k = key_seg[None, :]
    above = (
        (seg_k == seg_q)
        | (seg_k == 0)
        | (seg_k >= 1) & (seg_k <= 4) & (seg_q >= 5) & ((seg_q - 5) // 2 + 1 == seg_k)
    )
    same_tree = query_row[:, None] // TREE_TOKENS == key_row[None, :] // TREE_TOKENS
    return above & same_tree & (key_pos[None, :] <= query_pos[:, None])


def block_scores(query_part, key_rows, allowed, scale):
    scores = (
        jnp.einsum("qkgd,pkd->kgqp", query_part, key_rows, preferred_element_type=jnp.float32)
        * scale
    )
    return jnp.where(allowed[None, None], scores, -1e30)


def attend_forward(query_rows, key_rows, value_rows, segment, position):
    total_rows = query_rows.shape[0]
    scale = query_rows.shape[-1] ** (-0.5)
    row_ids = jnp.arange(total_rows, dtype=jnp.int32)
    allowed = visible_block(segment, position, row_ids, segment, position, row_ids)
    scores = block_scores(query_rows, key_rows, allowed, scale)
    top_score = jnp.max(scores, axis=-1, keepdims=True)
    weights = jnp.exp(scores - top_score)
    weight_sum = jnp.sum(weights, axis=-1, keepdims=True)
    probs = (weights / weight_sum).astype(jnp.bfloat16)
    outputs = jnp.einsum(
        "kgqp,pkd->qkgd", probs, value_rows, preferred_element_type=jnp.float32
    ).astype(jnp.bfloat16)
    log_sums = [top_score + jnp.log(weight_sum)]
    return (outputs, log_sums)


def attend_backward(
    query_rows, key_rows, value_rows, segment, position, log_sums, grad_heads, block_rows
):
    total_rows = query_rows.shape[0]
    scale = query_rows.shape[-1] ** (-0.5)
    row_ids = jnp.arange(total_rows, dtype=jnp.int32)
    grad_keys = jnp.zeros(key_rows.shape, jnp.float32)
    grad_values = jnp.zeros(value_rows.shape, jnp.float32)
    grad_query = []
    for number, first_row in enumerate(range(0, total_rows, block_rows)):
        allowed = visible_block(segment, position, row_ids, segment, position, row_ids)
        scores = block_scores(query_rows, key_rows, allowed, scale)
        probs = jnp.where(allowed[None, None], jnp.exp(scores - log_sums[number]), 0.0)
        grad_values = jnp.einsum(
            "kgqp,qkgd->pkd",
            probs.astype(jnp.bfloat16),
            grad_heads,
            preferred_element_type=jnp.float32,
        )
        grad_probs = jnp.einsum(
            "qkgd,pkd->kgqp", grad_heads, value_rows, preferred_element_type=jnp.float32
        )
        inner = jnp.sum(probs * grad_probs, axis=-1, keepdims=True)
        grad_scores = (probs * (grad_probs - inner)).astype(jnp.bfloat16)
        grad_query.append(
            jnp.einsum("kgqp,pkd->qkgd", grad_scores, key_rows, preferred_element_type=jnp.float32)
            * scale
        )
        grad_keys = (
            jnp.einsum(
                "kgqp,qkgd->pkd", grad_scores, query_rows, preferred_element_type=jnp.float32
            )
            * scale
        )
    return (grad_query[0], grad_keys, grad_values)


def local(
    hidden_in,
    gain_attn,
    w_query,
    key_projection_weight,
    value_projection_weight,
    w_out,
    gain_ffn,
    w_router,
    w_gate,
    w_up,
    w_down,
    expert_ids,
    slot_order,
    segment,
    position,
    cotangent,
):
    model_width = w_query.shape[1]
    head_width = HEAD_DIMENSION
    local_heads = w_query.shape[0] // head_width
    local_kv = key_projection_weight.shape[0] // head_width
    group_factor = local_heads // local_kv
    token_count = expert_ids.shape[0]
    share = hidden_in.shape[0]
    row_start = lax.axis_index("tp") * share
    expert_count = w_router.shape[0]
    per_owner = w_gate.shape[0]
    block_rows = 512
    used, kept = kept_pairs(expert_ids, slot_order, expert_count, row_start, share)
    cot_all = gather_all(cotangent)
    inputs_own = hidden_in.astype(jnp.float32)
    gain_one = gain_attn.astype(jnp.float32)
    gain_two = gain_ffn.astype(jnp.float32)
    scale_one = norm_scale(inputs_own)
    first_normalized = group_rows((inputs_own * scale_one * gain_one).astype(jnp.bfloat16))
    cosine_lookup, sine_lookup = rope_tables(position, head_width)
    query_proj = jnp.einsum(
        "rd,fd->rf", first_normalized, w_query, preferred_element_type=jnp.float32
    ).reshape(token_count, local_heads, head_width)
    key_proj = jnp.einsum(
        "rd,fd->rf", first_normalized, key_projection_weight, preferred_element_type=jnp.float32
    ).reshape(token_count, local_kv, head_width)
    query_rows = (
        apply_rotation(query_proj, cosine_lookup, sine_lookup)
        .astype(jnp.bfloat16)
        .reshape(token_count, local_kv, group_factor, head_width)
    )
    key_rows = apply_rotation(key_proj, cosine_lookup, sine_lookup).astype(jnp.bfloat16)
    value_rows = (
        jnp.einsum(
            "rd,fd->rf",
            first_normalized,
            value_projection_weight,
            preferred_element_type=jnp.float32,
        )
        .astype(jnp.bfloat16)
        .reshape(token_count, local_kv, head_width)
    )
    head_outputs, log_sums = attend_forward(query_rows, key_rows, value_rows, segment, position)
    head_outputs = head_outputs.reshape(token_count, local_heads * head_width)
    middle_own = inputs_own + group_totals(
        jnp.dot(head_outputs, w_out, preferred_element_type=jnp.float32)
    )
    scale_two = norm_scale(middle_own)
    normed_own = (middle_own * scale_two * gain_two).astype(jnp.bfloat16)
    normed_two = gather_all(normed_own)
    logits = jnp.einsum("rd,ed->re", normed_own, w_router, preferred_element_type=jnp.float32)
    top_logit = jnp.max(jnp.where(used, logits, -jnp.inf), axis=-1, keepdims=True)
    powers = jnp.where(used, jnp.exp(logits - top_logit), 0.0)
    gates = powers / jnp.sum(powers, axis=-1, keepdims=True)
    first_expert = lax.axis_index("ep") * per_owner
    kept_all = lax.dynamic_slice_in_dim(
        gather_all(kept.astype(jnp.float32)), first_expert, per_owner, 1
    )
    gate_all = lax.dynamic_slice_in_dim(
        gather_all(jnp.where(kept, gates, 0.0)), first_expert, per_owner, 1
    )
    units = w_gate.shape[2]
    gate_in = jnp.concatenate([w_gate[e] for e in range(per_owner)], axis=1)
    up_in = jnp.concatenate([w_up[e] for e in range(per_owner)], axis=1)
    down_in = w_down.reshape(per_owner * units, model_width)
    spread = jnp.repeat(gate_all, units, axis=1)
    gate_act = jnp.dot(normed_two, gate_in, preferred_element_type=jnp.float32)
    up_act = jnp.dot(normed_two, up_in, preferred_element_type=jnp.float32)
    back_act = jnp.einsum("rd,fd->rf", cot_all, down_in, preferred_element_type=jnp.float32)
    sigma = jax.nn.sigmoid(gate_act)
    hidden = gate_act * sigma * up_act
    weighted_hidden = (spread * hidden).astype(jnp.bfloat16)
    grad_hidden = spread * back_act
    grad_gate_act = (grad_hidden * up_act * sigma * (1.0 + gate_act * (1.0 - sigma))).astype(
        jnp.bfloat16
    )
    grad_up_act = (grad_hidden * gate_act * sigma).astype(jnp.bfloat16)
    grad_gates_part = kept_all * jnp.sum(
        (hidden * back_act).reshape(-1, per_owner, units), axis=2
    )
    grad_rows = (
        jnp.einsum("rf,df->rd", grad_gate_act, gate_in, preferred_element_type=jnp.float32)
        + jnp.einsum("rf,df->rd", grad_up_act, up_in, preferred_element_type=jnp.float32)
    ).astype(jnp.bfloat16)
    grad_normed_own = total_all(grad_rows).astype(jnp.float32)
    grad_gates_own = total_all(
        lax.dynamic_update_slice_in_dim(
            jnp.zeros((normed_two.shape[0], expert_count), jnp.float32),
            grad_gates_part,
            first_expert,
            1,
        )
    )
    combined = jnp.dot(weighted_hidden, down_in, preferred_element_type=jnp.float32).astype(
        jnp.bfloat16
    )
    output_own = (middle_own + total_all(combined).astype(jnp.float32)).astype(jnp.bfloat16)
    grad_w_gate = jnp.einsum(
        "rd,ref->edf",
        normed_two,
        grad_gate_act.reshape(-1, per_owner, units),
        preferred_element_type=jnp.float32,
    )
    grad_w_up = jnp.einsum(
        "rd,ref->edf",
        normed_two,
        grad_up_act.reshape(-1, per_owner, units),
        preferred_element_type=jnp.float32,
    )
    grad_w_down = jnp.einsum(
        "rf,rd->fd", weighted_hidden, cot_all, preferred_element_type=jnp.float32
    ).reshape(per_owner, units, model_width)
    inner_gate = jnp.sum(gates * grad_gates_own, axis=-1, keepdims=True)
    grad_logits = gates * (grad_gates_own - inner_gate)
    router_f = w_router.astype(jnp.float32)
    grad_normed_own = grad_normed_own + jnp.dot(grad_logits, router_f, precision=EXACT_PRECISION)
    grad_router = jnp.dot(grad_logits.T, normed_own.astype(jnp.float32), precision=EXACT_PRECISION)
    grad_middle_back, grad_gain_ffn = norm_back(middle_own, scale_two, gain_two, grad_normed_own)
    grad_middle = cotangent.astype(jnp.float32) + grad_middle_back
    grad_attn = group_rows(grad_middle.astype(jnp.bfloat16))
    grad_w_out = jnp.einsum(
        "rf,rd->fd", head_outputs, grad_attn, preferred_element_type=jnp.float32
    )
    grad_heads = (
        jnp.einsum("rd,fd->rf", grad_attn, w_out, preferred_element_type=jnp.float32)
        .astype(jnp.bfloat16)
        .reshape(token_count, local_kv, group_factor, head_width)
    )
    grad_query, grad_keys, grad_values = attend_backward(
        query_rows, key_rows, value_rows, segment, position, log_sums, grad_heads, block_rows
    )
    grad_query_proj = (
        rotate_back(
            grad_query.reshape(token_count, local_heads, head_width), cosine_lookup, sine_lookup
        )
        .astype(jnp.bfloat16)
        .reshape(token_count, local_heads * head_width)
    )
    grad_key_proj = (
        rotate_back(grad_keys, cosine_lookup, sine_lookup)
        .astype(jnp.bfloat16)
        .reshape(token_count, local_kv * head_width)
    )
    grad_value_proj = grad_values.astype(jnp.bfloat16).reshape(token_count, local_kv * head_width)
    grad_w_query = jnp.einsum(
        "rf,rd->fd", grad_query_proj, first_normalized, preferred_element_type=jnp.float32
    )
    grad_w_key = jnp.einsum(
        "rf,rd->fd", grad_key_proj, first_normalized, preferred_element_type=jnp.float32
    )
    grad_w_value = jnp.einsum(
        "rf,rd->fd", grad_value_proj, first_normalized, preferred_element_type=jnp.float32
    )
    grad_normed_one = jnp.einsum(
        "rf,fd->rd", grad_query_proj, w_query, preferred_element_type=jnp.float32
    )
    grad_normed_one = grad_normed_one + jnp.einsum(
        "rf,fd->rd", grad_key_proj, key_projection_weight, preferred_element_type=jnp.float32
    )
    grad_normed_one = grad_normed_one + jnp.einsum(
        "rf,fd->rd", grad_value_proj, value_projection_weight, preferred_element_type=jnp.float32
    )
    grad_one_own = group_totals(grad_normed_one)
    grad_inputs_back, grad_gain_attn = norm_back(inputs_own, scale_one, gain_one, grad_one_own)
    grad_input = grad_middle + grad_inputs_back
    grad_w_query, grad_w_key, grad_w_value, grad_w_out = (
        lax.psum(grad_w_query.astype(jnp.bfloat16), "ep").astype(jnp.float32),
        lax.psum(grad_w_key.astype(jnp.bfloat16), "ep").astype(jnp.float32),
        lax.psum(grad_w_value.astype(jnp.bfloat16), "ep").astype(jnp.float32),
        lax.psum(grad_w_out.astype(jnp.bfloat16), "ep").astype(jnp.float32),
    )
    grad_gain_attn, grad_gain_ffn, grad_router = lax.psum(
        (grad_gain_attn, grad_gain_ffn, grad_router), ("ep", "tp")
    )
    return (
        output_own,
        grad_input,
        grad_gain_attn,
        grad_w_query,
        grad_w_key,
        grad_w_value,
        grad_w_out,
        grad_gain_ffn,
        grad_router,
        grad_w_gate,
        grad_w_up,
        grad_w_down,
    )


def solution(mesh):
    placed = (
        P(("ep", "tp"), None),
        P(),
        P("tp", None),
        P("tp", None),
        P("tp", None),
        P("tp", None),
        P(),
        P(),
        P("ep", None, "tp"),
        P("ep", None, "tp"),
        P("ep", "tp", None),
        P("ep", None),
        P("ep", None),
        P("ep"),
        P("ep"),
        P(("ep", "tp"), None),
    )
    return jax.shard_map(
        local,
        mesh=mesh,
        in_specs=placed,
        out_specs=(
            P(("ep", "tp"), None),
            P(("ep", "tp"), None),
            P(),
            P("tp", None),
            P("tp", None),
            P("tp", None),
            P("tp", None),
            P(),
            P(),
            P("ep", None, "tp"),
            P("ep", None, "tp"),
            P("ep", "tp", None),
        ),
        check_vma=False,
    )
```

```python
import functools

import jax
import jax.numpy as jnp
from jax import lax
from jax.experimental import pallas as pl
from jax.experimental.pallas import tpu as pltpu
from jax.sharding import PartitionSpec as P

HEAD_DIMENSION = 64
TREE_TOKENS = 512
CAP = 2304


EPSILON = 1e-06
ROPE_BASE = 10000.0
EXACT_PRECISION = lax.Precision.HIGHEST


def rope_tables(position, head_width):
    half_width = head_width // 2
    freqs = ROPE_BASE ** (-(jnp.arange(half_width, dtype=jnp.float32) * 2.0 / head_width))
    angle = position.astype(jnp.float32)[:, None] * freqs[None, :]
    return (jnp.cos(angle)[:, None, :], jnp.sin(angle)[:, None, :])


def apply_rotation(value_rows, cosine_lookup, sine_lookup):
    half_width = value_rows.shape[-1] // 2
    first = value_rows[..., :half_width]
    second = value_rows[..., half_width:]
    return jnp.concatenate(
        [
            first * cosine_lookup - second * sine_lookup,
            first * sine_lookup + second * cosine_lookup,
        ],
        axis=-1,
    )


def rotate_back(grads, cosine_lookup, sine_lookup):
    half_width = grads.shape[-1] // 2
    first = grads[..., :half_width]
    second = grads[..., half_width:]
    return jnp.concatenate(
        [
            first * cosine_lookup + second * sine_lookup,
            second * cosine_lookup - first * sine_lookup,
        ],
        axis=-1,
    )


def norm_scale(value_rows):
    return lax.rsqrt(jnp.mean(value_rows * value_rows, axis=-1, keepdims=True) + EPSILON)


def norm_back(value_rows, scale, gain, grad_normed):
    weighted = grad_normed * gain
    inner = jnp.mean(value_rows * weighted, axis=-1, keepdims=True)
    grad_values = scale * weighted - value_rows * (scale * scale * scale) * inner
    return (grad_values, jnp.sum(grad_normed * value_rows * scale, axis=0))


def group_rows(value_rows):
    return lax.all_gather(value_rows, "tp", axis=0, tiled=True)


def group_totals(value_rows):
    return lax.psum_scatter(value_rows, "tp", scatter_dimension=0, tiled=True)


MESH = pl.DeviceIdType.MESH


class Place:
    def __init__(self, ep_size):
        self.depth = ep_size // 2
        ep, tp = lax.axis_index("ep"), lax.axis_index("tp")
        self.z, self.y = ep // 2, ep % 2
        self.x, self.c = tp // 2, tp % 2

    def device(self, z=None, y=None, x=None, c=None):
        z = self.z if z is None else z
        y = self.y if y is None else y
        x = self.x if x is None else x
        c = self.c if c is None else c
        return (z * 2 + y, x * 2 + c)

    def sibling(self):
        return self.device(c=1 - self.c)

    def x_peer(self):
        return self.device(x=1 - self.x)

    def y_peer(self):
        return self.device(y=1 - self.y)

    def after(self, step):
        return lax.rem(self.z + step, self.depth)

    def before(self, step):
        return lax.rem(self.z + self.depth - step, self.depth)


def meet(devices):
    barrier = pltpu.get_barrier_semaphore()
    for device in devices:
        pl.semaphore_signal(barrier, inc=1, device_id=device, device_id_type=MESH)
    pl.semaphore_wait(barrier, len(devices))


def send(src, dst, send_sem, recv_sem, device):
    copy = pltpu.make_async_remote_copy(
        src_ref=src,
        dst_ref=dst,
        send_sem=send_sem,
        recv_sem=recv_sem,
        device_id=device,
        device_id_type=MESH,
    )
    copy.start()
    return copy


def gather_kernel(ep_size, own, out, own_sem, z_sems, pair_sems, core_sems):
    me = Place(ep_size)
    depth = me.depth
    half = own.shape[0] // 2
    z_send, z_recv = z_sems.at[0], z_sems.at[1]
    pair_send, pair_recv = pair_sems.at[0], pair_sems.at[1]
    core_send, core_recv = core_sems.at[0], core_sems.at[1]
    meet(
        [me.sibling(), me.x_peer(), me.y_peer()]
        + [me.device(z=me.after(s)) for s in range(1, depth)]
    )

    def rows(part):
        return pl.ds(part * half, half)

    def block(step, y, x, part, c=None):
        return out.at[me.before(step), y, x, me.c if c is None else c, rows(part)]

    started = []

    def forward(source, target, sems, slot, device):
        started.append(send(source, target, sems[0].at[slot], sems[1].at[slot], device))

    for s in range(1, depth):
        for part in range(2):
            forward(
                own.at[rows(part)],
                out.at[me.z, me.y, me.x, me.c, rows(part)],
                (z_send, z_recv),
                (s - 1) * 2 + part,
                me.device(z=me.after(s)),
            )
    local = pltpu.make_async_copy(own, out.at[me.z, me.y, me.x, me.c], own_sem)
    local.start()
    local.wait()

    kinds = [
        (me.y, me.x, 0),
        (me.y, me.x, 1),
        (1 - me.y, me.x, 0),
        (me.y, 1 - me.x, 1),
        (1 - me.y, me.x, 1),
        (1 - me.y, 1 - me.x, 1),
        (me.y, 1 - me.x, 0),
        (1 - me.y, 1 - me.x, 0),
    ]
    x_route = {0: 6, 2: 7, 1: 3}
    y_route = {0: 2, 1: 4, 3: 5}

    def landed(step, kind):
        y, x, part = kinds[kind]
        place = block(step, y, x, part)
        if kind < 2:
            if step > 0:
                sem = z_recv.at[(step - 1) * 2 + part]
                pltpu.make_async_copy(place, place, sem).wait()
        else:
            pltpu.make_async_copy(place, place, pair_recv.at[step * 8 + kind]).wait()

    def pass_on(step, kind):
        y, x, part = kinds[kind]
        place = block(step, y, x, part)
        if kind in x_route:
            forward(place, place, (pair_send, pair_recv), step * 8 + x_route[kind], me.x_peer())
        if kind in y_route:
            forward(place, place, (pair_send, pair_recv), step * 8 + y_route[kind], me.y_peer())
        forward(place, place, (core_send, core_recv), step * 8 + kind, me.sibling())

    for turn in range(depth + 2):
        for step, group in ((turn, (0, 1)), (turn - 1, (2, 3)), (turn - 2, (4, 5, 6, 7))):
            if 0 <= step < depth:
                for kind in group:
                    landed(step, kind)
                    pass_on(step, kind)
    for step in range(depth):
        for kind in range(8):
            y, x, part = kinds[kind]
            place = block(step, y, x, part, 1 - me.c)
            pltpu.make_async_copy(place, place, core_recv.at[step * 8 + kind]).wait()
    for copy in started:
        copy.wait_send()


def gather_by_links(value_rows, ep_size):
    rows, width = value_rows.shape
    depth = ep_size // 2
    dma = pltpu.SemaphoreType.DMA
    every = pl.pallas_call(
        functools.partial(gather_kernel, ep_size),
        out_shape=jax.ShapeDtypeStruct((depth, 2, 2, 2, rows, width), value_rows.dtype),
        in_specs=[pl.BlockSpec(memory_space=pl.ANY)],
        out_specs=pl.BlockSpec(memory_space=pl.ANY),
        scratch_shapes=[
            dma,
            dma((2, 2 * depth - 2)),
            dma((2, 8 * depth)),
            dma((2, 8 * depth)),
        ],
        compiler_params=pltpu.CompilerParams(collective_id=1, has_side_effects=True),
        name="gather_by_links",
    )(value_rows)
    return every.reshape(-1, width)


def add_into(target, other):
    rows = target.shape[-2]

    def tile(i, carry):
        at = pl.ds(pl.multiple_of(i * 32, 32), 32)
        target[at, :] = target[at, :] + other[at, :]
        return carry

    lax.fori_loop(0, rows // 32, tile, 0)


def total_kernel(
    ep_size,
    first_in,
    second_in,
    small_in,
    first_out,
    second_out,
    small_out,
    parts,
    core_got,
    pair_got,
    last_got,
    z_got,
    small_got,
    load_sems,
    core_sems,
    pair_sems,
    last_sems,
    z_sems,
    small_sems,
    own_sem,
):
    me = Place(ep_size)
    depth = me.depth
    others = []
    for k in range(1, ep_size * 4):
        ep = lax.rem(lax.axis_index("ep") + k // 4, ep_size)
        tp = lax.rem(lax.axis_index("tp") + k % 4, 4)
        others.append((ep, tp))
    meet(others)
    small = []
    my_place = lax.axis_index("ep") * 4 + lax.axis_index("tp")
    for k, device in enumerate(others):
        small.append(
            send(
                small_in.at[device[0] * 4 + device[1]],
                small_got.at[my_place],
                small_sems.at[0, k],
                small_sems.at[1, k],
                device,
            )
        )
    own_small = pltpu.make_async_copy(small_in.at[my_place], small_got.at[my_place], own_sem)
    own_small.start()

    def load(step, which):
        source = (first_in, second_in)[which]
        slot = lax.rem(step, 2)
        return pltpu.make_async_copy(
            source.at[me.after(step + 1)], parts.at[slot, which], load_sems.at[slot, which]
        )

    def core_copy(step):
        return pltpu.make_async_remote_copy(
            src_ref=parts.at[lax.rem(step, 2), :, :, :, 1 - me.c],
            dst_ref=core_got.at[step],
            send_sem=core_sems.at[0, step],
            recv_sem=core_sems.at[1, step],
            device_id=me.sibling(),
            device_id_type=MESH,
        )

    def pair_copy(step, which):
        source = (core_got.at[step, 0, :, 1 - me.x], core_got.at[step, 1, 1 - me.y])[which]
        return pltpu.make_async_remote_copy(
            src_ref=source,
            dst_ref=pair_got.at[step, which],
            send_sem=pair_sems.at[0, step, which],
            recv_sem=pair_sems.at[1, step, which],
            device_id=(me.x_peer(), me.y_peer())[which],
            device_id_type=MESH,
        )

    def last_copy(step, which):
        return pltpu.make_async_remote_copy(
            src_ref=pair_got.at[step, which, (1 - me.y, 1 - me.x)[which]],
            dst_ref=last_got.at[step, which],
            send_sem=last_sems.at[0, step, which],
            recv_sem=last_sems.at[1, step, which],
            device_id=(me.y_peer(), me.x_peer())[which],
            device_id_type=MESH,
        )

    def z_copy(step):
        return pltpu.make_async_remote_copy(
            src_ref=last_got.at[step],
            dst_ref=z_got.at[step],
            send_sem=z_sems.at[0, step],
            recv_sem=z_sems.at[1, step],
            device_id=me.device(z=me.after(step + 1)),
            device_id_type=MESH,
        )

    def turn(i, carry):
        @pl.when(i < depth)
        def _():
            for which in range(2):
                load(i, which).start()
            for which in range(2):
                load(i, which).wait()
            core_copy(i).start()

        @pl.when((i >= 1) & (i <= depth))
        def _():
            step = i - 1
            core_copy(step).wait_recv()
            for y in range(2):
                for x in range(2):
                    for which in range(2):
                        add_into(
                            core_got.at[step, which, y, x],
                            parts.at[lax.rem(step, 2), which, y, x, me.c],
                        )
            for which in range(2):
                pair_copy(step, which).start()
            core_copy(step).wait_send()

        @pl.when((i >= 2) & (i <= depth + 1))
        def _():
            step = i - 2
            for which in range(2):
                pair_copy(step, which).wait_recv()
                for k in range(2):
                    mine = (core_got.at[step, 0, k, me.x], core_got.at[step, 1, me.y, k])[which]
                    add_into(pair_got.at[step, which, k], mine)
                last_copy(step, which).start()

        @pl.when(i >= 3)
        def _():
            step = i - 3
            for which in range(2):
                last_copy(step, which).wait_recv()
                add_into(last_got.at[step, which], pair_got.at[step, which, (me.y, me.x)[which]])

            @pl.when(step < depth - 1)
            def _():
                z_copy(step).start()

        return carry

    lax.fori_loop(0, depth + 3, turn, 0)
    for step in range(depth - 1):
        z_copy(step).wait_recv()

    def finish(which, target):
        def tile(i, carry):
            at = pl.ds(pl.multiple_of(i * 16, 16), 16)
            total = last_got[depth - 1, which, at, :].astype(jnp.float32)
            for step in range(depth - 1):
                total = total + z_got[step, which, at, :].astype(jnp.float32)
            target[at, :] = total
            return carry

        lax.fori_loop(0, target.shape[0] // 16, tile, 0)

    finish(0, first_out)
    finish(1, second_out)
    own_small.wait()
    for copy in small:
        copy.wait()
    for ep in range(ep_size):
        total = small_got[ep * 4]
        for tp in range(1, 4):
            total = total + small_got[ep * 4 + tp]
        small_out[ep] = total
    for step in range(depth):
        for which in range(2):
            pair_copy(step, which).wait_send()
            last_copy(step, which).wait_send()
        if step < depth - 1:
            z_copy(step).wait_send()


def totals_by_links(first, second, small, ep_size):
    total_rows, width = first.shape
    depth = ep_size // 2
    rows = total_rows // (4 * ep_size)
    whole = (depth, 2, 2, 2, rows, width)
    bf16, f32 = jnp.bfloat16, jnp.float32
    dma = pltpu.SemaphoreType.DMA
    vmem = pl.BlockSpec(memory_space=pltpu.VMEM)
    anywhere = pl.BlockSpec(memory_space=pl.ANY)
    return pl.pallas_call(
        functools.partial(total_kernel, ep_size),
        out_shape=(
            jax.ShapeDtypeStruct((rows, width), f32),
            jax.ShapeDtypeStruct((rows, width), f32),
            jax.ShapeDtypeStruct((ep_size,) + small.shape[1:], f32),
        ),
        in_specs=[anywhere, anywhere, vmem],
        out_specs=(vmem, vmem, vmem),
        scratch_shapes=[
            pltpu.VMEM((2, 2, 2, 2, 2, rows, width), bf16),
            pltpu.VMEM((depth, 2, 2, 2, rows, width), bf16),
            pltpu.VMEM((depth, 2, 2, rows, width), bf16),
            pltpu.VMEM((depth, 2, rows, width), bf16),
            pltpu.VMEM((depth - 1, 2, rows, width), bf16),
            pltpu.VMEM(small.shape, f32),
            dma((2, 2)),
            dma((2, depth)),
            dma((2, depth, 2)),
            dma((2, depth, 2)),
            dma((2, depth - 1)),
            dma((2, 4 * ep_size - 1)),
            dma,
        ],
        compiler_params=pltpu.CompilerParams(
            collective_id=2, has_side_effects=True, vmem_limit_bytes=56 * 1024 * 1024
        ),
        name="totals_by_links",
    )(first.reshape(whole), second.reshape(whole), small)


def gather_all(value_rows, by_links):
    if by_links:
        return gather_by_links(value_rows, lax.axis_size("ep"))
    return lax.all_gather(value_rows, ("ep", "tp"), axis=0, tiled=True)


def totals(first, second, small, by_links):
    ep_size, tp_size = lax.axis_size("ep"), lax.axis_size("tp")
    if by_links:
        rows = small.shape[1] // (ep_size * tp_size)
        blocks = small.reshape(small.shape[0], ep_size * tp_size, rows).swapaxes(0, 1)
        blocks = jnp.pad(blocks, ((0, 0), (0, -small.shape[0] % 8), (0, 0)))
        first, second, got = totals_by_links(first, second, blocks, ep_size)
        return first, second, got[:, : small.shape[0]].reshape(-1, rows).T

    def scatter(value_rows):
        return lax.psum_scatter(value_rows, ("ep", "tp"), scatter_dimension=0, tiled=True)

    columns = jnp.zeros((small.shape[1], small.shape[0] * ep_size), jnp.float32)
    columns = lax.dynamic_update_slice_in_dim(
        columns, small.T, lax.axis_index("ep") * small.shape[0], 1
    )
    return (
        scatter(first).astype(jnp.float32),
        scatter(second).astype(jnp.float32),
        scatter(columns),
    )


LAST = 1 << 30


def pair_order(expert_ids, slot_order, expert_count):
    experts = jnp.arange(expert_count, dtype=jnp.int32)
    chosen = expert_ids.T[None, :, :] == experts[:, None, None]
    return jnp.min(jnp.where(chosen, slot_order.T[None, :, :], LAST), axis=1)


def kept_pairs(order):
    used = order < LAST
    counts = jnp.sum(used.astype(jnp.int32), axis=2)
    block = jnp.arange(order.shape[0], dtype=jnp.int32)
    earlier = block[None, :] < block[:, None]
    offsets = jnp.sum(jnp.where(earlier[:, :, None], counts[None, :, :], 0), axis=1)
    whole = offsets + counts <= CAP
    edge = (offsets < CAP) & ~whole
    edge_order = jnp.sum(jnp.where(edge[:, :, None], order, 0), axis=0)
    rank = jnp.sum((edge_order[:, :, None] < edge_order[:, None, :]).astype(jnp.int32), axis=1)
    early = offsets[:, :, None] + rank[None, :, :] < CAP
    return used & (whole[:, :, None] | (edge[:, :, None] & early))


def masked_softmax(logits, used):
    top = jnp.max(jnp.where(used, logits, -jnp.inf), axis=-1, keepdims=True)
    powers = jnp.where(used, jnp.exp(logits - top), 0.0)
    return powers / jnp.sum(powers, axis=-1, keepdims=True)


def visible_block(query_seg, query_pos, query_row, key_seg, key_pos, key_row):
    seg_q = query_seg[:, None]
    seg_k = key_seg[None, :]
    above = (
        (seg_k == seg_q)
        | (seg_k == 0)
        | (seg_k >= 1) & (seg_k <= 4) & (seg_q >= 5) & ((seg_q - 5) // 2 + 1 == seg_k)
    )
    same_tree = query_row[:, None] // TREE_TOKENS == key_row[None, :] // TREE_TOKENS
    return above & same_tree & (key_pos[None, :] <= query_pos[:, None])


def block_scores(query_part, key_rows, allowed, scale):
    scores = (
        jnp.einsum("qkgd,pkd->kgqp", query_part, key_rows, preferred_element_type=jnp.float32)
        * scale
    )
    return jnp.where(allowed[None, None], scores, -1e30)


def attend_forward(query_rows, key_rows, value_rows, segment, position):
    total_rows = query_rows.shape[0]
    scale = query_rows.shape[-1] ** (-0.5)
    row_ids = jnp.arange(total_rows, dtype=jnp.int32)
    allowed = visible_block(segment, position, row_ids, segment, position, row_ids)
    scores = block_scores(query_rows, key_rows, allowed, scale)
    top_score = jnp.max(scores, axis=-1, keepdims=True)
    weights = jnp.exp(scores - top_score)
    weight_sum = jnp.sum(weights, axis=-1, keepdims=True)
    probs = (weights / weight_sum).astype(jnp.bfloat16)
    outputs = jnp.einsum(
        "kgqp,pkd->qkgd", probs, value_rows, preferred_element_type=jnp.float32
    ).astype(jnp.bfloat16)
    log_sums = [top_score + jnp.log(weight_sum)]
    return (outputs, log_sums)


def attend_backward(
    query_rows, key_rows, value_rows, segment, position, log_sums, grad_heads, block_rows
):
    total_rows = query_rows.shape[0]
    scale = query_rows.shape[-1] ** (-0.5)
    row_ids = jnp.arange(total_rows, dtype=jnp.int32)
    grad_keys = jnp.zeros(key_rows.shape, jnp.float32)
    grad_values = jnp.zeros(value_rows.shape, jnp.float32)
    grad_query = []
    for number, first_row in enumerate(range(0, total_rows, block_rows)):
        allowed = visible_block(segment, position, row_ids, segment, position, row_ids)
        scores = block_scores(query_rows, key_rows, allowed, scale)
        probs = jnp.where(allowed[None, None], jnp.exp(scores - log_sums[number]), 0.0)
        grad_values = jnp.einsum(
            "kgqp,qkgd->pkd",
            probs.astype(jnp.bfloat16),
            grad_heads,
            preferred_element_type=jnp.float32,
        )
        grad_probs = jnp.einsum(
            "qkgd,pkd->kgqp", grad_heads, value_rows, preferred_element_type=jnp.float32
        )
        inner = jnp.sum(probs * grad_probs, axis=-1, keepdims=True)
        grad_scores = (probs * (grad_probs - inner)).astype(jnp.bfloat16)
        grad_query.append(
            jnp.einsum("kgqp,pkd->qkgd", grad_scores, key_rows, preferred_element_type=jnp.float32)
            * scale
        )
        grad_keys = (
            jnp.einsum(
                "kgqp,qkgd->pkd", grad_scores, query_rows, preferred_element_type=jnp.float32
            )
            * scale
        )
    return (grad_query[0], grad_keys, grad_values)


def local(
    hidden_in,
    gain_attn,
    w_query,
    key_projection_weight,
    value_projection_weight,
    w_out,
    gain_ffn,
    w_router,
    w_gate,
    w_up,
    w_down,
    expert_ids,
    slot_order,
    segment,
    position,
    cotangent,
):
    model_width = w_query.shape[1]
    head_width = HEAD_DIMENSION
    local_heads = w_query.shape[0] // head_width
    local_kv = key_projection_weight.shape[0] // head_width
    group_factor = local_heads // local_kv
    token_count = expert_ids.shape[0]
    share = hidden_in.shape[0]
    row_start = lax.axis_index("tp") * share
    expert_count = w_router.shape[0]
    per_owner = w_gate.shape[0]
    block_rows = 512
    by_links = lax.axis_size("tp") == 4 and lax.axis_size("ep") == 8
    order = pair_order(expert_ids, slot_order, expert_count)
    order_all = lax.all_gather(order, "ep")
    cot_all = gather_all(cotangent, False)
    inputs_own = hidden_in.astype(jnp.float32)
    gain_one = gain_attn.astype(jnp.float32)
    gain_two = gain_ffn.astype(jnp.float32)
    scale_one = norm_scale(inputs_own)
    first_normalized = group_rows((inputs_own * scale_one * gain_one).astype(jnp.bfloat16))
    cosine_lookup, sine_lookup = rope_tables(position, head_width)
    query_proj = jnp.einsum(
        "rd,fd->rf", first_normalized, w_query, preferred_element_type=jnp.float32
    ).reshape(token_count, local_heads, head_width)
    key_proj = jnp.einsum(
        "rd,fd->rf", first_normalized, key_projection_weight, preferred_element_type=jnp.float32
    ).reshape(token_count, local_kv, head_width)
    query_rows = (
        apply_rotation(query_proj, cosine_lookup, sine_lookup)
        .astype(jnp.bfloat16)
        .reshape(token_count, local_kv, group_factor, head_width)
    )
    key_rows = apply_rotation(key_proj, cosine_lookup, sine_lookup).astype(jnp.bfloat16)
    value_rows = (
        jnp.einsum(
            "rd,fd->rf",
            first_normalized,
            value_projection_weight,
            preferred_element_type=jnp.float32,
        )
        .astype(jnp.bfloat16)
        .reshape(token_count, local_kv, head_width)
    )
    head_outputs, log_sums = attend_forward(query_rows, key_rows, value_rows, segment, position)
    head_outputs = head_outputs.reshape(token_count, local_heads * head_width)
    middle_own = inputs_own + group_totals(
        jnp.dot(head_outputs, w_out, preferred_element_type=jnp.float32)
    )
    scale_two = norm_scale(middle_own)
    normed_own = (middle_own * scale_two * gain_two).astype(jnp.bfloat16)
    normed_two = gather_all(normed_own, by_links)
    first_expert = lax.axis_index("ep") * per_owner
    used = lax.dynamic_slice_in_dim(order, row_start, share, 1).T < LAST
    gates = masked_softmax(
        jnp.einsum("rd,ed->re", normed_own, w_router, preferred_element_type=jnp.float32), used
    )
    kept_all = kept_pairs(
        lax.dynamic_slice_in_dim(order_all, first_expert, per_owner, 1)
    ).swapaxes(0, 1).reshape(per_owner, -1)
    all_gates = masked_softmax(
        jnp.einsum("rd,ed->re", normed_two, w_router, preferred_element_type=jnp.float32),
        order_all.swapaxes(1, 2).reshape(-1, expert_count) < LAST,
    )
    gate_all = jnp.where(
        kept_all.T, lax.dynamic_slice_in_dim(all_gates, first_expert, per_owner, 1), 0.0
    )
    units = w_gate.shape[2]
    gate_in = jnp.concatenate([w_gate[e] for e in range(per_owner)], axis=1)
    up_in = jnp.concatenate([w_up[e] for e in range(per_owner)], axis=1)
    down_in = w_down.reshape(per_owner * units, model_width)
    spread = jnp.repeat(gate_all, units, axis=1)
    gate_act = jnp.dot(normed_two, gate_in, preferred_element_type=jnp.float32)
    up_act = jnp.dot(normed_two, up_in, preferred_element_type=jnp.float32)
    back_act = jnp.einsum("rd,fd->rf", cot_all, down_in, preferred_element_type=jnp.float32)
    sigma = jax.nn.sigmoid(gate_act)
    hidden = gate_act * sigma * up_act
    weighted_hidden = (spread * hidden).astype(jnp.bfloat16)
    grad_hidden = spread * back_act
    grad_gate_act = (grad_hidden * up_act * sigma * (1.0 + gate_act * (1.0 - sigma))).astype(
        jnp.bfloat16
    )
    grad_up_act = (grad_hidden * gate_act * sigma).astype(jnp.bfloat16)
    grad_gates_part = jnp.where(
        kept_all, jnp.sum((hidden * back_act).reshape(-1, per_owner, units), axis=2).T, 0.0
    )
    grad_rows = (
        jnp.einsum("rf,df->rd", grad_gate_act, gate_in, preferred_element_type=jnp.float32)
        + jnp.einsum("rf,df->rd", grad_up_act, up_in, preferred_element_type=jnp.float32)
    ).astype(jnp.bfloat16)
    combined = jnp.dot(weighted_hidden, down_in, preferred_element_type=jnp.float32).astype(
        jnp.bfloat16
    )
    grad_normed_own, combined_own, grad_gates_own = totals(
        grad_rows, combined, grad_gates_part, by_links
    )
    output_own = (middle_own + combined_own).astype(jnp.bfloat16)
    grad_w_gate = jnp.einsum(
        "rd,ref->edf",
        normed_two,
        grad_gate_act.reshape(-1, per_owner, units),
        preferred_element_type=jnp.float32,
    )
    grad_w_up = jnp.einsum(
        "rd,ref->edf",
        normed_two,
        grad_up_act.reshape(-1, per_owner, units),
        preferred_element_type=jnp.float32,
    )
    grad_w_down = jnp.einsum(
        "rf,rd->fd", weighted_hidden, cot_all, preferred_element_type=jnp.float32
    ).reshape(per_owner, units, model_width)
    inner_gate = jnp.sum(gates * grad_gates_own, axis=-1, keepdims=True)
    grad_logits = gates * (grad_gates_own - inner_gate)
    router_f = w_router.astype(jnp.float32)
    grad_normed_own = grad_normed_own + jnp.dot(grad_logits, router_f, precision=EXACT_PRECISION)
    grad_router = jnp.dot(grad_logits.T, normed_own.astype(jnp.float32), precision=EXACT_PRECISION)
    grad_middle_back, grad_gain_ffn = norm_back(middle_own, scale_two, gain_two, grad_normed_own)
    grad_middle = cotangent.astype(jnp.float32) + grad_middle_back
    grad_attn = group_rows(grad_middle.astype(jnp.bfloat16))
    grad_w_out = jnp.einsum(
        "rf,rd->fd", head_outputs, grad_attn, preferred_element_type=jnp.float32
    )
    grad_heads = (
        jnp.einsum("rd,fd->rf", grad_attn, w_out, preferred_element_type=jnp.float32)
        .astype(jnp.bfloat16)
        .reshape(token_count, local_kv, group_factor, head_width)
    )
    grad_query, grad_keys, grad_values = attend_backward(
        query_rows, key_rows, value_rows, segment, position, log_sums, grad_heads, block_rows
    )
    grad_query_proj = (
        rotate_back(
            grad_query.reshape(token_count, local_heads, head_width), cosine_lookup, sine_lookup
        )
        .astype(jnp.bfloat16)
        .reshape(token_count, local_heads * head_width)
    )
    grad_key_proj = (
        rotate_back(grad_keys, cosine_lookup, sine_lookup)
        .astype(jnp.bfloat16)
        .reshape(token_count, local_kv * head_width)
    )
    grad_value_proj = grad_values.astype(jnp.bfloat16).reshape(token_count, local_kv * head_width)
    grad_w_query = jnp.einsum(
        "rf,rd->fd", grad_query_proj, first_normalized, preferred_element_type=jnp.float32
    )
    grad_w_key = jnp.einsum(
        "rf,rd->fd", grad_key_proj, first_normalized, preferred_element_type=jnp.float32
    )
    grad_w_value = jnp.einsum(
        "rf,rd->fd", grad_value_proj, first_normalized, preferred_element_type=jnp.float32
    )
    grad_normed_one = jnp.einsum(
        "rf,fd->rd", grad_query_proj, w_query, preferred_element_type=jnp.float32
    )
    grad_normed_one = grad_normed_one + jnp.einsum(
        "rf,fd->rd", grad_key_proj, key_projection_weight, preferred_element_type=jnp.float32
    )
    grad_normed_one = grad_normed_one + jnp.einsum(
        "rf,fd->rd", grad_value_proj, value_projection_weight, preferred_element_type=jnp.float32
    )
    grad_one_own = group_totals(grad_normed_one)
    grad_inputs_back, grad_gain_attn = norm_back(inputs_own, scale_one, gain_one, grad_one_own)
    grad_input = grad_middle + grad_inputs_back
    grad_w_query, grad_w_key, grad_w_value, grad_w_out = (
        lax.psum(grad_w_query.astype(jnp.bfloat16), "ep").astype(jnp.float32),
        lax.psum(grad_w_key.astype(jnp.bfloat16), "ep").astype(jnp.float32),
        lax.psum(grad_w_value.astype(jnp.bfloat16), "ep").astype(jnp.float32),
        lax.psum(grad_w_out.astype(jnp.bfloat16), "ep").astype(jnp.float32),
    )
    grad_gain_attn, grad_gain_ffn, grad_router = lax.psum(
        (grad_gain_attn, grad_gain_ffn, grad_router), ("ep", "tp")
    )
    return (
        output_own,
        grad_input,
        grad_gain_attn,
        grad_w_query,
        grad_w_key,
        grad_w_value,
        grad_w_out,
        grad_gain_ffn,
        grad_router,
        grad_w_gate,
        grad_w_up,
        grad_w_down,
    )


def solution(mesh):
    placed = (
        P(("ep", "tp"), None),
        P(),
        P("tp", None),
        P("tp", None),
        P("tp", None),
        P("tp", None),
        P(),
        P(),
        P("ep", None, "tp"),
        P("ep", None, "tp"),
        P("ep", "tp", None),
        P("ep", None),
        P("ep", None),
        P("ep"),
        P("ep"),
        P(("ep", "tp"), None),
    )
    return jax.shard_map(
        local,
        mesh=mesh,
        in_specs=placed,
        out_specs=(
            P(("ep", "tp"), None),
            P(("ep", "tp"), None),
            P(),
            P("tp", None),
            P("tp", None),
            P("tp", None),
            P("tp", None),
            P(),
            P(),
            P("ep", None, "tp"),
            P("ep", None, "tp"),
            P("ep", "tp", None),
        ),
        check_vma=False,
    )
```

```python
import functools

import jax
import jax.numpy as jnp
from jax import lax
from jax.experimental import pallas as pl
from jax.experimental.pallas import tpu as pltpu
from jax.sharding import PartitionSpec as P

HEAD_DIMENSION = 64
TREE_TOKENS = 512
CAP = 2304


EPSILON = 1e-06
ROPE_BASE = 10000.0
EXACT_PRECISION = lax.Precision.HIGHEST


def rope_tables(position, head_width):
    half_width = head_width // 2
    freqs = ROPE_BASE ** (-(jnp.arange(half_width, dtype=jnp.float32) * 2.0 / head_width))
    angle = position.astype(jnp.float32)[:, None] * freqs[None, :]
    return (jnp.cos(angle)[:, None, :], jnp.sin(angle)[:, None, :])


def apply_rotation(value_rows, cosine_lookup, sine_lookup):
    half_width = value_rows.shape[-1] // 2
    first = value_rows[..., :half_width]
    second = value_rows[..., half_width:]
    return jnp.concatenate(
        [
            first * cosine_lookup - second * sine_lookup,
            first * sine_lookup + second * cosine_lookup,
        ],
        axis=-1,
    )


def rotate_back(grads, cosine_lookup, sine_lookup):
    half_width = grads.shape[-1] // 2
    first = grads[..., :half_width]
    second = grads[..., half_width:]
    return jnp.concatenate(
        [
            first * cosine_lookup + second * sine_lookup,
            second * cosine_lookup - first * sine_lookup,
        ],
        axis=-1,
    )


def norm_scale(value_rows):
    return lax.rsqrt(jnp.mean(value_rows * value_rows, axis=-1, keepdims=True) + EPSILON)


def norm_back(value_rows, scale, gain, grad_normed):
    weighted = grad_normed * gain
    inner = jnp.mean(value_rows * weighted, axis=-1, keepdims=True)
    grad_values = scale * weighted - value_rows * (scale * scale * scale) * inner
    return grad_values


MESH = pl.DeviceIdType.MESH


class Place:
    def __init__(self, ep_size):
        self.depth = ep_size // 2
        ep, tp = lax.axis_index("ep"), lax.axis_index("tp")
        self.z, self.y = ep // 2, ep % 2
        self.x, self.c = tp // 2, tp % 2

    def device(self, z=None, y=None, x=None, c=None):
        z = self.z if z is None else z
        y = self.y if y is None else y
        x = self.x if x is None else x
        c = self.c if c is None else c
        return (z * 2 + y, x * 2 + c)

    def sibling(self):
        return self.device(c=1 - self.c)

    def x_peer(self):
        return self.device(x=1 - self.x)

    def y_peer(self):
        return self.device(y=1 - self.y)

    def after(self, step):
        return lax.rem(self.z + step, self.depth)

    def before(self, step):
        return lax.rem(self.z + self.depth - step, self.depth)


def meet(devices):
    barrier = pltpu.get_barrier_semaphore()
    for device in devices:
        pl.semaphore_signal(barrier, inc=1, device_id=device, device_id_type=MESH)
    pl.semaphore_wait(barrier, len(devices))


def send(src, dst, send_sem, recv_sem, device):
    copy = pltpu.make_async_remote_copy(
        src_ref=src,
        dst_ref=dst,
        send_sem=send_sem,
        recv_sem=recv_sem,
        device_id=device,
        device_id_type=MESH,
    )
    copy.start()
    return copy


def gather_kernel(ep_size, own, out, own_sem, z_sems, pair_sems, core_sems):
    me = Place(ep_size)
    depth = me.depth
    half = own.shape[0] // 2
    z_send, z_recv = z_sems.at[0], z_sems.at[1]
    pair_send, pair_recv = pair_sems.at[0], pair_sems.at[1]
    core_send, core_recv = core_sems.at[0], core_sems.at[1]
    meet(
        [me.sibling(), me.x_peer(), me.y_peer()]
        + [me.device(z=me.after(s)) for s in range(1, depth)]
    )

    def rows(part):
        return pl.ds(part * half, half)

    def block(step, y, x, part, c=None):
        return out.at[me.before(step), y, x, me.c if c is None else c, rows(part)]

    started = []

    def forward(source, target, sems, slot, device):
        started.append(send(source, target, sems[0].at[slot], sems[1].at[slot], device))

    for s in range(1, depth):
        for part in range(2):
            forward(
                own.at[rows(part)],
                out.at[me.z, me.y, me.x, me.c, rows(part)],
                (z_send, z_recv),
                (s - 1) * 2 + part,
                me.device(z=me.after(s)),
            )
    local = pltpu.make_async_copy(own, out.at[me.z, me.y, me.x, me.c], own_sem)
    local.start()
    local.wait()

    kinds = [
        (me.y, me.x, 0),
        (me.y, me.x, 1),
        (1 - me.y, me.x, 0),
        (me.y, 1 - me.x, 1),
        (1 - me.y, me.x, 1),
        (1 - me.y, 1 - me.x, 1),
        (me.y, 1 - me.x, 0),
        (1 - me.y, 1 - me.x, 0),
    ]
    x_route = {0: 6, 2: 7, 1: 3}
    y_route = {0: 2, 1: 4, 3: 5}

    def landed(step, kind):
        y, x, part = kinds[kind]
        place = block(step, y, x, part)
        if kind < 2:
            if step > 0:
                sem = z_recv.at[(step - 1) * 2 + part]
                pltpu.make_async_copy(place, place, sem).wait()
        else:
            pltpu.make_async_copy(place, place, pair_recv.at[step * 8 + kind]).wait()

    def pass_on(step, kind):
        y, x, part = kinds[kind]
        place = block(step, y, x, part)
        if kind in x_route:
            forward(place, place, (pair_send, pair_recv), step * 8 + x_route[kind], me.x_peer())
        if kind in y_route:
            forward(place, place, (pair_send, pair_recv), step * 8 + y_route[kind], me.y_peer())
        forward(place, place, (core_send, core_recv), step * 8 + kind, me.sibling())

    for turn in range(depth + 2):
        for step, group in ((turn, (0, 1)), (turn - 1, (2, 3)), (turn - 2, (4, 5, 6, 7))):
            if 0 <= step < depth:
                for kind in group:
                    landed(step, kind)
                    pass_on(step, kind)
    for step in range(depth):
        for kind in range(8):
            y, x, part = kinds[kind]
            place = block(step, y, x, part, 1 - me.c)
            pltpu.make_async_copy(place, place, core_recv.at[step * 8 + kind]).wait()
    for copy in started:
        copy.wait_send()


def gather_by_links(value_rows, ep_size):
    rows, width = value_rows.shape
    depth = ep_size // 2
    dma = pltpu.SemaphoreType.DMA
    every = pl.pallas_call(
        functools.partial(gather_kernel, ep_size),
        out_shape=jax.ShapeDtypeStruct((depth, 2, 2, 2, rows, width), value_rows.dtype),
        in_specs=[pl.BlockSpec(memory_space=pl.ANY)],
        out_specs=pl.BlockSpec(memory_space=pl.ANY),
        scratch_shapes=[
            dma,
            dma((2, 2 * depth - 2)),
            dma((2, 8 * depth)),
            dma((2, 8 * depth)),
        ],
        compiler_params=pltpu.CompilerParams(collective_id=1, has_side_effects=True),
        name="gather_by_links",
    )(value_rows)
    return every.reshape(-1, width)


def add_into(target, other):
    def tile(i, carry):
        at = pl.ds(pl.multiple_of(i * 16, 16), 16)
        target[at, :] = target[at, :] + other[at, :]
        return carry

    lax.fori_loop(0, target.shape[0] // 16, tile, 0)


def total_kernel(
    ep_size,
    first_in,
    second_in,
    small_in,
    first_out,
    second_out,
    small_out,
    parts,
    core_got,
    pair_got,
    last_got,
    z_got,
    small_got,
    load_sems,
    core_sems,
    pair_sems,
    last_sems,
    z_sems,
    small_sems,
    own_sem,
):
    me = Place(ep_size)
    depth = me.depth
    others = all_others(ep_size)
    meet(others)
    small = []
    my_place = lax.axis_index("ep") * 4 + lax.axis_index("tp")
    for k, device in enumerate(others):
        small.append(
            send(
                small_in.at[device[0] * 4 + device[1]],
                small_got.at[my_place],
                small_sems.at[0, k],
                small_sems.at[1, k],
                device,
            )
        )
    own_small = pltpu.make_async_copy(small_in.at[my_place], small_got.at[my_place], own_sem)
    own_small.start()

    def load(step, which):
        source = (first_in, second_in)[which]
        slot = lax.rem(step, 2)
        return pltpu.make_async_copy(
            source.at[me.after(step + 1)], parts.at[slot, which], load_sems.at[slot, which]
        )

    def core_copy(step):
        return pltpu.make_async_remote_copy(
            src_ref=parts.at[lax.rem(step, 2), :, :, :, 1 - me.c],
            dst_ref=core_got.at[step],
            send_sem=core_sems.at[0, step],
            recv_sem=core_sems.at[1, step],
            device_id=me.sibling(),
            device_id_type=MESH,
        )

    def pair_copy(step, which):
        source = (core_got.at[step, 0, :, 1 - me.x], core_got.at[step, 1, 1 - me.y])[which]
        return pltpu.make_async_remote_copy(
            src_ref=source,
            dst_ref=pair_got.at[step, which],
            send_sem=pair_sems.at[0, step, which],
            recv_sem=pair_sems.at[1, step, which],
            device_id=(me.x_peer(), me.y_peer())[which],
            device_id_type=MESH,
        )

    def last_copy(step, which):
        return pltpu.make_async_remote_copy(
            src_ref=pair_got.at[step, which, (1 - me.y, 1 - me.x)[which]],
            dst_ref=last_got.at[step, which],
            send_sem=last_sems.at[0, step, which],
            recv_sem=last_sems.at[1, step, which],
            device_id=(me.y_peer(), me.x_peer())[which],
            device_id_type=MESH,
        )

    def z_copy(step):
        return pltpu.make_async_remote_copy(
            src_ref=last_got.at[step],
            dst_ref=z_got.at[step],
            send_sem=z_sems.at[0, step],
            recv_sem=z_sems.at[1, step],
            device_id=me.device(z=me.after(step + 1)),
            device_id_type=MESH,
        )

    def turn(i, carry):
        @pl.when(i < depth)
        def _():
            for which in range(2):
                load(i, which).start()
            for which in range(2):
                load(i, which).wait()
            core_copy(i).start()

        @pl.when((i >= 1) & (i <= depth))
        def _():
            step = i - 1
            core_copy(step).wait_recv()
            for y in range(2):
                for x in range(2):
                    for which in range(2):
                        add_into(
                            core_got.at[step, which, y, x],
                            parts.at[lax.rem(step, 2), which, y, x, me.c],
                        )
            for which in range(2):
                pair_copy(step, which).start()
            core_copy(step).wait_send()

        @pl.when((i >= 2) & (i <= depth + 1))
        def _():
            step = i - 2
            for which in range(2):
                pair_copy(step, which).wait_recv()
                for k in range(2):
                    mine = (core_got.at[step, 0, k, me.x], core_got.at[step, 1, me.y, k])[which]
                    add_into(pair_got.at[step, which, k], mine)
                last_copy(step, which).start()

        @pl.when(i >= 3)
        def _():
            step = i - 3
            for which in range(2):
                last_copy(step, which).wait_recv()
                add_into(last_got.at[step, which], pair_got.at[step, which, (me.y, me.x)[which]])

            @pl.when(step < depth - 1)
            def _():
                z_copy(step).start()

        return carry

    lax.fori_loop(0, depth + 3, turn, 0)
    for step in range(depth - 1):
        z_copy(step).wait_recv()

    def finish(which, target):
        def tile(i, carry):
            at = pl.ds(pl.multiple_of(i * 16, 16), 16)
            total = last_got[depth - 1, which, at, :].astype(jnp.float32)
            for step in range(depth - 1):
                total = total + z_got[step, which, at, :].astype(jnp.float32)
            target[at, :] = total
            return carry

        lax.fori_loop(0, target.shape[0] // 16, tile, 0)

    finish(0, first_out)
    finish(1, second_out)
    own_small.wait()
    for copy in small:
        copy.wait()
    for ep in range(ep_size):
        total = small_got[ep * 4]
        for tp in range(1, 4):
            total = total + small_got[ep * 4 + tp]
        small_out[ep] = total
    for step in range(depth):
        for which in range(2):
            pair_copy(step, which).wait_send()
            last_copy(step, which).wait_send()
        if step < depth - 1:
            z_copy(step).wait_send()


def totals_by_links(first, second, small, ep_size):
    total_rows, width = first.shape
    depth = ep_size // 2
    rows = total_rows // (4 * ep_size)
    whole = (depth, 2, 2, 2, rows, width)
    bf16, f32 = jnp.bfloat16, jnp.float32
    dma = pltpu.SemaphoreType.DMA
    vmem = pl.BlockSpec(memory_space=pltpu.VMEM)
    anywhere = pl.BlockSpec(memory_space=pl.ANY)
    return pl.pallas_call(
        functools.partial(total_kernel, ep_size),
        out_shape=(
            jax.ShapeDtypeStruct((rows, width), f32),
            jax.ShapeDtypeStruct((rows, width), f32),
            jax.ShapeDtypeStruct((ep_size,) + small.shape[1:], f32),
        ),
        in_specs=[anywhere, anywhere, vmem],
        out_specs=(vmem, vmem, vmem),
        scratch_shapes=[
            pltpu.VMEM((2, 2, 2, 2, 2, rows, width), bf16),
            pltpu.VMEM((depth, 2, 2, 2, rows, width), bf16),
            pltpu.VMEM((depth, 2, 2, rows, width), bf16),
            pltpu.VMEM((depth, 2, rows, width), bf16),
            pltpu.VMEM((depth - 1, 2, rows, width), bf16),
            pltpu.VMEM(small.shape, f32),
            dma((2, 2)),
            dma((2, depth)),
            dma((2, depth, 2)),
            dma((2, depth, 2)),
            dma((2, depth - 1)),
            dma((2, 4 * ep_size - 1)),
            dma,
        ],
        compiler_params=pltpu.CompilerParams(
            collective_id=2, has_side_effects=True, vmem_limit_bytes=56 * 1024 * 1024
        ),
        name="totals_by_links",
    )(first.reshape(whole), second.reshape(whole), small)


def group_gather_kernel(ep_size, pieces, own, out, own_sem, sems):
    me = Place(ep_size)
    size = own.shape[0] // pieces
    meet([me.sibling(), me.x_peer()])
    started = []
    local = pltpu.make_async_copy(own, out.at[me.x, me.c], own_sem)
    local.start()

    def at(p):
        return pl.ds(p * size, size)

    def go(kind, p, src, dst, device):
        slot = kind * pieces + p
        started.append(send(src, dst, sems.at[0, slot], sems.at[1, slot], device))

    for p in range(pieces):
        go(0, p, own.at[at(p)], out.at[me.x, me.c, at(p)], me.x_peer())
    for p in range(pieces):
        go(1, p, own.at[at(p)], out.at[me.x, me.c, at(p)], me.sibling())
    for p in range(pieces):
        block = out.at[1 - me.x, me.c, at(p)]
        pltpu.make_async_copy(block, block, sems.at[1, p]).wait()
        go(2, p, block, block, me.sibling())
    for p in range(pieces):
        for kind, x in ((1, me.x), (2, 1 - me.x)):
            block = out.at[x, 1 - me.c, at(p)]
            pltpu.make_async_copy(block, block, sems.at[1, kind * pieces + p]).wait()
    local.wait()
    for copy in started:
        copy.wait_send()


def group_gather(value_rows, ep_size, call):
    rows, width = value_rows.shape
    pieces = 4
    dma = pltpu.SemaphoreType.DMA
    every = pl.pallas_call(
        functools.partial(group_gather_kernel, ep_size, pieces),
        out_shape=jax.ShapeDtypeStruct((2, 2, rows, width), value_rows.dtype),
        in_specs=[pl.BlockSpec(memory_space=pl.ANY)],
        out_specs=pl.BlockSpec(memory_space=pl.ANY),
        scratch_shapes=[dma, dma((2, 3 * pieces))],
        compiler_params=pltpu.CompilerParams(collective_id=call, has_side_effects=True),
        name="group_gather",
    )(value_rows)
    return every.reshape(-1, width)


class GroupTotal:
    def __init__(self, me, parts, core_got, pair_got, sems):
        self.me, self.parts, self.core_got, self.pair_got = me, parts, core_got, pair_got
        self.core = [
            pltpu.make_async_remote_copy(
                src_ref=parts.at[x, 1 - me.c],
                dst_ref=core_got.at[x],
                send_sem=sems.at[0, k],
                recv_sem=sems.at[1, k],
                device_id=me.sibling(),
                device_id_type=MESH,
            )
            for k, x in enumerate((1 - me.x, me.x))
        ]
        self.pair = pltpu.make_async_remote_copy(
            src_ref=core_got.at[1 - me.x],
            dst_ref=pair_got,
            send_sem=sems.at[0, 2],
            recv_sem=sems.at[1, 2],
            device_id=me.x_peer(),
            device_id_type=MESH,
        )

    def begin(self):
        for copy in self.core:
            copy.start()

    def exchange(self):
        self.core[0].wait_recv()
        far = 1 - self.me.x
        add_into(self.core_got.at[far], self.parts.at[far, self.me.c])
        self.pair.start()

    def finish(self, out):
        self.core[1].wait_recv()
        self.pair.wait_recv()

        def tile(i, carry):
            at = pl.ds(pl.multiple_of(i * 16, 16), 16)
            out[at, :] = (
                self.parts[self.me.x, self.me.c, at, :].astype(jnp.float32)
                + self.core_got[self.me.x, at, :].astype(jnp.float32)
                + self.pair_got[at, :].astype(jnp.float32)
            )
            return carry

        lax.fori_loop(0, out.shape[0] // 16, tile, 0)

    def sent(self):
        for copy in self.core + [self.pair]:
            copy.wait_send()


def group_total_kernel(ep_size, parts, out, core_got, pair_got, sems):
    me = Place(ep_size)
    meet([me.sibling(), me.x_peer()])
    total = GroupTotal(me, parts, core_got, pair_got, sems)
    total.begin()
    total.exchange()
    total.finish(out)
    total.sent()


def group_total(value_rows, ep_size, call):
    rows, width = value_rows.shape[0] // 4, value_rows.shape[1]
    vmem = pl.BlockSpec(memory_space=pltpu.VMEM)
    return pl.pallas_call(
        functools.partial(group_total_kernel, ep_size),
        out_shape=jax.ShapeDtypeStruct((rows, width), jnp.float32),
        in_specs=[vmem],
        out_specs=vmem,
        scratch_shapes=[
            pltpu.VMEM((2, rows, width), jnp.bfloat16),
            pltpu.VMEM((rows, width), jnp.bfloat16),
            pltpu.SemaphoreType.DMA((2, 3)),
        ],
        compiler_params=pltpu.CompilerParams(
            collective_id=call, has_side_effects=True, vmem_limit_bytes=32 * 1024 * 1024
        ),
        name="group_total",
    )(value_rows.reshape(2, 2, rows, width))


def all_others(ep_size):
    ep, tp = lax.axis_index("ep"), lax.axis_index("tp")
    return [
        (lax.rem(ep + k // 4, ep_size), lax.rem(tp + k % 4, 4)) for k in range(1, ep_size * 4)
    ]


def tail_kernel(
    ep_size,
    counts,
    *refs,
):
    n = len(counts)
    grads, rows_in, small_in = refs[:n], refs[n], refs[n + 1]
    outs, rows_out, small_out = refs[n + 2 : 2 * n + 2], refs[2 * n + 2], refs[2 * n + 3]
    (
        y_got,
        z_got,
        final,
        core_got,
        pair_got,
        small_got,
        small_sum,
        y_sems,
        z_sems,
        fz_sems,
        fy_sems,
        group_sems,
        small_sems,
        spread_sems,
        own_sem,
    ) = refs[2 * n + 4 :]
    me = Place(ep_size)
    depth = me.depth
    starts = [sum(counts[:i]) for i in range(n)]
    others = all_others(ep_size)
    meet(others)
    my_place = lax.axis_index("ep") * 4 + lax.axis_index("tp")

    def y_copy(step, i):
        return pltpu.make_async_remote_copy(
            src_ref=grads[i].at[me.after(step + 1), 1 - me.y],
            dst_ref=y_got.at[step, pl.ds(starts[i], counts[i])],
            send_sem=y_sems.at[0, step, i],
            recv_sem=y_sems.at[1, step, i],
            device_id=me.y_peer(),
            device_id_type=MESH,
        )

    def z_copy(step):
        return pltpu.make_async_remote_copy(
            src_ref=y_got.at[step],
            dst_ref=z_got.at[step],
            send_sem=z_sems.at[0, step],
            recv_sem=z_sems.at[1, step],
            device_id=me.device(z=me.after(step + 1)),
            device_id_type=MESH,
        )

    for step in range(depth):
        for i in range(n):
            y_copy(step, i).start()
    group = GroupTotal(me, rows_in, core_got, pair_got, group_sems)
    group.begin()
    small = [
        send(
            small_in.at[device[0] * 4 + device[1]],
            small_got.at[my_place],
            small_sems.at[0, k],
            small_sems.at[1, k],
            device,
        )
        for k, device in enumerate(others)
    ]
    own_small = pltpu.make_async_copy(small_in.at[my_place], small_got.at[my_place], own_sem)
    own_small.start()
    group.exchange()

    def y_sum(step):
        for i in range(n):
            y_copy(step, i).wait_recv()
            add_into(
                y_got.at[step, pl.ds(starts[i], counts[i])],
                grads[i].at[me.after(step + 1), me.y],
            )

    for step in range(depth - 1):
        y_sum(step)
        z_copy(step).start()
    own_small.wait()
    for copy in small:
        copy.wait_recv()
    total = small_got[0]
    for k in range(1, 4 * ep_size):
        total = total + small_got[k]
    small_sum[...] = total
    spread = [
        send(
            small_sum,
            small_out.at[my_place],
            spread_sems.at[0, k],
            spread_sems.at[1, k],
            device,
        )
        for k, device in enumerate(others)
    ]
    small_out[my_place] = total
    group.finish(rows_out)
    y_sum(depth - 1)
    for step in range(depth - 1):
        z_copy(step).wait_recv()

    def tile(i, carry):
        at = pl.ds(pl.multiple_of(i * 16, 16), 16)
        value = y_got[depth - 1, at, :].astype(jnp.float32)
        for step in range(depth - 1):
            value = value + z_got[step, at, :].astype(jnp.float32)
        final[me.z, me.y, at, :] = value.astype(final.dtype)
        return carry

    lax.fori_loop(0, sum(counts) // 16, tile, 0)
    mine = final.at[me.z, me.y]
    finals = []
    for s in range(1, depth):
        finals.append(
            send(mine, mine, fz_sems.at[0, s], fz_sems.at[1, s], me.device(z=me.after(s)))
        )
    finals.append(send(mine, mine, fy_sems.at[0, 0], fy_sems.at[1, 0], me.y_peer()))
    for s in range(1, depth):
        block = final.at[me.before(s), me.y]
        pltpu.make_async_copy(block, block, fz_sems.at[1, s]).wait()
        finals.append(send(block, block, fy_sems.at[0, s], fy_sems.at[1, s], me.y_peer()))

    def deliver(s, y):
        z = me.before(s)
        for i in range(n):

            def tile(t, carry):
                at = pl.multiple_of(t * 16, 16)
                outs[i][z, y, pl.ds(at, 16), :] = final[
                    z, y, pl.ds(starts[i] + at, 16), :
                ].astype(jnp.float32)
                return carry

            lax.fori_loop(0, counts[i] // 16, tile, 0)

    for s in range(depth):
        deliver(s, me.y)
    for s in range(depth):
        block = final.at[me.before(s), 1 - me.y]
        pltpu.make_async_copy(block, block, fy_sems.at[1, s]).wait()
        deliver(s, 1 - me.y)
    for copy in spread:
        copy.wait()
    for copy in small + finals:
        copy.wait_send()
    group.sent()
    for step in range(depth):
        for i in range(n):
            y_copy(step, i).wait_send()
        if step < depth - 1:
            z_copy(step).wait_send()


def tail_by_links(grads, rows_part, small, ep_size):
    width = rows_part.shape[1]
    depth = ep_size // 2
    rows = rows_part.shape[0] // 4
    counts = [g.shape[0] // ep_size for g in grads]
    total = sum(counts)
    places = 4 * ep_size
    bf16, f32 = jnp.bfloat16, jnp.float32
    dma = pltpu.SemaphoreType.DMA
    vmem = pl.BlockSpec(memory_space=pltpu.VMEM)
    lanes = width // 128
    blocks = jnp.pad(small, ((0, places - small.shape[0]), (0, 0))).reshape(places, lanes, 128)
    got = pl.pallas_call(
        functools.partial(tail_kernel, ep_size, counts),
        out_shape=tuple(jax.ShapeDtypeStruct((depth, 2, k, width), f32) for k in counts)
        + (
            jax.ShapeDtypeStruct((rows, width), f32),
            jax.ShapeDtypeStruct(blocks.shape, f32),
        ),
        in_specs=[vmem] * (len(grads) + 2),
        out_specs=(vmem,) * (len(grads) + 2),
        scratch_shapes=[
            pltpu.VMEM((depth, total, width), bf16),
            pltpu.VMEM((depth - 1, total, width), bf16),
            pltpu.VMEM((depth, 2, total, width), bf16),
            pltpu.VMEM((2, rows, width), bf16),
            pltpu.VMEM((rows, width), bf16),
            pltpu.VMEM(blocks.shape, f32),
            pltpu.VMEM(blocks.shape[1:], f32),
            dma((2, depth, len(grads))),
            dma((2, depth)),
            dma((2, depth)),
            dma((2, depth)),
            dma((2, 3)),
            dma((2, places - 1)),
            dma((2, places - 1)),
            dma,
        ],
        compiler_params=pltpu.CompilerParams(
            collective_id=5, has_side_effects=True, vmem_limit_bytes=56 * 1024 * 1024
        ),
        name="tail_by_links",
    )(
        *[g.reshape(depth, 2, k, width) for g, k in zip(grads, counts)],
        rows_part.reshape(2, 2, rows, width),
        blocks,
    )
    sums = [g.reshape(-1, width) for g in got[: len(grads)]]
    return sums, got[-2], got[-1].reshape(places, width)[: small.shape[0]]


def group_rows(value_rows, by_links, call):
    if by_links:
        return group_gather(value_rows, lax.axis_size("ep"), call)
    return lax.all_gather(value_rows, "tp", axis=0, tiled=True)


def group_totals(value_rows, by_links, call):
    if by_links:
        return group_total(value_rows, lax.axis_size("ep"), call)
    return lax.psum_scatter(value_rows, "tp", scatter_dimension=0, tiled=True).astype(jnp.float32)


def tail_totals(grads, rows_part, small, by_links):
    if by_links:
        return tail_by_links(grads, rows_part, small, lax.axis_size("ep"))
    sums = [lax.psum(g, "ep").astype(jnp.float32) for g in grads]
    return sums, group_totals(rows_part, by_links, None), lax.psum(small, ("ep", "tp"))


def gather_all(value_rows, by_links):
    if by_links:
        return gather_by_links(value_rows, lax.axis_size("ep"))
    return lax.all_gather(value_rows, ("ep", "tp"), axis=0, tiled=True)


def totals(first, second, small, by_links):
    ep_size, tp_size = lax.axis_size("ep"), lax.axis_size("tp")
    if by_links:
        rows = small.shape[1] // (ep_size * tp_size)
        blocks = small.reshape(small.shape[0], ep_size * tp_size, rows).swapaxes(0, 1)
        blocks = jnp.pad(blocks, ((0, 0), (0, -small.shape[0] % 8), (0, 0)))
        first, second, got = totals_by_links(first, second, blocks, ep_size)
        return first, second, got[:, : small.shape[0]].reshape(-1, rows).T

    def scatter(value_rows):
        return lax.psum_scatter(value_rows, ("ep", "tp"), scatter_dimension=0, tiled=True)

    columns = jnp.zeros((small.shape[1], small.shape[0] * ep_size), jnp.float32)
    columns = lax.dynamic_update_slice_in_dim(
        columns, small.T, lax.axis_index("ep") * small.shape[0], 1
    )
    return (
        scatter(first).astype(jnp.float32),
        scatter(second).astype(jnp.float32),
        scatter(columns),
    )


LAST = 1 << 30


def pair_order(expert_ids, slot_order, expert_count):
    experts = jnp.arange(expert_count, dtype=jnp.int32)
    chosen = expert_ids.T[None, :, :] == experts[:, None, None]
    return jnp.min(jnp.where(chosen, slot_order.T[None, :, :], LAST), axis=1)


def kept_pairs(order):
    used = order < LAST
    counts = jnp.sum(used.astype(jnp.int32), axis=2)
    block = jnp.arange(order.shape[0], dtype=jnp.int32)
    earlier = block[None, :] < block[:, None]
    offsets = jnp.sum(jnp.where(earlier[:, :, None], counts[None, :, :], 0), axis=1)
    whole = offsets + counts <= CAP
    edge = (offsets < CAP) & ~whole
    edge_order = jnp.sum(jnp.where(edge[:, :, None], order, 0), axis=0)
    rank = jnp.sum((edge_order[:, :, None] < edge_order[:, None, :]).astype(jnp.int32), axis=1)
    early = offsets[:, :, None] + rank[None, :, :] < CAP
    return used & (whole[:, :, None] | (edge[:, :, None] & early))


def masked_softmax(logits, used):
    top = jnp.max(jnp.where(used, logits, -jnp.inf), axis=-1, keepdims=True)
    powers = jnp.where(used, jnp.exp(logits - top), 0.0)
    return powers / jnp.sum(powers, axis=-1, keepdims=True)


def visible_block(query_seg, query_pos, query_row, key_seg, key_pos, key_row):
    seg_q = query_seg[:, None]
    seg_k = key_seg[None, :]
    above = (
        (seg_k == seg_q)
        | (seg_k == 0)
        | (seg_k >= 1) & (seg_k <= 4) & (seg_q >= 5) & ((seg_q - 5) // 2 + 1 == seg_k)
    )
    same_tree = query_row[:, None] // TREE_TOKENS == key_row[None, :] // TREE_TOKENS
    return above & same_tree & (key_pos[None, :] <= query_pos[:, None])


def block_scores(query_part, key_rows, allowed, scale):
    scores = (
        jnp.einsum("qkgd,pkd->kgqp", query_part, key_rows, preferred_element_type=jnp.float32)
        * scale
    )
    return jnp.where(allowed[None, None], scores, -1e30)


def attend_forward(query_rows, key_rows, value_rows, segment, position):
    total_rows = query_rows.shape[0]
    scale = query_rows.shape[-1] ** (-0.5)
    row_ids = jnp.arange(total_rows, dtype=jnp.int32)
    allowed = visible_block(segment, position, row_ids, segment, position, row_ids)
    scores = block_scores(query_rows, key_rows, allowed, scale)
    top_score = jnp.max(scores, axis=-1, keepdims=True)
    weights = jnp.exp(scores - top_score)
    weight_sum = jnp.sum(weights, axis=-1, keepdims=True)
    probs = (weights / weight_sum).astype(jnp.bfloat16)
    outputs = jnp.einsum(
        "kgqp,pkd->qkgd", probs, value_rows, preferred_element_type=jnp.float32
    ).astype(jnp.bfloat16)
    log_sums = [top_score + jnp.log(weight_sum)]
    return (outputs, log_sums)


def attend_backward(
    query_rows, key_rows, value_rows, segment, position, log_sums, grad_heads, block_rows
):
    total_rows = query_rows.shape[0]
    scale = query_rows.shape[-1] ** (-0.5)
    row_ids = jnp.arange(total_rows, dtype=jnp.int32)
    grad_keys = jnp.zeros(key_rows.shape, jnp.float32)
    grad_values = jnp.zeros(value_rows.shape, jnp.float32)
    grad_query = []
    for number, first_row in enumerate(range(0, total_rows, block_rows)):
        allowed = visible_block(segment, position, row_ids, segment, position, row_ids)
        scores = block_scores(query_rows, key_rows, allowed, scale)
        probs = jnp.where(allowed[None, None], jnp.exp(scores - log_sums[number]), 0.0)
        grad_values = jnp.einsum(
            "kgqp,qkgd->pkd",
            probs.astype(jnp.bfloat16),
            grad_heads,
            preferred_element_type=jnp.float32,
        )
        grad_probs = jnp.einsum(
            "qkgd,pkd->kgqp", grad_heads, value_rows, preferred_element_type=jnp.float32
        )
        inner = jnp.sum(probs * grad_probs, axis=-1, keepdims=True)
        grad_scores = (probs * (grad_probs - inner)).astype(jnp.bfloat16)
        grad_query.append(
            jnp.einsum("kgqp,pkd->qkgd", grad_scores, key_rows, preferred_element_type=jnp.float32)
            * scale
        )
        grad_keys = (
            jnp.einsum(
                "kgqp,qkgd->pkd", grad_scores, query_rows, preferred_element_type=jnp.float32
            )
            * scale
        )
    return (grad_query[0], grad_keys, grad_values)


def local(
    hidden_in,
    gain_attn,
    w_query,
    key_projection_weight,
    value_projection_weight,
    w_out,
    gain_ffn,
    w_router,
    w_gate,
    w_up,
    w_down,
    expert_ids,
    slot_order,
    segment,
    position,
    cotangent,
):
    model_width = w_query.shape[1]
    head_width = HEAD_DIMENSION
    local_heads = w_query.shape[0] // head_width
    local_kv = key_projection_weight.shape[0] // head_width
    group_factor = local_heads // local_kv
    token_count = expert_ids.shape[0]
    share = hidden_in.shape[0]
    row_start = lax.axis_index("tp") * share
    expert_count = w_router.shape[0]
    per_owner = w_gate.shape[0]
    block_rows = 512
    by_links = lax.axis_size("tp") == 4 and lax.axis_size("ep") == 8
    order = pair_order(expert_ids, slot_order, expert_count)
    order_all = lax.all_gather(order, "ep")
    cot_all = gather_all(cotangent, False)
    inputs_own = hidden_in.astype(jnp.float32)
    gain_one = gain_attn.astype(jnp.float32)
    gain_two = gain_ffn.astype(jnp.float32)
    scale_one = norm_scale(inputs_own)
    first_normalized = group_rows(
        (inputs_own * scale_one * gain_one).astype(jnp.bfloat16), by_links, 6
    )
    cosine_lookup, sine_lookup = rope_tables(position, head_width)
    query_proj = jnp.einsum(
        "rd,fd->rf", first_normalized, w_query, preferred_element_type=jnp.float32
    ).reshape(token_count, local_heads, head_width)
    key_proj = jnp.einsum(
        "rd,fd->rf", first_normalized, key_projection_weight, preferred_element_type=jnp.float32
    ).reshape(token_count, local_kv, head_width)
    query_rows = (
        apply_rotation(query_proj, cosine_lookup, sine_lookup)
        .astype(jnp.bfloat16)
        .reshape(token_count, local_kv, group_factor, head_width)
    )
    key_rows = apply_rotation(key_proj, cosine_lookup, sine_lookup).astype(jnp.bfloat16)
    value_rows = (
        jnp.einsum(
            "rd,fd->rf",
            first_normalized,
            value_projection_weight,
            preferred_element_type=jnp.float32,
        )
        .astype(jnp.bfloat16)
        .reshape(token_count, local_kv, head_width)
    )
    head_outputs, log_sums = attend_forward(query_rows, key_rows, value_rows, segment, position)
    head_outputs = head_outputs.reshape(token_count, local_heads * head_width)
    middle_own = inputs_own + group_totals(
        jnp.dot(head_outputs, w_out, preferred_element_type=jnp.float32).astype(jnp.bfloat16),
        by_links,
        3,
    )
    scale_two = norm_scale(middle_own)
    normed_own = (middle_own * scale_two * gain_two).astype(jnp.bfloat16)
    normed_two = gather_all(normed_own, by_links)
    first_expert = lax.axis_index("ep") * per_owner
    used = lax.dynamic_slice_in_dim(order, row_start, share, 1).T < LAST
    gates = masked_softmax(
        jnp.einsum("rd,ed->re", normed_own, w_router, preferred_element_type=jnp.float32), used
    )
    kept_all = kept_pairs(
        lax.dynamic_slice_in_dim(order_all, first_expert, per_owner, 1)
    ).swapaxes(0, 1).reshape(per_owner, -1)
    all_gates = masked_softmax(
        jnp.einsum("rd,ed->re", normed_two, w_router, preferred_element_type=jnp.float32),
        order_all.swapaxes(1, 2).reshape(-1, expert_count) < LAST,
    )
    gate_all = jnp.where(
        kept_all.T, lax.dynamic_slice_in_dim(all_gates, first_expert, per_owner, 1), 0.0
    )
    units = w_gate.shape[2]
    gate_in = jnp.concatenate([w_gate[e] for e in range(per_owner)], axis=1)
    up_in = jnp.concatenate([w_up[e] for e in range(per_owner)], axis=1)
    down_in = w_down.reshape(per_owner * units, model_width)
    spread = jnp.repeat(gate_all, units, axis=1)
    gate_act = jnp.dot(normed_two, gate_in, preferred_element_type=jnp.float32)
    up_act = jnp.dot(normed_two, up_in, preferred_element_type=jnp.float32)
    back_act = jnp.einsum("rd,fd->rf", cot_all, down_in, preferred_element_type=jnp.float32)
    sigma = jax.nn.sigmoid(gate_act)
    hidden = gate_act * sigma * up_act
    weighted_hidden = (spread * hidden).astype(jnp.bfloat16)
    grad_hidden = spread * back_act
    grad_gate_act = (grad_hidden * up_act * sigma * (1.0 + gate_act * (1.0 - sigma))).astype(
        jnp.bfloat16
    )
    grad_up_act = (grad_hidden * gate_act * sigma).astype(jnp.bfloat16)
    grad_gates_part = jnp.where(
        kept_all, jnp.sum((hidden * back_act).reshape(-1, per_owner, units), axis=2).T, 0.0
    )
    grad_rows = (
        jnp.einsum("rf,df->rd", grad_gate_act, gate_in, preferred_element_type=jnp.float32)
        + jnp.einsum("rf,df->rd", grad_up_act, up_in, preferred_element_type=jnp.float32)
    ).astype(jnp.bfloat16)
    combined = jnp.dot(weighted_hidden, down_in, preferred_element_type=jnp.float32).astype(
        jnp.bfloat16
    )
    grad_normed_own, combined_own, grad_gates_own = totals(
        grad_rows, combined, grad_gates_part, by_links
    )
    output_own = (middle_own + combined_own).astype(jnp.bfloat16)
    grad_w_gate = jnp.einsum(
        "rd,ref->edf",
        normed_two,
        grad_gate_act.reshape(-1, per_owner, units),
        preferred_element_type=jnp.float32,
    )
    grad_w_up = jnp.einsum(
        "rd,ref->edf",
        normed_two,
        grad_up_act.reshape(-1, per_owner, units),
        preferred_element_type=jnp.float32,
    )
    grad_w_down = jnp.einsum(
        "rf,rd->fd", weighted_hidden, cot_all, preferred_element_type=jnp.float32
    ).reshape(per_owner, units, model_width)
    inner_gate = jnp.sum(gates * grad_gates_own, axis=-1, keepdims=True)
    grad_logits = gates * (grad_gates_own - inner_gate)
    router_f = w_router.astype(jnp.float32)
    grad_normed_own = grad_normed_own + jnp.dot(grad_logits, router_f, precision=EXACT_PRECISION)
    grad_router = jnp.dot(grad_logits.T, normed_own.astype(jnp.float32), precision=EXACT_PRECISION)
    grad_gain_ffn = jnp.sum(grad_normed_own * middle_own * scale_two, axis=0)
    grad_middle = cotangent.astype(jnp.float32) + norm_back(
        middle_own, scale_two, gain_two, grad_normed_own
    )
    grad_attn = group_rows(grad_middle.astype(jnp.bfloat16), by_links, 7)
    grad_w_out = jnp.einsum(
        "rf,rd->fd", head_outputs, grad_attn, preferred_element_type=jnp.float32
    )
    grad_w_out = lax.psum(grad_w_out.astype(jnp.bfloat16), "ep").astype(jnp.float32)
    grad_heads = (
        jnp.einsum("rd,fd->rf", grad_attn, w_out, preferred_element_type=jnp.float32)
        .astype(jnp.bfloat16)
        .reshape(token_count, local_kv, group_factor, head_width)
    )
    grad_query, grad_keys, grad_values = attend_backward(
        query_rows, key_rows, value_rows, segment, position, log_sums, grad_heads, block_rows
    )
    grad_query_proj = (
        rotate_back(
            grad_query.reshape(token_count, local_heads, head_width), cosine_lookup, sine_lookup
        )
        .astype(jnp.bfloat16)
        .reshape(token_count, local_heads * head_width)
    )
    grad_key_proj = (
        rotate_back(grad_keys, cosine_lookup, sine_lookup)
        .astype(jnp.bfloat16)
        .reshape(token_count, local_kv * head_width)
    )
    grad_value_proj = grad_values.astype(jnp.bfloat16).reshape(token_count, local_kv * head_width)
    grad_w_query = jnp.einsum(
        "rf,rd->fd", grad_query_proj, first_normalized, preferred_element_type=jnp.float32
    )
    grad_w_key = jnp.einsum(
        "rf,rd->fd", grad_key_proj, first_normalized, preferred_element_type=jnp.float32
    )
    grad_w_value = jnp.einsum(
        "rf,rd->fd", grad_value_proj, first_normalized, preferred_element_type=jnp.float32
    )
    grad_normed_one = jnp.einsum(
        "rf,fd->rd", grad_query_proj, w_query, preferred_element_type=jnp.float32
    )
    grad_normed_one = grad_normed_one + jnp.einsum(
        "rf,fd->rd", grad_key_proj, key_projection_weight, preferred_element_type=jnp.float32
    )
    grad_normed_one = grad_normed_one + jnp.einsum(
        "rf,fd->rd", grad_value_proj, value_projection_weight, preferred_element_type=jnp.float32
    )
    grad_gain_attn = jnp.sum(grad_normed_one * first_normalized.astype(jnp.float32), axis=0)
    small = jnp.concatenate(
        [grad_router, grad_gain_ffn[None, :], (grad_gain_attn / gain_one)[None, :]], axis=0
    )
    (grad_w_query, grad_w_key, grad_w_value), grad_one_own, small = tail_totals(
        [g.astype(jnp.bfloat16) for g in (grad_w_query, grad_w_key, grad_w_value)],
        grad_normed_one.astype(jnp.bfloat16),
        small,
        by_links,
    )
    grad_router = small[:expert_count]
    grad_gain_ffn, grad_gain_attn = small[expert_count], small[expert_count + 1]
    grad_input = grad_middle + norm_back(inputs_own, scale_one, gain_one, grad_one_own)
    return (
        output_own,
        grad_input,
        grad_gain_attn,
        grad_w_query,
        grad_w_key,
        grad_w_value,
        grad_w_out,
        grad_gain_ffn,
        grad_router,
        grad_w_gate,
        grad_w_up,
        grad_w_down,
    )


def solution(mesh):
    placed = (
        P(("ep", "tp"), None),
        P(),
        P("tp", None),
        P("tp", None),
        P("tp", None),
        P("tp", None),
        P(),
        P(),
        P("ep", None, "tp"),
        P("ep", None, "tp"),
        P("ep", "tp", None),
        P("ep", None),
        P("ep", None),
        P("ep"),
        P("ep"),
        P(("ep", "tp"), None),
    )
    return jax.shard_map(
        local,
        mesh=mesh,
        in_specs=placed,
        out_specs=(
            P(("ep", "tp"), None),
            P(("ep", "tp"), None),
            P(),
            P("tp", None),
            P("tp", None),
            P("tp", None),
            P("tp", None),
            P(),
            P(),
            P("ep", None, "tp"),
            P("ep", None, "tp"),
            P("ep", "tp", None),
        ),
        check_vma=False,
    )
```

```python
import functools

import jax
import jax.numpy as jnp
from jax import lax
from jax.experimental import pallas as pl
from jax.experimental.pallas import tpu as pltpu
from jax.sharding import PartitionSpec as P

HEAD_DIMENSION = 64
TREE_TOKENS = 512
CAP = 2304


EPSILON = 1e-06
ROPE_BASE = 10000.0
EXACT_PRECISION = lax.Precision.HIGHEST


def rope_tables(position, head_width):
    half_width = head_width // 2
    freqs = ROPE_BASE ** (-(jnp.arange(half_width, dtype=jnp.float32) * 2.0 / head_width))
    angle = position.astype(jnp.float32)[:, None] * freqs[None, :]
    return (jnp.cos(angle)[:, None, :], jnp.sin(angle)[:, None, :])


def apply_rotation(value_rows, cosine_lookup, sine_lookup):
    half_width = value_rows.shape[-1] // 2
    first = value_rows[..., :half_width]
    second = value_rows[..., half_width:]
    return jnp.concatenate(
        [
            first * cosine_lookup - second * sine_lookup,
            first * sine_lookup + second * cosine_lookup,
        ],
        axis=-1,
    )


def rotate_back(grads, cosine_lookup, sine_lookup):
    half_width = grads.shape[-1] // 2
    first = grads[..., :half_width]
    second = grads[..., half_width:]
    return jnp.concatenate(
        [
            first * cosine_lookup + second * sine_lookup,
            second * cosine_lookup - first * sine_lookup,
        ],
        axis=-1,
    )


def norm_scale(value_rows):
    return lax.rsqrt(jnp.mean(value_rows * value_rows, axis=-1, keepdims=True) + EPSILON)


def norm_back(value_rows, scale, gain, grad_normed):
    weighted = grad_normed * gain
    inner = jnp.mean(value_rows * weighted, axis=-1, keepdims=True)
    grad_values = scale * weighted - value_rows * (scale * scale * scale) * inner
    return grad_values


MESH = pl.DeviceIdType.MESH


class Place:
    def __init__(self, ep_size):
        self.depth = ep_size // 2
        ep, tp = lax.axis_index("ep"), lax.axis_index("tp")
        self.z, self.y = ep // 2, ep % 2
        self.x, self.c = tp // 2, tp % 2

    def device(self, z=None, y=None, x=None, c=None):
        z = self.z if z is None else z
        y = self.y if y is None else y
        x = self.x if x is None else x
        c = self.c if c is None else c
        return (z * 2 + y, x * 2 + c)

    def sibling(self):
        return self.device(c=1 - self.c)

    def x_peer(self):
        return self.device(x=1 - self.x)

    def y_peer(self):
        return self.device(y=1 - self.y)

    def after(self, step):
        return lax.rem(self.z + step, self.depth)

    def before(self, step):
        return lax.rem(self.z + self.depth - step, self.depth)


def meet(devices):
    barrier = pltpu.get_barrier_semaphore()
    for device in devices:
        pl.semaphore_signal(barrier, inc=1, device_id=device, device_id_type=MESH)
    pl.semaphore_wait(barrier, len(devices))


def send(src, dst, send_sem, recv_sem, device):
    copy = pltpu.make_async_remote_copy(
        src_ref=src,
        dst_ref=dst,
        send_sem=send_sem,
        recv_sem=recv_sem,
        device_id=device,
        device_id_type=MESH,
    )
    copy.start()
    return copy


def gather_kernel(ep_size, own, out, own_sem, z_sems, pair_sems, core_sems):
    me = Place(ep_size)
    depth = me.depth
    half = own.shape[0] // 2
    z_send, z_recv = z_sems.at[0], z_sems.at[1]
    pair_send, pair_recv = pair_sems.at[0], pair_sems.at[1]
    core_send, core_recv = core_sems.at[0], core_sems.at[1]
    meet(
        [me.sibling(), me.x_peer(), me.y_peer()]
        + [me.device(z=me.after(s)) for s in range(1, depth)]
    )

    def rows(part):
        return pl.ds(part * half, half)

    def block(step, y, x, part, c=None):
        return out.at[me.before(step), y, x, me.c if c is None else c, rows(part)]

    started = []

    def forward(source, target, sems, slot, device):
        started.append(send(source, target, sems[0].at[slot], sems[1].at[slot], device))

    for s in range(1, depth):
        for part in range(2):
            forward(
                own.at[rows(part)],
                out.at[me.z, me.y, me.x, me.c, rows(part)],
                (z_send, z_recv),
                (s - 1) * 2 + part,
                me.device(z=me.after(s)),
            )
    local = pltpu.make_async_copy(own, out.at[me.z, me.y, me.x, me.c], own_sem)
    local.start()
    local.wait()

    kinds = [
        (me.y, me.x, 0),
        (me.y, me.x, 1),
        (1 - me.y, me.x, 0),
        (me.y, 1 - me.x, 1),
        (1 - me.y, me.x, 1),
        (1 - me.y, 1 - me.x, 1),
        (me.y, 1 - me.x, 0),
        (1 - me.y, 1 - me.x, 0),
    ]
    x_route = {0: 6, 2: 7, 1: 3}
    y_route = {0: 2, 1: 4, 3: 5}

    def landed(step, kind):
        y, x, part = kinds[kind]
        place = block(step, y, x, part)
        if kind < 2:
            if step > 0:
                sem = z_recv.at[(step - 1) * 2 + part]
                pltpu.make_async_copy(place, place, sem).wait()
        else:
            pltpu.make_async_copy(place, place, pair_recv.at[step * 8 + kind]).wait()

    def pass_on(step, kind):
        y, x, part = kinds[kind]
        place = block(step, y, x, part)
        if kind in x_route:
            forward(place, place, (pair_send, pair_recv), step * 8 + x_route[kind], me.x_peer())
        if kind in y_route:
            forward(place, place, (pair_send, pair_recv), step * 8 + y_route[kind], me.y_peer())
        forward(place, place, (core_send, core_recv), step * 8 + kind, me.sibling())

    for turn in range(depth + 2):
        for step, group in ((turn, (0, 1)), (turn - 1, (2, 3)), (turn - 2, (4, 5, 6, 7))):
            if 0 <= step < depth:
                for kind in group:
                    landed(step, kind)
                    pass_on(step, kind)
    for step in range(depth):
        for kind in range(8):
            y, x, part = kinds[kind]
            place = block(step, y, x, part, 1 - me.c)
            pltpu.make_async_copy(place, place, core_recv.at[step * 8 + kind]).wait()
    for copy in started:
        copy.wait_send()


def gather_by_links(value_rows, ep_size):
    rows, width = value_rows.shape
    depth = ep_size // 2
    dma = pltpu.SemaphoreType.DMA
    every = pl.pallas_call(
        functools.partial(gather_kernel, ep_size),
        out_shape=jax.ShapeDtypeStruct((depth, 2, 2, 2, rows, width), value_rows.dtype),
        in_specs=[pl.BlockSpec(memory_space=pl.ANY)],
        out_specs=pl.BlockSpec(memory_space=pl.ANY),
        scratch_shapes=[
            dma,
            dma((2, 2 * depth - 2)),
            dma((2, 8 * depth)),
            dma((2, 8 * depth)),
        ],
        compiler_params=pltpu.CompilerParams(collective_id=1, has_side_effects=True),
        name="gather_by_links",
    )(value_rows)
    return every.reshape(-1, width)


def add_into(target, other):
    def tile(i, carry):
        at = pl.ds(pl.multiple_of(i * 16, 16), 16)
        target[at, :] = target[at, :] + other[at, :]
        return carry

    lax.fori_loop(0, target.shape[0] // 16, tile, 0)


def front_gather_kernel(
    ep_size, pieces, own, table, out, tables, own_sem, sems, table_own_sem, table_sems
):
    me = Place(ep_size)
    mine = lax.axis_index("ep")
    tp = lax.axis_index("tp")
    peers = [(lax.rem(mine + k, ep_size), tp) for k in range(1, ep_size)]
    meet([me.sibling(), me.x_peer()] + peers)
    local = pltpu.make_async_copy(table, tables.at[mine], table_own_sem)
    local.start()
    copies = [
        send(table, tables.at[mine], table_sems.at[0, k], table_sems.at[1, k], device)
        for k, device in enumerate(peers)
    ]
    group_gather_body(me, pieces, own, out, own_sem, sems)
    local.wait()
    for copy in copies:
        copy.wait()


def front_gather(value_rows, table, ep_size):
    rows, width = value_rows.shape
    pieces = 4
    dma = pltpu.SemaphoreType.DMA
    anywhere = pl.BlockSpec(memory_space=pl.ANY)
    every, tables = pl.pallas_call(
        functools.partial(front_gather_kernel, ep_size, pieces),
        out_shape=(
            jax.ShapeDtypeStruct((2, 2, rows, width), value_rows.dtype),
            jax.ShapeDtypeStruct((ep_size,) + table.shape, table.dtype),
        ),
        in_specs=[anywhere] * 2,
        out_specs=(anywhere,) * 2,
        scratch_shapes=[dma, dma((2, 3 * pieces)), dma, dma((2, ep_size - 1))],
        compiler_params=pltpu.CompilerParams(collective_id=6, has_side_effects=True),
        name="front_gather",
    )(value_rows, table)
    return every.reshape(-1, width), tables


def group_gather_kernel(ep_size, pieces, own, out, own_sem, sems):
    me = Place(ep_size)
    meet([me.sibling(), me.x_peer()])
    group_gather_body(me, pieces, own, out, own_sem, sems)


def group_gather_body(me, pieces, own, out, own_sem, sems):
    size = own.shape[0] // pieces
    started = []
    local = pltpu.make_async_copy(own, out.at[me.x, me.c], own_sem)
    local.start()

    def at(p):
        return pl.ds(p * size, size)

    def go(kind, p, src, dst, device):
        slot = kind * pieces + p
        started.append(send(src, dst, sems.at[0, slot], sems.at[1, slot], device))

    for p in range(pieces):
        go(0, p, own.at[at(p)], out.at[me.x, me.c, at(p)], me.x_peer())
    for p in range(pieces):
        go(1, p, own.at[at(p)], out.at[me.x, me.c, at(p)], me.sibling())
    for p in range(pieces):
        block = out.at[1 - me.x, me.c, at(p)]
        pltpu.make_async_copy(block, block, sems.at[1, p]).wait()
        go(2, p, block, block, me.sibling())
    for p in range(pieces):
        for kind, x in ((1, me.x), (2, 1 - me.x)):
            block = out.at[x, 1 - me.c, at(p)]
            pltpu.make_async_copy(block, block, sems.at[1, kind * pieces + p]).wait()
    local.wait()
    for copy in started:
        copy.wait_send()


def group_gather(value_rows, ep_size, call):
    rows, width = value_rows.shape
    pieces = 4
    dma = pltpu.SemaphoreType.DMA
    every = pl.pallas_call(
        functools.partial(group_gather_kernel, ep_size, pieces),
        out_shape=jax.ShapeDtypeStruct((2, 2, rows, width), value_rows.dtype),
        in_specs=[pl.BlockSpec(memory_space=pl.ANY)],
        out_specs=pl.BlockSpec(memory_space=pl.ANY),
        scratch_shapes=[dma, dma((2, 3 * pieces))],
        compiler_params=pltpu.CompilerParams(collective_id=call, has_side_effects=True),
        name="group_gather",
    )(value_rows)
    return every.reshape(-1, width)


class GroupTotal:
    def __init__(self, me, parts, core_got, pair_got, sems):
        self.me, self.parts, self.core_got, self.pair_got = me, parts, core_got, pair_got
        self.core = [
            pltpu.make_async_remote_copy(
                src_ref=parts.at[x, 1 - me.c],
                dst_ref=core_got.at[x],
                send_sem=sems.at[0, k],
                recv_sem=sems.at[1, k],
                device_id=me.sibling(),
                device_id_type=MESH,
            )
            for k, x in enumerate((1 - me.x, me.x))
        ]
        self.pair = pltpu.make_async_remote_copy(
            src_ref=core_got.at[1 - me.x],
            dst_ref=pair_got,
            send_sem=sems.at[0, 2],
            recv_sem=sems.at[1, 2],
            device_id=me.x_peer(),
            device_id_type=MESH,
        )

    def begin(self):
        for copy in self.core:
            copy.start()

    def exchange(self):
        self.core[0].wait_recv()
        far = 1 - self.me.x
        add_into(self.core_got.at[far], self.parts.at[far, self.me.c])
        self.pair.start()

    def finish(self, out):
        self.core[1].wait_recv()
        self.pair.wait_recv()

        def tile(i, carry):
            at = pl.ds(pl.multiple_of(i * 16, 16), 16)
            out[at, :] = (
                self.parts[self.me.x, self.me.c, at, :].astype(jnp.float32)
                + self.core_got[self.me.x, at, :].astype(jnp.float32)
                + self.pair_got[at, :].astype(jnp.float32)
            )
            return carry

        lax.fori_loop(0, out.shape[0] // 16, tile, 0)

    def sent(self):
        for copy in self.core + [self.pair]:
            copy.wait_send()


def group_total_kernel(ep_size, parts, out, core_got, pair_got, sems):
    me = Place(ep_size)
    meet([me.sibling(), me.x_peer()])
    total = GroupTotal(me, parts, core_got, pair_got, sems)
    total.begin()
    total.exchange()
    total.finish(out)
    total.sent()


def group_total(value_rows, ep_size, call):
    rows, width = value_rows.shape[0] // 4, value_rows.shape[1]
    vmem = pl.BlockSpec(memory_space=pltpu.VMEM)
    return pl.pallas_call(
        functools.partial(group_total_kernel, ep_size),
        out_shape=jax.ShapeDtypeStruct((rows, width), jnp.float32),
        in_specs=[vmem],
        out_specs=vmem,
        scratch_shapes=[
            pltpu.VMEM((2, rows, width), jnp.bfloat16),
            pltpu.VMEM((rows, width), jnp.bfloat16),
            pltpu.SemaphoreType.DMA((2, 3)),
        ],
        compiler_params=pltpu.CompilerParams(
            collective_id=call, has_side_effects=True, vmem_limit_bytes=32 * 1024 * 1024
        ),
        name="group_total",
    )(value_rows.reshape(2, 2, rows, width))


def all_others(ep_size):
    ep, tp = lax.axis_index("ep"), lax.axis_index("tp")
    return [
        (lax.rem(ep + k // 4, ep_size), lax.rem(tp + k % 4, 4)) for k in range(1, ep_size * 4)
    ]


def experts_kernel(
    ep_size,
    per_owner,
    rows_in,
    cots_in,
    code_in,
    router,
    enter,
    leave,
    grad_out,
    sum_out,
    small_out,
    gate_out,
    up_out,
    down_out,
    rows_buf,
    cots_buf,
    weighted,
    turned,
    enter_sum,
    parts,
    core_got,
    pair_got,
    last_got,
    z_got,
    small_in,
    small_got,
    load_sems,
    core_sems,
    pair_sems,
    last_sems,
    z_sems,
    small_sems,
    own_sem,
):
    me = Place(ep_size)
    depth = me.depth
    blocks = 2 * depth
    width = router.shape[1]
    tokens = rows_buf.shape[1]
    share = tokens // 4
    units = leave.shape[0] // per_owner
    hidden = per_owner * units
    f32, bf16 = jnp.float32, jnp.bfloat16
    others = all_others(ep_size)
    meet(others)
    my_place = lax.axis_index("ep") * 4 + lax.axis_index("tp")

    def where(b):
        return me.after(b // 2 + 1), lax.rem(1 - me.y + b % 2, 2)

    def load(b, which):
        z, y = where(b)
        source, target = ((rows_in, rows_buf), (cots_in, cots_buf))[which]
        slot = lax.rem(b, 2)
        return pltpu.make_async_copy(
            source.at[z, y], target.at[slot], load_sems.at[slot, which]
        )

    def core_copy(b):
        y = where(b)[1]
        return pltpu.make_async_remote_copy(
            src_ref=parts.at[lax.rem(b, 2), :, :, 1 - me.c],
            dst_ref=core_got.at[b // 2, y],
            send_sem=core_sems.at[0, b],
            recv_sem=core_sems.at[1, b],
            device_id=me.sibling(),
            device_id_type=MESH,
        )

    def grad_pair(b):
        y = where(b)[1]
        return pltpu.make_async_remote_copy(
            src_ref=core_got.at[b // 2, y, 0, 1 - me.x],
            dst_ref=pair_got.at[b // 2, 0, y],
            send_sem=pair_sems.at[0, b],
            recv_sem=pair_sems.at[1, b],
            device_id=me.x_peer(),
            device_id_type=MESH,
        )

    def sum_pair(step):
        return pltpu.make_async_remote_copy(
            src_ref=core_got.at[step, 1 - me.y, 1],
            dst_ref=pair_got.at[step, 1],
            send_sem=pair_sems.at[0, blocks + step],
            recv_sem=pair_sems.at[1, blocks + step],
            device_id=me.y_peer(),
            device_id_type=MESH,
        )

    def last_copy(step, which):
        return pltpu.make_async_remote_copy(
            src_ref=pair_got.at[step, which, (1 - me.y, 1 - me.x)[which]],
            dst_ref=last_got.at[step, which],
            send_sem=last_sems.at[0, step, which],
            recv_sem=last_sems.at[1, step, which],
            device_id=(me.y_peer(), me.x_peer())[which],
            device_id_type=MESH,
        )

    def z_copy(step):
        return pltpu.make_async_remote_copy(
            src_ref=last_got.at[step],
            dst_ref=z_got.at[step],
            send_sem=z_sems.at[0, step],
            recv_sem=z_sems.at[1, step],
            device_id=me.device(z=me.after(step + 1)),
            device_id_type=MESH,
        )

    def small_copy(k, device):
        return pltpu.make_async_remote_copy(
            src_ref=small_in.at[device[0] * 4 + device[1]],
            dst_ref=small_got.at[my_place],
            send_sem=small_sems.at[0, k],
            recv_sem=small_sems.at[1, k],
            device_id=device,
            device_id_type=MESH,
        )

    def dot(a, b, contract):
        return lax.dot_general(
            a, b, ((contract[:1], contract[1:]), ((), ())), preferred_element_type=f32
        )

    def spread(columns):
        return jnp.concatenate(
            [jnp.broadcast_to(columns[:, e : e + 1], (tokens, units)) for e in range(per_owner)],
            axis=1,
        )

    def compute(b):
        z, y = where(b)
        slot = lax.rem(b, 2)
        rows, cots = rows_buf[slot], cots_buf[slot]
        code = code_in[pl.ds(pl.multiple_of((z * 2 + y) * tokens, tokens), tokens), :].astype(f32)
        used = code >= 0.0
        logits = jnp.where(used, dot(rows, router[...], (1, 1)), -1e30)
        top = jnp.max(logits, axis=1, keepdims=True)
        powers = jnp.where(used, jnp.exp(logits - top), 0.0)
        kept = jnp.where(code == 0.0, 1.0, 0.0)
        gates = spread(kept * powers / jnp.sum(powers, axis=1, keepdims=True))
        act = dot(rows, enter[...], (1, 0))
        gate_act, up_act = act[:, :hidden], act[:, hidden:]
        back_act = dot(cots, leave[...], (1, 1))
        sigma = jax.nn.sigmoid(gate_act)
        swish = gate_act * sigma
        value = swish * up_act
        gate_parts = spread(kept) * (value * back_act)
        lane = lax.broadcasted_iota(jnp.int32, (8, hidden), 1)
        pick = lax.broadcasted_iota(jnp.int32, (8, hidden), 0)
        mine = jnp.where((lane >= pick * units) & (lane < (pick + 1) * units), 1.0, 0.0)
        grad_gates = lax.dot_general(
            mine,
            gate_parts,
            (((1,), (1,)), ((), ())),
            precision=EXACT_PRECISION,
            preferred_element_type=f32,
        )
        for k in range(4):
            small_in[(z * 2 + y) * 4 + k] = grad_gates[:, k * share : (k + 1) * share]
        weighted[...] = (gates * value).astype(bf16)
        grad_hidden = gates * back_act
        turned[:, :hidden] = (
            grad_hidden * up_act * sigma * (1.0 + gate_act * (1.0 - sigma))
        ).astype(bf16)
        turned[:, hidden:] = (grad_hidden * swish).astype(bf16)
        tile = 512
        for n in range(width // tile):
            cols = slice(n * tile, (n + 1) * tile)
            grads = dot(turned[...], enter[cols, :], (1, 1)).astype(bf16)
            sums = dot(weighted[...], leave[:, cols], (1, 0)).astype(bf16)
            for x in range(2):
                for c in range(2):
                    at = slice((x * 2 + c) * share, (x * 2 + c + 1) * share)
                    parts[slot, 0, x, c, :, cols] = grads[at]
                    parts[slot, 1, x, c, :, cols] = sums[at]

    def weight_sums(b):
        slot = lax.rem(b, 2)
        tile = 512
        for n in range(width // tile):
            cols = slice(n * tile, (n + 1) * tile)
            enter_sum[:, cols] += dot(turned[...], rows_buf[slot, :, cols], (0, 0))
            down_out[:, cols] += dot(weighted[...], cots_buf[slot, :, cols], (0, 0))

    enter_sum[...] = jnp.zeros_like(enter_sum)
    down_out[...] = jnp.zeros_like(down_out)
    for which in range(2):
        load(0, which).start()

    def turn(b, carry):
        @pl.when(b < blocks)
        def _():
            for which in range(2):
                load(b, which).wait()

            @pl.when(b + 1 < blocks)
            def _():
                for which in range(2):
                    load(b + 1, which).start()

            compute(b)
            core_copy(b).start()
            weight_sums(b)

        @pl.when((b >= 1) & (b <= blocks))
        def _():
            j = b - 1
            y = where(j)[1]
            core_copy(j).wait_recv()
            for which in range(2):
                for x in range(2):
                    add_into(
                        core_got.at[j // 2, y, which, x],
                        parts.at[lax.rem(j, 2), which, x, me.c],
                    )
            grad_pair(j).start()

            @pl.when(j % 2 == 0)
            def _():
                sum_pair(j // 2).start()

            core_copy(j).wait_send()

        @pl.when((b >= 2) & (b <= blocks + 1))
        def _():
            j = b - 2
            y = where(j)[1]
            step = j // 2
            grad_pair(j).wait_recv()
            add_into(pair_got.at[step, 0, y], core_got.at[step, y, 0, me.x])

            @pl.when(j % 2 == 0)
            def _():
                last_copy(step, 0).start()
                sum_pair(step).wait_recv()
                for x in range(2):
                    add_into(pair_got.at[step, 1, x], core_got.at[step, me.y, 1, x])
                last_copy(step, 1).start()

        @pl.when((b >= 4) & (b % 2 == 0))
        def _():
            step = (b - 4) // 2
            for which in range(2):
                last_copy(step, which).wait_recv()
                add_into(last_got.at[step, which], pair_got.at[step, which, (me.y, me.x)[which]])

            @pl.when(step < depth - 1)
            def _():
                z_copy(step).start()

        @pl.when(b == blocks)
        def _():
            for k, device in enumerate(others):
                small_copy(k, device).start()
            pltpu.make_async_copy(
                small_in.at[my_place], small_got.at[my_place], own_sem
            ).start()
            for e in range(per_owner):
                gate_out[e] = enter_sum[e * units : (e + 1) * units, :].T
                up_out[e] = enter_sum[hidden + e * units : hidden + (e + 1) * units, :].T

        return carry

    lax.fori_loop(0, blocks + 3, turn, 0)
    pltpu.make_async_copy(small_in.at[my_place], small_got.at[my_place], own_sem).wait()
    for k, device in enumerate(others):
        small_copy(k, device).wait()
    for ep in range(ep_size):
        total = small_got[ep * 4]
        for tp in range(1, 4):
            total = total + small_got[ep * 4 + tp]
        small_out[ep] = total
    for step in range(depth - 1):
        z_copy(step).wait_recv()

    def finish(which, target):
        def tile(i, carry):
            at = pl.ds(pl.multiple_of(i * 16, 16), 16)
            total = last_got[depth - 1, which, at, :].astype(f32)
            for step in range(depth - 1):
                total = total + z_got[step, which, at, :].astype(f32)
            target[at, :] = total
            return carry

        lax.fori_loop(0, target.shape[0] // 16, tile, 0)

    finish(0, grad_out)
    finish(1, sum_out)
    for step in range(depth):
        grad_pair(2 * step).wait_send()
        grad_pair(2 * step + 1).wait_send()
        sum_pair(step).wait_send()
        for which in range(2):
            last_copy(step, which).wait_send()
        if step < depth - 1:
            z_copy(step).wait_send()


def experts_by_links(rows_all, cots_all, code, router, enter, leave, per_owner, ep_size):
    total_rows, width = rows_all.shape
    depth = ep_size // 2
    tokens = total_rows // ep_size
    rows = tokens // 4
    hidden = leave.shape[0]
    units = hidden // per_owner
    bf16, f32 = jnp.bfloat16, jnp.float32
    dma = pltpu.SemaphoreType.DMA
    vmem = pl.BlockSpec(memory_space=pltpu.VMEM)
    anywhere = pl.BlockSpec(memory_space=pl.ANY)
    places = 4 * ep_size
    blocks = (depth, 2, tokens, width)
    return pl.pallas_call(
        functools.partial(experts_kernel, ep_size, per_owner),
        out_shape=(
            jax.ShapeDtypeStruct((rows, width), f32),
            jax.ShapeDtypeStruct((rows, width), f32),
            jax.ShapeDtypeStruct((ep_size, 8, rows), f32),
            jax.ShapeDtypeStruct((per_owner, width, units), f32),
            jax.ShapeDtypeStruct((per_owner, width, units), f32),
            jax.ShapeDtypeStruct((hidden, width), f32),
        ),
        in_specs=[anywhere, anywhere, vmem, vmem, vmem, vmem],
        out_specs=(vmem,) * 6,
        scratch_shapes=[
            pltpu.VMEM((2, tokens, width), bf16),
            pltpu.VMEM((2, tokens, width), bf16),
            pltpu.VMEM((tokens, hidden), bf16),
            pltpu.VMEM((tokens, 2 * hidden), bf16),
            pltpu.VMEM((2 * hidden, width), f32),
            pltpu.VMEM((2, 2, 2, 2, rows, width), bf16),
            pltpu.VMEM((depth, 2, 2, 2, rows, width), bf16),
            pltpu.VMEM((depth, 2, 2, rows, width), bf16),
            pltpu.VMEM((depth, 2, rows, width), bf16),
            pltpu.VMEM((depth - 1, 2, rows, width), bf16),
            pltpu.VMEM((places, 8, rows), f32),
            pltpu.VMEM((places, 8, rows), f32),
            dma((2, 2)),
            dma((2, 2 * depth)),
            dma((2, 3 * depth)),
            dma((2, depth, 2)),
            dma((2, depth - 1)),
            dma((2, places - 1)),
            dma,
        ],
        compiler_params=pltpu.CompilerParams(
            collective_id=2, has_side_effects=True, vmem_limit_bytes=60 * 1024 * 1024
        ),
        name="experts_by_links",
    )(rows_all.reshape(blocks), cots_all.reshape(blocks), code, router, enter, leave)


def tail_kernel(
    ep_size,
    counts,
    *refs,
):
    n = len(counts)
    grads, rows_in, small_in = refs[:n], refs[n], refs[n + 1]
    outs, rows_out, small_out = refs[n + 2 : 2 * n + 2], refs[2 * n + 2], refs[2 * n + 3]
    (
        y_got,
        z_got,
        final,
        core_got,
        pair_got,
        small_got,
        small_sum,
        y_sems,
        z_sems,
        fz_sems,
        fy_sems,
        group_sems,
        small_sems,
        spread_sems,
        own_sem,
    ) = refs[2 * n + 4 :]
    me = Place(ep_size)
    depth = me.depth
    starts = [sum(counts[:i]) for i in range(n)]
    others = all_others(ep_size)
    meet(others)
    my_place = lax.axis_index("ep") * 4 + lax.axis_index("tp")

    def y_copy(step, i):
        return pltpu.make_async_remote_copy(
            src_ref=grads[i].at[me.after(step + 1), 1 - me.y],
            dst_ref=y_got.at[step, pl.ds(starts[i], counts[i])],
            send_sem=y_sems.at[0, step, i],
            recv_sem=y_sems.at[1, step, i],
            device_id=me.y_peer(),
            device_id_type=MESH,
        )

    def z_copy(step):
        return pltpu.make_async_remote_copy(
            src_ref=y_got.at[step],
            dst_ref=z_got.at[step],
            send_sem=z_sems.at[0, step],
            recv_sem=z_sems.at[1, step],
            device_id=me.device(z=me.after(step + 1)),
            device_id_type=MESH,
        )

    for step in range(depth):
        for i in range(n):
            y_copy(step, i).start()
    group = GroupTotal(me, rows_in, core_got, pair_got, group_sems)
    group.begin()
    small = [
        send(
            small_in.at[device[0] * 4 + device[1]],
            small_got.at[my_place],
            small_sems.at[0, k],
            small_sems.at[1, k],
            device,
        )
        for k, device in enumerate(others)
    ]
    own_small = pltpu.make_async_copy(small_in.at[my_place], small_got.at[my_place], own_sem)
    own_small.start()
    group.exchange()

    def y_sum(step):
        for i in range(n):
            y_copy(step, i).wait_recv()
            add_into(
                y_got.at[step, pl.ds(starts[i], counts[i])],
                grads[i].at[me.after(step + 1), me.y],
            )

    for step in range(depth - 1):
        y_sum(step)
        z_copy(step).start()
    own_small.wait()
    for copy in small:
        copy.wait_recv()
    total = small_got[0]
    for k in range(1, 4 * ep_size):
        total = total + small_got[k]
    small_sum[...] = total
    spread = [
        send(
            small_sum,
            small_out.at[my_place],
            spread_sems.at[0, k],
            spread_sems.at[1, k],
            device,
        )
        for k, device in enumerate(others)
    ]
    small_out[my_place] = total
    group.finish(rows_out)
    y_sum(depth - 1)
    for step in range(depth - 1):
        z_copy(step).wait_recv()

    def tile(i, carry):
        at = pl.ds(pl.multiple_of(i * 16, 16), 16)
        value = y_got[depth - 1, at, :].astype(jnp.float32)
        for step in range(depth - 1):
            value = value + z_got[step, at, :].astype(jnp.float32)
        final[me.z, me.y, at, :] = value.astype(final.dtype)
        return carry

    lax.fori_loop(0, sum(counts) // 16, tile, 0)
    mine = final.at[me.z, me.y]
    finals = []
    for s in range(1, depth):
        finals.append(
            send(mine, mine, fz_sems.at[0, s], fz_sems.at[1, s], me.device(z=me.after(s)))
        )
    finals.append(send(mine, mine, fy_sems.at[0, 0], fy_sems.at[1, 0], me.y_peer()))
    for s in range(1, depth):
        block = final.at[me.before(s), me.y]
        pltpu.make_async_copy(block, block, fz_sems.at[1, s]).wait()
        finals.append(send(block, block, fy_sems.at[0, s], fy_sems.at[1, s], me.y_peer()))

    def deliver(s, y):
        z = me.before(s)
        for i in range(n):

            def tile(t, carry):
                at = pl.multiple_of(t * 16, 16)
                outs[i][z, y, pl.ds(at, 16), :] = final[
                    z, y, pl.ds(starts[i] + at, 16), :
                ].astype(jnp.float32)
                return carry

            lax.fori_loop(0, counts[i] // 16, tile, 0)

    for s in range(depth):
        deliver(s, me.y)
    for s in range(depth):
        block = final.at[me.before(s), 1 - me.y]
        pltpu.make_async_copy(block, block, fy_sems.at[1, s]).wait()
        deliver(s, 1 - me.y)
    for copy in spread:
        copy.wait()
    for copy in small + finals:
        copy.wait_send()
    group.sent()
    for step in range(depth):
        for i in range(n):
            y_copy(step, i).wait_send()
        if step < depth - 1:
            z_copy(step).wait_send()


def tail_by_links(grads, rows_part, small, ep_size):
    width = rows_part.shape[1]
    depth = ep_size // 2
    rows = rows_part.shape[0] // 4
    counts = [g.shape[0] // ep_size for g in grads]
    total = sum(counts)
    places = 4 * ep_size
    bf16, f32 = jnp.bfloat16, jnp.float32
    dma = pltpu.SemaphoreType.DMA
    vmem = pl.BlockSpec(memory_space=pltpu.VMEM)
    lanes = width // 128
    blocks = jnp.pad(small, ((0, places - small.shape[0]), (0, 0))).reshape(places, lanes, 128)
    got = pl.pallas_call(
        functools.partial(tail_kernel, ep_size, counts),
        out_shape=tuple(jax.ShapeDtypeStruct((depth, 2, k, width), f32) for k in counts)
        + (
            jax.ShapeDtypeStruct((rows, width), f32),
            jax.ShapeDtypeStruct(blocks.shape, f32),
        ),
        in_specs=[vmem] * (len(grads) + 2),
        out_specs=(vmem,) * (len(grads) + 2),
        scratch_shapes=[
            pltpu.VMEM((depth, total, width), bf16),
            pltpu.VMEM((depth - 1, total, width), bf16),
            pltpu.VMEM((depth, 2, total, width), bf16),
            pltpu.VMEM((2, rows, width), bf16),
            pltpu.VMEM((rows, width), bf16),
            pltpu.VMEM(blocks.shape, f32),
            pltpu.VMEM(blocks.shape[1:], f32),
            dma((2, depth, len(grads))),
            dma((2, depth)),
            dma((2, depth)),
            dma((2, depth)),
            dma((2, 3)),
            dma((2, places - 1)),
            dma((2, places - 1)),
            dma,
        ],
        compiler_params=pltpu.CompilerParams(
            collective_id=5, has_side_effects=True, vmem_limit_bytes=56 * 1024 * 1024
        ),
        name="tail_by_links",
    )(
        *[g.reshape(depth, 2, k, width) for g, k in zip(grads, counts)],
        rows_part.reshape(2, 2, rows, width),
        blocks,
    )
    sums = [g.reshape(-1, width) for g in got[: len(grads)]]
    return sums, got[-2], got[-1].reshape(places, width)[: small.shape[0]]


def group_rows(value_rows, by_links, call):
    if by_links:
        return group_gather(value_rows, lax.axis_size("ep"), call)
    return lax.all_gather(value_rows, "tp", axis=0, tiled=True)


def group_totals(value_rows, by_links, call):
    if by_links:
        return group_total(value_rows, lax.axis_size("ep"), call)
    return lax.psum_scatter(value_rows, "tp", scatter_dimension=0, tiled=True).astype(jnp.float32)


def tail_totals(grads, rows_part, small, by_links):
    if by_links:
        return tail_by_links(grads, rows_part, small, lax.axis_size("ep"))
    sums = [lax.psum(g, "ep").astype(jnp.float32) for g in grads]
    return sums, group_totals(rows_part, by_links, None), lax.psum(small, ("ep", "tp"))


def gather_all(value_rows, by_links):
    if by_links:
        return gather_by_links(value_rows, lax.axis_size("ep"))
    return lax.all_gather(value_rows, ("ep", "tp"), axis=0, tiled=True)


LAST = 1 << 30


def pair_order(expert_ids, slot_order, expert_count):
    experts = jnp.arange(expert_count, dtype=jnp.int32)
    chosen = expert_ids.T[None, :, :] == experts[:, None, None]
    return jnp.min(jnp.where(chosen, slot_order.T[None, :, :], LAST), axis=1)


def kept_pairs(order):
    used = order < LAST
    counts = jnp.sum(used.astype(jnp.int32), axis=2)
    block = jnp.arange(order.shape[0], dtype=jnp.int32)
    earlier = block[None, :] < block[:, None]
    offsets = jnp.sum(jnp.where(earlier[:, :, None], counts[None, :, :], 0), axis=1)
    whole = offsets + counts <= CAP
    edge = (offsets < CAP) & ~whole
    edge_order = jnp.sum(jnp.where(edge[:, :, None], order, 0), axis=0)
    rank = jnp.sum((edge_order[:, :, None] < edge_order[:, None, :]).astype(jnp.int32), axis=1)
    early = offsets[:, :, None] + rank[None, :, :] < CAP
    return used & (whole[:, :, None] | (edge[:, :, None] & early))


def masked_softmax(logits, used):
    top = jnp.max(jnp.where(used, logits, -1e30), axis=-1, keepdims=True)
    powers = jnp.where(used, jnp.exp(logits - top), 0.0)
    return powers / jnp.sum(powers, axis=-1, keepdims=True)


def pair_codes(order_all, per_owner):
    expert_count = order_all.shape[1]
    first = lax.axis_index("ep") * per_owner
    turned = jnp.roll(order_all, -first, axis=1)
    kept = kept_pairs(turned[:, :per_owner])
    dropped = jnp.pad(~kept, ((0, 0), (0, expert_count - per_owner), (0, 0)))
    code = jnp.where(turned < LAST, dropped.astype(jnp.float32), -1.0)
    code = code.swapaxes(1, 2).reshape(-1, expert_count)
    lanes = -expert_count % 128
    return jnp.pad(code, ((0, 0), (0, lanes)), constant_values=-1.0).astype(jnp.bfloat16)


def run_experts(rows_all, cots_all, code, w_router, w_gate, w_up, w_down, by_links):
    per_owner, width, units = w_gate.shape
    expert_count = w_router.shape[0]
    ep_size, tp_size = lax.axis_size("ep"), lax.axis_size("tp")
    hidden = per_owner * units
    router = jnp.roll(w_router, -lax.axis_index("ep") * per_owner, axis=0)
    router = jnp.pad(router, ((0, -expert_count % 128), (0, 0)))
    enter = jnp.concatenate([w[e] for w in (w_gate, w_up) for e in range(per_owner)], axis=1)
    leave = w_down.reshape(hidden, width)
    if by_links:
        grads, sums, small, gate, up, down = experts_by_links(
            rows_all, cots_all, code, router, enter, leave, per_owner, ep_size
        )
        share = grads.shape[0]
        return (
            grads,
            sums,
            small[:, :per_owner].reshape(expert_count, share).T,
            gate,
            up,
            down.reshape(w_down.shape),
        )
    used, kept = code >= 0, (code == 0).astype(jnp.float32)
    logits = jnp.einsum("rd,ed->re", rows_all, router, preferred_element_type=jnp.float32)
    gates = jnp.repeat((kept * masked_softmax(logits, used))[:, :per_owner], units, axis=1)
    act = jnp.dot(rows_all, enter, preferred_element_type=jnp.float32)
    gate_act, up_act = act[:, :hidden], act[:, hidden:]
    back_act = jnp.einsum("rd,fd->rf", cots_all, leave, preferred_element_type=jnp.float32)
    sigma = jax.nn.sigmoid(gate_act)
    value = gate_act * sigma * up_act
    weighted = (gates * value).astype(jnp.bfloat16)
    grad_hidden = gates * back_act
    turned = jnp.concatenate(
        [
            grad_hidden * up_act * sigma * (1.0 + gate_act * (1.0 - sigma)),
            grad_hidden * gate_act * sigma,
        ],
        axis=1,
    ).astype(jnp.bfloat16)
    small = kept[:, :per_owner] * jnp.sum((value * back_act).reshape(-1, per_owner, units), axis=2)
    grads = jnp.einsum("rf,df->rd", turned, enter, preferred_element_type=jnp.float32)
    sums = jnp.dot(weighted, leave, preferred_element_type=jnp.float32)

    def scatter(value_rows):
        return lax.psum_scatter(value_rows, ("ep", "tp"), scatter_dimension=0, tiled=True)

    columns = lax.dynamic_update_slice_in_dim(
        jnp.zeros((small.shape[0], expert_count), jnp.float32),
        small,
        lax.axis_index("ep") * per_owner,
        1,
    )
    both = jnp.einsum(
        "rd,rwef->wedf",
        rows_all,
        turned.reshape(-1, 2, per_owner, units),
        preferred_element_type=jnp.float32,
    )
    down = jnp.einsum("rf,rd->fd", weighted, cots_all, preferred_element_type=jnp.float32)
    return (
        scatter(grads.astype(jnp.bfloat16)).astype(jnp.float32),
        scatter(sums.astype(jnp.bfloat16)).astype(jnp.float32),
        scatter(columns),
        both[0],
        both[1],
        down.reshape(w_down.shape),
    )


def visible_block(query_seg, query_pos, query_row, key_seg, key_pos, key_row):
    seg_q = query_seg[:, None]
    seg_k = key_seg[None, :]
    above = (
        (seg_k == seg_q)
        | (seg_k == 0)
        | (seg_k >= 1) & (seg_k <= 4) & (seg_q >= 5) & ((seg_q - 5) // 2 + 1 == seg_k)
    )
    same_tree = query_row[:, None] // TREE_TOKENS == key_row[None, :] // TREE_TOKENS
    return above & same_tree & (key_pos[None, :] <= query_pos[:, None])


def block_scores(query_part, key_rows, allowed, scale):
    scores = (
        jnp.einsum("qkgd,pkd->kgqp", query_part, key_rows, preferred_element_type=jnp.float32)
        * scale
    )
    return jnp.where(allowed[None, None], scores, -1e30)


def attend_forward(query_rows, key_rows, value_rows, segment, position):
    total_rows = query_rows.shape[0]
    scale = query_rows.shape[-1] ** (-0.5)
    row_ids = jnp.arange(total_rows, dtype=jnp.int32)
    allowed = visible_block(segment, position, row_ids, segment, position, row_ids)
    scores = block_scores(query_rows, key_rows, allowed, scale)
    top_score = jnp.max(scores, axis=-1, keepdims=True)
    weights = jnp.exp(scores - top_score)
    weight_sum = jnp.sum(weights, axis=-1, keepdims=True)
    probs = (weights / weight_sum).astype(jnp.bfloat16)
    outputs = jnp.einsum(
        "kgqp,pkd->qkgd", probs, value_rows, preferred_element_type=jnp.float32
    ).astype(jnp.bfloat16)
    log_sums = [top_score + jnp.log(weight_sum)]
    return (outputs, log_sums)


def attend_backward(
    query_rows, key_rows, value_rows, segment, position, log_sums, grad_heads, block_rows
):
    total_rows = query_rows.shape[0]
    scale = query_rows.shape[-1] ** (-0.5)
    row_ids = jnp.arange(total_rows, dtype=jnp.int32)
    grad_keys = jnp.zeros(key_rows.shape, jnp.float32)
    grad_values = jnp.zeros(value_rows.shape, jnp.float32)
    grad_query = []
    for number, first_row in enumerate(range(0, total_rows, block_rows)):
        allowed = visible_block(segment, position, row_ids, segment, position, row_ids)
        scores = block_scores(query_rows, key_rows, allowed, scale)
        probs = jnp.where(allowed[None, None], jnp.exp(scores - log_sums[number]), 0.0)
        grad_values = jnp.einsum(
            "kgqp,qkgd->pkd",
            probs.astype(jnp.bfloat16),
            grad_heads,
            preferred_element_type=jnp.float32,
        )
        grad_probs = jnp.einsum(
            "qkgd,pkd->kgqp", grad_heads, value_rows, preferred_element_type=jnp.float32
        )
        inner = jnp.sum(probs * grad_probs, axis=-1, keepdims=True)
        grad_scores = (probs * (grad_probs - inner)).astype(jnp.bfloat16)
        grad_query.append(
            jnp.einsum("kgqp,pkd->qkgd", grad_scores, key_rows, preferred_element_type=jnp.float32)
            * scale
        )
        grad_keys = (
            jnp.einsum(
                "kgqp,qkgd->pkd", grad_scores, query_rows, preferred_element_type=jnp.float32
            )
            * scale
        )
    return (grad_query[0], grad_keys, grad_values)


def local(
    hidden_in,
    gain_attn,
    w_query,
    key_projection_weight,
    value_projection_weight,
    w_out,
    gain_ffn,
    w_router,
    w_gate,
    w_up,
    w_down,
    expert_ids,
    slot_order,
    segment,
    position,
    cotangent,
):
    model_width = w_query.shape[1]
    head_width = HEAD_DIMENSION
    local_heads = w_query.shape[0] // head_width
    local_kv = key_projection_weight.shape[0] // head_width
    group_factor = local_heads // local_kv
    token_count = expert_ids.shape[0]
    share = hidden_in.shape[0]
    row_start = lax.axis_index("tp") * share
    expert_count = w_router.shape[0]
    per_owner = w_gate.shape[0]
    block_rows = 512
    by_links = lax.axis_size("tp") == 4 and lax.axis_size("ep") == 8
    order = pair_order(expert_ids, slot_order, expert_count)
    cot_all = gather_all(cotangent, False)
    inputs_own = hidden_in.astype(jnp.float32)
    gain_one = gain_attn.astype(jnp.float32)
    gain_two = gain_ffn.astype(jnp.float32)
    scale_one = norm_scale(inputs_own)
    first_own = (inputs_own * scale_one * gain_one).astype(jnp.bfloat16)
    if by_links:
        first_normalized, order_all = front_gather(first_own, order, lax.axis_size("ep"))
    else:
        first_normalized = group_rows(first_own, by_links, None)
        order_all = lax.all_gather(order, "ep")
    code = pair_codes(order_all, per_owner)
    cosine_lookup, sine_lookup = rope_tables(position, head_width)
    query_proj = jnp.einsum(
        "rd,fd->rf", first_normalized, w_query, preferred_element_type=jnp.float32
    ).reshape(token_count, local_heads, head_width)
    key_proj = jnp.einsum(
        "rd,fd->rf", first_normalized, key_projection_weight, preferred_element_type=jnp.float32
    ).reshape(token_count, local_kv, head_width)
    query_rows = (
        apply_rotation(query_proj, cosine_lookup, sine_lookup)
        .astype(jnp.bfloat16)
        .reshape(token_count, local_kv, group_factor, head_width)
    )
    key_rows = apply_rotation(key_proj, cosine_lookup, sine_lookup).astype(jnp.bfloat16)
    value_rows = (
        jnp.einsum(
            "rd,fd->rf",
            first_normalized,
            value_projection_weight,
            preferred_element_type=jnp.float32,
        )
        .astype(jnp.bfloat16)
        .reshape(token_count, local_kv, head_width)
    )
    head_outputs, log_sums = attend_forward(query_rows, key_rows, value_rows, segment, position)
    head_outputs = head_outputs.reshape(token_count, local_heads * head_width)
    middle_own = inputs_own + group_totals(
        jnp.dot(head_outputs, w_out, preferred_element_type=jnp.float32).astype(jnp.bfloat16),
        by_links,
        3,
    )
    scale_two = norm_scale(middle_own)
    normed_own = (middle_own * scale_two * gain_two).astype(jnp.bfloat16)
    normed_two = gather_all(normed_own, by_links)
    used = lax.dynamic_slice_in_dim(order, row_start, share, 1).T < LAST
    gates = masked_softmax(
        jnp.einsum("rd,ed->re", normed_own, w_router, preferred_element_type=jnp.float32), used
    )
    grad_normed_own, combined_own, grad_gates_own, grad_w_gate, grad_w_up, grad_w_down = (
        run_experts(normed_two, cot_all, code, w_router, w_gate, w_up, w_down, by_links)
    )
    output_own = (middle_own + combined_own).astype(jnp.bfloat16)
    inner_gate = jnp.sum(gates * grad_gates_own, axis=-1, keepdims=True)
    grad_logits = gates * (grad_gates_own - inner_gate)
    router_f = w_router.astype(jnp.float32)
    grad_normed_own = grad_normed_own + jnp.dot(grad_logits, router_f, precision=EXACT_PRECISION)
    grad_router = jnp.dot(grad_logits.T, normed_own.astype(jnp.float32), precision=EXACT_PRECISION)
    grad_gain_ffn = jnp.sum(grad_normed_own * middle_own * scale_two, axis=0)
    grad_middle = cotangent.astype(jnp.float32) + norm_back(
        middle_own, scale_two, gain_two, grad_normed_own
    )
    grad_attn = group_rows(grad_middle.astype(jnp.bfloat16), by_links, 7)
    grad_w_out = jnp.einsum(
        "rf,rd->fd", head_outputs, grad_attn, preferred_element_type=jnp.float32
    )
    grad_w_out = lax.psum(grad_w_out.astype(jnp.bfloat16), "ep").astype(jnp.float32)
    grad_heads = (
        jnp.einsum("rd,fd->rf", grad_attn, w_out, preferred_element_type=jnp.float32)
        .astype(jnp.bfloat16)
        .reshape(token_count, local_kv, group_factor, head_width)
    )
    grad_query, grad_keys, grad_values = attend_backward(
        query_rows, key_rows, value_rows, segment, position, log_sums, grad_heads, block_rows
    )
    grad_query_proj = (
        rotate_back(
            grad_query.reshape(token_count, local_heads, head_width), cosine_lookup, sine_lookup
        )
        .astype(jnp.bfloat16)
        .reshape(token_count, local_heads * head_width)
    )
    grad_key_proj = (
        rotate_back(grad_keys, cosine_lookup, sine_lookup)
        .astype(jnp.bfloat16)
        .reshape(token_count, local_kv * head_width)
    )
    grad_value_proj = grad_values.astype(jnp.bfloat16).reshape(token_count, local_kv * head_width)
    grad_w_query = jnp.einsum(
        "rf,rd->fd", grad_query_proj, first_normalized, preferred_element_type=jnp.float32
    )
    grad_w_key = jnp.einsum(
        "rf,rd->fd", grad_key_proj, first_normalized, preferred_element_type=jnp.float32
    )
    grad_w_value = jnp.einsum(
        "rf,rd->fd", grad_value_proj, first_normalized, preferred_element_type=jnp.float32
    )
    grad_normed_one = jnp.einsum(
        "rf,fd->rd", grad_query_proj, w_query, preferred_element_type=jnp.float32
    )
    grad_normed_one = grad_normed_one + jnp.einsum(
        "rf,fd->rd", grad_key_proj, key_projection_weight, preferred_element_type=jnp.float32
    )
    grad_normed_one = grad_normed_one + jnp.einsum(
        "rf,fd->rd", grad_value_proj, value_projection_weight, preferred_element_type=jnp.float32
    )
    grad_gain_attn = jnp.sum(grad_normed_one * first_normalized.astype(jnp.float32), axis=0)
    small = jnp.concatenate(
        [grad_router, grad_gain_ffn[None, :], (grad_gain_attn / gain_one)[None, :]], axis=0
    )
    (grad_w_query, grad_w_key, grad_w_value), grad_one_own, small = tail_totals(
        [g.astype(jnp.bfloat16) for g in (grad_w_query, grad_w_key, grad_w_value)],
        grad_normed_one.astype(jnp.bfloat16),
        small,
        by_links,
    )
    grad_router = small[:expert_count]
    grad_gain_ffn, grad_gain_attn = small[expert_count], small[expert_count + 1]
    grad_input = grad_middle + norm_back(inputs_own, scale_one, gain_one, grad_one_own)
    return (
        output_own,
        grad_input,
        grad_gain_attn,
        grad_w_query,
        grad_w_key,
        grad_w_value,
        grad_w_out,
        grad_gain_ffn,
        grad_router,
        grad_w_gate,
        grad_w_up,
        grad_w_down,
    )


def solution(mesh):
    placed = (
        P(("ep", "tp"), None),
        P(),
        P("tp", None),
        P("tp", None),
        P("tp", None),
        P("tp", None),
        P(),
        P(),
        P("ep", None, "tp"),
        P("ep", None, "tp"),
        P("ep", "tp", None),
        P("ep", None),
        P("ep", None),
        P("ep"),
        P("ep"),
        P(("ep", "tp"), None),
    )
    return jax.shard_map(
        local,
        mesh=mesh,
        in_specs=placed,
        out_specs=(
            P(("ep", "tp"), None),
            P(("ep", "tp"), None),
            P(),
            P("tp", None),
            P("tp", None),
            P("tp", None),
            P("tp", None),
            P(),
            P(),
            P("ep", None, "tp"),
            P("ep", None, "tp"),
            P("ep", "tp", None),
        ),
        check_vma=False,
    )
```

```python
import functools

import jax
import jax.numpy as jnp
from jax import lax
from jax.experimental import pallas as pl
from jax.experimental.pallas import tpu as pltpu
from jax.sharding import PartitionSpec as P

HEAD_DIMENSION = 64
TREE_TOKENS = 512
CAP = 2304


EPSILON = 1e-06
ROPE_BASE = 10000.0
EXACT_PRECISION = lax.Precision.HIGHEST


def rope_tables(position, head_width):
    half_width = head_width // 2
    freqs = ROPE_BASE ** (-(jnp.arange(half_width, dtype=jnp.float32) * 2.0 / head_width))
    angle = position.astype(jnp.float32)[:, None] * freqs[None, :]
    return (jnp.cos(angle)[:, None, :], jnp.sin(angle)[:, None, :])


def apply_rotation(value_rows, cosine_lookup, sine_lookup):
    half_width = value_rows.shape[-1] // 2
    first = value_rows[..., :half_width]
    second = value_rows[..., half_width:]
    return jnp.concatenate(
        [
            first * cosine_lookup - second * sine_lookup,
            first * sine_lookup + second * cosine_lookup,
        ],
        axis=-1,
    )


def rotate_back(grads, cosine_lookup, sine_lookup):
    half_width = grads.shape[-1] // 2
    first = grads[..., :half_width]
    second = grads[..., half_width:]
    return jnp.concatenate(
        [
            first * cosine_lookup + second * sine_lookup,
            second * cosine_lookup - first * sine_lookup,
        ],
        axis=-1,
    )


def norm_scale(value_rows):
    return lax.rsqrt(jnp.mean(value_rows * value_rows, axis=-1, keepdims=True) + EPSILON)


def norm_back(value_rows, scale, gain, grad_normed):
    weighted = grad_normed * gain
    inner = jnp.mean(value_rows * weighted, axis=-1, keepdims=True)
    grad_values = scale * weighted - value_rows * (scale * scale * scale) * inner
    return grad_values


MESH = pl.DeviceIdType.MESH


class Place:
    def __init__(self, ep_size):
        self.depth = ep_size // 2
        ep, tp = lax.axis_index("ep"), lax.axis_index("tp")
        self.z, self.y = ep // 2, ep % 2
        self.x, self.c = tp // 2, tp % 2

    def device(self, z=None, y=None, x=None, c=None):
        z = self.z if z is None else z
        y = self.y if y is None else y
        x = self.x if x is None else x
        c = self.c if c is None else c
        return (z * 2 + y, x * 2 + c)

    def sibling(self):
        return self.device(c=1 - self.c)

    def x_peer(self):
        return self.device(x=1 - self.x)

    def y_peer(self):
        return self.device(y=1 - self.y)

    def after(self, step):
        return lax.rem(self.z + step, self.depth)

    def before(self, step):
        return lax.rem(self.z + self.depth - step, self.depth)


def meet(devices):
    barrier = pltpu.get_barrier_semaphore()
    for device in devices:
        pl.semaphore_signal(barrier, inc=1, device_id=device, device_id_type=MESH)
    pl.semaphore_wait(barrier, len(devices))


def send(src, dst, send_sem, recv_sem, device):
    copy = pltpu.make_async_remote_copy(
        src_ref=src,
        dst_ref=dst,
        send_sem=send_sem,
        recv_sem=recv_sem,
        device_id=device,
        device_id_type=MESH,
    )
    copy.start()
    return copy


def gather_kernel(ep_size, own, out, own_sem, z_sems, pair_sems, core_sems):
    me = Place(ep_size)
    depth = me.depth
    half = own.shape[0] // 2
    z_send, z_recv = z_sems.at[0], z_sems.at[1]
    pair_send, pair_recv = pair_sems.at[0], pair_sems.at[1]
    core_send, core_recv = core_sems.at[0], core_sems.at[1]
    meet(
        [me.sibling(), me.x_peer(), me.y_peer()]
        + [me.device(z=me.after(s)) for s in range(1, depth)]
    )

    def rows(part):
        return pl.ds(part * half, half)

    def block(step, y, x, part, c=None):
        return out.at[me.before(step), y, x, me.c if c is None else c, rows(part)]

    started = []

    def forward(source, target, sems, slot, device):
        started.append(send(source, target, sems[0].at[slot], sems[1].at[slot], device))

    for s in range(1, depth):
        for part in range(2):
            forward(
                own.at[rows(part)],
                out.at[me.z, me.y, me.x, me.c, rows(part)],
                (z_send, z_recv),
                (s - 1) * 2 + part,
                me.device(z=me.after(s)),
            )
    local = pltpu.make_async_copy(own, out.at[me.z, me.y, me.x, me.c], own_sem)
    local.start()
    local.wait()

    kinds = [
        (me.y, me.x, 0),
        (me.y, me.x, 1),
        (1 - me.y, me.x, 0),
        (me.y, 1 - me.x, 1),
        (1 - me.y, me.x, 1),
        (1 - me.y, 1 - me.x, 1),
        (me.y, 1 - me.x, 0),
        (1 - me.y, 1 - me.x, 0),
    ]
    x_route = {0: 6, 2: 7, 1: 3}
    y_route = {0: 2, 1: 4, 3: 5}

    def landed(step, kind):
        y, x, part = kinds[kind]
        place = block(step, y, x, part)
        if kind < 2:
            if step > 0:
                sem = z_recv.at[(step - 1) * 2 + part]
                pltpu.make_async_copy(place, place, sem).wait()
        else:
            pltpu.make_async_copy(place, place, pair_recv.at[step * 8 + kind]).wait()

    def pass_on(step, kind):
        y, x, part = kinds[kind]
        place = block(step, y, x, part)
        if kind in x_route:
            forward(place, place, (pair_send, pair_recv), step * 8 + x_route[kind], me.x_peer())
        if kind in y_route:
            forward(place, place, (pair_send, pair_recv), step * 8 + y_route[kind], me.y_peer())
        forward(place, place, (core_send, core_recv), step * 8 + kind, me.sibling())

    for turn in range(depth + 2):
        for step, group in ((turn, (0, 1)), (turn - 1, (2, 3)), (turn - 2, (4, 5, 6, 7))):
            if 0 <= step < depth:
                for kind in group:
                    landed(step, kind)
                    pass_on(step, kind)
    for step in range(depth):
        for kind in range(8):
            y, x, part = kinds[kind]
            place = block(step, y, x, part, 1 - me.c)
            pltpu.make_async_copy(place, place, core_recv.at[step * 8 + kind]).wait()
    for copy in started:
        copy.wait_send()


def gather_by_links(value_rows, ep_size):
    rows, width = value_rows.shape
    depth = ep_size // 2
    dma = pltpu.SemaphoreType.DMA
    every = pl.pallas_call(
        functools.partial(gather_kernel, ep_size),
        out_shape=jax.ShapeDtypeStruct((depth, 2, 2, 2, rows, width), value_rows.dtype),
        in_specs=[pl.BlockSpec(memory_space=pl.ANY)],
        out_specs=pl.BlockSpec(memory_space=pl.ANY),
        scratch_shapes=[
            dma,
            dma((2, 2 * depth - 2)),
            dma((2, 8 * depth)),
            dma((2, 8 * depth)),
        ],
        compiler_params=pltpu.CompilerParams(collective_id=1, has_side_effects=True),
        name="gather_by_links",
    )(value_rows)
    return every.reshape(-1, width)


def add_into(target, other):
    def tile(i, carry):
        at = pl.ds(pl.multiple_of(i * 16, 16), 16)
        target[at, :] = target[at, :] + other[at, :]
        return carry

    lax.fori_loop(0, target.shape[0] // 16, tile, 0)


def front_gather_kernel(
    ep_size, pieces, own, table, out, tables, own_sem, sems, table_own_sem, table_sems
):
    me = Place(ep_size)
    mine = lax.axis_index("ep")
    tp = lax.axis_index("tp")
    peers = [(lax.rem(mine + k, ep_size), tp) for k in range(1, ep_size)]
    meet([me.sibling(), me.x_peer()] + peers)
    local = pltpu.make_async_copy(table, tables.at[mine], table_own_sem)
    local.start()
    copies = [
        send(table, tables.at[mine], table_sems.at[0, k], table_sems.at[1, k], device)
        for k, device in enumerate(peers)
    ]
    group_gather_body(me, pieces, own, out, own_sem, sems)
    local.wait()
    for copy in copies:
        copy.wait()


def front_gather(value_rows, table, ep_size):
    rows, width = value_rows.shape
    pieces = 4
    dma = pltpu.SemaphoreType.DMA
    anywhere = pl.BlockSpec(memory_space=pl.ANY)
    every, tables = pl.pallas_call(
        functools.partial(front_gather_kernel, ep_size, pieces),
        out_shape=(
            jax.ShapeDtypeStruct((2, 2, rows, width), value_rows.dtype),
            jax.ShapeDtypeStruct((ep_size,) + table.shape, table.dtype),
        ),
        in_specs=[anywhere] * 2,
        out_specs=(anywhere,) * 2,
        scratch_shapes=[dma, dma((2, 3 * pieces)), dma, dma((2, ep_size - 1))],
        compiler_params=pltpu.CompilerParams(collective_id=6, has_side_effects=True),
        name="front_gather",
    )(value_rows, table)
    return every.reshape(-1, width), tables


def group_gather_kernel(ep_size, pieces, own, out, own_sem, sems):
    me = Place(ep_size)
    meet([me.sibling(), me.x_peer()])
    group_gather_body(me, pieces, own, out, own_sem, sems)


def group_gather_body(me, pieces, own, out, own_sem, sems):
    size = own.shape[0] // pieces
    started = []
    local = pltpu.make_async_copy(own, out.at[me.x, me.c], own_sem)
    local.start()

    def at(p):
        return pl.ds(p * size, size)

    def go(kind, p, src, dst, device):
        slot = kind * pieces + p
        started.append(send(src, dst, sems.at[0, slot], sems.at[1, slot], device))

    for p in range(pieces):
        go(0, p, own.at[at(p)], out.at[me.x, me.c, at(p)], me.x_peer())
    for p in range(pieces):
        go(1, p, own.at[at(p)], out.at[me.x, me.c, at(p)], me.sibling())
    for p in range(pieces):
        block = out.at[1 - me.x, me.c, at(p)]
        pltpu.make_async_copy(block, block, sems.at[1, p]).wait()
        go(2, p, block, block, me.sibling())
    for p in range(pieces):
        for kind, x in ((1, me.x), (2, 1 - me.x)):
            block = out.at[x, 1 - me.c, at(p)]
            pltpu.make_async_copy(block, block, sems.at[1, kind * pieces + p]).wait()
    local.wait()
    for copy in started:
        copy.wait_send()


def group_gather(value_rows, ep_size, call):
    rows, width = value_rows.shape
    pieces = 4
    dma = pltpu.SemaphoreType.DMA
    every = pl.pallas_call(
        functools.partial(group_gather_kernel, ep_size, pieces),
        out_shape=jax.ShapeDtypeStruct((2, 2, rows, width), value_rows.dtype),
        in_specs=[pl.BlockSpec(memory_space=pl.ANY)],
        out_specs=pl.BlockSpec(memory_space=pl.ANY),
        scratch_shapes=[dma, dma((2, 3 * pieces))],
        compiler_params=pltpu.CompilerParams(collective_id=call, has_side_effects=True),
        name="group_gather",
    )(value_rows)
    return every.reshape(-1, width)


class GroupTotal:
    def __init__(self, me, parts, core_got, pair_got, sems):
        self.me, self.parts, self.core_got, self.pair_got = me, parts, core_got, pair_got
        self.core = [
            pltpu.make_async_remote_copy(
                src_ref=parts.at[x, 1 - me.c],
                dst_ref=core_got.at[x],
                send_sem=sems.at[0, k],
                recv_sem=sems.at[1, k],
                device_id=me.sibling(),
                device_id_type=MESH,
            )
            for k, x in enumerate((1 - me.x, me.x))
        ]
        self.pair = pltpu.make_async_remote_copy(
            src_ref=core_got.at[1 - me.x],
            dst_ref=pair_got,
            send_sem=sems.at[0, 2],
            recv_sem=sems.at[1, 2],
            device_id=me.x_peer(),
            device_id_type=MESH,
        )

    def begin(self):
        for copy in self.core:
            copy.start()

    def exchange(self):
        self.core[0].wait_recv()
        far = 1 - self.me.x
        add_into(self.core_got.at[far], self.parts.at[far, self.me.c])
        self.pair.start()

    def finish(self, out):
        self.core[1].wait_recv()
        self.pair.wait_recv()

        def tile(i, carry):
            at = pl.ds(pl.multiple_of(i * 16, 16), 16)
            out[at, :] = (
                self.parts[self.me.x, self.me.c, at, :].astype(jnp.float32)
                + self.core_got[self.me.x, at, :].astype(jnp.float32)
                + self.pair_got[at, :].astype(jnp.float32)
            )
            return carry

        lax.fori_loop(0, out.shape[0] // 16, tile, 0)

    def sent(self):
        for copy in self.core + [self.pair]:
            copy.wait_send()


def group_total_kernel(ep_size, parts, out, core_got, pair_got, sems):
    me = Place(ep_size)
    meet([me.sibling(), me.x_peer()])
    total = GroupTotal(me, parts, core_got, pair_got, sems)
    total.begin()
    total.exchange()
    total.finish(out)
    total.sent()


def group_total(value_rows, ep_size, call):
    rows, width = value_rows.shape[0] // 4, value_rows.shape[1]
    vmem = pl.BlockSpec(memory_space=pltpu.VMEM)
    return pl.pallas_call(
        functools.partial(group_total_kernel, ep_size),
        out_shape=jax.ShapeDtypeStruct((rows, width), jnp.float32),
        in_specs=[vmem],
        out_specs=vmem,
        scratch_shapes=[
            pltpu.VMEM((2, rows, width), jnp.bfloat16),
            pltpu.VMEM((rows, width), jnp.bfloat16),
            pltpu.SemaphoreType.DMA((2, 3)),
        ],
        compiler_params=pltpu.CompilerParams(
            collective_id=call, has_side_effects=True, vmem_limit_bytes=32 * 1024 * 1024
        ),
        name="group_total",
    )(value_rows.reshape(2, 2, rows, width))


def all_others(ep_size):
    ep, tp = lax.axis_index("ep"), lax.axis_index("tp")
    return [
        (lax.rem(ep + k // 4, ep_size), lax.rem(tp + k % 4, 4)) for k in range(1, ep_size * 4)
    ]


def experts_kernel(
    ep_size,
    per_owner,
    rows_in,
    cots_in,
    code_in,
    router,
    enter,
    leave,
    grad_out,
    sum_out,
    small_out,
    gate_out,
    up_out,
    down_out,
    rows_buf,
    cots_buf,
    weighted,
    turned,
    enter_sum,
    parts,
    core_got,
    pair_got,
    last_got,
    z_got,
    small_in,
    small_got,
    load_sems,
    core_sems,
    pair_sems,
    last_sems,
    z_sems,
    small_sems,
    own_sem,
):
    me = Place(ep_size)
    depth = me.depth
    steps = 2 * depth
    blocks = 2 * steps
    width = router.shape[1]
    share = rows_buf.shape[2]
    tokens = 4 * share
    units = leave.shape[0] // per_owner
    hidden = per_owner * units
    f32, bf16 = jnp.float32, jnp.bfloat16
    others = all_others(ep_size)
    meet(others)
    my_place = lax.axis_index("ep") * 4 + lax.axis_index("tp")

    def where(b):
        return me.after(b // 4 + 1), lax.rem(1 - me.y + b % 2, 2)

    def half(b):
        return pl.ds(pl.multiple_of(b // 2 % 2 * share, share), share)

    def load(b, which):
        z, y = where(b)
        source, target = ((rows_in, rows_buf), (cots_in, cots_buf))[which]
        slot = lax.rem(b, 2)
        return pltpu.make_async_copy(
            source.at[z, y, :, half(b)], target.at[slot], load_sems.at[slot, which]
        )

    def core_copy(b):
        y = where(b)[1]
        return pltpu.make_async_remote_copy(
            src_ref=parts.at[lax.rem(b, 2), :, :, 1 - me.c],
            dst_ref=core_got.at[b // 2, y],
            send_sem=core_sems.at[0, b],
            recv_sem=core_sems.at[1, b],
            device_id=me.sibling(),
            device_id_type=MESH,
        )

    def grad_pair(b):
        y = where(b)[1]
        return pltpu.make_async_remote_copy(
            src_ref=core_got.at[b // 2, y, 0, 1 - me.x],
            dst_ref=pair_got.at[b // 2, 0, y],
            send_sem=pair_sems.at[0, b],
            recv_sem=pair_sems.at[1, b],
            device_id=me.x_peer(),
            device_id_type=MESH,
        )

    def sum_pair(step):
        return pltpu.make_async_remote_copy(
            src_ref=core_got.at[step, 1 - me.y, 1],
            dst_ref=pair_got.at[step, 1],
            send_sem=pair_sems.at[0, blocks + step],
            recv_sem=pair_sems.at[1, blocks + step],
            device_id=me.y_peer(),
            device_id_type=MESH,
        )

    def last_copy(step, which):
        return pltpu.make_async_remote_copy(
            src_ref=pair_got.at[step, which, (1 - me.y, 1 - me.x)[which]],
            dst_ref=last_got.at[step, which],
            send_sem=last_sems.at[0, step, which],
            recv_sem=last_sems.at[1, step, which],
            device_id=(me.y_peer(), me.x_peer())[which],
            device_id_type=MESH,
        )

    def z_copy(step, which):
        return pltpu.make_async_remote_copy(
            src_ref=last_got.at[step, which],
            dst_ref=z_got.at[step, which],
            send_sem=z_sems.at[0, step, which],
            recv_sem=z_sems.at[1, step, which],
            device_id=me.device(z=me.after(step // 2 + 1)),
            device_id_type=MESH,
        )

    def small_copy(k, device):
        return pltpu.make_async_remote_copy(
            src_ref=small_in.at[device[0] * 4 + device[1]],
            dst_ref=small_got.at[my_place],
            send_sem=small_sems.at[0, k],
            recv_sem=small_sems.at[1, k],
            device_id=device,
            device_id_type=MESH,
        )

    def dot(a, b, contract):
        return lax.dot_general(
            a, b, ((contract[:1], contract[1:]), ((), ())), preferred_element_type=f32
        )

    def spread(columns):
        return jnp.concatenate(
            [jnp.broadcast_to(columns[:, e : e + 1], (tokens, units)) for e in range(per_owner)],
            axis=1,
        )

    def compute(b):
        z, y = where(b)
        slot = lax.rem(b, 2)
        rows = rows_buf[slot].reshape(tokens, width)
        cots = cots_buf[slot].reshape(tokens, width)
        code = code_in[z * 2 + y, :, half(b), :].astype(f32).reshape(tokens, -1)
        used = code >= 0.0
        logits = jnp.where(used, dot(rows, router[...], (1, 1)), -1e30)
        top = jnp.max(logits, axis=1, keepdims=True)
        powers = jnp.where(used, jnp.exp(logits - top), 0.0)
        kept = jnp.where(code == 0.0, 1.0, 0.0)
        gates = spread(kept * powers / jnp.sum(powers, axis=1, keepdims=True))
        act = dot(rows, enter[...], (1, 0))
        gate_act, up_act = act[:, :hidden], act[:, hidden:]
        back_act = dot(cots, leave[...], (1, 1))
        sigma = jax.nn.sigmoid(gate_act)
        swish = gate_act * sigma
        value = swish * up_act
        gate_parts = spread(kept) * (value * back_act)
        lane = lax.broadcasted_iota(jnp.int32, (8, hidden), 1)
        pick = lax.broadcasted_iota(jnp.int32, (8, hidden), 0)
        mine = jnp.where((lane >= pick * units) & (lane < (pick + 1) * units), 1.0, 0.0)
        grad_gates = lax.dot_general(
            mine,
            gate_parts,
            (((1,), (1,)), ((), ())),
            precision=EXACT_PRECISION,
            preferred_element_type=f32,
        )
        for k in range(4):
            small_in[(z * 2 + y) * 4 + k, b // 2 % 2, :, :share] = grad_gates[
                :, k * share : (k + 1) * share
            ]
        weighted[...] = (gates * value).astype(bf16)
        grad_hidden = gates * back_act
        turned[:, :hidden] = (
            grad_hidden * up_act * sigma * (1.0 + gate_act * (1.0 - sigma))
        ).astype(bf16)
        turned[:, hidden:] = (grad_hidden * swish).astype(bf16)
        tile = 512
        for n in range(width // tile):
            cols = slice(n * tile, (n + 1) * tile)
            grads = dot(turned[...], enter[cols, :], (1, 1)).astype(bf16)
            sums = dot(weighted[...], leave[:, cols], (1, 0)).astype(bf16)
            for x in range(2):
                for c in range(2):
                    at = slice((x * 2 + c) * share, (x * 2 + c + 1) * share)
                    parts[slot, 0, x, c, :, cols] = grads[at]
                    parts[slot, 1, x, c, :, cols] = sums[at]

    def weight_sums(b):
        slot = lax.rem(b, 2)
        tile = 512
        for n in range(width // tile):
            cols = slice(n * tile, (n + 1) * tile)
            rows = rows_buf[slot, :, :, cols].reshape(tokens, tile)
            cots = cots_buf[slot, :, :, cols].reshape(tokens, tile)
            enter_sum[:, cols] += dot(turned[...], rows, (0, 0))
            down_out[:, cols] += dot(weighted[...], cots, (0, 0))

    enter_sum[...] = jnp.zeros_like(enter_sum)
    down_out[...] = jnp.zeros_like(down_out)
    small_in[...] = jnp.zeros_like(small_in)
    for which in range(2):
        load(0, which).start()

    def during(i, lag, body, even=False):
        b = i - lag
        inside = (b >= 0) & (b < blocks)
        if even:
            inside &= b % 2 == 0
        pl.when(inside)(lambda: body(b))

    def finish_sum(which):
        def body(b):
            step = b // 2
            last_copy(step, which).wait_recv()
            add_into(last_got.at[step, which], pair_got.at[step, which, (me.y, me.x)[which]])

            @pl.when(step < steps - 2)
            def _():
                z_copy(step, which).start()

        return body

    def work(b):
        for which in range(2):
            load(b, which).wait()

        @pl.when(b + 1 < blocks)
        def _():
            for which in range(2):
                load(b + 1, which).start()

        compute(b)
        core_copy(b).start()
        weight_sums(b)

    def core_sum(b):
        y = where(b)[1]
        core_copy(b).wait_recv()
        for which in range(2):
            for x in range(2):
                add_into(
                    core_got.at[b // 2, y, which, x], parts.at[lax.rem(b, 2), which, x, me.c]
                )
        grad_pair(b).start()

        @pl.when(b % 2 == 0)
        def _():
            sum_pair(b // 2).start()

        core_copy(b).wait_send()

    def out_pair(b):
        step = b // 2
        sum_pair(step).wait_recv()
        for x in range(2):
            add_into(pair_got.at[step, 1, x], core_got.at[step, me.y, 1, x])
        last_copy(step, 1).start()

    def back_pair(b):
        y = where(b)[1]
        step = b // 2
        grad_pair(b).wait_recv()
        add_into(pair_got.at[step, 0, y], core_got.at[step, y, 0, me.x])

        @pl.when(b % 2 == 0)
        def _():
            last_copy(step, 0).start()

    def small_send(b):
        for k, device in enumerate(others):
            small_copy(k, device).start()
        pltpu.make_async_copy(small_in.at[my_place], small_got.at[my_place], own_sem).start()
        for e in range(per_owner):
            gate_out[e] = enter_sum[e * units : (e + 1) * units, :].T
            up_out[e] = enter_sum[hidden + e * units : hidden + (e + 1) * units, :].T

    def turn(i, carry):
        during(i, 6, finish_sum(1), True)
        during(i, 0, work)
        during(i, 1, core_sum)
        during(i, 7, finish_sum(0), True)
        during(i, 3, out_pair, True)
        during(i, 4, back_pair)
        pl.when(i == blocks)(lambda: small_send(i))
        return carry

    lax.fori_loop(0, blocks + 7, turn, 0)
    pltpu.make_async_copy(small_in.at[my_place], small_got.at[my_place], own_sem).wait()
    for k, device in enumerate(others):
        small_copy(k, device).wait()
    for ep in range(ep_size):
        total = small_got[ep * 4]
        for tp in range(1, 4):
            total = total + small_got[ep * 4 + tp]
        small_out[ep] = total
    for step in range(steps - 2):
        for which in range(2):
            z_copy(step, which).wait_recv()

    def finish(which, part, target):
        def tile(i, carry):
            at = pl.multiple_of(i * 16, 16)
            total = last_got[steps - 2 + part, which, pl.ds(at, 16), :].astype(f32)
            for step in range(depth - 1):
                total = total + z_got[2 * step + part, which, pl.ds(at, 16), :].astype(f32)
            target[pl.ds(part * share + at, 16), :] = total
            return carry

        lax.fori_loop(0, share // 16, tile, 0)

    for part in range(2):
        finish(0, part, grad_out)
        finish(1, part, sum_out)

    def sent(step, carry):
        grad_pair(2 * step).wait_send()
        grad_pair(2 * step + 1).wait_send()
        sum_pair(step).wait_send()
        for which in range(2):
            last_copy(step, which).wait_send()

        @pl.when(step < steps - 2)
        def _():
            for which in range(2):
                z_copy(step, which).wait_send()

        return carry

    lax.fori_loop(0, steps, sent, 0)


def experts_by_links(rows_all, cots_all, code, router, enter, leave, per_owner, ep_size):
    total_rows, width = rows_all.shape
    depth = ep_size // 2
    tokens = total_rows // ep_size
    rows = tokens // 4
    half, steps = rows // 2, 2 * depth
    hidden = leave.shape[0]
    units = hidden // per_owner
    bf16, f32 = jnp.bfloat16, jnp.float32
    dma = pltpu.SemaphoreType.DMA
    vmem = pl.BlockSpec(memory_space=pltpu.VMEM)
    anywhere = pl.BlockSpec(memory_space=pl.ANY)
    places = 4 * ep_size
    blocks = (depth, 2, 4, rows, width)
    return pl.pallas_call(
        functools.partial(experts_kernel, ep_size, per_owner),
        out_shape=(
            jax.ShapeDtypeStruct((rows, width), f32),
            jax.ShapeDtypeStruct((rows, width), f32),
            jax.ShapeDtypeStruct((ep_size, 2, 8, 128), f32),
            jax.ShapeDtypeStruct((per_owner, width, units), f32),
            jax.ShapeDtypeStruct((per_owner, width, units), f32),
            jax.ShapeDtypeStruct((hidden, width), f32),
        ),
        in_specs=[anywhere, anywhere, vmem, vmem, vmem, vmem],
        out_specs=(vmem,) * 6,
        scratch_shapes=[
            pltpu.VMEM((2, 4, half, width), bf16),
            pltpu.VMEM((2, 4, half, width), bf16),
            pltpu.VMEM((4 * half, hidden), bf16),
            pltpu.VMEM((4 * half, 2 * hidden), bf16),
            pltpu.VMEM((2 * hidden, width), f32),
            pltpu.VMEM((2, 2, 2, 2, half, width), bf16),
            pltpu.VMEM((steps, 2, 2, 2, half, width), bf16),
            pltpu.VMEM((steps, 2, 2, half, width), bf16),
            pltpu.VMEM((steps, 2, half, width), bf16),
            pltpu.VMEM((steps - 2, 2, half, width), bf16),
            pltpu.VMEM((places, 2, 8, 128), f32),
            pltpu.VMEM((places, 2, 8, 128), f32),
            dma((2, 2)),
            dma((2, 2 * steps)),
            dma((2, 3 * steps)),
            dma((2, steps, 2)),
            dma((2, steps - 2, 2)),
            dma((2, places - 1)),
            dma,
        ],
        compiler_params=pltpu.CompilerParams(
            collective_id=2, has_side_effects=True, vmem_limit_bytes=60 * 1024 * 1024
        ),
        name="experts_by_links",
    )(
        rows_all.reshape(blocks),
        cots_all.reshape(blocks),
        code.reshape(ep_size, 4, rows, -1),
        router,
        enter,
        leave,
    )


def tail_kernel(
    ep_size,
    counts,
    *refs,
):
    n = len(counts)
    grads, rows_in, small_in = refs[:n], refs[n], refs[n + 1]
    outs, rows_out, small_out = refs[n + 2 : 2 * n + 2], refs[2 * n + 2], refs[2 * n + 3]
    (
        y_got,
        z_got,
        final,
        core_got,
        pair_got,
        small_got,
        small_sum,
        y_sems,
        z_sems,
        fz_sems,
        fy_sems,
        group_sems,
        small_sems,
        spread_sems,
        own_sem,
    ) = refs[2 * n + 4 :]
    me = Place(ep_size)
    depth = me.depth
    starts = [sum(counts[:i]) for i in range(n)]
    others = all_others(ep_size)
    meet(others)
    my_place = lax.axis_index("ep") * 4 + lax.axis_index("tp")

    def y_copy(step, i):
        return pltpu.make_async_remote_copy(
            src_ref=grads[i].at[me.after(step + 1), 1 - me.y],
            dst_ref=y_got.at[step, pl.ds(starts[i], counts[i])],
            send_sem=y_sems.at[0, step, i],
            recv_sem=y_sems.at[1, step, i],
            device_id=me.y_peer(),
            device_id_type=MESH,
        )

    def z_copy(step):
        return pltpu.make_async_remote_copy(
            src_ref=y_got.at[step],
            dst_ref=z_got.at[step],
            send_sem=z_sems.at[0, step],
            recv_sem=z_sems.at[1, step],
            device_id=me.device(z=me.after(step + 1)),
            device_id_type=MESH,
        )

    for step in range(depth):
        for i in range(n):
            y_copy(step, i).start()
    group = GroupTotal(me, rows_in, core_got, pair_got, group_sems)
    group.begin()
    small = [
        send(
            small_in.at[device[0] * 4 + device[1]],
            small_got.at[my_place],
            small_sems.at[0, k],
            small_sems.at[1, k],
            device,
        )
        for k, device in enumerate(others)
    ]
    own_small = pltpu.make_async_copy(small_in.at[my_place], small_got.at[my_place], own_sem)
    own_small.start()
    group.exchange()

    def y_sum(step):
        for i in range(n):
            y_copy(step, i).wait_recv()
            add_into(
                y_got.at[step, pl.ds(starts[i], counts[i])],
                grads[i].at[me.after(step + 1), me.y],
            )

    for step in range(depth - 1):
        y_sum(step)
        z_copy(step).start()
    own_small.wait()
    for copy in small:
        copy.wait_recv()
    total = small_got[0]
    for k in range(1, 4 * ep_size):
        total = total + small_got[k]
    small_sum[...] = total
    spread = [
        send(
            small_sum,
            small_out.at[my_place],
            spread_sems.at[0, k],
            spread_sems.at[1, k],
            device,
        )
        for k, device in enumerate(others)
    ]
    small_out[my_place] = total
    group.finish(rows_out)
    y_sum(depth - 1)
    for step in range(depth - 1):
        z_copy(step).wait_recv()

    def tile(i, carry):
        at = pl.ds(pl.multiple_of(i * 16, 16), 16)
        value = y_got[depth - 1, at, :].astype(jnp.float32)
        for step in range(depth - 1):
            value = value + z_got[step, at, :].astype(jnp.float32)
        final[me.z, me.y, at, :] = value.astype(final.dtype)
        return carry

    lax.fori_loop(0, sum(counts) // 16, tile, 0)
    mine = final.at[me.z, me.y]
    finals = []
    for s in range(1, depth):
        finals.append(
            send(mine, mine, fz_sems.at[0, s], fz_sems.at[1, s], me.device(z=me.after(s)))
        )
    finals.append(send(mine, mine, fy_sems.at[0, 0], fy_sems.at[1, 0], me.y_peer()))
    for s in range(1, depth):
        block = final.at[me.before(s), me.y]
        pltpu.make_async_copy(block, block, fz_sems.at[1, s]).wait()
        finals.append(send(block, block, fy_sems.at[0, s], fy_sems.at[1, s], me.y_peer()))

    def deliver(s, y):
        z = me.before(s)
        for i in range(n):

            def tile(t, carry):
                at = pl.multiple_of(t * 16, 16)
                outs[i][z, y, pl.ds(at, 16), :] = final[
                    z, y, pl.ds(starts[i] + at, 16), :
                ].astype(jnp.float32)
                return carry

            lax.fori_loop(0, counts[i] // 16, tile, 0)

    for s in range(depth):
        deliver(s, me.y)
    for s in range(depth):
        block = final.at[me.before(s), 1 - me.y]
        pltpu.make_async_copy(block, block, fy_sems.at[1, s]).wait()
        deliver(s, 1 - me.y)
    for copy in spread:
        copy.wait()
    for copy in small + finals:
        copy.wait_send()
    group.sent()
    for step in range(depth):
        for i in range(n):
            y_copy(step, i).wait_send()
        if step < depth - 1:
            z_copy(step).wait_send()


def tail_by_links(grads, rows_part, small, ep_size):
    width = rows_part.shape[1]
    depth = ep_size // 2
    rows = rows_part.shape[0] // 4
    counts = [g.shape[0] // ep_size for g in grads]
    total = sum(counts)
    places = 4 * ep_size
    bf16, f32 = jnp.bfloat16, jnp.float32
    dma = pltpu.SemaphoreType.DMA
    vmem = pl.BlockSpec(memory_space=pltpu.VMEM)
    lanes = width // 128
    blocks = jnp.pad(small, ((0, places - small.shape[0]), (0, 0))).reshape(places, lanes, 128)
    got = pl.pallas_call(
        functools.partial(tail_kernel, ep_size, counts),
        out_shape=tuple(jax.ShapeDtypeStruct((depth, 2, k, width), f32) for k in counts)
        + (
            jax.ShapeDtypeStruct((rows, width), f32),
            jax.ShapeDtypeStruct(blocks.shape, f32),
        ),
        in_specs=[vmem] * (len(grads) + 2),
        out_specs=(vmem,) * (len(grads) + 2),
        scratch_shapes=[
            pltpu.VMEM((depth, total, width), bf16),
            pltpu.VMEM((depth - 1, total, width), bf16),
            pltpu.VMEM((depth, 2, total, width), bf16),
            pltpu.VMEM((2, rows, width), bf16),
            pltpu.VMEM((rows, width), bf16),
            pltpu.VMEM(blocks.shape, f32),
            pltpu.VMEM(blocks.shape[1:], f32),
            dma((2, depth, len(grads))),
            dma((2, depth)),
            dma((2, depth)),
            dma((2, depth)),
            dma((2, 3)),
            dma((2, places - 1)),
            dma((2, places - 1)),
            dma,
        ],
        compiler_params=pltpu.CompilerParams(
            collective_id=5, has_side_effects=True, vmem_limit_bytes=56 * 1024 * 1024
        ),
        name="tail_by_links",
    )(
        *[g.reshape(depth, 2, k, width) for g, k in zip(grads, counts)],
        rows_part.reshape(2, 2, rows, width),
        blocks,
    )
    sums = [g.reshape(-1, width) for g in got[: len(grads)]]
    return sums, got[-2], got[-1].reshape(places, width)[: small.shape[0]]


def group_rows(value_rows, by_links, call):
    if by_links:
        return group_gather(value_rows, lax.axis_size("ep"), call)
    return lax.all_gather(value_rows, "tp", axis=0, tiled=True)


def group_totals(value_rows, by_links, call):
    if by_links:
        return group_total(value_rows, lax.axis_size("ep"), call)
    return lax.psum_scatter(value_rows, "tp", scatter_dimension=0, tiled=True).astype(jnp.float32)


def tail_totals(grads, rows_part, small, by_links):
    if by_links:
        return tail_by_links(grads, rows_part, small, lax.axis_size("ep"))
    sums = [lax.psum(g, "ep").astype(jnp.float32) for g in grads]
    return sums, group_totals(rows_part, by_links, None), lax.psum(small, ("ep", "tp"))


def gather_all(value_rows, by_links):
    if by_links:
        return gather_by_links(value_rows, lax.axis_size("ep"))
    return lax.all_gather(value_rows, ("ep", "tp"), axis=0, tiled=True)


LAST = 1 << 30


def pair_order(expert_ids, slot_order, expert_count):
    experts = jnp.arange(expert_count, dtype=jnp.int32)
    chosen = expert_ids.T[None, :, :] == experts[:, None, None]
    return jnp.min(jnp.where(chosen, slot_order.T[None, :, :], LAST), axis=1)


def kept_pairs(order):
    used = order < LAST
    counts = jnp.sum(used.astype(jnp.int32), axis=2)
    block = jnp.arange(order.shape[0], dtype=jnp.int32)
    earlier = block[None, :] < block[:, None]
    offsets = jnp.sum(jnp.where(earlier[:, :, None], counts[None, :, :], 0), axis=1)
    whole = offsets + counts <= CAP
    edge = (offsets < CAP) & ~whole
    edge_order = jnp.sum(jnp.where(edge[:, :, None], order, 0), axis=0)
    rank = jnp.sum((edge_order[:, :, None] < edge_order[:, None, :]).astype(jnp.int32), axis=1)
    early = offsets[:, :, None] + rank[None, :, :] < CAP
    return used & (whole[:, :, None] | (edge[:, :, None] & early))


def masked_softmax(logits, used):
    top = jnp.max(jnp.where(used, logits, -1e30), axis=-1, keepdims=True)
    powers = jnp.where(used, jnp.exp(logits - top), 0.0)
    return powers / jnp.sum(powers, axis=-1, keepdims=True)


def pair_codes(order_all, per_owner):
    expert_count = order_all.shape[1]
    first = lax.axis_index("ep") * per_owner
    turned = jnp.roll(order_all, -first, axis=1)
    kept = kept_pairs(turned[:, :per_owner])
    dropped = jnp.pad(~kept, ((0, 0), (0, expert_count - per_owner), (0, 0)))
    code = jnp.where(turned < LAST, dropped.astype(jnp.float32), -1.0)
    code = code.swapaxes(1, 2).reshape(-1, expert_count)
    lanes = -expert_count % 128
    return jnp.pad(code, ((0, 0), (0, lanes)), constant_values=-1.0).astype(jnp.bfloat16)


def run_experts(rows_all, cots_all, code, w_router, w_gate, w_up, w_down, by_links):
    per_owner, width, units = w_gate.shape
    expert_count = w_router.shape[0]
    ep_size, tp_size = lax.axis_size("ep"), lax.axis_size("tp")
    hidden = per_owner * units
    router = jnp.roll(w_router, -lax.axis_index("ep") * per_owner, axis=0)
    router = jnp.pad(router, ((0, -expert_count % 128), (0, 0)))
    enter = jnp.concatenate([w[e] for w in (w_gate, w_up) for e in range(per_owner)], axis=1)
    leave = w_down.reshape(hidden, width)
    if by_links:
        grads, sums, small, gate, up, down = experts_by_links(
            rows_all, cots_all, code, router, enter, leave, per_owner, ep_size
        )
        share = grads.shape[0]
        return (
            grads,
            sums,
            small[:, :, :per_owner, : share // 2].swapaxes(1, 2).reshape(expert_count, share).T,
            gate,
            up,
            down.reshape(w_down.shape),
        )
    used, kept = code >= 0, (code == 0).astype(jnp.float32)
    logits = jnp.einsum("rd,ed->re", rows_all, router, preferred_element_type=jnp.float32)
    gates = jnp.repeat((kept * masked_softmax(logits, used))[:, :per_owner], units, axis=1)
    act = jnp.dot(rows_all, enter, preferred_element_type=jnp.float32)
    gate_act, up_act = act[:, :hidden], act[:, hidden:]
    back_act = jnp.einsum("rd,fd->rf", cots_all, leave, preferred_element_type=jnp.float32)
    sigma = jax.nn.sigmoid(gate_act)
    value = gate_act * sigma * up_act
    weighted = (gates * value).astype(jnp.bfloat16)
    grad_hidden = gates * back_act
    turned = jnp.concatenate(
        [
            grad_hidden * up_act * sigma * (1.0 + gate_act * (1.0 - sigma)),
            grad_hidden * gate_act * sigma,
        ],
        axis=1,
    ).astype(jnp.bfloat16)
    small = kept[:, :per_owner] * jnp.sum((value * back_act).reshape(-1, per_owner, units), axis=2)
    grads = jnp.einsum("rf,df->rd", turned, enter, preferred_element_type=jnp.float32)
    sums = jnp.dot(weighted, leave, preferred_element_type=jnp.float32)

    def scatter(value_rows):
        return lax.psum_scatter(value_rows, ("ep", "tp"), scatter_dimension=0, tiled=True)

    columns = lax.dynamic_update_slice_in_dim(
        jnp.zeros((small.shape[0], expert_count), jnp.float32),
        small,
        lax.axis_index("ep") * per_owner,
        1,
    )
    both = jnp.einsum(
        "rd,rwef->wedf",
        rows_all,
        turned.reshape(-1, 2, per_owner, units),
        preferred_element_type=jnp.float32,
    )
    down = jnp.einsum("rf,rd->fd", weighted, cots_all, preferred_element_type=jnp.float32)
    return (
        scatter(grads.astype(jnp.bfloat16)).astype(jnp.float32),
        scatter(sums.astype(jnp.bfloat16)).astype(jnp.float32),
        scatter(columns),
        both[0],
        both[1],
        down.reshape(w_down.shape),
    )


def visible_block(query_seg, query_pos, query_row, key_seg, key_pos, key_row):
    seg_q = query_seg[:, None]
    seg_k = key_seg[None, :]
    above = (
        (seg_k == seg_q)
        | (seg_k == 0)
        | (seg_k >= 1) & (seg_k <= 4) & (seg_q >= 5) & ((seg_q - 5) // 2 + 1 == seg_k)
    )
    same_tree = query_row[:, None] // TREE_TOKENS == key_row[None, :] // TREE_TOKENS
    return above & same_tree & (key_pos[None, :] <= query_pos[:, None])


def block_scores(query_part, key_rows, allowed, scale):
    scores = (
        jnp.einsum("qkgd,pkd->kgqp", query_part, key_rows, preferred_element_type=jnp.float32)
        * scale
    )
    return jnp.where(allowed[None, None], scores, -1e30)


def attend_forward(query_rows, key_rows, value_rows, segment, position):
    total_rows = query_rows.shape[0]
    scale = query_rows.shape[-1] ** (-0.5)
    row_ids = jnp.arange(total_rows, dtype=jnp.int32)
    allowed = visible_block(segment, position, row_ids, segment, position, row_ids)
    scores = block_scores(query_rows, key_rows, allowed, scale)
    top_score = jnp.max(scores, axis=-1, keepdims=True)
    weights = jnp.exp(scores - top_score)
    weight_sum = jnp.sum(weights, axis=-1, keepdims=True)
    probs = (weights / weight_sum).astype(jnp.bfloat16)
    outputs = jnp.einsum(
        "kgqp,pkd->qkgd", probs, value_rows, preferred_element_type=jnp.float32
    ).astype(jnp.bfloat16)
    log_sums = [top_score + jnp.log(weight_sum)]
    return (outputs, log_sums)


def attend_backward(
    query_rows, key_rows, value_rows, segment, position, log_sums, grad_heads, block_rows
):
    total_rows = query_rows.shape[0]
    scale = query_rows.shape[-1] ** (-0.5)
    row_ids = jnp.arange(total_rows, dtype=jnp.int32)
    grad_keys = jnp.zeros(key_rows.shape, jnp.float32)
    grad_values = jnp.zeros(value_rows.shape, jnp.float32)
    grad_query = []
    for number, first_row in enumerate(range(0, total_rows, block_rows)):
        allowed = visible_block(segment, position, row_ids, segment, position, row_ids)
        scores = block_scores(query_rows, key_rows, allowed, scale)
        probs = jnp.where(allowed[None, None], jnp.exp(scores - log_sums[number]), 0.0)
        grad_values = jnp.einsum(
            "kgqp,qkgd->pkd",
            probs.astype(jnp.bfloat16),
            grad_heads,
            preferred_element_type=jnp.float32,
        )
        grad_probs = jnp.einsum(
            "qkgd,pkd->kgqp", grad_heads, value_rows, preferred_element_type=jnp.float32
        )
        inner = jnp.sum(probs * grad_probs, axis=-1, keepdims=True)
        grad_scores = (probs * (grad_probs - inner)).astype(jnp.bfloat16)
        grad_query.append(
            jnp.einsum("kgqp,pkd->qkgd", grad_scores, key_rows, preferred_element_type=jnp.float32)
            * scale
        )
        grad_keys = (
            jnp.einsum(
                "kgqp,qkgd->pkd", grad_scores, query_rows, preferred_element_type=jnp.float32
            )
            * scale
        )
    return (grad_query[0], grad_keys, grad_values)


def local(
    hidden_in,
    gain_attn,
    w_query,
    key_projection_weight,
    value_projection_weight,
    w_out,
    gain_ffn,
    w_router,
    w_gate,
    w_up,
    w_down,
    expert_ids,
    slot_order,
    segment,
    position,
    cotangent,
):
    model_width = w_query.shape[1]
    head_width = HEAD_DIMENSION
    local_heads = w_query.shape[0] // head_width
    local_kv = key_projection_weight.shape[0] // head_width
    group_factor = local_heads // local_kv
    token_count = expert_ids.shape[0]
    share = hidden_in.shape[0]
    row_start = lax.axis_index("tp") * share
    expert_count = w_router.shape[0]
    per_owner = w_gate.shape[0]
    block_rows = 512
    by_links = lax.axis_size("tp") == 4 and lax.axis_size("ep") == 8
    order = pair_order(expert_ids, slot_order, expert_count)
    cot_all = gather_all(cotangent, False)
    inputs_own = hidden_in.astype(jnp.float32)
    gain_one = gain_attn.astype(jnp.float32)
    gain_two = gain_ffn.astype(jnp.float32)
    scale_one = norm_scale(inputs_own)
    first_own = (inputs_own * scale_one * gain_one).astype(jnp.bfloat16)
    if by_links:
        first_normalized, order_all = front_gather(first_own, order, lax.axis_size("ep"))
    else:
        first_normalized = group_rows(first_own, by_links, None)
        order_all = lax.all_gather(order, "ep")
    code = pair_codes(order_all, per_owner)
    cosine_lookup, sine_lookup = rope_tables(position, head_width)
    query_proj = jnp.einsum(
        "rd,fd->rf", first_normalized, w_query, preferred_element_type=jnp.float32
    ).reshape(token_count, local_heads, head_width)
    key_proj = jnp.einsum(
        "rd,fd->rf", first_normalized, key_projection_weight, preferred_element_type=jnp.float32
    ).reshape(token_count, local_kv, head_width)
    query_rows = (
        apply_rotation(query_proj, cosine_lookup, sine_lookup)
        .astype(jnp.bfloat16)
        .reshape(token_count, local_kv, group_factor, head_width)
    )
    key_rows = apply_rotation(key_proj, cosine_lookup, sine_lookup).astype(jnp.bfloat16)
    value_rows = (
        jnp.einsum(
            "rd,fd->rf",
            first_normalized,
            value_projection_weight,
            preferred_element_type=jnp.float32,
        )
        .astype(jnp.bfloat16)
        .reshape(token_count, local_kv, head_width)
    )
    head_outputs, log_sums = attend_forward(query_rows, key_rows, value_rows, segment, position)
    head_outputs = head_outputs.reshape(token_count, local_heads * head_width)
    middle_own = inputs_own + group_totals(
        jnp.dot(head_outputs, w_out, preferred_element_type=jnp.float32).astype(jnp.bfloat16),
        by_links,
        3,
    )
    scale_two = norm_scale(middle_own)
    normed_own = (middle_own * scale_two * gain_two).astype(jnp.bfloat16)
    normed_two = gather_all(normed_own, by_links)
    used = lax.dynamic_slice_in_dim(order, row_start, share, 1).T < LAST
    gates = masked_softmax(
        jnp.einsum("rd,ed->re", normed_own, w_router, preferred_element_type=jnp.float32), used
    )
    grad_normed_own, combined_own, grad_gates_own, grad_w_gate, grad_w_up, grad_w_down = (
        run_experts(normed_two, cot_all, code, w_router, w_gate, w_up, w_down, by_links)
    )
    output_own = (middle_own + combined_own).astype(jnp.bfloat16)
    inner_gate = jnp.sum(gates * grad_gates_own, axis=-1, keepdims=True)
    grad_logits = gates * (grad_gates_own - inner_gate)
    router_f = w_router.astype(jnp.float32)
    grad_normed_own = grad_normed_own + jnp.dot(grad_logits, router_f, precision=EXACT_PRECISION)
    grad_router = jnp.dot(grad_logits.T, normed_own.astype(jnp.float32), precision=EXACT_PRECISION)
    grad_gain_ffn = jnp.sum(grad_normed_own * middle_own * scale_two, axis=0)
    grad_middle = cotangent.astype(jnp.float32) + norm_back(
        middle_own, scale_two, gain_two, grad_normed_own
    )
    grad_attn = group_rows(grad_middle.astype(jnp.bfloat16), by_links, 7)
    grad_w_out = jnp.einsum(
        "rf,rd->fd", head_outputs, grad_attn, preferred_element_type=jnp.float32
    )
    grad_w_out = lax.psum(grad_w_out.astype(jnp.bfloat16), "ep").astype(jnp.float32)
    grad_heads = (
        jnp.einsum("rd,fd->rf", grad_attn, w_out, preferred_element_type=jnp.float32)
        .astype(jnp.bfloat16)
        .reshape(token_count, local_kv, group_factor, head_width)
    )
    grad_query, grad_keys, grad_values = attend_backward(
        query_rows, key_rows, value_rows, segment, position, log_sums, grad_heads, block_rows
    )
    grad_query_proj = (
        rotate_back(
            grad_query.reshape(token_count, local_heads, head_width), cosine_lookup, sine_lookup
        )
        .astype(jnp.bfloat16)
        .reshape(token_count, local_heads * head_width)
    )
    grad_key_proj = (
        rotate_back(grad_keys, cosine_lookup, sine_lookup)
        .astype(jnp.bfloat16)
        .reshape(token_count, local_kv * head_width)
    )
    grad_value_proj = grad_values.astype(jnp.bfloat16).reshape(token_count, local_kv * head_width)
    grad_w_query = jnp.einsum(
        "rf,rd->fd", grad_query_proj, first_normalized, preferred_element_type=jnp.float32
    )
    grad_w_key = jnp.einsum(
        "rf,rd->fd", grad_key_proj, first_normalized, preferred_element_type=jnp.float32
    )
    grad_w_value = jnp.einsum(
        "rf,rd->fd", grad_value_proj, first_normalized, preferred_element_type=jnp.float32
    )
    grad_normed_one = jnp.einsum(
        "rf,fd->rd", grad_query_proj, w_query, preferred_element_type=jnp.float32
    )
    grad_normed_one = grad_normed_one + jnp.einsum(
        "rf,fd->rd", grad_key_proj, key_projection_weight, preferred_element_type=jnp.float32
    )
    grad_normed_one = grad_normed_one + jnp.einsum(
        "rf,fd->rd", grad_value_proj, value_projection_weight, preferred_element_type=jnp.float32
    )
    grad_gain_attn = jnp.sum(grad_normed_one * first_normalized.astype(jnp.float32), axis=0)
    small = jnp.concatenate(
        [grad_router, grad_gain_ffn[None, :], (grad_gain_attn / gain_one)[None, :]], axis=0
    )
    (grad_w_query, grad_w_key, grad_w_value), grad_one_own, small = tail_totals(
        [g.astype(jnp.bfloat16) for g in (grad_w_query, grad_w_key, grad_w_value)],
        grad_normed_one.astype(jnp.bfloat16),
        small,
        by_links,
    )
    grad_router = small[:expert_count]
    grad_gain_ffn, grad_gain_attn = small[expert_count], small[expert_count + 1]
    grad_input = grad_middle + norm_back(inputs_own, scale_one, gain_one, grad_one_own)
    return (
        output_own,
        grad_input,
        grad_gain_attn,
        grad_w_query,
        grad_w_key,
        grad_w_value,
        grad_w_out,
        grad_gain_ffn,
        grad_router,
        grad_w_gate,
        grad_w_up,
        grad_w_down,
    )


def solution(mesh):
    placed = (
        P(("ep", "tp"), None),
        P(),
        P("tp", None),
        P("tp", None),
        P("tp", None),
        P("tp", None),
        P(),
        P(),
        P("ep", None, "tp"),
        P("ep", None, "tp"),
        P("ep", "tp", None),
        P("ep", None),
        P("ep", None),
        P("ep"),
        P("ep"),
        P(("ep", "tp"), None),
    )
    return jax.shard_map(
        local,
        mesh=mesh,
        in_specs=placed,
        out_specs=(
            P(("ep", "tp"), None),
            P(("ep", "tp"), None),
            P(),
            P("tp", None),
            P("tp", None),
            P("tp", None),
            P("tp", None),
            P(),
            P(),
            P("ep", None, "tp"),
            P("ep", None, "tp"),
            P("ep", "tp", None),
        ),
        check_vma=False,
    )
```

```python
import functools

import jax
import jax.numpy as jnp
from jax import lax
from jax.experimental import pallas as pl
from jax.experimental.pallas import tpu as pltpu
from jax.sharding import PartitionSpec as P

HEAD_DIMENSION = 64
TREE_TOKENS = 512
CAP = 2304


EPSILON = 1e-06
ROPE_BASE = 10000.0
EXACT_PRECISION = lax.Precision.HIGHEST


def rope_tables(position, head_width):
    half_width = head_width // 2
    freqs = ROPE_BASE ** (-(jnp.arange(half_width, dtype=jnp.float32) * 2.0 / head_width))
    angle = position.astype(jnp.float32)[:, None] * freqs[None, :]
    return (jnp.cos(angle)[:, None, :], jnp.sin(angle)[:, None, :])


def apply_rotation(value_rows, cosine_lookup, sine_lookup):
    half_width = value_rows.shape[-1] // 2
    first = value_rows[..., :half_width]
    second = value_rows[..., half_width:]
    return jnp.concatenate(
        [
            first * cosine_lookup - second * sine_lookup,
            first * sine_lookup + second * cosine_lookup,
        ],
        axis=-1,
    )


def rotate_back(grads, cosine_lookup, sine_lookup):
    half_width = grads.shape[-1] // 2
    first = grads[..., :half_width]
    second = grads[..., half_width:]
    return jnp.concatenate(
        [
            first * cosine_lookup + second * sine_lookup,
            second * cosine_lookup - first * sine_lookup,
        ],
        axis=-1,
    )


def norm_scale(value_rows):
    return lax.rsqrt(jnp.mean(value_rows * value_rows, axis=-1, keepdims=True) + EPSILON)


def norm_back(value_rows, scale, gain, grad_normed):
    weighted = grad_normed * gain
    inner = jnp.mean(value_rows * weighted, axis=-1, keepdims=True)
    grad_values = scale * weighted - value_rows * (scale * scale * scale) * inner
    return grad_values


MESH = pl.DeviceIdType.MESH


class Place:
    def __init__(self, ep_size):
        self.depth = ep_size // 2
        ep, tp = lax.axis_index("ep"), lax.axis_index("tp")
        self.z, self.y = ep // 2, ep % 2
        self.x, self.c = tp // 2, tp % 2

    def device(self, z=None, y=None, x=None, c=None):
        z = self.z if z is None else z
        y = self.y if y is None else y
        x = self.x if x is None else x
        c = self.c if c is None else c
        return (z * 2 + y, x * 2 + c)

    def sibling(self):
        return self.device(c=1 - self.c)

    def x_peer(self):
        return self.device(x=1 - self.x)

    def y_peer(self):
        return self.device(y=1 - self.y)

    def after(self, step):
        return lax.rem(self.z + step, self.depth)

    def before(self, step):
        return lax.rem(self.z + self.depth - step, self.depth)


def meet(devices):
    barrier = pltpu.get_barrier_semaphore()
    for device in devices:
        pl.semaphore_signal(barrier, inc=1, device_id=device, device_id_type=MESH)
    pl.semaphore_wait(barrier, len(devices))


def send(src, dst, send_sem, recv_sem, device):
    copy = pltpu.make_async_remote_copy(
        src_ref=src,
        dst_ref=dst,
        send_sem=send_sem,
        recv_sem=recv_sem,
        device_id=device,
        device_id_type=MESH,
    )
    copy.start()
    return copy


def gather_kernel(ep_size, own, out, own_sem, z_sems, pair_sems, core_sems):
    me = Place(ep_size)
    depth = me.depth
    half = own.shape[0] // 2
    z_send, z_recv = z_sems.at[0], z_sems.at[1]
    pair_send, pair_recv = pair_sems.at[0], pair_sems.at[1]
    core_send, core_recv = core_sems.at[0], core_sems.at[1]
    meet(
        [me.sibling(), me.x_peer(), me.y_peer()]
        + [me.device(z=me.after(s)) for s in range(1, depth)]
    )

    def rows(part):
        return pl.ds(part * half, half)

    def block(step, y, x, part, c=None):
        return out.at[me.before(step), y, x, me.c if c is None else c, rows(part)]

    started = []

    def forward(source, target, sems, slot, device):
        started.append(send(source, target, sems[0].at[slot], sems[1].at[slot], device))

    for s in range(1, depth):
        for part in range(2):
            forward(
                own.at[rows(part)],
                out.at[me.z, me.y, me.x, me.c, rows(part)],
                (z_send, z_recv),
                (s - 1) * 2 + part,
                me.device(z=me.after(s)),
            )
    local = pltpu.make_async_copy(own, out.at[me.z, me.y, me.x, me.c], own_sem)
    local.start()
    local.wait()

    kinds = [
        (me.y, me.x, 0),
        (me.y, me.x, 1),
        (1 - me.y, me.x, 0),
        (me.y, 1 - me.x, 1),
        (1 - me.y, me.x, 1),
        (1 - me.y, 1 - me.x, 1),
        (me.y, 1 - me.x, 0),
        (1 - me.y, 1 - me.x, 0),
    ]
    x_route = {0: 6, 2: 7, 1: 3}
    y_route = {0: 2, 1: 4, 3: 5}

    def landed(step, kind):
        y, x, part = kinds[kind]
        place = block(step, y, x, part)
        if kind < 2:
            if step > 0:
                sem = z_recv.at[(step - 1) * 2 + part]
                pltpu.make_async_copy(place, place, sem).wait()
        else:
            pltpu.make_async_copy(place, place, pair_recv.at[step * 8 + kind]).wait()

    def pass_on(step, kind):
        y, x, part = kinds[kind]
        place = block(step, y, x, part)
        if kind in x_route:
            forward(place, place, (pair_send, pair_recv), step * 8 + x_route[kind], me.x_peer())
        if kind in y_route:
            forward(place, place, (pair_send, pair_recv), step * 8 + y_route[kind], me.y_peer())
        forward(place, place, (core_send, core_recv), step * 8 + kind, me.sibling())

    for turn in range(depth + 2):
        for step, group in ((turn, (0, 1)), (turn - 1, (2, 3)), (turn - 2, (4, 5, 6, 7))):
            if 0 <= step < depth:
                for kind in group:
                    landed(step, kind)
                    pass_on(step, kind)
    for step in range(depth):
        for kind in range(8):
            y, x, part = kinds[kind]
            place = block(step, y, x, part, 1 - me.c)
            pltpu.make_async_copy(place, place, core_recv.at[step * 8 + kind]).wait()
    for copy in started:
        copy.wait_send()


def gather_by_links(value_rows, ep_size):
    rows, width = value_rows.shape
    depth = ep_size // 2
    dma = pltpu.SemaphoreType.DMA
    every = pl.pallas_call(
        functools.partial(gather_kernel, ep_size),
        out_shape=jax.ShapeDtypeStruct((depth, 2, 2, 2, rows, width), value_rows.dtype),
        in_specs=[pl.BlockSpec(memory_space=pl.ANY)],
        out_specs=pl.BlockSpec(memory_space=pl.ANY),
        scratch_shapes=[
            dma,
            dma((2, 2 * depth - 2)),
            dma((2, 8 * depth)),
            dma((2, 8 * depth)),
        ],
        compiler_params=pltpu.CompilerParams(collective_id=1, has_side_effects=True),
        name="gather_by_links",
    )(value_rows)
    return every.reshape(-1, width)


def add_into(target, other):
    def tile(i, carry):
        at = pl.ds(pl.multiple_of(i * 16, 16), 16)
        target[at, :] = target[at, :] + other[at, :]
        return carry

    lax.fori_loop(0, target.shape[0] // 16, tile, 0)


def front_gather_kernel(
    ep_size, pieces, own, table, out, tables, own_sem, sems, table_own_sem, table_sems
):
    me = Place(ep_size)
    mine = lax.axis_index("ep")
    tp = lax.axis_index("tp")
    peers = [(lax.rem(mine + k, ep_size), tp) for k in range(1, ep_size)]
    meet([me.sibling(), me.x_peer()] + peers)
    local = pltpu.make_async_copy(table, tables.at[mine], table_own_sem)
    local.start()
    copies = [
        send(table, tables.at[mine], table_sems.at[0, k], table_sems.at[1, k], device)
        for k, device in enumerate(peers)
    ]
    group_gather_body(me, pieces, own, out, own_sem, sems)
    local.wait()
    for copy in copies:
        copy.wait()


def front_gather(value_rows, table, ep_size):
    rows, width = value_rows.shape
    pieces = 4
    dma = pltpu.SemaphoreType.DMA
    anywhere = pl.BlockSpec(memory_space=pl.ANY)
    every, tables = pl.pallas_call(
        functools.partial(front_gather_kernel, ep_size, pieces),
        out_shape=(
            jax.ShapeDtypeStruct((2, 2, rows, width), value_rows.dtype),
            jax.ShapeDtypeStruct((ep_size,) + table.shape, table.dtype),
        ),
        in_specs=[anywhere] * 2,
        out_specs=(anywhere,) * 2,
        scratch_shapes=[dma, dma((2, 3 * pieces)), dma, dma((2, ep_size - 1))],
        compiler_params=pltpu.CompilerParams(collective_id=6, has_side_effects=True),
        name="front_gather",
    )(value_rows, table)
    return every.reshape(-1, width), tables


def group_gather_body(me, pieces, own, out, own_sem, sems):
    size = own.shape[0] // pieces
    started = []
    local = pltpu.make_async_copy(own, out.at[me.x, me.c], own_sem)
    local.start()

    def at(p):
        return pl.ds(p * size, size)

    def go(kind, p, src, dst, device):
        slot = kind * pieces + p
        started.append(send(src, dst, sems.at[0, slot], sems.at[1, slot], device))

    for p in range(pieces):
        go(0, p, own.at[at(p)], out.at[me.x, me.c, at(p)], me.x_peer())
    for p in range(pieces):
        go(1, p, own.at[at(p)], out.at[me.x, me.c, at(p)], me.sibling())
    for p in range(pieces):
        block = out.at[1 - me.x, me.c, at(p)]
        pltpu.make_async_copy(block, block, sems.at[1, p]).wait()
        go(2, p, block, block, me.sibling())
    for p in range(pieces):
        for kind, x in ((1, me.x), (2, 1 - me.x)):
            block = out.at[x, 1 - me.c, at(p)]
            pltpu.make_async_copy(block, block, sems.at[1, kind * pieces + p]).wait()
    local.wait()
    for copy in started:
        copy.wait_send()


class GroupTotal:
    def __init__(self, me, parts, core_got, pair_got, sems):
        self.me, self.parts, self.core_got, self.pair_got = me, parts, core_got, pair_got
        self.core = [
            pltpu.make_async_remote_copy(
                src_ref=parts.at[x, 1 - me.c],
                dst_ref=core_got.at[x],
                send_sem=sems.at[0, k],
                recv_sem=sems.at[1, k],
                device_id=me.sibling(),
                device_id_type=MESH,
            )
            for k, x in enumerate((1 - me.x, me.x))
        ]
        self.pair = pltpu.make_async_remote_copy(
            src_ref=core_got.at[1 - me.x],
            dst_ref=pair_got,
            send_sem=sems.at[0, 2],
            recv_sem=sems.at[1, 2],
            device_id=me.x_peer(),
            device_id_type=MESH,
        )

    def begin(self):
        for copy in self.core:
            copy.start()

    def exchange(self):
        self.core[0].wait_recv()
        far = 1 - self.me.x
        add_into(self.core_got.at[far], self.parts.at[far, self.me.c])
        self.pair.start()

    def finish(self, out, change=lambda value, at: value):
        self.core[1].wait_recv()
        self.pair.wait_recv()

        def tile(i, carry):
            at = pl.ds(pl.multiple_of(i * 16, 16), 16)
            value = (
                self.parts[self.me.x, self.me.c, at, :].astype(jnp.float32)
                + self.core_got[self.me.x, at, :].astype(jnp.float32)
                + self.pair_got[at, :].astype(jnp.float32)
            )
            out[at, :] = change(value, at)
            return carry

        lax.fori_loop(0, out.shape[0] // 16, tile, 0)

    def sent(self):
        for copy in self.core + [self.pair]:
            copy.wait_send()


def group_total_kernel(ep_size, parts, out, core_got, pair_got, sems):
    me = Place(ep_size)
    meet([me.sibling(), me.x_peer()])
    total = GroupTotal(me, parts, core_got, pair_got, sems)
    total.begin()
    total.exchange()
    total.finish(out)
    total.sent()


def group_total(value_rows, ep_size, call):
    rows, width = value_rows.shape[0] // 4, value_rows.shape[1]
    vmem = pl.BlockSpec(memory_space=pltpu.VMEM)
    return pl.pallas_call(
        functools.partial(group_total_kernel, ep_size),
        out_shape=jax.ShapeDtypeStruct((rows, width), jnp.float32),
        in_specs=[vmem],
        out_specs=vmem,
        scratch_shapes=[
            pltpu.VMEM((2, rows, width), jnp.bfloat16),
            pltpu.VMEM((rows, width), jnp.bfloat16),
            pltpu.SemaphoreType.DMA((2, 3)),
        ],
        compiler_params=pltpu.CompilerParams(
            collective_id=call, has_side_effects=True, vmem_limit_bytes=32 * 1024 * 1024
        ),
        name="group_total",
    )(value_rows.reshape(2, 2, rows, width))


def all_others(ep_size):
    ep, tp = lax.axis_index("ep"), lax.axis_index("tp")
    return [
        (lax.rem(ep + k // 4, ep_size), lax.rem(tp + k % 4, 4)) for k in range(1, ep_size * 4)
    ]


def experts_kernel(
    ep_size,
    per_owner,
    rows_in,
    cots_in,
    code_in,
    router,
    enter,
    leave,
    grad_out,
    sum_out,
    small_out,
    gate_out,
    up_out,
    down_out,
    rows_buf,
    cots_buf,
    weighted,
    turned,
    enter_sum,
    parts,
    core_got,
    pair_got,
    last_got,
    z_got,
    small_in,
    small_got,
    load_sems,
    core_sems,
    pair_sems,
    last_sems,
    z_sems,
    small_sems,
    own_sem,
):
    me = Place(ep_size)
    depth = me.depth
    steps = 2 * depth
    blocks = 2 * steps
    width = router.shape[1]
    share = rows_buf.shape[2]
    tokens = 4 * share
    units = leave.shape[0] // per_owner
    hidden = per_owner * units
    f32, bf16 = jnp.float32, jnp.bfloat16
    others = all_others(ep_size)
    meet(others)
    my_place = lax.axis_index("ep") * 4 + lax.axis_index("tp")

    def where(b):
        return me.after(b // 4 + 1), lax.rem(1 - me.y + b % 2, 2)

    def half(b):
        return pl.ds(pl.multiple_of(b // 2 % 2 * share, share), share)

    def load(b, which):
        z, y = where(b)
        source, target = ((rows_in, rows_buf), (cots_in, cots_buf))[which]
        slot = lax.rem(b, 2)
        return pltpu.make_async_copy(
            source.at[z, y, :, half(b)], target.at[slot], load_sems.at[slot, which]
        )

    def core_copy(b):
        y = where(b)[1]
        return pltpu.make_async_remote_copy(
            src_ref=parts.at[lax.rem(b, 2), :, :, 1 - me.c],
            dst_ref=core_got.at[b // 2, y],
            send_sem=core_sems.at[0, b],
            recv_sem=core_sems.at[1, b],
            device_id=me.sibling(),
            device_id_type=MESH,
        )

    def grad_pair(b):
        y = where(b)[1]
        return pltpu.make_async_remote_copy(
            src_ref=core_got.at[b // 2, y, 0, 1 - me.x],
            dst_ref=pair_got.at[b // 2, 0, y],
            send_sem=pair_sems.at[0, b],
            recv_sem=pair_sems.at[1, b],
            device_id=me.x_peer(),
            device_id_type=MESH,
        )

    def sum_pair(step):
        return pltpu.make_async_remote_copy(
            src_ref=core_got.at[step, 1 - me.y, 1],
            dst_ref=pair_got.at[step, 1],
            send_sem=pair_sems.at[0, blocks + step],
            recv_sem=pair_sems.at[1, blocks + step],
            device_id=me.y_peer(),
            device_id_type=MESH,
        )

    def last_copy(step, which):
        return pltpu.make_async_remote_copy(
            src_ref=pair_got.at[step, which, (1 - me.y, 1 - me.x)[which]],
            dst_ref=last_got.at[step, which],
            send_sem=last_sems.at[0, step, which],
            recv_sem=last_sems.at[1, step, which],
            device_id=(me.y_peer(), me.x_peer())[which],
            device_id_type=MESH,
        )

    def z_copy(step, which):
        return pltpu.make_async_remote_copy(
            src_ref=last_got.at[step, which],
            dst_ref=z_got.at[step, which],
            send_sem=z_sems.at[0, step, which],
            recv_sem=z_sems.at[1, step, which],
            device_id=me.device(z=me.after(step // 2 + 1)),
            device_id_type=MESH,
        )

    def small_copy(k, device):
        return pltpu.make_async_remote_copy(
            src_ref=small_in.at[device[0] * 4 + device[1]],
            dst_ref=small_got.at[my_place],
            send_sem=small_sems.at[0, k],
            recv_sem=small_sems.at[1, k],
            device_id=device,
            device_id_type=MESH,
        )

    def dot(a, b, contract):
        return lax.dot_general(
            a, b, ((contract[:1], contract[1:]), ((), ())), preferred_element_type=f32
        )

    def spread(columns):
        return jnp.concatenate(
            [jnp.broadcast_to(columns[:, e : e + 1], (tokens, units)) for e in range(per_owner)],
            axis=1,
        )

    def compute(b):
        z, y = where(b)
        slot = lax.rem(b, 2)
        rows = rows_buf[slot].reshape(tokens, width)
        cots = cots_buf[slot].reshape(tokens, width)
        code = code_in[z * 2 + y, :, half(b), :].astype(f32).reshape(tokens, -1)
        used = code >= 0.0
        logits = jnp.where(used, dot(rows, router[...], (1, 1)), -1e30)
        top = jnp.max(logits, axis=1, keepdims=True)
        powers = jnp.where(used, jnp.exp(logits - top), 0.0)
        kept = jnp.where(code == 0.0, 1.0, 0.0)
        gates = spread(kept * powers / jnp.sum(powers, axis=1, keepdims=True))
        act = dot(rows, enter[...], (1, 0))
        gate_act, up_act = act[:, :hidden], act[:, hidden:]
        back_act = dot(cots, leave[...], (1, 1))
        sigma = jax.nn.sigmoid(gate_act)
        swish = gate_act * sigma
        value = swish * up_act
        gate_parts = spread(kept) * (value * back_act)
        lane = lax.broadcasted_iota(jnp.int32, (8, hidden), 1)
        pick = lax.broadcasted_iota(jnp.int32, (8, hidden), 0)
        mine = jnp.where((lane >= pick * units) & (lane < (pick + 1) * units), 1.0, 0.0)
        grad_gates = lax.dot_general(
            mine,
            gate_parts,
            (((1,), (1,)), ((), ())),
            precision=EXACT_PRECISION,
            preferred_element_type=f32,
        )
        for k in range(4):
            small_in[(z * 2 + y) * 4 + k, b // 2 % 2, :, :share] = grad_gates[
                :, k * share : (k + 1) * share
            ]
        weighted[...] = (gates * value).astype(bf16)
        grad_hidden = gates * back_act
        turned[:, :hidden] = (
            grad_hidden * up_act * sigma * (1.0 + gate_act * (1.0 - sigma))
        ).astype(bf16)
        turned[:, hidden:] = (grad_hidden * swish).astype(bf16)
        tile = 512
        for n in range(width // tile):
            cols = slice(n * tile, (n + 1) * tile)
            grads = dot(turned[...], enter[cols, :], (1, 1)).astype(bf16)
            sums = dot(weighted[...], leave[:, cols], (1, 0)).astype(bf16)
            for x in range(2):
                for c in range(2):
                    at = slice((x * 2 + c) * share, (x * 2 + c + 1) * share)
                    parts[slot, 0, x, c, :, cols] = grads[at]
                    parts[slot, 1, x, c, :, cols] = sums[at]

    def weight_sums(b):
        slot = lax.rem(b, 2)
        tile = 512
        for n in range(width // tile):
            cols = slice(n * tile, (n + 1) * tile)
            rows = rows_buf[slot, :, :, cols].reshape(tokens, tile)
            cots = cots_buf[slot, :, :, cols].reshape(tokens, tile)
            enter_sum[:, cols] += dot(turned[...], rows, (0, 0))
            down_out[:, cols] += dot(weighted[...], cots, (0, 0))

    enter_sum[...] = jnp.zeros_like(enter_sum)
    down_out[...] = jnp.zeros_like(down_out)
    small_in[...] = jnp.zeros_like(small_in)
    for which in range(2):
        load(0, which).start()

    def during(i, lag, body, even=False):
        b = i - lag
        inside = (b >= 0) & (b < blocks)
        if even:
            inside &= b % 2 == 0
        pl.when(inside)(lambda: body(b))

    def finish_sum(which):
        def body(b):
            step = b // 2
            last_copy(step, which).wait_recv()
            add_into(last_got.at[step, which], pair_got.at[step, which, (me.y, me.x)[which]])

            @pl.when(step < steps - 2)
            def _():
                z_copy(step, which).start()

        return body

    def work(b):
        for which in range(2):
            load(b, which).wait()

        @pl.when(b + 1 < blocks)
        def _():
            for which in range(2):
                load(b + 1, which).start()

        compute(b)
        core_copy(b).start()
        weight_sums(b)

    def core_sum(b):
        y = where(b)[1]
        core_copy(b).wait_recv()
        for which in range(2):
            for x in range(2):
                add_into(
                    core_got.at[b // 2, y, which, x], parts.at[lax.rem(b, 2), which, x, me.c]
                )
        grad_pair(b).start()

        @pl.when(b % 2 == 0)
        def _():
            sum_pair(b // 2).start()

        core_copy(b).wait_send()

    def out_pair(b):
        step = b // 2
        sum_pair(step).wait_recv()
        for x in range(2):
            add_into(pair_got.at[step, 1, x], core_got.at[step, me.y, 1, x])
        last_copy(step, 1).start()

    def back_pair(b):
        y = where(b)[1]
        step = b // 2
        grad_pair(b).wait_recv()
        add_into(pair_got.at[step, 0, y], core_got.at[step, y, 0, me.x])

        @pl.when(b % 2 == 0)
        def _():
            last_copy(step, 0).start()

    def small_send(b):
        for k, device in enumerate(others):
            small_copy(k, device).start()
        pltpu.make_async_copy(small_in.at[my_place], small_got.at[my_place], own_sem).start()
        for e in range(per_owner):
            gate_out[e] = enter_sum[e * units : (e + 1) * units, :].T
            up_out[e] = enter_sum[hidden + e * units : hidden + (e + 1) * units, :].T

    def turn(i, carry):
        during(i, 6, finish_sum(1), True)
        during(i, 0, work)
        during(i, 1, core_sum)
        during(i, 7, finish_sum(0), True)
        during(i, 3, out_pair, True)
        during(i, 4, back_pair)
        pl.when(i == blocks)(lambda: small_send(i))
        return carry

    lax.fori_loop(0, blocks + 7, turn, 0)
    pltpu.make_async_copy(small_in.at[my_place], small_got.at[my_place], own_sem).wait()
    for k, device in enumerate(others):
        small_copy(k, device).wait()
    for ep in range(ep_size):
        total = small_got[ep * 4]
        for tp in range(1, 4):
            total = total + small_got[ep * 4 + tp]
        small_out[ep] = total
    for step in range(steps - 2):
        for which in range(2):
            z_copy(step, which).wait_recv()

    def finish(which, part, target):
        def tile(i, carry):
            at = pl.multiple_of(i * 16, 16)
            total = last_got[steps - 2 + part, which, pl.ds(at, 16), :].astype(f32)
            for step in range(depth - 1):
                total = total + z_got[2 * step + part, which, pl.ds(at, 16), :].astype(f32)
            target[pl.ds(part * share + at, 16), :] = total
            return carry

        lax.fori_loop(0, share // 16, tile, 0)

    for part in range(2):
        finish(0, part, grad_out)
        finish(1, part, sum_out)

    def sent(step, carry):
        grad_pair(2 * step).wait_send()
        grad_pair(2 * step + 1).wait_send()
        sum_pair(step).wait_send()
        for which in range(2):
            last_copy(step, which).wait_send()

        @pl.when(step < steps - 2)
        def _():
            for which in range(2):
                z_copy(step, which).wait_send()

        return carry

    lax.fori_loop(0, steps, sent, 0)


def experts_by_links(rows_all, cots_all, code, router, enter, leave, per_owner, ep_size):
    total_rows, width = rows_all.shape
    depth = ep_size // 2
    tokens = total_rows // ep_size
    rows = tokens // 4
    half, steps = rows // 2, 2 * depth
    hidden = leave.shape[0]
    units = hidden // per_owner
    bf16, f32 = jnp.bfloat16, jnp.float32
    dma = pltpu.SemaphoreType.DMA
    vmem = pl.BlockSpec(memory_space=pltpu.VMEM)
    anywhere = pl.BlockSpec(memory_space=pl.ANY)
    places = 4 * ep_size
    blocks = (depth, 2, 4, rows, width)
    return pl.pallas_call(
        functools.partial(experts_kernel, ep_size, per_owner),
        out_shape=(
            jax.ShapeDtypeStruct((rows, width), f32),
            jax.ShapeDtypeStruct((rows, width), f32),
            jax.ShapeDtypeStruct((ep_size, 2, 8, 128), f32),
            jax.ShapeDtypeStruct((per_owner, width, units), f32),
            jax.ShapeDtypeStruct((per_owner, width, units), f32),
            jax.ShapeDtypeStruct((hidden, width), f32),
        ),
        in_specs=[anywhere, anywhere, vmem, vmem, vmem, vmem],
        out_specs=(vmem,) * 6,
        scratch_shapes=[
            pltpu.VMEM((2, 4, half, width), bf16),
            pltpu.VMEM((2, 4, half, width), bf16),
            pltpu.VMEM((4 * half, hidden), bf16),
            pltpu.VMEM((4 * half, 2 * hidden), bf16),
            pltpu.VMEM((2 * hidden, width), f32),
            pltpu.VMEM((2, 2, 2, 2, half, width), bf16),
            pltpu.VMEM((steps, 2, 2, 2, half, width), bf16),
            pltpu.VMEM((steps, 2, 2, half, width), bf16),
            pltpu.VMEM((steps, 2, half, width), bf16),
            pltpu.VMEM((steps - 2, 2, half, width), bf16),
            pltpu.VMEM((places, 2, 8, 128), f32),
            pltpu.VMEM((places, 2, 8, 128), f32),
            dma((2, 2)),
            dma((2, 2 * steps)),
            dma((2, 3 * steps)),
            dma((2, steps, 2)),
            dma((2, steps - 2, 2)),
            dma((2, places - 1)),
            dma,
        ],
        compiler_params=pltpu.CompilerParams(
            collective_id=2, has_side_effects=True, vmem_limit_bytes=60 * 1024 * 1024
        ),
        name="experts_by_links",
    )(
        rows_all.reshape(blocks),
        cots_all.reshape(blocks),
        code.reshape(ep_size, 4, rows, -1),
        router,
        enter,
        leave,
    )


class EpSum:
    def __init__(self, me, grads, outs, y_got, z_got, final, sems):
        self.me, self.grads, self.outs = me, grads, outs
        self.y_got, self.z_got, self.final = y_got, z_got, final
        self.y_sems, self.z_sems, self.fz_sems, self.fy_sems = sems
        self.counts = [g.shape[2] for g in grads]
        self.starts = [sum(self.counts[:i]) for i in range(len(grads))]
        self.finals = []

    def y_copy(self, step, i):
        me = self.me
        return pltpu.make_async_remote_copy(
            src_ref=self.grads[i].at[me.after(step + 1), 1 - me.y],
            dst_ref=self.y_got.at[step, pl.ds(self.starts[i], self.counts[i])],
            send_sem=self.y_sems.at[0, step, i],
            recv_sem=self.y_sems.at[1, step, i],
            device_id=me.y_peer(),
            device_id_type=MESH,
        )

    def z_copy(self, step):
        return pltpu.make_async_remote_copy(
            src_ref=self.y_got.at[step],
            dst_ref=self.z_got.at[step],
            send_sem=self.z_sems.at[0, step],
            recv_sem=self.z_sems.at[1, step],
            device_id=self.me.device(z=self.me.after(step + 1)),
            device_id_type=MESH,
        )

    def begin(self):
        for step in range(self.me.depth):
            for i in range(len(self.grads)):
                self.y_copy(step, i).start()

    def fold(self, step):
        me = self.me
        for i in range(len(self.grads)):
            self.y_copy(step, i).wait_recv()
            add_into(
                self.y_got.at[step, pl.ds(self.starts[i], self.counts[i])],
                self.grads[i].at[me.after(step + 1), me.y],
            )
        if step < me.depth - 1:
            self.z_copy(step).start()

    def settle(self):
        me, depth = self.me, self.me.depth
        for step in range(depth - 1):
            self.z_copy(step).wait_recv()

        def tile(i, carry):
            at = pl.ds(pl.multiple_of(i * 16, 16), 16)
            value = self.y_got[depth - 1, at, :].astype(jnp.float32)
            for step in range(depth - 1):
                value = value + self.z_got[step, at, :].astype(jnp.float32)
            self.final[me.z, me.y, at, :] = value.astype(self.final.dtype)
            return carry

        lax.fori_loop(0, sum(self.counts) // 16, tile, 0)
        mine = self.final.at[me.z, me.y]
        for s in range(1, depth):
            self.spread(mine, self.fz_sems, s, me.device(z=me.after(s)))
        self.spread(mine, self.fy_sems, 0, me.y_peer())

    def spread(self, block, sems, slot, device):
        self.finals.append(send(block, block, sems.at[0, slot], sems.at[1, slot], device))

    def pass_on(self):
        me = self.me
        for s in range(1, me.depth):
            block = self.final.at[me.before(s), me.y]
            pltpu.make_async_copy(block, block, self.fz_sems.at[1, s]).wait()
            self.spread(block, self.fy_sems, s, me.y_peer())

    def deliver(self, y):
        me = self.me
        for s in range(me.depth):
            z = me.before(s)
            for i, out in enumerate(self.outs):

                def tile(t, carry):
                    at = pl.multiple_of(t * 16, 16)
                    out[z, y, pl.ds(at, 16), :] = self.final[
                        z, y, pl.ds(self.starts[i] + at, 16), :
                    ].astype(jnp.float32)
                    return carry

                lax.fori_loop(0, self.counts[i] // 16, tile, 0)

    def finish(self):
        me = self.me
        for s in range(me.depth):
            block = self.final.at[me.before(s), 1 - me.y]
            pltpu.make_async_copy(block, block, self.fy_sems.at[1, s]).wait()
        self.deliver(1 - me.y)

    def sent(self):
        for copy in self.finals:
            copy.wait_send()
        for step in range(self.me.depth):
            for i in range(len(self.grads)):
                self.y_copy(step, i).wait_send()
            if step < self.me.depth - 1:
                self.z_copy(step).wait_send()


def visible_columns(info_cols, info_rows):
    key_seg, key_pos = info_cols[:, 0:1], info_cols[:, 1:2]
    query_seg, query_pos = info_rows[0:1, :], info_rows[1:2, :]
    parent = jnp.where(query_seg >= 5, (query_seg - 5) // 2 + 1, -1)
    above = (key_seg == query_seg) | (key_seg == 0) | (key_seg == parent)
    return above & (key_pos <= query_pos)


def back_kernel(
    ep_size,
    heads,
    last_row,
    datt_own,
    heads_in,
    w_out,
    queries,
    keys,
    values,
    log_sums,
    info_cols,
    info_rows,
    cosine,
    sine,
    rows_in,
    w_query,
    w_key,
    w_value,
    small_in,
    gain,
    inputs,
    middle,
    query_out,
    key_out,
    value_out,
    out_out,
    grad_input,
    small_out,
    datt,
    bias,
    grad_heads,
    grad_proj,
    key_sum,
    value_sum,
    part_query,
    part_key,
    part_value,
    part_out,
    y_got,
    z_got,
    final,
    y_got_out,
    z_got_out,
    final_out,
    parts,
    core_got,
    pair_got,
    small_src,
    small_got,
    small_sum,
    own_sem,
    gather_sems,
    y_sems,
    z_sems,
    fz_sems,
    fy_sems,
    y_sems_out,
    z_sems_out,
    fz_sems_out,
    fy_sems_out,
    group_sems,
    small_sems,
    spread_sems,
    own_small_sem,
):
    me = Place(ep_size)
    depth = me.depth
    f32, bf16 = jnp.float32, jnp.bfloat16
    others = all_others(ep_size)
    meet(others)
    my_place = lax.axis_index("ep") * 4 + lax.axis_index("tp")
    tokens, width = rows_in.shape
    share = datt_own.shape[0]
    size = HEAD_DIMENSION
    groups = keys.shape[1] // size
    per_group = heads // groups
    scale = size ** (-0.5)
    tile = 512

    def dot(a, b, contract):
        return lax.dot_general(
            a, b, ((contract[:1], contract[1:]), ((), ())), preferred_element_type=f32
        )

    bias[...] = jnp.where(visible_columns(info_cols[...], info_rows[...]), 0.0, -1e30)
    group_gather_body(me, 4, datt_own, datt, own_sem, gather_sems)
    for n in range(width // tile):
        cols = slice(n * tile, (n + 1) * tile)
        grads = dot(heads_in[...], datt[:, :, :, cols].reshape(tokens, tile), (0, 0))
        part_out[:, :, :, cols] = grads.astype(bf16).reshape(depth, 2, -1, tile)
    out_sum = EpSum(
        me,
        [part_out],
        [out_out],
        y_got_out,
        z_got_out,
        final_out,
        (y_sems_out, z_sems_out, fz_sems_out, fy_sems_out),
    )
    out_sum.begin()
    for x in range(2):
        for c in range(2):
            at = pl.ds((x * 2 + c) * share, share)
            grad_heads[at, :] = dot(datt[x, c], w_out[...], (1, 1)).astype(bf16)

    def rotate_back_rows(grads):
        turned = jnp.concatenate([grads[:, size // 2 :], grads[:, : size // 2]], axis=1)
        return (grads * cosine[...] + turned * sine[...]).astype(bf16)

    for head in range(heads):
        group = head // per_group
        mine = slice(head * size, (head + 1) * size)
        shared = slice(group * size, (group + 1) * size)
        query, grad_head = queries[:, mine], grad_heads[:, mine]
        key, value = keys[:, shared], values[:, shared]
        scores = dot(key, query, (1, 1)) * scale + bias[...]
        probs = jnp.exp(scores - log_sums[head : head + 1, :])
        grad_probs = dot(value, grad_head, (1, 1))
        inner = jnp.sum(probs * grad_probs, axis=0, keepdims=True)
        grad_scores = (probs * (grad_probs - inner)).astype(bf16)
        grad_value = dot(probs.astype(bf16), grad_head, (1, 0))
        grad_key = dot(grad_scores, query, (1, 0)) * scale
        if head % per_group:
            grad_value = grad_value + value_sum[...]
            grad_key = grad_key + key_sum[...]
        value_sum[...] = grad_value
        key_sum[...] = grad_key
        grad_query = dot(grad_scores, key, (0, 0)) * scale
        grad_proj[:, mine] = rotate_back_rows(grad_query)
        if head % per_group == per_group - 1:
            at = heads * size + group * size
            grad_proj[:, at : at + size] = rotate_back_rows(grad_key)
            at += groups * size
            grad_proj[:, at : at + size] = grad_value.astype(bf16)
        if 1 <= head <= depth:
            out_sum.fold(head - 1)
    for step in range(max(heads - 1, 0), depth):
        out_sum.fold(step)
    out_sum.settle()

    ends = (heads * size, (heads + groups) * size, (heads + 2 * groups) * size)
    for n in range(width // tile):
        cols = slice(n * tile, (n + 1) * tile)
        grads = dot(grad_proj[...], rows_in[:, cols], (0, 0)).astype(bf16)
        part_query[:, :, :, cols] = grads[: ends[0]].reshape(depth, 2, -1, tile)
        part_key[:, :, :, cols] = grads[ends[0] : ends[1]].reshape(depth, 2, -1, tile)
        part_value[:, :, :, cols] = grads[ends[1] :].reshape(depth, 2, -1, tile)
    all_sum = EpSum(
        me,
        [part_query, part_key, part_value],
        [query_out, key_out, value_out],
        y_got,
        z_got,
        final,
        (y_sems, z_sems, fz_sems, fy_sems),
    )
    all_sum.begin()
    small_src[...] = small_in[...]
    for n in range(width // tile):
        cols = slice(n * tile, (n + 1) * tile)
        grads = (
            dot(grad_proj[:, : ends[0]], w_query[:, cols], (1, 0))
            + dot(grad_proj[:, ends[0] : ends[1]], w_key[:, cols], (1, 0))
            + dot(grad_proj[:, ends[1] :], w_value[:, cols], (1, 0))
        )
        parts[:, :, :, cols] = grads.astype(bf16).reshape(2, 2, share, tile)
        gained = jnp.sum(grads * rows_in[:, cols].astype(f32), axis=0, keepdims=True)
        gained = gained / gain[:, cols]
        for k in range(tile // 128):
            row = n * (tile // 128) + k
            small_src[last_row, row : row + 1, :] = gained[:, k * 128 : (k + 1) * 128]
    group = GroupTotal(me, parts, core_got, pair_got, group_sems)
    group.begin()
    small = [
        send(
            small_src.at[device[0] * 4 + device[1]],
            small_got.at[my_place],
            small_sems.at[0, k],
            small_sems.at[1, k],
            device,
        )
        for k, device in enumerate(others)
    ]
    own_small = pltpu.make_async_copy(
        small_src.at[my_place], small_got.at[my_place], own_small_sem
    )
    own_small.start()
    group.exchange()
    all_sum.fold(0)
    out_sum.pass_on()
    for step in range(1, depth):
        all_sum.fold(step)
    own_small.wait()
    for copy in small:
        copy.wait_recv()
    total = small_got[0]
    for k in range(1, 4 * ep_size):
        total = total + small_got[k]
    small_sum[...] = total
    spread = [
        send(
            small_sum,
            small_out.at[my_place],
            spread_sems.at[0, k],
            spread_sems.at[1, k],
            device,
        )
        for k, device in enumerate(others)
    ]
    small_out[my_place] = total

    def last(value, at):
        values_own = inputs[at, :].astype(f32)
        factor = norm_scale(values_own)
        return middle[at, :] + norm_back(values_own, factor, gain[...], value)

    group.finish(grad_input, last)
    out_sum.deliver(me.y)
    out_sum.finish()
    all_sum.settle()
    all_sum.pass_on()
    all_sum.deliver(me.y)
    all_sum.finish()
    for copy in spread:
        copy.wait()
    for copy in small:
        copy.wait_send()
    group.sent()
    out_sum.sent()
    all_sum.sent()


def back_by_links(
    datt_own,
    heads_in,
    w_out,
    queries,
    keys,
    values,
    log_sums,
    segment,
    position,
    rows_in,
    w_query,
    w_key,
    w_value,
    small,
    gain,
    inputs,
    middle,
    ep_size,
):
    tokens, width = rows_in.shape
    share = datt_own.shape[0]
    depth = ep_size // 2
    heads = queries.shape[1] // HEAD_DIMENSION
    places = 4 * ep_size
    bf16, f32 = jnp.bfloat16, jnp.float32
    dma = pltpu.SemaphoreType.DMA
    vmem = pl.BlockSpec(memory_space=pltpu.VMEM)
    cosine, sine = rope_tables(position, HEAD_DIMENSION)
    cosine = jnp.concatenate([cosine[:, 0], cosine[:, 0]], axis=1)
    sine = jnp.concatenate([sine[:, 0], -sine[:, 0]], axis=1)
    table = jnp.stack([segment, position])
    info_rows = jnp.pad(table, ((0, 6), (0, 0)))
    info_cols = jnp.pad(table.T, ((0, 0), (0, 126)))
    blocks = jnp.pad(small, ((0, places - small.shape[0]), (0, 0))).reshape(places, -1, 128)
    sizes = [w.shape[0] // ep_size for w in (w_query, w_key, w_value, w_out)]
    total = sum(sizes[:3])

    def partial(rows, dtype):
        return (depth, 2, rows, width), dtype

    def ep_buffers(rows):
        return [
            pltpu.VMEM((depth, rows, width), bf16),
            pltpu.VMEM((depth - 1, rows, width), bf16),
            pltpu.VMEM((depth, 2, rows, width), bf16),
        ]

    def ep_sems(arrays):
        return [dma((2, depth, arrays)), dma((2, depth)), dma((2, depth)), dma((2, depth))]

    got = pl.pallas_call(
        functools.partial(back_kernel, ep_size, heads, small.shape[0]),
        out_shape=tuple(jax.ShapeDtypeStruct(*partial(k, f32)) for k in sizes)
        + (
            jax.ShapeDtypeStruct((share, width), f32),
            jax.ShapeDtypeStruct(blocks.shape, f32),
        ),
        in_specs=[vmem] * 19,
        out_specs=(vmem,) * 6,
        scratch_shapes=[
            pltpu.VMEM((2, 2, share, width), bf16),
            pltpu.VMEM((tokens, tokens), f32),
            pltpu.VMEM(queries.shape, bf16),
            pltpu.VMEM((tokens, queries.shape[1] + 2 * keys.shape[1]), bf16),
            pltpu.VMEM((tokens, HEAD_DIMENSION), f32),
            pltpu.VMEM((tokens, HEAD_DIMENSION), f32),
        ]
        + [pltpu.VMEM(*partial(k, bf16)) for k in sizes]
        + ep_buffers(total)
        + ep_buffers(sizes[3])
        + [
            pltpu.VMEM((2, 2, share, width), bf16),
            pltpu.VMEM((2, share, width), bf16),
            pltpu.VMEM((share, width), bf16),
            pltpu.VMEM(blocks.shape, f32),
            pltpu.VMEM(blocks.shape, f32),
            pltpu.VMEM(blocks.shape[1:], f32),
            dma,
            dma((2, 12)),
        ]
        + ep_sems(3)
        + ep_sems(1)
        + [dma((2, 3)), dma((2, places - 1)), dma((2, places - 1)), dma],
        compiler_params=pltpu.CompilerParams(
            collective_id=5, has_side_effects=True, vmem_limit_bytes=60 * 1024 * 1024
        ),
        name="back_by_links",
    )(
        datt_own,
        heads_in,
        w_out,
        queries,
        keys,
        values,
        log_sums,
        info_cols,
        info_rows,
        cosine,
        sine,
        rows_in,
        w_query,
        w_key,
        w_value,
        blocks,
        gain[None, :],
        inputs,
        middle,
    )
    sums = [g.reshape(-1, width) for g in got[:4]]
    return sums, got[4], got[5].reshape(places, width)[: small.shape[0] + 1]


def group_rows(value_rows):
    return lax.all_gather(value_rows, "tp", axis=0, tiled=True)


def group_totals(value_rows, by_links, call):
    if by_links:
        return group_total(value_rows, lax.axis_size("ep"), call)
    return lax.psum_scatter(value_rows, "tp", scatter_dimension=0, tiled=True).astype(jnp.float32)


def gather_all(value_rows, by_links):
    if by_links:
        return gather_by_links(value_rows, lax.axis_size("ep"))
    return lax.all_gather(value_rows, ("ep", "tp"), axis=0, tiled=True)


LAST = 1 << 30


def pair_order(expert_ids, slot_order, expert_count):
    experts = jnp.arange(expert_count, dtype=jnp.int32)
    chosen = expert_ids.T[None, :, :] == experts[:, None, None]
    return jnp.min(jnp.where(chosen, slot_order.T[None, :, :], LAST), axis=1)


def kept_pairs(order):
    used = order < LAST
    counts = jnp.sum(used.astype(jnp.int32), axis=2)
    block = jnp.arange(order.shape[0], dtype=jnp.int32)
    earlier = block[None, :] < block[:, None]
    offsets = jnp.sum(jnp.where(earlier[:, :, None], counts[None, :, :], 0), axis=1)
    whole = offsets + counts <= CAP
    edge = (offsets < CAP) & ~whole
    edge_order = jnp.sum(jnp.where(edge[:, :, None], order, 0), axis=0)
    rank = jnp.sum((edge_order[:, :, None] < edge_order[:, None, :]).astype(jnp.int32), axis=1)
    early = offsets[:, :, None] + rank[None, :, :] < CAP
    return used & (whole[:, :, None] | (edge[:, :, None] & early))


def masked_softmax(logits, used):
    top = jnp.max(jnp.where(used, logits, -1e30), axis=-1, keepdims=True)
    powers = jnp.where(used, jnp.exp(logits - top), 0.0)
    return powers / jnp.sum(powers, axis=-1, keepdims=True)


def pair_codes(order_all, per_owner):
    expert_count = order_all.shape[1]
    first = lax.axis_index("ep") * per_owner
    turned = jnp.roll(order_all, -first, axis=1)
    kept = kept_pairs(turned[:, :per_owner])
    dropped = jnp.pad(~kept, ((0, 0), (0, expert_count - per_owner), (0, 0)))
    code = jnp.where(turned < LAST, dropped.astype(jnp.float32), -1.0)
    code = code.swapaxes(1, 2).reshape(-1, expert_count)
    lanes = -expert_count % 128
    return jnp.pad(code, ((0, 0), (0, lanes)), constant_values=-1.0).astype(jnp.bfloat16)


def run_experts(rows_all, cots_all, code, w_router, w_gate, w_up, w_down, by_links):
    per_owner, width, units = w_gate.shape
    expert_count = w_router.shape[0]
    ep_size, tp_size = lax.axis_size("ep"), lax.axis_size("tp")
    hidden = per_owner * units
    router = jnp.roll(w_router, -lax.axis_index("ep") * per_owner, axis=0)
    router = jnp.pad(router, ((0, -expert_count % 128), (0, 0)))
    enter = jnp.concatenate([w[e] for w in (w_gate, w_up) for e in range(per_owner)], axis=1)
    leave = w_down.reshape(hidden, width)
    if by_links:
        grads, sums, small, gate, up, down = experts_by_links(
            rows_all, cots_all, code, router, enter, leave, per_owner, ep_size
        )
        share = grads.shape[0]
        return (
            grads,
            sums,
            small[:, :, :per_owner, : share // 2].swapaxes(1, 2).reshape(expert_count, share).T,
            gate,
            up,
            down.reshape(w_down.shape),
        )
    used, kept = code >= 0, (code == 0).astype(jnp.float32)
    logits = jnp.einsum("rd,ed->re", rows_all, router, preferred_element_type=jnp.float32)
    gates = jnp.repeat((kept * masked_softmax(logits, used))[:, :per_owner], units, axis=1)
    act = jnp.dot(rows_all, enter, preferred_element_type=jnp.float32)
    gate_act, up_act = act[:, :hidden], act[:, hidden:]
    back_act = jnp.einsum("rd,fd->rf", cots_all, leave, preferred_element_type=jnp.float32)
    sigma = jax.nn.sigmoid(gate_act)
    value = gate_act * sigma * up_act
    weighted = (gates * value).astype(jnp.bfloat16)
    grad_hidden = gates * back_act
    turned = jnp.concatenate(
        [
            grad_hidden * up_act * sigma * (1.0 + gate_act * (1.0 - sigma)),
            grad_hidden * gate_act * sigma,
        ],
        axis=1,
    ).astype(jnp.bfloat16)
    small = kept[:, :per_owner] * jnp.sum((value * back_act).reshape(-1, per_owner, units), axis=2)
    grads = jnp.einsum("rf,df->rd", turned, enter, preferred_element_type=jnp.float32)
    sums = jnp.dot(weighted, leave, preferred_element_type=jnp.float32)

    def scatter(value_rows):
        return lax.psum_scatter(value_rows, ("ep", "tp"), scatter_dimension=0, tiled=True)

    columns = lax.dynamic_update_slice_in_dim(
        jnp.zeros((small.shape[0], expert_count), jnp.float32),
        small,
        lax.axis_index("ep") * per_owner,
        1,
    )
    both = jnp.einsum(
        "rd,rwef->wedf",
        rows_all,
        turned.reshape(-1, 2, per_owner, units),
        preferred_element_type=jnp.float32,
    )
    down = jnp.einsum("rf,rd->fd", weighted, cots_all, preferred_element_type=jnp.float32)
    return (
        scatter(grads.astype(jnp.bfloat16)).astype(jnp.float32),
        scatter(sums.astype(jnp.bfloat16)).astype(jnp.float32),
        scatter(columns),
        both[0],
        both[1],
        down.reshape(w_down.shape),
    )


def visible_block(query_seg, query_pos, query_row, key_seg, key_pos, key_row):
    seg_q = query_seg[:, None]
    seg_k = key_seg[None, :]
    above = (
        (seg_k == seg_q)
        | (seg_k == 0)
        | (seg_k >= 1) & (seg_k <= 4) & (seg_q >= 5) & ((seg_q - 5) // 2 + 1 == seg_k)
    )
    same_tree = query_row[:, None] // TREE_TOKENS == key_row[None, :] // TREE_TOKENS
    return above & same_tree & (key_pos[None, :] <= query_pos[:, None])


def block_scores(query_part, key_rows, allowed, scale):
    scores = (
        jnp.einsum("qkgd,pkd->kgqp", query_part, key_rows, preferred_element_type=jnp.float32)
        * scale
    )
    return jnp.where(allowed[None, None], scores, -1e30)


def attend_forward(query_rows, key_rows, value_rows, segment, position):
    total_rows = query_rows.shape[0]
    scale = query_rows.shape[-1] ** (-0.5)
    row_ids = jnp.arange(total_rows, dtype=jnp.int32)
    allowed = visible_block(segment, position, row_ids, segment, position, row_ids)
    scores = block_scores(query_rows, key_rows, allowed, scale)
    top_score = jnp.max(scores, axis=-1, keepdims=True)
    weights = jnp.exp(scores - top_score)
    weight_sum = jnp.sum(weights, axis=-1, keepdims=True)
    probs = (weights / weight_sum).astype(jnp.bfloat16)
    outputs = jnp.einsum(
        "kgqp,pkd->qkgd", probs, value_rows, preferred_element_type=jnp.float32
    ).astype(jnp.bfloat16)
    log_sums = [top_score + jnp.log(weight_sum)]
    return (outputs, log_sums)


def attend_backward(
    query_rows, key_rows, value_rows, segment, position, log_sums, grad_heads, block_rows
):
    total_rows = query_rows.shape[0]
    scale = query_rows.shape[-1] ** (-0.5)
    row_ids = jnp.arange(total_rows, dtype=jnp.int32)
    grad_keys = jnp.zeros(key_rows.shape, jnp.float32)
    grad_values = jnp.zeros(value_rows.shape, jnp.float32)
    grad_query = []
    for number, first_row in enumerate(range(0, total_rows, block_rows)):
        allowed = visible_block(segment, position, row_ids, segment, position, row_ids)
        scores = block_scores(query_rows, key_rows, allowed, scale)
        probs = jnp.where(allowed[None, None], jnp.exp(scores - log_sums[number]), 0.0)
        grad_values = jnp.einsum(
            "kgqp,qkgd->pkd",
            probs.astype(jnp.bfloat16),
            grad_heads,
            preferred_element_type=jnp.float32,
        )
        grad_probs = jnp.einsum(
            "qkgd,pkd->kgqp", grad_heads, value_rows, preferred_element_type=jnp.float32
        )
        inner = jnp.sum(probs * grad_probs, axis=-1, keepdims=True)
        grad_scores = (probs * (grad_probs - inner)).astype(jnp.bfloat16)
        grad_query.append(
            jnp.einsum("kgqp,pkd->qkgd", grad_scores, key_rows, preferred_element_type=jnp.float32)
            * scale
        )
        grad_keys = (
            jnp.einsum(
                "kgqp,qkgd->pkd", grad_scores, query_rows, preferred_element_type=jnp.float32
            )
            * scale
        )
    return (grad_query[0], grad_keys, grad_values)


def local(
    hidden_in,
    gain_attn,
    w_query,
    key_projection_weight,
    value_projection_weight,
    w_out,
    gain_ffn,
    w_router,
    w_gate,
    w_up,
    w_down,
    expert_ids,
    slot_order,
    segment,
    position,
    cotangent,
):
    model_width = w_query.shape[1]
    head_width = HEAD_DIMENSION
    local_heads = w_query.shape[0] // head_width
    local_kv = key_projection_weight.shape[0] // head_width
    group_factor = local_heads // local_kv
    token_count = expert_ids.shape[0]
    share = hidden_in.shape[0]
    row_start = lax.axis_index("tp") * share
    expert_count = w_router.shape[0]
    per_owner = w_gate.shape[0]
    block_rows = 512
    by_links = lax.axis_size("tp") == 4 and lax.axis_size("ep") == 8
    order = pair_order(expert_ids, slot_order, expert_count)
    cot_all = gather_all(cotangent, False)
    inputs_own = hidden_in.astype(jnp.float32)
    gain_one = gain_attn.astype(jnp.float32)
    gain_two = gain_ffn.astype(jnp.float32)
    scale_one = norm_scale(inputs_own)
    first_own = (inputs_own * scale_one * gain_one).astype(jnp.bfloat16)
    if by_links:
        first_normalized, order_all = front_gather(first_own, order, lax.axis_size("ep"))
    else:
        first_normalized = group_rows(first_own)
        order_all = lax.all_gather(order, "ep")
    code = pair_codes(order_all, per_owner)
    cosine_lookup, sine_lookup = rope_tables(position, head_width)
    query_proj = jnp.einsum(
        "rd,fd->rf", first_normalized, w_query, preferred_element_type=jnp.float32
    ).reshape(token_count, local_heads, head_width)
    key_proj = jnp.einsum(
        "rd,fd->rf", first_normalized, key_projection_weight, preferred_element_type=jnp.float32
    ).reshape(token_count, local_kv, head_width)
    query_rows = (
        apply_rotation(query_proj, cosine_lookup, sine_lookup)
        .astype(jnp.bfloat16)
        .reshape(token_count, local_kv, group_factor, head_width)
    )
    key_rows = apply_rotation(key_proj, cosine_lookup, sine_lookup).astype(jnp.bfloat16)
    value_rows = (
        jnp.einsum(
            "rd,fd->rf",
            first_normalized,
            value_projection_weight,
            preferred_element_type=jnp.float32,
        )
        .astype(jnp.bfloat16)
        .reshape(token_count, local_kv, head_width)
    )
    head_outputs, log_sums = attend_forward(query_rows, key_rows, value_rows, segment, position)
    head_outputs = head_outputs.reshape(token_count, local_heads * head_width)
    middle_own = inputs_own + group_totals(
        jnp.dot(head_outputs, w_out, preferred_element_type=jnp.float32).astype(jnp.bfloat16),
        by_links,
        3,
    )
    scale_two = norm_scale(middle_own)
    normed_own = (middle_own * scale_two * gain_two).astype(jnp.bfloat16)
    normed_two = gather_all(normed_own, by_links)
    used = lax.dynamic_slice_in_dim(order, row_start, share, 1).T < LAST
    gates = masked_softmax(
        jnp.einsum("rd,ed->re", normed_own, w_router, preferred_element_type=jnp.float32), used
    )
    grad_normed_own, combined_own, grad_gates_own, grad_w_gate, grad_w_up, grad_w_down = (
        run_experts(normed_two, cot_all, code, w_router, w_gate, w_up, w_down, by_links)
    )
    output_own = (middle_own + combined_own).astype(jnp.bfloat16)
    inner_gate = jnp.sum(gates * grad_gates_own, axis=-1, keepdims=True)
    grad_logits = gates * (grad_gates_own - inner_gate)
    router_f = w_router.astype(jnp.float32)
    grad_normed_own = grad_normed_own + jnp.dot(grad_logits, router_f, precision=EXACT_PRECISION)
    grad_router = jnp.dot(grad_logits.T, normed_own.astype(jnp.float32), precision=EXACT_PRECISION)
    grad_gain_ffn = jnp.sum(grad_normed_own * middle_own * scale_two, axis=0)
    grad_middle = cotangent.astype(jnp.float32) + norm_back(
        middle_own, scale_two, gain_two, grad_normed_own
    )
    if by_links:
        (grad_w_query, grad_w_key, grad_w_value, grad_w_out), grad_input, small = back_by_links(
            grad_middle.astype(jnp.bfloat16),
            head_outputs,
            w_out,
            query_rows.reshape(token_count, -1),
            key_rows.reshape(token_count, -1),
            value_rows.reshape(token_count, -1),
            jnp.pad(log_sums[0].reshape(local_heads, token_count), ((0, -local_heads % 8), (0, 0))),
            segment,
            position,
            first_normalized,
            w_query,
            key_projection_weight,
            value_projection_weight,
            jnp.concatenate([grad_router, grad_gain_ffn[None, :]], axis=0),
            gain_one,
            hidden_in,
            grad_middle,
            lax.axis_size("ep"),
        )
    else:
        grad_attn = group_rows(grad_middle.astype(jnp.bfloat16))
        grad_w_out = jnp.einsum(
            "rf,rd->fd", head_outputs, grad_attn, preferred_element_type=jnp.float32
        )
        grad_w_out = lax.psum(grad_w_out.astype(jnp.bfloat16), "ep").astype(jnp.float32)
        grad_heads = (
            jnp.einsum("rd,fd->rf", grad_attn, w_out, preferred_element_type=jnp.float32)
            .astype(jnp.bfloat16)
            .reshape(token_count, local_kv, group_factor, head_width)
        )
        grad_query, grad_keys, grad_values = attend_backward(
            query_rows, key_rows, value_rows, segment, position, log_sums, grad_heads, block_rows
        )
        grad_query_proj = (
            rotate_back(
                grad_query.reshape(token_count, local_heads, head_width), cosine_lookup, sine_lookup
            )
            .astype(jnp.bfloat16)
            .reshape(token_count, local_heads * head_width)
        )
        grad_key_proj = (
            rotate_back(grad_keys, cosine_lookup, sine_lookup)
            .astype(jnp.bfloat16)
            .reshape(token_count, local_kv * head_width)
        )
        grad_value_proj = grad_values.astype(jnp.bfloat16).reshape(token_count, local_kv * head_width)
        grad_w_query = jnp.einsum(
            "rf,rd->fd", grad_query_proj, first_normalized, preferred_element_type=jnp.float32
        )
        grad_w_key = jnp.einsum(
            "rf,rd->fd", grad_key_proj, first_normalized, preferred_element_type=jnp.float32
        )
        grad_w_value = jnp.einsum(
            "rf,rd->fd", grad_value_proj, first_normalized, preferred_element_type=jnp.float32
        )
        grad_normed_one = jnp.einsum(
            "rf,fd->rd", grad_query_proj, w_query, preferred_element_type=jnp.float32
        )
        grad_normed_one = grad_normed_one + jnp.einsum(
            "rf,fd->rd", grad_key_proj, key_projection_weight, preferred_element_type=jnp.float32
        )
        grad_normed_one = grad_normed_one + jnp.einsum(
            "rf,fd->rd", grad_value_proj, value_projection_weight, preferred_element_type=jnp.float32
        )
        grad_gain_attn = jnp.sum(grad_normed_one * first_normalized.astype(jnp.float32), axis=0)
        small = jnp.concatenate(
            [grad_router, grad_gain_ffn[None, :], (grad_gain_attn / gain_one)[None, :]], axis=0
        )
        grad_w_query, grad_w_key, grad_w_value = (
            lax.psum(g.astype(jnp.bfloat16), "ep").astype(jnp.float32)
            for g in (grad_w_query, grad_w_key, grad_w_value)
        )
        grad_one_own = group_totals(grad_normed_one.astype(jnp.bfloat16), by_links, None)
        small = lax.psum(small, ("ep", "tp"))
        grad_input = grad_middle + norm_back(inputs_own, scale_one, gain_one, grad_one_own)
    grad_router = small[:expert_count]
    grad_gain_ffn, grad_gain_attn = small[expert_count], small[expert_count + 1]
    return (
        output_own,
        grad_input,
        grad_gain_attn,
        grad_w_query,
        grad_w_key,
        grad_w_value,
        grad_w_out,
        grad_gain_ffn,
        grad_router,
        grad_w_gate,
        grad_w_up,
        grad_w_down,
    )


def solution(mesh):
    placed = (
        P(("ep", "tp"), None),
        P(),
        P("tp", None),
        P("tp", None),
        P("tp", None),
        P("tp", None),
        P(),
        P(),
        P("ep", None, "tp"),
        P("ep", None, "tp"),
        P("ep", "tp", None),
        P("ep", None),
        P("ep", None),
        P("ep"),
        P("ep"),
        P(("ep", "tp"), None),
    )
    return jax.shard_map(
        local,
        mesh=mesh,
        in_specs=placed,
        out_specs=(
            P(("ep", "tp"), None),
            P(("ep", "tp"), None),
            P(),
            P("tp", None),
            P("tp", None),
            P("tp", None),
            P("tp", None),
            P(),
            P(),
            P("ep", None, "tp"),
            P("ep", None, "tp"),
            P("ep", "tp", None),
        ),
        check_vma=False,
    )
```

```python
import functools

import jax
import jax.numpy as jnp
from jax import lax
from jax.experimental import pallas as pl
from jax.experimental.pallas import tpu as pltpu
from jax.sharding import PartitionSpec as P

HEAD_DIMENSION = 64
TREE_TOKENS = 512
CAP = 2304


EPSILON = 1e-06
ROPE_BASE = 10000.0
EXACT_PRECISION = lax.Precision.HIGHEST


def rope_tables(position, head_width):
    half_width = head_width // 2
    freqs = ROPE_BASE ** (-(jnp.arange(half_width, dtype=jnp.float32) * 2.0 / head_width))
    angle = position.astype(jnp.float32)[:, None] * freqs[None, :]
    return (jnp.cos(angle)[:, None, :], jnp.sin(angle)[:, None, :])


def apply_rotation(value_rows, cosine_lookup, sine_lookup):
    half_width = value_rows.shape[-1] // 2
    first = value_rows[..., :half_width]
    second = value_rows[..., half_width:]
    return jnp.concatenate(
        [
            first * cosine_lookup - second * sine_lookup,
            first * sine_lookup + second * cosine_lookup,
        ],
        axis=-1,
    )


def rotate_back(grads, cosine_lookup, sine_lookup):
    half_width = grads.shape[-1] // 2
    first = grads[..., :half_width]
    second = grads[..., half_width:]
    return jnp.concatenate(
        [
            first * cosine_lookup + second * sine_lookup,
            second * cosine_lookup - first * sine_lookup,
        ],
        axis=-1,
    )


def norm_scale(value_rows):
    return lax.rsqrt(jnp.mean(value_rows * value_rows, axis=-1, keepdims=True) + EPSILON)


def norm_back(value_rows, scale, gain, grad_normed):
    weighted = grad_normed * gain
    inner = jnp.mean(value_rows * weighted, axis=-1, keepdims=True)
    grad_values = scale * weighted - value_rows * (scale * scale * scale) * inner
    return grad_values


MESH = pl.DeviceIdType.MESH


class Place:
    def __init__(self, ep_size):
        self.depth = ep_size // 2
        ep, tp = lax.axis_index("ep"), lax.axis_index("tp")
        self.z, self.y = ep // 2, ep % 2
        self.x, self.c = tp // 2, tp % 2

    def device(self, z=None, y=None, x=None, c=None):
        z = self.z if z is None else z
        y = self.y if y is None else y
        x = self.x if x is None else x
        c = self.c if c is None else c
        return (z * 2 + y, x * 2 + c)

    def sibling(self):
        return self.device(c=1 - self.c)

    def x_peer(self):
        return self.device(x=1 - self.x)

    def y_peer(self):
        return self.device(y=1 - self.y)

    def after(self, step):
        return lax.rem(self.z + step, self.depth)

    def before(self, step):
        return lax.rem(self.z + self.depth - step, self.depth)


def meet(devices):
    barrier = pltpu.get_barrier_semaphore()
    for device in devices:
        pl.semaphore_signal(barrier, inc=1, device_id=device, device_id_type=MESH)
    pl.semaphore_wait(barrier, len(devices))


def send(src, dst, send_sem, recv_sem, device):
    copy = pltpu.make_async_remote_copy(
        src_ref=src,
        dst_ref=dst,
        send_sem=send_sem,
        recv_sem=recv_sem,
        device_id=device,
        device_id_type=MESH,
    )
    copy.start()
    return copy


def gather_kernel(ep_size, own, out, own_sem, z_sems, pair_sems, core_sems):
    me = Place(ep_size)
    depth = me.depth
    half = own.shape[0] // 2
    z_send, z_recv = z_sems.at[0], z_sems.at[1]
    pair_send, pair_recv = pair_sems.at[0], pair_sems.at[1]
    core_send, core_recv = core_sems.at[0], core_sems.at[1]
    meet(
        [me.sibling(), me.x_peer(), me.y_peer()]
        + [me.device(z=me.after(s)) for s in range(1, depth)]
    )

    def rows(part):
        return pl.ds(part * half, half)

    def block(step, y, x, part, c=None):
        return out.at[me.before(step), y, x, me.c if c is None else c, rows(part)]

    started = []

    def forward(source, target, sems, slot, device):
        started.append(send(source, target, sems[0].at[slot], sems[1].at[slot], device))

    for s in range(1, depth):
        for part in range(2):
            forward(
                own.at[rows(part)],
                out.at[me.z, me.y, me.x, me.c, rows(part)],
                (z_send, z_recv),
                (s - 1) * 2 + part,
                me.device(z=me.after(s)),
            )
    local = pltpu.make_async_copy(own, out.at[me.z, me.y, me.x, me.c], own_sem)
    local.start()
    local.wait()

    kinds = [
        (me.y, me.x, 0),
        (me.y, me.x, 1),
        (1 - me.y, me.x, 0),
        (me.y, 1 - me.x, 1),
        (1 - me.y, me.x, 1),
        (1 - me.y, 1 - me.x, 1),
        (me.y, 1 - me.x, 0),
        (1 - me.y, 1 - me.x, 0),
    ]
    x_route = {0: 6, 2: 7, 1: 3}
    y_route = {0: 2, 1: 4, 3: 5}

    def landed(step, kind):
        y, x, part = kinds[kind]
        place = block(step, y, x, part)
        if kind < 2:
            if step > 0:
                sem = z_recv.at[(step - 1) * 2 + part]
                pltpu.make_async_copy(place, place, sem).wait()
        else:
            pltpu.make_async_copy(place, place, pair_recv.at[step * 8 + kind]).wait()

    def pass_on(step, kind):
        y, x, part = kinds[kind]
        place = block(step, y, x, part)
        if kind in x_route:
            forward(place, place, (pair_send, pair_recv), step * 8 + x_route[kind], me.x_peer())
        if kind in y_route:
            forward(place, place, (pair_send, pair_recv), step * 8 + y_route[kind], me.y_peer())
        forward(place, place, (core_send, core_recv), step * 8 + kind, me.sibling())

    for turn in range(depth + 2):
        for step, group in ((turn, (0, 1)), (turn - 1, (2, 3)), (turn - 2, (4, 5, 6, 7))):
            if 0 <= step < depth:
                for kind in group:
                    landed(step, kind)
                    pass_on(step, kind)
    for step in range(depth):
        for kind in range(8):
            y, x, part = kinds[kind]
            place = block(step, y, x, part, 1 - me.c)
            pltpu.make_async_copy(place, place, core_recv.at[step * 8 + kind]).wait()
    for copy in started:
        copy.wait_send()


def gather_by_links(value_rows, ep_size):
    rows, width = value_rows.shape
    depth = ep_size // 2
    dma = pltpu.SemaphoreType.DMA
    every = pl.pallas_call(
        functools.partial(gather_kernel, ep_size),
        out_shape=jax.ShapeDtypeStruct((depth, 2, 2, 2, rows, width), value_rows.dtype),
        in_specs=[pl.BlockSpec(memory_space=pl.ANY)],
        out_specs=pl.BlockSpec(memory_space=pl.ANY),
        scratch_shapes=[
            dma,
            dma((2, 2 * depth - 2)),
            dma((2, 8 * depth)),
            dma((2, 8 * depth)),
        ],
        compiler_params=pltpu.CompilerParams(collective_id=1, has_side_effects=True),
        name="gather_by_links",
    )(value_rows)
    return every.reshape(-1, width)


def add_into(target, other):
    def tile(i, carry):
        at = pl.ds(pl.multiple_of(i * 16, 16), 16)
        target[at, :] = target[at, :] + other[at, :]
        return carry

    lax.fori_loop(0, target.shape[0] // 16, tile, 0)


def front_gather_kernel(
    ep_size, pieces, own, table, out, tables, own_sem, sems, table_own_sem, table_sems
):
    me = Place(ep_size)
    mine = lax.axis_index("ep")
    tp = lax.axis_index("tp")
    peers = [(lax.rem(mine + k, ep_size), tp) for k in range(1, ep_size)]
    meet([me.sibling(), me.x_peer()] + peers)
    local = pltpu.make_async_copy(table, tables.at[mine], table_own_sem)
    local.start()
    copies = [
        send(table, tables.at[mine], table_sems.at[0, k], table_sems.at[1, k], device)
        for k, device in enumerate(peers)
    ]
    group_gather_body(me, pieces, own, out, own_sem, sems)
    local.wait()
    for copy in copies:
        copy.wait()


def front_gather(value_rows, table, ep_size):
    rows, width = value_rows.shape
    pieces = 4
    dma = pltpu.SemaphoreType.DMA
    anywhere = pl.BlockSpec(memory_space=pl.ANY)
    every, tables = pl.pallas_call(
        functools.partial(front_gather_kernel, ep_size, pieces),
        out_shape=(
            jax.ShapeDtypeStruct((2, 2, rows, width), value_rows.dtype),
            jax.ShapeDtypeStruct((ep_size,) + table.shape, table.dtype),
        ),
        in_specs=[anywhere] * 2,
        out_specs=(anywhere,) * 2,
        scratch_shapes=[dma, dma((2, 3 * pieces)), dma, dma((2, ep_size - 1))],
        compiler_params=pltpu.CompilerParams(collective_id=6, has_side_effects=True),
        name="front_gather",
    )(value_rows, table)
    return every.reshape(-1, width), tables


def group_gather_body(me, pieces, own, out, own_sem, sems):
    size = own.shape[0] // pieces
    started = []
    local = pltpu.make_async_copy(own, out.at[me.x, me.c], own_sem)
    local.start()

    def at(p):
        return pl.ds(p * size, size)

    def go(kind, p, src, dst, device):
        slot = kind * pieces + p
        started.append(send(src, dst, sems.at[0, slot], sems.at[1, slot], device))

    for p in range(pieces):
        go(0, p, own.at[at(p)], out.at[me.x, me.c, at(p)], me.x_peer())
    for p in range(pieces):
        go(1, p, own.at[at(p)], out.at[me.x, me.c, at(p)], me.sibling())
    for p in range(pieces):
        block = out.at[1 - me.x, me.c, at(p)]
        pltpu.make_async_copy(block, block, sems.at[1, p]).wait()
        go(2, p, block, block, me.sibling())
    for p in range(pieces):
        for kind, x in ((1, me.x), (2, 1 - me.x)):
            block = out.at[x, 1 - me.c, at(p)]
            pltpu.make_async_copy(block, block, sems.at[1, kind * pieces + p]).wait()
    local.wait()
    for copy in started:
        copy.wait_send()


class GroupTotal:
    def __init__(self, me, parts, core_got, pair_got, sems):
        self.me, self.parts, self.core_got, self.pair_got = me, parts, core_got, pair_got
        self.core = [
            pltpu.make_async_remote_copy(
                src_ref=parts.at[x, 1 - me.c],
                dst_ref=core_got.at[x],
                send_sem=sems.at[0, k],
                recv_sem=sems.at[1, k],
                device_id=me.sibling(),
                device_id_type=MESH,
            )
            for k, x in enumerate((1 - me.x, me.x))
        ]
        self.pair = pltpu.make_async_remote_copy(
            src_ref=core_got.at[1 - me.x],
            dst_ref=pair_got,
            send_sem=sems.at[0, 2],
            recv_sem=sems.at[1, 2],
            device_id=me.x_peer(),
            device_id_type=MESH,
        )

    def begin(self):
        for copy in self.core:
            copy.start()

    def exchange(self):
        self.core[0].wait_recv()
        far = 1 - self.me.x
        add_into(self.core_got.at[far], self.parts.at[far, self.me.c])
        self.pair.start()

    def finish(self, out, change=lambda value, at: value):
        self.core[1].wait_recv()
        self.pair.wait_recv()

        def tile(i, carry):
            at = pl.ds(pl.multiple_of(i * 16, 16), 16)
            value = (
                self.parts[self.me.x, self.me.c, at, :].astype(jnp.float32)
                + self.core_got[self.me.x, at, :].astype(jnp.float32)
                + self.pair_got[at, :].astype(jnp.float32)
            )
            out[at, :] = change(value, at)
            return carry

        lax.fori_loop(0, out.shape[0] // 16, tile, 0)

    def sent(self):
        for copy in self.core + [self.pair]:
            copy.wait_send()


def group_total_kernel(ep_size, parts, out, core_got, pair_got, sems):
    me = Place(ep_size)
    meet([me.sibling(), me.x_peer()])
    total = GroupTotal(me, parts, core_got, pair_got, sems)
    total.begin()
    total.exchange()
    total.finish(out)
    total.sent()


def group_total(value_rows, ep_size, call):
    rows, width = value_rows.shape[0] // 4, value_rows.shape[1]
    vmem = pl.BlockSpec(memory_space=pltpu.VMEM)
    return pl.pallas_call(
        functools.partial(group_total_kernel, ep_size),
        out_shape=jax.ShapeDtypeStruct((rows, width), jnp.float32),
        in_specs=[vmem],
        out_specs=vmem,
        scratch_shapes=[
            pltpu.VMEM((2, rows, width), jnp.bfloat16),
            pltpu.VMEM((rows, width), jnp.bfloat16),
            pltpu.SemaphoreType.DMA((2, 3)),
        ],
        compiler_params=pltpu.CompilerParams(
            collective_id=call, has_side_effects=True, vmem_limit_bytes=32 * 1024 * 1024
        ),
        name="group_total",
    )(value_rows.reshape(2, 2, rows, width))


def all_others(ep_size):
    ep, tp = lax.axis_index("ep"), lax.axis_index("tp")
    return [
        (lax.rem(ep + k // 4, ep_size), lax.rem(tp + k % 4, 4)) for k in range(1, ep_size * 4)
    ]


def experts_kernel(
    ep_size,
    per_owner,
    rows_in,
    cots_in,
    code_in,
    router,
    enter,
    leave,
    grad_out,
    sum_out,
    small_out,
    gate_out,
    up_out,
    down_out,
    rows_buf,
    cots_buf,
    weighted,
    turned,
    enter_sum,
    parts,
    core_got,
    pair_got,
    last_got,
    z_got,
    small_in,
    small_got,
    load_sems,
    core_sems,
    pair_sems,
    last_sems,
    z_sems,
    small_sems,
    own_sem,
):
    me = Place(ep_size)
    depth = me.depth
    steps = 2 * depth
    blocks = 2 * steps
    width = router.shape[1]
    share = rows_buf.shape[2]
    tokens = 4 * share
    units = leave.shape[0] // per_owner
    hidden = per_owner * units
    f32, bf16 = jnp.float32, jnp.bfloat16
    others = all_others(ep_size)
    meet(others)
    my_place = lax.axis_index("ep") * 4 + lax.axis_index("tp")

    def where(b):
        return me.after(b // 4 + 1), lax.rem(1 - me.y + b % 2, 2)

    def half(b):
        return pl.ds(pl.multiple_of(b // 2 % 2 * share, share), share)

    def load(b, which):
        z, y = where(b)
        source, target = ((rows_in, rows_buf), (cots_in, cots_buf))[which]
        slot = lax.rem(b, 2)
        return pltpu.make_async_copy(
            source.at[z, y, :, half(b)], target.at[slot], load_sems.at[slot, which]
        )

    def core_copy(b):
        y = where(b)[1]
        return pltpu.make_async_remote_copy(
            src_ref=parts.at[lax.rem(b, 2), :, :, 1 - me.c],
            dst_ref=core_got.at[b // 2, y],
            send_sem=core_sems.at[0, b],
            recv_sem=core_sems.at[1, b],
            device_id=me.sibling(),
            device_id_type=MESH,
        )

    def grad_pair(b):
        y = where(b)[1]
        return pltpu.make_async_remote_copy(
            src_ref=core_got.at[b // 2, y, 0, 1 - me.x],
            dst_ref=pair_got.at[b // 2, 0, y],
            send_sem=pair_sems.at[0, b],
            recv_sem=pair_sems.at[1, b],
            device_id=me.x_peer(),
            device_id_type=MESH,
        )

    def sum_pair(step):
        return pltpu.make_async_remote_copy(
            src_ref=core_got.at[step, 1 - me.y, 1],
            dst_ref=pair_got.at[step, 1],
            send_sem=pair_sems.at[0, blocks + step],
            recv_sem=pair_sems.at[1, blocks + step],
            device_id=me.y_peer(),
            device_id_type=MESH,
        )

    def last_copy(step, which):
        return pltpu.make_async_remote_copy(
            src_ref=pair_got.at[step, which, (1 - me.y, 1 - me.x)[which]],
            dst_ref=last_got.at[step, which],
            send_sem=last_sems.at[0, step, which],
            recv_sem=last_sems.at[1, step, which],
            device_id=(me.y_peer(), me.x_peer())[which],
            device_id_type=MESH,
        )

    def z_copy(step, which):
        return pltpu.make_async_remote_copy(
            src_ref=last_got.at[step, which],
            dst_ref=z_got.at[step, which],
            send_sem=z_sems.at[0, step, which],
            recv_sem=z_sems.at[1, step, which],
            device_id=me.device(z=me.after(step // 2 + 1)),
            device_id_type=MESH,
        )

    def small_copy(k, device):
        return pltpu.make_async_remote_copy(
            src_ref=small_in.at[device[0] * 4 + device[1]],
            dst_ref=small_got.at[my_place],
            send_sem=small_sems.at[0, k],
            recv_sem=small_sems.at[1, k],
            device_id=device,
            device_id_type=MESH,
        )

    def dot(a, b, contract):
        return lax.dot_general(
            a, b, ((contract[:1], contract[1:]), ((), ())), preferred_element_type=f32
        )

    def spread(columns):
        return jnp.concatenate(
            [jnp.broadcast_to(columns[:, e : e + 1], (tokens, units)) for e in range(per_owner)],
            axis=1,
        )

    def compute(b):
        z, y = where(b)
        slot = lax.rem(b, 2)
        rows = rows_buf[slot].reshape(tokens, width)
        cots = cots_buf[slot].reshape(tokens, width)
        code = code_in[z * 2 + y, :, half(b), :].astype(f32).reshape(tokens, -1)
        used = code >= 0.0
        logits = jnp.where(used, dot(rows, router[...], (1, 1)), -1e30)
        top = jnp.max(logits, axis=1, keepdims=True)
        powers = jnp.where(used, jnp.exp(logits - top), 0.0)
        kept = jnp.where(code == 0.0, 1.0, 0.0)
        gates = spread(kept * powers / jnp.sum(powers, axis=1, keepdims=True))
        act = dot(rows, enter[...], (1, 0))
        gate_act, up_act = act[:, :hidden], act[:, hidden:]
        back_act = dot(cots, leave[...], (1, 1))
        sigma = jax.nn.sigmoid(gate_act)
        swish = gate_act * sigma
        value = swish * up_act
        gate_parts = spread(kept) * (value * back_act)
        lane = lax.broadcasted_iota(jnp.int32, (8, hidden), 1)
        pick = lax.broadcasted_iota(jnp.int32, (8, hidden), 0)
        mine = jnp.where((lane >= pick * units) & (lane < (pick + 1) * units), 1.0, 0.0)
        grad_gates = lax.dot_general(
            mine,
            gate_parts,
            (((1,), (1,)), ((), ())),
            precision=EXACT_PRECISION,
            preferred_element_type=f32,
        )
        for k in range(4):
            small_in[(z * 2 + y) * 4 + k, b // 2 % 2, :, :share] = grad_gates[
                :, k * share : (k + 1) * share
            ]
        weighted[...] = (gates * value).astype(bf16)
        grad_hidden = gates * back_act
        turned[:, :hidden] = (
            grad_hidden * up_act * sigma * (1.0 + gate_act * (1.0 - sigma))
        ).astype(bf16)
        turned[:, hidden:] = (grad_hidden * swish).astype(bf16)
        tile = 512
        for n in range(width // tile):
            cols = slice(n * tile, (n + 1) * tile)
            grads = dot(turned[...], enter[cols, :], (1, 1)).astype(bf16)
            sums = dot(weighted[...], leave[:, cols], (1, 0)).astype(bf16)
            for x in range(2):
                for c in range(2):
                    at = slice((x * 2 + c) * share, (x * 2 + c + 1) * share)
                    parts[slot, 0, x, c, :, cols] = grads[at]
                    parts[slot, 1, x, c, :, cols] = sums[at]

    def weight_sums(b):
        slot = lax.rem(b, 2)
        tile = 512
        for n in range(width // tile):
            cols = slice(n * tile, (n + 1) * tile)
            rows = rows_buf[slot, :, :, cols].reshape(tokens, tile)
            cots = cots_buf[slot, :, :, cols].reshape(tokens, tile)
            enter_sum[:, cols] += dot(turned[...], rows, (0, 0))
            down_out[:, cols] += dot(weighted[...], cots, (0, 0))

    enter_sum[...] = jnp.zeros_like(enter_sum)
    down_out[...] = jnp.zeros_like(down_out)
    small_in[...] = jnp.zeros_like(small_in)
    for which in range(2):
        load(0, which).start()

    def during(i, lag, body, even=False):
        b = i - lag
        inside = (b >= 0) & (b < blocks)
        if even:
            inside &= b % 2 == 0
        pl.when(inside)(lambda: body(b))

    def finish_sum(which):
        def body(b):
            step = b // 2
            last_copy(step, which).wait_recv()
            add_into(last_got.at[step, which], pair_got.at[step, which, (me.y, me.x)[which]])

            @pl.when(step < steps - 2)
            def _():
                z_copy(step, which).start()

        return body

    def work(b):
        for which in range(2):
            load(b, which).wait()

        @pl.when(b + 1 < blocks)
        def _():
            for which in range(2):
                load(b + 1, which).start()

        compute(b)
        core_copy(b).start()
        weight_sums(b)

    def core_sum(b):
        y = where(b)[1]
        core_copy(b).wait_recv()
        for which in range(2):
            for x in range(2):
                add_into(
                    core_got.at[b // 2, y, which, x], parts.at[lax.rem(b, 2), which, x, me.c]
                )
        grad_pair(b).start()

        @pl.when(b % 2 == 0)
        def _():
            sum_pair(b // 2).start()

        core_copy(b).wait_send()

    def out_pair(b):
        step = b // 2
        sum_pair(step).wait_recv()
        for x in range(2):
            add_into(pair_got.at[step, 1, x], core_got.at[step, me.y, 1, x])
        last_copy(step, 1).start()

    def back_pair(b):
        y = where(b)[1]
        step = b // 2
        grad_pair(b).wait_recv()
        add_into(pair_got.at[step, 0, y], core_got.at[step, y, 0, me.x])

        @pl.when(b % 2 == 0)
        def _():
            last_copy(step, 0).start()

    def small_send(b):
        for k, device in enumerate(others):
            small_copy(k, device).start()
        pltpu.make_async_copy(small_in.at[my_place], small_got.at[my_place], own_sem).start()
        for e in range(per_owner):
            gate_out[e] = enter_sum[e * units : (e + 1) * units, :].T
            up_out[e] = enter_sum[hidden + e * units : hidden + (e + 1) * units, :].T

    def turn(i, carry):
        during(i, 6, finish_sum(1), True)
        during(i, 0, work)
        during(i, 1, core_sum)
        during(i, 7, finish_sum(0), True)
        during(i, 3, out_pair, True)
        during(i, 4, back_pair)
        pl.when(i == blocks)(lambda: small_send(i))
        return carry

    lax.fori_loop(0, blocks + 7, turn, 0)
    pltpu.make_async_copy(small_in.at[my_place], small_got.at[my_place], own_sem).wait()
    for k, device in enumerate(others):
        small_copy(k, device).wait()
    for ep in range(ep_size):
        total = small_got[ep * 4]
        for tp in range(1, 4):
            total = total + small_got[ep * 4 + tp]
        small_out[ep] = total
    for step in range(steps - 2):
        for which in range(2):
            z_copy(step, which).wait_recv()

    def finish(which, part, target):
        def tile(i, carry):
            at = pl.multiple_of(i * 16, 16)
            total = last_got[steps - 2 + part, which, pl.ds(at, 16), :].astype(f32)
            for step in range(depth - 1):
                total = total + z_got[2 * step + part, which, pl.ds(at, 16), :].astype(f32)
            target[pl.ds(part * share + at, 16), :] = total
            return carry

        lax.fori_loop(0, share // 16, tile, 0)

    for part in range(2):
        finish(0, part, grad_out)
        finish(1, part, sum_out)

    def sent(step, carry):
        grad_pair(2 * step).wait_send()
        grad_pair(2 * step + 1).wait_send()
        sum_pair(step).wait_send()
        for which in range(2):
            last_copy(step, which).wait_send()

        @pl.when(step < steps - 2)
        def _():
            for which in range(2):
                z_copy(step, which).wait_send()

        return carry

    lax.fori_loop(0, steps, sent, 0)


def experts_by_links(rows_all, cots_all, code, router, enter, leave, per_owner, ep_size):
    total_rows, width = rows_all.shape
    depth = ep_size // 2
    tokens = total_rows // ep_size
    rows = tokens // 4
    half, steps = rows // 2, 2 * depth
    hidden = leave.shape[0]
    units = hidden // per_owner
    bf16, f32 = jnp.bfloat16, jnp.float32
    dma = pltpu.SemaphoreType.DMA
    vmem = pl.BlockSpec(memory_space=pltpu.VMEM)
    anywhere = pl.BlockSpec(memory_space=pl.ANY)
    places = 4 * ep_size
    blocks = (depth, 2, 4, rows, width)
    return pl.pallas_call(
        functools.partial(experts_kernel, ep_size, per_owner),
        out_shape=(
            jax.ShapeDtypeStruct((rows, width), f32),
            jax.ShapeDtypeStruct((rows, width), f32),
            jax.ShapeDtypeStruct((ep_size, 2, 8, 128), f32),
            jax.ShapeDtypeStruct((per_owner, width, units), f32),
            jax.ShapeDtypeStruct((per_owner, width, units), f32),
            jax.ShapeDtypeStruct((hidden, width), f32),
        ),
        in_specs=[anywhere, anywhere, vmem, vmem, vmem, vmem],
        out_specs=(vmem,) * 6,
        scratch_shapes=[
            pltpu.VMEM((2, 4, half, width), bf16),
            pltpu.VMEM((2, 4, half, width), bf16),
            pltpu.VMEM((4 * half, hidden), bf16),
            pltpu.VMEM((4 * half, 2 * hidden), bf16),
            pltpu.VMEM((2 * hidden, width), f32),
            pltpu.VMEM((2, 2, 2, 2, half, width), bf16),
            pltpu.VMEM((steps, 2, 2, 2, half, width), bf16),
            pltpu.VMEM((steps, 2, 2, half, width), bf16),
            pltpu.VMEM((steps, 2, half, width), bf16),
            pltpu.VMEM((steps - 2, 2, half, width), bf16),
            pltpu.VMEM((places, 2, 8, 128), f32),
            pltpu.VMEM((places, 2, 8, 128), f32),
            dma((2, 2)),
            dma((2, 2 * steps)),
            dma((2, 3 * steps)),
            dma((2, steps, 2)),
            dma((2, steps - 2, 2)),
            dma((2, places - 1)),
            dma,
        ],
        compiler_params=pltpu.CompilerParams(
            collective_id=2, has_side_effects=True, vmem_limit_bytes=60 * 1024 * 1024
        ),
        name="experts_by_links",
    )(
        rows_all.reshape(blocks),
        cots_all.reshape(blocks),
        code.reshape(ep_size, 4, rows, -1),
        router,
        enter,
        leave,
    )


class EpSum:
    def __init__(self, me, grads, y_got, z_got, final, sems):
        self.me, self.grads = me, grads
        self.y_got, self.z_got, self.final = y_got, z_got, final
        self.y_sems, self.z_sems, self.fz_sems, self.fy_sems = sems
        self.counts = [g.shape[2] for g in grads]
        self.starts = [sum(self.counts[:i]) for i in range(len(grads))]
        self.finals = []

    def y_copy(self, step, i):
        me = self.me
        return pltpu.make_async_remote_copy(
            src_ref=self.grads[i].at[me.after(step + 1), 1 - me.y],
            dst_ref=self.y_got.at[step, pl.ds(self.starts[i], self.counts[i])],
            send_sem=self.y_sems.at[0, step, i],
            recv_sem=self.y_sems.at[1, step, i],
            device_id=me.y_peer(),
            device_id_type=MESH,
        )

    def z_copy(self, step):
        return pltpu.make_async_remote_copy(
            src_ref=self.y_got.at[step],
            dst_ref=self.z_got.at[step],
            send_sem=self.z_sems.at[0, step],
            recv_sem=self.z_sems.at[1, step],
            device_id=self.me.device(z=self.me.after(step + 1)),
            device_id_type=MESH,
        )

    def begin(self):
        for step in range(self.me.depth):
            for i in range(len(self.grads)):
                self.y_copy(step, i).start()

    def fold(self, step):
        me = self.me
        for i in range(len(self.grads)):
            self.y_copy(step, i).wait_recv()
            add_into(
                self.y_got.at[step, pl.ds(self.starts[i], self.counts[i])],
                self.grads[i].at[me.after(step + 1), me.y],
            )
        if step < me.depth - 1:
            self.z_copy(step).start()

    def settle(self):
        me, depth = self.me, self.me.depth
        for step in range(depth - 1):
            self.z_copy(step).wait_recv()

        def tile(i, carry):
            at = pl.ds(pl.multiple_of(i * 16, 16), 16)
            value = self.y_got[depth - 1, at, :].astype(jnp.float32)
            for step in range(depth - 1):
                value = value + self.z_got[step, at, :].astype(jnp.float32)
            self.final[me.z, me.y, at, :] = value.astype(self.final.dtype)
            return carry

        lax.fori_loop(0, sum(self.counts) // 16, tile, 0)
        mine = self.final.at[me.z, me.y]
        for s in range(1, depth):
            self.spread(mine, self.fz_sems, s, me.device(z=me.after(s)))
        self.spread(mine, self.fy_sems, 0, me.y_peer())

    def spread(self, block, sems, slot, device):
        self.finals.append(send(block, block, sems.at[0, slot], sems.at[1, slot], device))

    def pass_on(self):
        me = self.me
        for s in range(1, me.depth):
            block = self.final.at[me.before(s), me.y]
            pltpu.make_async_copy(block, block, self.fz_sems.at[1, s]).wait()
            self.spread(block, self.fy_sems, s, me.y_peer())

    def finish(self):
        me = self.me
        for s in range(me.depth):
            block = self.final.at[me.before(s), 1 - me.y]
            pltpu.make_async_copy(block, block, self.fy_sems.at[1, s]).wait()

    def sent(self):
        for copy in self.finals:
            copy.wait_send()
        for step in range(self.me.depth):
            for i in range(len(self.grads)):
                self.y_copy(step, i).wait_send()
            if step < self.me.depth - 1:
                self.z_copy(step).wait_send()


def visible_columns(info_cols, info_rows):
    key_seg, key_pos = info_cols[:, 0:1], info_cols[:, 1:2]
    query_seg, query_pos = info_rows[0:1, :], info_rows[1:2, :]
    parent = jnp.where(query_seg >= 5, (query_seg - 5) // 2 + 1, -1)
    above = (key_seg == query_seg) | (key_seg == 0) | (key_seg == parent)
    return above & (key_pos <= query_pos)


def back_kernel(
    ep_size,
    heads,
    last_row,
    datt_own,
    heads_in,
    w_out,
    queries,
    keys,
    values,
    log_sums,
    info_cols,
    info_rows,
    cosine,
    sine,
    rows_in,
    w_query,
    w_key,
    w_value,
    small_in,
    gain,
    inputs,
    middle,
    first_final,
    second_final,
    out_final,
    grad_input,
    small_out,
    datt,
    bias,
    grad_heads,
    grad_proj,
    key_sum,
    value_sum,
    part_query,
    part_key,
    part_value,
    part_out,
    y_got,
    z_got,
    y_got_out,
    z_got_out,
    parts,
    core_got,
    pair_got,
    small_src,
    small_got,
    small_sum,
    own_sem,
    gather_sems,
    y_sems,
    z_sems,
    fz_sems,
    fy_sems,
    y_sems_out,
    z_sems_out,
    fz_sems_out,
    fy_sems_out,
    group_sems,
    small_sems,
    spread_sems,
    own_small_sem,
):
    me = Place(ep_size)
    depth = me.depth
    f32, bf16 = jnp.float32, jnp.bfloat16
    others = all_others(ep_size)
    meet(others)
    my_place = lax.axis_index("ep") * 4 + lax.axis_index("tp")
    tokens, width = rows_in.shape
    share = datt_own.shape[0]
    size = HEAD_DIMENSION
    groups = keys.shape[1] // size
    per_group = heads // groups
    scale = size ** (-0.5)
    tile = 512

    def dot(a, b, contract):
        return lax.dot_general(
            a, b, ((contract[:1], contract[1:]), ((), ())), preferred_element_type=f32
        )

    bias[...] = jnp.where(visible_columns(info_cols[...], info_rows[...]), 0.0, -1e30)
    group_gather_body(me, 4, datt_own, datt, own_sem, gather_sems)
    for n in range(width // tile):
        cols = slice(n * tile, (n + 1) * tile)
        grads = dot(heads_in[...], datt[:, :, :, cols].reshape(tokens, tile), (0, 0))
        part_out[:, :, :, cols] = grads.astype(bf16).reshape(depth, 2, -1, tile)
    out_sum = EpSum(
        me,
        [part_out],
        y_got_out,
        z_got_out,
        out_final,
        (y_sems_out, z_sems_out, fz_sems_out, fy_sems_out),
    )
    out_sum.begin()
    for x in range(2):
        for c in range(2):
            at = pl.ds((x * 2 + c) * share, share)
            grad_heads[at, :] = dot(datt[x, c], w_out[...], (1, 1)).astype(bf16)

    def rotate_back_rows(grads):
        turned = jnp.concatenate([grads[:, size // 2 :], grads[:, : size // 2]], axis=1)
        return (grads * cosine[...] + turned * sine[...]).astype(bf16)

    for head in range(heads):
        group = head // per_group
        mine = slice(head * size, (head + 1) * size)
        shared = slice(group * size, (group + 1) * size)
        query, grad_head = queries[:, mine], grad_heads[:, mine]
        key, value = keys[:, shared], values[:, shared]
        scores = dot(key, query, (1, 1)) * scale + bias[...]
        probs = jnp.exp(scores - log_sums[head : head + 1, :])
        grad_probs = dot(value, grad_head, (1, 1))
        inner = jnp.sum(probs * grad_probs, axis=0, keepdims=True)
        grad_scores = (probs * (grad_probs - inner)).astype(bf16)
        grad_value = dot(probs.astype(bf16), grad_head, (1, 0))
        grad_key = dot(grad_scores, query, (1, 0)) * scale
        if head % per_group:
            grad_value = grad_value + value_sum[...]
            grad_key = grad_key + key_sum[...]
        value_sum[...] = grad_value
        key_sum[...] = grad_key
        grad_query = dot(grad_scores, key, (0, 0)) * scale
        grad_proj[:, mine] = rotate_back_rows(grad_query)
        if head % per_group == per_group - 1:
            at = heads * size + group * size
            grad_proj[:, at : at + size] = rotate_back_rows(grad_key)
            at += groups * size
            grad_proj[:, at : at + size] = grad_value.astype(bf16)
        if 1 <= head <= depth:
            out_sum.fold(head - 1)
    for step in range(max(heads - 1, 0), depth):
        out_sum.fold(step)

    ends = (heads * size, (heads + groups) * size, (heads + 2 * groups) * size)
    wide = width // 2
    sums = []
    for n, final in enumerate((first_final, second_final)):
        cols = slice(n * wide, (n + 1) * wide)
        grads = dot(grad_proj[...], rows_in[:, cols], (0, 0)).astype(bf16)
        part_query[n] = grads[: ends[0]].reshape(depth, 2, -1, wide)
        part_key[n] = grads[ends[0] : ends[1]].reshape(depth, 2, -1, wide)
        part_value[n] = grads[ends[1] :].reshape(depth, 2, -1, wide)
        sums.append(
            EpSum(
                me,
                [part_query.at[n], part_key.at[n], part_value.at[n]],
                y_got.at[n],
                z_got.at[n],
                final,
                (y_sems.at[n], z_sems.at[n], fz_sems.at[n], fy_sems.at[n]),
            )
        )
        sums[n].begin()
        if n == 0:
            out_sum.settle()
    first_sum, second_sum = sums
    small_src[...] = small_in[...]
    for n in range(width // tile):
        cols = slice(n * tile, (n + 1) * tile)
        grads = (
            dot(grad_proj[:, : ends[0]], w_query[:, cols], (1, 0))
            + dot(grad_proj[:, ends[0] : ends[1]], w_key[:, cols], (1, 0))
            + dot(grad_proj[:, ends[1] :], w_value[:, cols], (1, 0))
        )
        parts[:, :, :, cols] = grads.astype(bf16).reshape(2, 2, share, tile)
        gained = jnp.sum(grads * rows_in[:, cols].astype(f32), axis=0, keepdims=True)
        gained = gained / gain[:, cols]
        for k in range(tile // 128):
            row = n * (tile // 128) + k
            small_src[last_row, row : row + 1, :] = gained[:, k * 128 : (k + 1) * 128]
    group = GroupTotal(me, parts, core_got, pair_got, group_sems)
    group.begin()
    small = [
        send(
            small_src.at[device[0] * 4 + device[1]],
            small_got.at[my_place],
            small_sems.at[0, k],
            small_sems.at[1, k],
            device,
        )
        for k, device in enumerate(others)
    ]
    own_small = pltpu.make_async_copy(
        small_src.at[my_place], small_got.at[my_place], own_small_sem
    )
    own_small.start()
    group.exchange()
    first_sum.fold(0)
    out_sum.pass_on()
    for step in range(1, depth):
        first_sum.fold(step)
    second_sum.fold(0)
    own_small.wait()
    for copy in small:
        copy.wait_recv()
    total = small_got[0]
    for k in range(1, 4 * ep_size):
        total = total + small_got[k]
    small_sum[...] = total
    spread = [
        send(
            small_sum,
            small_out.at[my_place],
            spread_sems.at[0, k],
            spread_sems.at[1, k],
            device,
        )
        for k, device in enumerate(others)
    ]
    small_out[my_place] = total

    def last(value, at):
        values_own = inputs[at, :].astype(f32)
        factor = norm_scale(values_own)
        return middle[at, :] + norm_back(values_own, factor, gain[...], value)

    group.finish(grad_input, last)
    second_sum.fold(1)
    first_sum.settle()
    for step in range(2, depth):
        second_sum.fold(step)
    first_sum.pass_on()
    second_sum.settle()
    out_sum.finish()
    second_sum.pass_on()
    first_sum.finish()
    second_sum.finish()
    for copy in spread:
        copy.wait()
    for copy in small:
        copy.wait_send()
    group.sent()
    for each in [out_sum] + sums:
        each.sent()


def back_by_links(
    datt_own,
    heads_in,
    w_out,
    queries,
    keys,
    values,
    log_sums,
    segment,
    position,
    rows_in,
    w_query,
    w_key,
    w_value,
    small,
    gain,
    inputs,
    middle,
    ep_size,
):
    tokens, width = rows_in.shape
    share = datt_own.shape[0]
    depth = ep_size // 2
    heads = queries.shape[1] // HEAD_DIMENSION
    places = 4 * ep_size
    bf16, f32 = jnp.bfloat16, jnp.float32
    dma = pltpu.SemaphoreType.DMA
    vmem = pl.BlockSpec(memory_space=pltpu.VMEM)
    cosine, sine = rope_tables(position, HEAD_DIMENSION)
    cosine = jnp.concatenate([cosine[:, 0], cosine[:, 0]], axis=1)
    sine = jnp.concatenate([sine[:, 0], -sine[:, 0]], axis=1)
    table = jnp.stack([segment, position])
    info_rows = jnp.pad(table, ((0, 6), (0, 0)))
    info_cols = jnp.pad(table.T, ((0, 0), (0, 126)))
    blocks = jnp.pad(small, ((0, places - small.shape[0]), (0, 0))).reshape(places, -1, 128)
    sizes = [w.shape[0] // ep_size for w in (w_query, w_key, w_value, w_out)]
    total = sum(sizes[:3])

    def partial(rows, columns):
        return (depth, 2, rows, columns), bf16

    wide = width // 2
    got = pl.pallas_call(
        functools.partial(back_kernel, ep_size, heads, small.shape[0]),
        out_shape=(
            jax.ShapeDtypeStruct(*partial(total, wide)),
            jax.ShapeDtypeStruct(*partial(total, wide)),
            jax.ShapeDtypeStruct(*partial(sizes[3], width)),
            jax.ShapeDtypeStruct((share, width), f32),
            jax.ShapeDtypeStruct(blocks.shape, f32),
        ),
        in_specs=[vmem] * 19,
        out_specs=(vmem,) * 5,
        scratch_shapes=[
            pltpu.VMEM((2, 2, share, width), bf16),
            pltpu.VMEM((tokens, tokens), f32),
            pltpu.VMEM(queries.shape, bf16),
            pltpu.VMEM((tokens, queries.shape[1] + 2 * keys.shape[1]), bf16),
            pltpu.VMEM((tokens, HEAD_DIMENSION), f32),
            pltpu.VMEM((tokens, HEAD_DIMENSION), f32),
        ]
        + [pltpu.VMEM((2, depth, 2, k, wide), bf16) for k in sizes[:3]]
        + [
            pltpu.VMEM((depth, 2, sizes[3], width), bf16),
            pltpu.VMEM((2, depth, total, wide), bf16),
            pltpu.VMEM((2, depth - 1, total, wide), bf16),
            pltpu.VMEM((depth, sizes[3], width), bf16),
            pltpu.VMEM((depth - 1, sizes[3], width), bf16),
            pltpu.VMEM((2, 2, share, width), bf16),
            pltpu.VMEM((2, share, width), bf16),
            pltpu.VMEM((share, width), bf16),
            pltpu.VMEM(blocks.shape, f32),
            pltpu.VMEM(blocks.shape, f32),
            pltpu.VMEM(blocks.shape[1:], f32),
            dma,
            dma((2, 12)),
        ]
        + [dma((2, 2, depth, 3))]
        + [dma((2, 2, depth))] * 3
        + [dma((2, depth, 1))]
        + [dma((2, depth))] * 3
        + [dma((2, 3)), dma((2, places - 1)), dma((2, places - 1)), dma],
        compiler_params=pltpu.CompilerParams(
            collective_id=5, has_side_effects=True, vmem_limit_bytes=60 * 1024 * 1024
        ),
        name="back_by_links",
    )(
        datt_own,
        heads_in,
        w_out,
        queries,
        keys,
        values,
        log_sums,
        info_cols,
        info_rows,
        cosine,
        sine,
        rows_in,
        w_query,
        w_key,
        w_value,
        blocks,
        gain[None, :],
        inputs,
        middle,
    )
    return got


def deliver_kernel(
    ep_size,
    sizes,
    gate_in,
    up_in,
    down_in,
    rows_in,
    sums_in,
    first,
    second,
    third,
    small,
    gate_out,
    up_out,
    down_out,
    rows_out,
    sums_out,
    query_out,
    key_out,
    value_out,
    out_out,
    router_out,
    first_gain,
    second_gain,
    query,
    key,
    value,
    out,
    sems,
):
    pairs = ((gate_in, gate_out), (up_in, up_out), (down_in, down_out), (rows_in, rows_out))
    pairs += ((sums_in, sums_out),)
    copies = [
        pltpu.make_async_copy(source, target, sems.at[i]) for i, (source, target) in enumerate(pairs)
    ]
    for copy in copies:
        copy.start()
    wide = first.shape[2]
    f32 = jnp.float32

    def leave(source, target, i):
        copies.append(pltpu.make_async_copy(source, target, sems.at[i]))
        copies[-1].start()

    out[...] = third[...].astype(f32)
    leave(out, out_out, 5)
    at = 0
    for i, (source, target) in enumerate(((query, query_out), (key, key_out), (value, value_out))):
        for n, part in enumerate((first, second)):
            source[:, :, n * wide : (n + 1) * wide] = part[:, at : at + sizes[i], :].astype(f32)
        at += sizes[i]
        leave(source, target, 6 + i)
    experts = router_out.shape[0]
    for j in range(small.shape[1]):
        cols = slice(j * 128, (j + 1) * 128)
        router_out[:, cols] = small[:experts, j, :]
        first_gain[:, cols] = small[experts + 1 : experts + 2, j, :]
        second_gain[:, cols] = small[experts : experts + 1, j, :]
    for copy in copies:
        copy.wait()


def deliver(gate, up, down, rows, sums, got, small, sizes, expert_count, ep_size):
    width = rows.shape[1]
    f32 = jnp.float32
    vmem, anywhere = pl.BlockSpec(memory_space=pltpu.VMEM), pl.BlockSpec(memory_space=pl.ANY)
    first, second, third = (g.reshape((ep_size,) + g.shape[2:]) for g in got)

    def like(value):
        return jax.ShapeDtypeStruct(value.shape, value.dtype)

    shapes = [(ep_size, k, width) for k in sizes]
    results = pl.pallas_call(
        functools.partial(deliver_kernel, ep_size, sizes),
        out_shape=(like(gate), like(up), like(down), like(rows), like(sums))
        + tuple(jax.ShapeDtypeStruct(shape, f32) for shape in shapes)
        + (
            jax.ShapeDtypeStruct((expert_count, width), f32),
            jax.ShapeDtypeStruct((1, width), f32),
            jax.ShapeDtypeStruct((1, width), f32),
        ),
        in_specs=[anywhere] * 5 + [vmem] * 4,
        out_specs=(anywhere,) * 9 + (vmem,) * 3,
        scratch_shapes=[pltpu.VMEM(shape, f32) for shape in shapes]
        + [pltpu.SemaphoreType.DMA((9,))],
        compiler_params=pltpu.CompilerParams(vmem_limit_bytes=32 * 1024 * 1024),
        name="deliver",
    )(gate, up, down, rows, sums, first, second, third, small)
    gate, up, down, rows, sums = results[:5]
    query, key, value, out = (g.reshape(-1, width) for g in results[5:9])
    router, first_gain, second_gain = results[9:]
    return (
        sums,
        rows,
        first_gain[0],
        query,
        key,
        value,
        out,
        second_gain[0],
        router,
        gate,
        up,
        down,
    )


def group_rows(value_rows):
    return lax.all_gather(value_rows, "tp", axis=0, tiled=True)


def group_totals(value_rows, by_links, call):
    if by_links:
        return group_total(value_rows, lax.axis_size("ep"), call)
    return lax.psum_scatter(value_rows, "tp", scatter_dimension=0, tiled=True).astype(jnp.float32)


def gather_all(value_rows, by_links):
    if by_links:
        return gather_by_links(value_rows, lax.axis_size("ep"))
    return lax.all_gather(value_rows, ("ep", "tp"), axis=0, tiled=True)


LAST = 1 << 30


def pair_order(expert_ids, slot_order, expert_count):
    experts = jnp.arange(expert_count, dtype=jnp.int32)
    chosen = expert_ids.T[None, :, :] == experts[:, None, None]
    return jnp.min(jnp.where(chosen, slot_order.T[None, :, :], LAST), axis=1)


def kept_pairs(order):
    used = order < LAST
    counts = jnp.sum(used.astype(jnp.int32), axis=2)
    block = jnp.arange(order.shape[0], dtype=jnp.int32)
    earlier = block[None, :] < block[:, None]
    offsets = jnp.sum(jnp.where(earlier[:, :, None], counts[None, :, :], 0), axis=1)
    whole = offsets + counts <= CAP
    edge = (offsets < CAP) & ~whole
    edge_order = jnp.sum(jnp.where(edge[:, :, None], order, 0), axis=0)
    rank = jnp.sum((edge_order[:, :, None] < edge_order[:, None, :]).astype(jnp.int32), axis=1)
    early = offsets[:, :, None] + rank[None, :, :] < CAP
    return used & (whole[:, :, None] | (edge[:, :, None] & early))


def masked_softmax(logits, used):
    top = jnp.max(jnp.where(used, logits, -1e30), axis=-1, keepdims=True)
    powers = jnp.where(used, jnp.exp(logits - top), 0.0)
    return powers / jnp.sum(powers, axis=-1, keepdims=True)


def pair_codes(order_all, per_owner):
    expert_count = order_all.shape[1]
    first = lax.axis_index("ep") * per_owner
    turned = jnp.roll(order_all, -first, axis=1)
    kept = kept_pairs(turned[:, :per_owner])
    dropped = jnp.pad(~kept, ((0, 0), (0, expert_count - per_owner), (0, 0)))
    code = jnp.where(turned < LAST, dropped.astype(jnp.float32), -1.0)
    code = code.swapaxes(1, 2).reshape(-1, expert_count)
    lanes = -expert_count % 128
    return jnp.pad(code, ((0, 0), (0, lanes)), constant_values=-1.0).astype(jnp.bfloat16)


def run_experts(rows_all, cots_all, code, w_router, w_gate, w_up, w_down, by_links):
    per_owner, width, units = w_gate.shape
    expert_count = w_router.shape[0]
    ep_size, tp_size = lax.axis_size("ep"), lax.axis_size("tp")
    hidden = per_owner * units
    router = jnp.roll(w_router, -lax.axis_index("ep") * per_owner, axis=0)
    router = jnp.pad(router, ((0, -expert_count % 128), (0, 0)))
    enter = jnp.concatenate([w[e] for w in (w_gate, w_up) for e in range(per_owner)], axis=1)
    leave = w_down.reshape(hidden, width)
    if by_links:
        grads, sums, small, gate, up, down = experts_by_links(
            rows_all, cots_all, code, router, enter, leave, per_owner, ep_size
        )
        share = grads.shape[0]
        return (
            grads,
            sums,
            small[:, :, :per_owner, : share // 2].swapaxes(1, 2).reshape(expert_count, share).T,
            gate,
            up,
            down.reshape(w_down.shape),
        )
    used, kept = code >= 0, (code == 0).astype(jnp.float32)
    logits = jnp.einsum("rd,ed->re", rows_all, router, preferred_element_type=jnp.float32)
    gates = jnp.repeat((kept * masked_softmax(logits, used))[:, :per_owner], units, axis=1)
    act = jnp.dot(rows_all, enter, preferred_element_type=jnp.float32)
    gate_act, up_act = act[:, :hidden], act[:, hidden:]
    back_act = jnp.einsum("rd,fd->rf", cots_all, leave, preferred_element_type=jnp.float32)
    sigma = jax.nn.sigmoid(gate_act)
    value = gate_act * sigma * up_act
    weighted = (gates * value).astype(jnp.bfloat16)
    grad_hidden = gates * back_act
    turned = jnp.concatenate(
        [
            grad_hidden * up_act * sigma * (1.0 + gate_act * (1.0 - sigma)),
            grad_hidden * gate_act * sigma,
        ],
        axis=1,
    ).astype(jnp.bfloat16)
    small = kept[:, :per_owner] * jnp.sum((value * back_act).reshape(-1, per_owner, units), axis=2)
    grads = jnp.einsum("rf,df->rd", turned, enter, preferred_element_type=jnp.float32)
    sums = jnp.dot(weighted, leave, preferred_element_type=jnp.float32)

    def scatter(value_rows):
        return lax.psum_scatter(value_rows, ("ep", "tp"), scatter_dimension=0, tiled=True)

    columns = lax.dynamic_update_slice_in_dim(
        jnp.zeros((small.shape[0], expert_count), jnp.float32),
        small,
        lax.axis_index("ep") * per_owner,
        1,
    )
    both = jnp.einsum(
        "rd,rwef->wedf",
        rows_all,
        turned.reshape(-1, 2, per_owner, units),
        preferred_element_type=jnp.float32,
    )
    down = jnp.einsum("rf,rd->fd", weighted, cots_all, preferred_element_type=jnp.float32)
    return (
        scatter(grads.astype(jnp.bfloat16)).astype(jnp.float32),
        scatter(sums.astype(jnp.bfloat16)).astype(jnp.float32),
        scatter(columns),
        both[0],
        both[1],
        down.reshape(w_down.shape),
    )


def visible_block(query_seg, query_pos, query_row, key_seg, key_pos, key_row):
    seg_q = query_seg[:, None]
    seg_k = key_seg[None, :]
    above = (
        (seg_k == seg_q)
        | (seg_k == 0)
        | (seg_k >= 1) & (seg_k <= 4) & (seg_q >= 5) & ((seg_q - 5) // 2 + 1 == seg_k)
    )
    same_tree = query_row[:, None] // TREE_TOKENS == key_row[None, :] // TREE_TOKENS
    return above & same_tree & (key_pos[None, :] <= query_pos[:, None])


def block_scores(query_part, key_rows, allowed, scale):
    scores = (
        jnp.einsum("qkgd,pkd->kgqp", query_part, key_rows, preferred_element_type=jnp.float32)
        * scale
    )
    return jnp.where(allowed[None, None], scores, -1e30)


def attend_forward(query_rows, key_rows, value_rows, segment, position):
    total_rows = query_rows.shape[0]
    scale = query_rows.shape[-1] ** (-0.5)
    row_ids = jnp.arange(total_rows, dtype=jnp.int32)
    allowed = visible_block(segment, position, row_ids, segment, position, row_ids)
    scores = block_scores(query_rows, key_rows, allowed, scale)
    top_score = jnp.max(scores, axis=-1, keepdims=True)
    weights = jnp.exp(scores - top_score)
    weight_sum = jnp.sum(weights, axis=-1, keepdims=True)
    probs = (weights / weight_sum).astype(jnp.bfloat16)
    outputs = jnp.einsum(
        "kgqp,pkd->qkgd", probs, value_rows, preferred_element_type=jnp.float32
    ).astype(jnp.bfloat16)
    log_sums = [top_score + jnp.log(weight_sum)]
    return (outputs, log_sums)


def attend_backward(
    query_rows, key_rows, value_rows, segment, position, log_sums, grad_heads, block_rows
):
    total_rows = query_rows.shape[0]
    scale = query_rows.shape[-1] ** (-0.5)
    row_ids = jnp.arange(total_rows, dtype=jnp.int32)
    grad_keys = jnp.zeros(key_rows.shape, jnp.float32)
    grad_values = jnp.zeros(value_rows.shape, jnp.float32)
    grad_query = []
    for number, first_row in enumerate(range(0, total_rows, block_rows)):
        allowed = visible_block(segment, position, row_ids, segment, position, row_ids)
        scores = block_scores(query_rows, key_rows, allowed, scale)
        probs = jnp.where(allowed[None, None], jnp.exp(scores - log_sums[number]), 0.0)
        grad_values = jnp.einsum(
            "kgqp,qkgd->pkd",
            probs.astype(jnp.bfloat16),
            grad_heads,
            preferred_element_type=jnp.float32,
        )
        grad_probs = jnp.einsum(
            "qkgd,pkd->kgqp", grad_heads, value_rows, preferred_element_type=jnp.float32
        )
        inner = jnp.sum(probs * grad_probs, axis=-1, keepdims=True)
        grad_scores = (probs * (grad_probs - inner)).astype(jnp.bfloat16)
        grad_query.append(
            jnp.einsum("kgqp,pkd->qkgd", grad_scores, key_rows, preferred_element_type=jnp.float32)
            * scale
        )
        grad_keys = (
            jnp.einsum(
                "kgqp,qkgd->pkd", grad_scores, query_rows, preferred_element_type=jnp.float32
            )
            * scale
        )
    return (grad_query[0], grad_keys, grad_values)


def local(
    hidden_in,
    gain_attn,
    w_query,
    key_projection_weight,
    value_projection_weight,
    w_out,
    gain_ffn,
    w_router,
    w_gate,
    w_up,
    w_down,
    expert_ids,
    slot_order,
    segment,
    position,
    cotangent,
):
    model_width = w_query.shape[1]
    head_width = HEAD_DIMENSION
    local_heads = w_query.shape[0] // head_width
    local_kv = key_projection_weight.shape[0] // head_width
    group_factor = local_heads // local_kv
    token_count = expert_ids.shape[0]
    share = hidden_in.shape[0]
    row_start = lax.axis_index("tp") * share
    expert_count = w_router.shape[0]
    per_owner = w_gate.shape[0]
    block_rows = 512
    by_links = lax.axis_size("tp") == 4 and lax.axis_size("ep") == 8
    order = pair_order(expert_ids, slot_order, expert_count)
    cot_all = gather_all(cotangent, False)
    inputs_own = hidden_in.astype(jnp.float32)
    gain_one = gain_attn.astype(jnp.float32)
    gain_two = gain_ffn.astype(jnp.float32)
    scale_one = norm_scale(inputs_own)
    first_own = (inputs_own * scale_one * gain_one).astype(jnp.bfloat16)
    if by_links:
        first_normalized, order_all = front_gather(first_own, order, lax.axis_size("ep"))
    else:
        first_normalized = group_rows(first_own)
        order_all = lax.all_gather(order, "ep")
    code = pair_codes(order_all, per_owner)
    cosine_lookup, sine_lookup = rope_tables(position, head_width)
    query_proj = jnp.einsum(
        "rd,fd->rf", first_normalized, w_query, preferred_element_type=jnp.float32
    ).reshape(token_count, local_heads, head_width)
    key_proj = jnp.einsum(
        "rd,fd->rf", first_normalized, key_projection_weight, preferred_element_type=jnp.float32
    ).reshape(token_count, local_kv, head_width)
    query_rows = (
        apply_rotation(query_proj, cosine_lookup, sine_lookup)
        .astype(jnp.bfloat16)
        .reshape(token_count, local_kv, group_factor, head_width)
    )
    key_rows = apply_rotation(key_proj, cosine_lookup, sine_lookup).astype(jnp.bfloat16)
    value_rows = (
        jnp.einsum(
            "rd,fd->rf",
            first_normalized,
            value_projection_weight,
            preferred_element_type=jnp.float32,
        )
        .astype(jnp.bfloat16)
        .reshape(token_count, local_kv, head_width)
    )
    head_outputs, log_sums = attend_forward(query_rows, key_rows, value_rows, segment, position)
    head_outputs = head_outputs.reshape(token_count, local_heads * head_width)
    middle_own = inputs_own + group_totals(
        jnp.dot(head_outputs, w_out, preferred_element_type=jnp.float32).astype(jnp.bfloat16),
        by_links,
        3,
    )
    scale_two = norm_scale(middle_own)
    normed_own = (middle_own * scale_two * gain_two).astype(jnp.bfloat16)
    normed_two = gather_all(normed_own, by_links)
    used = lax.dynamic_slice_in_dim(order, row_start, share, 1).T < LAST
    gates = masked_softmax(
        jnp.einsum("rd,ed->re", normed_own, w_router, preferred_element_type=jnp.float32), used
    )
    grad_normed_own, combined_own, grad_gates_own, grad_w_gate, grad_w_up, grad_w_down = (
        run_experts(normed_two, cot_all, code, w_router, w_gate, w_up, w_down, by_links)
    )
    output_own = (middle_own + combined_own).astype(jnp.bfloat16)
    inner_gate = jnp.sum(gates * grad_gates_own, axis=-1, keepdims=True)
    grad_logits = gates * (grad_gates_own - inner_gate)
    router_f = w_router.astype(jnp.float32)
    grad_normed_own = grad_normed_own + jnp.dot(grad_logits, router_f, precision=EXACT_PRECISION)
    grad_router = jnp.dot(grad_logits.T, normed_own.astype(jnp.float32), precision=EXACT_PRECISION)
    grad_gain_ffn = jnp.sum(grad_normed_own * middle_own * scale_two, axis=0)
    grad_middle = cotangent.astype(jnp.float32) + norm_back(
        middle_own, scale_two, gain_two, grad_normed_own
    )
    if by_links:
        *got, grad_input, small = back_by_links(
            grad_middle.astype(jnp.bfloat16),
            head_outputs,
            w_out,
            query_rows.reshape(token_count, -1),
            key_rows.reshape(token_count, -1),
            value_rows.reshape(token_count, -1),
            jnp.pad(log_sums[0].reshape(local_heads, token_count), ((0, -local_heads % 8), (0, 0))),
            segment,
            position,
            first_normalized,
            w_query,
            key_projection_weight,
            value_projection_weight,
            jnp.concatenate([grad_router, grad_gain_ffn[None, :]], axis=0),
            gain_one,
            hidden_in,
            grad_middle,
            lax.axis_size("ep"),
        )
        ep_size = lax.axis_size("ep")
        weights = (w_query, key_projection_weight, value_projection_weight, w_out)
        return deliver(
            grad_w_gate,
            grad_w_up,
            grad_w_down,
            grad_input,
            output_own,
            got,
            small,
            [w.shape[0] // ep_size for w in weights],
            expert_count,
            ep_size,
        )
    grad_attn = group_rows(grad_middle.astype(jnp.bfloat16))
    grad_w_out = jnp.einsum(
        "rf,rd->fd", head_outputs, grad_attn, preferred_element_type=jnp.float32
    )
    grad_w_out = lax.psum(grad_w_out.astype(jnp.bfloat16), "ep").astype(jnp.float32)
    grad_heads = (
        jnp.einsum("rd,fd->rf", grad_attn, w_out, preferred_element_type=jnp.float32)
        .astype(jnp.bfloat16)
        .reshape(token_count, local_kv, group_factor, head_width)
    )
    grad_query, grad_keys, grad_values = attend_backward(
        query_rows, key_rows, value_rows, segment, position, log_sums, grad_heads, block_rows
    )
    grad_query_proj = (
        rotate_back(
            grad_query.reshape(token_count, local_heads, head_width), cosine_lookup, sine_lookup
        )
        .astype(jnp.bfloat16)
        .reshape(token_count, local_heads * head_width)
    )
    grad_key_proj = (
        rotate_back(grad_keys, cosine_lookup, sine_lookup)
        .astype(jnp.bfloat16)
        .reshape(token_count, local_kv * head_width)
    )
    grad_value_proj = grad_values.astype(jnp.bfloat16).reshape(token_count, local_kv * head_width)
    grad_w_query = jnp.einsum(
        "rf,rd->fd", grad_query_proj, first_normalized, preferred_element_type=jnp.float32
    )
    grad_w_key = jnp.einsum(
        "rf,rd->fd", grad_key_proj, first_normalized, preferred_element_type=jnp.float32
    )
    grad_w_value = jnp.einsum(
        "rf,rd->fd", grad_value_proj, first_normalized, preferred_element_type=jnp.float32
    )
    grad_normed_one = jnp.einsum(
        "rf,fd->rd", grad_query_proj, w_query, preferred_element_type=jnp.float32
    )
    grad_normed_one = grad_normed_one + jnp.einsum(
        "rf,fd->rd", grad_key_proj, key_projection_weight, preferred_element_type=jnp.float32
    )
    grad_normed_one = grad_normed_one + jnp.einsum(
        "rf,fd->rd", grad_value_proj, value_projection_weight, preferred_element_type=jnp.float32
    )
    grad_gain_attn = jnp.sum(grad_normed_one * first_normalized.astype(jnp.float32), axis=0)
    small = jnp.concatenate(
        [grad_router, grad_gain_ffn[None, :], (grad_gain_attn / gain_one)[None, :]], axis=0
    )
    grad_w_query, grad_w_key, grad_w_value = (
        lax.psum(g.astype(jnp.bfloat16), "ep").astype(jnp.float32)
        for g in (grad_w_query, grad_w_key, grad_w_value)
    )
    grad_one_own = group_totals(grad_normed_one.astype(jnp.bfloat16), by_links, None)
    small = lax.psum(small, ("ep", "tp"))
    grad_input = grad_middle + norm_back(inputs_own, scale_one, gain_one, grad_one_own)
    grad_router = small[:expert_count]
    grad_gain_ffn, grad_gain_attn = small[expert_count], small[expert_count + 1]
    return (
        output_own,
        grad_input,
        grad_gain_attn,
        grad_w_query,
        grad_w_key,
        grad_w_value,
        grad_w_out,
        grad_gain_ffn,
        grad_router,
        grad_w_gate,
        grad_w_up,
        grad_w_down,
    )


def solution(mesh):
    placed = (
        P(("ep", "tp"), None),
        P(),
        P("tp", None),
        P("tp", None),
        P("tp", None),
        P("tp", None),
        P(),
        P(),
        P("ep", None, "tp"),
        P("ep", None, "tp"),
        P("ep", "tp", None),
        P("ep", None),
        P("ep", None),
        P("ep"),
        P("ep"),
        P(("ep", "tp"), None),
    )
    return jax.shard_map(
        local,
        mesh=mesh,
        in_specs=placed,
        out_specs=(
            P(("ep", "tp"), None),
            P(("ep", "tp"), None),
            P(),
            P("tp", None),
            P("tp", None),
            P("tp", None),
            P("tp", None),
            P(),
            P(),
            P("ep", None, "tp"),
            P("ep", None, "tp"),
            P("ep", "tp", None),
        ),
        check_vma=False,
    )
```

```python
import functools

import jax
import jax.numpy as jnp
from jax import lax
from jax.experimental import pallas as pl
from jax.experimental.pallas import tpu as pltpu
from jax.sharding import PartitionSpec as P

HEAD_DIMENSION = 64
TREE_TOKENS = 512
CAP = 2304


EPSILON = 1e-06
ROPE_BASE = 10000.0
EXACT_PRECISION = lax.Precision.HIGHEST


def rope_tables(position, head_width):
    half_width = head_width // 2
    freqs = ROPE_BASE ** (-(jnp.arange(half_width, dtype=jnp.float32) * 2.0 / head_width))
    angle = position.astype(jnp.float32)[:, None] * freqs[None, :]
    return (jnp.cos(angle)[:, None, :], jnp.sin(angle)[:, None, :])


def apply_rotation(value_rows, cosine_lookup, sine_lookup):
    half_width = value_rows.shape[-1] // 2
    first = value_rows[..., :half_width]
    second = value_rows[..., half_width:]
    return jnp.concatenate(
        [
            first * cosine_lookup - second * sine_lookup,
            first * sine_lookup + second * cosine_lookup,
        ],
        axis=-1,
    )


def rotate_back(grads, cosine_lookup, sine_lookup):
    half_width = grads.shape[-1] // 2
    first = grads[..., :half_width]
    second = grads[..., half_width:]
    return jnp.concatenate(
        [
            first * cosine_lookup + second * sine_lookup,
            second * cosine_lookup - first * sine_lookup,
        ],
        axis=-1,
    )


def norm_scale(value_rows):
    return lax.rsqrt(jnp.mean(value_rows * value_rows, axis=-1, keepdims=True) + EPSILON)


def norm_back(value_rows, scale, gain, grad_normed):
    weighted = grad_normed * gain
    inner = jnp.mean(value_rows * weighted, axis=-1, keepdims=True)
    grad_values = scale * weighted - value_rows * (scale * scale * scale) * inner
    return grad_values


MESH = pl.DeviceIdType.MESH


class Place:
    def __init__(self, ep_size):
        self.depth = ep_size // 2
        ep, tp = lax.axis_index("ep"), lax.axis_index("tp")
        self.z, self.y = ep // 2, ep % 2
        self.x, self.c = tp // 2, tp % 2

    def device(self, z=None, y=None, x=None, c=None):
        z = self.z if z is None else z
        y = self.y if y is None else y
        x = self.x if x is None else x
        c = self.c if c is None else c
        return (z * 2 + y, x * 2 + c)

    def sibling(self):
        return self.device(c=1 - self.c)

    def x_peer(self):
        return self.device(x=1 - self.x)

    def y_peer(self):
        return self.device(y=1 - self.y)

    def after(self, step):
        return lax.rem(self.z + step, self.depth)

    def before(self, step):
        return lax.rem(self.z + self.depth - step, self.depth)


def meet(devices):
    barrier = pltpu.get_barrier_semaphore()
    for device in devices:
        pl.semaphore_signal(barrier, inc=1, device_id=device, device_id_type=MESH)
    pl.semaphore_wait(barrier, len(devices))


def send(src, dst, send_sem, recv_sem, device):
    copy = pltpu.make_async_remote_copy(
        src_ref=src,
        dst_ref=dst,
        send_sem=send_sem,
        recv_sem=recv_sem,
        device_id=device,
        device_id_type=MESH,
    )
    copy.start()
    return copy


def gather_kernel(ep_size, count, *refs):
    owns, outs = refs[:count], refs[count : 2 * count]
    own_sems, z_sems, y_sems, core_sems = refs[2 * count :]
    me = Place(ep_size)
    depth = me.depth
    meet([me.sibling(), me.y_peer()] + [me.device(z=me.after(s)) for s in range(1, depth)])
    started = []

    def forward(source, target, sems, a, slot, device):
        started.append(send(source, target, sems.at[0, a, slot], sems.at[1, a, slot], device))

    def landed(block, sems, a, slot):
        pltpu.make_async_copy(block, block, sems.at[1, a, slot]).wait()

    local = []
    for a in range(count):
        own, mine = owns[a], outs[a].at[me.z, me.y, me.c]
        for s in range(1, depth):
            forward(own, mine, z_sems, a, s, me.device(z=me.after(s)))
        forward(own, mine, y_sems, a, 0, me.y_peer())
        forward(own, mine, core_sems, a, 0, me.sibling())
        local.append(pltpu.make_async_copy(own, mine, own_sems.at[a]))
        local[a].start()
    for a in range(count):
        for s in range(1, depth):
            block = outs[a].at[me.before(s), me.y, me.c]
            landed(block, z_sems, a, s)
            forward(block, block, y_sems, a, s, me.y_peer())
            forward(block, block, core_sems, a, s, me.sibling())
    for a in range(count):
        for s in range(depth):
            block = outs[a].at[me.before(s), 1 - me.y, me.c]
            landed(block, y_sems, a, s)
            forward(block, block, core_sems, a, depth + s, me.sibling())
    for a in range(count):
        local[a].wait()
        for s in range(depth):
            for y, slot in ((me.y, s), (1 - me.y, depth + s)):
                landed(outs[a].at[me.before(s), y, 1 - me.c], core_sems, a, slot)
    for copy in started:
        copy.wait_send()


def gather_by_links(arrays, ep_size):
    rows, width = arrays[0].shape
    depth, count = ep_size // 2, len(arrays)
    dma = pltpu.SemaphoreType.DMA
    anywhere = pl.BlockSpec(memory_space=pltpu.HBM)
    return pl.pallas_call(
        functools.partial(gather_kernel, ep_size, count),
        out_shape=tuple(
            jax.ShapeDtypeStruct((depth, 2, 2, rows, width), a.dtype) for a in arrays
        ),
        in_specs=[anywhere] * count,
        out_specs=(anywhere,) * count,
        scratch_shapes=[
            dma((count,)),
            dma((2, count, depth)),
            dma((2, count, depth)),
            dma((2, count, 2 * depth)),
        ],
        compiler_params=pltpu.CompilerParams(collective_id=1, has_side_effects=True),
        name="gather_by_links",
    )(*arrays)


def add_into(target, other):
    def tile(i, carry):
        at = pl.ds(pl.multiple_of(i * 16, 16), 16)
        target[at, :] = target[at, :] + other[at, :]
        return carry

    lax.fori_loop(0, target.shape[0] // 16, tile, 0)


def front_gather_kernel(
    ep_size, pieces, own, table, out, tables, own_sem, sems, table_own_sem, table_sems
):
    me = Place(ep_size)
    mine = lax.axis_index("ep")
    tp = lax.axis_index("tp")
    peers = [(lax.rem(mine + k, ep_size), tp) for k in range(1, ep_size)]
    meet([me.sibling(), me.x_peer()] + peers)
    local = pltpu.make_async_copy(table, tables.at[mine], table_own_sem)
    local.start()
    copies = [
        send(table, tables.at[mine], table_sems.at[0, k], table_sems.at[1, k], device)
        for k, device in enumerate(peers)
    ]
    group_gather_body(me, pieces, own, out, own_sem, sems)
    local.wait()
    for copy in copies:
        copy.wait()


def front_gather(value_rows, table, ep_size):
    rows, width = value_rows.shape
    pieces = 4
    dma = pltpu.SemaphoreType.DMA
    anywhere = pl.BlockSpec(memory_space=pltpu.HBM)
    every, tables = pl.pallas_call(
        functools.partial(front_gather_kernel, ep_size, pieces),
        out_shape=(
            jax.ShapeDtypeStruct((2, 2, rows, width), value_rows.dtype),
            jax.ShapeDtypeStruct((ep_size,) + table.shape, table.dtype),
        ),
        in_specs=[anywhere] * 2,
        out_specs=(anywhere,) * 2,
        scratch_shapes=[dma, dma((2, 3 * pieces)), dma, dma((2, ep_size - 1))],
        compiler_params=pltpu.CompilerParams(collective_id=6, has_side_effects=True),
        name="front_gather",
    )(value_rows, table)
    return every.reshape(-1, width), tables


def group_gather_body(me, pieces, own, out, own_sem, sems):
    size = own.shape[0] // pieces
    started = []
    local = pltpu.make_async_copy(own, out.at[me.x, me.c], own_sem)
    local.start()

    def at(p):
        return pl.ds(p * size, size)

    def go(kind, p, src, dst, device):
        slot = kind * pieces + p
        started.append(send(src, dst, sems.at[0, slot], sems.at[1, slot], device))

    for p in range(pieces):
        go(0, p, own.at[at(p)], out.at[me.x, me.c, at(p)], me.x_peer())
    for p in range(pieces):
        go(1, p, own.at[at(p)], out.at[me.x, me.c, at(p)], me.sibling())
    for p in range(pieces):
        block = out.at[1 - me.x, me.c, at(p)]
        pltpu.make_async_copy(block, block, sems.at[1, p]).wait()
        go(2, p, block, block, me.sibling())
    for p in range(pieces):
        for kind, x in ((1, me.x), (2, 1 - me.x)):
            block = out.at[x, 1 - me.c, at(p)]
            pltpu.make_async_copy(block, block, sems.at[1, kind * pieces + p]).wait()
    local.wait()
    for copy in started:
        copy.wait_send()


class GroupTotal:
    def __init__(self, me, parts, core_got, pair_got, sems):
        self.me, self.parts, self.core_got, self.pair_got = me, parts, core_got, pair_got
        self.core = [
            pltpu.make_async_remote_copy(
                src_ref=parts.at[x, 1 - me.c],
                dst_ref=core_got.at[x],
                send_sem=sems.at[0, k],
                recv_sem=sems.at[1, k],
                device_id=me.sibling(),
                device_id_type=MESH,
            )
            for k, x in enumerate((1 - me.x, me.x))
        ]
        self.pair = pltpu.make_async_remote_copy(
            src_ref=core_got.at[1 - me.x],
            dst_ref=pair_got,
            send_sem=sems.at[0, 2],
            recv_sem=sems.at[1, 2],
            device_id=me.x_peer(),
            device_id_type=MESH,
        )

    def begin(self):
        for copy in self.core:
            copy.start()

    def exchange(self):
        self.core[0].wait_recv()
        far = 1 - self.me.x
        add_into(self.core_got.at[far], self.parts.at[far, self.me.c])
        self.pair.start()

    def finish(self, out, change=lambda value, at: value):
        self.core[1].wait_recv()
        self.pair.wait_recv()

        def tile(i, carry):
            at = pl.ds(pl.multiple_of(i * 16, 16), 16)
            value = (
                self.parts[self.me.x, self.me.c, at, :].astype(jnp.float32)
                + self.core_got[self.me.x, at, :].astype(jnp.float32)
                + self.pair_got[at, :].astype(jnp.float32)
            )
            out[at, :] = change(value, at)
            return carry

        lax.fori_loop(0, out.shape[0] // 16, tile, 0)

    def sent(self):
        for copy in self.core + [self.pair]:
            copy.wait_send()


def group_total_kernel(ep_size, parts, out, core_got, pair_got, sems):
    me = Place(ep_size)
    meet([me.sibling(), me.x_peer()])
    total = GroupTotal(me, parts, core_got, pair_got, sems)
    total.begin()
    total.exchange()
    total.finish(out)
    total.sent()


def group_total(value_rows, ep_size, call):
    rows, width = value_rows.shape[0] // 4, value_rows.shape[1]
    vmem = pl.BlockSpec(memory_space=pltpu.VMEM)
    return pl.pallas_call(
        functools.partial(group_total_kernel, ep_size),
        out_shape=jax.ShapeDtypeStruct((rows, width), jnp.float32),
        in_specs=[vmem],
        out_specs=vmem,
        scratch_shapes=[
            pltpu.VMEM((2, rows, width), jnp.bfloat16),
            pltpu.VMEM((rows, width), jnp.bfloat16),
            pltpu.SemaphoreType.DMA((2, 3)),
        ],
        compiler_params=pltpu.CompilerParams(
            collective_id=call, has_side_effects=True, vmem_limit_bytes=32 * 1024 * 1024
        ),
        name="group_total",
    )(value_rows.reshape(2, 2, rows, width))


def all_others(ep_size):
    ep, tp = lax.axis_index("ep"), lax.axis_index("tp")
    return [
        (lax.rem(ep + k // 4, ep_size), lax.rem(tp + k % 4, 4)) for k in range(1, ep_size * 4)
    ]


def experts_kernel(
    ep_size,
    per_owner,
    rows_in,
    cots_in,
    code_in,
    router,
    enter_own,
    enter_peer,
    leave_own,
    leave_peer,
    grad_out,
    sum_out,
    small_out,
    gate_out,
    up_out,
    down_out,
    gate_peer,
    up_peer,
    down_peer,
    rows_buf,
    cots_buf,
    weighted,
    turned,
    enter_sum,
    down_sum,
    parts,
    core_got,
    y_got,
    z_got,
    small_in,
    small_got,
    load_sems,
    core_sems,
    y_sems,
    z_sems,
    small_sems,
    own_sem,
):
    me = Place(ep_size)
    depth = me.depth
    blocks = 2 * depth
    width = router.shape[1]
    share = rows_buf.shape[2]
    tokens = 2 * share
    hidden = leave_own.shape[0]
    units = hidden // per_owner
    f32, bf16 = jnp.float32, jnp.bfloat16
    ep = lax.axis_index("ep")
    others = [
        (lax.rem(ep + k // 2, ep_size), me.x * 2 + lax.rem(me.c + k % 2, 2))
        for k in range(1, 2 * ep_size)
    ]
    meet(others)
    my_place = ep * 2 + me.c
    halves = ((enter_own, leave_own), (enter_peer, leave_peer))

    def where(b):
        return me.after(b // 2 + 1), lax.rem(1 - me.y + b % 2, 2)

    def load(b, which):
        z, y = where(b)
        source, target = ((rows_in, rows_buf), (cots_in, cots_buf))[which]
        slot = lax.rem(b, 2)
        return pltpu.make_async_copy(
            source.at[z, y], target.at[slot], load_sems.at[slot, which]
        )

    def core_copy(b):
        return pltpu.make_async_remote_copy(
            src_ref=parts.at[lax.rem(b, 2), :, 1 - me.c],
            dst_ref=core_got.at[b // 2, where(b)[1]],
            send_sem=core_sems.at[0, b],
            recv_sem=core_sems.at[1, b],
            device_id=me.sibling(),
            device_id_type=MESH,
        )

    def y_copy(step, which):
        return pltpu.make_async_remote_copy(
            src_ref=core_got.at[step, 1 - me.y, which],
            dst_ref=y_got.at[step, which],
            send_sem=y_sems.at[0, step, which],
            recv_sem=y_sems.at[1, step, which],
            device_id=me.y_peer(),
            device_id_type=MESH,
        )

    def z_copy(step, which):
        return pltpu.make_async_remote_copy(
            src_ref=y_got.at[step, which],
            dst_ref=z_got.at[step, which],
            send_sem=z_sems.at[0, step, which],
            recv_sem=z_sems.at[1, step, which],
            device_id=me.device(z=me.after(step + 1)),
            device_id_type=MESH,
        )

    def small_copy(k, device):
        return pltpu.make_async_remote_copy(
            src_ref=small_in.at[device[0] * 2 + device[1] % 2],
            dst_ref=small_got.at[my_place],
            send_sem=small_sems.at[0, k],
            recv_sem=small_sems.at[1, k],
            device_id=device,
            device_id_type=MESH,
        )

    def dot(a, b, contract):
        return lax.dot_general(
            a, b, ((contract[:1], contract[1:]), ((), ())), preferred_element_type=f32
        )

    def spread(columns):
        return jnp.concatenate(
            [jnp.broadcast_to(columns[:, e : e + 1], (tokens, units)) for e in range(per_owner)],
            axis=1,
        )

    def compute(b):
        z, y = where(b)
        slot = lax.rem(b, 2)
        rows = rows_buf[slot].reshape(tokens, width)
        cots = cots_buf[slot].reshape(tokens, width)
        code = code_in[z * 2 + y, me.x].astype(f32).reshape(tokens, -1)
        used = code >= 0.0
        logits = jnp.where(used, dot(rows, router[...], (1, 1)), -1e30)
        top = jnp.max(logits, axis=1, keepdims=True)
        powers = jnp.where(used, jnp.exp(logits - top), 0.0)
        kept = jnp.where(code == 0.0, 1.0, 0.0)
        gates = spread(kept * powers / jnp.sum(powers, axis=1, keepdims=True))
        products = jnp.zeros((tokens, hidden), f32)
        for h, (enter, leave) in enumerate(halves):
            act = dot(rows, enter[...], (1, 0))
            gate_act, up_act = act[:, :hidden], act[:, hidden:]
            back_act = dot(cots, leave[...], (1, 1))
            sigma = jax.nn.sigmoid(gate_act)
            swish = gate_act * sigma
            value = swish * up_act
            products = products + value * back_act
            weighted[:, h * hidden : (h + 1) * hidden] = (gates * value).astype(bf16)
            grad_hidden = gates * back_act
            at = 2 * h * hidden
            turned[:, at : at + hidden] = (
                grad_hidden * up_act * sigma * (1.0 + gate_act * (1.0 - sigma))
            ).astype(bf16)
            turned[:, at + hidden : at + 2 * hidden] = (grad_hidden * swish).astype(bf16)
        lane = lax.broadcasted_iota(jnp.int32, (8, hidden), 1)
        pick = lax.broadcasted_iota(jnp.int32, (8, hidden), 0)
        mine = jnp.where((lane >= pick * units) & (lane < (pick + 1) * units), 1.0, 0.0)
        grad_gates = lax.dot_general(
            mine,
            spread(kept) * products,
            (((1,), (1,)), ((), ())),
            precision=EXACT_PRECISION,
            preferred_element_type=f32,
        )
        for k in range(2):
            small_in[(z * 2 + y) * 2 + k] = grad_gates[:, k * share : (k + 1) * share]
        tile = 512
        for n in range(width // tile):
            cols = slice(n * tile, (n + 1) * tile)
            grads = (
                dot(turned[:, : 2 * hidden], enter_own[cols, :], (1, 1))
                + dot(turned[:, 2 * hidden :], enter_peer[cols, :], (1, 1))
            ).astype(bf16)
            sums = (
                dot(weighted[:, :hidden], leave_own[:, cols], (1, 0))
                + dot(weighted[:, hidden:], leave_peer[:, cols], (1, 0))
            ).astype(bf16)
            for c in range(2):
                at = slice(c * share, (c + 1) * share)
                parts[slot, 0, c, :, cols] = grads[at]
                parts[slot, 1, c, :, cols] = sums[at]

    def weight_sums(b):
        slot = lax.rem(b, 2)
        tile = 512
        for n in range(width // tile):
            cols = slice(n * tile, (n + 1) * tile)
            rows = rows_buf[slot, :, :, cols].reshape(tokens, tile)
            cots = cots_buf[slot, :, :, cols].reshape(tokens, tile)
            enter_sum[:, cols] += dot(turned[...], rows, (0, 0))
            down_sum[:, cols] += dot(weighted[...], cots, (0, 0))

    enter_sum[...] = jnp.zeros_like(enter_sum)
    down_sum[...] = jnp.zeros_like(down_sum)
    for which in range(2):
        load(0, which).start()

    def during(i, lag, body, even=False):
        b = i - lag
        inside = (b >= 0) & (b < blocks)
        if even:
            inside &= b % 2 == 0
        pl.when(inside)(lambda: body(b))

    def work(b):
        for which in range(2):
            load(b, which).wait()

        @pl.when(b + 1 < blocks)
        def _():
            for which in range(2):
                load(b + 1, which).start()

        compute(b)
        core_copy(b).start()
        weight_sums(b)

    def core_sum(b):
        step, y = b // 2, where(b)[1]
        core_copy(b).wait_recv()
        for which in range(2):
            add_into(core_got.at[step, y, which], parts.at[lax.rem(b, 2), which, me.c])

        @pl.when(b % 2 == 0)
        def _():
            for which in range(2):
                y_copy(step, which).start()

        core_copy(b).wait_send()

    def y_sum(which):
        def body(b):
            step = b // 2
            y_copy(step, which).wait_recv()
            add_into(y_got.at[step, which], core_got.at[step, me.y, which])

            @pl.when(step < depth - 1)
            def _():
                z_copy(step, which).start()

        return body

    def small_send(b):
        for k, device in enumerate(others):
            small_copy(k, device).start()
        pltpu.make_async_copy(small_in.at[my_place], small_got.at[my_place], own_sem).start()
        for e in range(per_owner):
            own, peer = e * units, 2 * hidden + e * units
            gate_out[e] = enter_sum[own : own + units, :].T
            up_out[e] = enter_sum[hidden + own : hidden + own + units, :].T
            gate_peer[e] = enter_sum[peer : peer + units, :].T.astype(bf16)
            up_peer[e] = enter_sum[hidden + peer : hidden + peer + units, :].T.astype(bf16)
        down_out[...] = down_sum[:hidden, :]
        down_peer[...] = down_sum[hidden:, :].astype(bf16)

    def turn(i, carry):
        during(i, 0, work)
        during(i, 1, core_sum)
        during(i, 2, y_sum(0), True)
        during(i, 3, y_sum(1), True)
        pl.when(i == blocks)(lambda: small_send(i))
        return carry

    lax.fori_loop(0, blocks + 2, turn, 0)
    pltpu.make_async_copy(small_in.at[my_place], small_got.at[my_place], own_sem).wait()
    for k, device in enumerate(others):
        small_copy(k, device).wait()
    for k in range(ep_size):
        small_out[k] = small_got[2 * k] + small_got[2 * k + 1]
    for step in range(depth - 1):
        for which in range(2):
            z_copy(step, which).wait_recv()

    def finish(which, target):
        def tile(i, carry):
            at = pl.ds(pl.multiple_of(i * 16, 16), 16)
            total = y_got[depth - 1, which, at, :].astype(f32)
            for step in range(depth - 1):
                total = total + z_got[step, which, at, :].astype(f32)
            target[at, :] = total
            return carry

        lax.fori_loop(0, share // 16, tile, 0)

    finish(0, grad_out)
    finish(1, sum_out)
    for step in range(depth):
        for which in range(2):
            y_copy(step, which).wait_send()
            if step < depth - 1:
                z_copy(step, which).wait_send()


def experts_by_links(rows_all, cots_all, code, router, weights, per_owner, ep_size):
    depth, _, _, rows, width = rows_all.shape
    hidden = weights[2].shape[0]
    units = hidden // per_owner
    bf16, f32 = jnp.bfloat16, jnp.float32
    dma = pltpu.SemaphoreType.DMA
    vmem = pl.BlockSpec(memory_space=pltpu.VMEM)
    anywhere = pl.BlockSpec(memory_space=pltpu.HBM)
    places = 2 * ep_size
    return pl.pallas_call(
        functools.partial(experts_kernel, ep_size, per_owner),
        out_shape=(
            jax.ShapeDtypeStruct((rows, width), f32),
            jax.ShapeDtypeStruct((rows, width), f32),
            jax.ShapeDtypeStruct((ep_size, 8, rows), f32),
            jax.ShapeDtypeStruct((per_owner, width, units), f32),
            jax.ShapeDtypeStruct((per_owner, width, units), f32),
            jax.ShapeDtypeStruct((hidden, width), f32),
            jax.ShapeDtypeStruct((per_owner, width, units), bf16),
            jax.ShapeDtypeStruct((per_owner, width, units), bf16),
            jax.ShapeDtypeStruct((hidden, width), bf16),
        ),
        in_specs=[anywhere, anywhere] + [vmem] * 6,
        out_specs=(vmem,) * 9,
        scratch_shapes=[
            pltpu.VMEM((2, 2, rows, width), bf16),
            pltpu.VMEM((2, 2, rows, width), bf16),
            pltpu.VMEM((2 * rows, 2 * hidden), bf16),
            pltpu.VMEM((2 * rows, 4 * hidden), bf16),
            pltpu.VMEM((4 * hidden, width), f32),
            pltpu.VMEM((2 * hidden, width), f32),
            pltpu.VMEM((2, 2, 2, rows, width), bf16),
            pltpu.VMEM((depth, 2, 2, rows, width), bf16),
            pltpu.VMEM((depth, 2, rows, width), bf16),
            pltpu.VMEM((depth - 1, 2, rows, width), bf16),
            pltpu.VMEM((places, 8, rows), f32),
            pltpu.VMEM((places, 8, rows), f32),
            dma((2, 2)),
            dma((2, 2 * depth)),
            dma((2, depth, 2)),
            dma((2, depth - 1, 2)),
            dma((2, places - 1)),
            dma,
        ],
        compiler_params=pltpu.CompilerParams(
            collective_id=2, has_side_effects=True, vmem_limit_bytes=60 * 1024 * 1024
        ),
        name="experts_by_links",
    )(rows_all, cots_all, code.reshape(ep_size, 2, 2, rows, -1), router, *weights)


class EpSum:
    def __init__(self, me, grads, y_got, z_got, final, sems):
        self.me, self.grads = me, grads
        self.y_got, self.z_got, self.final = y_got, z_got, final
        self.y_sems, self.z_sems, self.fz_sems, self.fy_sems = sems
        self.counts = [g.shape[2] for g in grads]
        self.starts = [sum(self.counts[:i]) for i in range(len(grads))]
        self.finals = []

    def y_copy(self, step, i):
        me = self.me
        return pltpu.make_async_remote_copy(
            src_ref=self.grads[i].at[me.after(step + 1), 1 - me.y],
            dst_ref=self.y_got.at[step, pl.ds(self.starts[i], self.counts[i])],
            send_sem=self.y_sems.at[0, step, i],
            recv_sem=self.y_sems.at[1, step, i],
            device_id=me.y_peer(),
            device_id_type=MESH,
        )

    def z_copy(self, step):
        return pltpu.make_async_remote_copy(
            src_ref=self.y_got.at[step],
            dst_ref=self.z_got.at[step],
            send_sem=self.z_sems.at[0, step],
            recv_sem=self.z_sems.at[1, step],
            device_id=self.me.device(z=self.me.after(step + 1)),
            device_id_type=MESH,
        )

    def begin(self):
        for step in range(self.me.depth):
            for i in range(len(self.grads)):
                self.y_copy(step, i).start()

    def fold(self, step):
        me = self.me
        for i in range(len(self.grads)):
            self.y_copy(step, i).wait_recv()
            add_into(
                self.y_got.at[step, pl.ds(self.starts[i], self.counts[i])],
                self.grads[i].at[me.after(step + 1), me.y],
            )
        if step < me.depth - 1:
            self.z_copy(step).start()

    def settle(self):
        me, depth = self.me, self.me.depth
        for step in range(depth - 1):
            self.z_copy(step).wait_recv()

        def tile(i, carry):
            at = pl.ds(pl.multiple_of(i * 16, 16), 16)
            value = self.y_got[depth - 1, at, :].astype(jnp.float32)
            for step in range(depth - 1):
                value = value + self.z_got[step, at, :].astype(jnp.float32)
            self.final[me.z, me.y, at, :] = value.astype(self.final.dtype)
            return carry

        lax.fori_loop(0, sum(self.counts) // 16, tile, 0)
        mine = self.final.at[me.z, me.y]
        for s in range(1, depth):
            self.spread(mine, self.fz_sems, s, me.device(z=me.after(s)))
        self.spread(mine, self.fy_sems, 0, me.y_peer())

    def spread(self, block, sems, slot, device):
        self.finals.append(send(block, block, sems.at[0, slot], sems.at[1, slot], device))

    def pass_on(self):
        me = self.me
        for s in range(1, me.depth):
            block = self.final.at[me.before(s), me.y]
            pltpu.make_async_copy(block, block, self.fz_sems.at[1, s]).wait()
            self.spread(block, self.fy_sems, s, me.y_peer())

    def finish(self):
        me = self.me
        for s in range(me.depth):
            block = self.final.at[me.before(s), 1 - me.y]
            pltpu.make_async_copy(block, block, self.fy_sems.at[1, s]).wait()

    def sent(self):
        for copy in self.finals:
            copy.wait_send()
        for step in range(self.me.depth):
            for i in range(len(self.grads)):
                self.y_copy(step, i).wait_send()
            if step < self.me.depth - 1:
                self.z_copy(step).wait_send()


def visible_columns(info_cols, info_rows):
    key_seg, key_pos = info_cols[:, 0:1], info_cols[:, 1:2]
    query_seg, query_pos = info_rows[0:1, :], info_rows[1:2, :]
    parent = jnp.where(query_seg >= 5, (query_seg - 5) // 2 + 1, -1)
    above = (key_seg == query_seg) | (key_seg == 0) | (key_seg == parent)
    return above & (key_pos <= query_pos)


def back_kernel(
    ep_size,
    heads,
    last_row,
    datt_own,
    heads_in,
    w_out,
    queries,
    keys,
    values,
    log_sums,
    info_cols,
    info_rows,
    cosine,
    sine,
    rows_in,
    w_query,
    w_key,
    w_value,
    small_in,
    gain,
    inputs,
    middle,
    gate_peer,
    up_peer,
    down_peer,
    first_final,
    second_final,
    out_final,
    grad_input,
    small_out,
    gate_got,
    up_got,
    down_got,
    datt,
    bias,
    grad_heads,
    grad_proj,
    key_sum,
    value_sum,
    part_query,
    part_key,
    part_value,
    part_out,
    y_got,
    z_got,
    y_got_out,
    z_got_out,
    parts,
    core_got,
    pair_got,
    small_src,
    small_got,
    small_sum,
    own_sem,
    gather_sems,
    y_sems,
    z_sems,
    fz_sems,
    fy_sems,
    y_sems_out,
    z_sems_out,
    fz_sems_out,
    fy_sems_out,
    group_sems,
    small_sems,
    spread_sems,
    own_small_sem,
    peer_sems,
):
    me = Place(ep_size)
    depth = me.depth
    f32, bf16 = jnp.float32, jnp.bfloat16
    others = all_others(ep_size)
    meet(others)
    my_place = lax.axis_index("ep") * 4 + lax.axis_index("tp")
    tokens, width = rows_in.shape
    share = datt_own.shape[0]
    size = HEAD_DIMENSION
    groups = keys.shape[1] // size
    per_group = heads // groups
    scale = size ** (-0.5)
    tile = 512

    def dot(a, b, contract):
        return lax.dot_general(
            a, b, ((contract[:1], contract[1:]), ((), ())), preferred_element_type=f32
        )

    bias[...] = jnp.where(visible_columns(info_cols[...], info_rows[...]), 0.0, -1e30)
    group_gather_body(me, 4, datt_own, datt, own_sem, gather_sems)

    def to_peer(i):
        source, target = ((gate_peer, gate_got), (up_peer, up_got), (down_peer, down_got))[i]
        return send(source, target, peer_sems.at[0, i], peer_sems.at[1, i], me.x_peer())

    exchanged = [to_peer(0)]
    for n in range(width // tile):
        cols = slice(n * tile, (n + 1) * tile)
        grads = dot(heads_in[...], datt[:, :, :, cols].reshape(tokens, tile), (0, 0))
        part_out[:, :, :, cols] = grads.astype(bf16).reshape(depth, 2, -1, tile)
    out_sum = EpSum(
        me,
        [part_out],
        y_got_out,
        z_got_out,
        out_final,
        (y_sems_out, z_sems_out, fz_sems_out, fy_sems_out),
    )
    out_sum.begin()
    for x in range(2):
        for c in range(2):
            at = pl.ds((x * 2 + c) * share, share)
            grad_heads[at, :] = dot(datt[x, c], w_out[...], (1, 1)).astype(bf16)

    def rotate_back_rows(grads):
        turned = jnp.concatenate([grads[:, size // 2 :], grads[:, : size // 2]], axis=1)
        return (grads * cosine[...] + turned * sine[...]).astype(bf16)

    for head in range(heads):
        group = head // per_group
        mine = slice(head * size, (head + 1) * size)
        shared = slice(group * size, (group + 1) * size)
        query, grad_head = queries[:, mine], grad_heads[:, mine]
        key, value = keys[:, shared], values[:, shared]
        scores = dot(key, query, (1, 1)) * scale + bias[...]
        probs = jnp.exp(scores - log_sums[head : head + 1, :])
        grad_probs = dot(value, grad_head, (1, 1))
        inner = jnp.sum(probs * grad_probs, axis=0, keepdims=True)
        grad_scores = (probs * (grad_probs - inner)).astype(bf16)
        grad_value = dot(probs.astype(bf16), grad_head, (1, 0))
        grad_key = dot(grad_scores, query, (1, 0)) * scale
        if head % per_group:
            grad_value = grad_value + value_sum[...]
            grad_key = grad_key + key_sum[...]
        value_sum[...] = grad_value
        key_sum[...] = grad_key
        grad_query = dot(grad_scores, key, (0, 0)) * scale
        grad_proj[:, mine] = rotate_back_rows(grad_query)
        if head % per_group == per_group - 1:
            at = heads * size + group * size
            grad_proj[:, at : at + size] = rotate_back_rows(grad_key)
            at += groups * size
            grad_proj[:, at : at + size] = grad_value.astype(bf16)
        if 1 <= head <= depth:
            out_sum.fold(head - 1)
    for step in range(max(heads - 1, 0), depth):
        out_sum.fold(step)

    ends = (heads * size, (heads + groups) * size, (heads + 2 * groups) * size)
    wide = width // 2
    sums = []
    for n, final in enumerate((first_final, second_final)):
        cols = slice(n * wide, (n + 1) * wide)
        grads = dot(grad_proj[...], rows_in[:, cols], (0, 0)).astype(bf16)
        part_query[n] = grads[: ends[0]].reshape(depth, 2, -1, wide)
        part_key[n] = grads[ends[0] : ends[1]].reshape(depth, 2, -1, wide)
        part_value[n] = grads[ends[1] :].reshape(depth, 2, -1, wide)
        sums.append(
            EpSum(
                me,
                [part_query.at[n], part_key.at[n], part_value.at[n]],
                y_got.at[n],
                z_got.at[n],
                final,
                (y_sems.at[n], z_sems.at[n], fz_sems.at[n], fy_sems.at[n]),
            )
        )
        sums[n].begin()
        if n == 0:
            out_sum.settle()
    first_sum, second_sum = sums
    small_src[...] = small_in[...]
    for n in range(width // tile):
        cols = slice(n * tile, (n + 1) * tile)
        grads = (
            dot(grad_proj[:, : ends[0]], w_query[:, cols], (1, 0))
            + dot(grad_proj[:, ends[0] : ends[1]], w_key[:, cols], (1, 0))
            + dot(grad_proj[:, ends[1] :], w_value[:, cols], (1, 0))
        )
        parts[:, :, :, cols] = grads.astype(bf16).reshape(2, 2, share, tile)
        gained = jnp.sum(grads * rows_in[:, cols].astype(f32), axis=0, keepdims=True)
        gained = gained / gain[:, cols]
        for k in range(tile // 128):
            row = n * (tile // 128) + k
            small_src[last_row, row : row + 1, :] = gained[:, k * 128 : (k + 1) * 128]
        first_sum.fold(n)
    for step in range(width // tile, depth):
        first_sum.fold(step)
    group = GroupTotal(me, parts, core_got, pair_got, group_sems)
    group.begin()
    second_sum.fold(0)
    group.exchange()
    exchanged += [to_peer(1), to_peer(2)]
    out_sum.pass_on()
    second_sum.fold(1)
    small = [
        send(
            small_src.at[device[0] * 4 + device[1]],
            small_got.at[my_place],
            small_sems.at[0, k],
            small_sems.at[1, k],
            device,
        )
        for k, device in enumerate(others)
    ]
    own_small = pltpu.make_async_copy(
        small_src.at[my_place], small_got.at[my_place], own_small_sem
    )
    own_small.start()
    for step in range(2, depth):
        second_sum.fold(step)
    first_sum.settle()

    def last(value, at):
        values_own = inputs[at, :].astype(f32)
        factor = norm_scale(values_own)
        return middle[at, :] + norm_back(values_own, factor, gain[...], value)

    group.finish(grad_input, last)
    second_sum.settle()
    own_small.wait()
    for copy in small:
        copy.wait_recv()
    total = small_got[0]
    for k in range(1, 4 * ep_size):
        total = total + small_got[k]
    small_sum[...] = total
    spread = [
        send(
            small_sum,
            small_out.at[my_place],
            spread_sems.at[0, k],
            spread_sems.at[1, k],
            device,
        )
        for k, device in enumerate(others)
    ]
    small_out[my_place] = total
    first_sum.pass_on()
    out_sum.finish()
    second_sum.pass_on()
    first_sum.finish()
    second_sum.finish()
    for copy in spread:
        copy.wait()
    for copy in small:
        copy.wait_send()
    group.sent()
    for each in [out_sum] + sums:
        each.sent()
    for copy in exchanged:
        copy.wait()


def back_by_links(
    datt_own,
    heads_in,
    w_out,
    queries,
    keys,
    values,
    log_sums,
    segment,
    position,
    rows_in,
    w_query,
    w_key,
    w_value,
    small,
    gain,
    inputs,
    middle,
    peers,
    ep_size,
):
    tokens, width = rows_in.shape
    share = datt_own.shape[0]
    depth = ep_size // 2
    heads = queries.shape[1] // HEAD_DIMENSION
    places = 4 * ep_size
    bf16, f32 = jnp.bfloat16, jnp.float32
    dma = pltpu.SemaphoreType.DMA
    vmem = pl.BlockSpec(memory_space=pltpu.VMEM)
    anywhere = pl.BlockSpec(memory_space=pltpu.HBM)
    cosine, sine = rope_tables(position, HEAD_DIMENSION)
    cosine = jnp.concatenate([cosine[:, 0], cosine[:, 0]], axis=1)
    sine = jnp.concatenate([sine[:, 0], -sine[:, 0]], axis=1)
    table = jnp.stack([segment, position])
    info_rows = jnp.pad(table, ((0, 6), (0, 0)))
    info_cols = jnp.pad(table.T, ((0, 0), (0, 126)))
    blocks = jnp.pad(small, ((0, places - small.shape[0]), (0, 0))).reshape(places, -1, 128)
    sizes = [w.shape[0] // ep_size for w in (w_query, w_key, w_value, w_out)]
    total = sum(sizes[:3])

    def partial(rows, columns):
        return (depth, 2, rows, columns), bf16

    wide = width // 2
    got = pl.pallas_call(
        functools.partial(back_kernel, ep_size, heads, small.shape[0]),
        out_shape=(
            jax.ShapeDtypeStruct(*partial(total, wide)),
            jax.ShapeDtypeStruct(*partial(total, wide)),
            jax.ShapeDtypeStruct(*partial(sizes[3], width)),
            jax.ShapeDtypeStruct((share, width), f32),
            jax.ShapeDtypeStruct(blocks.shape, f32),
        )
        + tuple(jax.ShapeDtypeStruct(p.shape, p.dtype) for p in peers),
        in_specs=[vmem] * 19 + [anywhere] * 3,
        out_specs=(vmem,) * 5 + (anywhere,) * 3,
        scratch_shapes=[
            pltpu.VMEM((2, 2, share, width), bf16),
            pltpu.VMEM((tokens, tokens), f32),
            pltpu.VMEM(queries.shape, bf16),
            pltpu.VMEM((tokens, queries.shape[1] + 2 * keys.shape[1]), bf16),
            pltpu.VMEM((tokens, HEAD_DIMENSION), f32),
            pltpu.VMEM((tokens, HEAD_DIMENSION), f32),
        ]
        + [pltpu.VMEM((2, depth, 2, k, wide), bf16) for k in sizes[:3]]
        + [
            pltpu.VMEM((depth, 2, sizes[3], width), bf16),
            pltpu.VMEM((2, depth, total, wide), bf16),
            pltpu.VMEM((2, depth - 1, total, wide), bf16),
            pltpu.VMEM((depth, sizes[3], width), bf16),
            pltpu.VMEM((depth - 1, sizes[3], width), bf16),
            pltpu.VMEM((2, 2, share, width), bf16),
            pltpu.VMEM((2, share, width), bf16),
            pltpu.VMEM((share, width), bf16),
            pltpu.VMEM(blocks.shape, f32),
            pltpu.VMEM(blocks.shape, f32),
            pltpu.VMEM(blocks.shape[1:], f32),
            dma,
            dma((2, 12)),
        ]
        + [dma((2, 2, depth, 3))]
        + [dma((2, 2, depth))] * 3
        + [dma((2, depth, 1))]
        + [dma((2, depth))] * 3
        + [dma((2, 3)), dma((2, places - 1)), dma((2, places - 1)), dma, dma((2, 3))],
        compiler_params=pltpu.CompilerParams(
            collective_id=5, has_side_effects=True, vmem_limit_bytes=60 * 1024 * 1024
        ),
        name="back_by_links",
    )(
        datt_own,
        heads_in,
        w_out,
        queries,
        keys,
        values,
        log_sums,
        info_cols,
        info_rows,
        cosine,
        sine,
        rows_in,
        w_query,
        w_key,
        w_value,
        blocks,
        gain[None, :],
        inputs,
        middle,
        *peers,
    )
    return got


def deliver_kernel(
    ep_size,
    sizes,
    rows_in,
    sums_in,
    gate_in,
    up_in,
    down_in,
    gate_got,
    up_got,
    down_got,
    first,
    second,
    third,
    small,
    gate_out,
    up_out,
    down_out,
    rows_out,
    sums_out,
    query_out,
    key_out,
    value_out,
    out_out,
    router_out,
    first_gain,
    second_gain,
    query,
    key,
    value,
    out,
    gate,
    up,
    down,
    sems,
):
    pairs = ((rows_in, rows_out), (sums_in, sums_out))
    copies = [
        pltpu.make_async_copy(source, target, sems.at[i]) for i, (source, target) in enumerate(pairs)
    ]
    for copy in copies:
        copy.start()
    wide = first.shape[2]
    f32 = jnp.float32

    def leave(source, target, i):
        copies.append(pltpu.make_async_copy(source, target, sems.at[i]))
        copies[-1].start()

    trios = ((gate, gate_in, gate_got), (up, up_in, up_got), (down, down_in, down_got))
    for i, (total, mine, got) in enumerate(trios):
        total[...] = mine[...] + got[...].astype(f32)
        leave(total, (gate_out, up_out, down_out)[i], 2 + i)
    out[...] = third[...].astype(f32)
    leave(out, out_out, 5)
    at = 0
    for i, (source, target) in enumerate(((query, query_out), (key, key_out), (value, value_out))):
        for n, part in enumerate((first, second)):
            source[:, :, n * wide : (n + 1) * wide] = part[:, at : at + sizes[i], :].astype(f32)
        at += sizes[i]
        leave(source, target, 6 + i)
    experts = router_out.shape[0]
    for j in range(small.shape[1]):
        cols = slice(j * 128, (j + 1) * 128)
        router_out[:, cols] = small[:experts, j, :]
        first_gain[:, cols] = small[experts + 1 : experts + 2, j, :]
        second_gain[:, cols] = small[experts : experts + 1, j, :]
    for copy in copies:
        copy.wait()


def deliver(owned, peers, rows, sums, got, small, sizes, expert_count, ep_size):
    width = rows.shape[1]
    f32 = jnp.float32
    vmem, anywhere = pl.BlockSpec(memory_space=pltpu.VMEM), pl.BlockSpec(memory_space=pltpu.HBM)
    first, second, third = (g.reshape((ep_size,) + g.shape[2:]) for g in got)

    def like(value):
        return jax.ShapeDtypeStruct(value.shape, value.dtype)

    shapes = [(ep_size, k, width) for k in sizes]
    results = pl.pallas_call(
        functools.partial(deliver_kernel, ep_size, sizes),
        out_shape=tuple(like(a) for a in owned)
        + (like(rows), like(sums))
        + tuple(jax.ShapeDtypeStruct(shape, f32) for shape in shapes)
        + (
            jax.ShapeDtypeStruct((expert_count, width), f32),
            jax.ShapeDtypeStruct((1, width), f32),
            jax.ShapeDtypeStruct((1, width), f32),
        ),
        in_specs=[anywhere] * 2 + [vmem] * 10,
        out_specs=(anywhere,) * 9 + (vmem,) * 3,
        scratch_shapes=[pltpu.VMEM(shape, f32) for shape in shapes]
        + [pltpu.VMEM(a.shape, f32) for a in owned]
        + [pltpu.SemaphoreType.DMA((9,))],
        compiler_params=pltpu.CompilerParams(vmem_limit_bytes=40 * 1024 * 1024),
        name="deliver",
    )(rows, sums, *owned, *peers, first, second, third, small)
    gate, up, down, rows, sums = results[:5]
    query, key, value, out = (g.reshape(-1, width) for g in results[5:9])
    router, first_gain, second_gain = results[9:]
    return (
        sums,
        rows,
        first_gain[0],
        query,
        key,
        value,
        out,
        second_gain[0],
        router,
        gate,
        up,
        down.reshape(gate.shape[0], -1, width),
    )


def group_rows(value_rows):
    return lax.all_gather(value_rows, "tp", axis=0, tiled=True)


def group_totals(value_rows, by_links, call):
    if by_links:
        return group_total(value_rows, lax.axis_size("ep"), call)
    return lax.psum_scatter(value_rows, "tp", scatter_dimension=0, tiled=True).astype(jnp.float32)


def gather_all(value_rows):
    return lax.all_gather(value_rows, ("ep", "tp"), axis=0, tiled=True)


LAST = 1 << 30


def pair_order(expert_ids, slot_order, expert_count):
    experts = jnp.arange(expert_count, dtype=jnp.int32)
    chosen = expert_ids.T[None, :, :] == experts[:, None, None]
    return jnp.min(jnp.where(chosen, slot_order.T[None, :, :], LAST), axis=1)


def kept_pairs(order):
    used = order < LAST
    counts = jnp.sum(used.astype(jnp.int32), axis=2)
    block = jnp.arange(order.shape[0], dtype=jnp.int32)
    earlier = block[None, :] < block[:, None]
    offsets = jnp.sum(jnp.where(earlier[:, :, None], counts[None, :, :], 0), axis=1)
    whole = offsets + counts <= CAP
    edge = (offsets < CAP) & ~whole
    edge_order = jnp.sum(jnp.where(edge[:, :, None], order, 0), axis=0)
    rank = jnp.sum((edge_order[:, :, None] < edge_order[:, None, :]).astype(jnp.int32), axis=1)
    early = offsets[:, :, None] + rank[None, :, :] < CAP
    return used & (whole[:, :, None] | (edge[:, :, None] & early))


def masked_softmax(logits, used):
    top = jnp.max(jnp.where(used, logits, -1e30), axis=-1, keepdims=True)
    powers = jnp.where(used, jnp.exp(logits - top), 0.0)
    return powers / jnp.sum(powers, axis=-1, keepdims=True)


def pair_codes(order_all, per_owner):
    expert_count = order_all.shape[1]
    first = lax.axis_index("ep") * per_owner
    turned = jnp.roll(order_all, -first, axis=1)
    kept = kept_pairs(turned[:, :per_owner])
    dropped = jnp.pad(~kept, ((0, 0), (0, expert_count - per_owner), (0, 0)))
    code = jnp.where(turned < LAST, dropped.astype(jnp.float32), -1.0)
    code = code.swapaxes(1, 2).reshape(-1, expert_count)
    lanes = -expert_count % 128
    return jnp.pad(code, ((0, 0), (0, lanes)), constant_values=-1.0).astype(jnp.bfloat16)


def expert_weights(w_gate, w_up, w_down):
    enter = jnp.concatenate([w[e] for w in (w_gate, w_up) for e in range(w.shape[0])], axis=1)
    return enter, w_down.reshape(-1, w_down.shape[2])


def run_experts(rows_all, cots_all, code, w_router, w_gate, w_up, w_down, weights, by_links):
    per_owner, width, units = w_gate.shape
    expert_count = w_router.shape[0]
    ep_size, tp_size = lax.axis_size("ep"), lax.axis_size("tp")
    hidden = per_owner * units
    router = jnp.roll(w_router, -lax.axis_index("ep") * per_owner, axis=0)
    router = jnp.pad(router, ((0, -expert_count % 128), (0, 0)))
    if by_links:
        grads, sums, small, *owned = experts_by_links(
            rows_all, cots_all, code, router, weights, per_owner, ep_size
        )
        share = grads.shape[0]
        return (
            grads,
            sums,
            small[:, :per_owner].reshape(expert_count, share).T,
            owned[:3],
            owned[3:],
        )
    enter, leave = expert_weights(w_gate, w_up, w_down)
    used, kept = code >= 0, (code == 0).astype(jnp.float32)
    logits = jnp.einsum("rd,ed->re", rows_all, router, preferred_element_type=jnp.float32)
    gates = jnp.repeat((kept * masked_softmax(logits, used))[:, :per_owner], units, axis=1)
    act = jnp.dot(rows_all, enter, preferred_element_type=jnp.float32)
    gate_act, up_act = act[:, :hidden], act[:, hidden:]
    back_act = jnp.einsum("rd,fd->rf", cots_all, leave, preferred_element_type=jnp.float32)
    sigma = jax.nn.sigmoid(gate_act)
    value = gate_act * sigma * up_act
    weighted = (gates * value).astype(jnp.bfloat16)
    grad_hidden = gates * back_act
    turned = jnp.concatenate(
        [
            grad_hidden * up_act * sigma * (1.0 + gate_act * (1.0 - sigma)),
            grad_hidden * gate_act * sigma,
        ],
        axis=1,
    ).astype(jnp.bfloat16)
    small = kept[:, :per_owner] * jnp.sum((value * back_act).reshape(-1, per_owner, units), axis=2)
    grads = jnp.einsum("rf,df->rd", turned, enter, preferred_element_type=jnp.float32)
    sums = jnp.dot(weighted, leave, preferred_element_type=jnp.float32)

    def scatter(value_rows):
        return lax.psum_scatter(value_rows, ("ep", "tp"), scatter_dimension=0, tiled=True)

    columns = lax.dynamic_update_slice_in_dim(
        jnp.zeros((small.shape[0], expert_count), jnp.float32),
        small,
        lax.axis_index("ep") * per_owner,
        1,
    )
    both = jnp.einsum(
        "rd,rwef->wedf",
        rows_all,
        turned.reshape(-1, 2, per_owner, units),
        preferred_element_type=jnp.float32,
    )
    down = jnp.einsum("rf,rd->fd", weighted, cots_all, preferred_element_type=jnp.float32)
    return (
        scatter(grads.astype(jnp.bfloat16)).astype(jnp.float32),
        scatter(sums.astype(jnp.bfloat16)).astype(jnp.float32),
        scatter(columns),
        (both[0], both[1], down),
        None,
    )


def visible_block(query_seg, query_pos, query_row, key_seg, key_pos, key_row):
    seg_q = query_seg[:, None]
    seg_k = key_seg[None, :]
    above = (
        (seg_k == seg_q)
        | (seg_k == 0)
        | (seg_k >= 1) & (seg_k <= 4) & (seg_q >= 5) & ((seg_q - 5) // 2 + 1 == seg_k)
    )
    same_tree = query_row[:, None] // TREE_TOKENS == key_row[None, :] // TREE_TOKENS
    return above & same_tree & (key_pos[None, :] <= query_pos[:, None])


def block_scores(query_part, key_rows, allowed, scale):
    scores = (
        jnp.einsum("qkgd,pkd->kgqp", query_part, key_rows, preferred_element_type=jnp.float32)
        * scale
    )
    return jnp.where(allowed[None, None], scores, -1e30)


def attend_forward(query_rows, key_rows, value_rows, segment, position):
    total_rows = query_rows.shape[0]
    scale = query_rows.shape[-1] ** (-0.5)
    row_ids = jnp.arange(total_rows, dtype=jnp.int32)
    allowed = visible_block(segment, position, row_ids, segment, position, row_ids)
    scores = block_scores(query_rows, key_rows, allowed, scale)
    top_score = jnp.max(scores, axis=-1, keepdims=True)
    weights = jnp.exp(scores - top_score)
    weight_sum = jnp.sum(weights, axis=-1, keepdims=True)
    probs = (weights / weight_sum).astype(jnp.bfloat16)
    outputs = jnp.einsum(
        "kgqp,pkd->qkgd", probs, value_rows, preferred_element_type=jnp.float32
    ).astype(jnp.bfloat16)
    log_sums = [top_score + jnp.log(weight_sum)]
    return (outputs, log_sums)


def attend_backward(
    query_rows, key_rows, value_rows, segment, position, log_sums, grad_heads, block_rows
):
    total_rows = query_rows.shape[0]
    scale = query_rows.shape[-1] ** (-0.5)
    row_ids = jnp.arange(total_rows, dtype=jnp.int32)
    grad_keys = jnp.zeros(key_rows.shape, jnp.float32)
    grad_values = jnp.zeros(value_rows.shape, jnp.float32)
    grad_query = []
    for number, first_row in enumerate(range(0, total_rows, block_rows)):
        allowed = visible_block(segment, position, row_ids, segment, position, row_ids)
        scores = block_scores(query_rows, key_rows, allowed, scale)
        probs = jnp.where(allowed[None, None], jnp.exp(scores - log_sums[number]), 0.0)
        grad_values = jnp.einsum(
            "kgqp,qkgd->pkd",
            probs.astype(jnp.bfloat16),
            grad_heads,
            preferred_element_type=jnp.float32,
        )
        grad_probs = jnp.einsum(
            "qkgd,pkd->kgqp", grad_heads, value_rows, preferred_element_type=jnp.float32
        )
        inner = jnp.sum(probs * grad_probs, axis=-1, keepdims=True)
        grad_scores = (probs * (grad_probs - inner)).astype(jnp.bfloat16)
        grad_query.append(
            jnp.einsum("kgqp,pkd->qkgd", grad_scores, key_rows, preferred_element_type=jnp.float32)
            * scale
        )
        grad_keys = (
            jnp.einsum(
                "kgqp,qkgd->pkd", grad_scores, query_rows, preferred_element_type=jnp.float32
            )
            * scale
        )
    return (grad_query[0], grad_keys, grad_values)


def local(
    hidden_in,
    gain_attn,
    w_query,
    key_projection_weight,
    value_projection_weight,
    w_out,
    gain_ffn,
    w_router,
    w_gate,
    w_up,
    w_down,
    expert_ids,
    slot_order,
    segment,
    position,
    cotangent,
):
    model_width = w_query.shape[1]
    head_width = HEAD_DIMENSION
    local_heads = w_query.shape[0] // head_width
    local_kv = key_projection_weight.shape[0] // head_width
    group_factor = local_heads // local_kv
    token_count = expert_ids.shape[0]
    share = hidden_in.shape[0]
    row_start = lax.axis_index("tp") * share
    expert_count = w_router.shape[0]
    per_owner = w_gate.shape[0]
    block_rows = 512
    by_links = lax.axis_size("tp") == 4 and lax.axis_size("ep") == 8
    order = pair_order(expert_ids, slot_order, expert_count)
    if by_links:
        near = expert_weights(w_gate, w_up, w_down)
        far = [lax.ppermute(w, "tp", [(0, 2), (1, 3), (2, 0), (3, 1)]) for w in near]
        weights = (near[0], far[0], near[1], far[1])
    else:
        weights = None
    inputs_own = hidden_in.astype(jnp.float32)
    gain_one = gain_attn.astype(jnp.float32)
    gain_two = gain_ffn.astype(jnp.float32)
    scale_one = norm_scale(inputs_own)
    first_own = (inputs_own * scale_one * gain_one).astype(jnp.bfloat16)
    if by_links:
        first_normalized, order_all = front_gather(first_own, order, lax.axis_size("ep"))
    else:
        first_normalized = group_rows(first_own)
        order_all = lax.all_gather(order, "ep")
    code = pair_codes(order_all, per_owner)
    cosine_lookup, sine_lookup = rope_tables(position, head_width)
    query_proj = jnp.einsum(
        "rd,fd->rf", first_normalized, w_query, preferred_element_type=jnp.float32
    ).reshape(token_count, local_heads, head_width)
    key_proj = jnp.einsum(
        "rd,fd->rf", first_normalized, key_projection_weight, preferred_element_type=jnp.float32
    ).reshape(token_count, local_kv, head_width)
    query_rows = (
        apply_rotation(query_proj, cosine_lookup, sine_lookup)
        .astype(jnp.bfloat16)
        .reshape(token_count, local_kv, group_factor, head_width)
    )
    key_rows = apply_rotation(key_proj, cosine_lookup, sine_lookup).astype(jnp.bfloat16)
    value_rows = (
        jnp.einsum(
            "rd,fd->rf",
            first_normalized,
            value_projection_weight,
            preferred_element_type=jnp.float32,
        )
        .astype(jnp.bfloat16)
        .reshape(token_count, local_kv, head_width)
    )
    head_outputs, log_sums = attend_forward(query_rows, key_rows, value_rows, segment, position)
    head_outputs = head_outputs.reshape(token_count, local_heads * head_width)
    middle_own = inputs_own + group_totals(
        jnp.dot(head_outputs, w_out, preferred_element_type=jnp.float32).astype(jnp.bfloat16),
        by_links,
        3,
    )
    scale_two = norm_scale(middle_own)
    normed_own = (middle_own * scale_two * gain_two).astype(jnp.bfloat16)
    if by_links:
        normed_two, cot_all = gather_by_links([normed_own, cotangent], lax.axis_size("ep"))
    else:
        normed_two, cot_all = gather_all(normed_own), gather_all(cotangent)
    used = lax.dynamic_slice_in_dim(order, row_start, share, 1).T < LAST
    gates = masked_softmax(
        jnp.einsum("rd,ed->re", normed_own, w_router, preferred_element_type=jnp.float32), used
    )
    grad_normed_own, combined_own, grad_gates_own, owned, peers = run_experts(
        normed_two, cot_all, code, w_router, w_gate, w_up, w_down, weights, by_links
    )
    output_own = (middle_own + combined_own).astype(jnp.bfloat16)
    inner_gate = jnp.sum(gates * grad_gates_own, axis=-1, keepdims=True)
    grad_logits = gates * (grad_gates_own - inner_gate)
    router_f = w_router.astype(jnp.float32)
    grad_normed_own = grad_normed_own + jnp.dot(grad_logits, router_f, precision=EXACT_PRECISION)
    grad_router = jnp.dot(grad_logits.T, normed_own.astype(jnp.float32), precision=EXACT_PRECISION)
    grad_gain_ffn = jnp.sum(grad_normed_own * middle_own * scale_two, axis=0)
    grad_middle = cotangent.astype(jnp.float32) + norm_back(
        middle_own, scale_two, gain_two, grad_normed_own
    )
    if by_links:
        *got, grad_input, small, gate_got, up_got, down_got = back_by_links(
            grad_middle.astype(jnp.bfloat16),
            head_outputs,
            w_out,
            query_rows.reshape(token_count, -1),
            key_rows.reshape(token_count, -1),
            value_rows.reshape(token_count, -1),
            jnp.pad(log_sums[0].reshape(local_heads, token_count), ((0, -local_heads % 8), (0, 0))),
            segment,
            position,
            first_normalized,
            w_query,
            key_projection_weight,
            value_projection_weight,
            jnp.concatenate([grad_router, grad_gain_ffn[None, :]], axis=0),
            gain_one,
            hidden_in,
            grad_middle,
            peers,
            lax.axis_size("ep"),
        )
        ep_size = lax.axis_size("ep")
        weights = (w_query, key_projection_weight, value_projection_weight, w_out)
        return deliver(
            owned,
            (gate_got, up_got, down_got),
            grad_input,
            output_own,
            got,
            small,
            [w.shape[0] // ep_size for w in weights],
            expert_count,
            ep_size,
        )
    grad_attn = group_rows(grad_middle.astype(jnp.bfloat16))
    grad_w_out = jnp.einsum(
        "rf,rd->fd", head_outputs, grad_attn, preferred_element_type=jnp.float32
    )
    grad_w_out = lax.psum(grad_w_out.astype(jnp.bfloat16), "ep").astype(jnp.float32)
    grad_heads = (
        jnp.einsum("rd,fd->rf", grad_attn, w_out, preferred_element_type=jnp.float32)
        .astype(jnp.bfloat16)
        .reshape(token_count, local_kv, group_factor, head_width)
    )
    grad_query, grad_keys, grad_values = attend_backward(
        query_rows, key_rows, value_rows, segment, position, log_sums, grad_heads, block_rows
    )
    grad_query_proj = (
        rotate_back(
            grad_query.reshape(token_count, local_heads, head_width), cosine_lookup, sine_lookup
        )
        .astype(jnp.bfloat16)
        .reshape(token_count, local_heads * head_width)
    )
    grad_key_proj = (
        rotate_back(grad_keys, cosine_lookup, sine_lookup)
        .astype(jnp.bfloat16)
        .reshape(token_count, local_kv * head_width)
    )
    grad_value_proj = grad_values.astype(jnp.bfloat16).reshape(token_count, local_kv * head_width)
    grad_w_query = jnp.einsum(
        "rf,rd->fd", grad_query_proj, first_normalized, preferred_element_type=jnp.float32
    )
    grad_w_key = jnp.einsum(
        "rf,rd->fd", grad_key_proj, first_normalized, preferred_element_type=jnp.float32
    )
    grad_w_value = jnp.einsum(
        "rf,rd->fd", grad_value_proj, first_normalized, preferred_element_type=jnp.float32
    )
    grad_normed_one = jnp.einsum(
        "rf,fd->rd", grad_query_proj, w_query, preferred_element_type=jnp.float32
    )
    grad_normed_one = grad_normed_one + jnp.einsum(
        "rf,fd->rd", grad_key_proj, key_projection_weight, preferred_element_type=jnp.float32
    )
    grad_normed_one = grad_normed_one + jnp.einsum(
        "rf,fd->rd", grad_value_proj, value_projection_weight, preferred_element_type=jnp.float32
    )
    grad_gain_attn = jnp.sum(grad_normed_one * first_normalized.astype(jnp.float32), axis=0)
    small = jnp.concatenate(
        [grad_router, grad_gain_ffn[None, :], (grad_gain_attn / gain_one)[None, :]], axis=0
    )
    grad_w_query, grad_w_key, grad_w_value = (
        lax.psum(g.astype(jnp.bfloat16), "ep").astype(jnp.float32)
        for g in (grad_w_query, grad_w_key, grad_w_value)
    )
    grad_one_own = group_totals(grad_normed_one.astype(jnp.bfloat16), by_links, None)
    small = lax.psum(small, ("ep", "tp"))
    grad_input = grad_middle + norm_back(inputs_own, scale_one, gain_one, grad_one_own)
    grad_router = small[:expert_count]
    grad_gain_ffn, grad_gain_attn = small[expert_count], small[expert_count + 1]
    return (
        output_own,
        grad_input,
        grad_gain_attn,
        grad_w_query,
        grad_w_key,
        grad_w_value,
        grad_w_out,
        grad_gain_ffn,
        grad_router,
        owned[0],
        owned[1],
        owned[2].reshape(w_down.shape),
    )


def solution(mesh):
    placed = (
        P(("ep", "tp"), None),
        P(),
        P("tp", None),
        P("tp", None),
        P("tp", None),
        P("tp", None),
        P(),
        P(),
        P("ep", None, "tp"),
        P("ep", None, "tp"),
        P("ep", "tp", None),
        P("ep", None),
        P("ep", None),
        P("ep"),
        P("ep"),
        P(("ep", "tp"), None),
    )
    return jax.shard_map(
        local,
        mesh=mesh,
        in_specs=placed,
        out_specs=(
            P(("ep", "tp"), None),
            P(("ep", "tp"), None),
            P(),
            P("tp", None),
            P("tp", None),
            P("tp", None),
            P("tp", None),
            P(),
            P(),
            P("ep", None, "tp"),
            P("ep", None, "tp"),
            P("ep", "tp", None),
        ),
        check_vma=False,
    )
```

```python
import functools

import jax
import jax.numpy as jnp
from jax import lax
from jax.experimental import pallas as pl
from jax.experimental.pallas import tpu as pltpu
from jax.sharding import PartitionSpec as P

HEAD_DIMENSION = 64
TREE_TOKENS = 512
CAP = 2304


EPSILON = 1e-06
ROPE_BASE = 10000.0
EXACT_PRECISION = lax.Precision.HIGHEST


def rope_tables(position, head_width):
    half_width = head_width // 2
    freqs = ROPE_BASE ** (-(jnp.arange(half_width, dtype=jnp.float32) * 2.0 / head_width))
    angle = position.astype(jnp.float32)[:, None] * freqs[None, :]
    return (jnp.cos(angle)[:, None, :], jnp.sin(angle)[:, None, :])


def apply_rotation(value_rows, cosine_lookup, sine_lookup):
    half_width = value_rows.shape[-1] // 2
    first = value_rows[..., :half_width]
    second = value_rows[..., half_width:]
    return jnp.concatenate(
        [
            first * cosine_lookup - second * sine_lookup,
            first * sine_lookup + second * cosine_lookup,
        ],
        axis=-1,
    )


def rotate_back(grads, cosine_lookup, sine_lookup):
    half_width = grads.shape[-1] // 2
    first = grads[..., :half_width]
    second = grads[..., half_width:]
    return jnp.concatenate(
        [
            first * cosine_lookup + second * sine_lookup,
            second * cosine_lookup - first * sine_lookup,
        ],
        axis=-1,
    )


def norm_scale(value_rows):
    return lax.rsqrt(jnp.mean(value_rows * value_rows, axis=-1, keepdims=True) + EPSILON)


def norm_back(value_rows, scale, gain, grad_normed):
    weighted = grad_normed * gain
    inner = jnp.mean(value_rows * weighted, axis=-1, keepdims=True)
    grad_values = scale * weighted - value_rows * (scale * scale * scale) * inner
    return grad_values


MESH = pl.DeviceIdType.MESH


class Place:
    def __init__(self, ep_size):
        self.depth = ep_size // 2
        ep, tp = lax.axis_index("ep"), lax.axis_index("tp")
        self.z, self.y = ep // 2, ep % 2
        self.x, self.c = tp // 2, tp % 2

    def device(self, z=None, y=None, x=None, c=None):
        z = self.z if z is None else z
        y = self.y if y is None else y
        x = self.x if x is None else x
        c = self.c if c is None else c
        return (z * 2 + y, x * 2 + c)

    def sibling(self):
        return self.device(c=1 - self.c)

    def x_peer(self):
        return self.device(x=1 - self.x)

    def y_peer(self):
        return self.device(y=1 - self.y)

    def after(self, step):
        return lax.rem(self.z + step, self.depth)

    def before(self, step):
        return lax.rem(self.z + self.depth - step, self.depth)


def meet(devices):
    barrier = pltpu.get_barrier_semaphore()
    for device in devices:
        pl.semaphore_signal(barrier, inc=1, device_id=device, device_id_type=MESH)
    pl.semaphore_wait(barrier, len(devices))


def send(src, dst, send_sem, recv_sem, device):
    copy = pltpu.make_async_remote_copy(
        src_ref=src,
        dst_ref=dst,
        send_sem=send_sem,
        recv_sem=recv_sem,
        device_id=device,
        device_id_type=MESH,
    )
    copy.start()
    return copy


def add_into(target, other):
    def tile(i, carry):
        at = pl.ds(pl.multiple_of(i * 16, 16), 16)
        target[at, :] = target[at, :] + other[at, :]
        return carry

    lax.fori_loop(0, target.shape[0] // 16, tile, 0)


def group_gather_body(me, pieces, own, out, own_sem, sems):
    size = own.shape[0] // pieces
    started = []
    local = pltpu.make_async_copy(own, out.at[me.x, me.c], own_sem)
    local.start()

    def at(p):
        return pl.ds(p * size, size)

    def go(kind, p, src, dst, device):
        slot = kind * pieces + p
        started.append(send(src, dst, sems.at[0, slot], sems.at[1, slot], device))

    for p in range(pieces):
        go(0, p, own.at[at(p)], out.at[me.x, me.c, at(p)], me.x_peer())
    for p in range(pieces):
        go(1, p, own.at[at(p)], out.at[me.x, me.c, at(p)], me.sibling())
    for p in range(pieces):
        block = out.at[1 - me.x, me.c, at(p)]
        pltpu.make_async_copy(block, block, sems.at[1, p]).wait()
        go(2, p, block, block, me.sibling())
    for p in range(pieces):
        for kind, x in ((1, me.x), (2, 1 - me.x)):
            block = out.at[x, 1 - me.c, at(p)]
            pltpu.make_async_copy(block, block, sems.at[1, kind * pieces + p]).wait()
    local.wait()
    for copy in started:
        copy.wait_send()


class GroupTotal:
    def __init__(self, me, parts, core_got, pair_got, sems):
        self.me, self.parts, self.core_got, self.pair_got = me, parts, core_got, pair_got
        self.core = [
            pltpu.make_async_remote_copy(
                src_ref=parts.at[x, 1 - me.c],
                dst_ref=core_got.at[x],
                send_sem=sems.at[0, k],
                recv_sem=sems.at[1, k],
                device_id=me.sibling(),
                device_id_type=MESH,
            )
            for k, x in enumerate((1 - me.x, me.x))
        ]
        self.pair = pltpu.make_async_remote_copy(
            src_ref=core_got.at[1 - me.x],
            dst_ref=pair_got,
            send_sem=sems.at[0, 2],
            recv_sem=sems.at[1, 2],
            device_id=me.x_peer(),
            device_id_type=MESH,
        )

    def begin(self):
        for copy in self.core:
            copy.start()

    def exchange(self):
        self.core[0].wait_recv()
        far = 1 - self.me.x
        add_into(self.core_got.at[far], self.parts.at[far, self.me.c])
        self.pair.start()

    def finish(self, out, change=lambda value, at: value):
        self.core[1].wait_recv()
        self.pair.wait_recv()

        def tile(i, carry):
            at = pl.ds(pl.multiple_of(i * 16, 16), 16)
            value = (
                self.parts[self.me.x, self.me.c, at, :].astype(jnp.float32)
                + self.core_got[self.me.x, at, :].astype(jnp.float32)
                + self.pair_got[at, :].astype(jnp.float32)
            )
            out[at, :] = change(value, at)
            return carry

        lax.fori_loop(0, out.shape[0] // 16, tile, 0)

    def sent(self):
        for copy in self.core + [self.pair]:
            copy.wait_send()


def all_others(ep_size):
    ep, tp = lax.axis_index("ep"), lax.axis_index("tp")
    return [
        (lax.rem(ep + k // 4, ep_size), lax.rem(tp + k % 4, 4)) for k in range(1, ep_size * 4)
    ]


def experts_kernel(
    ep_size,
    per_owner,
    rows_in,
    cots_in,
    code_in,
    router,
    enter_own,
    enter_peer,
    leave_own,
    leave_peer,
    grad_out,
    sum_out,
    small_out,
    gate_out,
    up_out,
    down_out,
    gate_peer,
    up_peer,
    down_peer,
    rows_buf,
    cots_buf,
    weighted,
    turned,
    enter_sum,
    down_sum,
    parts,
    core_got,
    y_got,
    z_got,
    small_in,
    small_got,
    load_sems,
    core_sems,
    y_sems,
    z_sems,
    small_sems,
    own_sem,
):
    me = Place(ep_size)
    depth = me.depth
    blocks = 2 * depth
    width = router.shape[1]
    share = rows_buf.shape[2]
    tokens = 2 * share
    hidden = leave_own.shape[0]
    units = hidden // per_owner
    f32, bf16 = jnp.float32, jnp.bfloat16
    ep = lax.axis_index("ep")
    others = [
        (lax.rem(ep + k // 2, ep_size), me.x * 2 + lax.rem(me.c + k % 2, 2))
        for k in range(1, 2 * ep_size)
    ]
    meet(others)
    my_place = ep * 2 + me.c
    halves = ((enter_own, leave_own), (enter_peer, leave_peer))

    def where(b):
        return me.after(b // 2 + 1), lax.rem(1 - me.y + b % 2, 2)

    def load(b, which):
        z, y = where(b)
        source, target = ((rows_in, rows_buf), (cots_in, cots_buf))[which]
        slot = lax.rem(b, 2)
        return pltpu.make_async_copy(
            source.at[z, y], target.at[slot], load_sems.at[slot, which]
        )

    def core_copy(b):
        return pltpu.make_async_remote_copy(
            src_ref=parts.at[lax.rem(b, 2), :, 1 - me.c],
            dst_ref=core_got.at[b // 2, where(b)[1]],
            send_sem=core_sems.at[0, b],
            recv_sem=core_sems.at[1, b],
            device_id=me.sibling(),
            device_id_type=MESH,
        )

    def y_copy(step, which):
        return pltpu.make_async_remote_copy(
            src_ref=core_got.at[step, 1 - me.y, which],
            dst_ref=y_got.at[step, which],
            send_sem=y_sems.at[0, step, which],
            recv_sem=y_sems.at[1, step, which],
            device_id=me.y_peer(),
            device_id_type=MESH,
        )

    def z_copy(step, which):
        return pltpu.make_async_remote_copy(
            src_ref=y_got.at[step, which],
            dst_ref=z_got.at[step, which],
            send_sem=z_sems.at[0, step, which],
            recv_sem=z_sems.at[1, step, which],
            device_id=me.device(z=me.after(step + 1)),
            device_id_type=MESH,
        )

    def small_copy(k, device):
        return pltpu.make_async_remote_copy(
            src_ref=small_in.at[device[0] * 2 + device[1] % 2],
            dst_ref=small_got.at[my_place],
            send_sem=small_sems.at[0, k],
            recv_sem=small_sems.at[1, k],
            device_id=device,
            device_id_type=MESH,
        )

    def dot(a, b, contract):
        return lax.dot_general(
            a, b, ((contract[:1], contract[1:]), ((), ())), preferred_element_type=f32
        )

    def spread(columns):
        return jnp.concatenate(
            [jnp.broadcast_to(columns[:, e : e + 1], (tokens, units)) for e in range(per_owner)],
            axis=1,
        )

    def compute(b):
        z, y = where(b)
        slot = lax.rem(b, 2)
        rows = rows_buf[slot].reshape(tokens, width)
        cots = cots_buf[slot].reshape(tokens, width)
        code = code_in[z * 2 + y, me.x].astype(f32).reshape(tokens, -1)
        used = code >= 0.0
        logits = jnp.where(used, dot(rows, router[...], (1, 1)), -1e30)
        top = jnp.max(logits, axis=1, keepdims=True)
        powers = jnp.where(used, jnp.exp(logits - top), 0.0)
        kept = jnp.where(code == 0.0, 1.0, 0.0)
        gates = spread(kept * powers / jnp.sum(powers, axis=1, keepdims=True))
        products = jnp.zeros((tokens, hidden), f32)
        for h, (enter, leave) in enumerate(halves):
            act = dot(rows, enter[...], (1, 0))
            gate_act, up_act = act[:, :hidden], act[:, hidden:]
            back_act = dot(cots, leave[...], (1, 1))
            sigma = jax.nn.sigmoid(gate_act)
            swish = gate_act * sigma
            value = swish * up_act
            products = products + value * back_act
            weighted[:, h * hidden : (h + 1) * hidden] = (gates * value).astype(bf16)
            grad_hidden = gates * back_act
            at = 2 * h * hidden
            turned[:, at : at + hidden] = (
                grad_hidden * up_act * sigma * (1.0 + gate_act * (1.0 - sigma))
            ).astype(bf16)
            turned[:, at + hidden : at + 2 * hidden] = (grad_hidden * swish).astype(bf16)
        lane = lax.broadcasted_iota(jnp.int32, (8, hidden), 1)
        pick = lax.broadcasted_iota(jnp.int32, (8, hidden), 0)
        mine = jnp.where((lane >= pick * units) & (lane < (pick + 1) * units), 1.0, 0.0)
        grad_gates = lax.dot_general(
            mine,
            spread(kept) * products,
            (((1,), (1,)), ((), ())),
            precision=EXACT_PRECISION,
            preferred_element_type=f32,
        )
        for k in range(2):
            small_in[(z * 2 + y) * 2 + k] = grad_gates[:, k * share : (k + 1) * share]
        tile = 512
        for n in range(width // tile):
            cols = slice(n * tile, (n + 1) * tile)
            grads = (
                dot(turned[:, : 2 * hidden], enter_own[cols, :], (1, 1))
                + dot(turned[:, 2 * hidden :], enter_peer[cols, :], (1, 1))
            ).astype(bf16)
            sums = (
                dot(weighted[:, :hidden], leave_own[:, cols], (1, 0))
                + dot(weighted[:, hidden:], leave_peer[:, cols], (1, 0))
            ).astype(bf16)
            for c in range(2):
                at = slice(c * share, (c + 1) * share)
                parts[slot, 0, c, :, cols] = grads[at]
                parts[slot, 1, c, :, cols] = sums[at]

    def weight_sums(b):
        slot = lax.rem(b, 2)
        tile = 512
        for n in range(width // tile):
            cols = slice(n * tile, (n + 1) * tile)
            rows = rows_buf[slot, :, :, cols].reshape(tokens, tile)
            cots = cots_buf[slot, :, :, cols].reshape(tokens, tile)
            enter_sum[:, cols] += dot(turned[...], rows, (0, 0))
            down_sum[:, cols] += dot(weighted[...], cots, (0, 0))

    enter_sum[...] = jnp.zeros_like(enter_sum)
    down_sum[...] = jnp.zeros_like(down_sum)
    for which in range(2):
        load(0, which).start()

    def during(i, lag, body, even=False):
        b = i - lag
        inside = (b >= 0) & (b < blocks)
        if even:
            inside &= b % 2 == 0
        pl.when(inside)(lambda: body(b))

    def work(b):
        for which in range(2):
            load(b, which).wait()

        @pl.when(b + 1 < blocks)
        def _():
            for which in range(2):
                load(b + 1, which).start()

        compute(b)
        core_copy(b).start()
        weight_sums(b)

    def core_sum(b):
        step, y = b // 2, where(b)[1]
        core_copy(b).wait_recv()
        for which in range(2):
            add_into(core_got.at[step, y, which], parts.at[lax.rem(b, 2), which, me.c])

        @pl.when(b % 2 == 0)
        def _():
            for which in range(2):
                y_copy(step, which).start()

        core_copy(b).wait_send()

    def y_sum(which):
        def body(b):
            step = b // 2
            y_copy(step, which).wait_recv()
            add_into(y_got.at[step, which], core_got.at[step, me.y, which])

            @pl.when(step < depth - 1)
            def _():
                z_copy(step, which).start()

        return body

    def small_send(b):
        for k, device in enumerate(others):
            small_copy(k, device).start()
        pltpu.make_async_copy(small_in.at[my_place], small_got.at[my_place], own_sem).start()
        for e in range(per_owner):
            own, peer = e * units, 2 * hidden + e * units
            gate_out[e] = enter_sum[own : own + units, :].T
            up_out[e] = enter_sum[hidden + own : hidden + own + units, :].T
            gate_peer[e] = enter_sum[peer : peer + units, :].T.astype(bf16)
            up_peer[e] = enter_sum[hidden + peer : hidden + peer + units, :].T.astype(bf16)
        down_out[...] = down_sum[:hidden, :]
        down_peer[...] = down_sum[hidden:, :].astype(bf16)

    def turn(i, carry):
        during(i, 0, work)
        during(i, 1, core_sum)
        during(i, 2, y_sum(0), True)
        during(i, 3, y_sum(1), True)
        pl.when(i == blocks)(lambda: small_send(i))
        return carry

    lax.fori_loop(0, blocks + 2, turn, 0)
    pltpu.make_async_copy(small_in.at[my_place], small_got.at[my_place], own_sem).wait()
    for k, device in enumerate(others):
        small_copy(k, device).wait()
    for k in range(ep_size):
        small_out[k] = small_got[2 * k] + small_got[2 * k + 1]
    for step in range(depth - 1):
        for which in range(2):
            z_copy(step, which).wait_recv()

    def finish(which, target):
        def tile(i, carry):
            at = pl.ds(pl.multiple_of(i * 16, 16), 16)
            total = y_got[depth - 1, which, at, :].astype(f32)
            for step in range(depth - 1):
                total = total + z_got[step, which, at, :].astype(f32)
            target[at, :] = total
            return carry

        lax.fori_loop(0, share // 16, tile, 0)

    finish(0, grad_out)
    finish(1, sum_out)
    for step in range(depth):
        for which in range(2):
            y_copy(step, which).wait_send()
            if step < depth - 1:
                z_copy(step, which).wait_send()


def experts_by_links(rows_all, cots_all, code, router, weights, per_owner, ep_size):
    depth, _, _, rows, width = rows_all.shape
    hidden = weights[2].shape[0]
    units = hidden // per_owner
    bf16, f32 = jnp.bfloat16, jnp.float32
    dma = pltpu.SemaphoreType.DMA
    vmem = pl.BlockSpec(memory_space=pltpu.VMEM)
    anywhere = pl.BlockSpec(memory_space=pltpu.HBM)
    places = 2 * ep_size
    return pl.pallas_call(
        functools.partial(experts_kernel, ep_size, per_owner),
        out_shape=(
            jax.ShapeDtypeStruct((rows, width), f32),
            jax.ShapeDtypeStruct((rows, width), f32),
            jax.ShapeDtypeStruct((ep_size, 8, rows), f32),
            jax.ShapeDtypeStruct((per_owner, width, units), f32),
            jax.ShapeDtypeStruct((per_owner, width, units), f32),
            jax.ShapeDtypeStruct((hidden, width), f32),
            jax.ShapeDtypeStruct((per_owner, width, units), bf16),
            jax.ShapeDtypeStruct((per_owner, width, units), bf16),
            jax.ShapeDtypeStruct((hidden, width), bf16),
        ),
        in_specs=[anywhere, anywhere] + [vmem] * 6,
        out_specs=(vmem,) * 9,
        scratch_shapes=[
            pltpu.VMEM((2, 2, rows, width), bf16),
            pltpu.VMEM((2, 2, rows, width), bf16),
            pltpu.VMEM((2 * rows, 2 * hidden), bf16),
            pltpu.VMEM((2 * rows, 4 * hidden), bf16),
            pltpu.VMEM((4 * hidden, width), f32),
            pltpu.VMEM((2 * hidden, width), f32),
            pltpu.VMEM((2, 2, 2, rows, width), bf16),
            pltpu.VMEM((depth, 2, 2, rows, width), bf16),
            pltpu.VMEM((depth, 2, rows, width), bf16),
            pltpu.VMEM((depth - 1, 2, rows, width), bf16),
            pltpu.VMEM((places, 8, rows), f32),
            pltpu.VMEM((places, 8, rows), f32),
            dma((2, 2)),
            dma((2, 2 * depth)),
            dma((2, depth, 2)),
            dma((2, depth - 1, 2)),
            dma((2, places - 1)),
            dma,
        ],
        compiler_params=pltpu.CompilerParams(
            collective_id=2, has_side_effects=True, vmem_limit_bytes=60 * 1024 * 1024
        ),
        name="experts_by_links",
    )(rows_all, cots_all, code.reshape(ep_size, 2, 2, rows, -1), router, *weights)


class EpSum:
    def __init__(self, me, grads, y_got, z_got, final, sems):
        self.me, self.grads = me, grads
        self.y_got, self.z_got, self.final = y_got, z_got, final
        self.y_sems, self.z_sems, self.fz_sems, self.fy_sems = sems
        self.counts = [g.shape[2] for g in grads]
        self.starts = [sum(self.counts[:i]) for i in range(len(grads))]
        self.finals = []

    def y_copy(self, step, i):
        me = self.me
        return pltpu.make_async_remote_copy(
            src_ref=self.grads[i].at[me.after(step + 1), 1 - me.y],
            dst_ref=self.y_got.at[step, pl.ds(self.starts[i], self.counts[i])],
            send_sem=self.y_sems.at[0, step, i],
            recv_sem=self.y_sems.at[1, step, i],
            device_id=me.y_peer(),
            device_id_type=MESH,
        )

    def z_copy(self, step):
        return pltpu.make_async_remote_copy(
            src_ref=self.y_got.at[step],
            dst_ref=self.z_got.at[step],
            send_sem=self.z_sems.at[0, step],
            recv_sem=self.z_sems.at[1, step],
            device_id=self.me.device(z=self.me.after(step + 1)),
            device_id_type=MESH,
        )

    def begin(self):
        for step in range(self.me.depth):
            for i in range(len(self.grads)):
                self.y_copy(step, i).start()

    def fold(self, step):
        me = self.me
        for i in range(len(self.grads)):
            self.y_copy(step, i).wait_recv()
            add_into(
                self.y_got.at[step, pl.ds(self.starts[i], self.counts[i])],
                self.grads[i].at[me.after(step + 1), me.y],
            )
        if step < me.depth - 1:
            self.z_copy(step).start()

    def settle(self):
        me, depth = self.me, self.me.depth
        for step in range(depth - 1):
            self.z_copy(step).wait_recv()

        def tile(i, carry):
            at = pl.ds(pl.multiple_of(i * 16, 16), 16)
            value = self.y_got[depth - 1, at, :].astype(jnp.float32)
            for step in range(depth - 1):
                value = value + self.z_got[step, at, :].astype(jnp.float32)
            self.final[me.z, me.y, at, :] = value.astype(self.final.dtype)
            return carry

        lax.fori_loop(0, sum(self.counts) // 16, tile, 0)
        mine = self.final.at[me.z, me.y]
        for s in range(1, depth):
            self.spread(mine, self.fz_sems, s, me.device(z=me.after(s)))
        self.spread(mine, self.fy_sems, 0, me.y_peer())

    def spread(self, block, sems, slot, device):
        self.finals.append(send(block, block, sems.at[0, slot], sems.at[1, slot], device))

    def pass_on(self):
        me = self.me
        for s in range(1, me.depth):
            block = self.final.at[me.before(s), me.y]
            pltpu.make_async_copy(block, block, self.fz_sems.at[1, s]).wait()
            self.spread(block, self.fy_sems, s, me.y_peer())

    def finish(self):
        me = self.me
        for s in range(me.depth):
            block = self.final.at[me.before(s), 1 - me.y]
            pltpu.make_async_copy(block, block, self.fy_sems.at[1, s]).wait()

    def sent(self):
        for copy in self.finals:
            copy.wait_send()
        for step in range(self.me.depth):
            for i in range(len(self.grads)):
                self.y_copy(step, i).wait_send()
            if step < self.me.depth - 1:
                self.z_copy(step).wait_send()


def visible_columns(info_cols, info_rows):
    key_seg, key_pos = info_cols[:, 0:1], info_cols[:, 1:2]
    query_seg, query_pos = info_rows[0:1, :], info_rows[1:2, :]
    parent = jnp.where(query_seg >= 5, (query_seg - 5) // 2 + 1, -1)
    above = (key_seg == query_seg) | (key_seg == 0) | (key_seg == parent)
    return above & (key_pos <= query_pos)


class LinkGather:
    def __init__(self, me, own, out, sems):
        self.me, self.own, self.out = me, own, out
        self.own_sem, self.z_sems, self.y_sems, self.core_sems = sems
        self.begun = []
        depth = me.depth
        self.found = [(me.z, 0, None)]
        for d in range(1, depth):
            self.found.append((me.z - d, d, me.z >= d))
            self.found.append((me.z + d, depth - 1 + d, me.z + d < depth))

    def guard(self, *conditions):
        given = [c for c in conditions if c is not None]
        if not given:
            return lambda body: body()
        total = given[0]
        for c in given[1:]:
            total = total & c
        return pl.when(total)

    def go(self, source, place, sems, slot, device, *conditions):
        def copy():
            return pltpu.make_async_remote_copy(
                src_ref=source,
                dst_ref=place,
                send_sem=sems.at[0, slot],
                recv_sem=sems.at[1, slot],
                device_id=device,
                device_id_type=MESH,
            )

        self.guard(*conditions)(lambda: copy().start())
        self.begun.append((copy, conditions))

    def landed(self, place, sems, slot, condition):
        self.guard(condition)(
            lambda: pltpu.make_async_copy(place, place, sems.at[1, slot]).wait()
        )

    def up(self, source, place, d, condition):
        me = self.me
        device = me.device(z=lax.rem(me.z + 1, me.depth))
        self.go(source, place, self.z_sems, d, device, condition, me.z < me.depth - 1)

    def down(self, source, place, d, condition):
        me = self.me
        device = me.device(z=lax.rem(me.z + me.depth - 1, me.depth))
        self.go(source, place, self.z_sems, me.depth - 1 + d, device, condition, me.z > 0)

    def place(self, z, y, c):
        return self.out.at[lax.rem(z + self.me.depth, self.me.depth), y, c]

    def begin(self):
        me = self.me
        mine = self.place(me.z, me.y, me.c)
        self.up(self.own, mine, 1, None)
        self.down(self.own, mine, 1, None)
        self.go(self.own, mine, self.y_sems, 0, me.y_peer())
        self.go(self.own, mine, self.core_sems, 0, me.sibling())
        self.local = pltpu.make_async_copy(self.own, mine, self.own_sem)
        self.local.start()

    def relay(self, d):
        me = self.me
        for z, slot, condition in self.found[2 * d - 1 : 2 * d + 1]:
            block = self.place(z, me.y, me.c)
            self.landed(block, self.z_sems, slot, condition)
            if d < me.depth - 1:
                (self.up if slot < me.depth else self.down)(block, block, d + 1, condition)
            self.go(block, block, self.y_sems, slot, me.y_peer(), condition)
            self.go(block, block, self.core_sems, slot, me.sibling(), condition)

    def cross(self, first, last):
        me = self.me
        for z, slot, condition in self.found[first:last]:
            block = self.place(z, 1 - me.y, me.c)
            self.landed(block, self.y_sems, slot, condition)
            self.go(
                block, block, self.core_sems, 2 * me.depth - 1 + slot, me.sibling(), condition
            )

    def finish(self):
        me = self.me
        for z, slot, condition in self.found:
            for y, at in ((me.y, slot), (1 - me.y, 2 * me.depth - 1 + slot)):
                self.landed(self.place(z, y, 1 - me.c), self.core_sems, at, condition)
        self.local.wait()
        for copy, conditions in self.begun:
            self.guard(*conditions)(lambda: copy().wait_send())


def front_kernel(
    ep_size,
    heads,
    inputs,
    gain_one,
    gain_two,
    w_query,
    w_key,
    w_value,
    w_out,
    cosine,
    sine,
    info_cols,
    info_rows,
    table,
    cots,
    enter_near,
    leave_near,
    rows_out,
    queries,
    keys,
    values,
    heads_out,
    log_sums,
    middle,
    tables,
    cots_all,
    normed_all,
    normed_own,
    enter_far,
    leave_far,
    first_own,
    bias,
    parts,
    core_got,
    pair_got,
    own_sem,
    gather_sems,
    table_own_sem,
    table_sems,
    group_sems,
    far_sems,
    cots_sems,
    normed_sems,
):
    me = Place(ep_size)
    depth = me.depth
    f32, bf16 = jnp.float32, jnp.bfloat16
    share, width = inputs.shape
    tokens = 4 * share
    size = HEAD_DIMENSION
    groups = keys.shape[1] // size
    per_group = heads // groups
    scale = size ** (-0.5)
    ep, tp = lax.axis_index("ep"), lax.axis_index("tp")
    peers = [(lax.rem(ep + k, ep_size), tp) for k in range(1, ep_size)]
    meet([me.sibling(), me.x_peer()] + peers)

    def dot(a, b, contract):
        return lax.dot_general(
            a, b, ((contract[:1], contract[1:]), ((), ())), preferred_element_type=f32
        )

    cots_gather = LinkGather(me, cots, cots_all, cots_sems)
    cots_gather.begin()
    for i in range(share // 16):
        at = slice(i * 16, (i + 1) * 16)
        value = inputs[at, :].astype(f32)
        first_own[at, :] = (value * norm_scale(value) * gain_one[...]).astype(bf16)
    table_local = pltpu.make_async_copy(table, tables.at[ep], table_own_sem)
    table_local.start()
    table_copies = [
        send(table, tables.at[ep], table_sems.at[0, k], table_sems.at[1, k], device)
        for k, device in enumerate(peers)
    ]
    bias[...] = jnp.where(visible_columns(info_cols[...], info_rows[...]), 0.0, -1e30)
    log_sums[...] = jnp.zeros_like(log_sums)
    group_gather_body(me, 4, first_own, rows_out, own_sem, gather_sems)

    def to_peer(i):
        source, target = ((leave_near, leave_far), (enter_near, enter_far))[i]
        return send(source, target, far_sems.at[0, i], far_sems.at[1, i], me.x_peer())

    exchanged = [to_peer(0)]
    cots_gather.relay(1)
    rows = rows_out[...].reshape(tokens, width)

    def rotate(part):
        turned = jnp.concatenate([part[:, size // 2 :], part[:, : size // 2]], axis=1)
        return (part * cosine[...] - turned * sine[...]).astype(bf16)

    projected = dot(rows, w_query[...], (1, 1))
    for head in range(heads):
        mine = slice(head * size, (head + 1) * size)
        queries[:, mine] = rotate(projected[:, mine])
    projected = dot(rows, w_key[...], (1, 1))
    for group in range(groups):
        mine = slice(group * size, (group + 1) * size)
        keys[:, mine] = rotate(projected[:, mine])
    values[...] = dot(rows, w_value[...], (1, 1)).astype(bf16)
    for head in range(heads):
        mine = slice(head * size, (head + 1) * size)
        shared = slice(head // per_group * size, (head // per_group + 1) * size)
        scores = dot(keys[:, shared], queries[:, mine], (1, 1)) * scale + bias[...]
        top = jnp.max(scores, axis=0, keepdims=True)
        powers = jnp.exp(scores - top)
        total = jnp.sum(powers, axis=0, keepdims=True)
        log_sums[head : head + 1, :] = top + jnp.log(total)
        probs = (powers / total).astype(bf16)
        heads_out[:, mine] = dot(probs, values[:, shared], (0, 0)).astype(bf16)
        if head == 1:
            cots_gather.relay(2)
    tile = 512
    for n in range(width // tile):
        cols = slice(n * tile, (n + 1) * tile)
        sums = dot(heads_out[...], w_out[:, cols], (1, 0)).astype(bf16)
        parts[:, :, :, cols] = sums.reshape(2, 2, share, tile)
    group = GroupTotal(me, parts, core_got, pair_got, group_sems)
    group.begin()
    for step in range(3, depth):
        cots_gather.relay(step)
    group.exchange()
    exchanged.append(to_peer(1))
    cots_gather.cross(0, 3)

    def last(value, at):
        total = inputs[at, :].astype(f32) + value
        normed_own[at, :] = (total * norm_scale(total) * gain_two[...]).astype(bf16)
        return total

    group.finish(middle, last)
    normed_gather = LinkGather(me, normed_own, normed_all, normed_sems)
    normed_gather.begin()
    cots_gather.cross(3, 2 * depth - 1)
    for step in range(1, depth):
        normed_gather.relay(step)
    normed_gather.cross(0, 2 * depth - 1)
    cots_gather.finish()
    normed_gather.finish()
    group.sent()
    table_local.wait()
    for copy in table_copies + exchanged:
        copy.wait()


def token_tables(segment, position):
    cosine, sine = rope_tables(position, HEAD_DIMENSION)
    table = jnp.stack([segment, position])
    return (
        jnp.concatenate([cosine[:, 0], cosine[:, 0]], axis=1),
        jnp.concatenate([sine[:, 0], -sine[:, 0]], axis=1),
        jnp.pad(table.T, ((0, 0), (0, 126))),
        jnp.pad(table, ((0, 6), (0, 0))),
    )


def front_by_links(inputs, gains, projections, w_out, tables, order, cots, near, ep_size):
    share, width = inputs.shape
    depth = ep_size // 2
    tokens = 4 * share
    heads = w_out.shape[0] // HEAD_DIMENSION
    bf16, f32 = jnp.bfloat16, jnp.float32
    dma = pltpu.SemaphoreType.DMA
    vmem, anywhere = pl.BlockSpec(memory_space=pltpu.VMEM), pl.BlockSpec(memory_space=pltpu.HBM)

    def like(*shape, dtype=bf16):
        return jax.ShapeDtypeStruct(shape, dtype)

    def gather_sems():
        return (dma, dma((2, 2 * depth)), dma((2, 2 * depth)), dma((2, 4 * depth)))

    widths = [w.shape[0] for w in projections]
    everywhere = (depth, 2, 2, share, width)
    return pl.pallas_call(
        functools.partial(front_kernel, ep_size, heads),
        out_shape=(
            like(2, 2, share, width),
            like(tokens, widths[0]),
            like(tokens, widths[1]),
            like(tokens, widths[2]),
            like(tokens, widths[0]),
            like(8, tokens, dtype=f32),
            like(share, width, dtype=f32),
            like(ep_size, *order.shape, dtype=order.dtype),
            like(*everywhere),
            like(*everywhere),
            like(share, width),
            like(*near[0].shape),
            like(*near[1].shape),
        ),
        in_specs=[vmem] * 11 + [anywhere] * 4,
        out_specs=(vmem,) * 7 + (anywhere,) * 3 + (vmem,) + (anywhere,) * 2,
        scratch_shapes=[
            pltpu.VMEM((share, width), bf16),
            pltpu.VMEM((tokens, tokens), f32),
            pltpu.VMEM((2, 2, share, width), bf16),
            pltpu.VMEM((2, share, width), bf16),
            pltpu.VMEM((share, width), bf16),
            dma,
            dma((2, 12)),
            dma,
            dma((2, ep_size - 1)),
            dma((2, 3)),
            dma((2, 2)),
            gather_sems(),
            gather_sems(),
        ],
        compiler_params=pltpu.CompilerParams(
            collective_id=6, has_side_effects=True, vmem_limit_bytes=56 * 1024 * 1024
        ),
        name="front_by_links",
    )(
        inputs,
        gains[0][None, :],
        gains[1][None, :],
        *projections,
        w_out,
        *tables,
        order,
        cots,
        *near,
    )


def back_kernel(
    ep_size,
    heads,
    last_row,
    datt_own,
    heads_in,
    w_out,
    queries,
    keys,
    values,
    log_sums,
    info_cols,
    info_rows,
    cosine,
    sine,
    rows_in,
    w_query,
    w_key,
    w_value,
    small_in,
    gain,
    inputs,
    middle,
    gate_peer,
    up_peer,
    down_peer,
    first_final,
    second_final,
    out_final,
    grad_input,
    small_out,
    gate_got,
    up_got,
    down_got,
    datt,
    bias,
    grad_heads,
    grad_proj,
    key_sum,
    value_sum,
    part_query,
    part_key,
    part_value,
    part_out,
    y_got,
    z_got,
    y_got_out,
    z_got_out,
    parts,
    core_got,
    pair_got,
    small_src,
    small_got,
    small_sum,
    own_sem,
    gather_sems,
    y_sems,
    z_sems,
    fz_sems,
    fy_sems,
    y_sems_out,
    z_sems_out,
    fz_sems_out,
    fy_sems_out,
    group_sems,
    small_sems,
    spread_sems,
    own_small_sem,
    peer_sems,
):
    me = Place(ep_size)
    depth = me.depth
    f32, bf16 = jnp.float32, jnp.bfloat16
    others = all_others(ep_size)
    meet(others)
    my_place = lax.axis_index("ep") * 4 + lax.axis_index("tp")
    tokens, width = rows_in.shape
    share = datt_own.shape[0]
    size = HEAD_DIMENSION
    groups = keys.shape[1] // size
    per_group = heads // groups
    scale = size ** (-0.5)
    tile = 512

    def dot(a, b, contract):
        return lax.dot_general(
            a, b, ((contract[:1], contract[1:]), ((), ())), preferred_element_type=f32
        )

    bias[...] = jnp.where(visible_columns(info_cols[...], info_rows[...]), 0.0, -1e30)
    group_gather_body(me, 4, datt_own, datt, own_sem, gather_sems)

    def to_peer(i):
        source, target = ((gate_peer, gate_got), (up_peer, up_got), (down_peer, down_got))[i]
        return send(source, target, peer_sems.at[0, i], peer_sems.at[1, i], me.x_peer())

    exchanged = [to_peer(0)]
    for n in range(width // tile):
        cols = slice(n * tile, (n + 1) * tile)
        grads = dot(heads_in[...], datt[:, :, :, cols].reshape(tokens, tile), (0, 0))
        part_out[:, :, :, cols] = grads.astype(bf16).reshape(depth, 2, -1, tile)
    out_sum = EpSum(
        me,
        [part_out],
        y_got_out,
        z_got_out,
        out_final,
        (y_sems_out, z_sems_out, fz_sems_out, fy_sems_out),
    )
    out_sum.begin()
    for x in range(2):
        for c in range(2):
            at = pl.ds((x * 2 + c) * share, share)
            grad_heads[at, :] = dot(datt[x, c], w_out[...], (1, 1)).astype(bf16)

    def rotate_back_rows(grads):
        turned = jnp.concatenate([grads[:, size // 2 :], grads[:, : size // 2]], axis=1)
        return (grads * cosine[...] + turned * sine[...]).astype(bf16)

    for head in range(heads):
        group = head // per_group
        mine = slice(head * size, (head + 1) * size)
        shared = slice(group * size, (group + 1) * size)
        query, grad_head = queries[:, mine], grad_heads[:, mine]
        key, value = keys[:, shared], values[:, shared]
        scores = dot(key, query, (1, 1)) * scale + bias[...]
        probs = jnp.exp(scores - log_sums[head : head + 1, :])
        grad_probs = dot(value, grad_head, (1, 1))
        inner = jnp.sum(probs * grad_probs, axis=0, keepdims=True)
        grad_scores = (probs * (grad_probs - inner)).astype(bf16)
        grad_value = dot(probs.astype(bf16), grad_head, (1, 0))
        grad_key = dot(grad_scores, query, (1, 0)) * scale
        if head % per_group:
            grad_value = grad_value + value_sum[...]
            grad_key = grad_key + key_sum[...]
        value_sum[...] = grad_value
        key_sum[...] = grad_key
        grad_query = dot(grad_scores, key, (0, 0)) * scale
        grad_proj[:, mine] = rotate_back_rows(grad_query)
        if head % per_group == per_group - 1:
            at = heads * size + group * size
            grad_proj[:, at : at + size] = rotate_back_rows(grad_key)
            at += groups * size
            grad_proj[:, at : at + size] = grad_value.astype(bf16)
        if 1 <= head <= depth:
            out_sum.fold(head - 1)
    for step in range(max(heads - 1, 0), depth):
        out_sum.fold(step)

    ends = (heads * size, (heads + groups) * size, (heads + 2 * groups) * size)
    wide = width // 2
    sums = []
    for n, final in enumerate((first_final, second_final)):
        cols = slice(n * wide, (n + 1) * wide)
        grads = dot(grad_proj[...], rows_in[:, cols], (0, 0)).astype(bf16)
        part_query[n] = grads[: ends[0]].reshape(depth, 2, -1, wide)
        part_key[n] = grads[ends[0] : ends[1]].reshape(depth, 2, -1, wide)
        part_value[n] = grads[ends[1] :].reshape(depth, 2, -1, wide)
        sums.append(
            EpSum(
                me,
                [part_query.at[n], part_key.at[n], part_value.at[n]],
                y_got.at[n],
                z_got.at[n],
                final,
                (y_sems.at[n], z_sems.at[n], fz_sems.at[n], fy_sems.at[n]),
            )
        )
        sums[n].begin()
        if n == 0:
            out_sum.settle()
    first_sum, second_sum = sums
    small_src[...] = small_in[...]
    for n in range(width // tile):
        cols = slice(n * tile, (n + 1) * tile)
        grads = (
            dot(grad_proj[:, : ends[0]], w_query[:, cols], (1, 0))
            + dot(grad_proj[:, ends[0] : ends[1]], w_key[:, cols], (1, 0))
            + dot(grad_proj[:, ends[1] :], w_value[:, cols], (1, 0))
        )
        parts[:, :, :, cols] = grads.astype(bf16).reshape(2, 2, share, tile)
        gained = jnp.sum(grads * rows_in[:, cols].astype(f32), axis=0, keepdims=True)
        gained = gained / gain[:, cols]
        for k in range(tile // 128):
            row = n * (tile // 128) + k
            small_src[last_row, row : row + 1, :] = gained[:, k * 128 : (k + 1) * 128]
        first_sum.fold(n)
    for step in range(width // tile, depth):
        first_sum.fold(step)
    group = GroupTotal(me, parts, core_got, pair_got, group_sems)
    group.begin()
    second_sum.fold(0)
    group.exchange()
    exchanged += [to_peer(1), to_peer(2)]
    out_sum.pass_on()
    second_sum.fold(1)
    small = [
        send(
            small_src.at[device[0] * 4 + device[1]],
            small_got.at[my_place],
            small_sems.at[0, k],
            small_sems.at[1, k],
            device,
        )
        for k, device in enumerate(others)
    ]
    own_small = pltpu.make_async_copy(
        small_src.at[my_place], small_got.at[my_place], own_small_sem
    )
    own_small.start()
    for step in range(2, depth):
        second_sum.fold(step)
    first_sum.settle()

    def last(value, at):
        values_own = inputs[at, :].astype(f32)
        factor = norm_scale(values_own)
        return middle[at, :] + norm_back(values_own, factor, gain[...], value)

    group.finish(grad_input, last)
    second_sum.settle()
    own_small.wait()
    for copy in small:
        copy.wait_recv()
    total = small_got[0]
    for k in range(1, 4 * ep_size):
        total = total + small_got[k]
    small_sum[...] = total
    spread = [
        send(
            small_sum,
            small_out.at[my_place],
            spread_sems.at[0, k],
            spread_sems.at[1, k],
            device,
        )
        for k, device in enumerate(others)
    ]
    small_out[my_place] = total
    first_sum.pass_on()
    out_sum.finish()
    second_sum.pass_on()
    first_sum.finish()
    second_sum.finish()
    for copy in spread:
        copy.wait()
    for copy in small:
        copy.wait_send()
    group.sent()
    for each in [out_sum] + sums:
        each.sent()
    for copy in exchanged:
        copy.wait()


def back_by_links(
    datt_own,
    heads_in,
    w_out,
    queries,
    keys,
    values,
    log_sums,
    tables,
    rows_in,
    w_query,
    w_key,
    w_value,
    small,
    gain,
    inputs,
    middle,
    peers,
    ep_size,
):
    tokens, width = rows_in.shape
    share = datt_own.shape[0]
    depth = ep_size // 2
    heads = queries.shape[1] // HEAD_DIMENSION
    places = 4 * ep_size
    bf16, f32 = jnp.bfloat16, jnp.float32
    dma = pltpu.SemaphoreType.DMA
    vmem = pl.BlockSpec(memory_space=pltpu.VMEM)
    anywhere = pl.BlockSpec(memory_space=pltpu.HBM)
    cosine, sine, info_cols, info_rows = tables
    blocks = jnp.pad(small, ((0, places - small.shape[0]), (0, 0))).reshape(places, -1, 128)
    sizes = [w.shape[0] // ep_size for w in (w_query, w_key, w_value, w_out)]
    total = sum(sizes[:3])

    def partial(rows, columns):
        return (depth, 2, rows, columns), bf16

    wide = width // 2
    got = pl.pallas_call(
        functools.partial(back_kernel, ep_size, heads, small.shape[0]),
        out_shape=(
            jax.ShapeDtypeStruct(*partial(total, wide)),
            jax.ShapeDtypeStruct(*partial(total, wide)),
            jax.ShapeDtypeStruct(*partial(sizes[3], width)),
            jax.ShapeDtypeStruct((share, width), f32),
            jax.ShapeDtypeStruct(blocks.shape, f32),
        )
        + tuple(jax.ShapeDtypeStruct(p.shape, p.dtype) for p in peers),
        in_specs=[vmem] * 19 + [anywhere] * 3,
        out_specs=(vmem,) * 5 + (anywhere,) * 3,
        scratch_shapes=[
            pltpu.VMEM((2, 2, share, width), bf16),
            pltpu.VMEM((tokens, tokens), f32),
            pltpu.VMEM(queries.shape, bf16),
            pltpu.VMEM((tokens, queries.shape[1] + 2 * keys.shape[1]), bf16),
            pltpu.VMEM((tokens, HEAD_DIMENSION), f32),
            pltpu.VMEM((tokens, HEAD_DIMENSION), f32),
        ]
        + [pltpu.VMEM((2, depth, 2, k, wide), bf16) for k in sizes[:3]]
        + [
            pltpu.VMEM((depth, 2, sizes[3], width), bf16),
            pltpu.VMEM((2, depth, total, wide), bf16),
            pltpu.VMEM((2, depth - 1, total, wide), bf16),
            pltpu.VMEM((depth, sizes[3], width), bf16),
            pltpu.VMEM((depth - 1, sizes[3], width), bf16),
            pltpu.VMEM((2, 2, share, width), bf16),
            pltpu.VMEM((2, share, width), bf16),
            pltpu.VMEM((share, width), bf16),
            pltpu.VMEM(blocks.shape, f32),
            pltpu.VMEM(blocks.shape, f32),
            pltpu.VMEM(blocks.shape[1:], f32),
            dma,
            dma((2, 12)),
        ]
        + [dma((2, 2, depth, 3))]
        + [dma((2, 2, depth))] * 3
        + [dma((2, depth, 1))]
        + [dma((2, depth))] * 3
        + [dma((2, 3)), dma((2, places - 1)), dma((2, places - 1)), dma, dma((2, 3))],
        compiler_params=pltpu.CompilerParams(
            collective_id=5, has_side_effects=True, vmem_limit_bytes=60 * 1024 * 1024
        ),
        name="back_by_links",
    )(
        datt_own,
        heads_in,
        w_out,
        queries,
        keys,
        values,
        log_sums,
        info_cols,
        info_rows,
        cosine,
        sine,
        rows_in,
        w_query,
        w_key,
        w_value,
        blocks,
        gain[None, :],
        inputs,
        middle,
        *peers,
    )
    return got


def deliver_kernel(
    ep_size,
    sizes,
    rows_in,
    sums_in,
    gate_in,
    up_in,
    down_in,
    gate_got,
    up_got,
    down_got,
    first_in,
    second_in,
    third_in,
    small,
    gate_out,
    up_out,
    down_out,
    rows_out,
    sums_out,
    query_out,
    key_out,
    value_out,
    out_out,
    router_out,
    first_gain,
    second_gain,
    query,
    key,
    value,
    out,
    gate,
    up,
    down,
    gate_far,
    up_far,
    down_far,
    first,
    second,
    third,
    sems,
    load_sems,
):
    pairs = ((rows_in, rows_out), (sums_in, sums_out))
    loads = [
        pltpu.make_async_copy(source, target, load_sems.at[i])
        for i, (source, target) in enumerate(
            (
                (third_in, third),
                (first_in, first),
                (second_in, second),
                (gate_in, gate),
                (gate_got, gate_far),
                (up_in, up),
                (up_got, up_far),
                (down_in, down),
                (down_got, down_far),
            )
        )
    ]
    for load in loads:
        load.start()
    copies = [
        pltpu.make_async_copy(source, target, sems.at[i]) for i, (source, target) in enumerate(pairs)
    ]
    for copy in copies:
        copy.start()
    wide = first.shape[2]
    f32 = jnp.float32

    def leave(source, target, i):
        copies.append(pltpu.make_async_copy(source, target, sems.at[i]))
        copies[-1].start()

    loads[0].wait()
    out[...] = third[...].astype(f32)
    leave(out, out_out, 5)
    for load in loads[1:3]:
        load.wait()
    at = 0
    for i, (source, target) in enumerate(((query, query_out), (key, key_out), (value, value_out))):
        for n, part in enumerate((first, second)):
            source[:, :, n * wide : (n + 1) * wide] = part[:, at : at + sizes[i], :].astype(f32)
        at += sizes[i]
        leave(source, target, 6 + i)
    for i, (total, far) in enumerate(((gate, gate_far), (up, up_far), (down, down_far))):
        for load in loads[3 + 2 * i : 5 + 2 * i]:
            load.wait()
        total[...] = total[...] + far[...].astype(f32)
        leave(total, (gate_out, up_out, down_out)[i], 2 + i)
    experts = router_out.shape[0]
    for j in range(small.shape[1]):
        cols = slice(j * 128, (j + 1) * 128)
        router_out[:, cols] = small[:experts, j, :]
        first_gain[:, cols] = small[experts + 1 : experts + 2, j, :]
        second_gain[:, cols] = small[experts : experts + 1, j, :]
    for copy in copies:
        copy.wait()


def deliver(owned, peers, rows, sums, got, small, sizes, expert_count, ep_size):
    width = rows.shape[1]
    f32 = jnp.float32
    vmem, anywhere = pl.BlockSpec(memory_space=pltpu.VMEM), pl.BlockSpec(memory_space=pltpu.HBM)
    first, second, third = (g.reshape((ep_size,) + g.shape[2:]) for g in got)

    def like(value):
        return jax.ShapeDtypeStruct(value.shape, value.dtype)

    shapes = [(ep_size, k, width) for k in sizes]
    results = pl.pallas_call(
        functools.partial(deliver_kernel, ep_size, sizes),
        out_shape=tuple(like(a) for a in owned)
        + (like(rows), like(sums))
        + tuple(jax.ShapeDtypeStruct(shape, f32) for shape in shapes)
        + (
            jax.ShapeDtypeStruct((expert_count, width), f32),
            jax.ShapeDtypeStruct((1, width), f32),
            jax.ShapeDtypeStruct((1, width), f32),
        ),
        in_specs=[anywhere] * 11 + [vmem],
        out_specs=(anywhere,) * 9 + (vmem,) * 3,
        scratch_shapes=[pltpu.VMEM(shape, f32) for shape in shapes]
        + [pltpu.VMEM(a.shape, a.dtype) for a in (*owned, *peers, first, second, third)]
        + [pltpu.SemaphoreType.DMA((9,))] * 2,
        compiler_params=pltpu.CompilerParams(vmem_limit_bytes=40 * 1024 * 1024),
        name="deliver",
    )(rows, sums, *owned, *peers, first, second, third, small)
    gate, up, down, rows, sums = results[:5]
    query, key, value, out = (g.reshape(-1, width) for g in results[5:9])
    router, first_gain, second_gain = results[9:]
    return (
        sums,
        rows,
        first_gain[0],
        query,
        key,
        value,
        out,
        second_gain[0],
        router,
        gate,
        up,
        down.reshape(gate.shape[0], -1, width),
    )


def group_rows(value_rows):
    return lax.all_gather(value_rows, "tp", axis=0, tiled=True)


def group_totals(value_rows):
    return lax.psum_scatter(value_rows, "tp", scatter_dimension=0, tiled=True).astype(jnp.float32)


def gather_all(value_rows):
    return lax.all_gather(value_rows, ("ep", "tp"), axis=0, tiled=True)


LAST = 1 << 30


def pair_order(expert_ids, slot_order, expert_count):
    experts = jnp.arange(expert_count, dtype=jnp.int32)
    chosen = expert_ids.T[None, :, :] == experts[:, None, None]
    return jnp.min(jnp.where(chosen, slot_order.T[None, :, :], LAST), axis=1)


def kept_pairs(order):
    used = order < LAST
    counts = jnp.sum(used.astype(jnp.int32), axis=2)
    block = jnp.arange(order.shape[0], dtype=jnp.int32)
    earlier = block[None, :] < block[:, None]
    offsets = jnp.sum(jnp.where(earlier[:, :, None], counts[None, :, :], 0), axis=1)
    whole = offsets + counts <= CAP
    edge = (offsets < CAP) & ~whole
    edge_order = jnp.sum(jnp.where(edge[:, :, None], order, 0), axis=0)
    rank = jnp.sum((edge_order[:, :, None] < edge_order[:, None, :]).astype(jnp.int32), axis=1)
    early = offsets[:, :, None] + rank[None, :, :] < CAP
    return used & (whole[:, :, None] | (edge[:, :, None] & early))


def masked_softmax(logits, used):
    top = jnp.max(jnp.where(used, logits, -1e30), axis=-1, keepdims=True)
    powers = jnp.where(used, jnp.exp(logits - top), 0.0)
    return powers / jnp.sum(powers, axis=-1, keepdims=True)


def pair_codes(order_all, per_owner):
    expert_count = order_all.shape[1]
    first = lax.axis_index("ep") * per_owner
    turned = jnp.roll(order_all, -first, axis=1)
    kept = kept_pairs(turned[:, :per_owner])
    dropped = jnp.pad(~kept, ((0, 0), (0, expert_count - per_owner), (0, 0)))
    code = jnp.where(turned < LAST, dropped.astype(jnp.float32), -1.0)
    code = code.swapaxes(1, 2).reshape(-1, expert_count)
    lanes = -expert_count % 128
    return jnp.pad(code, ((0, 0), (0, lanes)), constant_values=-1.0).astype(jnp.bfloat16)


def expert_weights(w_gate, w_up, w_down):
    enter = jnp.concatenate([w[e] for w in (w_gate, w_up) for e in range(w.shape[0])], axis=1)
    return enter, w_down.reshape(-1, w_down.shape[2])


def run_experts(rows_all, cots_all, code, w_router, w_gate, w_up, w_down, weights, by_links):
    per_owner, width, units = w_gate.shape
    expert_count = w_router.shape[0]
    ep_size, tp_size = lax.axis_size("ep"), lax.axis_size("tp")
    hidden = per_owner * units
    router = jnp.roll(w_router, -lax.axis_index("ep") * per_owner, axis=0)
    router = jnp.pad(router, ((0, -expert_count % 128), (0, 0)))
    if by_links:
        grads, sums, small, *owned = experts_by_links(
            rows_all, cots_all, code, router, weights, per_owner, ep_size
        )
        share = grads.shape[0]
        return (
            grads,
            sums,
            small[:, :per_owner].reshape(expert_count, share).T,
            owned[:3],
            owned[3:],
        )
    enter, leave = expert_weights(w_gate, w_up, w_down)
    used, kept = code >= 0, (code == 0).astype(jnp.float32)
    logits = jnp.einsum("rd,ed->re", rows_all, router, preferred_element_type=jnp.float32)
    gates = jnp.repeat((kept * masked_softmax(logits, used))[:, :per_owner], units, axis=1)
    act = jnp.dot(rows_all, enter, preferred_element_type=jnp.float32)
    gate_act, up_act = act[:, :hidden], act[:, hidden:]
    back_act = jnp.einsum("rd,fd->rf", cots_all, leave, preferred_element_type=jnp.float32)
    sigma = jax.nn.sigmoid(gate_act)
    value = gate_act * sigma * up_act
    weighted = (gates * value).astype(jnp.bfloat16)
    grad_hidden = gates * back_act
    turned = jnp.concatenate(
        [
            grad_hidden * up_act * sigma * (1.0 + gate_act * (1.0 - sigma)),
            grad_hidden * gate_act * sigma,
        ],
        axis=1,
    ).astype(jnp.bfloat16)
    small = kept[:, :per_owner] * jnp.sum((value * back_act).reshape(-1, per_owner, units), axis=2)
    grads = jnp.einsum("rf,df->rd", turned, enter, preferred_element_type=jnp.float32)
    sums = jnp.dot(weighted, leave, preferred_element_type=jnp.float32)

    def scatter(value_rows):
        return lax.psum_scatter(value_rows, ("ep", "tp"), scatter_dimension=0, tiled=True)

    columns = lax.dynamic_update_slice_in_dim(
        jnp.zeros((small.shape[0], expert_count), jnp.float32),
        small,
        lax.axis_index("ep") * per_owner,
        1,
    )
    both = jnp.einsum(
        "rd,rwef->wedf",
        rows_all,
        turned.reshape(-1, 2, per_owner, units),
        preferred_element_type=jnp.float32,
    )
    down = jnp.einsum("rf,rd->fd", weighted, cots_all, preferred_element_type=jnp.float32)
    return (
        scatter(grads.astype(jnp.bfloat16)).astype(jnp.float32),
        scatter(sums.astype(jnp.bfloat16)).astype(jnp.float32),
        scatter(columns),
        (both[0], both[1], down),
        None,
    )


def visible_block(query_seg, query_pos, query_row, key_seg, key_pos, key_row):
    seg_q = query_seg[:, None]
    seg_k = key_seg[None, :]
    above = (
        (seg_k == seg_q)
        | (seg_k == 0)
        | (seg_k >= 1) & (seg_k <= 4) & (seg_q >= 5) & ((seg_q - 5) // 2 + 1 == seg_k)
    )
    same_tree = query_row[:, None] // TREE_TOKENS == key_row[None, :] // TREE_TOKENS
    return above & same_tree & (key_pos[None, :] <= query_pos[:, None])


def block_scores(query_part, key_rows, allowed, scale):
    scores = (
        jnp.einsum("qkgd,pkd->kgqp", query_part, key_rows, preferred_element_type=jnp.float32)
        * scale
    )
    return jnp.where(allowed[None, None], scores, -1e30)


def attend_forward(query_rows, key_rows, value_rows, segment, position):
    total_rows = query_rows.shape[0]
    scale = query_rows.shape[-1] ** (-0.5)
    row_ids = jnp.arange(total_rows, dtype=jnp.int32)
    allowed = visible_block(segment, position, row_ids, segment, position, row_ids)
    scores = block_scores(query_rows, key_rows, allowed, scale)
    top_score = jnp.max(scores, axis=-1, keepdims=True)
    weights = jnp.exp(scores - top_score)
    weight_sum = jnp.sum(weights, axis=-1, keepdims=True)
    probs = (weights / weight_sum).astype(jnp.bfloat16)
    outputs = jnp.einsum(
        "kgqp,pkd->qkgd", probs, value_rows, preferred_element_type=jnp.float32
    ).astype(jnp.bfloat16)
    log_sums = [top_score + jnp.log(weight_sum)]
    return (outputs, log_sums)


def attend_backward(
    query_rows, key_rows, value_rows, segment, position, log_sums, grad_heads, block_rows
):
    total_rows = query_rows.shape[0]
    scale = query_rows.shape[-1] ** (-0.5)
    row_ids = jnp.arange(total_rows, dtype=jnp.int32)
    grad_keys = jnp.zeros(key_rows.shape, jnp.float32)
    grad_values = jnp.zeros(value_rows.shape, jnp.float32)
    grad_query = []
    for number, first_row in enumerate(range(0, total_rows, block_rows)):
        allowed = visible_block(segment, position, row_ids, segment, position, row_ids)
        scores = block_scores(query_rows, key_rows, allowed, scale)
        probs = jnp.where(allowed[None, None], jnp.exp(scores - log_sums[number]), 0.0)
        grad_values = jnp.einsum(
            "kgqp,qkgd->pkd",
            probs.astype(jnp.bfloat16),
            grad_heads,
            preferred_element_type=jnp.float32,
        )
        grad_probs = jnp.einsum(
            "qkgd,pkd->kgqp", grad_heads, value_rows, preferred_element_type=jnp.float32
        )
        inner = jnp.sum(probs * grad_probs, axis=-1, keepdims=True)
        grad_scores = (probs * (grad_probs - inner)).astype(jnp.bfloat16)
        grad_query.append(
            jnp.einsum("kgqp,pkd->qkgd", grad_scores, key_rows, preferred_element_type=jnp.float32)
            * scale
        )
        grad_keys = (
            jnp.einsum(
                "kgqp,qkgd->pkd", grad_scores, query_rows, preferred_element_type=jnp.float32
            )
            * scale
        )
    return (grad_query[0], grad_keys, grad_values)


def local(
    hidden_in,
    gain_attn,
    w_query,
    key_projection_weight,
    value_projection_weight,
    w_out,
    gain_ffn,
    w_router,
    w_gate,
    w_up,
    w_down,
    expert_ids,
    slot_order,
    segment,
    position,
    cotangent,
):
    model_width = w_query.shape[1]
    head_width = HEAD_DIMENSION
    local_heads = w_query.shape[0] // head_width
    local_kv = key_projection_weight.shape[0] // head_width
    group_factor = local_heads // local_kv
    token_count = expert_ids.shape[0]
    share = hidden_in.shape[0]
    row_start = lax.axis_index("tp") * share
    expert_count = w_router.shape[0]
    per_owner = w_gate.shape[0]
    block_rows = 512
    by_links = lax.axis_size("tp") == 4 and lax.axis_size("ep") == 8
    order = pair_order(expert_ids, slot_order, expert_count)
    gain_one = gain_attn.astype(jnp.float32)
    gain_two = gain_ffn.astype(jnp.float32)
    inputs_own = hidden_in.astype(jnp.float32)
    if by_links:
        near = expert_weights(w_gate, w_up, w_down)
        token_info = token_tables(segment, position)
        (
            first_normalized,
            query_rows,
            key_rows,
            value_rows,
            head_outputs,
            log_sums,
            middle_own,
            order_all,
            cot_all,
            normed_two,
            normed_own,
            *far,
        ) = front_by_links(
            hidden_in,
            (gain_one, gain_two),
            (w_query, key_projection_weight, value_projection_weight),
            w_out,
            token_info,
            order,
            cotangent,
            near,
            lax.axis_size("ep"),
        )
        weights = (near[0], far[0], near[1], far[1])
        scale_two = norm_scale(middle_own)
    else:
        weights = None
        scale_one = norm_scale(inputs_own)
        first_normalized = group_rows((inputs_own * scale_one * gain_one).astype(jnp.bfloat16))
        order_all = lax.all_gather(order, "ep")
        cosine_lookup, sine_lookup = rope_tables(position, head_width)
        query_proj = jnp.einsum(
            "rd,fd->rf", first_normalized, w_query, preferred_element_type=jnp.float32
        ).reshape(token_count, local_heads, head_width)
        key_proj = jnp.einsum(
            "rd,fd->rf", first_normalized, key_projection_weight, preferred_element_type=jnp.float32
        ).reshape(token_count, local_kv, head_width)
        query_rows = (
            apply_rotation(query_proj, cosine_lookup, sine_lookup)
            .astype(jnp.bfloat16)
            .reshape(token_count, local_kv, group_factor, head_width)
        )
        key_rows = apply_rotation(key_proj, cosine_lookup, sine_lookup).astype(jnp.bfloat16)
        value_rows = (
            jnp.einsum(
                "rd,fd->rf",
                first_normalized,
                value_projection_weight,
                preferred_element_type=jnp.float32,
            )
            .astype(jnp.bfloat16)
            .reshape(token_count, local_kv, head_width)
        )
        head_outputs, log_sums = attend_forward(query_rows, key_rows, value_rows, segment, position)
        head_outputs = head_outputs.reshape(token_count, local_heads * head_width)
        middle_own = inputs_own + group_totals(
            jnp.dot(head_outputs, w_out, preferred_element_type=jnp.float32).astype(jnp.bfloat16)
        )
        scale_two = norm_scale(middle_own)
        normed_own = (middle_own * scale_two * gain_two).astype(jnp.bfloat16)
        normed_two, cot_all = gather_all(normed_own), gather_all(cotangent)
    code = pair_codes(order_all, per_owner)
    used = lax.dynamic_slice_in_dim(order, row_start, share, 1).T < LAST
    gates = masked_softmax(
        jnp.einsum("rd,ed->re", normed_own, w_router, preferred_element_type=jnp.float32), used
    )
    grad_normed_own, combined_own, grad_gates_own, owned, peers = run_experts(
        normed_two, cot_all, code, w_router, w_gate, w_up, w_down, weights, by_links
    )
    output_own = (middle_own + combined_own).astype(jnp.bfloat16)
    inner_gate = jnp.sum(gates * grad_gates_own, axis=-1, keepdims=True)
    grad_logits = gates * (grad_gates_own - inner_gate)
    router_f = w_router.astype(jnp.float32)
    grad_normed_own = grad_normed_own + jnp.dot(grad_logits, router_f, precision=EXACT_PRECISION)
    grad_router = jnp.dot(grad_logits.T, normed_own.astype(jnp.float32), precision=EXACT_PRECISION)
    grad_gain_ffn = jnp.sum(grad_normed_own * middle_own * scale_two, axis=0)
    grad_middle = cotangent.astype(jnp.float32) + norm_back(
        middle_own, scale_two, gain_two, grad_normed_own
    )
    if by_links:
        *got, grad_input, small, gate_got, up_got, down_got = back_by_links(
            grad_middle.astype(jnp.bfloat16),
            head_outputs,
            w_out,
            query_rows,
            key_rows,
            value_rows,
            log_sums,
            token_info,
            first_normalized.reshape(token_count, model_width),
            w_query,
            key_projection_weight,
            value_projection_weight,
            jnp.concatenate([grad_router, grad_gain_ffn[None, :]], axis=0),
            gain_one,
            hidden_in,
            grad_middle,
            peers,
            lax.axis_size("ep"),
        )
        ep_size = lax.axis_size("ep")
        weights = (w_query, key_projection_weight, value_projection_weight, w_out)
        return deliver(
            owned,
            (gate_got, up_got, down_got),
            grad_input,
            output_own,
            got,
            small,
            [w.shape[0] // ep_size for w in weights],
            expert_count,
            ep_size,
        )
    grad_attn = group_rows(grad_middle.astype(jnp.bfloat16))
    grad_w_out = jnp.einsum(
        "rf,rd->fd", head_outputs, grad_attn, preferred_element_type=jnp.float32
    )
    grad_w_out = lax.psum(grad_w_out.astype(jnp.bfloat16), "ep").astype(jnp.float32)
    grad_heads = (
        jnp.einsum("rd,fd->rf", grad_attn, w_out, preferred_element_type=jnp.float32)
        .astype(jnp.bfloat16)
        .reshape(token_count, local_kv, group_factor, head_width)
    )
    grad_query, grad_keys, grad_values = attend_backward(
        query_rows, key_rows, value_rows, segment, position, log_sums, grad_heads, block_rows
    )
    grad_query_proj = (
        rotate_back(
            grad_query.reshape(token_count, local_heads, head_width), cosine_lookup, sine_lookup
        )
        .astype(jnp.bfloat16)
        .reshape(token_count, local_heads * head_width)
    )
    grad_key_proj = (
        rotate_back(grad_keys, cosine_lookup, sine_lookup)
        .astype(jnp.bfloat16)
        .reshape(token_count, local_kv * head_width)
    )
    grad_value_proj = grad_values.astype(jnp.bfloat16).reshape(token_count, local_kv * head_width)
    grad_w_query = jnp.einsum(
        "rf,rd->fd", grad_query_proj, first_normalized, preferred_element_type=jnp.float32
    )
    grad_w_key = jnp.einsum(
        "rf,rd->fd", grad_key_proj, first_normalized, preferred_element_type=jnp.float32
    )
    grad_w_value = jnp.einsum(
        "rf,rd->fd", grad_value_proj, first_normalized, preferred_element_type=jnp.float32
    )
    grad_normed_one = jnp.einsum(
        "rf,fd->rd", grad_query_proj, w_query, preferred_element_type=jnp.float32
    )
    grad_normed_one = grad_normed_one + jnp.einsum(
        "rf,fd->rd", grad_key_proj, key_projection_weight, preferred_element_type=jnp.float32
    )
    grad_normed_one = grad_normed_one + jnp.einsum(
        "rf,fd->rd", grad_value_proj, value_projection_weight, preferred_element_type=jnp.float32
    )
    grad_gain_attn = jnp.sum(grad_normed_one * first_normalized.astype(jnp.float32), axis=0)
    small = jnp.concatenate(
        [grad_router, grad_gain_ffn[None, :], (grad_gain_attn / gain_one)[None, :]], axis=0
    )
    grad_w_query, grad_w_key, grad_w_value = (
        lax.psum(g.astype(jnp.bfloat16), "ep").astype(jnp.float32)
        for g in (grad_w_query, grad_w_key, grad_w_value)
    )
    grad_one_own = group_totals(grad_normed_one.astype(jnp.bfloat16))
    small = lax.psum(small, ("ep", "tp"))
    grad_input = grad_middle + norm_back(inputs_own, scale_one, gain_one, grad_one_own)
    grad_router = small[:expert_count]
    grad_gain_ffn, grad_gain_attn = small[expert_count], small[expert_count + 1]
    return (
        output_own,
        grad_input,
        grad_gain_attn,
        grad_w_query,
        grad_w_key,
        grad_w_value,
        grad_w_out,
        grad_gain_ffn,
        grad_router,
        owned[0],
        owned[1],
        owned[2].reshape(w_down.shape),
    )


def solution(mesh):
    placed = (
        P(("ep", "tp"), None),
        P(),
        P("tp", None),
        P("tp", None),
        P("tp", None),
        P("tp", None),
        P(),
        P(),
        P("ep", None, "tp"),
        P("ep", None, "tp"),
        P("ep", "tp", None),
        P("ep", None),
        P("ep", None),
        P("ep"),
        P("ep"),
        P(("ep", "tp"), None),
    )
    return jax.shard_map(
        local,
        mesh=mesh,
        in_specs=placed,
        out_specs=(
            P(("ep", "tp"), None),
            P(("ep", "tp"), None),
            P(),
            P("tp", None),
            P("tp", None),
            P("tp", None),
            P("tp", None),
            P(),
            P(),
            P("ep", None, "tp"),
            P("ep", None, "tp"),
            P("ep", "tp", None),
        ),
        check_vma=False,
    )
```

```python
import functools

import jax
import jax.numpy as jnp
from jax import lax
from jax.experimental import pallas as pl
from jax.experimental.pallas import tpu as pltpu
from jax.sharding import PartitionSpec as P

HEAD_DIMENSION = 64
TREE_TOKENS = 512
CAP = 2304


EPSILON = 1e-06
ROPE_BASE = 10000.0
EXACT_PRECISION = lax.Precision.HIGHEST


def rope_tables(position, head_width):
    half_width = head_width // 2
    freqs = ROPE_BASE ** (-(jnp.arange(half_width, dtype=jnp.float32) * 2.0 / head_width))
    angle = position.astype(jnp.float32)[:, None] * freqs[None, :]
    return (jnp.cos(angle)[:, None, :], jnp.sin(angle)[:, None, :])


def apply_rotation(value_rows, cosine_lookup, sine_lookup):
    half_width = value_rows.shape[-1] // 2
    first = value_rows[..., :half_width]
    second = value_rows[..., half_width:]
    return jnp.concatenate(
        [
            first * cosine_lookup - second * sine_lookup,
            first * sine_lookup + second * cosine_lookup,
        ],
        axis=-1,
    )


def rotate_back(grads, cosine_lookup, sine_lookup):
    half_width = grads.shape[-1] // 2
    first = grads[..., :half_width]
    second = grads[..., half_width:]
    return jnp.concatenate(
        [
            first * cosine_lookup + second * sine_lookup,
            second * cosine_lookup - first * sine_lookup,
        ],
        axis=-1,
    )


def norm_scale(value_rows):
    return lax.rsqrt(jnp.mean(value_rows * value_rows, axis=-1, keepdims=True) + EPSILON)


def norm_back(value_rows, scale, gain, grad_normed):
    weighted = grad_normed * gain
    inner = jnp.mean(value_rows * weighted, axis=-1, keepdims=True)
    grad_values = scale * weighted - value_rows * (scale * scale * scale) * inner
    return grad_values


MESH = pl.DeviceIdType.MESH


class Place:
    def __init__(self, ep_size):
        self.depth = ep_size // 2
        ep, tp = lax.axis_index("ep"), lax.axis_index("tp")
        self.z, self.y = ep // 2, ep % 2
        self.x, self.c = tp // 2, tp % 2

    def device(self, z=None, y=None, x=None, c=None):
        z = self.z if z is None else z
        y = self.y if y is None else y
        x = self.x if x is None else x
        c = self.c if c is None else c
        return (z * 2 + y, x * 2 + c)

    def sibling(self):
        return self.device(c=1 - self.c)

    def x_peer(self):
        return self.device(x=1 - self.x)

    def y_peer(self):
        return self.device(y=1 - self.y)

    def after(self, step):
        return lax.rem(self.z + step, self.depth)

    def before(self, step):
        return lax.rem(self.z + self.depth - step, self.depth)


def meet(devices):
    barrier = pltpu.get_barrier_semaphore()
    for device in devices:
        pl.semaphore_signal(barrier, inc=1, device_id=device, device_id_type=MESH)
    pl.semaphore_wait(barrier, len(devices))


def send(src, dst, send_sem, recv_sem, device):
    copy = pltpu.make_async_remote_copy(
        src_ref=src,
        dst_ref=dst,
        send_sem=send_sem,
        recv_sem=recv_sem,
        device_id=device,
        device_id_type=MESH,
    )
    copy.start()
    return copy


def add_into(target, other):
    def tile(i, carry):
        at = pl.ds(pl.multiple_of(i * 16, 16), 16)
        target[at, :] = target[at, :] + other[at, :]
        return carry

    lax.fori_loop(0, target.shape[0] // 16, tile, 0)


def group_gather_body(me, pieces, own, out, own_sem, sems):
    size = own.shape[0] // pieces
    started = []
    local = pltpu.make_async_copy(own, out.at[me.x, me.c], own_sem)
    local.start()

    def at(p):
        return pl.ds(p * size, size)

    def go(kind, p, src, dst, device):
        slot = kind * pieces + p
        started.append(send(src, dst, sems.at[0, slot], sems.at[1, slot], device))

    for p in range(pieces):
        go(0, p, own.at[at(p)], out.at[me.x, me.c, at(p)], me.x_peer())
    for p in range(pieces):
        go(1, p, own.at[at(p)], out.at[me.x, me.c, at(p)], me.sibling())
    for p in range(pieces):
        block = out.at[1 - me.x, me.c, at(p)]
        pltpu.make_async_copy(block, block, sems.at[1, p]).wait()
        go(2, p, block, block, me.sibling())
    for p in range(pieces):
        for kind, x in ((1, me.x), (2, 1 - me.x)):
            block = out.at[x, 1 - me.c, at(p)]
            pltpu.make_async_copy(block, block, sems.at[1, kind * pieces + p]).wait()
    local.wait()
    for copy in started:
        copy.wait_send()


class GroupTotal:
    def __init__(self, me, parts, core_got, pair_got, sems):
        self.me, self.parts, self.core_got, self.pair_got = me, parts, core_got, pair_got
        self.core = [
            pltpu.make_async_remote_copy(
                src_ref=parts.at[x, 1 - me.c],
                dst_ref=core_got.at[x],
                send_sem=sems.at[0, k],
                recv_sem=sems.at[1, k],
                device_id=me.sibling(),
                device_id_type=MESH,
            )
            for k, x in enumerate((1 - me.x, me.x))
        ]
        self.pair = pltpu.make_async_remote_copy(
            src_ref=core_got.at[1 - me.x],
            dst_ref=pair_got,
            send_sem=sems.at[0, 2],
            recv_sem=sems.at[1, 2],
            device_id=me.x_peer(),
            device_id_type=MESH,
        )

    def begin(self):
        for copy in self.core:
            copy.start()

    def exchange(self):
        self.core[0].wait_recv()
        far = 1 - self.me.x
        add_into(self.core_got.at[far], self.parts.at[far, self.me.c])
        self.pair.start()

    def finish(self, out, change=lambda value, at: value):
        self.core[1].wait_recv()
        self.pair.wait_recv()

        def tile(i, carry):
            at = pl.ds(pl.multiple_of(i * 16, 16), 16)
            value = (
                self.parts[self.me.x, self.me.c, at, :].astype(jnp.float32)
                + self.core_got[self.me.x, at, :].astype(jnp.float32)
                + self.pair_got[at, :].astype(jnp.float32)
            )
            out[at, :] = change(value, at)
            return carry

        lax.fori_loop(0, out.shape[0] // 16, tile, 0)

    def sent(self):
        for copy in self.core + [self.pair]:
            copy.wait_send()


def all_others(ep_size):
    ep, tp = lax.axis_index("ep"), lax.axis_index("tp")
    return [
        (lax.rem(ep + k // 4, ep_size), lax.rem(tp + k % 4, 4)) for k in range(1, ep_size * 4)
    ]


def experts_kernel(
    ep_size,
    per_owner,
    rows_in,
    cots_in,
    code_in,
    router,
    enter_own,
    enter_peer,
    leave_own,
    leave_peer,
    grad_out,
    sum_out,
    small_out,
    gate_out,
    up_out,
    down_out,
    gate_peer,
    up_peer,
    down_peer,
    rows_buf,
    cots_buf,
    weighted,
    turned,
    enter_sum,
    down_sum,
    parts,
    core_got,
    y_got,
    z_got,
    small_in,
    small_got,
    load_sems,
    core_sems,
    y_sems,
    z_sems,
    small_sems,
    own_sem,
):
    me = Place(ep_size)
    depth = me.depth
    blocks = 2 * depth
    width = router.shape[1]
    share = rows_buf.shape[2]
    tokens = 2 * share
    hidden = leave_own.shape[0]
    units = hidden // per_owner
    f32, bf16 = jnp.float32, jnp.bfloat16
    ep = lax.axis_index("ep")
    others = [
        (lax.rem(ep + k // 2, ep_size), me.x * 2 + lax.rem(me.c + k % 2, 2))
        for k in range(1, 2 * ep_size)
    ]
    meet(others)
    my_place = ep * 2 + me.c
    halves = ((enter_own, leave_own), (enter_peer, leave_peer))

    def where(b):
        return me.after(b // 2 + 1), lax.rem(1 - me.y + b % 2, 2)

    def load(b, which):
        z, y = where(b)
        source, target = ((rows_in, rows_buf), (cots_in, cots_buf))[which]
        slot = lax.rem(b, 2)
        return pltpu.make_async_copy(
            source.at[z, y], target.at[slot], load_sems.at[slot, which]
        )

    def core_copy(b):
        return pltpu.make_async_remote_copy(
            src_ref=parts.at[lax.rem(b, 2), :, 1 - me.c],
            dst_ref=core_got.at[b // 2, where(b)[1]],
            send_sem=core_sems.at[0, b],
            recv_sem=core_sems.at[1, b],
            device_id=me.sibling(),
            device_id_type=MESH,
        )

    def y_copy(step, which):
        return pltpu.make_async_remote_copy(
            src_ref=core_got.at[step, 1 - me.y, which],
            dst_ref=y_got.at[step, which],
            send_sem=y_sems.at[0, step, which],
            recv_sem=y_sems.at[1, step, which],
            device_id=me.y_peer(),
            device_id_type=MESH,
        )

    def z_copy(step, which):
        return pltpu.make_async_remote_copy(
            src_ref=y_got.at[step, which],
            dst_ref=z_got.at[step, which],
            send_sem=z_sems.at[0, step, which],
            recv_sem=z_sems.at[1, step, which],
            device_id=me.device(z=me.after(step + 1)),
            device_id_type=MESH,
        )

    def small_copy(k, device):
        return pltpu.make_async_remote_copy(
            src_ref=small_in.at[device[0] * 2 + device[1] % 2],
            dst_ref=small_got.at[my_place],
            send_sem=small_sems.at[0, k],
            recv_sem=small_sems.at[1, k],
            device_id=device,
            device_id_type=MESH,
        )

    def dot(a, b, contract):
        return lax.dot_general(
            a, b, ((contract[:1], contract[1:]), ((), ())), preferred_element_type=f32
        )

    def spread(columns):
        return jnp.concatenate(
            [jnp.broadcast_to(columns[:, e : e + 1], (tokens, units)) for e in range(per_owner)],
            axis=1,
        )

    def compute(b):
        z, y = where(b)
        slot = lax.rem(b, 2)
        rows = rows_buf[slot].reshape(tokens, width)
        cots = cots_buf[slot].reshape(tokens, width)
        code = code_in[z * 2 + y, me.x].astype(f32).reshape(tokens, -1)
        used = code >= 0.0
        logits = jnp.where(used, dot(rows, router[...], (1, 1)), -1e30)
        top = jnp.max(logits, axis=1, keepdims=True)
        powers = jnp.where(used, jnp.exp(logits - top), 0.0)
        kept = jnp.where(code == 0.0, 1.0, 0.0)
        gates = spread(kept * powers / jnp.sum(powers, axis=1, keepdims=True))
        products = jnp.zeros((tokens, hidden), f32)
        for h, (enter, leave) in enumerate(halves):
            act = dot(rows, enter[...], (1, 0))
            gate_act, up_act = act[:, :hidden], act[:, hidden:]
            back_act = dot(cots, leave[...], (1, 1))
            sigma = jax.nn.sigmoid(gate_act)
            swish = gate_act * sigma
            value = swish * up_act
            products = products + value * back_act
            weighted[:, h * hidden : (h + 1) * hidden] = (gates * value).astype(bf16)
            grad_hidden = gates * back_act
            at = 2 * h * hidden
            turned[:, at : at + hidden] = (
                grad_hidden * up_act * sigma * (1.0 + gate_act * (1.0 - sigma))
            ).astype(bf16)
            turned[:, at + hidden : at + 2 * hidden] = (grad_hidden * swish).astype(bf16)
        lane = lax.broadcasted_iota(jnp.int32, (8, hidden), 1)
        pick = lax.broadcasted_iota(jnp.int32, (8, hidden), 0)
        mine = jnp.where((lane >= pick * units) & (lane < (pick + 1) * units), 1.0, 0.0)
        grad_gates = lax.dot_general(
            mine,
            spread(kept) * products,
            (((1,), (1,)), ((), ())),
            precision=EXACT_PRECISION,
            preferred_element_type=f32,
        )
        for k in range(2):
            small_in[(z * 2 + y) * 2 + k] = grad_gates[:, k * share : (k + 1) * share]
        tile = 512
        for n in range(width // tile):
            cols = slice(n * tile, (n + 1) * tile)
            grads = (
                dot(turned[:, : 2 * hidden], enter_own[cols, :], (1, 1))
                + dot(turned[:, 2 * hidden :], enter_peer[cols, :], (1, 1))
            ).astype(bf16)
            sums = (
                dot(weighted[:, :hidden], leave_own[:, cols], (1, 0))
                + dot(weighted[:, hidden:], leave_peer[:, cols], (1, 0))
            ).astype(bf16)
            for c in range(2):
                at = slice(c * share, (c + 1) * share)
                parts[slot, 0, c, :, cols] = grads[at]
                parts[slot, 1, c, :, cols] = sums[at]

    def weight_sums(b):
        slot = lax.rem(b, 2)
        tile = 512
        for n in range(width // tile):
            cols = slice(n * tile, (n + 1) * tile)
            rows = rows_buf[slot, :, :, cols].reshape(tokens, tile)
            cots = cots_buf[slot, :, :, cols].reshape(tokens, tile)
            enter_sum[:, cols] += dot(turned[...], rows, (0, 0))
            down_sum[:, cols] += dot(weighted[...], cots, (0, 0))

    enter_sum[...] = jnp.zeros_like(enter_sum)
    down_sum[...] = jnp.zeros_like(down_sum)
    for which in range(2):
        load(0, which).start()

    def during(i, lag, body, even=False):
        b = i - lag
        inside = (b >= 0) & (b < blocks)
        if even:
            inside &= b % 2 == 0
        pl.when(inside)(lambda: body(b))

    def work(b):
        for which in range(2):
            load(b, which).wait()

        @pl.when(b + 1 < blocks)
        def _():
            for which in range(2):
                load(b + 1, which).start()

        compute(b)
        core_copy(b).start()
        weight_sums(b)

    def core_sum(b):
        step, y = b // 2, where(b)[1]
        core_copy(b).wait_recv()
        for which in range(2):
            add_into(core_got.at[step, y, which], parts.at[lax.rem(b, 2), which, me.c])

        @pl.when(b % 2 == 0)
        def _():
            for which in range(2):
                y_copy(step, which).start()

        core_copy(b).wait_send()

    def y_sum(which):
        def body(b):
            step = b // 2
            y_copy(step, which).wait_recv()
            add_into(y_got.at[step, which], core_got.at[step, me.y, which])

            @pl.when(step < depth - 1)
            def _():
                z_copy(step, which).start()

        return body

    def small_send(b):
        for k, device in enumerate(others):
            small_copy(k, device).start()
        pltpu.make_async_copy(small_in.at[my_place], small_got.at[my_place], own_sem).start()
        for e in range(per_owner):
            own, peer = e * units, 2 * hidden + e * units
            gate_out[e] = enter_sum[own : own + units, :].T
            up_out[e] = enter_sum[hidden + own : hidden + own + units, :].T
            gate_peer[e] = enter_sum[peer : peer + units, :].T.astype(bf16)
            up_peer[e] = enter_sum[hidden + peer : hidden + peer + units, :].T.astype(bf16)
        down_out[...] = down_sum[:hidden, :]
        down_peer[...] = down_sum[hidden:, :].astype(bf16)

    def turn(i, carry):
        during(i, 0, work)
        during(i, 1, core_sum)
        during(i, 2, y_sum(0), True)
        during(i, 3, y_sum(1), True)
        pl.when(i == blocks)(lambda: small_send(i))
        return carry

    lax.fori_loop(0, blocks + 2, turn, 0)
    pltpu.make_async_copy(small_in.at[my_place], small_got.at[my_place], own_sem).wait()
    for k, device in enumerate(others):
        small_copy(k, device).wait()
    for k in range(ep_size):
        small_out[k] = small_got[2 * k] + small_got[2 * k + 1]
    for step in range(depth - 1):
        for which in range(2):
            z_copy(step, which).wait_recv()

    def finish(which, target):
        def tile(i, carry):
            at = pl.ds(pl.multiple_of(i * 16, 16), 16)
            total = y_got[depth - 1, which, at, :].astype(f32)
            for step in range(depth - 1):
                total = total + z_got[step, which, at, :].astype(f32)
            target[at, :] = total
            return carry

        lax.fori_loop(0, share // 16, tile, 0)

    finish(0, grad_out)
    finish(1, sum_out)
    for step in range(depth):
        for which in range(2):
            y_copy(step, which).wait_send()
            if step < depth - 1:
                z_copy(step, which).wait_send()


def experts_by_links(rows_all, cots_all, code, router, weights, per_owner, ep_size):
    depth, _, _, rows, width = rows_all.shape
    hidden = weights[2].shape[0]
    units = hidden // per_owner
    bf16, f32 = jnp.bfloat16, jnp.float32
    dma = pltpu.SemaphoreType.DMA
    vmem = pl.BlockSpec(memory_space=pltpu.VMEM)
    anywhere = pl.BlockSpec(memory_space=pltpu.HBM)
    places = 2 * ep_size
    return pl.pallas_call(
        functools.partial(experts_kernel, ep_size, per_owner),
        out_shape=(
            jax.ShapeDtypeStruct((rows, width), f32),
            jax.ShapeDtypeStruct((rows, width), f32),
            jax.ShapeDtypeStruct((ep_size, 8, rows), f32),
            jax.ShapeDtypeStruct((per_owner, width, units), f32),
            jax.ShapeDtypeStruct((per_owner, width, units), f32),
            jax.ShapeDtypeStruct((hidden, width), f32),
            jax.ShapeDtypeStruct((per_owner, width, units), bf16),
            jax.ShapeDtypeStruct((per_owner, width, units), bf16),
            jax.ShapeDtypeStruct((hidden, width), bf16),
        ),
        in_specs=[anywhere, anywhere] + [vmem] * 6,
        out_specs=(vmem,) * 9,
        scratch_shapes=[
            pltpu.VMEM((2, 2, rows, width), bf16),
            pltpu.VMEM((2, 2, rows, width), bf16),
            pltpu.VMEM((2 * rows, 2 * hidden), bf16),
            pltpu.VMEM((2 * rows, 4 * hidden), bf16),
            pltpu.VMEM((4 * hidden, width), f32),
            pltpu.VMEM((2 * hidden, width), f32),
            pltpu.VMEM((2, 2, 2, rows, width), bf16),
            pltpu.VMEM((depth, 2, 2, rows, width), bf16),
            pltpu.VMEM((depth, 2, rows, width), bf16),
            pltpu.VMEM((depth - 1, 2, rows, width), bf16),
            pltpu.VMEM((places, 8, rows), f32),
            pltpu.VMEM((places, 8, rows), f32),
            dma((2, 2)),
            dma((2, 2 * depth)),
            dma((2, depth, 2)),
            dma((2, depth - 1, 2)),
            dma((2, places - 1)),
            dma,
        ],
        compiler_params=pltpu.CompilerParams(
            collective_id=2, has_side_effects=True, vmem_limit_bytes=60 * 1024 * 1024
        ),
        name="experts_by_links",
    )(rows_all, cots_all, code.reshape(ep_size, 2, 2, rows, -1), router, *weights)


class LinkGather:
    def __init__(self, me, own, out, own_sem, z_sems, y_sems, core_sems):
        self.me, self.own, self.out = me, own, out
        self.own_sem, self.z_sems, self.y_sems, self.core_sems = own_sem, z_sems, y_sems, core_sems
        self.begun = []
        depth = me.depth
        self.found = [(me.z, 0, None)]
        for d in range(1, depth):
            self.found.append((me.z - d, d, me.z >= d))
            self.found.append((me.z + d, depth - 1 + d, me.z + d < depth))

    def guard(self, *conditions):
        given = [c for c in conditions if c is not None]
        if not given:
            return lambda body: body()
        total = given[0]
        for c in given[1:]:
            total = total & c
        return pl.when(total)

    def go(self, source, place, sems, slot, device, *conditions):
        def copy():
            return pltpu.make_async_remote_copy(
                src_ref=source,
                dst_ref=place,
                send_sem=sems.at[0, slot],
                recv_sem=sems.at[1, slot],
                device_id=device,
                device_id_type=MESH,
            )

        self.guard(*conditions)(lambda: copy().start())
        self.begun.append((copy, conditions))

    def landed(self, place, sems, slot, condition):
        self.guard(condition)(
            lambda: pltpu.make_async_copy(place, place, sems.at[1, slot]).wait()
        )

    def up(self, source, place, d, condition):
        me = self.me
        device = me.device(z=lax.rem(me.z + 1, me.depth))
        self.go(source, place, self.z_sems, d, device, condition, me.z < me.depth - 1)

    def down(self, source, place, d, condition):
        me = self.me
        device = me.device(z=lax.rem(me.z + me.depth - 1, me.depth))
        self.go(source, place, self.z_sems, me.depth - 1 + d, device, condition, me.z > 0)

    def place(self, z, y, c):
        at = (lax.rem(z + self.me.depth, self.me.depth), y)
        return self.out.at[at + (c,) if self.core_sems is not None else at]

    def to_sibling(self, block, slot, *conditions):
        if self.core_sems is not None:
            self.go(block[0], block[1], self.core_sems, slot, self.me.sibling(), *conditions)

    def begin(self):
        me = self.me
        mine = self.place(me.z, me.y, me.c)
        self.up(self.own, mine, 1, None)
        self.down(self.own, mine, 1, None)
        self.go(self.own, mine, self.y_sems, 0, me.y_peer())
        if self.core_sems is None:
            return
        self.to_sibling((self.own, mine), 0)
        self.local = pltpu.make_async_copy(self.own, mine, self.own_sem)
        self.local.start()

    def relay(self, d):
        me = self.me
        for z, slot, condition in self.found[2 * d - 1 : 2 * d + 1]:
            block = self.place(z, me.y, me.c)
            self.landed(block, self.z_sems, slot, condition)
            if d < me.depth - 1:
                (self.up if slot < me.depth else self.down)(block, block, d + 1, condition)
            self.go(block, block, self.y_sems, slot, me.y_peer(), condition)
            self.to_sibling((block, block), slot, condition)

    def cross(self, first, last):
        me = self.me
        for z, slot, condition in self.found[first:last]:
            block = self.place(z, 1 - me.y, me.c)
            self.landed(block, self.y_sems, slot, condition)
            self.to_sibling((block, block), 2 * me.depth - 1 + slot, condition)

    def finish(self):
        me = self.me
        for z, slot, condition in self.found:
            for y, at in ((me.y, slot), (1 - me.y, 2 * me.depth - 1 + slot)):
                self.landed(self.place(z, y, 1 - me.c), self.core_sems, at, condition)
        self.local.wait()
        self.sent()

    def sent(self):
        for copy, conditions in self.begun:
            self.guard(*conditions)(lambda: copy().wait_send())


class EpSum:
    def __init__(self, me, grads, y_got, z_got, final, sems):
        self.me, self.grads = me, grads
        self.y_got, self.z_got, self.final = y_got, z_got, final
        self.y_sems, self.z_sems, self.fz_sems, self.fy_sems = sems

    def y_copy(self, step):
        me = self.me
        return pltpu.make_async_remote_copy(
            src_ref=self.grads.at[me.after(step + 1), 1 - me.y],
            dst_ref=self.y_got.at[step],
            send_sem=self.y_sems.at[0, step],
            recv_sem=self.y_sems.at[1, step],
            device_id=me.y_peer(),
            device_id_type=MESH,
        )

    def z_copy(self, step):
        return pltpu.make_async_remote_copy(
            src_ref=self.y_got.at[step],
            dst_ref=self.z_got.at[step],
            send_sem=self.z_sems.at[0, step],
            recv_sem=self.z_sems.at[1, step],
            device_id=self.me.device(z=self.me.after(step + 1)),
            device_id_type=MESH,
        )

    def begin(self):
        for step in range(self.me.depth):
            self.y_copy(step).start()

    def fold(self, step):
        me = self.me
        self.y_copy(step).wait_recv()
        add_into(self.y_got.at[step], self.grads.at[me.after(step + 1), me.y])
        if step < me.depth - 1:
            self.z_copy(step).start()

    def settle(self):
        me, depth = self.me, self.me.depth
        for step in range(depth - 1):
            self.z_copy(step).wait_recv()

        def tile(i, carry):
            at = pl.ds(pl.multiple_of(i * 16, 16), 16)
            value = self.y_got[depth - 1, at, :].astype(jnp.float32)
            for step in range(depth - 1):
                value = value + self.z_got[step, at, :].astype(jnp.float32)
            self.final[me.z, me.y, at, :] = value.astype(self.final.dtype)
            return carry

        lax.fori_loop(0, self.final.shape[2] // 16, tile, 0)
        mine = self.final.at[me.z, me.y]
        self.spread = LinkGather(me, mine, self.final, None, self.fz_sems, self.fy_sems, None)
        self.spread.begin()

    def relay(self, d):
        self.spread.relay(d)

    def finish(self):
        self.spread.cross(0, 2 * self.me.depth - 1)

    def sent(self):
        self.spread.sent()
        for step in range(self.me.depth):
            self.y_copy(step).wait_send()
            if step < self.me.depth - 1:
                self.z_copy(step).wait_send()


def visible_columns(info_cols, info_rows):
    key_seg, key_pos = info_cols[:, 0:1], info_cols[:, 1:2]
    query_seg, query_pos = info_rows[0:1, :], info_rows[1:2, :]
    parent = jnp.where(query_seg >= 5, (query_seg - 5) // 2 + 1, -1)
    above = (key_seg == query_seg) | (key_seg == 0) | (key_seg == parent)
    return above & (key_pos <= query_pos)


def front_kernel(
    ep_size,
    heads,
    inputs,
    gain_one,
    gain_two,
    w_query,
    w_key,
    w_value,
    w_out,
    cosine,
    sine,
    info_cols,
    info_rows,
    table,
    cots,
    enter_near,
    leave_near,
    rows_out,
    queries,
    keys,
    values,
    heads_out,
    log_sums,
    middle,
    tables,
    cots_all,
    normed_all,
    normed_own,
    enter_far,
    leave_far,
    first_own,
    bias,
    parts,
    core_got,
    pair_got,
    own_sem,
    gather_sems,
    table_own_sem,
    table_sems,
    group_sems,
    far_sems,
    cots_sems,
    normed_sems,
):
    me = Place(ep_size)
    depth = me.depth
    f32, bf16 = jnp.float32, jnp.bfloat16
    share, width = inputs.shape
    tokens = 4 * share
    size = HEAD_DIMENSION
    groups = keys.shape[1] // size
    per_group = heads // groups
    scale = size ** (-0.5)
    ep, tp = lax.axis_index("ep"), lax.axis_index("tp")
    peers = [(lax.rem(ep + k, ep_size), tp) for k in range(1, ep_size)]
    meet([me.sibling(), me.x_peer()] + peers)

    def dot(a, b, contract):
        return lax.dot_general(
            a, b, ((contract[:1], contract[1:]), ((), ())), preferred_element_type=f32
        )

    cots_gather = LinkGather(me, cots, cots_all, *cots_sems)
    cots_gather.begin()
    for i in range(share // 16):
        at = slice(i * 16, (i + 1) * 16)
        value = inputs[at, :].astype(f32)
        first_own[at, :] = (value * norm_scale(value) * gain_one[...]).astype(bf16)
    table_local = pltpu.make_async_copy(table, tables.at[ep], table_own_sem)
    table_local.start()
    table_copies = [
        send(table, tables.at[ep], table_sems.at[0, k], table_sems.at[1, k], device)
        for k, device in enumerate(peers)
    ]
    bias[...] = jnp.where(visible_columns(info_cols[...], info_rows[...]), 0.0, -1e30)
    log_sums[...] = jnp.zeros_like(log_sums)
    group_gather_body(me, 4, first_own, rows_out, own_sem, gather_sems)

    def to_peer(i):
        source, target = ((leave_near, leave_far), (enter_near, enter_far))[i]
        return send(source, target, far_sems.at[0, i], far_sems.at[1, i], me.x_peer())

    exchanged = [to_peer(0)]
    cots_gather.relay(1)
    rows = rows_out[...].reshape(tokens, width)

    def rotate(part):
        turned = jnp.concatenate([part[:, size // 2 :], part[:, : size // 2]], axis=1)
        return (part * cosine[...] - turned * sine[...]).astype(bf16)

    projected = dot(rows, w_query[...], (1, 1))
    for head in range(heads):
        mine = slice(head * size, (head + 1) * size)
        queries[:, mine] = rotate(projected[:, mine])
    projected = dot(rows, w_key[...], (1, 1))
    for group in range(groups):
        mine = slice(group * size, (group + 1) * size)
        keys[:, mine] = rotate(projected[:, mine])
    values[...] = dot(rows, w_value[...], (1, 1)).astype(bf16)
    for head in range(heads):
        mine = slice(head * size, (head + 1) * size)
        shared = slice(head // per_group * size, (head // per_group + 1) * size)
        scores = dot(keys[:, shared], queries[:, mine], (1, 1)) * scale + bias[...]
        top = jnp.max(scores, axis=0, keepdims=True)
        powers = jnp.exp(scores - top)
        total = jnp.sum(powers, axis=0, keepdims=True)
        log_sums[head : head + 1, :] = top + jnp.log(total)
        probs = (powers / total).astype(bf16)
        heads_out[:, mine] = dot(probs, values[:, shared], (0, 0)).astype(bf16)
        if head == 1:
            cots_gather.relay(2)
    tile = 512
    for n in range(width // tile):
        cols = slice(n * tile, (n + 1) * tile)
        sums = dot(heads_out[...], w_out[:, cols], (1, 0)).astype(bf16)
        parts[:, :, :, cols] = sums.reshape(2, 2, share, tile)
    group = GroupTotal(me, parts, core_got, pair_got, group_sems)
    group.begin()
    for step in range(3, depth):
        cots_gather.relay(step)
    group.exchange()
    exchanged.append(to_peer(1))
    cots_gather.cross(0, 3)

    def last(value, at):
        total = inputs[at, :].astype(f32) + value
        normed_own[at, :] = (total * norm_scale(total) * gain_two[...]).astype(bf16)
        return total

    group.finish(middle, last)
    normed_gather = LinkGather(me, normed_own, normed_all, *normed_sems)
    normed_gather.begin()
    cots_gather.cross(3, 2 * depth - 1)
    for step in range(1, depth):
        normed_gather.relay(step)
    normed_gather.cross(0, 2 * depth - 1)
    cots_gather.finish()
    normed_gather.finish()
    group.sent()
    table_local.wait()
    for copy in table_copies + exchanged:
        copy.wait()


def token_tables(segment, position):
    cosine, sine = rope_tables(position, HEAD_DIMENSION)
    table = jnp.stack([segment, position])
    return (
        jnp.concatenate([cosine[:, 0], cosine[:, 0]], axis=1),
        jnp.concatenate([sine[:, 0], -sine[:, 0]], axis=1),
        jnp.pad(table.T, ((0, 0), (0, 126))),
        jnp.pad(table, ((0, 6), (0, 0))),
    )


def front_by_links(inputs, gains, projections, w_out, tables, order, cots, near, ep_size):
    share, width = inputs.shape
    depth = ep_size // 2
    tokens = 4 * share
    heads = w_out.shape[0] // HEAD_DIMENSION
    bf16, f32 = jnp.bfloat16, jnp.float32
    dma = pltpu.SemaphoreType.DMA
    vmem, anywhere = pl.BlockSpec(memory_space=pltpu.VMEM), pl.BlockSpec(memory_space=pltpu.HBM)

    def like(*shape, dtype=bf16):
        return jax.ShapeDtypeStruct(shape, dtype)

    def gather_sems():
        return (dma, dma((2, 2 * depth)), dma((2, 2 * depth)), dma((2, 4 * depth)))

    widths = [w.shape[0] for w in projections]
    everywhere = (depth, 2, 2, share, width)
    return pl.pallas_call(
        functools.partial(front_kernel, ep_size, heads),
        out_shape=(
            like(2, 2, share, width),
            like(tokens, widths[0]),
            like(tokens, widths[1]),
            like(tokens, widths[2]),
            like(tokens, widths[0]),
            like(8, tokens, dtype=f32),
            like(share, width, dtype=f32),
            like(ep_size, *order.shape, dtype=order.dtype),
            like(*everywhere),
            like(*everywhere),
            like(share, width),
            like(*near[0].shape),
            like(*near[1].shape),
        ),
        in_specs=[vmem] * 11 + [anywhere] * 4,
        out_specs=(vmem,) * 7 + (anywhere,) * 3 + (vmem,) + (anywhere,) * 2,
        scratch_shapes=[
            pltpu.VMEM((share, width), bf16),
            pltpu.VMEM((tokens, tokens), f32),
            pltpu.VMEM((2, 2, share, width), bf16),
            pltpu.VMEM((2, share, width), bf16),
            pltpu.VMEM((share, width), bf16),
            dma,
            dma((2, 12)),
            dma,
            dma((2, ep_size - 1)),
            dma((2, 3)),
            dma((2, 2)),
            gather_sems(),
            gather_sems(),
        ],
        compiler_params=pltpu.CompilerParams(
            collective_id=6, has_side_effects=True, vmem_limit_bytes=56 * 1024 * 1024
        ),
        name="front_by_links",
    )(
        inputs,
        gains[0][None, :],
        gains[1][None, :],
        *projections,
        w_out,
        *tables,
        order,
        cots,
        *near,
    )


def back_kernel(
    ep_size,
    heads,
    last_row,
    datt_own,
    heads_in,
    w_out,
    queries,
    keys,
    values,
    log_sums,
    info_cols,
    info_rows,
    cosine,
    sine,
    rows_in,
    w_query,
    w_key,
    w_value,
    small_in,
    gain,
    inputs,
    middle,
    gate_peer,
    up_peer,
    down_peer,
    first_final,
    second_final,
    out_final,
    grad_input,
    small_out,
    gate_got,
    up_got,
    down_got,
    datt,
    bias,
    grad_heads,
    grad_proj,
    key_sum,
    value_sum,
    part_proj,
    part_out,
    y_got,
    z_got,
    y_got_out,
    z_got_out,
    parts,
    core_got,
    pair_got,
    small_src,
    small_got,
    small_sum,
    own_sem,
    gather_sems,
    y_sems,
    z_sems,
    fz_sems,
    fy_sems,
    y_sems_out,
    z_sems_out,
    fz_sems_out,
    fy_sems_out,
    group_sems,
    small_sems,
    spread_sems,
    own_small_sem,
    peer_sems,
):
    me = Place(ep_size)
    depth = me.depth
    f32, bf16 = jnp.float32, jnp.bfloat16
    others = all_others(ep_size)
    meet(others)
    my_place = lax.axis_index("ep") * 4 + lax.axis_index("tp")
    tokens, width = rows_in.shape
    share = datt_own.shape[0]
    size = HEAD_DIMENSION
    groups = keys.shape[1] // size
    per_group = heads // groups
    scale = size ** (-0.5)
    tile = 512

    def dot(a, b, contract):
        return lax.dot_general(
            a, b, ((contract[:1], contract[1:]), ((), ())), preferred_element_type=f32
        )

    bias[...] = jnp.where(visible_columns(info_cols[...], info_rows[...]), 0.0, -1e30)
    group_gather_body(me, 4, datt_own, datt, own_sem, gather_sems)

    def to_peer(i):
        source, target = ((gate_peer, gate_got), (up_peer, up_got), (down_peer, down_got))[i]
        return send(source, target, peer_sems.at[0, i], peer_sems.at[1, i], me.x_peer())

    exchanged = [to_peer(i) for i in range(3)]
    for n in range(width // tile):
        cols = slice(n * tile, (n + 1) * tile)
        grads = dot(heads_in[...], datt[:, :, :, cols].reshape(tokens, tile), (0, 0))
        part_out[:, :, :, cols] = grads.astype(bf16).reshape(depth, 2, -1, tile)
    out_sum = EpSum(
        me,
        part_out,
        y_got_out,
        z_got_out,
        out_final,
        (y_sems_out, z_sems_out, fz_sems_out, fy_sems_out),
    )
    out_sum.begin()
    for x in range(2):
        for c in range(2):
            at = pl.ds((x * 2 + c) * share, share)
            grad_heads[at, :] = dot(datt[x, c], w_out[...], (1, 1)).astype(bf16)

    def rotate_back_rows(grads):
        turned = jnp.concatenate([grads[:, size // 2 :], grads[:, : size // 2]], axis=1)
        return (grads * cosine[...] + turned * sine[...]).astype(bf16)

    for head in range(heads):
        group = head // per_group
        mine = slice(head * size, (head + 1) * size)
        shared = slice(group * size, (group + 1) * size)
        query, grad_head = queries[:, mine], grad_heads[:, mine]
        key, value = keys[:, shared], values[:, shared]
        scores = dot(key, query, (1, 1)) * scale + bias[...]
        probs = jnp.exp(scores - log_sums[head : head + 1, :])
        grad_probs = dot(value, grad_head, (1, 1))
        inner = jnp.sum(probs * grad_probs, axis=0, keepdims=True)
        grad_scores = (probs * (grad_probs - inner)).astype(bf16)
        grad_value = dot(probs.astype(bf16), grad_head, (1, 0))
        grad_key = dot(grad_scores, query, (1, 0)) * scale
        if head % per_group:
            grad_value = grad_value + value_sum[...]
            grad_key = grad_key + key_sum[...]
        value_sum[...] = grad_value
        key_sum[...] = grad_key
        grad_query = dot(grad_scores, key, (0, 0)) * scale
        grad_proj[:, mine] = rotate_back_rows(grad_query)
        if head % per_group == per_group - 1:
            at = heads * size + group * size
            grad_proj[:, at : at + size] = rotate_back_rows(grad_key)
            at += groups * size
            grad_proj[:, at : at + size] = grad_value.astype(bf16)
        if head % 2 and head // 2 < depth - 2:
            out_sum.fold(head // 2)
    folded = min(heads // 2, depth - 2)

    ends = (heads * size, (heads + groups) * size, (heads + 2 * groups) * size)
    wide = width // 2
    sums = []
    for n, final in enumerate((first_final, second_final)):
        cols = slice(n * wide, (n + 1) * wide)
        grads = dot(grad_proj[...], rows_in[:, cols], (0, 0)).astype(bf16)
        at, first = 0, 0
        for end in ends:
            piece = grads[first:end].reshape(depth, 2, -1, wide)
            part_proj[n, :, :, at : at + piece.shape[2]] = piece
            at, first = at + piece.shape[2], end
        sums.append(
            EpSum(
                me,
                part_proj.at[n],
                y_got.at[n],
                z_got.at[n],
                final,
                (y_sems.at[n], z_sems.at[n], fz_sems.at[n], fy_sems.at[n]),
            )
        )
        if n == 1:
            sums[0].fold(0)
            for step in range(max(folded, depth - 1), depth):
                out_sum.fold(step)
            sums[0].fold(1)
        sums[n].begin()
        if n == 0:
            for step in range(folded, depth - 1):
                out_sum.fold(step)
    first_sum, second_sum = sums
    small_src[...] = small_in[...]
    for n in range(width // tile):
        cols = slice(n * tile, (n + 1) * tile)
        grads = (
            dot(grad_proj[:, : ends[0]], w_query[:, cols], (1, 0))
            + dot(grad_proj[:, ends[0] : ends[1]], w_key[:, cols], (1, 0))
            + dot(grad_proj[:, ends[1] :], w_value[:, cols], (1, 0))
        )
        parts[:, :, :, cols] = grads.astype(bf16).reshape(2, 2, share, tile)
        gained = jnp.sum(grads * rows_in[:, cols].astype(f32), axis=0, keepdims=True)
        gained = gained / gain[:, cols]
        for k in range(tile // 128):
            row = n * (tile // 128) + k
            small_src[last_row, row : row + 1, :] = gained[:, k * 128 : (k + 1) * 128]
    for step in range(2, depth - 1):
        first_sum.fold(step)
    out_sum.settle()
    small = [
        send(
            small_src.at[device[0] * 4 + device[1]],
            small_got.at[my_place],
            small_sems.at[0, k],
            small_sems.at[1, k],
            device,
        )
        for k, device in enumerate(others)
    ]
    own_small = pltpu.make_async_copy(
        small_src.at[my_place], small_got.at[my_place], own_small_sem
    )
    own_small.start()
    second_sum.fold(0)
    first_sum.fold(depth - 1)
    first_sum.settle()
    out_sum.relay(1)
    second_sum.fold(1)
    own_small.wait()
    for copy in small:
        copy.wait_recv()
    total = small_got[0]
    for k in range(1, 4 * ep_size):
        total = total + small_got[k]
    small_sum[...] = total
    spread = [
        send(
            small_sum,
            small_out.at[my_place],
            spread_sems.at[0, k],
            spread_sems.at[1, k],
            device,
        )
        for k, device in enumerate(others)
    ]
    small_out[my_place] = total
    group = GroupTotal(me, parts, core_got, pair_got, group_sems)
    group.begin()
    out_sum.relay(2)
    for step in range(2, depth - 1):
        second_sum.fold(step)
    group.exchange()
    first_sum.relay(1)
    second_sum.fold(depth - 1)
    for step in range(3, depth):
        out_sum.relay(step)
    second_sum.settle()
    out_sum.finish()
    first_sum.relay(2)

    def last(value, at):
        values_own = inputs[at, :].astype(f32)
        factor = norm_scale(values_own)
        return middle[at, :] + norm_back(values_own, factor, gain[...], value)

    group.finish(grad_input, last)
    second_sum.relay(1)
    for step in range(3, depth):
        first_sum.relay(step)
    for step in range(2, depth):
        second_sum.relay(step)
    first_sum.finish()
    second_sum.finish()
    for copy in spread:
        copy.wait()
    for copy in small:
        copy.wait_send()
    group.sent()
    for each in [out_sum] + sums:
        each.sent()
    for copy in exchanged:
        copy.wait()


def back_by_links(
    datt_own,
    heads_in,
    w_out,
    queries,
    keys,
    values,
    log_sums,
    tables,
    rows_in,
    w_query,
    w_key,
    w_value,
    small,
    gain,
    inputs,
    middle,
    peers,
    ep_size,
):
    tokens, width = rows_in.shape
    share = datt_own.shape[0]
    depth = ep_size // 2
    heads = queries.shape[1] // HEAD_DIMENSION
    places = 4 * ep_size
    bf16, f32 = jnp.bfloat16, jnp.float32
    dma = pltpu.SemaphoreType.DMA
    vmem = pl.BlockSpec(memory_space=pltpu.VMEM)
    anywhere = pl.BlockSpec(memory_space=pltpu.HBM)
    cosine, sine, info_cols, info_rows = tables
    blocks = jnp.pad(small, ((0, places - small.shape[0]), (0, 0))).reshape(places, -1, 128)
    sizes = [w.shape[0] // ep_size for w in (w_query, w_key, w_value, w_out)]
    total = sum(sizes[:3])

    def partial(rows, columns):
        return (depth, 2, rows, columns), bf16

    wide = width // 2
    got = pl.pallas_call(
        functools.partial(back_kernel, ep_size, heads, small.shape[0]),
        out_shape=(
            jax.ShapeDtypeStruct(*partial(total, wide)),
            jax.ShapeDtypeStruct(*partial(total, wide)),
            jax.ShapeDtypeStruct(*partial(sizes[3], width)),
            jax.ShapeDtypeStruct((share, width), f32),
            jax.ShapeDtypeStruct(blocks.shape, f32),
        )
        + tuple(jax.ShapeDtypeStruct(p.shape, p.dtype) for p in peers),
        in_specs=[vmem] * 19 + [anywhere] * 3,
        out_specs=(vmem,) * 5 + (anywhere,) * 3,
        scratch_shapes=[
            pltpu.VMEM((2, 2, share, width), bf16),
            pltpu.VMEM((tokens, tokens), f32),
            pltpu.VMEM(queries.shape, bf16),
            pltpu.VMEM((tokens, queries.shape[1] + 2 * keys.shape[1]), bf16),
            pltpu.VMEM((tokens, HEAD_DIMENSION), f32),
            pltpu.VMEM((tokens, HEAD_DIMENSION), f32),
        ]
        + [
            pltpu.VMEM((2, depth, 2, total, wide), bf16),
            pltpu.VMEM((depth, 2, sizes[3], width), bf16),
            pltpu.VMEM((2, depth, total, wide), bf16),
            pltpu.VMEM((2, depth - 1, total, wide), bf16),
            pltpu.VMEM((depth, sizes[3], width), bf16),
            pltpu.VMEM((depth - 1, sizes[3], width), bf16),
            pltpu.VMEM((2, 2, share, width), bf16),
            pltpu.VMEM((2, share, width), bf16),
            pltpu.VMEM((share, width), bf16),
            pltpu.VMEM(blocks.shape, f32),
            pltpu.VMEM(blocks.shape, f32),
            pltpu.VMEM(blocks.shape[1:], f32),
            dma,
            dma((2, 12)),
        ]
        + [dma((2, 2, depth)), dma((2, 2, depth))]
        + [dma((2, 2, 2 * depth))] * 2
        + [dma((2, depth)), dma((2, depth))]
        + [dma((2, 2 * depth))] * 2
        + [dma((2, 3)), dma((2, places - 1)), dma((2, places - 1)), dma, dma((2, 3))],
        compiler_params=pltpu.CompilerParams(
            collective_id=5, has_side_effects=True, vmem_limit_bytes=60 * 1024 * 1024
        ),
        name="back_by_links",
    )(
        datt_own,
        heads_in,
        w_out,
        queries,
        keys,
        values,
        log_sums,
        info_cols,
        info_rows,
        cosine,
        sine,
        rows_in,
        w_query,
        w_key,
        w_value,
        blocks,
        gain[None, :],
        inputs,
        middle,
        *peers,
    )
    return got


def deliver_kernel(
    ep_size,
    sizes,
    rows_in,
    sums_in,
    gate_in,
    up_in,
    down_in,
    gate_got,
    up_got,
    down_got,
    first_in,
    second_in,
    third_in,
    small,
    gate_out,
    up_out,
    down_out,
    rows_out,
    sums_out,
    query_out,
    key_out,
    value_out,
    out_out,
    router_out,
    first_gain,
    second_gain,
    query,
    key,
    value,
    out,
    gate,
    up,
    down,
    gate_far,
    up_far,
    down_far,
    first,
    second,
    third,
    sems,
    load_sems,
):
    pairs = ((rows_in, rows_out), (sums_in, sums_out))
    loads = [
        pltpu.make_async_copy(source, target, load_sems.at[i])
        for i, (source, target) in enumerate(
            (
                (third_in, third),
                (first_in, first),
                (second_in, second),
                (gate_in, gate),
                (gate_got, gate_far),
                (up_in, up),
                (up_got, up_far),
                (down_in, down),
                (down_got, down_far),
            )
        )
    ]
    for load in loads:
        load.start()
    copies = [
        pltpu.make_async_copy(source, target, sems.at[i]) for i, (source, target) in enumerate(pairs)
    ]
    for copy in copies:
        copy.start()
    wide = first.shape[2]
    f32 = jnp.float32

    def leave(source, target, i):
        copies.append(pltpu.make_async_copy(source, target, sems.at[i]))
        copies[-1].start()

    loads[0].wait()
    out[...] = third[...].astype(f32)
    leave(out, out_out, 5)
    for load in loads[1:3]:
        load.wait()
    at = 0
    for i, (source, target) in enumerate(((query, query_out), (key, key_out), (value, value_out))):
        for n, part in enumerate((first, second)):
            source[:, :, n * wide : (n + 1) * wide] = part[:, at : at + sizes[i], :].astype(f32)
        at += sizes[i]
        leave(source, target, 6 + i)
    for i, (total, far) in enumerate(((gate, gate_far), (up, up_far), (down, down_far))):
        for load in loads[3 + 2 * i : 5 + 2 * i]:
            load.wait()
        total[...] = total[...] + far[...].astype(f32)
        leave(total, (gate_out, up_out, down_out)[i], 2 + i)
    experts = router_out.shape[0]
    for j in range(small.shape[1]):
        cols = slice(j * 128, (j + 1) * 128)
        router_out[:, cols] = small[:experts, j, :]
        first_gain[:, cols] = small[experts + 1 : experts + 2, j, :]
        second_gain[:, cols] = small[experts : experts + 1, j, :]
    for copy in copies:
        copy.wait()


def deliver(owned, peers, rows, sums, got, small, sizes, expert_count, ep_size):
    width = rows.shape[1]
    f32 = jnp.float32
    vmem, anywhere = pl.BlockSpec(memory_space=pltpu.VMEM), pl.BlockSpec(memory_space=pltpu.HBM)
    first, second, third = (g.reshape((ep_size,) + g.shape[2:]) for g in got)

    def like(value):
        return jax.ShapeDtypeStruct(value.shape, value.dtype)

    shapes = [(ep_size, k, width) for k in sizes]
    results = pl.pallas_call(
        functools.partial(deliver_kernel, ep_size, sizes),
        out_shape=tuple(like(a) for a in owned)
        + (like(rows), like(sums))
        + tuple(jax.ShapeDtypeStruct(shape, f32) for shape in shapes)
        + (
            jax.ShapeDtypeStruct((expert_count, width), f32),
            jax.ShapeDtypeStruct((1, width), f32),
            jax.ShapeDtypeStruct((1, width), f32),
        ),
        in_specs=[anywhere] * 11 + [vmem],
        out_specs=(anywhere,) * 9 + (vmem,) * 3,
        scratch_shapes=[pltpu.VMEM(shape, f32) for shape in shapes]
        + [pltpu.VMEM(a.shape, a.dtype) for a in (*owned, *peers, first, second, third)]
        + [pltpu.SemaphoreType.DMA((9,))] * 2,
        compiler_params=pltpu.CompilerParams(vmem_limit_bytes=60 * 1024 * 1024),
        name="deliver",
    )(rows, sums, *owned, *peers, first, second, third, small)
    gate, up, down, rows, sums = results[:5]
    query, key, value, out = (g.reshape(-1, width) for g in results[5:9])
    router, first_gain, second_gain = results[9:]
    return (
        sums,
        rows,
        first_gain.reshape(width),
        query,
        key,
        value,
        out,
        second_gain.reshape(width),
        router,
        gate,
        up,
        down.reshape(gate.shape[0], -1, width),
    )


def group_rows(value_rows):
    return lax.all_gather(value_rows, "tp", axis=0, tiled=True)


def group_totals(value_rows):
    return lax.psum_scatter(value_rows, "tp", scatter_dimension=0, tiled=True).astype(jnp.float32)


def gather_all(value_rows):
    return lax.all_gather(value_rows, ("ep", "tp"), axis=0, tiled=True)


LAST = 1 << 30


def pair_order(expert_ids, slot_order, expert_count):
    experts = jnp.arange(expert_count, dtype=jnp.int32)
    chosen = expert_ids.T[None, :, :] == experts[:, None, None]
    return jnp.min(jnp.where(chosen, slot_order.T[None, :, :], LAST), axis=1)


def kept_pairs(order):
    used = order < LAST
    counts = jnp.sum(used.astype(jnp.int32), axis=2)
    block = jnp.arange(order.shape[0], dtype=jnp.int32)
    earlier = block[None, :] < block[:, None]
    offsets = jnp.sum(jnp.where(earlier[:, :, None], counts[None, :, :], 0), axis=1)
    whole = offsets + counts <= CAP
    edge = (offsets < CAP) & ~whole
    edge_order = jnp.sum(jnp.where(edge[:, :, None], order, 0), axis=0)
    rank = jnp.sum((edge_order[:, :, None] < edge_order[:, None, :]).astype(jnp.int32), axis=1)
    early = offsets[:, :, None] + rank[None, :, :] < CAP
    return used & (whole[:, :, None] | (edge[:, :, None] & early))


def masked_softmax(logits, used):
    top = jnp.max(jnp.where(used, logits, -1e30), axis=-1, keepdims=True)
    powers = jnp.where(used, jnp.exp(logits - top), 0.0)
    return powers / jnp.sum(powers, axis=-1, keepdims=True)


def pair_codes(order_all, per_owner):
    expert_count = order_all.shape[1]
    first = lax.axis_index("ep") * per_owner
    turned = jnp.roll(order_all, -first, axis=1)
    kept = kept_pairs(turned[:, :per_owner])
    dropped = jnp.pad(~kept, ((0, 0), (0, expert_count - per_owner), (0, 0)))
    code = jnp.where(turned < LAST, dropped.astype(jnp.float32), -1.0)
    code = code.swapaxes(1, 2).reshape(-1, expert_count)
    lanes = -expert_count % 128
    return jnp.pad(code, ((0, 0), (0, lanes)), constant_values=-1.0).astype(jnp.bfloat16)


def expert_weights(w_gate, w_up, w_down):
    enter = jnp.concatenate([w[e] for w in (w_gate, w_up) for e in range(w.shape[0])], axis=1)
    return enter, w_down.reshape(-1, w_down.shape[2])


def run_experts(rows_all, cots_all, code, w_router, w_gate, w_up, w_down, weights, by_links):
    per_owner, width, units = w_gate.shape
    expert_count = w_router.shape[0]
    ep_size, tp_size = lax.axis_size("ep"), lax.axis_size("tp")
    hidden = per_owner * units
    router = jnp.roll(w_router, -lax.axis_index("ep") * per_owner, axis=0)
    router = jnp.pad(router, ((0, -expert_count % 128), (0, 0)))
    if by_links:
        grads, sums, small, *owned = experts_by_links(
            rows_all, cots_all, code, router, weights, per_owner, ep_size
        )
        share = grads.shape[0]
        return (
            grads,
            sums,
            small[:, :per_owner].reshape(expert_count, share).T,
            owned[:3],
            owned[3:],
        )
    enter, leave = expert_weights(w_gate, w_up, w_down)
    used, kept = code >= 0, (code == 0).astype(jnp.float32)
    logits = jnp.einsum("rd,ed->re", rows_all, router, preferred_element_type=jnp.float32)
    gates = jnp.repeat((kept * masked_softmax(logits, used))[:, :per_owner], units, axis=1)
    act = jnp.dot(rows_all, enter, preferred_element_type=jnp.float32)
    gate_act, up_act = act[:, :hidden], act[:, hidden:]
    back_act = jnp.einsum("rd,fd->rf", cots_all, leave, preferred_element_type=jnp.float32)
    sigma = jax.nn.sigmoid(gate_act)
    value = gate_act * sigma * up_act
    weighted = (gates * value).astype(jnp.bfloat16)
    grad_hidden = gates * back_act
    turned = jnp.concatenate(
        [
            grad_hidden * up_act * sigma * (1.0 + gate_act * (1.0 - sigma)),
            grad_hidden * gate_act * sigma,
        ],
        axis=1,
    ).astype(jnp.bfloat16)
    small = kept[:, :per_owner] * jnp.sum((value * back_act).reshape(-1, per_owner, units), axis=2)
    grads = jnp.einsum("rf,df->rd", turned, enter, preferred_element_type=jnp.float32)
    sums = jnp.dot(weighted, leave, preferred_element_type=jnp.float32)

    def scatter(value_rows):
        return lax.psum_scatter(value_rows, ("ep", "tp"), scatter_dimension=0, tiled=True)

    columns = lax.dynamic_update_slice_in_dim(
        jnp.zeros((small.shape[0], expert_count), jnp.float32),
        small,
        lax.axis_index("ep") * per_owner,
        1,
    )
    both = jnp.einsum(
        "rd,rwef->wedf",
        rows_all,
        turned.reshape(-1, 2, per_owner, units),
        preferred_element_type=jnp.float32,
    )
    down = jnp.einsum("rf,rd->fd", weighted, cots_all, preferred_element_type=jnp.float32)
    return (
        scatter(grads.astype(jnp.bfloat16)).astype(jnp.float32),
        scatter(sums.astype(jnp.bfloat16)).astype(jnp.float32),
        scatter(columns),
        (both[0], both[1], down),
        None,
    )


def visible_block(query_seg, query_pos, query_row, key_seg, key_pos, key_row):
    seg_q = query_seg[:, None]
    seg_k = key_seg[None, :]
    above = (
        (seg_k == seg_q)
        | (seg_k == 0)
        | (seg_k >= 1) & (seg_k <= 4) & (seg_q >= 5) & ((seg_q - 5) // 2 + 1 == seg_k)
    )
    same_tree = query_row[:, None] // TREE_TOKENS == key_row[None, :] // TREE_TOKENS
    return above & same_tree & (key_pos[None, :] <= query_pos[:, None])


def block_scores(query_part, key_rows, allowed, scale):
    scores = (
        jnp.einsum("qkgd,pkd->kgqp", query_part, key_rows, preferred_element_type=jnp.float32)
        * scale
    )
    return jnp.where(allowed[None, None], scores, -1e30)


def attend_forward(query_rows, key_rows, value_rows, segment, position):
    total_rows = query_rows.shape[0]
    scale = query_rows.shape[-1] ** (-0.5)
    row_ids = jnp.arange(total_rows, dtype=jnp.int32)
    allowed = visible_block(segment, position, row_ids, segment, position, row_ids)
    scores = block_scores(query_rows, key_rows, allowed, scale)
    top_score = jnp.max(scores, axis=-1, keepdims=True)
    weights = jnp.exp(scores - top_score)
    weight_sum = jnp.sum(weights, axis=-1, keepdims=True)
    probs = (weights / weight_sum).astype(jnp.bfloat16)
    outputs = jnp.einsum(
        "kgqp,pkd->qkgd", probs, value_rows, preferred_element_type=jnp.float32
    ).astype(jnp.bfloat16)
    log_sums = [top_score + jnp.log(weight_sum)]
    return (outputs, log_sums)


def attend_backward(
    query_rows, key_rows, value_rows, segment, position, log_sums, grad_heads, block_rows
):
    total_rows = query_rows.shape[0]
    scale = query_rows.shape[-1] ** (-0.5)
    row_ids = jnp.arange(total_rows, dtype=jnp.int32)
    grad_keys = jnp.zeros(key_rows.shape, jnp.float32)
    grad_values = jnp.zeros(value_rows.shape, jnp.float32)
    grad_query = []
    for number, first_row in enumerate(range(0, total_rows, block_rows)):
        allowed = visible_block(segment, position, row_ids, segment, position, row_ids)
        scores = block_scores(query_rows, key_rows, allowed, scale)
        probs = jnp.where(allowed[None, None], jnp.exp(scores - log_sums[number]), 0.0)
        grad_values = jnp.einsum(
            "kgqp,qkgd->pkd",
            probs.astype(jnp.bfloat16),
            grad_heads,
            preferred_element_type=jnp.float32,
        )
        grad_probs = jnp.einsum(
            "qkgd,pkd->kgqp", grad_heads, value_rows, preferred_element_type=jnp.float32
        )
        inner = jnp.sum(probs * grad_probs, axis=-1, keepdims=True)
        grad_scores = (probs * (grad_probs - inner)).astype(jnp.bfloat16)
        grad_query.append(
            jnp.einsum("kgqp,pkd->qkgd", grad_scores, key_rows, preferred_element_type=jnp.float32)
            * scale
        )
        grad_keys = (
            jnp.einsum(
                "kgqp,qkgd->pkd", grad_scores, query_rows, preferred_element_type=jnp.float32
            )
            * scale
        )
    return (grad_query[0], grad_keys, grad_values)


def local(
    hidden_in,
    gain_attn,
    w_query,
    key_projection_weight,
    value_projection_weight,
    w_out,
    gain_ffn,
    w_router,
    w_gate,
    w_up,
    w_down,
    expert_ids,
    slot_order,
    segment,
    position,
    cotangent,
):
    model_width = w_query.shape[1]
    head_width = HEAD_DIMENSION
    local_heads = w_query.shape[0] // head_width
    local_kv = key_projection_weight.shape[0] // head_width
    group_factor = local_heads // local_kv
    token_count = expert_ids.shape[0]
    share = hidden_in.shape[0]
    row_start = lax.axis_index("tp") * share
    expert_count = w_router.shape[0]
    per_owner = w_gate.shape[0]
    block_rows = 512
    by_links = lax.axis_size("tp") == 4 and lax.axis_size("ep") == 8
    order = pair_order(expert_ids, slot_order, expert_count)
    gain_one = gain_attn.astype(jnp.float32)
    gain_two = gain_ffn.astype(jnp.float32)
    inputs_own = hidden_in.astype(jnp.float32)
    if by_links:
        near = expert_weights(w_gate, w_up, w_down)
        token_info = token_tables(segment, position)
        (
            first_normalized,
            query_rows,
            key_rows,
            value_rows,
            head_outputs,
            log_sums,
            middle_own,
            order_all,
            cot_all,
            normed_two,
            normed_own,
            *far,
        ) = front_by_links(
            hidden_in,
            (gain_one, gain_two),
            (w_query, key_projection_weight, value_projection_weight),
            w_out,
            token_info,
            order,
            cotangent,
            near,
            lax.axis_size("ep"),
        )
        weights = (near[0], far[0], near[1], far[1])
        scale_two = norm_scale(middle_own)
    else:
        weights = None
        scale_one = norm_scale(inputs_own)
        first_normalized = group_rows((inputs_own * scale_one * gain_one).astype(jnp.bfloat16))
        order_all = lax.all_gather(order, "ep")
        cosine_lookup, sine_lookup = rope_tables(position, head_width)
        query_proj = jnp.einsum(
            "rd,fd->rf", first_normalized, w_query, preferred_element_type=jnp.float32
        ).reshape(token_count, local_heads, head_width)
        key_proj = jnp.einsum(
            "rd,fd->rf", first_normalized, key_projection_weight, preferred_element_type=jnp.float32
        ).reshape(token_count, local_kv, head_width)
        query_rows = (
            apply_rotation(query_proj, cosine_lookup, sine_lookup)
            .astype(jnp.bfloat16)
            .reshape(token_count, local_kv, group_factor, head_width)
        )
        key_rows = apply_rotation(key_proj, cosine_lookup, sine_lookup).astype(jnp.bfloat16)
        value_rows = (
            jnp.einsum(
                "rd,fd->rf",
                first_normalized,
                value_projection_weight,
                preferred_element_type=jnp.float32,
            )
            .astype(jnp.bfloat16)
            .reshape(token_count, local_kv, head_width)
        )
        head_outputs, log_sums = attend_forward(query_rows, key_rows, value_rows, segment, position)
        head_outputs = head_outputs.reshape(token_count, local_heads * head_width)
        middle_own = inputs_own + group_totals(
            jnp.dot(head_outputs, w_out, preferred_element_type=jnp.float32).astype(jnp.bfloat16)
        )
        scale_two = norm_scale(middle_own)
        normed_own = (middle_own * scale_two * gain_two).astype(jnp.bfloat16)
        normed_two, cot_all = gather_all(normed_own), gather_all(cotangent)
    code = pair_codes(order_all, per_owner)
    used = lax.dynamic_slice_in_dim(order, row_start, share, 1).T < LAST
    gates = masked_softmax(
        jnp.einsum("rd,ed->re", normed_own, w_router, preferred_element_type=jnp.float32), used
    )
    grad_normed_own, combined_own, grad_gates_own, owned, peers = run_experts(
        normed_two, cot_all, code, w_router, w_gate, w_up, w_down, weights, by_links
    )
    output_own = (middle_own + combined_own).astype(jnp.bfloat16)
    inner_gate = jnp.sum(gates * grad_gates_own, axis=-1, keepdims=True)
    grad_logits = gates * (grad_gates_own - inner_gate)
    router_f = w_router.astype(jnp.float32)
    grad_normed_own = grad_normed_own + jnp.dot(grad_logits, router_f, precision=EXACT_PRECISION)
    grad_router = jnp.dot(grad_logits.T, normed_own.astype(jnp.float32), precision=EXACT_PRECISION)
    grad_gain_ffn = jnp.sum(grad_normed_own * middle_own * scale_two, axis=0)
    grad_middle = cotangent.astype(jnp.float32) + norm_back(
        middle_own, scale_two, gain_two, grad_normed_own
    )
    if by_links:
        *got, grad_input, small, gate_got, up_got, down_got = back_by_links(
            grad_middle.astype(jnp.bfloat16),
            head_outputs,
            w_out,
            query_rows,
            key_rows,
            value_rows,
            log_sums,
            token_info,
            first_normalized.reshape(token_count, model_width),
            w_query,
            key_projection_weight,
            value_projection_weight,
            jnp.concatenate([grad_router, grad_gain_ffn[None, :]], axis=0),
            gain_one,
            hidden_in,
            grad_middle,
            peers,
            lax.axis_size("ep"),
        )
        ep_size = lax.axis_size("ep")
        weights = (w_query, key_projection_weight, value_projection_weight, w_out)
        return deliver(
            owned,
            (gate_got, up_got, down_got),
            grad_input,
            output_own,
            got,
            small,
            [w.shape[0] // ep_size for w in weights],
            expert_count,
            ep_size,
        )
    grad_attn = group_rows(grad_middle.astype(jnp.bfloat16))
    grad_w_out = jnp.einsum(
        "rf,rd->fd", head_outputs, grad_attn, preferred_element_type=jnp.float32
    )
    grad_w_out = lax.psum(grad_w_out.astype(jnp.bfloat16), "ep").astype(jnp.float32)
    grad_heads = (
        jnp.einsum("rd,fd->rf", grad_attn, w_out, preferred_element_type=jnp.float32)
        .astype(jnp.bfloat16)
        .reshape(token_count, local_kv, group_factor, head_width)
    )
    grad_query, grad_keys, grad_values = attend_backward(
        query_rows, key_rows, value_rows, segment, position, log_sums, grad_heads, block_rows
    )
    grad_query_proj = (
        rotate_back(
            grad_query.reshape(token_count, local_heads, head_width), cosine_lookup, sine_lookup
        )
        .astype(jnp.bfloat16)
        .reshape(token_count, local_heads * head_width)
    )
    grad_key_proj = (
        rotate_back(grad_keys, cosine_lookup, sine_lookup)
        .astype(jnp.bfloat16)
        .reshape(token_count, local_kv * head_width)
    )
    grad_value_proj = grad_values.astype(jnp.bfloat16).reshape(token_count, local_kv * head_width)
    grad_w_query = jnp.einsum(
        "rf,rd->fd", grad_query_proj, first_normalized, preferred_element_type=jnp.float32
    )
    grad_w_key = jnp.einsum(
        "rf,rd->fd", grad_key_proj, first_normalized, preferred_element_type=jnp.float32
    )
    grad_w_value = jnp.einsum(
        "rf,rd->fd", grad_value_proj, first_normalized, preferred_element_type=jnp.float32
    )
    grad_normed_one = jnp.einsum(
        "rf,fd->rd", grad_query_proj, w_query, preferred_element_type=jnp.float32
    )
    grad_normed_one = grad_normed_one + jnp.einsum(
        "rf,fd->rd", grad_key_proj, key_projection_weight, preferred_element_type=jnp.float32
    )
    grad_normed_one = grad_normed_one + jnp.einsum(
        "rf,fd->rd", grad_value_proj, value_projection_weight, preferred_element_type=jnp.float32
    )
    grad_gain_attn = jnp.sum(grad_normed_one * first_normalized.astype(jnp.float32), axis=0)
    small = jnp.concatenate(
        [grad_router, grad_gain_ffn[None, :], (grad_gain_attn / gain_one)[None, :]], axis=0
    )
    grad_w_query, grad_w_key, grad_w_value = (
        lax.psum(g.astype(jnp.bfloat16), "ep").astype(jnp.float32)
        for g in (grad_w_query, grad_w_key, grad_w_value)
    )
    grad_one_own = group_totals(grad_normed_one.astype(jnp.bfloat16))
    small = lax.psum(small, ("ep", "tp"))
    grad_input = grad_middle + norm_back(inputs_own, scale_one, gain_one, grad_one_own)
    grad_router = small[:expert_count]
    grad_gain_ffn, grad_gain_attn = small[expert_count], small[expert_count + 1]
    return (
        output_own,
        grad_input,
        grad_gain_attn,
        grad_w_query,
        grad_w_key,
        grad_w_value,
        grad_w_out,
        grad_gain_ffn,
        grad_router,
        owned[0],
        owned[1],
        owned[2].reshape(w_down.shape),
    )


def solution(mesh):
    placed = (
        P(("ep", "tp"), None),
        P(),
        P("tp", None),
        P("tp", None),
        P("tp", None),
        P("tp", None),
        P(),
        P(),
        P("ep", None, "tp"),
        P("ep", None, "tp"),
        P("ep", "tp", None),
        P("ep", None),
        P("ep", None),
        P("ep"),
        P("ep"),
        P(("ep", "tp"), None),
    )
    return jax.shard_map(
        local,
        mesh=mesh,
        in_specs=placed,
        out_specs=(
            P(("ep", "tp"), None),
            P(("ep", "tp"), None),
            P(),
            P("tp", None),
            P("tp", None),
            P("tp", None),
            P("tp", None),
            P(),
            P(),
            P("ep", None, "tp"),
            P("ep", None, "tp"),
            P("ep", "tp", None),
        ),
        check_vma=False,
    )
```

```python
import functools

import jax
import jax.numpy as jnp
from jax import lax
from jax.experimental import pallas as pl
from jax.experimental.pallas import tpu as pltpu
from jax.sharding import PartitionSpec as P

HEAD_DIMENSION = 64
TREE_TOKENS = 512
CAP = 2304


EPSILON = 1e-06
ROPE_BASE = 10000.0
EXACT_PRECISION = lax.Precision.HIGHEST


def rope_tables(position, head_width):
    half_width = head_width // 2
    freqs = ROPE_BASE ** (-(jnp.arange(half_width, dtype=jnp.float32) * 2.0 / head_width))
    angle = position.astype(jnp.float32)[:, None] * freqs[None, :]
    return (jnp.cos(angle)[:, None, :], jnp.sin(angle)[:, None, :])


def apply_rotation(value_rows, cosine_lookup, sine_lookup):
    half_width = value_rows.shape[-1] // 2
    first = value_rows[..., :half_width]
    second = value_rows[..., half_width:]
    return jnp.concatenate(
        [
            first * cosine_lookup - second * sine_lookup,
            first * sine_lookup + second * cosine_lookup,
        ],
        axis=-1,
    )


def rotate_back(grads, cosine_lookup, sine_lookup):
    half_width = grads.shape[-1] // 2
    first = grads[..., :half_width]
    second = grads[..., half_width:]
    return jnp.concatenate(
        [
            first * cosine_lookup + second * sine_lookup,
            second * cosine_lookup - first * sine_lookup,
        ],
        axis=-1,
    )


def norm_scale(value_rows):
    return lax.rsqrt(jnp.mean(value_rows * value_rows, axis=-1, keepdims=True) + EPSILON)


def norm_back(value_rows, scale, gain, grad_normed):
    weighted = grad_normed * gain
    inner = jnp.mean(value_rows * weighted, axis=-1, keepdims=True)
    grad_values = scale * weighted - value_rows * (scale * scale * scale) * inner
    return grad_values


MESH = pl.DeviceIdType.MESH


class Place:
    def __init__(self, ep_size):
        self.depth = ep_size // 2
        ep, tp = lax.axis_index("ep"), lax.axis_index("tp")
        self.z, self.y = ep // 2, ep % 2
        self.x, self.c = tp // 2, tp % 2

    def device(self, z=None, y=None, x=None, c=None):
        z = self.z if z is None else z
        y = self.y if y is None else y
        x = self.x if x is None else x
        c = self.c if c is None else c
        return (z * 2 + y, x * 2 + c)

    def sibling(self):
        return self.device(c=1 - self.c)

    def x_peer(self):
        return self.device(x=1 - self.x)

    def y_peer(self):
        return self.device(y=1 - self.y)

    def target(self, step):
        side = 1 - 2 * (self.z % 2)
        offset = 2 * (1 - step % 2) + side * (1 - step // 2)
        return lax.rem(self.z + offset + self.depth, self.depth)

    def z_peer(self, step):
        return self.device(z=self.target((1, 1, 2)[step]))


def meet(devices):
    barrier = pltpu.get_barrier_semaphore()
    for device in devices:
        pl.semaphore_signal(barrier, inc=1, device_id=device, device_id_type=MESH)
    pl.semaphore_wait(barrier, len(devices))


def send(src, dst, send_sem, recv_sem, device):
    copy = pltpu.make_async_remote_copy(
        src_ref=src,
        dst_ref=dst,
        send_sem=send_sem,
        recv_sem=recv_sem,
        device_id=device,
        device_id_type=MESH,
    )
    copy.start()
    return copy


def add_into(target, other):
    def tile(i, carry):
        at = pl.ds(pl.multiple_of(i * 16, 16), 16)
        target[at, :] = target[at, :] + other[at, :]
        return carry

    lax.fori_loop(0, target.shape[0] // 16, tile, 0)


def group_gather_body(me, pieces, own, out, own_sem, sems):
    size = own.shape[0] // pieces
    started = []
    local = pltpu.make_async_copy(own, out.at[me.x, me.c], own_sem)
    local.start()

    def at(p):
        return pl.ds(p * size, size)

    def go(kind, p, src, dst, device):
        slot = kind * pieces + p
        started.append(send(src, dst, sems.at[0, slot], sems.at[1, slot], device))

    for p in range(pieces):
        go(0, p, own.at[at(p)], out.at[me.x, me.c, at(p)], me.x_peer())
    for p in range(pieces):
        go(1, p, own.at[at(p)], out.at[me.x, me.c, at(p)], me.sibling())
    for p in range(pieces):
        block = out.at[1 - me.x, me.c, at(p)]
        pltpu.make_async_copy(block, block, sems.at[1, p]).wait()
        go(2, p, block, block, me.sibling())
    for p in range(pieces):
        for kind, x in ((1, me.x), (2, 1 - me.x)):
            block = out.at[x, 1 - me.c, at(p)]
            pltpu.make_async_copy(block, block, sems.at[1, kind * pieces + p]).wait()
    local.wait()
    for copy in started:
        copy.wait_send()


class GroupTotal:
    def __init__(self, me, parts, core_got, pair_got, sems):
        self.me, self.parts, self.core_got, self.pair_got = me, parts, core_got, pair_got
        self.core = [
            pltpu.make_async_remote_copy(
                src_ref=parts.at[x, 1 - me.c],
                dst_ref=core_got.at[x],
                send_sem=sems.at[0, k],
                recv_sem=sems.at[1, k],
                device_id=me.sibling(),
                device_id_type=MESH,
            )
            for k, x in enumerate((1 - me.x, me.x))
        ]
        self.pair = pltpu.make_async_remote_copy(
            src_ref=core_got.at[1 - me.x],
            dst_ref=pair_got,
            send_sem=sems.at[0, 2],
            recv_sem=sems.at[1, 2],
            device_id=me.x_peer(),
            device_id_type=MESH,
        )

    def begin(self):
        for copy in self.core:
            copy.start()

    def exchange(self):
        self.core[0].wait_recv()
        far = 1 - self.me.x
        add_into(self.core_got.at[far], self.parts.at[far, self.me.c])
        self.pair.start()

    def finish(self, out, change=lambda value, at: value):
        self.core[1].wait_recv()
        self.pair.wait_recv()

        def tile(i, carry):
            at = pl.ds(pl.multiple_of(i * 16, 16), 16)
            value = (
                self.parts[self.me.x, self.me.c, at, :].astype(jnp.float32)
                + self.core_got[self.me.x, at, :].astype(jnp.float32)
                + self.pair_got[at, :].astype(jnp.float32)
            )
            out[at, :] = change(value, at)
            return carry

        lax.fori_loop(0, out.shape[0] // 16, tile, 0)

    def sent(self):
        for copy in self.core + [self.pair]:
            copy.wait_send()


def all_others(ep_size):
    ep, tp = lax.axis_index("ep"), lax.axis_index("tp")
    return [
        (lax.rem(ep + k // 4, ep_size), lax.rem(tp + k % 4, 4)) for k in range(1, ep_size * 4)
    ]


def experts_kernel(
    ep_size,
    per_owner,
    rows_in,
    cots_in,
    code_in,
    router,
    enter_own,
    enter_peer,
    leave_own,
    leave_peer,
    grad_out,
    sum_out,
    small_out,
    gate_out,
    up_out,
    down_out,
    gate_peer,
    up_peer,
    down_peer,
    rows_buf,
    cots_buf,
    weighted,
    turned,
    enter_sum,
    down_sum,
    parts,
    core_got,
    y_got,
    z_got,
    small_in,
    small_got,
    load_sems,
    core_sems,
    y_sems,
    z_sems,
    small_sems,
    own_sem,
):
    me = Place(ep_size)
    depth = me.depth
    blocks = 2 * depth
    width = router.shape[1]
    share = rows_buf.shape[2]
    tokens = 2 * share
    hidden = leave_own.shape[0]
    units = hidden // per_owner
    f32, bf16 = jnp.float32, jnp.bfloat16
    ep = lax.axis_index("ep")
    others = [
        (lax.rem(ep + k // 2, ep_size), me.x * 2 + lax.rem(me.c + k % 2, 2))
        for k in range(1, 2 * ep_size)
    ]
    meet(others)
    my_place = ep * 2 + me.c
    halves = ((enter_own, leave_own), (enter_peer, leave_peer))

    def where(b):
        return me.target(b // 2), lax.rem(1 - me.y + b % 2, 2)

    def load(b, which):
        z, y = where(b)
        source, target = ((rows_in, rows_buf), (cots_in, cots_buf))[which]
        slot = lax.rem(b, 2)
        return pltpu.make_async_copy(
            source.at[z, y], target.at[slot], load_sems.at[slot, which]
        )

    def core_copy(b):
        return pltpu.make_async_remote_copy(
            src_ref=parts.at[lax.rem(b, 2), :, 1 - me.c],
            dst_ref=core_got.at[b // 2, where(b)[1]],
            send_sem=core_sems.at[0, b],
            recv_sem=core_sems.at[1, b],
            device_id=me.sibling(),
            device_id_type=MESH,
        )

    def y_copy(step, which):
        return pltpu.make_async_remote_copy(
            src_ref=core_got.at[step, 1 - me.y, which],
            dst_ref=y_got.at[step, which],
            send_sem=y_sems.at[0, step, which],
            recv_sem=y_sems.at[1, step, which],
            device_id=me.y_peer(),
            device_id_type=MESH,
        )

    def z_copy(step, which):
        return pltpu.make_async_remote_copy(
            src_ref=y_got.at[step, which],
            dst_ref=z_got.at[step, which],
            send_sem=z_sems.at[0, step, which],
            recv_sem=z_sems.at[1, step, which],
            device_id=me.z_peer(step),
            device_id_type=MESH,
        )

    def small_copy(k, device):
        return pltpu.make_async_remote_copy(
            src_ref=small_in.at[device[0] * 2 + device[1] % 2],
            dst_ref=small_got.at[my_place],
            send_sem=small_sems.at[0, k],
            recv_sem=small_sems.at[1, k],
            device_id=device,
            device_id_type=MESH,
        )

    def dot(a, b, contract):
        return lax.dot_general(
            a, b, ((contract[:1], contract[1:]), ((), ())), preferred_element_type=f32
        )

    def spread(columns):
        return jnp.concatenate(
            [jnp.broadcast_to(columns[:, e : e + 1], (tokens, units)) for e in range(per_owner)],
            axis=1,
        )

    def compute(b):
        z, y = where(b)
        slot = lax.rem(b, 2)
        rows = rows_buf[slot].reshape(tokens, width)
        cots = cots_buf[slot].reshape(tokens, width)
        code = code_in[z * 2 + y, me.x].astype(f32).reshape(tokens, -1)
        used = code >= 0.0
        logits = jnp.where(used, dot(rows, router[...], (1, 1)), -1e30)
        top = jnp.max(logits, axis=1, keepdims=True)
        powers = jnp.where(used, jnp.exp(logits - top), 0.0)
        kept = jnp.where(code == 0.0, 1.0, 0.0)
        gates = spread(kept * powers / jnp.sum(powers, axis=1, keepdims=True))
        products = jnp.zeros((tokens, hidden), f32)
        for h, (enter, leave) in enumerate(halves):
            act = dot(rows, enter[...], (1, 0))
            gate_act, up_act = act[:, :hidden], act[:, hidden:]
            back_act = dot(cots, leave[...], (1, 1))
            sigma = jax.nn.sigmoid(gate_act)
            swish = gate_act * sigma
            value = swish * up_act
            products = products + value * back_act
            weighted[:, h * hidden : (h + 1) * hidden] = (gates * value).astype(bf16)
            grad_hidden = gates * back_act
            at = 2 * h * hidden
            turned[:, at : at + hidden] = (
                grad_hidden * up_act * sigma * (1.0 + gate_act * (1.0 - sigma))
            ).astype(bf16)
            turned[:, at + hidden : at + 2 * hidden] = (grad_hidden * swish).astype(bf16)
        lane = lax.broadcasted_iota(jnp.int32, (8, hidden), 1)
        pick = lax.broadcasted_iota(jnp.int32, (8, hidden), 0)
        mine = jnp.where((lane >= pick * units) & (lane < (pick + 1) * units), 1.0, 0.0)
        grad_gates = lax.dot_general(
            mine,
            spread(kept) * products,
            (((1,), (1,)), ((), ())),
            precision=EXACT_PRECISION,
            preferred_element_type=f32,
        )
        for k in range(2):
            small_in[(z * 2 + y) * 2 + k] = grad_gates[:, k * share : (k + 1) * share]
        tile = 512
        for n in range(width // tile):
            cols = slice(n * tile, (n + 1) * tile)
            grads = (
                dot(turned[:, : 2 * hidden], enter_own[cols, :], (1, 1))
                + dot(turned[:, 2 * hidden :], enter_peer[cols, :], (1, 1))
            ).astype(bf16)
            sums = (
                dot(weighted[:, :hidden], leave_own[:, cols], (1, 0))
                + dot(weighted[:, hidden:], leave_peer[:, cols], (1, 0))
            ).astype(bf16)
            for c in range(2):
                at = slice(c * share, (c + 1) * share)
                parts[slot, 0, c, :, cols] = grads[at]
                parts[slot, 1, c, :, cols] = sums[at]

    def weight_sums(b):
        slot = lax.rem(b, 2)
        tile = 512
        for n in range(width // tile):
            cols = slice(n * tile, (n + 1) * tile)
            rows = rows_buf[slot, :, :, cols].reshape(tokens, tile)
            cots = cots_buf[slot, :, :, cols].reshape(tokens, tile)
            enter_sum[:, cols] += dot(turned[...], rows, (0, 0))
            down_sum[:, cols] += dot(weighted[...], cots, (0, 0))

    enter_sum[...] = jnp.zeros_like(enter_sum)
    down_sum[...] = jnp.zeros_like(down_sum)
    for which in range(2):
        load(0, which).start()

    def during(i, lag, body, parity=None):
        b = i - lag
        inside = (b >= 0) & (b < blocks)
        if parity is not None:
            inside &= lax.rem(b + 2 * lag, 2) == parity
        pl.when(inside)(lambda: body(b))

    def work(b):
        for which in range(2):
            load(b, which).wait()

        @pl.when(b + 1 < blocks)
        def _():
            for which in range(2):
                load(b + 1, which).start()

        compute(b)
        core_copy(b).start()
        weight_sums(b)

    def core_sum(b):
        step, y = b // 2, where(b)[1]
        core_copy(b).wait_recv()
        for which in range(2):
            add_into(core_got.at[step, y, which], parts.at[lax.rem(b, 2), which, me.c])

        @pl.when(b % 2 == 0)
        def _():
            for which in range(2):
                y_copy(step, which).start()

        core_copy(b).wait_send()

    def y_sum(which):
        def body(b):
            step = b // 2
            y_copy(step, which).wait_recv()
            add_into(y_got.at[step, which], core_got.at[step, me.y, which])
            for k in range(2):
                pl.when(step == k)(lambda: z_copy(k, which).start())

            @pl.when(step == 2)
            def _():
                z_copy(0, which).wait_recv()
                add_into(y_got.at[2, which], z_got.at[0, which])
                z_copy(2, which).start()

        return body

    def small_send(b):
        for k, device in enumerate(others):
            small_copy(k, device).start()
        pltpu.make_async_copy(small_in.at[my_place], small_got.at[my_place], own_sem).start()
        for e in range(per_owner):
            own, peer = e * units, 2 * hidden + e * units
            gate_out[e] = enter_sum[own : own + units, :].T
            up_out[e] = enter_sum[hidden + own : hidden + own + units, :].T
            gate_peer[e] = enter_sum[peer : peer + units, :].T.astype(bf16)
            up_peer[e] = enter_sum[hidden + peer : hidden + peer + units, :].T.astype(bf16)
        down_out[...] = down_sum[:hidden, :]
        down_peer[...] = down_sum[hidden:, :].astype(bf16)

    def turn(i, carry):
        during(i, 0, work)
        during(i, 1, core_sum, 1)
        during(i, 2, y_sum(0), 0)
        during(i, 3, y_sum(1), 0)
        during(i, 0, core_sum, 0)
        pl.when(i == blocks)(lambda: small_send(i))
        return carry

    lax.fori_loop(0, blocks + 2, turn, 0)
    pltpu.make_async_copy(small_in.at[my_place], small_got.at[my_place], own_sem).wait()
    for k, device in enumerate(others):
        small_copy(k, device).wait()
    for k in range(ep_size):
        small_out[k] = small_got[2 * k] + small_got[2 * k + 1]
    for step in range(1, 3):
        for which in range(2):
            z_copy(step, which).wait_recv()

    def finish(which, target):
        def tile(i, carry):
            at = pl.ds(pl.multiple_of(i * 16, 16), 16)
            total = y_got[depth - 1, which, at, :].astype(f32)
            for step in range(1, 3):
                total = total + z_got[step, which, at, :].astype(f32)
            target[at, :] = total
            return carry

        lax.fori_loop(0, share // 16, tile, 0)

    finish(0, grad_out)
    finish(1, sum_out)
    for step in range(depth):
        for which in range(2):
            y_copy(step, which).wait_send()
            if step < depth - 1:
                z_copy(step, which).wait_send()


def experts_by_links(rows_all, cots_all, code, router, weights, per_owner, ep_size):
    depth, _, _, rows, width = rows_all.shape
    hidden = weights[2].shape[0]
    units = hidden // per_owner
    bf16, f32 = jnp.bfloat16, jnp.float32
    dma = pltpu.SemaphoreType.DMA
    vmem = pl.BlockSpec(memory_space=pltpu.VMEM)
    anywhere = pl.BlockSpec(memory_space=pltpu.HBM)
    places = 2 * ep_size
    return pl.pallas_call(
        functools.partial(experts_kernel, ep_size, per_owner),
        out_shape=(
            jax.ShapeDtypeStruct((rows, width), f32),
            jax.ShapeDtypeStruct((rows, width), f32),
            jax.ShapeDtypeStruct((ep_size, 8, rows), f32),
            jax.ShapeDtypeStruct((per_owner, width, units), f32),
            jax.ShapeDtypeStruct((per_owner, width, units), f32),
            jax.ShapeDtypeStruct((hidden, width), f32),
            jax.ShapeDtypeStruct((per_owner, width, units), bf16),
            jax.ShapeDtypeStruct((per_owner, width, units), bf16),
            jax.ShapeDtypeStruct((hidden, width), bf16),
        ),
        in_specs=[anywhere, anywhere] + [vmem] * 6,
        out_specs=(vmem,) * 9,
        scratch_shapes=[
            pltpu.VMEM((2, 2, rows, width), bf16),
            pltpu.VMEM((2, 2, rows, width), bf16),
            pltpu.VMEM((2 * rows, 2 * hidden), bf16),
            pltpu.VMEM((2 * rows, 4 * hidden), bf16),
            pltpu.VMEM((4 * hidden, width), f32),
            pltpu.VMEM((2 * hidden, width), f32),
            pltpu.VMEM((2, 2, 2, rows, width), bf16),
            pltpu.VMEM((depth, 2, 2, rows, width), bf16),
            pltpu.VMEM((depth, 2, rows, width), bf16),
            pltpu.VMEM((depth - 1, 2, rows, width), bf16),
            pltpu.VMEM((places, 8, rows), f32),
            pltpu.VMEM((places, 8, rows), f32),
            dma((2, 2)),
            dma((2, 2 * depth)),
            dma((2, depth, 2)),
            dma((2, depth - 1, 2)),
            dma((2, places - 1)),
            dma,
        ],
        compiler_params=pltpu.CompilerParams(
            collective_id=2, has_side_effects=True, vmem_limit_bytes=60 * 1024 * 1024
        ),
        name="experts_by_links",
    )(rows_all, cots_all, code.reshape(ep_size, 2, 2, rows, -1), router, *weights)


class LinkGather:
    def __init__(self, me, own, out, own_sem, z_sems, y_sems, core_sems):
        self.me, self.own, self.out = me, own, out
        self.own_sem, self.z_sems, self.y_sems, self.core_sems = own_sem, z_sems, y_sems, core_sems
        self.begun = []
        depth = me.depth
        self.found = [(me.z, 0, None)]
        for d in range(1, depth):
            self.found.append((me.z - d, d, me.z >= d))
            self.found.append((me.z + d, depth - 1 + d, me.z + d < depth))

    def guard(self, *conditions):
        given = [c for c in conditions if c is not None]
        if not given:
            return lambda body: body()
        total = given[0]
        for c in given[1:]:
            total = total & c
        return pl.when(total)

    def go(self, source, place, sems, slot, device, *conditions):
        def copy():
            return pltpu.make_async_remote_copy(
                src_ref=source,
                dst_ref=place,
                send_sem=sems.at[0, slot],
                recv_sem=sems.at[1, slot],
                device_id=device,
                device_id_type=MESH,
            )

        self.guard(*conditions)(lambda: copy().start())
        self.begun.append((copy, conditions))

    def landed(self, place, sems, slot, condition):
        self.guard(condition)(
            lambda: pltpu.make_async_copy(place, place, sems.at[1, slot]).wait()
        )

    def up(self, source, place, d, condition):
        me = self.me
        device = me.device(z=lax.rem(me.z + 1, me.depth))
        self.go(source, place, self.z_sems, d, device, condition, me.z < me.depth - 1)

    def down(self, source, place, d, condition):
        me = self.me
        device = me.device(z=lax.rem(me.z + me.depth - 1, me.depth))
        self.go(source, place, self.z_sems, me.depth - 1 + d, device, condition, me.z > 0)

    def place(self, z, y, c):
        at = (lax.rem(z + self.me.depth, self.me.depth), y)
        return self.out.at[at + (c,) if self.core_sems is not None else at]

    def to_sibling(self, block, slot, *conditions):
        if self.core_sems is not None:
            self.go(block[0], block[1], self.core_sems, slot, self.me.sibling(), *conditions)

    def begin(self):
        me = self.me
        mine = self.place(me.z, me.y, me.c)
        self.up(self.own, mine, 1, None)
        self.down(self.own, mine, 1, None)
        self.go(self.own, mine, self.y_sems, 0, me.y_peer())
        if self.core_sems is None:
            return
        self.to_sibling((self.own, mine), 0)
        self.local = pltpu.make_async_copy(self.own, mine, self.own_sem)
        self.local.start()

    def relay(self, d):
        me = self.me
        for z, slot, condition in self.found[2 * d - 1 : 2 * d + 1]:
            block = self.place(z, me.y, me.c)
            self.landed(block, self.z_sems, slot, condition)
            if d < me.depth - 1:
                (self.up if slot < me.depth else self.down)(block, block, d + 1, condition)
            self.go(block, block, self.y_sems, slot, me.y_peer(), condition)
            self.to_sibling((block, block), slot, condition)

    def cross(self, first, last):
        me = self.me
        for z, slot, condition in self.found[first:last]:
            block = self.place(z, 1 - me.y, me.c)
            self.landed(block, self.y_sems, slot, condition)
            self.to_sibling((block, block), 2 * me.depth - 1 + slot, condition)

    def finish(self):
        me = self.me
        for z, slot, condition in self.found:
            for y, at in ((me.y, slot), (1 - me.y, 2 * me.depth - 1 + slot)):
                self.landed(self.place(z, y, 1 - me.c), self.core_sems, at, condition)
        self.local.wait()
        self.sent()

    def sent(self):
        for copy, conditions in self.begun:
            self.guard(*conditions)(lambda: copy().wait_send())


class EpSum:
    def __init__(self, me, grads, y_got, z_got, final, sems):
        self.me, self.grads = me, grads
        self.y_got, self.z_got, self.final = y_got, z_got, final
        self.y_sems, self.z_sems, self.fz_sems, self.fy_sems = sems

    def y_copy(self, step):
        me = self.me
        return pltpu.make_async_remote_copy(
            src_ref=self.grads.at[me.target(step), 1 - me.y],
            dst_ref=self.y_got.at[step],
            send_sem=self.y_sems.at[0, step],
            recv_sem=self.y_sems.at[1, step],
            device_id=me.y_peer(),
            device_id_type=MESH,
        )

    def z_copy(self, step):
        return pltpu.make_async_remote_copy(
            src_ref=self.y_got.at[step],
            dst_ref=self.z_got.at[step],
            send_sem=self.z_sems.at[0, step],
            recv_sem=self.z_sems.at[1, step],
            device_id=self.me.z_peer(step),
            device_id_type=MESH,
        )

    def begin(self):
        for step in range(self.me.depth):
            self.y_copy(step).start()

    def fold(self, step):
        me = self.me
        self.y_copy(step).wait_recv()
        add_into(self.y_got.at[step], self.grads.at[me.target(step), me.y])
        if step == 2:
            self.z_copy(0).wait_recv()
            add_into(self.y_got.at[2], self.z_got.at[0])
        if step < me.depth - 1:
            self.z_copy(step).start()

    def settle(self):
        me, depth = self.me, self.me.depth
        for step in range(1, 3):
            self.z_copy(step).wait_recv()

        def tile(i, carry):
            at = pl.ds(pl.multiple_of(i * 16, 16), 16)
            value = self.y_got[depth - 1, at, :].astype(jnp.float32)
            for step in range(1, 3):
                value = value + self.z_got[step, at, :].astype(jnp.float32)
            self.final[me.z, me.y, at, :] = value.astype(self.final.dtype)
            return carry

        lax.fori_loop(0, self.final.shape[2] // 16, tile, 0)
        mine = self.final.at[me.z, me.y]
        self.spread = LinkGather(me, mine, self.final, None, self.fz_sems, self.fy_sems, None)
        self.spread.begin()

    def relay(self, d):
        self.spread.relay(d)

    def finish(self):
        self.spread.cross(0, 2 * self.me.depth - 1)

    def sent(self):
        self.spread.sent()
        for step in range(self.me.depth):
            self.y_copy(step).wait_send()
            if step < self.me.depth - 1:
                self.z_copy(step).wait_send()


def tree_bias(segment, position):
    query_seg, query_pos = segment[...].reshape(1, -1), position[...].reshape(1, -1)
    table = jnp.concatenate([query_seg] * 4 + [query_pos] * 4, axis=0).astype(jnp.float32).T
    key_seg, key_pos = table[:, 0:1].astype(jnp.int32), table[:, 4:5].astype(jnp.int32)
    parent = jnp.where(query_seg >= 5, (query_seg - 5) // 2 + 1, -1)
    above = (key_seg == query_seg) | (key_seg == 0) | (key_seg == parent)
    return jnp.where(above & (key_pos <= query_pos), 0.0, -1e30)


def front_kernel(
    ep_size,
    heads,
    inputs,
    gain_one,
    gain_two,
    w_query,
    w_key,
    w_value,
    w_out,
    cosine,
    sine,
    segment,
    position,
    table,
    cots,
    enter_near,
    leave_near,
    rows_out,
    queries,
    keys,
    values,
    heads_out,
    log_sums,
    middle,
    tables,
    cots_all,
    normed_all,
    normed_own,
    enter_far,
    leave_far,
    first_own,
    bias,
    parts,
    core_got,
    pair_got,
    own_sem,
    gather_sems,
    table_own_sem,
    table_sems,
    group_sems,
    far_sems,
    cots_sems,
    normed_sems,
):
    me = Place(ep_size)
    depth = me.depth
    f32, bf16 = jnp.float32, jnp.bfloat16
    share, width = inputs.shape
    tokens = 4 * share
    size = HEAD_DIMENSION
    groups = keys.shape[1] // size
    per_group = heads // groups
    scale = size ** (-0.5)
    ep, tp = lax.axis_index("ep"), lax.axis_index("tp")
    peers = [(lax.rem(ep + k, ep_size), tp) for k in range(1, ep_size)]
    meet([me.sibling(), me.x_peer()] + peers)

    def dot(a, b, contract):
        return lax.dot_general(
            a, b, ((contract[:1], contract[1:]), ((), ())), preferred_element_type=f32
        )

    first_gain = gain_one[...].astype(f32).reshape(1, width)
    second_gain = gain_two[...].astype(f32).reshape(1, width)
    cots_gather = LinkGather(me, cots, cots_all, *cots_sems)
    cots_gather.begin()
    for i in range(share // 16):
        at = slice(i * 16, (i + 1) * 16)
        value = inputs[at, :].astype(f32)
        first_own[at, :] = (value * norm_scale(value) * first_gain).astype(bf16)
    table_local = pltpu.make_async_copy(table, tables.at[ep], table_own_sem)
    table_local.start()
    table_copies = [
        send(table, tables.at[ep], table_sems.at[0, k], table_sems.at[1, k], device)
        for k, device in enumerate(peers)
    ]
    bias[...] = tree_bias(segment, position)
    log_sums[...] = jnp.zeros_like(log_sums)
    group_gather_body(me, 4, first_own, rows_out, own_sem, gather_sems)

    early = width // 3

    def to_peer(i):
        source, target = ((leave_near, leave_far), (enter_near, enter_far))[min(i, 1)]
        at = (pl.ds(0, leave_near.shape[0]), pl.ds(0, early), pl.ds(early, width - early))[i]
        return send(source.at[at], target.at[at], far_sems.at[0, i], far_sems.at[1, i], me.x_peer())

    exchanged = [to_peer(0)]
    cots_gather.relay(1)
    rows = rows_out[...].reshape(tokens, width)

    def rotate(part):
        turned = jnp.concatenate([part[:, size // 2 :], part[:, : size // 2]], axis=1)
        return (part * cosine[...] - turned * sine[...]).astype(bf16)

    projected = dot(rows, w_query[...], (1, 1))
    for head in range(heads):
        mine = slice(head * size, (head + 1) * size)
        queries[:, mine] = rotate(projected[:, mine] * scale)
    projected = dot(rows, w_key[...], (1, 1))
    for group in range(groups):
        mine = slice(group * size, (group + 1) * size)
        keys[:, mine] = rotate(projected[:, mine])
    values[...] = dot(rows, w_value[...], (1, 1)).astype(bf16)
    for head in range(heads):
        mine = slice(head * size, (head + 1) * size)
        shared = slice(head // per_group * size, (head // per_group + 1) * size)
        scores = dot(keys[:, shared], queries[:, mine], (1, 1)) + bias[...]
        top = jnp.max(scores, axis=0, keepdims=True)
        powers = jnp.exp(scores - top)
        total = jnp.sum(powers, axis=0, keepdims=True)
        log_sums[head : head + 1, :] = top + jnp.log(total)
        probs = (powers * (1.0 / total)).astype(bf16)
        heads_out[:, mine] = dot(probs, values[:, shared], (0, 0)).astype(bf16)
        if head == 1:
            cots_gather.relay(2)
    tile = 512
    for n in range(width // tile):
        cols = slice(n * tile, (n + 1) * tile)
        sums = dot(heads_out[...], w_out[:, cols], (1, 0)).astype(bf16)
        parts[:, :, :, cols] = sums.reshape(2, 2, share, tile)
    group = GroupTotal(me, parts, core_got, pair_got, group_sems)
    group.begin()
    for step in range(3, depth):
        cots_gather.relay(step)
    group.exchange()
    exchanged += [to_peer(1), to_peer(2)]
    cots_gather.cross(0, 3)

    def last(value, at):
        total = inputs[at, :].astype(f32) + value
        normed_own[at, :] = (total * norm_scale(total) * second_gain).astype(bf16)
        return total

    group.finish(middle, last)
    normed_gather = LinkGather(me, normed_own, normed_all, *normed_sems)
    normed_gather.begin()
    cots_gather.cross(3, 2 * depth - 1)
    for step in range(1, depth):
        normed_gather.relay(step)
    normed_gather.cross(0, 2 * depth - 1)
    cots_gather.finish()
    normed_gather.finish()
    group.sent()
    table_local.wait()
    for copy in table_copies + exchanged:
        copy.wait()


def token_tables(segment, position):
    cosine, sine = rope_tables(position, HEAD_DIMENSION)
    return (
        jnp.concatenate([cosine[:, 0], cosine[:, 0]], axis=1),
        jnp.concatenate([sine[:, 0], -sine[:, 0]], axis=1),
        segment,
        position,
    )


def front_by_links(inputs, gains, projections, w_out, tables, order, cots, near, ep_size):
    share, width = inputs.shape
    depth = ep_size // 2
    tokens = 4 * share
    heads = w_out.shape[0] // HEAD_DIMENSION
    bf16, f32 = jnp.bfloat16, jnp.float32
    dma = pltpu.SemaphoreType.DMA
    vmem, anywhere = pl.BlockSpec(memory_space=pltpu.VMEM), pl.BlockSpec(memory_space=pltpu.HBM)

    def like(*shape, dtype=bf16):
        return jax.ShapeDtypeStruct(shape, dtype)

    def gather_sems():
        return (dma, dma((2, 2 * depth)), dma((2, 2 * depth)), dma((2, 4 * depth)))

    widths = [w.shape[0] for w in projections]
    everywhere = (depth, 2, 2, share, width)
    return pl.pallas_call(
        functools.partial(front_kernel, ep_size, heads),
        out_shape=(
            like(2, 2, share, width),
            like(tokens, widths[0]),
            like(tokens, widths[1]),
            like(tokens, widths[2]),
            like(tokens, widths[0]),
            like(8, tokens, dtype=f32),
            like(share, width, dtype=f32),
            like(ep_size, *order.shape, dtype=order.dtype),
            like(*everywhere),
            like(*everywhere),
            like(share, width),
            like(*near[0].shape),
            like(*near[1].shape),
        ),
        in_specs=[vmem] * 11 + [anywhere] * 4,
        out_specs=(vmem,) * 7 + (anywhere,) * 3 + (vmem,) + (anywhere,) * 2,
        scratch_shapes=[
            pltpu.VMEM((share, width), bf16),
            pltpu.VMEM((tokens, tokens), f32),
            pltpu.VMEM((2, 2, share, width), bf16),
            pltpu.VMEM((2, share, width), bf16),
            pltpu.VMEM((share, width), bf16),
            dma,
            dma((2, 12)),
            dma,
            dma((2, ep_size - 1)),
            dma((2, 3)),
            dma((2, 3)),
            gather_sems(),
            gather_sems(),
        ],
        compiler_params=pltpu.CompilerParams(
            collective_id=6, has_side_effects=True, vmem_limit_bytes=56 * 1024 * 1024
        ),
        name="front_by_links",
    )(
        inputs,
        *gains,
        *projections,
        w_out,
        *tables,
        order,
        cots,
        *near,
    )


def back_kernel(
    ep_size,
    heads,
    last_row,
    datt_own,
    heads_in,
    w_out,
    queries,
    keys,
    values,
    log_sums,
    segment,
    position,
    cosine,
    sine,
    rows_in,
    w_query,
    w_key,
    w_value,
    small_in,
    gain,
    inputs,
    middle,
    gate_peer,
    up_peer,
    down_peer,
    first_final,
    second_final,
    out_final,
    grad_input,
    small_out,
    gate_got,
    up_got,
    down_got,
    datt,
    bias,
    grad_heads,
    grad_proj,
    key_sum,
    value_sum,
    part_proj,
    part_out,
    y_got,
    z_got,
    y_got_out,
    z_got_out,
    parts,
    core_got,
    pair_got,
    small_src,
    small_got,
    small_sum,
    own_sem,
    gather_sems,
    y_sems,
    z_sems,
    fz_sems,
    fy_sems,
    y_sems_out,
    z_sems_out,
    fz_sems_out,
    fy_sems_out,
    group_sems,
    small_sems,
    spread_sems,
    own_small_sem,
    peer_sems,
):
    me = Place(ep_size)
    depth = me.depth
    f32, bf16 = jnp.float32, jnp.bfloat16
    others = all_others(ep_size)
    meet(others)
    my_place = lax.axis_index("ep") * 4 + lax.axis_index("tp")
    tokens, width = rows_in.shape
    share = datt_own.shape[0]
    size = HEAD_DIMENSION
    groups = keys.shape[1] // size
    per_group = heads // groups
    scale = size ** (-0.5)
    tile = 512

    def dot(a, b, contract):
        return lax.dot_general(
            a, b, ((contract[:1], contract[1:]), ((), ())), preferred_element_type=f32
        )

    bias[...] = tree_bias(segment, position)
    group_gather_body(me, 4, datt_own, datt, own_sem, gather_sems)

    def to_peer(i):
        source, target = ((gate_peer, gate_got), (up_peer, up_got), (down_peer, down_got))[i]
        return send(source, target, peer_sems.at[0, i], peer_sems.at[1, i], me.x_peer())

    exchanged = [to_peer(i) for i in range(3)]
    for n in range(width // tile):
        cols = slice(n * tile, (n + 1) * tile)
        grads = dot(heads_in[...], datt[:, :, :, cols].reshape(tokens, tile), (0, 0))
        part_out[:, :, :, cols] = grads.astype(bf16).reshape(depth, 2, -1, tile)
    out_sum = EpSum(
        me,
        part_out,
        y_got_out,
        z_got_out,
        out_final,
        (y_sems_out, z_sems_out, fz_sems_out, fy_sems_out),
    )
    out_sum.begin()
    for x in range(2):
        for c in range(2):
            at = pl.ds((x * 2 + c) * share, share)
            grad_heads[at, :] = dot(datt[x, c], w_out[...], (1, 1)).astype(bf16)

    def rotate_back_rows(grads):
        turned = jnp.concatenate([grads[:, size // 2 :], grads[:, : size // 2]], axis=1)
        return (grads * cosine[...] + turned * sine[...]).astype(bf16)

    for head in range(heads):
        group = head // per_group
        mine = slice(head * size, (head + 1) * size)
        shared = slice(group * size, (group + 1) * size)
        query, grad_head = queries[:, mine], grad_heads[:, mine]
        key, value = keys[:, shared], values[:, shared]
        scores = dot(key, query, (1, 1)) + bias[...]
        probs = jnp.exp(scores - log_sums[head : head + 1, :])
        grad_probs = dot(value, grad_head, (1, 1))
        inner = jnp.sum(probs * grad_probs, axis=0, keepdims=True)
        grad_scores = (probs * (grad_probs - inner)).astype(bf16)
        grad_value = dot(probs.astype(bf16), grad_head, (1, 0))
        grad_key = dot(grad_scores, query, (1, 0))
        if head % per_group:
            grad_value = grad_value + value_sum[...]
            grad_key = grad_key + key_sum[...]
        value_sum[...] = grad_value
        key_sum[...] = grad_key
        grad_query = dot(grad_scores, key, (0, 0)) * scale
        grad_proj[:, mine] = rotate_back_rows(grad_query)
        if head % per_group == per_group - 1:
            at = heads * size + group * size
            grad_proj[:, at : at + size] = rotate_back_rows(grad_key)
            at += groups * size
            grad_proj[:, at : at + size] = grad_value.astype(bf16)
        if head % 2 and head // 2 < depth - 2:
            out_sum.fold(head // 2)
    folded = min(heads // 2, depth - 2)

    ends = (heads * size, (heads + groups) * size, (heads + 2 * groups) * size)
    wide = width // 2
    sums = []
    for n, final in enumerate((first_final, second_final)):
        cols = slice(n * wide, (n + 1) * wide)
        grads = dot(grad_proj[...], rows_in[:, cols], (0, 0)).astype(bf16)
        at, first = 0, 0
        for end in ends:
            piece = grads[first:end].reshape(depth, 2, -1, wide)
            part_proj[n, :, :, at : at + piece.shape[2]] = piece
            at, first = at + piece.shape[2], end
        sums.append(
            EpSum(
                me,
                part_proj.at[n],
                y_got.at[n],
                z_got.at[n],
                final,
                (y_sems.at[n], z_sems.at[n], fz_sems.at[n], fy_sems.at[n]),
            )
        )
        if n == 1:
            sums[0].fold(0)
            for step in range(max(folded, depth - 1), depth):
                out_sum.fold(step)
            sums[0].fold(1)
        sums[n].begin()
        if n == 0:
            for step in range(folded, depth - 1):
                out_sum.fold(step)
    first_sum, second_sum = sums
    small_src[...] = small_in[...]
    own_gain = gain[...].astype(f32).reshape(1, width)
    for n in range(width // tile):
        cols = slice(n * tile, (n + 1) * tile)
        grads = (
            dot(grad_proj[:, : ends[0]], w_query[:, cols], (1, 0))
            + dot(grad_proj[:, ends[0] : ends[1]], w_key[:, cols], (1, 0))
            + dot(grad_proj[:, ends[1] :], w_value[:, cols], (1, 0))
        )
        parts[:, :, :, cols] = grads.astype(bf16).reshape(2, 2, share, tile)
        gained = jnp.sum(grads * rows_in[:, cols].astype(f32), axis=0, keepdims=True)
        gained = gained / own_gain[:, cols]
        for k in range(tile // 128):
            row = n * (tile // 128) + k
            small_src[last_row, row : row + 1, :] = gained[:, k * 128 : (k + 1) * 128]
    for step in range(2, depth - 1):
        first_sum.fold(step)
    out_sum.settle()
    small = [
        send(
            small_src.at[device[0] * 4 + device[1]],
            small_got.at[my_place],
            small_sems.at[0, k],
            small_sems.at[1, k],
            device,
        )
        for k, device in enumerate(others)
    ]
    own_small = pltpu.make_async_copy(
        small_src.at[my_place], small_got.at[my_place], own_small_sem
    )
    own_small.start()
    second_sum.fold(0)
    first_sum.fold(depth - 1)
    first_sum.settle()
    out_sum.relay(1)
    second_sum.fold(1)
    own_small.wait()
    for copy in small:
        copy.wait_recv()
    total = small_got[0]
    for k in range(1, 4 * ep_size):
        total = total + small_got[k]
    small_sum[...] = total
    spread = [
        send(
            small_sum,
            small_out.at[my_place],
            spread_sems.at[0, k],
            spread_sems.at[1, k],
            device,
        )
        for k, device in enumerate(others)
    ]
    small_out[my_place] = total
    group = GroupTotal(me, parts, core_got, pair_got, group_sems)
    group.begin()
    out_sum.relay(2)
    for step in range(2, depth - 1):
        second_sum.fold(step)
    group.exchange()
    first_sum.relay(1)
    second_sum.fold(depth - 1)
    for step in range(3, depth):
        out_sum.relay(step)
    second_sum.settle()
    out_sum.finish()
    first_sum.relay(2)

    def last(value, at):
        values_own = inputs[at, :].astype(f32)
        factor = norm_scale(values_own)
        return middle[at, :] + norm_back(values_own, factor, own_gain, value)

    group.finish(grad_input, last)
    second_sum.relay(1)
    for step in range(3, depth):
        first_sum.relay(step)
    for step in range(2, depth):
        second_sum.relay(step)
    first_sum.finish()
    second_sum.finish()
    for copy in spread:
        copy.wait()
    for copy in small:
        copy.wait_send()
    group.sent()
    for each in [out_sum] + sums:
        each.sent()
    for copy in exchanged:
        copy.wait()


def back_by_links(
    datt_own,
    heads_in,
    w_out,
    queries,
    keys,
    values,
    log_sums,
    tables,
    rows_in,
    w_query,
    w_key,
    w_value,
    small,
    gain,
    inputs,
    middle,
    peers,
    ep_size,
):
    tokens, width = rows_in.shape
    share = datt_own.shape[0]
    depth = ep_size // 2
    heads = queries.shape[1] // HEAD_DIMENSION
    places = 4 * ep_size
    bf16, f32 = jnp.bfloat16, jnp.float32
    dma = pltpu.SemaphoreType.DMA
    vmem = pl.BlockSpec(memory_space=pltpu.VMEM)
    anywhere = pl.BlockSpec(memory_space=pltpu.HBM)
    cosine, sine, segment, position = tables
    blocks = jnp.pad(small, ((0, places - small.shape[0]), (0, 0))).reshape(places, -1, 128)
    sizes = [w.shape[0] // ep_size for w in (w_query, w_key, w_value, w_out)]
    total = sum(sizes[:3])

    def partial(rows, columns):
        return (depth, 2, rows, columns), bf16

    wide = width // 2
    got = pl.pallas_call(
        functools.partial(back_kernel, ep_size, heads, small.shape[0]),
        out_shape=(
            jax.ShapeDtypeStruct(*partial(total, wide)),
            jax.ShapeDtypeStruct(*partial(total, wide)),
            jax.ShapeDtypeStruct(*partial(sizes[3], width)),
            jax.ShapeDtypeStruct((share, width), f32),
            jax.ShapeDtypeStruct(blocks.shape, f32),
        )
        + tuple(jax.ShapeDtypeStruct(p.shape, p.dtype) for p in peers),
        in_specs=[vmem] * 19 + [anywhere] * 3,
        out_specs=(vmem,) * 5 + (anywhere,) * 3,
        scratch_shapes=[
            pltpu.VMEM((2, 2, share, width), bf16),
            pltpu.VMEM((tokens, tokens), f32),
            pltpu.VMEM(queries.shape, bf16),
            pltpu.VMEM((tokens, queries.shape[1] + 2 * keys.shape[1]), bf16),
            pltpu.VMEM((tokens, HEAD_DIMENSION), f32),
            pltpu.VMEM((tokens, HEAD_DIMENSION), f32),
        ]
        + [
            pltpu.VMEM((2, depth, 2, total, wide), bf16),
            pltpu.VMEM((depth, 2, sizes[3], width), bf16),
            pltpu.VMEM((2, depth, total, wide), bf16),
            pltpu.VMEM((2, depth - 1, total, wide), bf16),
            pltpu.VMEM((depth, sizes[3], width), bf16),
            pltpu.VMEM((depth - 1, sizes[3], width), bf16),
            pltpu.VMEM((2, 2, share, width), bf16),
            pltpu.VMEM((2, share, width), bf16),
            pltpu.VMEM((share, width), bf16),
            pltpu.VMEM(blocks.shape, f32),
            pltpu.VMEM(blocks.shape, f32),
            pltpu.VMEM(blocks.shape[1:], f32),
            dma,
            dma((2, 12)),
        ]
        + [dma((2, 2, depth)), dma((2, 2, depth))]
        + [dma((2, 2, 2 * depth))] * 2
        + [dma((2, depth)), dma((2, depth))]
        + [dma((2, 2 * depth))] * 2
        + [dma((2, 3)), dma((2, places - 1)), dma((2, places - 1)), dma, dma((2, 3))],
        compiler_params=pltpu.CompilerParams(
            collective_id=5, has_side_effects=True, vmem_limit_bytes=60 * 1024 * 1024
        ),
        name="back_by_links",
    )(
        datt_own,
        heads_in,
        w_out,
        queries,
        keys,
        values,
        log_sums,
        segment,
        position,
        cosine,
        sine,
        rows_in,
        w_query,
        w_key,
        w_value,
        blocks,
        gain,
        inputs,
        middle,
        *peers,
    )
    return got


def deliver_kernel(
    ep_size,
    sizes,
    rows_in,
    sums_in,
    gate_in,
    up_in,
    down_in,
    gate_got,
    up_got,
    down_got,
    first_in,
    second_in,
    third_in,
    small,
    gate_out,
    up_out,
    down_out,
    rows_out,
    sums_out,
    query_out,
    key_out,
    value_out,
    out_out,
    router_out,
    first_gain,
    second_gain,
    query,
    key,
    value,
    out,
    gate,
    up,
    down,
    gate_far,
    up_far,
    down_far,
    first,
    second,
    third,
    rows,
    sums,
    sems,
    load_sems,
):
    loads = [
        pltpu.make_async_copy(source, target, load_sems.at[i])
        for i, (source, target) in enumerate(
            (
                (third_in, third),
                (first_in, first),
                (second_in, second),
                (gate_in, gate),
                (gate_got, gate_far),
                (up_in, up),
                (up_got, up_far),
                (down_in, down),
                (down_got, down_far),
                (rows_in, rows),
                (sums_in, sums),
            )
        )
    ]
    for load in loads:
        load.start()
    copies = []
    wide = first.shape[2]
    f32 = jnp.float32

    def leave(source, target, i):
        copies.append(pltpu.make_async_copy(source, target, sems.at[i]))
        copies[-1].start()

    loads[0].wait()
    out[...] = third[...].astype(f32)
    leave(out, out_out, 5)
    for load in loads[1:3]:
        load.wait()
    at = 0
    for i, (source, target) in enumerate(((query, query_out), (key, key_out), (value, value_out))):
        for n, part in enumerate((first, second)):
            source[:, :, n * wide : (n + 1) * wide] = part[:, at : at + sizes[i], :].astype(f32)
        at += sizes[i]
        leave(source, target, 6 + i)
    for i, (total, far) in enumerate(((gate, gate_far), (up, up_far), (down, down_far))):
        for load in loads[3 + 2 * i : 5 + 2 * i]:
            load.wait()
        total[...] = total[...] + far[...].astype(f32)
        leave(total, (gate_out, up_out, down_out)[i], 2 + i)
    for load in loads[9:]:
        load.wait()
    leave(rows, rows_out, 0)
    leave(sums, sums_out, 1)
    experts = router_out.shape[0]
    for j in range(small.shape[1]):
        cols = slice(j * 128, (j + 1) * 128)
        router_out[:, cols] = small[:experts, j, :]
        first_gain[cols] = small[experts + 1, j, :]
        second_gain[cols] = small[experts, j, :]
    for copy in copies:
        copy.wait()


def deliver(owned, peers, rows, sums, got, small, sizes, expert_count, ep_size):
    width = rows.shape[1]
    f32 = jnp.float32
    vmem, anywhere = pl.BlockSpec(memory_space=pltpu.VMEM), pl.BlockSpec(memory_space=pltpu.HBM)
    first, second, third = (g.reshape((ep_size,) + g.shape[2:]) for g in got)

    def like(value):
        return jax.ShapeDtypeStruct(value.shape, value.dtype)

    shapes = [(ep_size, k, width) for k in sizes]
    results = pl.pallas_call(
        functools.partial(deliver_kernel, ep_size, sizes),
        out_shape=tuple(like(a) for a in owned)
        + (like(rows), like(sums))
        + tuple(jax.ShapeDtypeStruct(shape, f32) for shape in shapes)
        + (
            jax.ShapeDtypeStruct((expert_count, width), f32),
            jax.ShapeDtypeStruct((width,), f32),
            jax.ShapeDtypeStruct((width,), f32),
        ),
        in_specs=[anywhere] * 11 + [vmem],
        out_specs=(anywhere,) * 9 + (vmem,) * 3,
        scratch_shapes=[pltpu.VMEM(shape, f32) for shape in shapes]
        + [pltpu.VMEM(a.shape, a.dtype) for a in (*owned, *peers, first, second, third)]
        + [pltpu.VMEM(a.shape, a.dtype) for a in (rows, sums)]
        + [pltpu.SemaphoreType.DMA((9,)), pltpu.SemaphoreType.DMA((11,))],
        compiler_params=pltpu.CompilerParams(vmem_limit_bytes=60 * 1024 * 1024),
        name="deliver",
    )(rows, sums, *owned, *peers, first, second, third, small)
    gate, up, down, rows, sums = results[:5]
    query, key, value, out = (g.reshape(-1, width) for g in results[5:9])
    router, first_gain, second_gain = results[9:]
    return (
        sums,
        rows,
        first_gain,
        query,
        key,
        value,
        out,
        second_gain,
        router,
        gate,
        up,
        down.reshape(gate.shape[0], -1, width),
    )


def group_rows(value_rows):
    return lax.all_gather(value_rows, "tp", axis=0, tiled=True)


def group_totals(value_rows):
    return lax.psum_scatter(value_rows, "tp", scatter_dimension=0, tiled=True).astype(jnp.float32)


def gather_all(value_rows):
    return lax.all_gather(value_rows, ("ep", "tp"), axis=0, tiled=True)


LAST = 1 << 30


def pair_order(expert_ids, slot_order, expert_count):
    experts = jnp.arange(expert_count, dtype=jnp.int32)
    chosen = expert_ids.T[None, :, :] == experts[:, None, None]
    return jnp.min(jnp.where(chosen, slot_order.T[None, :, :], LAST), axis=1)


def kept_pairs(order):
    used = order < LAST
    counts = jnp.sum(used.astype(jnp.int32), axis=2)
    block = jnp.arange(order.shape[0], dtype=jnp.int32)
    earlier = block[None, :] < block[:, None]
    offsets = jnp.sum(jnp.where(earlier[:, :, None], counts[None, :, :], 0), axis=1)
    whole = offsets + counts <= CAP
    edge = (offsets < CAP) & ~whole
    edge_order = jnp.sum(jnp.where(edge[:, :, None], order, 0), axis=0)
    rank = jnp.sum((edge_order[:, :, None] < edge_order[:, None, :]).astype(jnp.int32), axis=1)
    early = offsets[:, :, None] + rank[None, :, :] < CAP
    return used & (whole[:, :, None] | (edge[:, :, None] & early))


def masked_softmax(logits, used):
    top = jnp.max(jnp.where(used, logits, -1e30), axis=-1, keepdims=True)
    powers = jnp.where(used, jnp.exp(logits - top), 0.0)
    return powers / jnp.sum(powers, axis=-1, keepdims=True)


def pair_codes(order_all, per_owner):
    expert_count = order_all.shape[1]
    first = lax.axis_index("ep") * per_owner
    turned = jnp.roll(order_all, -first, axis=1)
    kept = kept_pairs(turned[:, :per_owner])
    dropped = jnp.pad(~kept, ((0, 0), (0, expert_count - per_owner), (0, 0)))
    code = jnp.where(turned < LAST, dropped.astype(jnp.float32), -1.0)
    return code.swapaxes(1, 2).reshape(-1, expert_count).astype(jnp.bfloat16)


def expert_weights(w_gate, w_up, w_down):
    enter = jnp.concatenate([w[e] for w in (w_gate, w_up) for e in range(w.shape[0])], axis=1)
    return enter, w_down.reshape(-1, w_down.shape[2])


def run_experts(rows_all, cots_all, code, w_router, w_gate, w_up, w_down, weights, by_links):
    per_owner, width, units = w_gate.shape
    expert_count = w_router.shape[0]
    ep_size, tp_size = lax.axis_size("ep"), lax.axis_size("tp")
    hidden = per_owner * units
    router = jnp.roll(w_router, -lax.axis_index("ep") * per_owner, axis=0)
    if by_links:
        grads, sums, small, *owned = experts_by_links(
            rows_all, cots_all, code, router, weights, per_owner, ep_size
        )
        share = grads.shape[0]
        return (
            grads,
            sums,
            small[:, :per_owner].reshape(expert_count, share).T,
            owned[:3],
            owned[3:],
        )
    enter, leave = expert_weights(w_gate, w_up, w_down)
    used, kept = code >= 0, (code == 0).astype(jnp.float32)
    logits = jnp.einsum("rd,ed->re", rows_all, router, preferred_element_type=jnp.float32)
    gates = jnp.repeat((kept * masked_softmax(logits, used))[:, :per_owner], units, axis=1)
    act = jnp.dot(rows_all, enter, preferred_element_type=jnp.float32)
    gate_act, up_act = act[:, :hidden], act[:, hidden:]
    back_act = jnp.einsum("rd,fd->rf", cots_all, leave, preferred_element_type=jnp.float32)
    sigma = jax.nn.sigmoid(gate_act)
    value = gate_act * sigma * up_act
    weighted = (gates * value).astype(jnp.bfloat16)
    grad_hidden = gates * back_act
    turned = jnp.concatenate(
        [
            grad_hidden * up_act * sigma * (1.0 + gate_act * (1.0 - sigma)),
            grad_hidden * gate_act * sigma,
        ],
        axis=1,
    ).astype(jnp.bfloat16)
    small = kept[:, :per_owner] * jnp.sum((value * back_act).reshape(-1, per_owner, units), axis=2)
    grads = jnp.einsum("rf,df->rd", turned, enter, preferred_element_type=jnp.float32)
    sums = jnp.dot(weighted, leave, preferred_element_type=jnp.float32)

    def scatter(value_rows):
        return lax.psum_scatter(value_rows, ("ep", "tp"), scatter_dimension=0, tiled=True)

    columns = lax.dynamic_update_slice_in_dim(
        jnp.zeros((small.shape[0], expert_count), jnp.float32),
        small,
        lax.axis_index("ep") * per_owner,
        1,
    )
    both = jnp.einsum(
        "rd,rwef->wedf",
        rows_all,
        turned.reshape(-1, 2, per_owner, units),
        preferred_element_type=jnp.float32,
    )
    down = jnp.einsum("rf,rd->fd", weighted, cots_all, preferred_element_type=jnp.float32)
    return (
        scatter(grads.astype(jnp.bfloat16)).astype(jnp.float32),
        scatter(sums.astype(jnp.bfloat16)).astype(jnp.float32),
        scatter(columns),
        (both[0], both[1], down),
        None,
    )


def visible_block(query_seg, query_pos, query_row, key_seg, key_pos, key_row):
    seg_q = query_seg[:, None]
    seg_k = key_seg[None, :]
    above = (
        (seg_k == seg_q)
        | (seg_k == 0)
        | (seg_k >= 1) & (seg_k <= 4) & (seg_q >= 5) & ((seg_q - 5) // 2 + 1 == seg_k)
    )
    same_tree = query_row[:, None] // TREE_TOKENS == key_row[None, :] // TREE_TOKENS
    return above & same_tree & (key_pos[None, :] <= query_pos[:, None])


def block_scores(query_part, key_rows, allowed, scale):
    scores = (
        jnp.einsum("qkgd,pkd->kgqp", query_part, key_rows, preferred_element_type=jnp.float32)
        * scale
    )
    return jnp.where(allowed[None, None], scores, -1e30)


def attend_forward(query_rows, key_rows, value_rows, segment, position):
    total_rows = query_rows.shape[0]
    scale = query_rows.shape[-1] ** (-0.5)
    row_ids = jnp.arange(total_rows, dtype=jnp.int32)
    allowed = visible_block(segment, position, row_ids, segment, position, row_ids)
    scores = block_scores(query_rows, key_rows, allowed, scale)
    top_score = jnp.max(scores, axis=-1, keepdims=True)
    weights = jnp.exp(scores - top_score)
    weight_sum = jnp.sum(weights, axis=-1, keepdims=True)
    probs = (weights / weight_sum).astype(jnp.bfloat16)
    outputs = jnp.einsum(
        "kgqp,pkd->qkgd", probs, value_rows, preferred_element_type=jnp.float32
    ).astype(jnp.bfloat16)
    log_sums = [top_score + jnp.log(weight_sum)]
    return (outputs, log_sums)


def attend_backward(
    query_rows, key_rows, value_rows, segment, position, log_sums, grad_heads, block_rows
):
    total_rows = query_rows.shape[0]
    scale = query_rows.shape[-1] ** (-0.5)
    row_ids = jnp.arange(total_rows, dtype=jnp.int32)
    grad_keys = jnp.zeros(key_rows.shape, jnp.float32)
    grad_values = jnp.zeros(value_rows.shape, jnp.float32)
    grad_query = []
    for number, first_row in enumerate(range(0, total_rows, block_rows)):
        allowed = visible_block(segment, position, row_ids, segment, position, row_ids)
        scores = block_scores(query_rows, key_rows, allowed, scale)
        probs = jnp.where(allowed[None, None], jnp.exp(scores - log_sums[number]), 0.0)
        grad_values = jnp.einsum(
            "kgqp,qkgd->pkd",
            probs.astype(jnp.bfloat16),
            grad_heads,
            preferred_element_type=jnp.float32,
        )
        grad_probs = jnp.einsum(
            "qkgd,pkd->kgqp", grad_heads, value_rows, preferred_element_type=jnp.float32
        )
        inner = jnp.sum(probs * grad_probs, axis=-1, keepdims=True)
        grad_scores = (probs * (grad_probs - inner)).astype(jnp.bfloat16)
        grad_query.append(
            jnp.einsum("kgqp,pkd->qkgd", grad_scores, key_rows, preferred_element_type=jnp.float32)
            * scale
        )
        grad_keys = (
            jnp.einsum(
                "kgqp,qkgd->pkd", grad_scores, query_rows, preferred_element_type=jnp.float32
            )
            * scale
        )
    return (grad_query[0], grad_keys, grad_values)


def local(
    hidden_in,
    gain_attn,
    w_query,
    key_projection_weight,
    value_projection_weight,
    w_out,
    gain_ffn,
    w_router,
    w_gate,
    w_up,
    w_down,
    expert_ids,
    slot_order,
    segment,
    position,
    cotangent,
):
    model_width = w_query.shape[1]
    head_width = HEAD_DIMENSION
    local_heads = w_query.shape[0] // head_width
    local_kv = key_projection_weight.shape[0] // head_width
    group_factor = local_heads // local_kv
    token_count = expert_ids.shape[0]
    share = hidden_in.shape[0]
    row_start = lax.axis_index("tp") * share
    expert_count = w_router.shape[0]
    per_owner = w_gate.shape[0]
    block_rows = 512
    by_links = lax.axis_size("tp") == 4 and lax.axis_size("ep") == 8
    order = pair_order(expert_ids, slot_order, expert_count)
    gain_one = gain_attn.astype(jnp.float32)
    gain_two = gain_ffn.astype(jnp.float32)
    inputs_own = hidden_in.astype(jnp.float32)
    if by_links:
        near = expert_weights(w_gate, w_up, w_down)
        token_info = token_tables(segment, position)
        (
            first_normalized,
            query_rows,
            key_rows,
            value_rows,
            head_outputs,
            log_sums,
            middle_own,
            order_all,
            cot_all,
            normed_two,
            normed_own,
            *far,
        ) = front_by_links(
            hidden_in,
            (gain_attn, gain_ffn),
            (w_query, key_projection_weight, value_projection_weight),
            w_out,
            token_info,
            order,
            cotangent,
            near,
            lax.axis_size("ep"),
        )
        weights = (near[0], far[0], near[1], far[1])
        scale_two = norm_scale(middle_own)
    else:
        weights = None
        scale_one = norm_scale(inputs_own)
        first_normalized = group_rows((inputs_own * scale_one * gain_one).astype(jnp.bfloat16))
        order_all = lax.all_gather(order, "ep")
        cosine_lookup, sine_lookup = rope_tables(position, head_width)
        query_proj = jnp.einsum(
            "rd,fd->rf", first_normalized, w_query, preferred_element_type=jnp.float32
        ).reshape(token_count, local_heads, head_width)
        key_proj = jnp.einsum(
            "rd,fd->rf", first_normalized, key_projection_weight, preferred_element_type=jnp.float32
        ).reshape(token_count, local_kv, head_width)
        query_rows = (
            apply_rotation(query_proj, cosine_lookup, sine_lookup)
            .astype(jnp.bfloat16)
            .reshape(token_count, local_kv, group_factor, head_width)
        )
        key_rows = apply_rotation(key_proj, cosine_lookup, sine_lookup).astype(jnp.bfloat16)
        value_rows = (
            jnp.einsum(
                "rd,fd->rf",
                first_normalized,
                value_projection_weight,
                preferred_element_type=jnp.float32,
            )
            .astype(jnp.bfloat16)
            .reshape(token_count, local_kv, head_width)
        )
        head_outputs, log_sums = attend_forward(query_rows, key_rows, value_rows, segment, position)
        head_outputs = head_outputs.reshape(token_count, local_heads * head_width)
        middle_own = inputs_own + group_totals(
            jnp.dot(head_outputs, w_out, preferred_element_type=jnp.float32).astype(jnp.bfloat16)
        )
        scale_two = norm_scale(middle_own)
        normed_own = (middle_own * scale_two * gain_two).astype(jnp.bfloat16)
        normed_two, cot_all = gather_all(normed_own), gather_all(cotangent)
    code = pair_codes(order_all, per_owner)
    used = lax.dynamic_slice_in_dim(order, row_start, share, 1).T < LAST
    gates = masked_softmax(
        jnp.einsum("rd,ed->re", normed_own, w_router, preferred_element_type=jnp.float32), used
    )
    grad_normed_own, combined_own, grad_gates_own, owned, peers = run_experts(
        normed_two, cot_all, code, w_router, w_gate, w_up, w_down, weights, by_links
    )
    output_own = (middle_own + combined_own).astype(jnp.bfloat16)
    inner_gate = jnp.sum(gates * grad_gates_own, axis=-1, keepdims=True)
    grad_logits = gates * (grad_gates_own - inner_gate)
    router_f = w_router.astype(jnp.float32)
    grad_normed_own = grad_normed_own + jnp.dot(grad_logits, router_f, precision=EXACT_PRECISION)
    grad_router = jnp.dot(grad_logits.T, normed_own.astype(jnp.float32), precision=EXACT_PRECISION)
    grad_gain_ffn = jnp.sum(grad_normed_own * middle_own * scale_two, axis=0)
    grad_middle = cotangent.astype(jnp.float32) + norm_back(
        middle_own, scale_two, gain_two, grad_normed_own
    )
    if by_links:
        *got, grad_input, small, gate_got, up_got, down_got = back_by_links(
            grad_middle.astype(jnp.bfloat16),
            head_outputs,
            w_out,
            query_rows,
            key_rows,
            value_rows,
            log_sums,
            token_info,
            first_normalized.reshape(token_count, model_width),
            w_query,
            key_projection_weight,
            value_projection_weight,
            jnp.concatenate([grad_router, grad_gain_ffn[None, :]], axis=0),
            gain_attn,
            hidden_in,
            grad_middle,
            peers,
            lax.axis_size("ep"),
        )
        ep_size = lax.axis_size("ep")
        weights = (w_query, key_projection_weight, value_projection_weight, w_out)
        return deliver(
            owned,
            (gate_got, up_got, down_got),
            grad_input,
            output_own,
            got,
            small,
            [w.shape[0] // ep_size for w in weights],
            expert_count,
            ep_size,
        )
    grad_attn = group_rows(grad_middle.astype(jnp.bfloat16))
    grad_w_out = jnp.einsum(
        "rf,rd->fd", head_outputs, grad_attn, preferred_element_type=jnp.float32
    )
    grad_w_out = lax.psum(grad_w_out.astype(jnp.bfloat16), "ep").astype(jnp.float32)
    grad_heads = (
        jnp.einsum("rd,fd->rf", grad_attn, w_out, preferred_element_type=jnp.float32)
        .astype(jnp.bfloat16)
        .reshape(token_count, local_kv, group_factor, head_width)
    )
    grad_query, grad_keys, grad_values = attend_backward(
        query_rows, key_rows, value_rows, segment, position, log_sums, grad_heads, block_rows
    )
    grad_query_proj = (
        rotate_back(
            grad_query.reshape(token_count, local_heads, head_width), cosine_lookup, sine_lookup
        )
        .astype(jnp.bfloat16)
        .reshape(token_count, local_heads * head_width)
    )
    grad_key_proj = (
        rotate_back(grad_keys, cosine_lookup, sine_lookup)
        .astype(jnp.bfloat16)
        .reshape(token_count, local_kv * head_width)
    )
    grad_value_proj = grad_values.astype(jnp.bfloat16).reshape(token_count, local_kv * head_width)
    grad_w_query = jnp.einsum(
        "rf,rd->fd", grad_query_proj, first_normalized, preferred_element_type=jnp.float32
    )
    grad_w_key = jnp.einsum(
        "rf,rd->fd", grad_key_proj, first_normalized, preferred_element_type=jnp.float32
    )
    grad_w_value = jnp.einsum(
        "rf,rd->fd", grad_value_proj, first_normalized, preferred_element_type=jnp.float32
    )
    grad_normed_one = jnp.einsum(
        "rf,fd->rd", grad_query_proj, w_query, preferred_element_type=jnp.float32
    )
    grad_normed_one = grad_normed_one + jnp.einsum(
        "rf,fd->rd", grad_key_proj, key_projection_weight, preferred_element_type=jnp.float32
    )
    grad_normed_one = grad_normed_one + jnp.einsum(
        "rf,fd->rd", grad_value_proj, value_projection_weight, preferred_element_type=jnp.float32
    )
    grad_gain_attn = jnp.sum(grad_normed_one * first_normalized.astype(jnp.float32), axis=0)
    small = jnp.concatenate(
        [grad_router, grad_gain_ffn[None, :], (grad_gain_attn / gain_one)[None, :]], axis=0
    )
    grad_w_query, grad_w_key, grad_w_value = (
        lax.psum(g.astype(jnp.bfloat16), "ep").astype(jnp.float32)
        for g in (grad_w_query, grad_w_key, grad_w_value)
    )
    grad_one_own = group_totals(grad_normed_one.astype(jnp.bfloat16))
    small = lax.psum(small, ("ep", "tp"))
    grad_input = grad_middle + norm_back(inputs_own, scale_one, gain_one, grad_one_own)
    grad_router = small[:expert_count]
    grad_gain_ffn, grad_gain_attn = small[expert_count], small[expert_count + 1]
    return (
        output_own,
        grad_input,
        grad_gain_attn,
        grad_w_query,
        grad_w_key,
        grad_w_value,
        grad_w_out,
        grad_gain_ffn,
        grad_router,
        owned[0],
        owned[1],
        owned[2].reshape(w_down.shape),
    )


def solution(mesh):
    placed = (
        P(("ep", "tp"), None),
        P(),
        P("tp", None),
        P("tp", None),
        P("tp", None),
        P("tp", None),
        P(),
        P(),
        P("ep", None, "tp"),
        P("ep", None, "tp"),
        P("ep", "tp", None),
        P("ep", None),
        P("ep", None),
        P("ep"),
        P("ep"),
        P(("ep", "tp"), None),
    )
    return jax.shard_map(
        local,
        mesh=mesh,
        in_specs=placed,
        out_specs=(
            P(("ep", "tp"), None),
            P(("ep", "tp"), None),
            P(),
            P("tp", None),
            P("tp", None),
            P("tp", None),
            P("tp", None),
            P(),
            P(),
            P("ep", None, "tp"),
            P("ep", None, "tp"),
            P("ep", "tp", None),
        ),
        check_vma=False,
    )
```

```python
import functools

import jax
import jax.numpy as jnp
from jax import lax
from jax.experimental import pallas as pl
from jax.experimental.pallas import tpu as pltpu
from jax.sharding import PartitionSpec as P

HEAD_DIMENSION = 64
TREE_TOKENS = 512
TRUNK = 256
CAP = 2304


EPSILON = 1e-06
ROPE_BASE = 10000.0
EXACT_PRECISION = lax.Precision.HIGHEST


def rope_tables(position, head_width):
    half_width = head_width // 2
    freqs = ROPE_BASE ** (-(jnp.arange(half_width, dtype=jnp.float32) * 2.0 / head_width))
    angle = position.astype(jnp.float32)[:, None] * freqs[None, :]
    return (jnp.cos(angle)[:, None, :], jnp.sin(angle)[:, None, :])


def apply_rotation(value_rows, cosine_lookup, sine_lookup):
    half_width = value_rows.shape[-1] // 2
    first = value_rows[..., :half_width]
    second = value_rows[..., half_width:]
    return jnp.concatenate(
        [
            first * cosine_lookup - second * sine_lookup,
            first * sine_lookup + second * cosine_lookup,
        ],
        axis=-1,
    )


def rotate_back(grads, cosine_lookup, sine_lookup):
    half_width = grads.shape[-1] // 2
    first = grads[..., :half_width]
    second = grads[..., half_width:]
    return jnp.concatenate(
        [
            first * cosine_lookup + second * sine_lookup,
            second * cosine_lookup - first * sine_lookup,
        ],
        axis=-1,
    )


def norm_scale(value_rows):
    return lax.rsqrt(jnp.mean(value_rows * value_rows, axis=-1, keepdims=True) + EPSILON)


def norm_back(value_rows, scale, gain, grad_normed):
    weighted = grad_normed * gain
    inner = jnp.mean(value_rows * weighted, axis=-1, keepdims=True)
    grad_values = scale * weighted - value_rows * (scale * scale * scale) * inner
    return grad_values


MESH = pl.DeviceIdType.MESH


class Place:
    def __init__(self, ep_size):
        self.depth = ep_size // 2
        ep, tp = lax.axis_index("ep"), lax.axis_index("tp")
        self.z, self.y = ep // 2, ep % 2
        self.x, self.c = tp // 2, tp % 2

    def device(self, z=None, y=None, x=None, c=None):
        z = self.z if z is None else z
        y = self.y if y is None else y
        x = self.x if x is None else x
        c = self.c if c is None else c
        return (z * 2 + y, x * 2 + c)

    def sibling(self):
        return self.device(c=1 - self.c)

    def x_peer(self):
        return self.device(x=1 - self.x)

    def y_peer(self):
        return self.device(y=1 - self.y)

    def target(self, step):
        side = 1 - 2 * (self.z % 2)
        offset = 2 * (1 - step % 2) + side * (1 - step // 2)
        return lax.rem(self.z + offset + self.depth, self.depth)

    def z_peer(self, step):
        return self.device(z=self.target((1, 1, 2)[step]))


def meet(devices):
    barrier = pltpu.get_barrier_semaphore()
    for device in devices:
        pl.semaphore_signal(barrier, inc=1, device_id=device, device_id_type=MESH)
    pl.semaphore_wait(barrier, len(devices))


def send(src, dst, send_sem, recv_sem, device):
    copy = pltpu.make_async_remote_copy(
        src_ref=src,
        dst_ref=dst,
        send_sem=send_sem,
        recv_sem=recv_sem,
        device_id=device,
        device_id_type=MESH,
    )
    copy.start()
    return copy


def add_into(target, other):
    def tile(i, carry):
        at = pl.ds(pl.multiple_of(i * 16, 16), 16)
        target[at, :] = target[at, :] + other[at, :]
        return carry

    lax.fori_loop(0, target.shape[0] // 16, tile, 0)


def group_gather_body(me, pieces, own, out, own_sem, sems):
    size = own.shape[0] // pieces
    started = []
    local = pltpu.make_async_copy(own, out.at[me.x, me.c], own_sem)
    local.start()

    def at(p):
        return pl.ds(p * size, size)

    def go(kind, p, src, dst, device):
        slot = kind * pieces + p
        started.append(send(src, dst, sems.at[0, slot], sems.at[1, slot], device))

    for p in range(pieces):
        go(0, p, own.at[at(p)], out.at[me.x, me.c, at(p)], me.x_peer())
    for p in range(pieces):
        go(1, p, own.at[at(p)], out.at[me.x, me.c, at(p)], me.sibling())
    for p in range(pieces):
        block = out.at[1 - me.x, me.c, at(p)]
        pltpu.make_async_copy(block, block, sems.at[1, p]).wait()
        go(2, p, block, block, me.sibling())
    for p in range(pieces):
        for kind, x in ((1, me.x), (2, 1 - me.x)):
            block = out.at[x, 1 - me.c, at(p)]
            pltpu.make_async_copy(block, block, sems.at[1, kind * pieces + p]).wait()
    local.wait()
    for copy in started:
        copy.wait_send()


class GroupTotal:
    def __init__(self, me, parts, core_got, pair_got, sems):
        self.me, self.parts, self.core_got, self.pair_got = me, parts, core_got, pair_got
        self.core = [
            pltpu.make_async_remote_copy(
                src_ref=parts.at[x, 1 - me.c],
                dst_ref=core_got.at[x],
                send_sem=sems.at[0, k],
                recv_sem=sems.at[1, k],
                device_id=me.sibling(),
                device_id_type=MESH,
            )
            for k, x in enumerate((1 - me.x, me.x))
        ]
        self.half = pair_got.shape[0] // 2
        self.pair = [
            pltpu.make_async_remote_copy(
                src_ref=core_got.at[1 - me.x, self.rows(part)],
                dst_ref=pair_got.at[self.rows(part)],
                send_sem=sems.at[0, 2 + part],
                recv_sem=sems.at[1, 2 + part],
                device_id=me.x_peer(),
                device_id_type=MESH,
            )
            for part in range(2)
        ]

    def rows(self, part):
        return pl.ds(part * self.half, self.half)

    def begin(self):
        for copy in self.core:
            copy.start()

    def exchange(self):
        self.core[0].wait_recv()
        far = 1 - self.me.x
        for part, copy in enumerate(self.pair):
            rows = self.rows(part)
            add_into(self.core_got.at[far, rows], self.parts.at[far, self.me.c, rows])
            copy.start()

    def finish(self, out, change, part):
        if part == 0:
            self.core[1].wait_recv()
        self.pair[part].wait_recv()

        def tile(i, carry):
            at = pl.ds(pl.multiple_of(part * self.half + i * 16, 16), 16)
            value = (
                self.parts[self.me.x, self.me.c, at, :].astype(jnp.float32)
                + self.core_got[self.me.x, at, :].astype(jnp.float32)
                + self.pair_got[at, :].astype(jnp.float32)
            )
            out[at, :] = change(value, at)
            return carry

        lax.fori_loop(0, self.half // 16, tile, 0)

    def sent(self):
        for copy in self.core + self.pair:
            copy.wait_send()


def all_others(ep_size):
    ep, tp = lax.axis_index("ep"), lax.axis_index("tp")
    return [
        (lax.rem(ep + k // 4, ep_size), lax.rem(tp + k % 4, 4)) for k in range(1, ep_size * 4)
    ]


def experts_kernel(
    ep_size,
    per_owner,
    rows_in,
    cots_in,
    code_in,
    router,
    enter_own,
    enter_peer,
    leave_own,
    leave_peer,
    grad_out,
    sum_out,
    small_out,
    gate_out,
    up_out,
    down_out,
    gate_peer,
    up_peer,
    down_peer,
    rows_buf,
    cots_buf,
    weighted,
    turned,
    enter_sum,
    down_sum,
    parts,
    core_got,
    y_got,
    z_got,
    small_in,
    small_got,
    load_sems,
    core_sems,
    y_sems,
    z_sems,
    small_sems,
    own_sem,
):
    me = Place(ep_size)
    depth = me.depth
    blocks = 2 * depth
    width = router.shape[1]
    share = rows_buf.shape[2]
    tokens = 2 * share
    hidden = leave_own.shape[0]
    units = hidden // per_owner
    f32, bf16 = jnp.float32, jnp.bfloat16
    ep = lax.axis_index("ep")
    others = [
        (lax.rem(ep + k // 2, ep_size), me.x * 2 + lax.rem(me.c + k % 2, 2))
        for k in range(1, 2 * ep_size)
    ]
    meet(others)
    my_place = ep * 2 + me.c
    halves = ((enter_own, leave_own), (enter_peer, leave_peer))

    def where(b):
        return me.target(b // 2), lax.rem(1 - me.y + b % 2, 2)

    def load(b, which):
        z, y = where(b)
        source, target = ((rows_in, rows_buf), (cots_in, cots_buf))[which]
        slot = lax.rem(b, 2)
        return pltpu.make_async_copy(
            source.at[z, y], target.at[slot], load_sems.at[slot, which]
        )

    def core_copy(b):
        return pltpu.make_async_remote_copy(
            src_ref=parts.at[lax.rem(b, 2), :, 1 - me.c],
            dst_ref=core_got.at[b // 2, where(b)[1]],
            send_sem=core_sems.at[0, b],
            recv_sem=core_sems.at[1, b],
            device_id=me.sibling(),
            device_id_type=MESH,
        )

    def y_copy(step, which):
        return pltpu.make_async_remote_copy(
            src_ref=core_got.at[step, 1 - me.y, which],
            dst_ref=y_got.at[step, which],
            send_sem=y_sems.at[0, step, which],
            recv_sem=y_sems.at[1, step, which],
            device_id=me.y_peer(),
            device_id_type=MESH,
        )

    def z_copy(step, which):
        return pltpu.make_async_remote_copy(
            src_ref=y_got.at[step, which],
            dst_ref=z_got.at[step, which],
            send_sem=z_sems.at[0, step, which],
            recv_sem=z_sems.at[1, step, which],
            device_id=me.z_peer(step),
            device_id_type=MESH,
        )

    def small_copy(k, device):
        return pltpu.make_async_remote_copy(
            src_ref=small_in.at[device[0] * 2 + device[1] % 2],
            dst_ref=small_got.at[my_place],
            send_sem=small_sems.at[0, k],
            recv_sem=small_sems.at[1, k],
            device_id=device,
            device_id_type=MESH,
        )

    def dot(a, b, contract):
        return lax.dot_general(
            a, b, ((contract[:1], contract[1:]), ((), ())), preferred_element_type=f32
        )

    def spread(columns):
        return jnp.concatenate(
            [jnp.broadcast_to(columns[:, e : e + 1], (tokens, units)) for e in range(per_owner)],
            axis=1,
        )

    def compute(b):
        z, y = where(b)
        slot = lax.rem(b, 2)
        rows = rows_buf[slot].reshape(tokens, width)
        cots = cots_buf[slot].reshape(tokens, width)
        code = code_in[z * 2 + y, me.x].astype(f32).reshape(tokens, -1)
        used = code >= 0.0
        logits = jnp.where(used, dot(rows, router[...], (1, 1)), -1e30)
        top = jnp.max(logits, axis=1, keepdims=True)
        powers = jnp.where(used, jnp.exp(logits - top), 0.0)
        kept = jnp.where(code == 0.0, 1.0, 0.0)
        gates = spread(kept * powers / jnp.sum(powers, axis=1, keepdims=True))
        products = jnp.zeros((tokens, hidden), f32)
        for h, (enter, leave) in enumerate(halves):
            act = dot(rows, enter[...], (1, 0))
            gate_act, up_act = act[:, :hidden], act[:, hidden:]
            back_act = dot(cots, leave[...], (1, 1))
            sigma = jax.nn.sigmoid(gate_act)
            swish = gate_act * sigma
            value = swish * up_act
            products = products + value * back_act
            weighted[:, h * hidden : (h + 1) * hidden] = (gates * value).astype(bf16)
            grad_hidden = gates * back_act
            at = 2 * h * hidden
            turned[:, at : at + hidden] = (
                grad_hidden * up_act * sigma * (1.0 + gate_act * (1.0 - sigma))
            ).astype(bf16)
            turned[:, at + hidden : at + 2 * hidden] = (grad_hidden * swish).astype(bf16)
        lane = lax.broadcasted_iota(jnp.int32, (8, hidden), 1)
        pick = lax.broadcasted_iota(jnp.int32, (8, hidden), 0)
        mine = jnp.where((lane >= pick * units) & (lane < (pick + 1) * units), 1.0, 0.0)
        grad_gates = lax.dot_general(
            mine,
            spread(kept) * products,
            (((1,), (1,)), ((), ())),
            precision=EXACT_PRECISION,
            preferred_element_type=f32,
        )
        for k in range(2):
            small_in[(z * 2 + y) * 2 + k] = grad_gates[:, k * share : (k + 1) * share]
        tile = 512
        for n in range(width // tile):
            cols = slice(n * tile, (n + 1) * tile)
            grads = (
                dot(turned[:, : 2 * hidden], enter_own[cols, :], (1, 1))
                + dot(turned[:, 2 * hidden :], enter_peer[cols, :], (1, 1))
            ).astype(bf16)
            sums = (
                dot(weighted[:, :hidden], leave_own[:, cols], (1, 0))
                + dot(weighted[:, hidden:], leave_peer[:, cols], (1, 0))
            ).astype(bf16)
            for c in range(2):
                at = slice(c * share, (c + 1) * share)
                parts[slot, 0, c, :, cols] = grads[at]
                parts[slot, 1, c, :, cols] = sums[at]

    def weight_sums(b):
        slot = lax.rem(b, 2)
        tile = 512
        for n in range(width // tile):
            cols = slice(n * tile, (n + 1) * tile)
            rows = rows_buf[slot, :, :, cols].reshape(tokens, tile)
            cots = cots_buf[slot, :, :, cols].reshape(tokens, tile)
            enter_sum[:, cols] += dot(turned[...], rows, (0, 0))
            down_sum[:, cols] += dot(weighted[...], cots, (0, 0))

    enter_sum[...] = jnp.zeros_like(enter_sum)
    down_sum[...] = jnp.zeros_like(down_sum)
    for which in range(2):
        load(0, which).start()

    def during(i, lag, body, parity=None):
        b = i - lag
        inside = (b >= 0) & (b < blocks)
        if parity is not None:
            inside &= lax.rem(b + 2 * lag, 2) == parity
        pl.when(inside)(lambda: body(b))

    def work(b):
        for which in range(2):
            load(b, which).wait()

        @pl.when(b + 1 < blocks)
        def _():
            for which in range(2):
                load(b + 1, which).start()

        compute(b)
        core_copy(b).start()
        weight_sums(b)

    def core_sum(b):
        step, y = b // 2, where(b)[1]
        core_copy(b).wait_recv()
        for which in range(2):
            add_into(core_got.at[step, y, which], parts.at[lax.rem(b, 2), which, me.c])

        @pl.when(b % 2 == 0)
        def _():
            for which in range(2):
                y_copy(step, which).start()

        core_copy(b).wait_send()

    def y_sum(which):
        def body(b):
            step = b // 2
            y_copy(step, which).wait_recv()
            add_into(y_got.at[step, which], core_got.at[step, me.y, which])
            for k in range(2):
                pl.when(step == k)(lambda: z_copy(k, which).start())

            @pl.when(step == 2)
            def _():
                z_copy(0, which).wait_recv()
                add_into(y_got.at[2, which], z_got.at[0, which])
                z_copy(2, which).start()

        return body

    def small_send(b):
        for k, device in enumerate(others):
            small_copy(k, device).start()
        pltpu.make_async_copy(small_in.at[my_place], small_got.at[my_place], own_sem).start()
        for e in range(per_owner):
            own, peer = e * units, 2 * hidden + e * units
            gate_out[e] = enter_sum[own : own + units, :].T
            up_out[e] = enter_sum[hidden + own : hidden + own + units, :].T
            gate_peer[e] = enter_sum[peer : peer + units, :].T.astype(bf16)
            up_peer[e] = enter_sum[hidden + peer : hidden + peer + units, :].T.astype(bf16)
        down_out[...] = down_sum[:hidden, :]
        down_peer[...] = down_sum[hidden:, :].astype(bf16)

    def turn(i, carry):
        during(i, 0, work)
        during(i, 1, core_sum, 1)
        during(i, 2, y_sum(0), 0)
        during(i, 3, y_sum(1), 0)
        during(i, 0, core_sum, 0)
        pl.when(i == blocks)(lambda: small_send(i))
        return carry

    lax.fori_loop(0, blocks + 2, turn, 0)
    pltpu.make_async_copy(small_in.at[my_place], small_got.at[my_place], own_sem).wait()
    for k, device in enumerate(others):
        small_copy(k, device).wait()
    for k in range(ep_size):
        small_out[k] = small_got[2 * k] + small_got[2 * k + 1]
    for step in range(1, 3):
        for which in range(2):
            z_copy(step, which).wait_recv()

    def finish(which, target):
        def tile(i, carry):
            at = pl.ds(pl.multiple_of(i * 16, 16), 16)
            total = y_got[depth - 1, which, at, :].astype(f32)
            for step in range(1, 3):
                total = total + z_got[step, which, at, :].astype(f32)
            target[at, :] = total
            return carry

        lax.fori_loop(0, share // 16, tile, 0)

    finish(0, grad_out)
    finish(1, sum_out)
    for step in range(depth):
        for which in range(2):
            y_copy(step, which).wait_send()
            if step < depth - 1:
                z_copy(step, which).wait_send()


def experts_by_links(rows_all, cots_all, code, router, weights, per_owner, ep_size):
    depth, _, _, rows, width = rows_all.shape
    hidden = weights[2].shape[0]
    units = hidden // per_owner
    bf16, f32 = jnp.bfloat16, jnp.float32
    dma = pltpu.SemaphoreType.DMA
    vmem = pl.BlockSpec(memory_space=pltpu.VMEM)
    anywhere = pl.BlockSpec(memory_space=pltpu.HBM)
    places = 2 * ep_size
    return pl.pallas_call(
        functools.partial(experts_kernel, ep_size, per_owner),
        out_shape=(
            jax.ShapeDtypeStruct((rows, width), f32),
            jax.ShapeDtypeStruct((rows, width), f32),
            jax.ShapeDtypeStruct((ep_size, 8, rows), f32),
            jax.ShapeDtypeStruct((per_owner, width, units), f32),
            jax.ShapeDtypeStruct((per_owner, width, units), f32),
            jax.ShapeDtypeStruct((hidden, width), f32),
            jax.ShapeDtypeStruct((per_owner, width, units), bf16),
            jax.ShapeDtypeStruct((per_owner, width, units), bf16),
            jax.ShapeDtypeStruct((hidden, width), bf16),
        ),
        in_specs=[anywhere, anywhere] + [vmem] * 6,
        out_specs=(vmem,) * 9,
        scratch_shapes=[
            pltpu.VMEM((2, 2, rows, width), bf16),
            pltpu.VMEM((2, 2, rows, width), bf16),
            pltpu.VMEM((2 * rows, 2 * hidden), bf16),
            pltpu.VMEM((2 * rows, 4 * hidden), bf16),
            pltpu.VMEM((4 * hidden, width), f32),
            pltpu.VMEM((2 * hidden, width), f32),
            pltpu.VMEM((2, 2, 2, rows, width), bf16),
            pltpu.VMEM((depth, 2, 2, rows, width), bf16),
            pltpu.VMEM((depth, 2, rows, width), bf16),
            pltpu.VMEM((depth - 1, 2, rows, width), bf16),
            pltpu.VMEM((places, 8, rows), f32),
            pltpu.VMEM((places, 8, rows), f32),
            dma((2, 2)),
            dma((2, 2 * depth)),
            dma((2, depth, 2)),
            dma((2, depth - 1, 2)),
            dma((2, places - 1)),
            dma,
        ],
        compiler_params=pltpu.CompilerParams(
            collective_id=2, has_side_effects=True, vmem_limit_bytes=60 * 1024 * 1024
        ),
        name="experts_by_links",
    )(rows_all, cots_all, code.reshape(ep_size, 2, 2, rows, -1), router, *weights)


class LinkGather:
    def __init__(self, me, own, out, own_sem, z_sems, y_sems, core_sems, rows=None):
        self.me, self.own, self.out, self.rows = me, own, out, rows
        if rows is not None:
            self.own = own.at[rows]
        self.own_sem, self.z_sems, self.y_sems, self.core_sems = own_sem, z_sems, y_sems, core_sems
        self.begun = []
        depth = me.depth
        self.found = [(me.z, 0, None)]
        for d in range(1, depth):
            self.found.append((me.z - d, d, me.z >= d))
            self.found.append((me.z + d, depth - 1 + d, me.z + d < depth))

    def guard(self, *conditions):
        given = [c for c in conditions if c is not None]
        if not given:
            return lambda body: body()
        total = given[0]
        for c in given[1:]:
            total = total & c
        return pl.when(total)

    def go(self, source, place, sems, slot, device, *conditions):
        def copy():
            return pltpu.make_async_remote_copy(
                src_ref=source,
                dst_ref=place,
                send_sem=sems.at[0, slot],
                recv_sem=sems.at[1, slot],
                device_id=device,
                device_id_type=MESH,
            )

        self.guard(*conditions)(lambda: copy().start())
        self.begun.append((copy, conditions))

    def landed(self, place, sems, slot, condition):
        self.guard(condition)(
            lambda: pltpu.make_async_copy(place, place, sems.at[1, slot]).wait()
        )

    def up(self, source, place, d, condition):
        me = self.me
        device = me.device(z=lax.rem(me.z + 1, me.depth))
        self.go(source, place, self.z_sems, d, device, condition, me.z < me.depth - 1)

    def down(self, source, place, d, condition):
        me = self.me
        device = me.device(z=lax.rem(me.z + me.depth - 1, me.depth))
        self.go(source, place, self.z_sems, me.depth - 1 + d, device, condition, me.z > 0)

    def place(self, z, y, c):
        at = (lax.rem(z + self.me.depth, self.me.depth), y)
        if self.core_sems is not None:
            at += (c,)
        return self.out.at[at if self.rows is None else at + (self.rows,)]

    def to_sibling(self, block, slot, *conditions):
        if self.core_sems is not None:
            self.go(block[0], block[1], self.core_sems, slot, self.me.sibling(), *conditions)

    def begin(self):
        me = self.me
        mine = self.place(me.z, me.y, me.c)
        self.up(self.own, mine, 1, None)
        self.down(self.own, mine, 1, None)
        self.go(self.own, mine, self.y_sems, 0, me.y_peer())
        if self.core_sems is None:
            return
        self.to_sibling((self.own, mine), 0)
        self.local = pltpu.make_async_copy(self.own, mine, self.own_sem)
        self.local.start()

    def relay(self, d):
        me = self.me
        for z, slot, condition in self.found[2 * d - 1 : 2 * d + 1]:
            block = self.place(z, me.y, me.c)
            self.landed(block, self.z_sems, slot, condition)
            if d < me.depth - 1:
                (self.up if slot < me.depth else self.down)(block, block, d + 1, condition)
            self.go(block, block, self.y_sems, slot, me.y_peer(), condition)
            self.to_sibling((block, block), slot, condition)

    def cross(self, first, last):
        me = self.me
        for z, slot, condition in self.found[first:last]:
            block = self.place(z, 1 - me.y, me.c)
            self.landed(block, self.y_sems, slot, condition)
            self.to_sibling((block, block), 2 * me.depth - 1 + slot, condition)

    def finish(self):
        me = self.me
        for z, slot, condition in self.found:
            for y, at in ((me.y, slot), (1 - me.y, 2 * me.depth - 1 + slot)):
                self.landed(self.place(z, y, 1 - me.c), self.core_sems, at, condition)
        self.local.wait()
        self.sent()

    def sent(self):
        for copy, conditions in self.begun:
            self.guard(*conditions)(lambda: copy().wait_send())


class EpSum:
    def __init__(self, me, grads, y_got, z_got, final, sems):
        self.me, self.grads = me, grads
        self.y_got, self.z_got, self.final = y_got, z_got, final
        self.y_sems, self.z_sems, self.fz_sems, self.fy_sems = sems

    def y_copy(self, step):
        me = self.me
        return pltpu.make_async_remote_copy(
            src_ref=self.grads.at[me.target(step), 1 - me.y],
            dst_ref=self.y_got.at[step],
            send_sem=self.y_sems.at[0, step],
            recv_sem=self.y_sems.at[1, step],
            device_id=me.y_peer(),
            device_id_type=MESH,
        )

    def z_copy(self, step):
        return pltpu.make_async_remote_copy(
            src_ref=self.y_got.at[step],
            dst_ref=self.z_got.at[step],
            send_sem=self.z_sems.at[0, step],
            recv_sem=self.z_sems.at[1, step],
            device_id=self.me.z_peer(step),
            device_id_type=MESH,
        )

    def begin(self):
        for step in range(self.me.depth):
            self.y_copy(step).start()

    def fold(self, step):
        me = self.me
        self.y_copy(step).wait_recv()
        add_into(self.y_got.at[step], self.grads.at[me.target(step), me.y])
        if step == 2:
            self.z_copy(0).wait_recv()
            add_into(self.y_got.at[2], self.z_got.at[0])
        if step < me.depth - 1:
            self.z_copy(step).start()

    def settle(self):
        me, depth = self.me, self.me.depth
        for step in range(1, 3):
            self.z_copy(step).wait_recv()

        def tile(i, carry):
            at = pl.ds(pl.multiple_of(i * 16, 16), 16)
            value = self.y_got[depth - 1, at, :].astype(jnp.float32)
            for step in range(1, 3):
                value = value + self.z_got[step, at, :].astype(jnp.float32)
            self.final[me.z, me.y, at, :] = value.astype(self.final.dtype)
            return carry

        lax.fori_loop(0, self.final.shape[2] // 16, tile, 0)
        mine = self.final.at[me.z, me.y]
        self.spread = LinkGather(me, mine, self.final, None, self.fz_sems, self.fy_sems, None)
        self.spread.begin()

    def relay(self, d):
        self.spread.relay(d)

    def finish(self):
        self.spread.cross(0, 2 * self.me.depth - 1)

    def sent(self):
        self.spread.sent()
        for step in range(self.me.depth):
            self.y_copy(step).wait_send()
            if step < self.me.depth - 1:
                self.z_copy(step).wait_send()


def parts_of_tree(tokens):
    return ((slice(0, TRUNK), TRUNK), (slice(TRUNK, tokens), tokens))


def tree_bias(segment, position):
    query_seg, query_pos = segment[...].reshape(1, -1), position[...].reshape(1, -1)
    table = jnp.concatenate([query_seg] * 4 + [query_pos] * 4, axis=0).astype(jnp.float32).T
    key_seg, key_pos = table[:, 0:1].astype(jnp.int32), table[:, 4:5].astype(jnp.int32)
    parent = jnp.where(query_seg >= 5, (query_seg - 5) // 2 + 1, -1)
    above = (key_seg == query_seg) | (key_seg == 0) | (key_seg == parent)
    return jnp.where(above & (key_pos <= query_pos), 0.0, -1e30)


def front_kernel(
    ep_size,
    heads,
    inputs,
    gain_one,
    gain_two,
    w_query,
    w_key,
    w_value,
    w_out,
    cosine,
    sine,
    segment,
    position,
    table,
    cots,
    enter_near,
    leave_near,
    rows_out,
    queries,
    keys,
    values,
    heads_out,
    log_sums,
    middle,
    tables,
    cots_all,
    normed_all,
    normed_own,
    enter_far,
    leave_far,
    first_own,
    bias,
    parts,
    core_got,
    pair_got,
    own_sem,
    gather_sems,
    table_own_sem,
    table_sems,
    group_sems,
    far_sems,
    cots_sems,
    first_sems,
    second_sems,
):
    me = Place(ep_size)
    depth = me.depth
    f32, bf16 = jnp.float32, jnp.bfloat16
    share, width = inputs.shape
    tokens = 4 * share
    size = HEAD_DIMENSION
    groups = keys.shape[1] // size
    per_group = heads // groups
    scale = size ** (-0.5)
    ep, tp = lax.axis_index("ep"), lax.axis_index("tp")
    peers = [(lax.rem(ep + k, ep_size), tp) for k in range(1, ep_size)]
    meet([me.sibling(), me.x_peer()] + peers)

    def dot(a, b, contract):
        return lax.dot_general(
            a, b, ((contract[:1], contract[1:]), ((), ())), preferred_element_type=f32
        )

    first_gain = gain_one[...].astype(f32).reshape(1, width)
    second_gain = gain_two[...].astype(f32).reshape(1, width)
    cots_gather = LinkGather(me, cots, cots_all, *cots_sems)
    cots_gather.begin()
    for i in range(share // 16):
        at = slice(i * 16, (i + 1) * 16)
        value = inputs[at, :].astype(f32)
        first_own[at, :] = (value * norm_scale(value) * first_gain).astype(bf16)
    table_local = pltpu.make_async_copy(table, tables.at[ep], table_own_sem)
    table_local.start()
    table_copies = [
        send(table, tables.at[ep], table_sems.at[0, k], table_sems.at[1, k], device)
        for k, device in enumerate(peers)
    ]
    bias[...] = tree_bias(segment, position)
    log_sums[...] = jnp.zeros_like(log_sums)
    group_gather_body(me, 4, first_own, rows_out, own_sem, gather_sems)

    early = width // 3

    def to_peer(i):
        source, target = ((leave_near, leave_far), (enter_near, enter_far))[min(i, 1)]
        at = (pl.ds(0, leave_near.shape[0]), pl.ds(0, early), pl.ds(early, width - early))[i]
        return send(source.at[at], target.at[at], far_sems.at[0, i], far_sems.at[1, i], me.x_peer())

    exchanged = [to_peer(0)]
    cots_gather.relay(1)
    rows = rows_out[...].reshape(tokens, width)

    def rotate(part):
        turned = jnp.concatenate([part[:, size // 2 :], part[:, : size // 2]], axis=1)
        return (part * cosine[...] - turned * sine[...]).astype(bf16)

    projected = dot(rows, w_query[...], (1, 1))
    for head in range(heads):
        mine = slice(head * size, (head + 1) * size)
        queries[:, mine] = rotate(projected[:, mine] * scale)
    projected = dot(rows, w_key[...], (1, 1))
    for group in range(groups):
        mine = slice(group * size, (group + 1) * size)
        keys[:, mine] = rotate(projected[:, mine])
    values[...] = dot(rows, w_value[...], (1, 1)).astype(bf16)
    for head in range(heads):
        mine = slice(head * size, (head + 1) * size)
        shared = slice(head // per_group * size, (head // per_group + 1) * size)
        for cols, last_key in parts_of_tree(tokens):
            scores = dot(keys[:last_key, shared], queries[cols, mine], (1, 1))
            scores = scores + bias[:last_key, cols]
            top = jnp.max(scores, axis=0, keepdims=True)
            powers = jnp.exp(scores - top)
            total = jnp.sum(powers, axis=0, keepdims=True)
            log_sums[head : head + 1, cols] = top + jnp.log(total)
            probs = (powers * (1.0 / total)).astype(bf16)
            heads_out[cols, mine] = dot(probs, values[:last_key, shared], (0, 0)).astype(bf16)
        if head == 1:
            cots_gather.relay(2)
    tile = 512
    for n in range(width // tile):
        cols = slice(n * tile, (n + 1) * tile)
        sums = dot(heads_out[...], w_out[:, cols], (1, 0)).astype(bf16)
        parts[:, :, :, cols] = sums.reshape(2, 2, share, tile)
    group = GroupTotal(me, parts, core_got, pair_got, group_sems)
    group.begin()
    for step in range(3, depth):
        cots_gather.relay(step)
    group.exchange()
    exchanged += [to_peer(1), to_peer(2)]
    cots_gather.cross(0, 3)

    def last(value, at):
        total = inputs[at, :].astype(f32) + value
        normed_own[at, :] = (total * norm_scale(total) * second_gain).astype(bf16)
        return total

    halves = []
    for part, sems in enumerate((first_sems, second_sems)):
        group.finish(middle, last, part)
        rows = pl.ds(part * (share // 2), share // 2)
        halves.append(LinkGather(me, normed_own, normed_all, *sems, rows))
        halves[part].begin()
    cots_gather.cross(3, 2 * depth - 1)
    for step in range(1, depth):
        for gather in halves:
            gather.relay(step)
    for gather in halves:
        gather.cross(0, 2 * depth - 1)
    for gather in [cots_gather] + halves:
        gather.finish()
    group.sent()
    table_local.wait()
    for copy in table_copies + exchanged:
        copy.wait()


def token_tables(segment, position):
    cosine, sine = rope_tables(position, HEAD_DIMENSION)
    return (
        jnp.concatenate([cosine[:, 0], cosine[:, 0]], axis=1),
        jnp.concatenate([sine[:, 0], -sine[:, 0]], axis=1),
        segment,
        position,
    )


def front_by_links(inputs, gains, projections, w_out, tables, order, cots, near, ep_size):
    share, width = inputs.shape
    depth = ep_size // 2
    tokens = 4 * share
    heads = w_out.shape[0] // HEAD_DIMENSION
    bf16, f32 = jnp.bfloat16, jnp.float32
    dma = pltpu.SemaphoreType.DMA
    vmem, anywhere = pl.BlockSpec(memory_space=pltpu.VMEM), pl.BlockSpec(memory_space=pltpu.HBM)

    def like(*shape, dtype=bf16):
        return jax.ShapeDtypeStruct(shape, dtype)

    def gather_sems():
        return (dma, dma((2, 2 * depth)), dma((2, 2 * depth)), dma((2, 4 * depth)))

    widths = [w.shape[0] for w in projections]
    everywhere = (depth, 2, 2, share, width)
    return pl.pallas_call(
        functools.partial(front_kernel, ep_size, heads),
        out_shape=(
            like(2, 2, share, width),
            like(tokens, widths[0]),
            like(tokens, widths[1]),
            like(tokens, widths[2]),
            like(tokens, widths[0]),
            like(8, tokens, dtype=f32),
            like(share, width, dtype=f32),
            like(ep_size, *order.shape, dtype=order.dtype),
            like(*everywhere),
            like(*everywhere),
            like(share, width),
            like(*near[0].shape),
            like(*near[1].shape),
        ),
        in_specs=[vmem] * 11 + [anywhere] * 4,
        out_specs=(vmem,) * 7 + (anywhere,) * 3 + (vmem,) + (anywhere,) * 2,
        scratch_shapes=[
            pltpu.VMEM((share, width), bf16),
            pltpu.VMEM((tokens, tokens), f32),
            pltpu.VMEM((2, 2, share, width), bf16),
            pltpu.VMEM((2, share, width), bf16),
            pltpu.VMEM((share, width), bf16),
            dma,
            dma((2, 12)),
            dma,
            dma((2, ep_size - 1)),
            dma((2, 4)),
            dma((2, 3)),
            gather_sems(),
            gather_sems(),
            gather_sems(),
        ],
        compiler_params=pltpu.CompilerParams(
            collective_id=6, has_side_effects=True, vmem_limit_bytes=56 * 1024 * 1024
        ),
        name="front_by_links",
    )(
        inputs,
        *gains,
        *projections,
        w_out,
        *tables,
        order,
        cots,
        *near,
    )


def back_kernel(
    ep_size,
    heads,
    last_row,
    datt_own,
    heads_in,
    w_out,
    queries,
    keys,
    values,
    log_sums,
    segment,
    position,
    cosine,
    sine,
    rows_in,
    w_query,
    w_key,
    w_value,
    small_in,
    gain,
    inputs,
    middle,
    gate_peer,
    up_peer,
    down_peer,
    first_final,
    second_final,
    out_final,
    grad_input,
    small_out,
    gate_got,
    up_got,
    down_got,
    datt,
    bias,
    grad_heads,
    grad_proj,
    key_sum,
    value_sum,
    part_proj,
    part_out,
    y_got,
    z_got,
    y_got_out,
    z_got_out,
    parts,
    core_got,
    pair_got,
    small_src,
    small_got,
    small_sum,
    own_sem,
    gather_sems,
    y_sems,
    z_sems,
    fz_sems,
    fy_sems,
    y_sems_out,
    z_sems_out,
    fz_sems_out,
    fy_sems_out,
    group_sems,
    small_sems,
    spread_sems,
    own_small_sem,
    peer_sems,
):
    me = Place(ep_size)
    depth = me.depth
    f32, bf16 = jnp.float32, jnp.bfloat16
    others = all_others(ep_size)
    meet(others)
    my_place = lax.axis_index("ep") * 4 + lax.axis_index("tp")
    tokens, width = rows_in.shape
    share = datt_own.shape[0]
    size = HEAD_DIMENSION
    groups = keys.shape[1] // size
    per_group = heads // groups
    scale = size ** (-0.5)
    tile = 512

    def dot(a, b, contract):
        return lax.dot_general(
            a, b, ((contract[:1], contract[1:]), ((), ())), preferred_element_type=f32
        )

    bias[...] = tree_bias(segment, position)
    group_gather_body(me, 4, datt_own, datt, own_sem, gather_sems)

    def to_peer(i):
        source, target = ((gate_peer, gate_got), (up_peer, up_got), (down_peer, down_got))[i]
        return send(source, target, peer_sems.at[0, i], peer_sems.at[1, i], me.x_peer())

    exchanged = [to_peer(i) for i in range(3)]
    for n in range(width // tile):
        cols = slice(n * tile, (n + 1) * tile)
        grads = dot(heads_in[...], datt[:, :, :, cols].reshape(tokens, tile), (0, 0))
        part_out[:, :, :, cols] = grads.astype(bf16).reshape(depth, 2, -1, tile)
    out_sum = EpSum(
        me,
        part_out,
        y_got_out,
        z_got_out,
        out_final,
        (y_sems_out, z_sems_out, fz_sems_out, fy_sems_out),
    )
    out_sum.begin()
    for x in range(2):
        for c in range(2):
            at = pl.ds((x * 2 + c) * share, share)
            grad_heads[at, :] = dot(datt[x, c], w_out[...], (1, 1)).astype(bf16)

    def rotate_back_rows(grads, at):
        turned = jnp.concatenate([grads[:, size // 2 :], grads[:, : size // 2]], axis=1)
        return (grads * cosine[at, :] + turned * sine[at, :]).astype(bf16)

    for head in range(heads):
        group = head // per_group
        mine = slice(head * size, (head + 1) * size)
        shared = slice(group * size, (group + 1) * size)
        grads = []
        for cols, last_key in parts_of_tree(tokens):
            query, grad_head = queries[cols, mine], grad_heads[cols, mine]
            key, value = keys[:last_key, shared], values[:last_key, shared]
            scores = dot(key, query, (1, 1)) + bias[:last_key, cols]
            probs = jnp.exp(scores - log_sums[head : head + 1, cols])
            grad_probs = dot(value, grad_head, (1, 1))
            inner = jnp.sum(probs * grad_probs, axis=0, keepdims=True)
            grad_scores = (probs * (grad_probs - inner)).astype(bf16)
            grads.append(
                (dot(probs.astype(bf16), grad_head, (1, 0)), dot(grad_scores, query, (1, 0)))
            )
            grad_query = dot(grad_scores, key, (0, 0)) * scale
            grad_proj[cols, mine] = rotate_back_rows(grad_query, cols)
        grad_value, grad_key = (
            jnp.concatenate([trunk + both[:TRUNK], both[TRUNK:]], axis=0)
            for trunk, both in zip(*grads)
        )
        if head % per_group:
            grad_value = grad_value + value_sum[...]
            grad_key = grad_key + key_sum[...]
        value_sum[...] = grad_value
        key_sum[...] = grad_key
        if head % per_group == per_group - 1:
            at = heads * size + group * size
            grad_proj[:, at : at + size] = rotate_back_rows(grad_key, slice(0, tokens))
            at += groups * size
            grad_proj[:, at : at + size] = grad_value.astype(bf16)
        if head % 2 and head // 2 < depth - 2:
            out_sum.fold(head // 2)
    folded = min(heads // 2, depth - 2)

    ends = (heads * size, (heads + groups) * size, (heads + 2 * groups) * size)
    wide = width // 2
    sums = []
    for n, final in enumerate((first_final, second_final)):
        cols = slice(n * wide, (n + 1) * wide)
        grads = dot(grad_proj[...], rows_in[:, cols], (0, 0)).astype(bf16)
        at, first = 0, 0
        for end in ends:
            piece = grads[first:end].reshape(depth, 2, -1, wide)
            part_proj[n, :, :, at : at + piece.shape[2]] = piece
            at, first = at + piece.shape[2], end
        sums.append(
            EpSum(
                me,
                part_proj.at[n],
                y_got.at[n],
                z_got.at[n],
                final,
                (y_sems.at[n], z_sems.at[n], fz_sems.at[n], fy_sems.at[n]),
            )
        )
        if n == 1:
            sums[0].fold(0)
            for step in range(max(folded, depth - 1), depth):
                out_sum.fold(step)
            sums[0].fold(1)
        sums[n].begin()
        if n == 0:
            for step in range(folded, depth - 1):
                out_sum.fold(step)
    first_sum, second_sum = sums
    small_src[...] = small_in[...]
    own_gain = gain[...].astype(f32).reshape(1, width)
    for n in range(width // tile):
        cols = slice(n * tile, (n + 1) * tile)
        grads = (
            dot(grad_proj[:, : ends[0]], w_query[:, cols], (1, 0))
            + dot(grad_proj[:, ends[0] : ends[1]], w_key[:, cols], (1, 0))
            + dot(grad_proj[:, ends[1] :], w_value[:, cols], (1, 0))
        )
        parts[:, :, :, cols] = grads.astype(bf16).reshape(2, 2, share, tile)
        gained = jnp.sum(grads * rows_in[:, cols].astype(f32), axis=0, keepdims=True)
        gained = gained / own_gain[:, cols]
        for k in range(tile // 128):
            row = n * (tile // 128) + k
            small_src[last_row, row : row + 1, :] = gained[:, k * 128 : (k + 1) * 128]
    for step in range(2, depth - 1):
        first_sum.fold(step)
    out_sum.settle()
    small = [
        send(
            small_src.at[device[0] * 4 + device[1]],
            small_got.at[my_place],
            small_sems.at[0, k],
            small_sems.at[1, k],
            device,
        )
        for k, device in enumerate(others)
    ]
    own_small = pltpu.make_async_copy(
        small_src.at[my_place], small_got.at[my_place], own_small_sem
    )
    own_small.start()
    second_sum.fold(0)
    first_sum.fold(depth - 1)
    first_sum.settle()
    out_sum.relay(1)
    second_sum.fold(1)
    own_small.wait()
    for copy in small:
        copy.wait_recv()
    total = small_got[0]
    for k in range(1, 4 * ep_size):
        total = total + small_got[k]
    small_sum[...] = total
    spread = [
        send(
            small_sum,
            small_out.at[my_place],
            spread_sems.at[0, k],
            spread_sems.at[1, k],
            device,
        )
        for k, device in enumerate(others)
    ]
    small_out[my_place] = total
    group = GroupTotal(me, parts, core_got, pair_got, group_sems)
    group.begin()
    out_sum.relay(2)
    for step in range(2, depth - 1):
        second_sum.fold(step)
    group.exchange()
    first_sum.relay(1)
    second_sum.fold(depth - 1)
    for step in range(3, depth):
        out_sum.relay(step)
    second_sum.settle()
    out_sum.finish()
    first_sum.relay(2)

    def last(value, at):
        values_own = inputs[at, :].astype(f32)
        factor = norm_scale(values_own)
        return middle[at, :] + norm_back(values_own, factor, own_gain, value)

    for part in range(2):
        group.finish(grad_input, last, part)
    second_sum.relay(1)
    for step in range(3, depth):
        first_sum.relay(step)
    for step in range(2, depth):
        second_sum.relay(step)
    first_sum.finish()
    second_sum.finish()
    for copy in spread:
        copy.wait()
    for copy in small:
        copy.wait_send()
    group.sent()
    for each in [out_sum] + sums:
        each.sent()
    for copy in exchanged:
        copy.wait()


def back_by_links(
    datt_own,
    heads_in,
    w_out,
    queries,
    keys,
    values,
    log_sums,
    tables,
    rows_in,
    w_query,
    w_key,
    w_value,
    small,
    gain,
    inputs,
    middle,
    peers,
    ep_size,
):
    tokens, width = rows_in.shape
    share = datt_own.shape[0]
    depth = ep_size // 2
    heads = queries.shape[1] // HEAD_DIMENSION
    places = 4 * ep_size
    bf16, f32 = jnp.bfloat16, jnp.float32
    dma = pltpu.SemaphoreType.DMA
    vmem = pl.BlockSpec(memory_space=pltpu.VMEM)
    anywhere = pl.BlockSpec(memory_space=pltpu.HBM)
    cosine, sine, segment, position = tables
    blocks = jnp.pad(small, ((0, places - small.shape[0]), (0, 0))).reshape(places, -1, 128)
    sizes = [w.shape[0] // ep_size for w in (w_query, w_key, w_value, w_out)]
    total = sum(sizes[:3])

    def partial(rows, columns):
        return (depth, 2, rows, columns), bf16

    wide = width // 2
    got = pl.pallas_call(
        functools.partial(back_kernel, ep_size, heads, small.shape[0]),
        out_shape=(
            jax.ShapeDtypeStruct(*partial(total, wide)),
            jax.ShapeDtypeStruct(*partial(total, wide)),
            jax.ShapeDtypeStruct(*partial(sizes[3], width)),
            jax.ShapeDtypeStruct((share, width), f32),
            jax.ShapeDtypeStruct(blocks.shape, f32),
        )
        + tuple(jax.ShapeDtypeStruct(p.shape, p.dtype) for p in peers),
        in_specs=[vmem] * 19 + [anywhere] * 3,
        out_specs=(vmem,) * 5 + (anywhere,) * 3,
        scratch_shapes=[
            pltpu.VMEM((2, 2, share, width), bf16),
            pltpu.VMEM((tokens, tokens), f32),
            pltpu.VMEM(queries.shape, bf16),
            pltpu.VMEM((tokens, queries.shape[1] + 2 * keys.shape[1]), bf16),
            pltpu.VMEM((tokens, HEAD_DIMENSION), f32),
            pltpu.VMEM((tokens, HEAD_DIMENSION), f32),
        ]
        + [
            pltpu.VMEM((2, depth, 2, total, wide), bf16),
            pltpu.VMEM((depth, 2, sizes[3], width), bf16),
            pltpu.VMEM((2, depth, total, wide), bf16),
            pltpu.VMEM((2, depth - 1, total, wide), bf16),
            pltpu.VMEM((depth, sizes[3], width), bf16),
            pltpu.VMEM((depth - 1, sizes[3], width), bf16),
            pltpu.VMEM((2, 2, share, width), bf16),
            pltpu.VMEM((2, share, width), bf16),
            pltpu.VMEM((share, width), bf16),
            pltpu.VMEM(blocks.shape, f32),
            pltpu.VMEM(blocks.shape, f32),
            pltpu.VMEM(blocks.shape[1:], f32),
            dma,
            dma((2, 12)),
        ]
        + [dma((2, 2, depth)), dma((2, 2, depth))]
        + [dma((2, 2, 2 * depth))] * 2
        + [dma((2, depth)), dma((2, depth))]
        + [dma((2, 2 * depth))] * 2
        + [dma((2, 4)), dma((2, places - 1)), dma((2, places - 1)), dma, dma((2, 3))],
        compiler_params=pltpu.CompilerParams(
            collective_id=5, has_side_effects=True, vmem_limit_bytes=60 * 1024 * 1024
        ),
        name="back_by_links",
    )(
        datt_own,
        heads_in,
        w_out,
        queries,
        keys,
        values,
        log_sums,
        segment,
        position,
        cosine,
        sine,
        rows_in,
        w_query,
        w_key,
        w_value,
        blocks,
        gain,
        inputs,
        middle,
        *peers,
    )
    return got


def deliver_kernel(
    ep_size,
    sizes,
    rows_in,
    sums_in,
    gate_in,
    up_in,
    down_in,
    gate_got,
    up_got,
    down_got,
    first_in,
    second_in,
    third_in,
    small,
    gate_out,
    up_out,
    down_out,
    rows_out,
    sums_out,
    query_out,
    key_out,
    value_out,
    out_out,
    router_out,
    first_gain,
    second_gain,
    query,
    key,
    value,
    out,
    gate,
    up,
    down,
    gate_far,
    up_far,
    down_far,
    first,
    second,
    third,
    rows,
    sums,
    sems,
    load_sems,
):
    loads = [
        pltpu.make_async_copy(source, target, load_sems.at[i])
        for i, (source, target) in enumerate(
            (
                (third_in, third),
                (first_in, first),
                (second_in, second),
                (gate_in, gate),
                (gate_got, gate_far),
                (up_in, up),
                (up_got, up_far),
                (down_in, down),
                (down_got, down_far),
                (rows_in, rows),
                (sums_in, sums),
            )
        )
    ]
    for load in loads:
        load.start()
    copies = []
    wide = first.shape[2]
    f32 = jnp.float32

    def leave(source, target, i):
        copies.append(pltpu.make_async_copy(source, target, sems.at[i]))
        copies[-1].start()

    loads[0].wait()
    out[...] = third[...].astype(f32)
    leave(out, out_out, 5)
    for load in loads[1:3]:
        load.wait()
    at = 0
    for i, (source, target) in enumerate(((query, query_out), (key, key_out), (value, value_out))):
        for n, part in enumerate((first, second)):
            source[:, :, n * wide : (n + 1) * wide] = part[:, at : at + sizes[i], :].astype(f32)
        at += sizes[i]
        leave(source, target, 6 + i)
    for i, (total, far) in enumerate(((gate, gate_far), (up, up_far), (down, down_far))):
        for load in loads[3 + 2 * i : 5 + 2 * i]:
            load.wait()
        total[...] = total[...] + far[...].astype(f32)
        leave(total, (gate_out, up_out, down_out)[i], 2 + i)
    for load in loads[9:]:
        load.wait()
    leave(rows, rows_out, 0)
    leave(sums, sums_out, 1)
    experts = router_out.shape[0]
    for j in range(small.shape[1]):
        cols = slice(j * 128, (j + 1) * 128)
        router_out[:, cols] = small[:experts, j, :]
        first_gain[cols] = small[experts + 1, j, :]
        second_gain[cols] = small[experts, j, :]
    for copy in copies:
        copy.wait()


def deliver(owned, peers, rows, sums, got, small, sizes, expert_count, ep_size):
    width = rows.shape[1]
    f32 = jnp.float32
    vmem, anywhere = pl.BlockSpec(memory_space=pltpu.VMEM), pl.BlockSpec(memory_space=pltpu.HBM)
    first, second, third = (g.reshape((ep_size,) + g.shape[2:]) for g in got)

    def like(value):
        return jax.ShapeDtypeStruct(value.shape, value.dtype)

    shapes = [(ep_size, k, width) for k in sizes]
    results = pl.pallas_call(
        functools.partial(deliver_kernel, ep_size, sizes),
        out_shape=tuple(like(a) for a in owned)
        + (like(rows), like(sums))
        + tuple(jax.ShapeDtypeStruct(shape, f32) for shape in shapes)
        + (
            jax.ShapeDtypeStruct((expert_count, width), f32),
            jax.ShapeDtypeStruct((width,), f32),
            jax.ShapeDtypeStruct((width,), f32),
        ),
        in_specs=[anywhere] * 11 + [vmem],
        out_specs=(anywhere,) * 9 + (vmem,) * 3,
        scratch_shapes=[pltpu.VMEM(shape, f32) for shape in shapes]
        + [pltpu.VMEM(a.shape, a.dtype) for a in (*owned, *peers, first, second, third)]
        + [pltpu.VMEM(a.shape, a.dtype) for a in (rows, sums)]
        + [pltpu.SemaphoreType.DMA((9,)), pltpu.SemaphoreType.DMA((11,))],
        compiler_params=pltpu.CompilerParams(vmem_limit_bytes=60 * 1024 * 1024),
        name="deliver",
    )(rows, sums, *owned, *peers, first, second, third, small)
    gate, up, down, rows, sums = results[:5]
    query, key, value, out = (g.reshape(-1, width) for g in results[5:9])
    router, first_gain, second_gain = results[9:]
    return (
        sums,
        rows,
        first_gain,
        query,
        key,
        value,
        out,
        second_gain,
        router,
        gate,
        up,
        down.reshape(gate.shape[0], -1, width),
    )


def group_rows(value_rows):
    return lax.all_gather(value_rows, "tp", axis=0, tiled=True)


def group_totals(value_rows):
    return lax.psum_scatter(value_rows, "tp", scatter_dimension=0, tiled=True).astype(jnp.float32)


def gather_all(value_rows):
    return lax.all_gather(value_rows, ("ep", "tp"), axis=0, tiled=True)


LAST = 1 << 30


def pair_order(expert_ids, slot_order, expert_count):
    experts = jnp.arange(expert_count, dtype=jnp.int32)
    chosen = expert_ids.T[None, :, :] == experts[:, None, None]
    return jnp.min(jnp.where(chosen, slot_order.T[None, :, :], LAST), axis=1)


def kept_pairs(order):
    used = order < LAST
    counts = jnp.sum(used.astype(jnp.int32), axis=2)
    block = jnp.arange(order.shape[0], dtype=jnp.int32)
    earlier = block[None, :] < block[:, None]
    offsets = jnp.sum(jnp.where(earlier[:, :, None], counts[None, :, :], 0), axis=1)
    whole = offsets + counts <= CAP
    edge = (offsets < CAP) & ~whole
    edge_order = jnp.sum(jnp.where(edge[:, :, None], order, 0), axis=0)
    rank = jnp.sum((edge_order[:, :, None] < edge_order[:, None, :]).astype(jnp.int32), axis=1)
    early = offsets[:, :, None] + rank[None, :, :] < CAP
    return used & (whole[:, :, None] | (edge[:, :, None] & early))


def masked_softmax(logits, used):
    top = jnp.max(jnp.where(used, logits, -1e30), axis=-1, keepdims=True)
    powers = jnp.where(used, jnp.exp(logits - top), 0.0)
    return powers / jnp.sum(powers, axis=-1, keepdims=True)


def pair_codes(order_all, per_owner):
    expert_count = order_all.shape[1]
    first = lax.axis_index("ep") * per_owner
    turned = jnp.roll(order_all, -first, axis=1)
    kept = kept_pairs(turned[:, :per_owner])
    dropped = jnp.pad(~kept, ((0, 0), (0, expert_count - per_owner), (0, 0)))
    code = jnp.where(turned < LAST, dropped.astype(jnp.float32), -1.0)
    return code.swapaxes(1, 2).reshape(-1, expert_count).astype(jnp.bfloat16)


def expert_weights(w_gate, w_up, w_down):
    enter = jnp.concatenate([w[e] for w in (w_gate, w_up) for e in range(w.shape[0])], axis=1)
    return enter, w_down.reshape(-1, w_down.shape[2])


def run_experts(rows_all, cots_all, code, w_router, w_gate, w_up, w_down, weights, by_links):
    per_owner, width, units = w_gate.shape
    expert_count = w_router.shape[0]
    ep_size, tp_size = lax.axis_size("ep"), lax.axis_size("tp")
    hidden = per_owner * units
    router = jnp.roll(w_router, -lax.axis_index("ep") * per_owner, axis=0)
    if by_links:
        grads, sums, small, *owned = experts_by_links(
            rows_all, cots_all, code, router, weights, per_owner, ep_size
        )
        share = grads.shape[0]
        return (
            grads,
            sums,
            small[:, :per_owner].reshape(expert_count, share).T,
            owned[:3],
            owned[3:],
        )
    enter, leave = expert_weights(w_gate, w_up, w_down)
    used, kept = code >= 0, (code == 0).astype(jnp.float32)
    logits = jnp.einsum("rd,ed->re", rows_all, router, preferred_element_type=jnp.float32)
    gates = jnp.repeat((kept * masked_softmax(logits, used))[:, :per_owner], units, axis=1)
    act = jnp.dot(rows_all, enter, preferred_element_type=jnp.float32)
    gate_act, up_act = act[:, :hidden], act[:, hidden:]
    back_act = jnp.einsum("rd,fd->rf", cots_all, leave, preferred_element_type=jnp.float32)
    sigma = jax.nn.sigmoid(gate_act)
    value = gate_act * sigma * up_act
    weighted = (gates * value).astype(jnp.bfloat16)
    grad_hidden = gates * back_act
    turned = jnp.concatenate(
        [
            grad_hidden * up_act * sigma * (1.0 + gate_act * (1.0 - sigma)),
            grad_hidden * gate_act * sigma,
        ],
        axis=1,
    ).astype(jnp.bfloat16)
    small = kept[:, :per_owner] * jnp.sum((value * back_act).reshape(-1, per_owner, units), axis=2)
    grads = jnp.einsum("rf,df->rd", turned, enter, preferred_element_type=jnp.float32)
    sums = jnp.dot(weighted, leave, preferred_element_type=jnp.float32)

    def scatter(value_rows):
        return lax.psum_scatter(value_rows, ("ep", "tp"), scatter_dimension=0, tiled=True)

    columns = lax.dynamic_update_slice_in_dim(
        jnp.zeros((small.shape[0], expert_count), jnp.float32),
        small,
        lax.axis_index("ep") * per_owner,
        1,
    )
    both = jnp.einsum(
        "rd,rwef->wedf",
        rows_all,
        turned.reshape(-1, 2, per_owner, units),
        preferred_element_type=jnp.float32,
    )
    down = jnp.einsum("rf,rd->fd", weighted, cots_all, preferred_element_type=jnp.float32)
    return (
        scatter(grads.astype(jnp.bfloat16)).astype(jnp.float32),
        scatter(sums.astype(jnp.bfloat16)).astype(jnp.float32),
        scatter(columns),
        (both[0], both[1], down),
        None,
    )


def visible_block(query_seg, query_pos, query_row, key_seg, key_pos, key_row):
    seg_q = query_seg[:, None]
    seg_k = key_seg[None, :]
    above = (
        (seg_k == seg_q)
        | (seg_k == 0)
        | (seg_k >= 1) & (seg_k <= 4) & (seg_q >= 5) & ((seg_q - 5) // 2 + 1 == seg_k)
    )
    same_tree = query_row[:, None] // TREE_TOKENS == key_row[None, :] // TREE_TOKENS
    return above & same_tree & (key_pos[None, :] <= query_pos[:, None])


def block_scores(query_part, key_rows, allowed, scale):
    scores = (
        jnp.einsum("qkgd,pkd->kgqp", query_part, key_rows, preferred_element_type=jnp.float32)
        * scale
    )
    return jnp.where(allowed[None, None], scores, -1e30)


def attend_forward(query_rows, key_rows, value_rows, segment, position):
    total_rows = query_rows.shape[0]
    scale = query_rows.shape[-1] ** (-0.5)
    row_ids = jnp.arange(total_rows, dtype=jnp.int32)
    allowed = visible_block(segment, position, row_ids, segment, position, row_ids)
    scores = block_scores(query_rows, key_rows, allowed, scale)
    top_score = jnp.max(scores, axis=-1, keepdims=True)
    weights = jnp.exp(scores - top_score)
    weight_sum = jnp.sum(weights, axis=-1, keepdims=True)
    probs = (weights / weight_sum).astype(jnp.bfloat16)
    outputs = jnp.einsum(
        "kgqp,pkd->qkgd", probs, value_rows, preferred_element_type=jnp.float32
    ).astype(jnp.bfloat16)
    log_sums = [top_score + jnp.log(weight_sum)]
    return (outputs, log_sums)


def attend_backward(
    query_rows, key_rows, value_rows, segment, position, log_sums, grad_heads, block_rows
):
    total_rows = query_rows.shape[0]
    scale = query_rows.shape[-1] ** (-0.5)
    row_ids = jnp.arange(total_rows, dtype=jnp.int32)
    grad_keys = jnp.zeros(key_rows.shape, jnp.float32)
    grad_values = jnp.zeros(value_rows.shape, jnp.float32)
    grad_query = []
    for number, first_row in enumerate(range(0, total_rows, block_rows)):
        allowed = visible_block(segment, position, row_ids, segment, position, row_ids)
        scores = block_scores(query_rows, key_rows, allowed, scale)
        probs = jnp.where(allowed[None, None], jnp.exp(scores - log_sums[number]), 0.0)
        grad_values = jnp.einsum(
            "kgqp,qkgd->pkd",
            probs.astype(jnp.bfloat16),
            grad_heads,
            preferred_element_type=jnp.float32,
        )
        grad_probs = jnp.einsum(
            "qkgd,pkd->kgqp", grad_heads, value_rows, preferred_element_type=jnp.float32
        )
        inner = jnp.sum(probs * grad_probs, axis=-1, keepdims=True)
        grad_scores = (probs * (grad_probs - inner)).astype(jnp.bfloat16)
        grad_query.append(
            jnp.einsum("kgqp,pkd->qkgd", grad_scores, key_rows, preferred_element_type=jnp.float32)
            * scale
        )
        grad_keys = (
            jnp.einsum(
                "kgqp,qkgd->pkd", grad_scores, query_rows, preferred_element_type=jnp.float32
            )
            * scale
        )
    return (grad_query[0], grad_keys, grad_values)


def local(
    hidden_in,
    gain_attn,
    w_query,
    key_projection_weight,
    value_projection_weight,
    w_out,
    gain_ffn,
    w_router,
    w_gate,
    w_up,
    w_down,
    expert_ids,
    slot_order,
    segment,
    position,
    cotangent,
):
    model_width = w_query.shape[1]
    head_width = HEAD_DIMENSION
    local_heads = w_query.shape[0] // head_width
    local_kv = key_projection_weight.shape[0] // head_width
    group_factor = local_heads // local_kv
    token_count = expert_ids.shape[0]
    share = hidden_in.shape[0]
    row_start = lax.axis_index("tp") * share
    expert_count = w_router.shape[0]
    per_owner = w_gate.shape[0]
    block_rows = 512
    by_links = lax.axis_size("tp") == 4 and lax.axis_size("ep") == 8
    order = pair_order(expert_ids, slot_order, expert_count)
    gain_one = gain_attn.astype(jnp.float32)
    gain_two = gain_ffn.astype(jnp.float32)
    inputs_own = hidden_in.astype(jnp.float32)
    if by_links:
        near = expert_weights(w_gate, w_up, w_down)
        token_info = token_tables(segment, position)
        (
            first_normalized,
            query_rows,
            key_rows,
            value_rows,
            head_outputs,
            log_sums,
            middle_own,
            order_all,
            cot_all,
            normed_two,
            normed_own,
            *far,
        ) = front_by_links(
            hidden_in,
            (gain_attn, gain_ffn),
            (w_query, key_projection_weight, value_projection_weight),
            w_out,
            token_info,
            order,
            cotangent,
            near,
            lax.axis_size("ep"),
        )
        weights = (near[0], far[0], near[1], far[1])
        scale_two = norm_scale(middle_own)
    else:
        weights = None
        scale_one = norm_scale(inputs_own)
        first_normalized = group_rows((inputs_own * scale_one * gain_one).astype(jnp.bfloat16))
        order_all = lax.all_gather(order, "ep")
        cosine_lookup, sine_lookup = rope_tables(position, head_width)
        query_proj = jnp.einsum(
            "rd,fd->rf", first_normalized, w_query, preferred_element_type=jnp.float32
        ).reshape(token_count, local_heads, head_width)
        key_proj = jnp.einsum(
            "rd,fd->rf", first_normalized, key_projection_weight, preferred_element_type=jnp.float32
        ).reshape(token_count, local_kv, head_width)
        query_rows = (
            apply_rotation(query_proj, cosine_lookup, sine_lookup)
            .astype(jnp.bfloat16)
            .reshape(token_count, local_kv, group_factor, head_width)
        )
        key_rows = apply_rotation(key_proj, cosine_lookup, sine_lookup).astype(jnp.bfloat16)
        value_rows = (
            jnp.einsum(
                "rd,fd->rf",
                first_normalized,
                value_projection_weight,
                preferred_element_type=jnp.float32,
            )
            .astype(jnp.bfloat16)
            .reshape(token_count, local_kv, head_width)
        )
        head_outputs, log_sums = attend_forward(query_rows, key_rows, value_rows, segment, position)
        head_outputs = head_outputs.reshape(token_count, local_heads * head_width)
        middle_own = inputs_own + group_totals(
            jnp.dot(head_outputs, w_out, preferred_element_type=jnp.float32).astype(jnp.bfloat16)
        )
        scale_two = norm_scale(middle_own)
        normed_own = (middle_own * scale_two * gain_two).astype(jnp.bfloat16)
        normed_two, cot_all = gather_all(normed_own), gather_all(cotangent)
    code = pair_codes(order_all, per_owner)
    used = lax.dynamic_slice_in_dim(order, row_start, share, 1).T < LAST
    gates = masked_softmax(
        jnp.einsum("rd,ed->re", normed_own, w_router, preferred_element_type=jnp.float32), used
    )
    grad_normed_own, combined_own, grad_gates_own, owned, peers = run_experts(
        normed_two, cot_all, code, w_router, w_gate, w_up, w_down, weights, by_links
    )
    output_own = (middle_own + combined_own).astype(jnp.bfloat16)
    inner_gate = jnp.sum(gates * grad_gates_own, axis=-1, keepdims=True)
    grad_logits = gates * (grad_gates_own - inner_gate)
    router_f = w_router.astype(jnp.float32)
    grad_normed_own = grad_normed_own + jnp.dot(grad_logits, router_f, precision=EXACT_PRECISION)
    grad_router = jnp.dot(grad_logits.T, normed_own.astype(jnp.float32), precision=EXACT_PRECISION)
    grad_gain_ffn = jnp.sum(grad_normed_own * middle_own * scale_two, axis=0)
    grad_middle = cotangent.astype(jnp.float32) + norm_back(
        middle_own, scale_two, gain_two, grad_normed_own
    )
    if by_links:
        *got, grad_input, small, gate_got, up_got, down_got = back_by_links(
            grad_middle.astype(jnp.bfloat16),
            head_outputs,
            w_out,
            query_rows,
            key_rows,
            value_rows,
            log_sums,
            token_info,
            first_normalized.reshape(token_count, model_width),
            w_query,
            key_projection_weight,
            value_projection_weight,
            jnp.concatenate([grad_router, grad_gain_ffn[None, :]], axis=0),
            gain_attn,
            hidden_in,
            grad_middle,
            peers,
            lax.axis_size("ep"),
        )
        ep_size = lax.axis_size("ep")
        weights = (w_query, key_projection_weight, value_projection_weight, w_out)
        return deliver(
            owned,
            (gate_got, up_got, down_got),
            grad_input,
            output_own,
            got,
            small,
            [w.shape[0] // ep_size for w in weights],
            expert_count,
            ep_size,
        )
    grad_attn = group_rows(grad_middle.astype(jnp.bfloat16))
    grad_w_out = jnp.einsum(
        "rf,rd->fd", head_outputs, grad_attn, preferred_element_type=jnp.float32
    )
    grad_w_out = lax.psum(grad_w_out.astype(jnp.bfloat16), "ep").astype(jnp.float32)
    grad_heads = (
        jnp.einsum("rd,fd->rf", grad_attn, w_out, preferred_element_type=jnp.float32)
        .astype(jnp.bfloat16)
        .reshape(token_count, local_kv, group_factor, head_width)
    )
    grad_query, grad_keys, grad_values = attend_backward(
        query_rows, key_rows, value_rows, segment, position, log_sums, grad_heads, block_rows
    )
    grad_query_proj = (
        rotate_back(
            grad_query.reshape(token_count, local_heads, head_width), cosine_lookup, sine_lookup
        )
        .astype(jnp.bfloat16)
        .reshape(token_count, local_heads * head_width)
    )
    grad_key_proj = (
        rotate_back(grad_keys, cosine_lookup, sine_lookup)
        .astype(jnp.bfloat16)
        .reshape(token_count, local_kv * head_width)
    )
    grad_value_proj = grad_values.astype(jnp.bfloat16).reshape(token_count, local_kv * head_width)
    grad_w_query = jnp.einsum(
        "rf,rd->fd", grad_query_proj, first_normalized, preferred_element_type=jnp.float32
    )
    grad_w_key = jnp.einsum(
        "rf,rd->fd", grad_key_proj, first_normalized, preferred_element_type=jnp.float32
    )
    grad_w_value = jnp.einsum(
        "rf,rd->fd", grad_value_proj, first_normalized, preferred_element_type=jnp.float32
    )
    grad_normed_one = jnp.einsum(
        "rf,fd->rd", grad_query_proj, w_query, preferred_element_type=jnp.float32
    )
    grad_normed_one = grad_normed_one + jnp.einsum(
        "rf,fd->rd", grad_key_proj, key_projection_weight, preferred_element_type=jnp.float32
    )
    grad_normed_one = grad_normed_one + jnp.einsum(
        "rf,fd->rd", grad_value_proj, value_projection_weight, preferred_element_type=jnp.float32
    )
    grad_gain_attn = jnp.sum(grad_normed_one * first_normalized.astype(jnp.float32), axis=0)
    small = jnp.concatenate(
        [grad_router, grad_gain_ffn[None, :], (grad_gain_attn / gain_one)[None, :]], axis=0
    )
    grad_w_query, grad_w_key, grad_w_value = (
        lax.psum(g.astype(jnp.bfloat16), "ep").astype(jnp.float32)
        for g in (grad_w_query, grad_w_key, grad_w_value)
    )
    grad_one_own = group_totals(grad_normed_one.astype(jnp.bfloat16))
    small = lax.psum(small, ("ep", "tp"))
    grad_input = grad_middle + norm_back(inputs_own, scale_one, gain_one, grad_one_own)
    grad_router = small[:expert_count]
    grad_gain_ffn, grad_gain_attn = small[expert_count], small[expert_count + 1]
    return (
        output_own,
        grad_input,
        grad_gain_attn,
        grad_w_query,
        grad_w_key,
        grad_w_value,
        grad_w_out,
        grad_gain_ffn,
        grad_router,
        owned[0],
        owned[1],
        owned[2].reshape(w_down.shape),
    )


def solution(mesh):
    placed = (
        P(("ep", "tp"), None),
        P(),
        P("tp", None),
        P("tp", None),
        P("tp", None),
        P("tp", None),
        P(),
        P(),
        P("ep", None, "tp"),
        P("ep", None, "tp"),
        P("ep", "tp", None),
        P("ep", None),
        P("ep", None),
        P("ep"),
        P("ep"),
        P(("ep", "tp"), None),
    )
    return jax.shard_map(
        local,
        mesh=mesh,
        in_specs=placed,
        out_specs=(
            P(("ep", "tp"), None),
            P(("ep", "tp"), None),
            P(),
            P("tp", None),
            P("tp", None),
            P("tp", None),
            P("tp", None),
            P(),
            P(),
            P("ep", None, "tp"),
            P("ep", None, "tp"),
            P("ep", "tp", None),
        ),
        check_vma=False,
    )
```

```python
import functools

import jax
import jax.numpy as jnp
from jax import lax
from jax.experimental import pallas as pl
from jax.experimental.pallas import tpu as pltpu
from jax.sharding import PartitionSpec as P

HEAD_DIMENSION = 64
TREE_TOKENS = 512
TRUNK = 256
CAP = 2304


EPSILON = 1e-06
ROPE_BASE = 10000.0
EXACT_PRECISION = lax.Precision.HIGHEST


def rope_tables(position, head_width):
    half_width = head_width // 2
    freqs = ROPE_BASE ** (-(jnp.arange(half_width, dtype=jnp.float32) * 2.0 / head_width))
    angle = position.astype(jnp.float32)[:, None] * freqs[None, :]
    return (jnp.cos(angle)[:, None, :], jnp.sin(angle)[:, None, :])


def apply_rotation(value_rows, cosine_lookup, sine_lookup):
    half_width = value_rows.shape[-1] // 2
    first = value_rows[..., :half_width]
    second = value_rows[..., half_width:]
    return jnp.concatenate(
        [
            first * cosine_lookup - second * sine_lookup,
            first * sine_lookup + second * cosine_lookup,
        ],
        axis=-1,
    )


def rotate_back(grads, cosine_lookup, sine_lookup):
    half_width = grads.shape[-1] // 2
    first = grads[..., :half_width]
    second = grads[..., half_width:]
    return jnp.concatenate(
        [
            first * cosine_lookup + second * sine_lookup,
            second * cosine_lookup - first * sine_lookup,
        ],
        axis=-1,
    )


def norm_scale(value_rows):
    return lax.rsqrt(jnp.mean(value_rows * value_rows, axis=-1, keepdims=True) + EPSILON)


def norm_back(value_rows, scale, gain, grad_normed):
    weighted = grad_normed * gain
    inner = jnp.mean(value_rows * weighted, axis=-1, keepdims=True)
    grad_values = scale * weighted - value_rows * (scale * scale * scale) * inner
    return grad_values


MESH = pl.DeviceIdType.MESH


class Place:
    def __init__(self, ep_size):
        self.depth = ep_size // 2
        ep, tp = lax.axis_index("ep"), lax.axis_index("tp")
        self.z, self.y = ep // 2, ep % 2
        self.x, self.c = tp // 2, tp % 2

    def device(self, z=None, y=None, x=None, c=None):
        z = self.z if z is None else z
        y = self.y if y is None else y
        x = self.x if x is None else x
        c = self.c if c is None else c
        return (z * 2 + y, x * 2 + c)

    def sibling(self):
        return self.device(c=1 - self.c)

    def x_peer(self):
        return self.device(x=1 - self.x)

    def y_peer(self):
        return self.device(y=1 - self.y)

    def target(self, step):
        side = 1 - 2 * (self.z % 2)
        offset = 2 * (1 - step % 2) + side * (1 - step // 2)
        return lax.rem(self.z + offset + self.depth, self.depth)

    def z_peer(self, step):
        return self.device(z=self.target((1, 1, 2)[step]))


def greet(devices):
    barrier = pltpu.get_barrier_semaphore()
    for device in devices:
        pl.semaphore_signal(barrier, inc=1, device_id=device, device_id_type=MESH)


def meet(devices):
    pl.semaphore_wait(pltpu.get_barrier_semaphore(), len(devices))


def send(src, dst, send_sem, recv_sem, device):
    copy = pltpu.make_async_remote_copy(
        src_ref=src,
        dst_ref=dst,
        send_sem=send_sem,
        recv_sem=recv_sem,
        device_id=device,
        device_id_type=MESH,
    )
    copy.start()
    return copy


def add_into(target, other):
    def tile(i, carry):
        at = pl.ds(pl.multiple_of(i * 16, 16), 16)
        target[at, :] = target[at, :] + other[at, :]
        return carry

    lax.fori_loop(0, target.shape[0] // 16, tile, 0)


def group_gather_body(me, pieces, own, out, own_sem, sems):
    size = own.shape[0] // pieces
    started = []
    local = pltpu.make_async_copy(own, out.at[me.x, me.c], own_sem)
    local.start()

    def at(p):
        return pl.ds(p * size, size)

    def go(kind, p, src, dst, device):
        slot = kind * pieces + p
        started.append(send(src, dst, sems.at[0, slot], sems.at[1, slot], device))

    for p in range(pieces):
        go(0, p, own.at[at(p)], out.at[me.x, me.c, at(p)], me.x_peer())
    for p in range(pieces):
        go(1, p, own.at[at(p)], out.at[me.x, me.c, at(p)], me.sibling())
    for p in range(pieces):
        block = out.at[1 - me.x, me.c, at(p)]
        pltpu.make_async_copy(block, block, sems.at[1, p]).wait()
        go(2, p, block, block, me.sibling())
    for p in range(pieces):
        for kind, x in ((1, me.x), (2, 1 - me.x)):
            block = out.at[x, 1 - me.c, at(p)]
            pltpu.make_async_copy(block, block, sems.at[1, kind * pieces + p]).wait()
    local.wait()
    for copy in started:
        copy.wait_send()


class GroupTotal:
    def __init__(self, me, parts, core_got, pair_got, sems):
        self.me, self.parts, self.core_got, self.pair_got = me, parts, core_got, pair_got
        self.core = [
            pltpu.make_async_remote_copy(
                src_ref=parts.at[x, 1 - me.c],
                dst_ref=core_got.at[x],
                send_sem=sems.at[0, k],
                recv_sem=sems.at[1, k],
                device_id=me.sibling(),
                device_id_type=MESH,
            )
            for k, x in enumerate((1 - me.x, me.x))
        ]
        self.half = pair_got.shape[0] // 2
        self.pair = [
            pltpu.make_async_remote_copy(
                src_ref=core_got.at[1 - me.x, self.rows(part)],
                dst_ref=pair_got.at[self.rows(part)],
                send_sem=sems.at[0, 2 + part],
                recv_sem=sems.at[1, 2 + part],
                device_id=me.x_peer(),
                device_id_type=MESH,
            )
            for part in range(2)
        ]

    def rows(self, part):
        return pl.ds(part * self.half, self.half)

    def begin(self):
        for copy in self.core:
            copy.start()

    def exchange(self):
        self.core[0].wait_recv()
        far = 1 - self.me.x
        for part, copy in enumerate(self.pair):
            rows = self.rows(part)
            add_into(self.core_got.at[far, rows], self.parts.at[far, self.me.c, rows])
            copy.start()

    def finish(self, out, change, part):
        if part == 0:
            self.core[1].wait_recv()
        self.pair[part].wait_recv()

        def tile(i, carry):
            at = pl.ds(pl.multiple_of(part * self.half + i * 16, 16), 16)
            value = (
                self.parts[self.me.x, self.me.c, at, :].astype(jnp.float32)
                + self.core_got[self.me.x, at, :].astype(jnp.float32)
                + self.pair_got[at, :].astype(jnp.float32)
            )
            out[at, :] = change(value, at)
            return carry

        lax.fori_loop(0, self.half // 16, tile, 0)

    def sent(self):
        for copy in self.core + self.pair:
            copy.wait_send()


def all_others(ep_size):
    ep, tp = lax.axis_index("ep"), lax.axis_index("tp")
    return [
        (lax.rem(ep + k // 4, ep_size), lax.rem(tp + k % 4, 4)) for k in range(1, ep_size * 4)
    ]


def experts_kernel(
    ep_size,
    per_owner,
    rows_in,
    cots_in,
    code_in,
    router,
    enter_own,
    enter_peer,
    leave_own,
    leave_peer,
    grad_out,
    sum_out,
    small_out,
    gate_out,
    up_out,
    down_out,
    gate_peer,
    up_peer,
    down_peer,
    rows_buf,
    cots_buf,
    weighted,
    turned,
    enter_sum,
    down_sum,
    parts,
    core_got,
    y_got,
    z_got,
    small_in,
    small_got,
    load_sems,
    core_sems,
    y_sems,
    z_sems,
    small_sems,
    own_sem,
):
    me = Place(ep_size)
    depth = me.depth
    blocks = 2 * depth
    width = router.shape[1]
    share = rows_buf.shape[2]
    tokens = 2 * share
    hidden = leave_own.shape[0]
    units = hidden // per_owner
    f32, bf16 = jnp.float32, jnp.bfloat16
    ep = lax.axis_index("ep")
    others = [
        (lax.rem(ep + k // 2, ep_size), me.x * 2 + lax.rem(me.c + k % 2, 2))
        for k in range(1, 2 * ep_size)
    ]
    greet(others)
    my_place = ep * 2 + me.c
    halves = ((enter_own, leave_own), (enter_peer, leave_peer))

    def where(b):
        return me.target(b // 2), lax.rem(1 - me.y + b % 2, 2)

    def load(b, which):
        z, y = where(b)
        source, target = ((rows_in, rows_buf), (cots_in, cots_buf))[which]
        slot = lax.rem(b, 2)
        return pltpu.make_async_copy(
            source.at[z, y], target.at[slot], load_sems.at[slot, which]
        )

    def core_copy(b):
        return pltpu.make_async_remote_copy(
            src_ref=parts.at[lax.rem(b, 2), :, 1 - me.c],
            dst_ref=core_got.at[b // 2, where(b)[1]],
            send_sem=core_sems.at[0, b],
            recv_sem=core_sems.at[1, b],
            device_id=me.sibling(),
            device_id_type=MESH,
        )

    def y_copy(step, which):
        return pltpu.make_async_remote_copy(
            src_ref=core_got.at[step, 1 - me.y, which],
            dst_ref=y_got.at[step, which],
            send_sem=y_sems.at[0, step, which],
            recv_sem=y_sems.at[1, step, which],
            device_id=me.y_peer(),
            device_id_type=MESH,
        )

    def z_copy(step, which):
        return pltpu.make_async_remote_copy(
            src_ref=y_got.at[step, which],
            dst_ref=z_got.at[step, which],
            send_sem=z_sems.at[0, step, which],
            recv_sem=z_sems.at[1, step, which],
            device_id=me.z_peer(step),
            device_id_type=MESH,
        )

    def small_copy(k, device):
        return pltpu.make_async_remote_copy(
            src_ref=small_in.at[device[0] * 2 + device[1] % 2],
            dst_ref=small_got.at[my_place],
            send_sem=small_sems.at[0, k],
            recv_sem=small_sems.at[1, k],
            device_id=device,
            device_id_type=MESH,
        )

    def dot(a, b, contract):
        return lax.dot_general(
            a, b, ((contract[:1], contract[1:]), ((), ())), preferred_element_type=f32
        )

    def spread(columns):
        return jnp.concatenate(
            [jnp.broadcast_to(columns[:, e : e + 1], (tokens, units)) for e in range(per_owner)],
            axis=1,
        )

    def compute(b):
        z, y = where(b)
        slot = lax.rem(b, 2)
        rows = rows_buf[slot].reshape(tokens, width)
        cots = cots_buf[slot].reshape(tokens, width)
        code = code_in[z * 2 + y, me.x].astype(f32).reshape(tokens, -1)
        used = code >= 0.0
        logits = jnp.where(used, dot(rows, router[...], (1, 1)), -1e30)
        top = jnp.max(logits, axis=1, keepdims=True)
        powers = jnp.where(used, jnp.exp(logits - top), 0.0)
        kept = jnp.where(code == 0.0, 1.0, 0.0)
        gates = spread(kept * powers / jnp.sum(powers, axis=1, keepdims=True))
        products = jnp.zeros((tokens, hidden), f32)
        for h, (enter, leave) in enumerate(halves):
            act = dot(rows, enter[...], (1, 0))
            gate_act, up_act = act[:, :hidden], act[:, hidden:]
            back_act = dot(cots, leave[...], (1, 1))
            sigma = jax.nn.sigmoid(gate_act)
            swish = gate_act * sigma
            value = swish * up_act
            products = products + value * back_act
            weighted[:, h * hidden : (h + 1) * hidden] = (gates * value).astype(bf16)
            grad_hidden = gates * back_act
            at = 2 * h * hidden
            turned[:, at : at + hidden] = (
                grad_hidden * up_act * sigma * (1.0 + gate_act * (1.0 - sigma))
            ).astype(bf16)
            turned[:, at + hidden : at + 2 * hidden] = (grad_hidden * swish).astype(bf16)
        lane = lax.broadcasted_iota(jnp.int32, (8, hidden), 1)
        pick = lax.broadcasted_iota(jnp.int32, (8, hidden), 0)
        mine = jnp.where((lane >= pick * units) & (lane < (pick + 1) * units), 1.0, 0.0)
        grad_gates = lax.dot_general(
            mine,
            spread(kept) * products,
            (((1,), (1,)), ((), ())),
            precision=EXACT_PRECISION,
            preferred_element_type=f32,
        )
        for k in range(2):
            small_in[(z * 2 + y) * 2 + k] = grad_gates[:, k * share : (k + 1) * share]
        tile = 512
        for n in range(width // tile):
            cols = slice(n * tile, (n + 1) * tile)
            grads = (
                dot(turned[:, : 2 * hidden], enter_own[cols, :], (1, 1))
                + dot(turned[:, 2 * hidden :], enter_peer[cols, :], (1, 1))
            ).astype(bf16)
            sums = (
                dot(weighted[:, :hidden], leave_own[:, cols], (1, 0))
                + dot(weighted[:, hidden:], leave_peer[:, cols], (1, 0))
            ).astype(bf16)
            for c in range(2):
                at = slice(c * share, (c + 1) * share)
                parts[slot, 0, c, :, cols] = grads[at]
                parts[slot, 1, c, :, cols] = sums[at]

    def weight_sums(b):
        slot = lax.rem(b, 2)
        tile = 512
        for n in range(width // tile):
            cols = slice(n * tile, (n + 1) * tile)
            rows = rows_buf[slot, :, :, cols].reshape(tokens, tile)
            cots = cots_buf[slot, :, :, cols].reshape(tokens, tile)
            enter_sum[:, cols] += dot(turned[...], rows, (0, 0))
            down_sum[:, cols] += dot(weighted[...], cots, (0, 0))

    for which in range(2):
        load(0, which).start()

    def during(i, lag, body, parity=None):
        b = i - lag
        inside = (b >= 0) & (b < blocks)
        if parity is not None:
            inside &= lax.rem(b + 2 * lag, 2) == parity
        pl.when(inside)(lambda: body(b))

    def work(b):
        for which in range(2):
            load(b, which).wait()

        @pl.when(b + 1 < blocks)
        def _():
            for which in range(2):
                load(b + 1, which).start()

        compute(b)
        pl.when(b == 0)(lambda: meet(others))
        core_copy(b).start()

        @pl.when(b == 0)
        def _():
            enter_sum[...] = jnp.zeros_like(enter_sum)
            down_sum[...] = jnp.zeros_like(down_sum)

        weight_sums(b)

    def core_sum(b):
        step, y = b // 2, where(b)[1]
        core_copy(b).wait_recv()
        for which in range(2):
            add_into(core_got.at[step, y, which], parts.at[lax.rem(b, 2), which, me.c])

        @pl.when(b % 2 == 0)
        def _():
            for which in range(2):
                y_copy(step, which).start()

        core_copy(b).wait_send()

    def y_sum(which):
        def body(b):
            step = b // 2
            y_copy(step, which).wait_recv()
            add_into(y_got.at[step, which], core_got.at[step, me.y, which])
            for k in range(2):
                pl.when(step == k)(lambda: z_copy(k, which).start())

            @pl.when(step == 2)
            def _():
                z_copy(0, which).wait_recv()
                add_into(y_got.at[2, which], z_got.at[0, which])
                z_copy(2, which).start()

        return body

    def small_send(b):
        for k, device in enumerate(others):
            small_copy(k, device).start()
        pltpu.make_async_copy(small_in.at[my_place], small_got.at[my_place], own_sem).start()
        for e in range(per_owner):
            own, peer = e * units, 2 * hidden + e * units
            gate_out[e] = enter_sum[own : own + units, :].T
            up_out[e] = enter_sum[hidden + own : hidden + own + units, :].T
            gate_peer[e] = enter_sum[peer : peer + units, :].T.astype(bf16)
            up_peer[e] = enter_sum[hidden + peer : hidden + peer + units, :].T.astype(bf16)
        down_out[...] = down_sum[:hidden, :]
        down_peer[...] = down_sum[hidden:, :].astype(bf16)

    def turn(i, carry):
        during(i, 0, work)
        during(i, 1, core_sum, 1)
        during(i, 2, y_sum(0), 0)
        during(i, 3, y_sum(1), 0)
        during(i, 0, core_sum, 0)
        pl.when(i == blocks)(lambda: small_send(i))
        return carry

    lax.fori_loop(0, blocks + 2, turn, 0)
    pltpu.make_async_copy(small_in.at[my_place], small_got.at[my_place], own_sem).wait()
    for k, device in enumerate(others):
        small_copy(k, device).wait()
    for k in range(ep_size):
        small_out[k] = small_got[2 * k] + small_got[2 * k + 1]
    for step in range(1, 3):
        for which in range(2):
            z_copy(step, which).wait_recv()

    def finish(which, target):
        def tile(i, carry):
            at = pl.ds(pl.multiple_of(i * 16, 16), 16)
            total = y_got[depth - 1, which, at, :].astype(f32)
            for step in range(1, 3):
                total = total + z_got[step, which, at, :].astype(f32)
            target[at, :] = total
            return carry

        lax.fori_loop(0, share // 16, tile, 0)

    finish(0, grad_out)
    finish(1, sum_out)
    for step in range(depth):
        for which in range(2):
            y_copy(step, which).wait_send()
            if step < depth - 1:
                z_copy(step, which).wait_send()


def experts_by_links(rows_all, cots_all, code, router, weights, per_owner, ep_size):
    depth, _, _, rows, width = rows_all.shape
    hidden = weights[2].shape[0]
    units = hidden // per_owner
    bf16, f32 = jnp.bfloat16, jnp.float32
    dma = pltpu.SemaphoreType.DMA
    vmem = pl.BlockSpec(memory_space=pltpu.VMEM)
    anywhere = pl.BlockSpec(memory_space=pltpu.HBM)
    places = 2 * ep_size
    return pl.pallas_call(
        functools.partial(experts_kernel, ep_size, per_owner),
        out_shape=(
            jax.ShapeDtypeStruct((rows, width), f32),
            jax.ShapeDtypeStruct((rows, width), f32),
            jax.ShapeDtypeStruct((ep_size, 8, rows), f32),
            jax.ShapeDtypeStruct((per_owner, width, units), f32),
            jax.ShapeDtypeStruct((per_owner, width, units), f32),
            jax.ShapeDtypeStruct((hidden, width), f32),
            jax.ShapeDtypeStruct((per_owner, width, units), bf16),
            jax.ShapeDtypeStruct((per_owner, width, units), bf16),
            jax.ShapeDtypeStruct((hidden, width), bf16),
        ),
        in_specs=[anywhere, anywhere] + [vmem] * 6,
        out_specs=(vmem,) * 9,
        scratch_shapes=[
            pltpu.VMEM((2, 2, rows, width), bf16),
            pltpu.VMEM((2, 2, rows, width), bf16),
            pltpu.VMEM((2 * rows, 2 * hidden), bf16),
            pltpu.VMEM((2 * rows, 4 * hidden), bf16),
            pltpu.VMEM((4 * hidden, width), f32),
            pltpu.VMEM((2 * hidden, width), f32),
            pltpu.VMEM((2, 2, 2, rows, width), bf16),
            pltpu.VMEM((depth, 2, 2, rows, width), bf16),
            pltpu.VMEM((depth, 2, rows, width), bf16),
            pltpu.VMEM((depth - 1, 2, rows, width), bf16),
            pltpu.VMEM((places, 8, rows), f32),
            pltpu.VMEM((places, 8, rows), f32),
            dma((2, 2)),
            dma((2, 2 * depth)),
            dma((2, depth, 2)),
            dma((2, depth - 1, 2)),
            dma((2, places - 1)),
            dma,
        ],
        compiler_params=pltpu.CompilerParams(
            collective_id=2, has_side_effects=True, vmem_limit_bytes=60 * 1024 * 1024
        ),
        name="experts_by_links",
    )(rows_all, cots_all, code.reshape(ep_size, 2, 2, rows, -1), router, *weights)


class LinkGather:
    def __init__(self, me, own, out, own_sem, z_sems, y_sems, core_sems, rows=None):
        self.me, self.own, self.out, self.rows = me, own, out, rows
        if rows is not None:
            self.own = own.at[rows]
        self.own_sem, self.z_sems, self.y_sems, self.core_sems = own_sem, z_sems, y_sems, core_sems
        self.begun = []
        depth = me.depth
        self.found = [(me.z, 0, None)]
        for d in range(1, depth):
            self.found.append((me.z - d, d, me.z >= d))
            self.found.append((me.z + d, depth - 1 + d, me.z + d < depth))

    def guard(self, *conditions):
        given = [c for c in conditions if c is not None]
        if not given:
            return lambda body: body()
        total = given[0]
        for c in given[1:]:
            total = total & c
        return pl.when(total)

    def go(self, source, place, sems, slot, device, *conditions):
        def copy():
            return pltpu.make_async_remote_copy(
                src_ref=source,
                dst_ref=place,
                send_sem=sems.at[0, slot],
                recv_sem=sems.at[1, slot],
                device_id=device,
                device_id_type=MESH,
            )

        self.guard(*conditions)(lambda: copy().start())
        self.begun.append((copy, conditions))

    def landed(self, place, sems, slot, condition):
        self.guard(condition)(
            lambda: pltpu.make_async_copy(place, place, sems.at[1, slot]).wait()
        )

    def up(self, source, place, d, condition):
        me = self.me
        device = me.device(z=lax.rem(me.z + 1, me.depth))
        self.go(source, place, self.z_sems, d, device, condition, me.z < me.depth - 1)

    def down(self, source, place, d, condition):
        me = self.me
        device = me.device(z=lax.rem(me.z + me.depth - 1, me.depth))
        self.go(source, place, self.z_sems, me.depth - 1 + d, device, condition, me.z > 0)

    def place(self, z, y, c):
        at = (lax.rem(z + self.me.depth, self.me.depth), y)
        if self.core_sems is not None:
            at += (c,)
        return self.out.at[at if self.rows is None else at + (self.rows,)]

    def to_sibling(self, block, slot, *conditions):
        if self.core_sems is not None:
            self.go(block[0], block[1], self.core_sems, slot, self.me.sibling(), *conditions)

    def begin(self):
        me = self.me
        mine = self.place(me.z, me.y, me.c)
        self.up(self.own, mine, 1, None)
        self.down(self.own, mine, 1, None)
        self.go(self.own, mine, self.y_sems, 0, me.y_peer())
        if self.core_sems is None:
            return
        self.to_sibling((self.own, mine), 0)
        self.local = pltpu.make_async_copy(self.own, mine, self.own_sem)
        self.local.start()

    def relay(self, d):
        me = self.me
        for z, slot, condition in self.found[2 * d - 1 : 2 * d + 1]:
            block = self.place(z, me.y, me.c)
            self.landed(block, self.z_sems, slot, condition)
            if d < me.depth - 1:
                (self.up if slot < me.depth else self.down)(block, block, d + 1, condition)
            self.go(block, block, self.y_sems, slot, me.y_peer(), condition)
            self.to_sibling((block, block), slot, condition)

    def cross(self, first, last):
        me = self.me
        for z, slot, condition in self.found[first:last]:
            block = self.place(z, 1 - me.y, me.c)
            self.landed(block, self.y_sems, slot, condition)
            self.to_sibling((block, block), 2 * me.depth - 1 + slot, condition)

    def finish(self):
        me = self.me
        for z, slot, condition in self.found:
            for y, at in ((me.y, slot), (1 - me.y, 2 * me.depth - 1 + slot)):
                self.landed(self.place(z, y, 1 - me.c), self.core_sems, at, condition)
        self.local.wait()
        self.sent()

    def sent(self):
        for copy, conditions in self.begun:
            self.guard(*conditions)(lambda: copy().wait_send())


class EpSum:
    def __init__(self, me, grads, y_got, z_got, final, sems):
        self.me, self.grads = me, grads
        self.y_got, self.z_got, self.final = y_got, z_got, final
        self.y_sems, self.z_sems, self.fz_sems, self.fy_sems = sems

    def y_copy(self, step):
        me = self.me
        return pltpu.make_async_remote_copy(
            src_ref=self.grads.at[me.target(step), 1 - me.y],
            dst_ref=self.y_got.at[step],
            send_sem=self.y_sems.at[0, step],
            recv_sem=self.y_sems.at[1, step],
            device_id=me.y_peer(),
            device_id_type=MESH,
        )

    def z_copy(self, step):
        return pltpu.make_async_remote_copy(
            src_ref=self.y_got.at[step],
            dst_ref=self.z_got.at[step],
            send_sem=self.z_sems.at[0, step],
            recv_sem=self.z_sems.at[1, step],
            device_id=self.me.z_peer(step),
            device_id_type=MESH,
        )

    def begin(self):
        for step in range(self.me.depth):
            self.y_copy(step).start()

    def fold(self, step):
        me = self.me
        self.y_copy(step).wait_recv()
        add_into(self.y_got.at[step], self.grads.at[me.target(step), me.y])
        if step == 2:
            self.z_copy(0).wait_recv()
            add_into(self.y_got.at[2], self.z_got.at[0])
        if step < me.depth - 1:
            self.z_copy(step).start()

    def settle(self):
        me, depth = self.me, self.me.depth
        for step in range(1, 3):
            self.z_copy(step).wait_recv()

        def tile(i, carry):
            at = pl.ds(pl.multiple_of(i * 16, 16), 16)
            value = self.y_got[depth - 1, at, :].astype(jnp.float32)
            for step in range(1, 3):
                value = value + self.z_got[step, at, :].astype(jnp.float32)
            self.final[me.z, me.y, at, :] = value.astype(self.final.dtype)
            return carry

        lax.fori_loop(0, self.final.shape[2] // 16, tile, 0)
        mine = self.final.at[me.z, me.y]
        self.spread = LinkGather(me, mine, self.final, None, self.fz_sems, self.fy_sems, None)
        self.spread.begin()

    def relay(self, d):
        self.spread.relay(d)

    def finish(self):
        self.spread.cross(0, 2 * self.me.depth - 1)

    def sent(self):
        self.spread.sent()
        for step in range(self.me.depth):
            self.y_copy(step).wait_send()
            if step < self.me.depth - 1:
                self.z_copy(step).wait_send()


def parts_of_tree(tokens):
    return ((slice(0, TRUNK), TRUNK), (slice(TRUNK, tokens), tokens))


def tree_bias(segment, position):
    query_seg, query_pos = segment[...].reshape(1, -1), position[...].reshape(1, -1)
    table = jnp.concatenate([query_seg] * 4 + [query_pos] * 4, axis=0).astype(jnp.float32).T
    key_seg, key_pos = table[:, 0:1].astype(jnp.int32), table[:, 4:5].astype(jnp.int32)
    parent = jnp.where(query_seg >= 5, (query_seg - 5) // 2 + 1, -1)
    above = (key_seg == query_seg) | (key_seg == 0) | (key_seg == parent)
    return jnp.where(above & (key_pos <= query_pos), 0.0, -1e30)


def front_kernel(
    ep_size,
    heads,
    inputs,
    gain_one,
    gain_two,
    w_query,
    w_key,
    w_value,
    w_out,
    cosine,
    sine,
    segment,
    position,
    table,
    cots,
    enter_near,
    leave_near,
    rows_out,
    queries,
    keys,
    values,
    heads_out,
    log_sums,
    middle,
    tables,
    cots_all,
    normed_all,
    normed_own,
    enter_far,
    leave_far,
    first_own,
    bias,
    parts,
    core_got,
    pair_got,
    own_sem,
    gather_sems,
    table_own_sem,
    table_sems,
    group_sems,
    far_sems,
    cots_sems,
    first_sems,
    second_sems,
):
    me = Place(ep_size)
    depth = me.depth
    f32, bf16 = jnp.float32, jnp.bfloat16
    share, width = inputs.shape
    tokens = 4 * share
    size = HEAD_DIMENSION
    groups = keys.shape[1] // size
    per_group = heads // groups
    scale = size ** (-0.5)
    ep, tp = lax.axis_index("ep"), lax.axis_index("tp")
    peers = [(lax.rem(ep + k, ep_size), tp) for k in range(1, ep_size)]
    friends = [me.sibling(), me.x_peer()] + peers
    greet(friends)

    def dot(a, b, contract):
        return lax.dot_general(
            a, b, ((contract[:1], contract[1:]), ((), ())), preferred_element_type=f32
        )

    first_gain = gain_one[...].astype(f32).reshape(1, width)
    second_gain = gain_two[...].astype(f32).reshape(1, width)
    for i in range(share // 16):
        at = slice(i * 16, (i + 1) * 16)
        value = inputs[at, :].astype(f32)
        first_own[at, :] = (value * norm_scale(value) * first_gain).astype(bf16)
    meet(friends)
    cots_gather = LinkGather(me, cots, cots_all, *cots_sems)
    cots_gather.begin()
    table_local = pltpu.make_async_copy(table, tables.at[ep], table_own_sem)
    table_local.start()
    table_copies = [
        send(table, tables.at[ep], table_sems.at[0, k], table_sems.at[1, k], device)
        for k, device in enumerate(peers)
    ]
    bias[...] = tree_bias(segment, position)
    log_sums[...] = jnp.zeros_like(log_sums)
    group_gather_body(me, 4, first_own, rows_out, own_sem, gather_sems)

    early = width // 3

    def to_peer(i):
        source, target = ((leave_near, leave_far), (enter_near, enter_far))[min(i, 1)]
        at = (pl.ds(0, leave_near.shape[0]), pl.ds(0, early), pl.ds(early, width - early))[i]
        return send(source.at[at], target.at[at], far_sems.at[0, i], far_sems.at[1, i], me.x_peer())

    exchanged = [to_peer(0)]
    cots_gather.relay(1)
    rows = rows_out[...].reshape(tokens, width)

    def rotate(part):
        turned = jnp.concatenate([part[:, size // 2 :], part[:, : size // 2]], axis=1)
        return (part * cosine[...] - turned * sine[...]).astype(bf16)

    projected = dot(rows, w_query[...], (1, 1))
    for head in range(heads):
        mine = slice(head * size, (head + 1) * size)
        queries[:, mine] = rotate(projected[:, mine] * scale)
    projected = dot(rows, w_key[...], (1, 1))
    for group in range(groups):
        mine = slice(group * size, (group + 1) * size)
        keys[:, mine] = rotate(projected[:, mine])
    values[...] = dot(rows, w_value[...], (1, 1)).astype(bf16)
    for head in range(heads):
        mine = slice(head * size, (head + 1) * size)
        shared = slice(head // per_group * size, (head // per_group + 1) * size)
        for cols, last_key in parts_of_tree(tokens):
            scores = dot(keys[:last_key, shared], queries[cols, mine], (1, 1))
            scores = scores + bias[:last_key, cols]
            top = jnp.max(scores, axis=0, keepdims=True)
            powers = jnp.exp(scores - top)
            total = jnp.sum(powers, axis=0, keepdims=True)
            log_sums[head : head + 1, cols] = top + jnp.log(total)
            probs = (powers * (1.0 / total)).astype(bf16)
            heads_out[cols, mine] = dot(probs, values[:last_key, shared], (0, 0)).astype(bf16)
        if head == 1:
            cots_gather.relay(2)
    tile = 512
    for n in range(width // tile):
        cols = slice(n * tile, (n + 1) * tile)
        sums = dot(heads_out[...], w_out[:, cols], (1, 0)).astype(bf16)
        parts[:, :, :, cols] = sums.reshape(2, 2, share, tile)
    group = GroupTotal(me, parts, core_got, pair_got, group_sems)
    group.begin()
    for step in range(3, depth):
        cots_gather.relay(step)
    group.exchange()
    exchanged += [to_peer(1), to_peer(2)]
    cots_gather.cross(0, 3)

    def last(value, at):
        total = inputs[at, :].astype(f32) + value
        normed_own[at, :] = (total * norm_scale(total) * second_gain).astype(bf16)
        return total

    halves = []
    for part, sems in enumerate((first_sems, second_sems)):
        group.finish(middle, last, part)
        rows = pl.ds(part * (share // 2), share // 2)
        halves.append(LinkGather(me, normed_own, normed_all, *sems, rows))
        halves[part].begin()
    cots_gather.cross(3, 2 * depth - 1)
    for step in range(1, depth):
        for gather in halves:
            gather.relay(step)
    for gather in halves:
        gather.cross(0, 2 * depth - 1)
    for gather in [cots_gather] + halves:
        gather.finish()
    group.sent()
    table_local.wait()
    for copy in table_copies + exchanged:
        copy.wait()


def token_tables(segment, position):
    cosine, sine = rope_tables(position, HEAD_DIMENSION)
    return (
        jnp.concatenate([cosine[:, 0], cosine[:, 0]], axis=1),
        jnp.concatenate([sine[:, 0], -sine[:, 0]], axis=1),
        segment,
        position,
    )


def front_by_links(inputs, gains, projections, w_out, tables, order, cots, near, ep_size):
    share, width = inputs.shape
    depth = ep_size // 2
    tokens = 4 * share
    heads = w_out.shape[0] // HEAD_DIMENSION
    bf16, f32 = jnp.bfloat16, jnp.float32
    dma = pltpu.SemaphoreType.DMA
    vmem, anywhere = pl.BlockSpec(memory_space=pltpu.VMEM), pl.BlockSpec(memory_space=pltpu.HBM)

    def like(*shape, dtype=bf16):
        return jax.ShapeDtypeStruct(shape, dtype)

    def gather_sems():
        return (dma, dma((2, 2 * depth)), dma((2, 2 * depth)), dma((2, 4 * depth)))

    widths = [w.shape[0] for w in projections]
    everywhere = (depth, 2, 2, share, width)
    return pl.pallas_call(
        functools.partial(front_kernel, ep_size, heads),
        out_shape=(
            like(2, 2, share, width),
            like(tokens, widths[0]),
            like(tokens, widths[1]),
            like(tokens, widths[2]),
            like(tokens, widths[0]),
            like(8, tokens, dtype=f32),
            like(share, width, dtype=f32),
            like(ep_size, *order.shape, dtype=order.dtype),
            like(*everywhere),
            like(*everywhere),
            like(share, width),
            like(*near[0].shape),
            like(*near[1].shape),
        ),
        in_specs=[vmem] * 11 + [anywhere] * 4,
        out_specs=(vmem,) * 7 + (anywhere,) * 3 + (vmem,) + (anywhere,) * 2,
        scratch_shapes=[
            pltpu.VMEM((share, width), bf16),
            pltpu.VMEM((tokens, tokens), f32),
            pltpu.VMEM((2, 2, share, width), bf16),
            pltpu.VMEM((2, share, width), bf16),
            pltpu.VMEM((share, width), bf16),
            dma,
            dma((2, 12)),
            dma,
            dma((2, ep_size - 1)),
            dma((2, 4)),
            dma((2, 3)),
            gather_sems(),
            gather_sems(),
            gather_sems(),
        ],
        compiler_params=pltpu.CompilerParams(
            collective_id=6, has_side_effects=True, vmem_limit_bytes=56 * 1024 * 1024
        ),
        name="front_by_links",
    )(
        inputs,
        *gains,
        *projections,
        w_out,
        *tables,
        order,
        cots,
        *near,
    )


def back_kernel(
    ep_size,
    heads,
    last_row,
    datt_own,
    heads_in,
    w_out,
    queries,
    keys,
    values,
    log_sums,
    segment,
    position,
    cosine,
    sine,
    rows_in,
    w_query,
    w_key,
    w_value,
    small_in,
    gain,
    inputs,
    middle,
    gate_peer,
    up_peer,
    down_peer,
    first_final,
    second_final,
    out_final,
    grad_input,
    small_out,
    gate_got,
    up_got,
    down_got,
    datt,
    bias,
    grad_heads,
    grad_proj,
    key_sum,
    value_sum,
    part_proj,
    part_out,
    y_got,
    z_got,
    y_got_out,
    z_got_out,
    parts,
    core_got,
    pair_got,
    small_src,
    small_got,
    small_sum,
    own_sem,
    gather_sems,
    y_sems,
    z_sems,
    fz_sems,
    fy_sems,
    y_sems_out,
    z_sems_out,
    fz_sems_out,
    fy_sems_out,
    group_sems,
    small_sems,
    spread_sems,
    own_small_sem,
    peer_sems,
):
    me = Place(ep_size)
    depth = me.depth
    f32, bf16 = jnp.float32, jnp.bfloat16
    others = all_others(ep_size)
    greet(others)
    my_place = lax.axis_index("ep") * 4 + lax.axis_index("tp")
    tokens, width = rows_in.shape
    share = datt_own.shape[0]
    size = HEAD_DIMENSION
    groups = keys.shape[1] // size
    per_group = heads // groups
    scale = size ** (-0.5)
    tile = 512

    def dot(a, b, contract):
        return lax.dot_general(
            a, b, ((contract[:1], contract[1:]), ((), ())), preferred_element_type=f32
        )

    bias[...] = tree_bias(segment, position)
    meet(others)
    group_gather_body(me, 4, datt_own, datt, own_sem, gather_sems)

    def to_peer(i):
        source, target = ((gate_peer, gate_got), (up_peer, up_got), (down_peer, down_got))[i]
        return send(source, target, peer_sems.at[0, i], peer_sems.at[1, i], me.x_peer())

    exchanged = [to_peer(i) for i in range(3)]
    for n in range(width // tile):
        cols = slice(n * tile, (n + 1) * tile)
        grads = dot(heads_in[...], datt[:, :, :, cols].reshape(tokens, tile), (0, 0))
        part_out[:, :, :, cols] = grads.astype(bf16).reshape(depth, 2, -1, tile)
    out_sum = EpSum(
        me,
        part_out,
        y_got_out,
        z_got_out,
        out_final,
        (y_sems_out, z_sems_out, fz_sems_out, fy_sems_out),
    )
    out_sum.begin()
    for x in range(2):
        for c in range(2):
            at = pl.ds((x * 2 + c) * share, share)
            grad_heads[at, :] = dot(datt[x, c], w_out[...], (1, 1)).astype(bf16)

    def rotate_back_rows(grads, at):
        turned = jnp.concatenate([grads[:, size // 2 :], grads[:, : size // 2]], axis=1)
        return (grads * cosine[at, :] + turned * sine[at, :]).astype(bf16)

    for head in range(heads):
        group = head // per_group
        mine = slice(head * size, (head + 1) * size)
        shared = slice(group * size, (group + 1) * size)
        grads = []
        for cols, last_key in parts_of_tree(tokens):
            query, grad_head = queries[cols, mine], grad_heads[cols, mine]
            key, value = keys[:last_key, shared], values[:last_key, shared]
            scores = dot(key, query, (1, 1)) + bias[:last_key, cols]
            probs = jnp.exp(scores - log_sums[head : head + 1, cols])
            grad_probs = dot(value, grad_head, (1, 1))
            inner = jnp.sum(probs * grad_probs, axis=0, keepdims=True)
            grad_scores = (probs * (grad_probs - inner)).astype(bf16)
            grads.append(
                (dot(probs.astype(bf16), grad_head, (1, 0)), dot(grad_scores, query, (1, 0)))
            )
            grad_query = dot(grad_scores, key, (0, 0)) * scale
            grad_proj[cols, mine] = rotate_back_rows(grad_query, cols)
        grad_value, grad_key = (
            jnp.concatenate([trunk + both[:TRUNK], both[TRUNK:]], axis=0)
            for trunk, both in zip(*grads)
        )
        if head % per_group:
            grad_value = grad_value + value_sum[...]
            grad_key = grad_key + key_sum[...]
        value_sum[...] = grad_value
        key_sum[...] = grad_key
        if head % per_group == per_group - 1:
            at = heads * size + group * size
            grad_proj[:, at : at + size] = rotate_back_rows(grad_key, slice(0, tokens))
            at += groups * size
            grad_proj[:, at : at + size] = grad_value.astype(bf16)
        if head % 2 and head // 2 < depth - 2:
            out_sum.fold(head // 2)
    folded = min(heads // 2, depth - 2)

    ends = (heads * size, (heads + groups) * size, (heads + 2 * groups) * size)
    wide = width // 2
    sums = []
    for n, final in enumerate((first_final, second_final)):
        cols = slice(n * wide, (n + 1) * wide)
        grads = dot(grad_proj[...], rows_in[:, cols], (0, 0)).astype(bf16)
        at, first = 0, 0
        for end in ends:
            piece = grads[first:end].reshape(depth, 2, -1, wide)
            part_proj[n, :, :, at : at + piece.shape[2]] = piece
            at, first = at + piece.shape[2], end
        sums.append(
            EpSum(
                me,
                part_proj.at[n],
                y_got.at[n],
                z_got.at[n],
                final,
                (y_sems.at[n], z_sems.at[n], fz_sems.at[n], fy_sems.at[n]),
            )
        )
        if n == 1:
            sums[0].fold(0)
            for step in range(max(folded, depth - 1), depth):
                out_sum.fold(step)
            sums[0].fold(1)
        sums[n].begin()
        if n == 0:
            for step in range(folded, depth - 1):
                out_sum.fold(step)
    first_sum, second_sum = sums
    small_src[...] = small_in[...]
    own_gain = gain[...].astype(f32).reshape(1, width)
    for n in range(width // tile):
        cols = slice(n * tile, (n + 1) * tile)
        grads = (
            dot(grad_proj[:, : ends[0]], w_query[:, cols], (1, 0))
            + dot(grad_proj[:, ends[0] : ends[1]], w_key[:, cols], (1, 0))
            + dot(grad_proj[:, ends[1] :], w_value[:, cols], (1, 0))
        )
        parts[:, :, :, cols] = grads.astype(bf16).reshape(2, 2, share, tile)
        gained = jnp.sum(grads * rows_in[:, cols].astype(f32), axis=0, keepdims=True)
        gained = gained / own_gain[:, cols]
        for k in range(tile // 128):
            row = n * (tile // 128) + k
            small_src[last_row, row : row + 1, :] = gained[:, k * 128 : (k + 1) * 128]
    for step in range(2, depth - 1):
        first_sum.fold(step)
    out_sum.settle()
    small = [
        send(
            small_src.at[device[0] * 4 + device[1]],
            small_got.at[my_place],
            small_sems.at[0, k],
            small_sems.at[1, k],
            device,
        )
        for k, device in enumerate(others)
    ]
    own_small = pltpu.make_async_copy(
        small_src.at[my_place], small_got.at[my_place], own_small_sem
    )
    own_small.start()
    second_sum.fold(0)
    first_sum.fold(depth - 1)
    first_sum.settle()
    out_sum.relay(1)
    second_sum.fold(1)
    own_small.wait()
    for copy in small:
        copy.wait_recv()
    total = small_got[0]
    for k in range(1, 4 * ep_size):
        total = total + small_got[k]
    small_sum[...] = total
    spread = [
        send(
            small_sum,
            small_out.at[my_place],
            spread_sems.at[0, k],
            spread_sems.at[1, k],
            device,
        )
        for k, device in enumerate(others)
    ]
    small_out[my_place] = total
    group = GroupTotal(me, parts, core_got, pair_got, group_sems)
    group.begin()
    out_sum.relay(2)
    for step in range(2, depth - 1):
        second_sum.fold(step)
    group.exchange()
    first_sum.relay(1)
    second_sum.fold(depth - 1)
    for step in range(3, depth):
        out_sum.relay(step)
    second_sum.settle()
    out_sum.finish()
    first_sum.relay(2)

    def last(value, at):
        values_own = inputs[at, :].astype(f32)
        factor = norm_scale(values_own)
        return middle[at, :] + norm_back(values_own, factor, own_gain, value)

    for part in range(2):
        group.finish(grad_input, last, part)
    second_sum.relay(1)
    for step in range(3, depth):
        first_sum.relay(step)
    for step in range(2, depth):
        second_sum.relay(step)
    first_sum.finish()
    second_sum.finish()
    for copy in spread:
        copy.wait()
    for copy in small:
        copy.wait_send()
    group.sent()
    for each in [out_sum] + sums:
        each.sent()
    for copy in exchanged:
        copy.wait()


def back_by_links(
    datt_own,
    heads_in,
    w_out,
    queries,
    keys,
    values,
    log_sums,
    tables,
    rows_in,
    w_query,
    w_key,
    w_value,
    small,
    gain,
    inputs,
    middle,
    peers,
    ep_size,
):
    tokens, width = rows_in.shape
    share = datt_own.shape[0]
    depth = ep_size // 2
    heads = queries.shape[1] // HEAD_DIMENSION
    places = 4 * ep_size
    bf16, f32 = jnp.bfloat16, jnp.float32
    dma = pltpu.SemaphoreType.DMA
    vmem = pl.BlockSpec(memory_space=pltpu.VMEM)
    anywhere = pl.BlockSpec(memory_space=pltpu.HBM)
    cosine, sine, segment, position = tables
    blocks = jnp.pad(small, ((0, places - small.shape[0]), (0, 0))).reshape(places, -1, 128)
    sizes = [w.shape[0] // ep_size for w in (w_query, w_key, w_value, w_out)]
    total = sum(sizes[:3])

    def partial(rows, columns):
        return (depth, 2, rows, columns), bf16

    wide = width // 2
    got = pl.pallas_call(
        functools.partial(back_kernel, ep_size, heads, small.shape[0]),
        out_shape=(
            jax.ShapeDtypeStruct(*partial(total, wide)),
            jax.ShapeDtypeStruct(*partial(total, wide)),
            jax.ShapeDtypeStruct(*partial(sizes[3], width)),
            jax.ShapeDtypeStruct((share, width), f32),
            jax.ShapeDtypeStruct(blocks.shape, f32),
        )
        + tuple(jax.ShapeDtypeStruct(p.shape, p.dtype) for p in peers),
        in_specs=[vmem] * 19 + [anywhere] * 3,
        out_specs=(vmem,) * 5 + (anywhere,) * 3,
        scratch_shapes=[
            pltpu.VMEM((2, 2, share, width), bf16),
            pltpu.VMEM((tokens, tokens), f32),
            pltpu.VMEM(queries.shape, bf16),
            pltpu.VMEM((tokens, queries.shape[1] + 2 * keys.shape[1]), bf16),
            pltpu.VMEM((tokens, HEAD_DIMENSION), f32),
            pltpu.VMEM((tokens, HEAD_DIMENSION), f32),
        ]
        + [
            pltpu.VMEM((2, depth, 2, total, wide), bf16),
            pltpu.VMEM((depth, 2, sizes[3], width), bf16),
            pltpu.VMEM((2, depth, total, wide), bf16),
            pltpu.VMEM((2, depth - 1, total, wide), bf16),
            pltpu.VMEM((depth, sizes[3], width), bf16),
            pltpu.VMEM((depth - 1, sizes[3], width), bf16),
            pltpu.VMEM((2, 2, share, width), bf16),
            pltpu.VMEM((2, share, width), bf16),
            pltpu.VMEM((share, width), bf16),
            pltpu.VMEM(blocks.shape, f32),
            pltpu.VMEM(blocks.shape, f32),
            pltpu.VMEM(blocks.shape[1:], f32),
            dma,
            dma((2, 12)),
        ]
        + [dma((2, 2, depth)), dma((2, 2, depth))]
        + [dma((2, 2, 2 * depth))] * 2
        + [dma((2, depth)), dma((2, depth))]
        + [dma((2, 2 * depth))] * 2
        + [dma((2, 4)), dma((2, places - 1)), dma((2, places - 1)), dma, dma((2, 3))],
        compiler_params=pltpu.CompilerParams(
            collective_id=5, has_side_effects=True, vmem_limit_bytes=60 * 1024 * 1024
        ),
        name="back_by_links",
    )(
        datt_own,
        heads_in,
        w_out,
        queries,
        keys,
        values,
        log_sums,
        segment,
        position,
        cosine,
        sine,
        rows_in,
        w_query,
        w_key,
        w_value,
        blocks,
        gain,
        inputs,
        middle,
        *peers,
    )
    return got


def deliver_kernel(
    ep_size,
    sizes,
    rows_in,
    sums_in,
    gate_in,
    up_in,
    down_in,
    gate_got,
    up_got,
    down_got,
    first_in,
    second_in,
    third_in,
    small,
    gate_out,
    up_out,
    down_out,
    rows_out,
    sums_out,
    query_out,
    key_out,
    value_out,
    out_out,
    router_out,
    first_gain,
    second_gain,
    query,
    key,
    value,
    out,
    gate,
    up,
    down,
    gate_far,
    up_far,
    down_far,
    first,
    second,
    third,
    rows,
    sums,
    sems,
    load_sems,
):
    loads = [
        pltpu.make_async_copy(source, target, load_sems.at[i])
        for i, (source, target) in enumerate(
            (
                (third_in, third),
                (first_in, first),
                (second_in, second),
                (gate_in, gate),
                (gate_got, gate_far),
                (up_in, up),
                (up_got, up_far),
                (down_in, down),
                (down_got, down_far),
                (rows_in, rows),
                (sums_in, sums),
            )
        )
    ]
    for load in loads[:3]:
        load.start()
    copies = []
    wide = first.shape[2]
    f32 = jnp.float32

    def leave(source, target, i):
        copies.append(pltpu.make_async_copy(source, target, sems.at[i]))
        copies[-1].start()

    loads[0].wait()
    for load in loads[3:5]:
        load.start()
    out[...] = third[...].astype(f32)
    leave(out, out_out, 5)
    for load in loads[1:3]:
        load.wait()
    for load in loads[5:]:
        load.start()
    at = 0
    for i, (source, target) in enumerate(((query, query_out), (key, key_out), (value, value_out))):
        for n, part in enumerate((first, second)):
            source[:, :, n * wide : (n + 1) * wide] = part[:, at : at + sizes[i], :].astype(f32)
        at += sizes[i]
        leave(source, target, 6 + i)
    for i, (total, far) in enumerate(((gate, gate_far), (up, up_far), (down, down_far))):
        for load in loads[3 + 2 * i : 5 + 2 * i]:
            load.wait()
        total[...] = total[...] + far[...].astype(f32)
        leave(total, (gate_out, up_out, down_out)[i], 2 + i)
    for load in loads[9:]:
        load.wait()
    leave(rows, rows_out, 0)
    leave(sums, sums_out, 1)
    experts = router_out.shape[0]
    for j in range(small.shape[1]):
        cols = slice(j * 128, (j + 1) * 128)
        router_out[:, cols] = small[:experts, j, :]
        first_gain[cols] = small[experts + 1, j, :]
        second_gain[cols] = small[experts, j, :]
    for copy in copies:
        copy.wait()


def deliver(owned, peers, rows, sums, got, small, sizes, expert_count, ep_size):
    width = rows.shape[1]
    f32 = jnp.float32
    vmem, anywhere = pl.BlockSpec(memory_space=pltpu.VMEM), pl.BlockSpec(memory_space=pltpu.HBM)
    first, second, third = (g.reshape((ep_size,) + g.shape[2:]) for g in got)

    def like(value):
        return jax.ShapeDtypeStruct(value.shape, value.dtype)

    shapes = [(ep_size, k, width) for k in sizes]
    results = pl.pallas_call(
        functools.partial(deliver_kernel, ep_size, sizes),
        out_shape=tuple(like(a) for a in owned)
        + (like(rows), like(sums))
        + tuple(jax.ShapeDtypeStruct(shape, f32) for shape in shapes)
        + (
            jax.ShapeDtypeStruct((expert_count, width), f32),
            jax.ShapeDtypeStruct((width,), f32),
            jax.ShapeDtypeStruct((width,), f32),
        ),
        in_specs=[anywhere] * 11 + [vmem],
        out_specs=(anywhere,) * 9 + (vmem,) * 3,
        scratch_shapes=[pltpu.VMEM(shape, f32) for shape in shapes]
        + [pltpu.VMEM(a.shape, a.dtype) for a in (*owned, *peers, first, second, third)]
        + [pltpu.VMEM(a.shape, a.dtype) for a in (rows, sums)]
        + [pltpu.SemaphoreType.DMA((9,)), pltpu.SemaphoreType.DMA((11,))],
        compiler_params=pltpu.CompilerParams(vmem_limit_bytes=60 * 1024 * 1024),
        name="deliver",
    )(rows, sums, *owned, *peers, first, second, third, small)
    gate, up, down, rows, sums = results[:5]
    query, key, value, out = (g.reshape(-1, width) for g in results[5:9])
    router, first_gain, second_gain = results[9:]
    return (
        sums,
        rows,
        first_gain,
        query,
        key,
        value,
        out,
        second_gain,
        router,
        gate,
        up,
        down.reshape(gate.shape[0], -1, width),
    )


def group_rows(value_rows):
    return lax.all_gather(value_rows, "tp", axis=0, tiled=True)


def group_totals(value_rows):
    return lax.psum_scatter(value_rows, "tp", scatter_dimension=0, tiled=True).astype(jnp.float32)


def gather_all(value_rows):
    return lax.all_gather(value_rows, ("ep", "tp"), axis=0, tiled=True)


LAST = 1 << 30


def pair_order(expert_ids, slot_order, expert_count):
    experts = jnp.arange(expert_count, dtype=jnp.int32)
    chosen = expert_ids.T[None, :, :] == experts[:, None, None]
    return jnp.min(jnp.where(chosen, slot_order.T[None, :, :], LAST), axis=1)


def kept_pairs(order):
    used = order < LAST
    counts = jnp.sum(used.astype(jnp.int32), axis=2)
    block = jnp.arange(order.shape[0], dtype=jnp.int32)
    earlier = block[None, :] < block[:, None]
    offsets = jnp.sum(jnp.where(earlier[:, :, None], counts[None, :, :], 0), axis=1)
    whole = offsets + counts <= CAP
    edge = (offsets < CAP) & ~whole
    edge_order = jnp.sum(jnp.where(edge[:, :, None], order, 0), axis=0)
    rank = jnp.sum((edge_order[:, :, None] < edge_order[:, None, :]).astype(jnp.int32), axis=1)
    early = offsets[:, :, None] + rank[None, :, :] < CAP
    return used & (whole[:, :, None] | (edge[:, :, None] & early))


def masked_softmax(logits, used):
    top = jnp.max(jnp.where(used, logits, -1e30), axis=-1, keepdims=True)
    powers = jnp.where(used, jnp.exp(logits - top), 0.0)
    return powers / jnp.sum(powers, axis=-1, keepdims=True)


def pair_codes(order_all, per_owner):
    expert_count = order_all.shape[1]
    first = lax.axis_index("ep") * per_owner
    turned = jnp.roll(order_all, -first, axis=1)
    kept = kept_pairs(turned[:, :per_owner])
    dropped = jnp.pad(~kept, ((0, 0), (0, expert_count - per_owner), (0, 0)))
    code = jnp.where(turned < LAST, dropped.astype(jnp.float32), -1.0)
    return code.swapaxes(1, 2).reshape(-1, expert_count).astype(jnp.bfloat16)


def expert_weights(w_gate, w_up, w_down):
    enter = jnp.concatenate([w[e] for w in (w_gate, w_up) for e in range(w.shape[0])], axis=1)
    return enter, w_down.reshape(-1, w_down.shape[2])


def run_experts(rows_all, cots_all, code, w_router, w_gate, w_up, w_down, weights, by_links):
    per_owner, width, units = w_gate.shape
    expert_count = w_router.shape[0]
    ep_size, tp_size = lax.axis_size("ep"), lax.axis_size("tp")
    hidden = per_owner * units
    router = jnp.roll(w_router, -lax.axis_index("ep") * per_owner, axis=0)
    if by_links:
        grads, sums, small, *owned = experts_by_links(
            rows_all, cots_all, code, router, weights, per_owner, ep_size
        )
        share = grads.shape[0]
        return (
            grads,
            sums,
            small[:, :per_owner].reshape(expert_count, share).T,
            owned[:3],
            owned[3:],
        )
    enter, leave = expert_weights(w_gate, w_up, w_down)
    used, kept = code >= 0, (code == 0).astype(jnp.float32)
    logits = jnp.einsum("rd,ed->re", rows_all, router, preferred_element_type=jnp.float32)
    gates = jnp.repeat((kept * masked_softmax(logits, used))[:, :per_owner], units, axis=1)
    act = jnp.dot(rows_all, enter, preferred_element_type=jnp.float32)
    gate_act, up_act = act[:, :hidden], act[:, hidden:]
    back_act = jnp.einsum("rd,fd->rf", cots_all, leave, preferred_element_type=jnp.float32)
    sigma = jax.nn.sigmoid(gate_act)
    value = gate_act * sigma * up_act
    weighted = (gates * value).astype(jnp.bfloat16)
    grad_hidden = gates * back_act
    turned = jnp.concatenate(
        [
            grad_hidden * up_act * sigma * (1.0 + gate_act * (1.0 - sigma)),
            grad_hidden * gate_act * sigma,
        ],
        axis=1,
    ).astype(jnp.bfloat16)
    small = kept[:, :per_owner] * jnp.sum((value * back_act).reshape(-1, per_owner, units), axis=2)
    grads = jnp.einsum("rf,df->rd", turned, enter, preferred_element_type=jnp.float32)
    sums = jnp.dot(weighted, leave, preferred_element_type=jnp.float32)

    def scatter(value_rows):
        return lax.psum_scatter(value_rows, ("ep", "tp"), scatter_dimension=0, tiled=True)

    columns = lax.dynamic_update_slice_in_dim(
        jnp.zeros((small.shape[0], expert_count), jnp.float32),
        small,
        lax.axis_index("ep") * per_owner,
        1,
    )
    both = jnp.einsum(
        "rd,rwef->wedf",
        rows_all,
        turned.reshape(-1, 2, per_owner, units),
        preferred_element_type=jnp.float32,
    )
    down = jnp.einsum("rf,rd->fd", weighted, cots_all, preferred_element_type=jnp.float32)
    return (
        scatter(grads.astype(jnp.bfloat16)).astype(jnp.float32),
        scatter(sums.astype(jnp.bfloat16)).astype(jnp.float32),
        scatter(columns),
        (both[0], both[1], down),
        None,
    )


def visible_block(query_seg, query_pos, query_row, key_seg, key_pos, key_row):
    seg_q = query_seg[:, None]
    seg_k = key_seg[None, :]
    above = (
        (seg_k == seg_q)
        | (seg_k == 0)
        | (seg_k >= 1) & (seg_k <= 4) & (seg_q >= 5) & ((seg_q - 5) // 2 + 1 == seg_k)
    )
    same_tree = query_row[:, None] // TREE_TOKENS == key_row[None, :] // TREE_TOKENS
    return above & same_tree & (key_pos[None, :] <= query_pos[:, None])


def block_scores(query_part, key_rows, allowed, scale):
    scores = (
        jnp.einsum("qkgd,pkd->kgqp", query_part, key_rows, preferred_element_type=jnp.float32)
        * scale
    )
    return jnp.where(allowed[None, None], scores, -1e30)


def attend_forward(query_rows, key_rows, value_rows, segment, position):
    total_rows = query_rows.shape[0]
    scale = query_rows.shape[-1] ** (-0.5)
    row_ids = jnp.arange(total_rows, dtype=jnp.int32)
    allowed = visible_block(segment, position, row_ids, segment, position, row_ids)
    scores = block_scores(query_rows, key_rows, allowed, scale)
    top_score = jnp.max(scores, axis=-1, keepdims=True)
    weights = jnp.exp(scores - top_score)
    weight_sum = jnp.sum(weights, axis=-1, keepdims=True)
    probs = (weights / weight_sum).astype(jnp.bfloat16)
    outputs = jnp.einsum(
        "kgqp,pkd->qkgd", probs, value_rows, preferred_element_type=jnp.float32
    ).astype(jnp.bfloat16)
    log_sums = [top_score + jnp.log(weight_sum)]
    return (outputs, log_sums)


def attend_backward(
    query_rows, key_rows, value_rows, segment, position, log_sums, grad_heads, block_rows
):
    total_rows = query_rows.shape[0]
    scale = query_rows.shape[-1] ** (-0.5)
    row_ids = jnp.arange(total_rows, dtype=jnp.int32)
    grad_keys = jnp.zeros(key_rows.shape, jnp.float32)
    grad_values = jnp.zeros(value_rows.shape, jnp.float32)
    grad_query = []
    for number, first_row in enumerate(range(0, total_rows, block_rows)):
        allowed = visible_block(segment, position, row_ids, segment, position, row_ids)
        scores = block_scores(query_rows, key_rows, allowed, scale)
        probs = jnp.where(allowed[None, None], jnp.exp(scores - log_sums[number]), 0.0)
        grad_values = jnp.einsum(
            "kgqp,qkgd->pkd",
            probs.astype(jnp.bfloat16),
            grad_heads,
            preferred_element_type=jnp.float32,
        )
        grad_probs = jnp.einsum(
            "qkgd,pkd->kgqp", grad_heads, value_rows, preferred_element_type=jnp.float32
        )
        inner = jnp.sum(probs * grad_probs, axis=-1, keepdims=True)
        grad_scores = (probs * (grad_probs - inner)).astype(jnp.bfloat16)
        grad_query.append(
            jnp.einsum("kgqp,pkd->qkgd", grad_scores, key_rows, preferred_element_type=jnp.float32)
            * scale
        )
        grad_keys = (
            jnp.einsum(
                "kgqp,qkgd->pkd", grad_scores, query_rows, preferred_element_type=jnp.float32
            )
            * scale
        )
    return (grad_query[0], grad_keys, grad_values)


def local(
    hidden_in,
    gain_attn,
    w_query,
    key_projection_weight,
    value_projection_weight,
    w_out,
    gain_ffn,
    w_router,
    w_gate,
    w_up,
    w_down,
    expert_ids,
    slot_order,
    segment,
    position,
    cotangent,
):
    model_width = w_query.shape[1]
    head_width = HEAD_DIMENSION
    local_heads = w_query.shape[0] // head_width
    local_kv = key_projection_weight.shape[0] // head_width
    group_factor = local_heads // local_kv
    token_count = expert_ids.shape[0]
    share = hidden_in.shape[0]
    row_start = lax.axis_index("tp") * share
    expert_count = w_router.shape[0]
    per_owner = w_gate.shape[0]
    block_rows = 512
    by_links = lax.axis_size("tp") == 4 and lax.axis_size("ep") == 8
    order = pair_order(expert_ids, slot_order, expert_count)
    gain_one = gain_attn.astype(jnp.float32)
    gain_two = gain_ffn.astype(jnp.float32)
    inputs_own = hidden_in.astype(jnp.float32)
    if by_links:
        near = expert_weights(w_gate, w_up, w_down)
        token_info = token_tables(segment, position)
        (
            first_normalized,
            query_rows,
            key_rows,
            value_rows,
            head_outputs,
            log_sums,
            middle_own,
            order_all,
            cot_all,
            normed_two,
            normed_own,
            *far,
        ) = front_by_links(
            hidden_in,
            (gain_attn, gain_ffn),
            (w_query, key_projection_weight, value_projection_weight),
            w_out,
            token_info,
            order,
            cotangent,
            near,
            lax.axis_size("ep"),
        )
        weights = (near[0], far[0], near[1], far[1])
        scale_two = norm_scale(middle_own)
    else:
        weights = None
        scale_one = norm_scale(inputs_own)
        first_normalized = group_rows((inputs_own * scale_one * gain_one).astype(jnp.bfloat16))
        order_all = lax.all_gather(order, "ep")
        cosine_lookup, sine_lookup = rope_tables(position, head_width)
        query_proj = jnp.einsum(
            "rd,fd->rf", first_normalized, w_query, preferred_element_type=jnp.float32
        ).reshape(token_count, local_heads, head_width)
        key_proj = jnp.einsum(
            "rd,fd->rf", first_normalized, key_projection_weight, preferred_element_type=jnp.float32
        ).reshape(token_count, local_kv, head_width)
        query_rows = (
            apply_rotation(query_proj, cosine_lookup, sine_lookup)
            .astype(jnp.bfloat16)
            .reshape(token_count, local_kv, group_factor, head_width)
        )
        key_rows = apply_rotation(key_proj, cosine_lookup, sine_lookup).astype(jnp.bfloat16)
        value_rows = (
            jnp.einsum(
                "rd,fd->rf",
                first_normalized,
                value_projection_weight,
                preferred_element_type=jnp.float32,
            )
            .astype(jnp.bfloat16)
            .reshape(token_count, local_kv, head_width)
        )
        head_outputs, log_sums = attend_forward(query_rows, key_rows, value_rows, segment, position)
        head_outputs = head_outputs.reshape(token_count, local_heads * head_width)
        middle_own = inputs_own + group_totals(
            jnp.dot(head_outputs, w_out, preferred_element_type=jnp.float32).astype(jnp.bfloat16)
        )
        scale_two = norm_scale(middle_own)
        normed_own = (middle_own * scale_two * gain_two).astype(jnp.bfloat16)
        normed_two, cot_all = gather_all(normed_own), gather_all(cotangent)
    code = pair_codes(order_all, per_owner)
    used = lax.dynamic_slice_in_dim(order, row_start, share, 1).T < LAST
    gates = masked_softmax(
        jnp.einsum("rd,ed->re", normed_own, w_router, preferred_element_type=jnp.float32), used
    )
    grad_normed_own, combined_own, grad_gates_own, owned, peers = run_experts(
        normed_two, cot_all, code, w_router, w_gate, w_up, w_down, weights, by_links
    )
    output_own = (middle_own + combined_own).astype(jnp.bfloat16)
    inner_gate = jnp.sum(gates * grad_gates_own, axis=-1, keepdims=True)
    grad_logits = gates * (grad_gates_own - inner_gate)
    router_f = w_router.astype(jnp.float32)
    grad_normed_own = grad_normed_own + jnp.dot(grad_logits, router_f, precision=EXACT_PRECISION)
    grad_router = jnp.dot(grad_logits.T, normed_own.astype(jnp.float32), precision=EXACT_PRECISION)
    grad_gain_ffn = jnp.sum(grad_normed_own * middle_own * scale_two, axis=0)
    grad_middle = cotangent.astype(jnp.float32) + norm_back(
        middle_own, scale_two, gain_two, grad_normed_own
    )
    if by_links:
        *got, grad_input, small, gate_got, up_got, down_got = back_by_links(
            grad_middle.astype(jnp.bfloat16),
            head_outputs,
            w_out,
            query_rows,
            key_rows,
            value_rows,
            log_sums,
            token_info,
            first_normalized.reshape(token_count, model_width),
            w_query,
            key_projection_weight,
            value_projection_weight,
            jnp.concatenate([grad_router, grad_gain_ffn[None, :]], axis=0),
            gain_attn,
            hidden_in,
            grad_middle,
            peers,
            lax.axis_size("ep"),
        )
        ep_size = lax.axis_size("ep")
        weights = (w_query, key_projection_weight, value_projection_weight, w_out)
        return deliver(
            owned,
            (gate_got, up_got, down_got),
            grad_input,
            output_own,
            got,
            small,
            [w.shape[0] // ep_size for w in weights],
            expert_count,
            ep_size,
        )
    grad_attn = group_rows(grad_middle.astype(jnp.bfloat16))
    grad_w_out = jnp.einsum(
        "rf,rd->fd", head_outputs, grad_attn, preferred_element_type=jnp.float32
    )
    grad_w_out = lax.psum(grad_w_out.astype(jnp.bfloat16), "ep").astype(jnp.float32)
    grad_heads = (
        jnp.einsum("rd,fd->rf", grad_attn, w_out, preferred_element_type=jnp.float32)
        .astype(jnp.bfloat16)
        .reshape(token_count, local_kv, group_factor, head_width)
    )
    grad_query, grad_keys, grad_values = attend_backward(
        query_rows, key_rows, value_rows, segment, position, log_sums, grad_heads, block_rows
    )
    grad_query_proj = (
        rotate_back(
            grad_query.reshape(token_count, local_heads, head_width), cosine_lookup, sine_lookup
        )
        .astype(jnp.bfloat16)
        .reshape(token_count, local_heads * head_width)
    )
    grad_key_proj = (
        rotate_back(grad_keys, cosine_lookup, sine_lookup)
        .astype(jnp.bfloat16)
        .reshape(token_count, local_kv * head_width)
    )
    grad_value_proj = grad_values.astype(jnp.bfloat16).reshape(token_count, local_kv * head_width)
    grad_w_query = jnp.einsum(
        "rf,rd->fd", grad_query_proj, first_normalized, preferred_element_type=jnp.float32
    )
    grad_w_key = jnp.einsum(
        "rf,rd->fd", grad_key_proj, first_normalized, preferred_element_type=jnp.float32
    )
    grad_w_value = jnp.einsum(
        "rf,rd->fd", grad_value_proj, first_normalized, preferred_element_type=jnp.float32
    )
    grad_normed_one = jnp.einsum(
        "rf,fd->rd", grad_query_proj, w_query, preferred_element_type=jnp.float32
    )
    grad_normed_one = grad_normed_one + jnp.einsum(
        "rf,fd->rd", grad_key_proj, key_projection_weight, preferred_element_type=jnp.float32
    )
    grad_normed_one = grad_normed_one + jnp.einsum(
        "rf,fd->rd", grad_value_proj, value_projection_weight, preferred_element_type=jnp.float32
    )
    grad_gain_attn = jnp.sum(grad_normed_one * first_normalized.astype(jnp.float32), axis=0)
    small = jnp.concatenate(
        [grad_router, grad_gain_ffn[None, :], (grad_gain_attn / gain_one)[None, :]], axis=0
    )
    grad_w_query, grad_w_key, grad_w_value = (
        lax.psum(g.astype(jnp.bfloat16), "ep").astype(jnp.float32)
        for g in (grad_w_query, grad_w_key, grad_w_value)
    )
    grad_one_own = group_totals(grad_normed_one.astype(jnp.bfloat16))
    small = lax.psum(small, ("ep", "tp"))
    grad_input = grad_middle + norm_back(inputs_own, scale_one, gain_one, grad_one_own)
    grad_router = small[:expert_count]
    grad_gain_ffn, grad_gain_attn = small[expert_count], small[expert_count + 1]
    return (
        output_own,
        grad_input,
        grad_gain_attn,
        grad_w_query,
        grad_w_key,
        grad_w_value,
        grad_w_out,
        grad_gain_ffn,
        grad_router,
        owned[0],
        owned[1],
        owned[2].reshape(w_down.shape),
    )


def solution(mesh):
    placed = (
        P(("ep", "tp"), None),
        P(),
        P("tp", None),
        P("tp", None),
        P("tp", None),
        P("tp", None),
        P(),
        P(),
        P("ep", None, "tp"),
        P("ep", None, "tp"),
        P("ep", "tp", None),
        P("ep", None),
        P("ep", None),
        P("ep"),
        P("ep"),
        P(("ep", "tp"), None),
    )
    return jax.shard_map(
        local,
        mesh=mesh,
        in_specs=placed,
        out_specs=(
            P(("ep", "tp"), None),
            P(("ep", "tp"), None),
            P(),
            P("tp", None),
            P("tp", None),
            P("tp", None),
            P("tp", None),
            P(),
            P(),
            P("ep", None, "tp"),
            P("ep", None, "tp"),
            P("ep", "tp", None),
        ),
        check_vma=False,
    )
```

```python
import functools

import jax
import jax.numpy as jnp
from jax import lax
from jax.experimental import pallas as pl
from jax.experimental.pallas import tpu as pltpu
from jax.sharding import PartitionSpec as P

HEAD_DIMENSION = 64
TREE_TOKENS = 512
TRUNK = 256
CAP = 2304


EPSILON = 1e-06
ROPE_BASE = 10000.0
EXACT_PRECISION = lax.Precision.HIGHEST


def rope_tables(position, head_width):
    half_width = head_width // 2
    freqs = ROPE_BASE ** (-(jnp.arange(half_width, dtype=jnp.float32) * 2.0 / head_width))
    angle = position.astype(jnp.float32)[:, None] * freqs[None, :]
    return (jnp.cos(angle)[:, None, :], jnp.sin(angle)[:, None, :])


def apply_rotation(value_rows, cosine_lookup, sine_lookup):
    half_width = value_rows.shape[-1] // 2
    first = value_rows[..., :half_width]
    second = value_rows[..., half_width:]
    return jnp.concatenate(
        [
            first * cosine_lookup - second * sine_lookup,
            first * sine_lookup + second * cosine_lookup,
        ],
        axis=-1,
    )


def rotate_back(grads, cosine_lookup, sine_lookup):
    half_width = grads.shape[-1] // 2
    first = grads[..., :half_width]
    second = grads[..., half_width:]
    return jnp.concatenate(
        [
            first * cosine_lookup + second * sine_lookup,
            second * cosine_lookup - first * sine_lookup,
        ],
        axis=-1,
    )


def norm_scale(value_rows):
    return lax.rsqrt(jnp.mean(value_rows * value_rows, axis=-1, keepdims=True) + EPSILON)


def norm_back(value_rows, scale, gain, grad_normed):
    weighted = grad_normed * gain
    inner = jnp.mean(value_rows * weighted, axis=-1, keepdims=True)
    grad_values = scale * weighted - value_rows * (scale * scale * scale) * inner
    return grad_values


MESH = pl.DeviceIdType.MESH


class Place:
    def __init__(self, ep_size):
        self.depth = ep_size // 2
        ep, tp = lax.axis_index("ep"), lax.axis_index("tp")
        self.z, self.y = ep // 2, ep % 2
        self.x, self.c = tp // 2, tp % 2

    def device(self, z=None, y=None, x=None, c=None):
        z = self.z if z is None else z
        y = self.y if y is None else y
        x = self.x if x is None else x
        c = self.c if c is None else c
        return (z * 2 + y, x * 2 + c)

    def sibling(self):
        return self.device(c=1 - self.c)

    def x_peer(self):
        return self.device(x=1 - self.x)

    def y_peer(self):
        return self.device(y=1 - self.y)

    def target(self, step):
        side = 1 - 2 * (self.z % 2)
        offset = 2 * (1 - step % 2) + side * (1 - step // 2)
        return lax.rem(self.z + offset + self.depth, self.depth)

    def z_peer(self, step):
        return self.device(z=self.target((1, 1, 2)[step]))


def greet(devices):
    barrier = pltpu.get_barrier_semaphore()
    for device in devices:
        pl.semaphore_signal(barrier, inc=1, device_id=device, device_id_type=MESH)


def meet(devices):
    pl.semaphore_wait(pltpu.get_barrier_semaphore(), len(devices))


def send(src, dst, send_sem, recv_sem, device):
    copy = pltpu.make_async_remote_copy(
        src_ref=src,
        dst_ref=dst,
        send_sem=send_sem,
        recv_sem=recv_sem,
        device_id=device,
        device_id_type=MESH,
    )
    copy.start()
    return copy


def add_into(target, other):
    def tile(i, carry):
        at = pl.ds(pl.multiple_of(i * 16, 16), 16)
        target[at, :] = target[at, :] + other[at, :]
        return carry

    lax.fori_loop(0, target.shape[0] // 16, tile, 0)


def group_gather_body(me, pieces, own, out, own_sem, sems):
    size = own.shape[0] // pieces
    started = []
    local = pltpu.make_async_copy(own, out.at[me.x, me.c], own_sem)
    local.start()

    def at(p):
        return pl.ds(p * size, size)

    def go(kind, p, src, dst, device):
        slot = kind * pieces + p
        started.append(send(src, dst, sems.at[0, slot], sems.at[1, slot], device))

    for p in range(pieces):
        go(0, p, own.at[at(p)], out.at[me.x, me.c, at(p)], me.x_peer())
    for p in range(pieces):
        go(1, p, own.at[at(p)], out.at[me.x, me.c, at(p)], me.sibling())
    for p in range(pieces):
        block = out.at[1 - me.x, me.c, at(p)]
        pltpu.make_async_copy(block, block, sems.at[1, p]).wait()
        go(2, p, block, block, me.sibling())
    for p in range(pieces):
        for kind, x in ((1, me.x), (2, 1 - me.x)):
            block = out.at[x, 1 - me.c, at(p)]
            pltpu.make_async_copy(block, block, sems.at[1, kind * pieces + p]).wait()
    local.wait()
    for copy in started:
        copy.wait_send()


class GroupTotal:
    def __init__(self, me, parts, core_got, pair_got, sems):
        self.me, self.parts, self.core_got, self.pair_got = me, parts, core_got, pair_got
        self.core = [
            pltpu.make_async_remote_copy(
                src_ref=parts.at[x, 1 - me.c],
                dst_ref=core_got.at[x],
                send_sem=sems.at[0, k],
                recv_sem=sems.at[1, k],
                device_id=me.sibling(),
                device_id_type=MESH,
            )
            for k, x in enumerate((1 - me.x, me.x))
        ]
        self.half = pair_got.shape[0] // 2
        self.pair = [
            pltpu.make_async_remote_copy(
                src_ref=core_got.at[1 - me.x, self.rows(part)],
                dst_ref=pair_got.at[self.rows(part)],
                send_sem=sems.at[0, 2 + part],
                recv_sem=sems.at[1, 2 + part],
                device_id=me.x_peer(),
                device_id_type=MESH,
            )
            for part in range(2)
        ]

    def rows(self, part):
        return pl.ds(part * self.half, self.half)

    def begin(self):
        for copy in self.core:
            copy.start()

    def exchange(self):
        self.core[0].wait_recv()
        far = 1 - self.me.x
        for part, copy in enumerate(self.pair):
            rows = self.rows(part)
            add_into(self.core_got.at[far, rows], self.parts.at[far, self.me.c, rows])
            copy.start()

    def finish(self, out, change, part):
        if part == 0:
            self.core[1].wait_recv()
        self.pair[part].wait_recv()

        def tile(i, carry):
            at = pl.ds(pl.multiple_of(part * self.half + i * 16, 16), 16)
            value = (
                self.parts[self.me.x, self.me.c, at, :].astype(jnp.float32)
                + self.core_got[self.me.x, at, :].astype(jnp.float32)
                + self.pair_got[at, :].astype(jnp.float32)
            )
            out[at, :] = change(value, at)
            return carry

        lax.fori_loop(0, self.half // 16, tile, 0)

    def sent(self):
        for copy in self.core + self.pair:
            copy.wait_send()


def all_others(ep_size):
    ep, tp = lax.axis_index("ep"), lax.axis_index("tp")
    return [
        (lax.rem(ep + k // 4, ep_size), lax.rem(tp + k % 4, 4)) for k in range(1, ep_size * 4)
    ]


def experts_kernel(
    ep_size,
    per_owner,
    rows_in,
    cots_in,
    code_in,
    router,
    enter_own,
    enter_peer,
    leave_own,
    leave_peer,
    grad_out,
    sum_out,
    small_out,
    gate_out,
    up_out,
    down_out,
    gate_peer,
    up_peer,
    down_peer,
    rows_buf,
    cots_buf,
    weighted,
    turned,
    enter_sum,
    down_sum,
    parts,
    core_got,
    y_got,
    z_got,
    small_in,
    small_got,
    load_sems,
    core_sems,
    y_sems,
    z_sems,
    small_sems,
    own_sem,
):
    me = Place(ep_size)
    depth = me.depth
    blocks = 2 * depth
    width = router.shape[1]
    share = rows_buf.shape[2]
    tokens = 2 * share
    hidden = leave_own.shape[0]
    units = hidden // per_owner
    f32, bf16 = jnp.float32, jnp.bfloat16
    ep = lax.axis_index("ep")
    others = [
        (lax.rem(ep + k // 2, ep_size), me.x * 2 + lax.rem(me.c + k % 2, 2))
        for k in range(1, 2 * ep_size)
    ]
    greet(others)
    my_place = ep * 2 + me.c
    halves = ((enter_own, leave_own), (enter_peer, leave_peer))

    def where(b):
        return me.target(b // 2), lax.rem(1 - me.y + b % 2, 2)

    def load(b, which):
        z, y = where(b)
        source, target = ((rows_in, rows_buf), (cots_in, cots_buf))[which]
        slot = lax.rem(b, 2)
        return pltpu.make_async_copy(
            source.at[z, y], target.at[slot], load_sems.at[slot, which]
        )

    def core_copy(b):
        return pltpu.make_async_remote_copy(
            src_ref=parts.at[lax.rem(b, 2), :, 1 - me.c],
            dst_ref=core_got.at[b // 2, where(b)[1]],
            send_sem=core_sems.at[0, b],
            recv_sem=core_sems.at[1, b],
            device_id=me.sibling(),
            device_id_type=MESH,
        )

    def y_copy(step, which):
        return pltpu.make_async_remote_copy(
            src_ref=core_got.at[step, 1 - me.y, which],
            dst_ref=y_got.at[step, which],
            send_sem=y_sems.at[0, step, which],
            recv_sem=y_sems.at[1, step, which],
            device_id=me.y_peer(),
            device_id_type=MESH,
        )

    def z_copy(step, which):
        return pltpu.make_async_remote_copy(
            src_ref=y_got.at[step, which],
            dst_ref=z_got.at[step, which],
            send_sem=z_sems.at[0, step, which],
            recv_sem=z_sems.at[1, step, which],
            device_id=me.z_peer(step),
            device_id_type=MESH,
        )

    def small_copy(k, device):
        return pltpu.make_async_remote_copy(
            src_ref=small_in.at[device[0] * 2 + device[1] % 2],
            dst_ref=small_got.at[my_place],
            send_sem=small_sems.at[0, k],
            recv_sem=small_sems.at[1, k],
            device_id=device,
            device_id_type=MESH,
        )

    def dot(a, b, contract):
        return lax.dot_general(
            a, b, ((contract[:1], contract[1:]), ((), ())), preferred_element_type=f32
        )

    def spread(columns):
        return jnp.concatenate(
            [jnp.broadcast_to(columns[:, e : e + 1], (tokens, units)) for e in range(per_owner)],
            axis=1,
        )

    def compute(b):
        z, y = where(b)
        slot = lax.rem(b, 2)
        rows = rows_buf[slot].reshape(tokens, width)
        cots = cots_buf[slot].reshape(tokens, width)
        code = code_in[z * 2 + y, me.x].astype(f32).reshape(tokens, -1)
        used = code >= 0.0
        logits = jnp.where(used, dot(rows, router[...], (1, 1)), -1e30)
        top = jnp.max(logits, axis=1, keepdims=True)
        powers = jnp.where(used, jnp.exp(logits - top), 0.0)
        kept = jnp.where(code == 0.0, 1.0, 0.0)
        gates = spread(kept * powers / jnp.sum(powers, axis=1, keepdims=True))
        products = jnp.zeros((tokens, hidden), f32)
        for h, (enter, leave) in enumerate(halves):
            act = dot(rows, enter[...], (1, 0))
            gate_act, up_act = act[:, :hidden], act[:, hidden:]
            back_act = dot(cots, leave[...], (1, 1))
            sigma = jax.nn.sigmoid(gate_act)
            swish = gate_act * sigma
            value = swish * up_act
            products = products + value * back_act
            weighted[:, h * hidden : (h + 1) * hidden] = (gates * value).astype(bf16)
            grad_hidden = gates * back_act
            at = 2 * h * hidden
            turned[:, at : at + hidden] = (
                grad_hidden * up_act * sigma * (1.0 + gate_act * (1.0 - sigma))
            ).astype(bf16)
            turned[:, at + hidden : at + 2 * hidden] = (grad_hidden * swish).astype(bf16)
        lane = lax.broadcasted_iota(jnp.int32, (8, hidden), 1)
        pick = lax.broadcasted_iota(jnp.int32, (8, hidden), 0)
        mine = jnp.where((lane >= pick * units) & (lane < (pick + 1) * units), 1.0, 0.0)
        grad_gates = lax.dot_general(
            mine,
            spread(kept) * products,
            (((1,), (1,)), ((), ())),
            precision=EXACT_PRECISION,
            preferred_element_type=f32,
        )
        for k in range(2):
            small_in[(z * 2 + y) * 2 + k] = grad_gates[:, k * share : (k + 1) * share]
        tile = 512
        for n in range(width // tile):
            cols = slice(n * tile, (n + 1) * tile)
            grads = (
                dot(turned[:, : 2 * hidden], enter_own[cols, :], (1, 1))
                + dot(turned[:, 2 * hidden :], enter_peer[cols, :], (1, 1))
            ).astype(bf16)
            sums = (
                dot(weighted[:, :hidden], leave_own[:, cols], (1, 0))
                + dot(weighted[:, hidden:], leave_peer[:, cols], (1, 0))
            ).astype(bf16)
            for c in range(2):
                at = slice(c * share, (c + 1) * share)
                parts[slot, 0, c, :, cols] = grads[at]
                parts[slot, 1, c, :, cols] = sums[at]

    def weight_sums(b):
        slot = lax.rem(b, 2)
        tile = 512
        for n in range(width // tile):
            cols = slice(n * tile, (n + 1) * tile)
            rows = rows_buf[slot, :, :, cols].reshape(tokens, tile)
            cots = cots_buf[slot, :, :, cols].reshape(tokens, tile)
            enter_sum[:, cols] += dot(turned[...], rows, (0, 0))
            down_sum[:, cols] += dot(weighted[...], cots, (0, 0))

    for which in range(2):
        load(0, which).start()

    def during(i, lag, body, parity=None):
        b = i - lag
        inside = (b >= 0) & (b < blocks)
        if parity is not None:
            inside &= lax.rem(b + 2 * lag, 2) == parity
        pl.when(inside)(lambda: body(b))

    def work(b):
        for which in range(2):
            load(b, which).wait()

        @pl.when(b + 1 < blocks)
        def _():
            for which in range(2):
                load(b + 1, which).start()

        compute(b)
        pl.when(b == 0)(lambda: meet(others))
        core_copy(b).start()

        @pl.when(b == 0)
        def _():
            enter_sum[...] = jnp.zeros_like(enter_sum)
            down_sum[...] = jnp.zeros_like(down_sum)

        weight_sums(b)

    def core_sum(b):
        step, y = b // 2, where(b)[1]
        core_copy(b).wait_recv()
        for which in range(2):
            add_into(core_got.at[step, y, which], parts.at[lax.rem(b, 2), which, me.c])

        @pl.when(b % 2 == 0)
        def _():
            for which in range(2):
                y_copy(step, which).start()

        core_copy(b).wait_send()

    def y_sum(which):
        def body(b):
            step = b // 2
            y_copy(step, which).wait_recv()
            add_into(y_got.at[step, which], core_got.at[step, me.y, which])
            for k in range(2):
                pl.when(step == k)(lambda: z_copy(k, which).start())

            @pl.when(step == 2)
            def _():
                z_copy(0, which).wait_recv()
                add_into(y_got.at[2, which], z_got.at[0, which])
                z_copy(2, which).start()

        return body

    def small_send(b):
        for k, device in enumerate(others):
            small_copy(k, device).start()
        pltpu.make_async_copy(small_in.at[my_place], small_got.at[my_place], own_sem).start()
        for e in range(per_owner):
            own, peer = e * units, 2 * hidden + e * units
            gate_out[e] = enter_sum[own : own + units, :].T
            up_out[e] = enter_sum[hidden + own : hidden + own + units, :].T
            gate_peer[e] = enter_sum[peer : peer + units, :].T.astype(bf16)
            up_peer[e] = enter_sum[hidden + peer : hidden + peer + units, :].T.astype(bf16)
        down_out[...] = down_sum[:hidden, :]
        down_peer[...] = down_sum[hidden:, :].astype(bf16)

    def turn(i, carry):
        during(i, 0, work)
        during(i, 1, core_sum, 1)
        pl.when(i == blocks)(lambda: small_send(i))
        during(i, 2, y_sum(0), 0)
        during(i, 3, y_sum(1), 0)
        during(i, 0, core_sum, 0)
        return carry

    lax.fori_loop(0, blocks + 2, turn, 0)
    pltpu.make_async_copy(small_in.at[my_place], small_got.at[my_place], own_sem).wait()
    for k, device in enumerate(others):
        small_copy(k, device).wait()
    for k in range(ep_size):
        small_out[k] = small_got[2 * k] + small_got[2 * k + 1]
    for step in range(1, 3):
        for which in range(2):
            z_copy(step, which).wait_recv()

    def finish(which, target):
        def tile(i, carry):
            at = pl.ds(pl.multiple_of(i * 16, 16), 16)
            total = y_got[depth - 1, which, at, :].astype(f32)
            for step in range(1, 3):
                total = total + z_got[step, which, at, :].astype(f32)
            target[at, :] = total
            return carry

        lax.fori_loop(0, share // 16, tile, 0)

    finish(0, grad_out)
    finish(1, sum_out)
    for step in range(depth):
        for which in range(2):
            y_copy(step, which).wait_send()
            if step < depth - 1:
                z_copy(step, which).wait_send()


def experts_by_links(rows_all, cots_all, code, router, weights, per_owner, ep_size):
    depth, _, _, rows, width = rows_all.shape
    hidden = weights[2].shape[0]
    units = hidden // per_owner
    bf16, f32 = jnp.bfloat16, jnp.float32
    dma = pltpu.SemaphoreType.DMA
    vmem = pl.BlockSpec(memory_space=pltpu.VMEM)
    anywhere = pl.BlockSpec(memory_space=pltpu.HBM)
    places = 2 * ep_size
    return pl.pallas_call(
        functools.partial(experts_kernel, ep_size, per_owner),
        out_shape=(
            jax.ShapeDtypeStruct((rows, width), f32),
            jax.ShapeDtypeStruct((rows, width), f32),
            jax.ShapeDtypeStruct((ep_size, 8, rows), f32),
            jax.ShapeDtypeStruct((per_owner, width, units), f32),
            jax.ShapeDtypeStruct((per_owner, width, units), f32),
            jax.ShapeDtypeStruct((hidden, width), f32),
            jax.ShapeDtypeStruct((per_owner, width, units), bf16),
            jax.ShapeDtypeStruct((per_owner, width, units), bf16),
            jax.ShapeDtypeStruct((hidden, width), bf16),
        ),
        in_specs=[anywhere, anywhere] + [vmem] * 6,
        out_specs=(vmem,) * 9,
        scratch_shapes=[
            pltpu.VMEM((2, 2, rows, width), bf16),
            pltpu.VMEM((2, 2, rows, width), bf16),
            pltpu.VMEM((2 * rows, 2 * hidden), bf16),
            pltpu.VMEM((2 * rows, 4 * hidden), bf16),
            pltpu.VMEM((4 * hidden, width), f32),
            pltpu.VMEM((2 * hidden, width), f32),
            pltpu.VMEM((2, 2, 2, rows, width), bf16),
            pltpu.VMEM((depth, 2, 2, rows, width), bf16),
            pltpu.VMEM((depth, 2, rows, width), bf16),
            pltpu.VMEM((depth - 1, 2, rows, width), bf16),
            pltpu.VMEM((places, 8, rows), f32),
            pltpu.VMEM((places, 8, rows), f32),
            dma((2, 2)),
            dma((2, 2 * depth)),
            dma((2, depth, 2)),
            dma((2, depth - 1, 2)),
            dma((2, places - 1)),
            dma,
        ],
        compiler_params=pltpu.CompilerParams(
            collective_id=2, has_side_effects=True, vmem_limit_bytes=60 * 1024 * 1024
        ),
        name="experts_by_links",
    )(rows_all, cots_all, code.reshape(ep_size, 2, 2, rows, -1), router, *weights)


class LinkGather:
    def __init__(self, me, own, out, own_sem, z_sems, y_sems, core_sems, rows=None):
        self.me, self.own, self.out, self.rows = me, own, out, rows
        if rows is not None:
            self.own = own.at[rows]
        self.own_sem, self.z_sems, self.y_sems, self.core_sems = own_sem, z_sems, y_sems, core_sems
        self.begun = []
        depth = me.depth
        self.found = [(me.z, 0, None)]
        for d in range(1, depth):
            self.found.append((me.z - d, d, me.z >= d))
            self.found.append((me.z + d, depth - 1 + d, me.z + d < depth))

    def guard(self, *conditions):
        given = [c for c in conditions if c is not None]
        if not given:
            return lambda body: body()
        total = given[0]
        for c in given[1:]:
            total = total & c
        return pl.when(total)

    def go(self, source, place, sems, slot, device, *conditions):
        def copy():
            return pltpu.make_async_remote_copy(
                src_ref=source,
                dst_ref=place,
                send_sem=sems.at[0, slot],
                recv_sem=sems.at[1, slot],
                device_id=device,
                device_id_type=MESH,
            )

        self.guard(*conditions)(lambda: copy().start())
        self.begun.append((copy, conditions))

    def landed(self, place, sems, slot, condition):
        self.guard(condition)(
            lambda: pltpu.make_async_copy(place, place, sems.at[1, slot]).wait()
        )

    def up(self, source, place, d, condition):
        me = self.me
        device = me.device(z=lax.rem(me.z + 1, me.depth))
        self.go(source, place, self.z_sems, d, device, condition, me.z < me.depth - 1)

    def down(self, source, place, d, condition):
        me = self.me
        device = me.device(z=lax.rem(me.z + me.depth - 1, me.depth))
        self.go(source, place, self.z_sems, me.depth - 1 + d, device, condition, me.z > 0)

    def place(self, z, y, c):
        at = (lax.rem(z + self.me.depth, self.me.depth), y)
        if self.core_sems is not None:
            at += (c,)
        return self.out.at[at if self.rows is None else at + (self.rows,)]

    def to_sibling(self, block, slot, *conditions):
        if self.core_sems is not None:
            self.go(block[0], block[1], self.core_sems, slot, self.me.sibling(), *conditions)

    def begin(self):
        me = self.me
        mine = self.place(me.z, me.y, me.c)
        self.up(self.own, mine, 1, None)
        self.down(self.own, mine, 1, None)
        self.go(self.own, mine, self.y_sems, 0, me.y_peer())
        if self.core_sems is None:
            return
        self.to_sibling((self.own, mine), 0)
        self.local = pltpu.make_async_copy(self.own, mine, self.own_sem)
        self.local.start()

    def relay(self, d):
        me = self.me
        for z, slot, condition in self.found[2 * d - 1 : 2 * d + 1]:
            block = self.place(z, me.y, me.c)
            self.landed(block, self.z_sems, slot, condition)
            if d < me.depth - 1:
                (self.up if slot < me.depth else self.down)(block, block, d + 1, condition)
            self.go(block, block, self.y_sems, slot, me.y_peer(), condition)
            self.to_sibling((block, block), slot, condition)

    def cross(self, first, last):
        me = self.me
        for z, slot, condition in self.found[first:last]:
            block = self.place(z, 1 - me.y, me.c)
            self.landed(block, self.y_sems, slot, condition)
            self.to_sibling((block, block), 2 * me.depth - 1 + slot, condition)

    def finish(self):
        me = self.me
        for z, slot, condition in self.found:
            for y, at in ((me.y, slot), (1 - me.y, 2 * me.depth - 1 + slot)):
                self.landed(self.place(z, y, 1 - me.c), self.core_sems, at, condition)
        self.local.wait()
        self.sent()

    def sent(self):
        for copy, conditions in self.begun:
            self.guard(*conditions)(lambda: copy().wait_send())


class EpSum:
    def __init__(self, me, grads, y_got, z_got, final, sems):
        self.me, self.grads = me, grads
        self.y_got, self.z_got, self.final = y_got, z_got, final
        self.y_sems, self.z_sems, self.fz_sems, self.fy_sems = sems

    def y_copy(self, step):
        me = self.me
        return pltpu.make_async_remote_copy(
            src_ref=self.grads.at[me.target(step), 1 - me.y],
            dst_ref=self.y_got.at[step],
            send_sem=self.y_sems.at[0, step],
            recv_sem=self.y_sems.at[1, step],
            device_id=me.y_peer(),
            device_id_type=MESH,
        )

    def z_copy(self, step):
        return pltpu.make_async_remote_copy(
            src_ref=self.y_got.at[step],
            dst_ref=self.z_got.at[step],
            send_sem=self.z_sems.at[0, step],
            recv_sem=self.z_sems.at[1, step],
            device_id=self.me.z_peer(step),
            device_id_type=MESH,
        )

    def begin(self):
        for step in range(self.me.depth):
            self.y_copy(step).start()

    def fold(self, step):
        me = self.me
        self.y_copy(step).wait_recv()
        add_into(self.y_got.at[step], self.grads.at[me.target(step), me.y])
        if step == 2:
            self.z_copy(0).wait_recv()
            add_into(self.y_got.at[2], self.z_got.at[0])
        if step < me.depth - 1:
            self.z_copy(step).start()

    def settle(self):
        me, depth = self.me, self.me.depth
        for step in range(1, 3):
            self.z_copy(step).wait_recv()

        def tile(i, carry):
            at = pl.ds(pl.multiple_of(i * 16, 16), 16)
            value = self.y_got[depth - 1, at, :].astype(jnp.float32)
            for step in range(1, 3):
                value = value + self.z_got[step, at, :].astype(jnp.float32)
            self.final[me.z, me.y, at, :] = value.astype(self.final.dtype)
            return carry

        lax.fori_loop(0, self.final.shape[2] // 16, tile, 0)
        mine = self.final.at[me.z, me.y]
        self.spread = LinkGather(me, mine, self.final, None, self.fz_sems, self.fy_sems, None)
        self.spread.begin()

    def relay(self, d):
        self.spread.relay(d)

    def finish(self):
        self.spread.cross(0, 2 * self.me.depth - 1)

    def sent(self):
        self.spread.sent()
        for step in range(self.me.depth):
            self.y_copy(step).wait_send()
            if step < self.me.depth - 1:
                self.z_copy(step).wait_send()


def parts_of_tree(tokens):
    return ((slice(0, TRUNK), TRUNK), (slice(TRUNK, tokens), tokens))


def tree_bias(segment, position):
    query_seg, query_pos = segment[...].reshape(1, -1), position[...].reshape(1, -1)
    table = jnp.concatenate([query_seg] * 4 + [query_pos] * 4, axis=0).astype(jnp.float32).T
    key_seg, key_pos = table[:, 0:1].astype(jnp.int32), table[:, 4:5].astype(jnp.int32)
    parent = jnp.where(query_seg >= 5, (query_seg - 5) // 2 + 1, -1)
    above = (key_seg == query_seg) | (key_seg == 0) | (key_seg == parent)
    return jnp.where(above & (key_pos <= query_pos), 0.0, -1e30)


def front_kernel(
    ep_size,
    heads,
    inputs,
    gain_one,
    gain_two,
    w_query,
    w_key,
    w_value,
    w_out,
    cosine,
    sine,
    segment,
    position,
    table,
    cots,
    enter_near,
    leave_near,
    rows_out,
    queries,
    keys,
    values,
    heads_out,
    log_sums,
    middle,
    tables,
    cots_all,
    normed_all,
    normed_own,
    enter_far,
    leave_far,
    first_own,
    bias,
    parts,
    core_got,
    pair_got,
    own_sem,
    gather_sems,
    table_own_sem,
    table_sems,
    group_sems,
    far_sems,
    cots_sems,
    first_sems,
    second_sems,
):
    me = Place(ep_size)
    depth = me.depth
    f32, bf16 = jnp.float32, jnp.bfloat16
    share, width = inputs.shape
    tokens = 4 * share
    size = HEAD_DIMENSION
    groups = keys.shape[1] // size
    per_group = heads // groups
    scale = size ** (-0.5)
    ep, tp = lax.axis_index("ep"), lax.axis_index("tp")
    peers = [(lax.rem(ep + k, ep_size), tp) for k in range(1, ep_size)]
    friends = [me.sibling(), me.x_peer()] + peers
    greet(friends)

    def dot(a, b, contract):
        return lax.dot_general(
            a, b, ((contract[:1], contract[1:]), ((), ())), preferred_element_type=f32
        )

    first_gain = gain_one[...].astype(f32).reshape(1, width)
    second_gain = gain_two[...].astype(f32).reshape(1, width)
    for i in range(share // 16):
        at = slice(i * 16, (i + 1) * 16)
        value = inputs[at, :].astype(f32)
        first_own[at, :] = (value * norm_scale(value) * first_gain).astype(bf16)
    meet(friends)
    cots_gather = LinkGather(me, cots, cots_all, *cots_sems)
    cots_gather.begin()
    table_local = pltpu.make_async_copy(table, tables.at[ep], table_own_sem)
    table_local.start()
    table_copies = [
        send(table, tables.at[ep], table_sems.at[0, k], table_sems.at[1, k], device)
        for k, device in enumerate(peers)
    ]
    bias[...] = tree_bias(segment, position)
    log_sums[...] = jnp.zeros_like(log_sums)
    group_gather_body(me, 4, first_own, rows_out, own_sem, gather_sems)

    early = width // 3

    def to_peer(i):
        source, target = ((leave_near, leave_far), (enter_near, enter_far))[min(i, 1)]
        at = (pl.ds(0, leave_near.shape[0]), pl.ds(0, early), pl.ds(early, width - early))[i]
        return send(source.at[at], target.at[at], far_sems.at[0, i], far_sems.at[1, i], me.x_peer())

    exchanged = [to_peer(0)]
    cots_gather.relay(1)
    rows = rows_out[...].reshape(tokens, width)

    def rotate(part):
        turned = jnp.concatenate([part[:, size // 2 :], part[:, : size // 2]], axis=1)
        return (part * cosine[...] - turned * sine[...]).astype(bf16)

    projected = dot(rows, w_query[...], (1, 1))
    for head in range(heads):
        mine = slice(head * size, (head + 1) * size)
        queries[:, mine] = rotate(projected[:, mine] * scale)
    projected = dot(rows, w_key[...], (1, 1))
    for group in range(groups):
        mine = slice(group * size, (group + 1) * size)
        keys[:, mine] = rotate(projected[:, mine])
    values[...] = dot(rows, w_value[...], (1, 1)).astype(bf16)
    for head in range(heads):
        mine = slice(head * size, (head + 1) * size)
        shared = slice(head // per_group * size, (head // per_group + 1) * size)
        for cols, last_key in parts_of_tree(tokens):
            scores = dot(keys[:last_key, shared], queries[cols, mine], (1, 1))
            scores = scores + bias[:last_key, cols]
            top = jnp.max(scores, axis=0, keepdims=True)
            powers = jnp.exp(scores - top)
            total = jnp.sum(powers, axis=0, keepdims=True)
            log_sums[head : head + 1, cols] = top + jnp.log(total)
            probs = (powers * (1.0 / total)).astype(bf16)
            heads_out[cols, mine] = dot(probs, values[:last_key, shared], (0, 0)).astype(bf16)
        if head == 1:
            cots_gather.relay(2)
    tile = 512
    for n in range(width // tile):
        cols = slice(n * tile, (n + 1) * tile)
        sums = dot(heads_out[...], w_out[:, cols], (1, 0)).astype(bf16)
        parts[:, :, :, cols] = sums.reshape(2, 2, share, tile)
    group = GroupTotal(me, parts, core_got, pair_got, group_sems)
    group.begin()
    for step in range(3, depth):
        cots_gather.relay(step)
    group.exchange()
    exchanged += [to_peer(1), to_peer(2)]
    cots_gather.cross(0, 3)

    def last(value, at):
        total = inputs[at, :].astype(f32) + value
        normed_own[at, :] = (total * norm_scale(total) * second_gain).astype(bf16)
        return total

    halves = []
    for part, sems in enumerate((first_sems, second_sems)):
        group.finish(middle, last, part)
        rows = pl.ds(part * (share // 2), share // 2)
        halves.append(LinkGather(me, normed_own, normed_all, *sems, rows))
        halves[part].begin()
    cots_gather.cross(3, 2 * depth - 1)
    for step in range(1, depth):
        for gather in halves:
            gather.relay(step)
    for gather in halves:
        gather.cross(0, 2 * depth - 1)
    for gather in [cots_gather] + halves:
        gather.finish()
    group.sent()
    table_local.wait()
    for copy in table_copies + exchanged:
        copy.wait()


def token_tables(segment, position):
    cosine, sine = rope_tables(position, HEAD_DIMENSION)
    return (
        jnp.concatenate([cosine[:, 0], cosine[:, 0]], axis=1),
        jnp.concatenate([sine[:, 0], -sine[:, 0]], axis=1),
        segment,
        position,
    )


def front_by_links(inputs, gains, projections, w_out, tables, order, cots, near, ep_size):
    share, width = inputs.shape
    depth = ep_size // 2
    tokens = 4 * share
    heads = w_out.shape[0] // HEAD_DIMENSION
    bf16, f32 = jnp.bfloat16, jnp.float32
    dma = pltpu.SemaphoreType.DMA
    vmem, anywhere = pl.BlockSpec(memory_space=pltpu.VMEM), pl.BlockSpec(memory_space=pltpu.HBM)

    def like(*shape, dtype=bf16):
        return jax.ShapeDtypeStruct(shape, dtype)

    def gather_sems():
        return (dma, dma((2, 2 * depth)), dma((2, 2 * depth)), dma((2, 4 * depth)))

    widths = [w.shape[0] for w in projections]
    everywhere = (depth, 2, 2, share, width)
    return pl.pallas_call(
        functools.partial(front_kernel, ep_size, heads),
        out_shape=(
            like(2, 2, share, width),
            like(tokens, widths[0]),
            like(tokens, widths[1]),
            like(tokens, widths[2]),
            like(tokens, widths[0]),
            like(8, tokens, dtype=f32),
            like(share, width, dtype=f32),
            like(ep_size, *order.shape, dtype=order.dtype),
            like(*everywhere),
            like(*everywhere),
            like(share, width),
            like(*near[0].shape),
            like(*near[1].shape),
        ),
        in_specs=[vmem] * 11 + [anywhere] * 4,
        out_specs=(vmem,) * 7 + (anywhere,) * 3 + (vmem,) + (anywhere,) * 2,
        scratch_shapes=[
            pltpu.VMEM((share, width), bf16),
            pltpu.VMEM((tokens, tokens), f32),
            pltpu.VMEM((2, 2, share, width), bf16),
            pltpu.VMEM((2, share, width), bf16),
            pltpu.VMEM((share, width), bf16),
            dma,
            dma((2, 12)),
            dma,
            dma((2, ep_size - 1)),
            dma((2, 4)),
            dma((2, 3)),
            gather_sems(),
            gather_sems(),
            gather_sems(),
        ],
        compiler_params=pltpu.CompilerParams(
            collective_id=6, has_side_effects=True, vmem_limit_bytes=56 * 1024 * 1024
        ),
        name="front_by_links",
    )(
        inputs,
        *gains,
        *projections,
        w_out,
        *tables,
        order,
        cots,
        *near,
    )


def back_kernel(
    ep_size,
    heads,
    last_row,
    datt_own,
    heads_in,
    w_out,
    queries,
    keys,
    values,
    log_sums,
    segment,
    position,
    cosine,
    sine,
    rows_in,
    w_query,
    w_key,
    w_value,
    small_in,
    gain,
    inputs,
    middle,
    gate_peer,
    up_peer,
    down_peer,
    first_final,
    second_final,
    out_final,
    grad_input,
    small_out,
    gate_got,
    up_got,
    down_got,
    datt,
    bias,
    grad_heads,
    grad_proj,
    key_sum,
    value_sum,
    part_proj,
    part_out,
    y_got,
    z_got,
    y_got_out,
    z_got_out,
    parts,
    core_got,
    pair_got,
    small_src,
    small_got,
    small_sum,
    own_sem,
    gather_sems,
    y_sems,
    z_sems,
    fz_sems,
    fy_sems,
    y_sems_out,
    z_sems_out,
    fz_sems_out,
    fy_sems_out,
    group_sems,
    small_sems,
    spread_sems,
    own_small_sem,
    peer_sems,
):
    me = Place(ep_size)
    depth = me.depth
    f32, bf16 = jnp.float32, jnp.bfloat16
    others = all_others(ep_size)
    greet(others)
    my_place = lax.axis_index("ep") * 4 + lax.axis_index("tp")
    tokens, width = rows_in.shape
    share = datt_own.shape[0]
    size = HEAD_DIMENSION
    groups = keys.shape[1] // size
    per_group = heads // groups
    scale = size ** (-0.5)
    tile = 512

    def dot(a, b, contract):
        return lax.dot_general(
            a, b, ((contract[:1], contract[1:]), ((), ())), preferred_element_type=f32
        )

    bias[...] = tree_bias(segment, position)
    meet(others)
    group_gather_body(me, 4, datt_own, datt, own_sem, gather_sems)

    def to_peer(i):
        source, target = ((gate_peer, gate_got), (up_peer, up_got), (down_peer, down_got))[i]
        return send(source, target, peer_sems.at[0, i], peer_sems.at[1, i], me.x_peer())

    exchanged = [to_peer(i) for i in range(3)]
    for n in range(width // tile):
        cols = slice(n * tile, (n + 1) * tile)
        grads = dot(heads_in[...], datt[:, :, :, cols].reshape(tokens, tile), (0, 0))
        part_out[:, :, :, cols] = grads.astype(bf16).reshape(depth, 2, -1, tile)
    out_sum = EpSum(
        me,
        part_out,
        y_got_out,
        z_got_out,
        out_final,
        (y_sems_out, z_sems_out, fz_sems_out, fy_sems_out),
    )
    out_sum.begin()
    for x in range(2):
        for c in range(2):
            at = pl.ds((x * 2 + c) * share, share)
            grad_heads[at, :] = dot(datt[x, c], w_out[...], (1, 1)).astype(bf16)

    def rotate_back_rows(grads, at):
        turned = jnp.concatenate([grads[:, size // 2 :], grads[:, : size // 2]], axis=1)
        return (grads * cosine[at, :] + turned * sine[at, :]).astype(bf16)

    for head in range(heads):
        group = head // per_group
        mine = slice(head * size, (head + 1) * size)
        shared = slice(group * size, (group + 1) * size)
        grads = []
        for cols, last_key in parts_of_tree(tokens):
            query, grad_head = queries[cols, mine], grad_heads[cols, mine]
            key, value = keys[:last_key, shared], values[:last_key, shared]
            scores = dot(key, query, (1, 1)) + bias[:last_key, cols]
            probs = jnp.exp(scores - log_sums[head : head + 1, cols])
            grad_probs = dot(value, grad_head, (1, 1))
            inner = jnp.sum(probs * grad_probs, axis=0, keepdims=True)
            grad_scores = (probs * (grad_probs - inner)).astype(bf16)
            grads.append(
                (dot(probs.astype(bf16), grad_head, (1, 0)), dot(grad_scores, query, (1, 0)))
            )
            grad_query = dot(grad_scores, key, (0, 0)) * scale
            grad_proj[cols, mine] = rotate_back_rows(grad_query, cols)
        grad_value, grad_key = (
            jnp.concatenate([trunk + both[:TRUNK], both[TRUNK:]], axis=0)
            for trunk, both in zip(*grads)
        )
        if head % per_group:
            grad_value = grad_value + value_sum[...]
            grad_key = grad_key + key_sum[...]
        value_sum[...] = grad_value
        key_sum[...] = grad_key
        if head % per_group == per_group - 1:
            at = heads * size + group * size
            grad_proj[:, at : at + size] = rotate_back_rows(grad_key, slice(0, tokens))
            at += groups * size
            grad_proj[:, at : at + size] = grad_value.astype(bf16)
        if head % 2 and head // 2 < depth - 2:
            out_sum.fold(head // 2)
    folded = min(heads // 2, depth - 2)

    ends = (heads * size, (heads + groups) * size, (heads + 2 * groups) * size)
    wide = width // 2
    sums = []
    for n, final in enumerate((first_final, second_final)):
        cols = slice(n * wide, (n + 1) * wide)
        grads = dot(grad_proj[...], rows_in[:, cols], (0, 0)).astype(bf16)
        at, first = 0, 0
        for end in ends:
            piece = grads[first:end].reshape(depth, 2, -1, wide)
            part_proj[n, :, :, at : at + piece.shape[2]] = piece
            at, first = at + piece.shape[2], end
        sums.append(
            EpSum(
                me,
                part_proj.at[n],
                y_got.at[n],
                z_got.at[n],
                final,
                (y_sems.at[n], z_sems.at[n], fz_sems.at[n], fy_sems.at[n]),
            )
        )
        if n == 1:
            sums[0].fold(0)
            for step in range(max(folded, depth - 1), depth):
                out_sum.fold(step)
            sums[0].fold(1)
        sums[n].begin()
        if n == 0:
            for step in range(folded, depth - 1):
                out_sum.fold(step)
    first_sum, second_sum = sums
    small_src[...] = jnp.zeros_like(small_src)
    for k in range(width // 128):
        small_src[:last_row, k, :] = small_in[:, k * 128 : (k + 1) * 128]
    own_gain = gain[...].astype(f32).reshape(1, width)
    for n in range(width // tile):
        cols = slice(n * tile, (n + 1) * tile)
        grads = (
            dot(grad_proj[:, : ends[0]], w_query[:, cols], (1, 0))
            + dot(grad_proj[:, ends[0] : ends[1]], w_key[:, cols], (1, 0))
            + dot(grad_proj[:, ends[1] :], w_value[:, cols], (1, 0))
        )
        parts[:, :, :, cols] = grads.astype(bf16).reshape(2, 2, share, tile)
        gained = jnp.sum(grads * rows_in[:, cols].astype(f32), axis=0, keepdims=True)
        gained = gained / own_gain[:, cols]
        for k in range(tile // 128):
            row = n * (tile // 128) + k
            small_src[last_row, row : row + 1, :] = gained[:, k * 128 : (k + 1) * 128]
    for step in range(2, depth - 1):
        first_sum.fold(step)
    out_sum.settle()
    small = [
        send(
            small_src.at[device[0] * 4 + device[1]],
            small_got.at[my_place],
            small_sems.at[0, k],
            small_sems.at[1, k],
            device,
        )
        for k, device in enumerate(others)
    ]
    own_small = pltpu.make_async_copy(
        small_src.at[my_place], small_got.at[my_place], own_small_sem
    )
    own_small.start()
    second_sum.fold(0)
    first_sum.fold(depth - 1)
    first_sum.settle()
    out_sum.relay(1)
    second_sum.fold(1)
    own_small.wait()
    for copy in small:
        copy.wait_recv()
    total = small_got[0]
    for k in range(1, 4 * ep_size):
        total = total + small_got[k]
    small_sum[...] = total
    spread = [
        send(
            small_sum,
            small_out.at[my_place],
            spread_sems.at[0, k],
            spread_sems.at[1, k],
            device,
        )
        for k, device in enumerate(others)
    ]
    small_out[my_place] = total
    group = GroupTotal(me, parts, core_got, pair_got, group_sems)
    group.begin()
    out_sum.relay(2)
    for step in range(2, depth - 1):
        second_sum.fold(step)
    group.exchange()
    first_sum.relay(1)
    second_sum.fold(depth - 1)
    for step in range(3, depth):
        out_sum.relay(step)
    second_sum.settle()
    out_sum.finish()
    first_sum.relay(2)

    def last(value, at):
        values_own = inputs[at, :].astype(f32)
        factor = norm_scale(values_own)
        return middle[at, :] + norm_back(values_own, factor, own_gain, value)

    for part in range(2):
        group.finish(grad_input, last, part)
    second_sum.relay(1)
    for step in range(3, depth):
        first_sum.relay(step)
    for step in range(2, depth):
        second_sum.relay(step)
    first_sum.finish()
    second_sum.finish()
    for copy in spread:
        copy.wait()
    for copy in small:
        copy.wait_send()
    group.sent()
    for each in [out_sum] + sums:
        each.sent()
    for copy in exchanged:
        copy.wait()


def back_by_links(
    datt_own,
    heads_in,
    w_out,
    queries,
    keys,
    values,
    log_sums,
    tables,
    rows_in,
    w_query,
    w_key,
    w_value,
    small,
    gain,
    inputs,
    middle,
    peers,
    ep_size,
):
    tokens, width = rows_in.shape
    share = datt_own.shape[0]
    depth = ep_size // 2
    heads = queries.shape[1] // HEAD_DIMENSION
    places = 4 * ep_size
    bf16, f32 = jnp.bfloat16, jnp.float32
    dma = pltpu.SemaphoreType.DMA
    vmem = pl.BlockSpec(memory_space=pltpu.VMEM)
    anywhere = pl.BlockSpec(memory_space=pltpu.HBM)
    cosine, sine, segment, position = tables
    blocks = jax.ShapeDtypeStruct((places, width // 128, 128), f32)
    sizes = [w.shape[0] // ep_size for w in (w_query, w_key, w_value, w_out)]
    total = sum(sizes[:3])

    def partial(rows, columns):
        return (depth, 2, rows, columns), bf16

    wide = width // 2
    got = pl.pallas_call(
        functools.partial(back_kernel, ep_size, heads, small.shape[0]),
        out_shape=(
            jax.ShapeDtypeStruct(*partial(total, wide)),
            jax.ShapeDtypeStruct(*partial(total, wide)),
            jax.ShapeDtypeStruct(*partial(sizes[3], width)),
            jax.ShapeDtypeStruct((share, width), f32),
            jax.ShapeDtypeStruct(blocks.shape, f32),
        )
        + tuple(jax.ShapeDtypeStruct(p.shape, p.dtype) for p in peers),
        in_specs=[vmem] * 19 + [anywhere] * 3,
        out_specs=(vmem,) * 5 + (anywhere,) * 3,
        scratch_shapes=[
            pltpu.VMEM((2, 2, share, width), bf16),
            pltpu.VMEM((tokens, tokens), f32),
            pltpu.VMEM(queries.shape, bf16),
            pltpu.VMEM((tokens, queries.shape[1] + 2 * keys.shape[1]), bf16),
            pltpu.VMEM((tokens, HEAD_DIMENSION), f32),
            pltpu.VMEM((tokens, HEAD_DIMENSION), f32),
        ]
        + [
            pltpu.VMEM((2, depth, 2, total, wide), bf16),
            pltpu.VMEM((depth, 2, sizes[3], width), bf16),
            pltpu.VMEM((2, depth, total, wide), bf16),
            pltpu.VMEM((2, depth - 1, total, wide), bf16),
            pltpu.VMEM((depth, sizes[3], width), bf16),
            pltpu.VMEM((depth - 1, sizes[3], width), bf16),
            pltpu.VMEM((2, 2, share, width), bf16),
            pltpu.VMEM((2, share, width), bf16),
            pltpu.VMEM((share, width), bf16),
            pltpu.VMEM(blocks.shape, f32),
            pltpu.VMEM(blocks.shape, f32),
            pltpu.VMEM(blocks.shape[1:], f32),
            dma,
            dma((2, 12)),
        ]
        + [dma((2, 2, depth)), dma((2, 2, depth))]
        + [dma((2, 2, 2 * depth))] * 2
        + [dma((2, depth)), dma((2, depth))]
        + [dma((2, 2 * depth))] * 2
        + [dma((2, 4)), dma((2, places - 1)), dma((2, places - 1)), dma, dma((2, 3))],
        compiler_params=pltpu.CompilerParams(
            collective_id=5, has_side_effects=True, vmem_limit_bytes=60 * 1024 * 1024
        ),
        name="back_by_links",
    )(
        datt_own,
        heads_in,
        w_out,
        queries,
        keys,
        values,
        log_sums,
        segment,
        position,
        cosine,
        sine,
        rows_in,
        w_query,
        w_key,
        w_value,
        small,
        gain,
        inputs,
        middle,
        *peers,
    )
    return got


def deliver_kernel(
    ep_size,
    sizes,
    rows_in,
    sums_in,
    gate_in,
    up_in,
    down_in,
    gate_got,
    up_got,
    down_got,
    first_in,
    second_in,
    third_in,
    small,
    gate_out,
    up_out,
    down_out,
    rows_out,
    sums_out,
    query_out,
    key_out,
    value_out,
    out_out,
    router_out,
    first_gain,
    second_gain,
    query,
    key,
    value,
    out,
    gate,
    up,
    down,
    gate_far,
    up_far,
    down_far,
    first,
    second,
    third,
    rows,
    sums,
    sems,
    load_sems,
):
    loads = [
        pltpu.make_async_copy(source, target, load_sems.at[i])
        for i, (source, target) in enumerate(
            (
                (third_in, third),
                (first_in, first),
                (second_in, second),
                (gate_in, gate),
                (gate_got, gate_far),
                (up_in, up),
                (up_got, up_far),
                (down_in, down),
                (down_got, down_far),
                (rows_in, rows),
                (sums_in, sums),
            )
        )
    ]
    for load in loads[:3]:
        load.start()
    copies = []
    wide = first.shape[2]
    f32 = jnp.float32

    def leave(source, target, i):
        copies.append(pltpu.make_async_copy(source, target, sems.at[i]))
        copies[-1].start()

    loads[0].wait()
    for load in loads[3:5]:
        load.start()
    out[...] = third[...].astype(f32)
    leave(out, out_out, 5)
    for load in loads[1:3]:
        load.wait()
    for load in loads[5:]:
        load.start()
    at = 0
    for i, (source, target) in enumerate(((query, query_out), (key, key_out), (value, value_out))):
        for n, part in enumerate((first, second)):
            source[:, :, n * wide : (n + 1) * wide] = part[:, at : at + sizes[i], :].astype(f32)
        at += sizes[i]
        leave(source, target, 6 + i)
    for i, (total, far) in enumerate(((gate, gate_far), (up, up_far), (down, down_far))):
        for load in loads[3 + 2 * i : 5 + 2 * i]:
            load.wait()
        total[...] = total[...] + far[...].astype(f32)
        leave(total, (gate_out, up_out, down_out)[i], 2 + i)
    for load in loads[9:]:
        load.wait()
    leave(rows, rows_out, 0)
    leave(sums, sums_out, 1)
    experts = router_out.shape[0]
    for j in range(small.shape[1]):
        cols = slice(j * 128, (j + 1) * 128)
        router_out[:, cols] = small[:experts, j, :]
        first_gain[cols] = small[experts + 1, j, :]
        second_gain[cols] = small[experts, j, :]
    for copy in copies:
        copy.wait()


def deliver(owned, peers, rows, sums, got, small, sizes, expert_count, ep_size):
    width = rows.shape[1]
    f32 = jnp.float32
    vmem, anywhere = pl.BlockSpec(memory_space=pltpu.VMEM), pl.BlockSpec(memory_space=pltpu.HBM)
    first, second, third = (g.reshape((ep_size,) + g.shape[2:]) for g in got)

    def like(value):
        return jax.ShapeDtypeStruct(value.shape, value.dtype)

    shapes = [(ep_size, k, width) for k in sizes]
    results = pl.pallas_call(
        functools.partial(deliver_kernel, ep_size, sizes),
        out_shape=tuple(like(a) for a in owned)
        + (like(rows), like(sums))
        + tuple(jax.ShapeDtypeStruct(shape, f32) for shape in shapes)
        + (
            jax.ShapeDtypeStruct((expert_count, width), f32),
            jax.ShapeDtypeStruct((width,), f32),
            jax.ShapeDtypeStruct((width,), f32),
        ),
        in_specs=[anywhere] * 11 + [vmem],
        out_specs=(anywhere,) * 9 + (vmem,) * 3,
        scratch_shapes=[pltpu.VMEM(shape, f32) for shape in shapes]
        + [pltpu.VMEM(a.shape, a.dtype) for a in (*owned, *peers, first, second, third)]
        + [pltpu.VMEM(a.shape, a.dtype) for a in (rows, sums)]
        + [pltpu.SemaphoreType.DMA((9,)), pltpu.SemaphoreType.DMA((11,))],
        compiler_params=pltpu.CompilerParams(vmem_limit_bytes=60 * 1024 * 1024),
        name="deliver",
    )(rows, sums, *owned, *peers, first, second, third, small)
    gate, up, down, rows, sums = results[:5]
    query, key, value, out = (g.reshape(-1, width) for g in results[5:9])
    router, first_gain, second_gain = results[9:]
    return (
        sums,
        rows,
        first_gain,
        query,
        key,
        value,
        out,
        second_gain,
        router,
        gate,
        up,
        down.reshape(gate.shape[0], -1, width),
    )


def group_rows(value_rows):
    return lax.all_gather(value_rows, "tp", axis=0, tiled=True)


def group_totals(value_rows):
    return lax.psum_scatter(value_rows, "tp", scatter_dimension=0, tiled=True).astype(jnp.float32)


def gather_all(value_rows):
    return lax.all_gather(value_rows, ("ep", "tp"), axis=0, tiled=True)


LAST = 1 << 30


def pair_order(expert_ids, slot_order, expert_count):
    experts = jnp.arange(expert_count, dtype=jnp.int32)
    chosen = expert_ids.T[None, :, :] == experts[:, None, None]
    return jnp.min(jnp.where(chosen, slot_order.T[None, :, :], LAST), axis=1)


def kept_pairs(order):
    used = order < LAST
    counts = jnp.sum(used.astype(jnp.int32), axis=2)
    block = jnp.arange(order.shape[0], dtype=jnp.int32)
    earlier = block[None, :] < block[:, None]
    offsets = jnp.sum(jnp.where(earlier[:, :, None], counts[None, :, :], 0), axis=1)
    whole = offsets + counts <= CAP
    edge = (offsets < CAP) & ~whole
    edge_order = jnp.sum(jnp.where(edge[:, :, None], order, 0), axis=0)
    rank = jnp.sum((edge_order[:, :, None] < edge_order[:, None, :]).astype(jnp.int32), axis=1)
    early = offsets[:, :, None] + rank[None, :, :] < CAP
    return used & (whole[:, :, None] | (edge[:, :, None] & early))


def masked_softmax(logits, used):
    top = jnp.max(jnp.where(used, logits, -1e30), axis=-1, keepdims=True)
    powers = jnp.where(used, jnp.exp(logits - top), 0.0)
    return powers / jnp.sum(powers, axis=-1, keepdims=True)


def pair_codes(order_all, per_owner):
    expert_count = order_all.shape[1]
    first = lax.axis_index("ep") * per_owner
    turned = jnp.roll(order_all, -first, axis=1)
    kept = kept_pairs(turned[:, :per_owner])
    dropped = jnp.pad(~kept, ((0, 0), (0, expert_count - per_owner), (0, 0)))
    code = jnp.where(turned < LAST, dropped.astype(jnp.float32), -1.0)
    return code.swapaxes(1, 2).reshape(-1, expert_count).astype(jnp.bfloat16)


def expert_weights(w_gate, w_up, w_down):
    enter = jnp.concatenate([w[e] for w in (w_gate, w_up) for e in range(w.shape[0])], axis=1)
    return enter, w_down.reshape(-1, w_down.shape[2])


def run_experts(rows_all, cots_all, code, w_router, w_gate, w_up, w_down, weights, by_links):
    per_owner, width, units = w_gate.shape
    expert_count = w_router.shape[0]
    ep_size, tp_size = lax.axis_size("ep"), lax.axis_size("tp")
    hidden = per_owner * units
    router = jnp.roll(w_router, -lax.axis_index("ep") * per_owner, axis=0)
    if by_links:
        grads, sums, small, *owned = experts_by_links(
            rows_all, cots_all, code, router, weights, per_owner, ep_size
        )
        share = grads.shape[0]
        return (
            grads,
            sums,
            small[:, :per_owner].reshape(expert_count, share).T,
            owned[:3],
            owned[3:],
        )
    enter, leave = expert_weights(w_gate, w_up, w_down)
    used, kept = code >= 0, (code == 0).astype(jnp.float32)
    logits = jnp.einsum("rd,ed->re", rows_all, router, preferred_element_type=jnp.float32)
    gates = jnp.repeat((kept * masked_softmax(logits, used))[:, :per_owner], units, axis=1)
    act = jnp.dot(rows_all, enter, preferred_element_type=jnp.float32)
    gate_act, up_act = act[:, :hidden], act[:, hidden:]
    back_act = jnp.einsum("rd,fd->rf", cots_all, leave, preferred_element_type=jnp.float32)
    sigma = jax.nn.sigmoid(gate_act)
    value = gate_act * sigma * up_act
    weighted = (gates * value).astype(jnp.bfloat16)
    grad_hidden = gates * back_act
    turned = jnp.concatenate(
        [
            grad_hidden * up_act * sigma * (1.0 + gate_act * (1.0 - sigma)),
            grad_hidden * gate_act * sigma,
        ],
        axis=1,
    ).astype(jnp.bfloat16)
    small = kept[:, :per_owner] * jnp.sum((value * back_act).reshape(-1, per_owner, units), axis=2)
    grads = jnp.einsum("rf,df->rd", turned, enter, preferred_element_type=jnp.float32)
    sums = jnp.dot(weighted, leave, preferred_element_type=jnp.float32)

    def scatter(value_rows):
        return lax.psum_scatter(value_rows, ("ep", "tp"), scatter_dimension=0, tiled=True)

    columns = lax.dynamic_update_slice_in_dim(
        jnp.zeros((small.shape[0], expert_count), jnp.float32),
        small,
        lax.axis_index("ep") * per_owner,
        1,
    )
    both = jnp.einsum(
        "rd,rwef->wedf",
        rows_all,
        turned.reshape(-1, 2, per_owner, units),
        preferred_element_type=jnp.float32,
    )
    down = jnp.einsum("rf,rd->fd", weighted, cots_all, preferred_element_type=jnp.float32)
    return (
        scatter(grads.astype(jnp.bfloat16)).astype(jnp.float32),
        scatter(sums.astype(jnp.bfloat16)).astype(jnp.float32),
        scatter(columns),
        (both[0], both[1], down),
        None,
    )


def visible_block(query_seg, query_pos, query_row, key_seg, key_pos, key_row):
    seg_q = query_seg[:, None]
    seg_k = key_seg[None, :]
    above = (
        (seg_k == seg_q)
        | (seg_k == 0)
        | (seg_k >= 1) & (seg_k <= 4) & (seg_q >= 5) & ((seg_q - 5) // 2 + 1 == seg_k)
    )
    same_tree = query_row[:, None] // TREE_TOKENS == key_row[None, :] // TREE_TOKENS
    return above & same_tree & (key_pos[None, :] <= query_pos[:, None])


def block_scores(query_part, key_rows, allowed, scale):
    scores = (
        jnp.einsum("qkgd,pkd->kgqp", query_part, key_rows, preferred_element_type=jnp.float32)
        * scale
    )
    return jnp.where(allowed[None, None], scores, -1e30)


def attend_forward(query_rows, key_rows, value_rows, segment, position):
    total_rows = query_rows.shape[0]
    scale = query_rows.shape[-1] ** (-0.5)
    row_ids = jnp.arange(total_rows, dtype=jnp.int32)
    allowed = visible_block(segment, position, row_ids, segment, position, row_ids)
    scores = block_scores(query_rows, key_rows, allowed, scale)
    top_score = jnp.max(scores, axis=-1, keepdims=True)
    weights = jnp.exp(scores - top_score)
    weight_sum = jnp.sum(weights, axis=-1, keepdims=True)
    probs = (weights / weight_sum).astype(jnp.bfloat16)
    outputs = jnp.einsum(
        "kgqp,pkd->qkgd", probs, value_rows, preferred_element_type=jnp.float32
    ).astype(jnp.bfloat16)
    log_sums = [top_score + jnp.log(weight_sum)]
    return (outputs, log_sums)


def attend_backward(
    query_rows, key_rows, value_rows, segment, position, log_sums, grad_heads, block_rows
):
    total_rows = query_rows.shape[0]
    scale = query_rows.shape[-1] ** (-0.5)
    row_ids = jnp.arange(total_rows, dtype=jnp.int32)
    grad_keys = jnp.zeros(key_rows.shape, jnp.float32)
    grad_values = jnp.zeros(value_rows.shape, jnp.float32)
    grad_query = []
    for number, first_row in enumerate(range(0, total_rows, block_rows)):
        allowed = visible_block(segment, position, row_ids, segment, position, row_ids)
        scores = block_scores(query_rows, key_rows, allowed, scale)
        probs = jnp.where(allowed[None, None], jnp.exp(scores - log_sums[number]), 0.0)
        grad_values = jnp.einsum(
            "kgqp,qkgd->pkd",
            probs.astype(jnp.bfloat16),
            grad_heads,
            preferred_element_type=jnp.float32,
        )
        grad_probs = jnp.einsum(
            "qkgd,pkd->kgqp", grad_heads, value_rows, preferred_element_type=jnp.float32
        )
        inner = jnp.sum(probs * grad_probs, axis=-1, keepdims=True)
        grad_scores = (probs * (grad_probs - inner)).astype(jnp.bfloat16)
        grad_query.append(
            jnp.einsum("kgqp,pkd->qkgd", grad_scores, key_rows, preferred_element_type=jnp.float32)
            * scale
        )
        grad_keys = (
            jnp.einsum(
                "kgqp,qkgd->pkd", grad_scores, query_rows, preferred_element_type=jnp.float32
            )
            * scale
        )
    return (grad_query[0], grad_keys, grad_values)


def local(
    hidden_in,
    gain_attn,
    w_query,
    key_projection_weight,
    value_projection_weight,
    w_out,
    gain_ffn,
    w_router,
    w_gate,
    w_up,
    w_down,
    expert_ids,
    slot_order,
    segment,
    position,
    cotangent,
):
    model_width = w_query.shape[1]
    head_width = HEAD_DIMENSION
    local_heads = w_query.shape[0] // head_width
    local_kv = key_projection_weight.shape[0] // head_width
    group_factor = local_heads // local_kv
    token_count = expert_ids.shape[0]
    share = hidden_in.shape[0]
    row_start = lax.axis_index("tp") * share
    expert_count = w_router.shape[0]
    per_owner = w_gate.shape[0]
    block_rows = 512
    by_links = lax.axis_size("tp") == 4 and lax.axis_size("ep") == 8
    order = pair_order(expert_ids, slot_order, expert_count)
    gain_one = gain_attn.astype(jnp.float32)
    gain_two = gain_ffn.astype(jnp.float32)
    inputs_own = hidden_in.astype(jnp.float32)
    if by_links:
        near = expert_weights(w_gate, w_up, w_down)
        token_info = token_tables(segment, position)
        (
            first_normalized,
            query_rows,
            key_rows,
            value_rows,
            head_outputs,
            log_sums,
            middle_own,
            order_all,
            cot_all,
            normed_two,
            normed_own,
            *far,
        ) = front_by_links(
            hidden_in,
            (gain_attn, gain_ffn),
            (w_query, key_projection_weight, value_projection_weight),
            w_out,
            token_info,
            order,
            cotangent,
            near,
            lax.axis_size("ep"),
        )
        weights = (near[0], far[0], near[1], far[1])
        scale_two = norm_scale(middle_own)
    else:
        weights = None
        scale_one = norm_scale(inputs_own)
        first_normalized = group_rows((inputs_own * scale_one * gain_one).astype(jnp.bfloat16))
        order_all = lax.all_gather(order, "ep")
        cosine_lookup, sine_lookup = rope_tables(position, head_width)
        query_proj = jnp.einsum(
            "rd,fd->rf", first_normalized, w_query, preferred_element_type=jnp.float32
        ).reshape(token_count, local_heads, head_width)
        key_proj = jnp.einsum(
            "rd,fd->rf", first_normalized, key_projection_weight, preferred_element_type=jnp.float32
        ).reshape(token_count, local_kv, head_width)
        query_rows = (
            apply_rotation(query_proj, cosine_lookup, sine_lookup)
            .astype(jnp.bfloat16)
            .reshape(token_count, local_kv, group_factor, head_width)
        )
        key_rows = apply_rotation(key_proj, cosine_lookup, sine_lookup).astype(jnp.bfloat16)
        value_rows = (
            jnp.einsum(
                "rd,fd->rf",
                first_normalized,
                value_projection_weight,
                preferred_element_type=jnp.float32,
            )
            .astype(jnp.bfloat16)
            .reshape(token_count, local_kv, head_width)
        )
        head_outputs, log_sums = attend_forward(query_rows, key_rows, value_rows, segment, position)
        head_outputs = head_outputs.reshape(token_count, local_heads * head_width)
        middle_own = inputs_own + group_totals(
            jnp.dot(head_outputs, w_out, preferred_element_type=jnp.float32).astype(jnp.bfloat16)
        )
        scale_two = norm_scale(middle_own)
        normed_own = (middle_own * scale_two * gain_two).astype(jnp.bfloat16)
        normed_two, cot_all = gather_all(normed_own), gather_all(cotangent)
    code = pair_codes(order_all, per_owner)
    used = lax.dynamic_slice_in_dim(order, row_start, share, 1).T < LAST
    gates = masked_softmax(
        jnp.einsum("rd,ed->re", normed_own, w_router, preferred_element_type=jnp.float32), used
    )
    grad_normed_own, combined_own, grad_gates_own, owned, peers = run_experts(
        normed_two, cot_all, code, w_router, w_gate, w_up, w_down, weights, by_links
    )
    output_own = (middle_own + combined_own).astype(jnp.bfloat16)
    inner_gate = jnp.sum(gates * grad_gates_own, axis=-1, keepdims=True)
    grad_logits = gates * (grad_gates_own - inner_gate)
    router_f = w_router.astype(jnp.float32)
    grad_normed_own = grad_normed_own + jnp.dot(grad_logits, router_f, precision=EXACT_PRECISION)
    grad_router = jnp.dot(grad_logits.T, normed_own.astype(jnp.float32), precision=EXACT_PRECISION)
    grad_gain_ffn = jnp.sum(grad_normed_own * middle_own * scale_two, axis=0)
    grad_middle = cotangent.astype(jnp.float32) + norm_back(
        middle_own, scale_two, gain_two, grad_normed_own
    )
    if by_links:
        *got, grad_input, small, gate_got, up_got, down_got = back_by_links(
            grad_middle.astype(jnp.bfloat16),
            head_outputs,
            w_out,
            query_rows,
            key_rows,
            value_rows,
            log_sums,
            token_info,
            first_normalized.reshape(token_count, model_width),
            w_query,
            key_projection_weight,
            value_projection_weight,
            jnp.concatenate([grad_router, grad_gain_ffn[None, :]], axis=0),
            gain_attn,
            hidden_in,
            grad_middle,
            peers,
            lax.axis_size("ep"),
        )
        ep_size = lax.axis_size("ep")
        weights = (w_query, key_projection_weight, value_projection_weight, w_out)
        return deliver(
            owned,
            (gate_got, up_got, down_got),
            grad_input,
            output_own,
            got,
            small,
            [w.shape[0] // ep_size for w in weights],
            expert_count,
            ep_size,
        )
    grad_attn = group_rows(grad_middle.astype(jnp.bfloat16))
    grad_w_out = jnp.einsum(
        "rf,rd->fd", head_outputs, grad_attn, preferred_element_type=jnp.float32
    )
    grad_w_out = lax.psum(grad_w_out.astype(jnp.bfloat16), "ep").astype(jnp.float32)
    grad_heads = (
        jnp.einsum("rd,fd->rf", grad_attn, w_out, preferred_element_type=jnp.float32)
        .astype(jnp.bfloat16)
        .reshape(token_count, local_kv, group_factor, head_width)
    )
    grad_query, grad_keys, grad_values = attend_backward(
        query_rows, key_rows, value_rows, segment, position, log_sums, grad_heads, block_rows
    )
    grad_query_proj = (
        rotate_back(
            grad_query.reshape(token_count, local_heads, head_width), cosine_lookup, sine_lookup
        )
        .astype(jnp.bfloat16)
        .reshape(token_count, local_heads * head_width)
    )
    grad_key_proj = (
        rotate_back(grad_keys, cosine_lookup, sine_lookup)
        .astype(jnp.bfloat16)
        .reshape(token_count, local_kv * head_width)
    )
    grad_value_proj = grad_values.astype(jnp.bfloat16).reshape(token_count, local_kv * head_width)
    grad_w_query = jnp.einsum(
        "rf,rd->fd", grad_query_proj, first_normalized, preferred_element_type=jnp.float32
    )
    grad_w_key = jnp.einsum(
        "rf,rd->fd", grad_key_proj, first_normalized, preferred_element_type=jnp.float32
    )
    grad_w_value = jnp.einsum(
        "rf,rd->fd", grad_value_proj, first_normalized, preferred_element_type=jnp.float32
    )
    grad_normed_one = jnp.einsum(
        "rf,fd->rd", grad_query_proj, w_query, preferred_element_type=jnp.float32
    )
    grad_normed_one = grad_normed_one + jnp.einsum(
        "rf,fd->rd", grad_key_proj, key_projection_weight, preferred_element_type=jnp.float32
    )
    grad_normed_one = grad_normed_one + jnp.einsum(
        "rf,fd->rd", grad_value_proj, value_projection_weight, preferred_element_type=jnp.float32
    )
    grad_gain_attn = jnp.sum(grad_normed_one * first_normalized.astype(jnp.float32), axis=0)
    small = jnp.concatenate(
        [grad_router, grad_gain_ffn[None, :], (grad_gain_attn / gain_one)[None, :]], axis=0
    )
    grad_w_query, grad_w_key, grad_w_value = (
        lax.psum(g.astype(jnp.bfloat16), "ep").astype(jnp.float32)
        for g in (grad_w_query, grad_w_key, grad_w_value)
    )
    grad_one_own = group_totals(grad_normed_one.astype(jnp.bfloat16))
    small = lax.psum(small, ("ep", "tp"))
    grad_input = grad_middle + norm_back(inputs_own, scale_one, gain_one, grad_one_own)
    grad_router = small[:expert_count]
    grad_gain_ffn, grad_gain_attn = small[expert_count], small[expert_count + 1]
    return (
        output_own,
        grad_input,
        grad_gain_attn,
        grad_w_query,
        grad_w_key,
        grad_w_value,
        grad_w_out,
        grad_gain_ffn,
        grad_router,
        owned[0],
        owned[1],
        owned[2].reshape(w_down.shape),
    )


def solution(mesh):
    placed = (
        P(("ep", "tp"), None),
        P(),
        P("tp", None),
        P("tp", None),
        P("tp", None),
        P("tp", None),
        P(),
        P(),
        P("ep", None, "tp"),
        P("ep", None, "tp"),
        P("ep", "tp", None),
        P("ep", None),
        P("ep", None),
        P("ep"),
        P("ep"),
        P(("ep", "tp"), None),
    )
    return jax.shard_map(
        local,
        mesh=mesh,
        in_specs=placed,
        out_specs=(
            P(("ep", "tp"), None),
            P(("ep", "tp"), None),
            P(),
            P("tp", None),
            P("tp", None),
            P("tp", None),
            P("tp", None),
            P(),
            P(),
            P("ep", None, "tp"),
            P("ep", None, "tp"),
            P("ep", "tp", None),
        ),
        check_vma=False,
    )
```
